32 devices in a mesh: tensor: 4 (over z), context: 4 (over y, core), dp: 2 (over x).
Axes of the slice: x: 2, y: 2, z: 4, core: 2. Of those that a mesh axis runs over, the one named last changes fastest.
Arguments:
- inputs: bfloat16 [2, 3072, 768], P('dp', ('context', 'tensor')), may hold values from -6 to 6
- first_gain: float32 [768], replicated, may hold values from 0.5 to 1.5
- first_shift: float32 [768], replicated, may hold values from -1 to 1
- project_weight: bfloat16 [3, 768, 768], P(None, None, 'tensor'), may hold values from -0.21875 to 0.21875
- project_bias: float32 [2, 768], P(None, 'tensor'), may hold values from -1.5 to 1.5
- attend_weight: bfloat16 [768, 768], P('tensor'), may hold values from -1.25 to 1.25
- attend_bias: float32 [768], replicated, may hold values from -1.5 to 1.5
- second_gain: float32 [768], replicated, may hold values from 0.5 to 1.5
- second_shift: float32 [768], replicated, may hold values from -1 to 1
- expand_weight: bfloat16 [768, 3072], P(None, 'tensor'), may hold values from -0.21875 to 0.21875
- expand_bias: float32 [3072], P('tensor'), may hold values from -1.5 to 1.5
- shrink_weight: bfloat16 [3072, 768], P('tensor'), may hold values from -0.109375 to 0.109375
- shrink_bias: float32 [768], replicated, may hold values from -1.5 to 1.5
- segments: int32 [2, 3072], P('dp'), may hold values from 0 to 15, never falling along the last dimension, each value on 1 to 1536 neighbouring positions
- block_order: int32 [8], replicated, may hold values from 0 to 7, each once
- cotangent: bfloat16 [2, 3072, 768], P('dp', ('context', 'tensor')), may hold values from -6 to 6
Outputs:
- outputs: bfloat16 [2, 3072, 768], P('dp', ('context', 'tensor'))
- grad_inputs: bfloat16 [2, 3072, 768], P('dp', ('context', 'tensor'))
- grad_first_gain: float32 [768], replicated
- grad_first_shift: float32 [768], replicated
- grad_project_weight: float32 [3, 768, 768], P(None, None, 'tensor')
- grad_project_bias: float32 [2, 768], P(None, 'tensor')
- grad_attend_weight: float32 [768, 768], P('tensor')
- grad_attend_bias: float32 [768], replicated
- grad_second_gain: float32 [768], replicated
- grad_second_shift: float32 [768], replicated
- grad_expand_weight: float32 [768, 3072], P(None, 'tensor')
- grad_expand_bias: float32 [3072], P('tensor')
- grad_shrink_weight: float32 [3072, 768], P('tensor')
- grad_shrink_bias: float32 [768], replicated
The draws below stay inside these ranges and needn't reach their ends.
Inputs may be any that keep to these rules, and one draw needn't show every extreme that they name: `segments`: in each sequence the document numbers never fall; every number appears, each document has 1 to 1536 tokens and one has exactly 1536. Each value appears once: stored block b of 384 tokens holds natural block block_order[b].
All inputs are finite; a program needn't handle non-finite values.
Results may differ from the reference program's by a relative error of at most 0.02.
Values may be sent and summed in bfloat16 or wider, within the bound.
A program may use at most 128 MiB of HBM per device.

```python
import math
import jax
import jax.numpy as jnp
import numpy as np
from jax import lax

D = 768
HEAD_DIM = 64
FF = 3072
TOK_DEV = 768
DOCS = 16
LENGTH = 3072
MOST = 1536
SEQS = 2
N_CONTEXT = 4


def steps_of(own_key, extent, split, least, largest):
    loudness = 1.0
    for axis_at, blocks in split:
        heights = jax.random.uniform(jax.random.fold_in(jax.random.fold_in(own_key, 6), axis_at), (blocks,), jnp.float32, least / len(split), largest / len(split))
        loudness = loudness * jnp.repeat(jnp.exp(heights), extent[axis_at] // blocks).reshape((-1,) + (1,) * (len(extent) - 1 - axis_at))
    return loudness


def length_profile(count, total, reach, slope):
    loads = [(1 << 20) // math.isqrt(grade ** slope) + 1 for grade in range(2, count + 1)]
    spare, given = total - reach - (count - 1), [1] * (count - 1)
    while spare > 0:
        movable = [i for i in range(count - 1) if given[i] < reach]
        whole, left = sum([loads[i] for i in movable]), spare
        for i in movable:
            more = min(reach - given[i], max(1, left * loads[i] // whole), spare)
            given[i] = given[i] + more
            spare = spare - more
    return np.array([reach] + given)


def ragged_sizes(stream_key, amount, total, most, slope):
    if amount == 2:
        one = jax.random.randint(stream_key, (), max(1, total - most), min(most, total - 1) + 1)
        return jnp.stack([one, total - one])
    tallies = jnp.asarray(length_profile(amount, total, most, slope), jnp.int32)
    pairs = (amount - 1) // 2
    source_of, sink = tallies[1:1 + 2 * pairs:2], tallies[2:2 + 2 * pairs:2]
    slack = jnp.minimum(source_of - 1, most - sink)
    moved = jax.random.randint(jax.random.fold_in(stream_key, 1), (pairs,), 0, 1 << 20) % (slack + 1)
    tallies = tallies.at[1:1 + 2 * pairs:2].set(source_of - moved).at[2:2 + 2 * pairs:2].set(sink + moved)
    return tallies[jax.random.permutation(jax.random.fold_in(stream_key, 2), amount)]


def normal_values(own_key, dims, width, reach, cuts=(), kind=jnp.bfloat16):
    loudness = steps_of(own_key, dims, cuts, -0.22, 0.18) if cuts else 1.0
    array = jax.random.normal(own_key, dims, jnp.float32) * width * loudness
    return jnp.minimum(jnp.maximum(array, -reach), reach).astype(kind)


def setup_inputs(seed: int = 0) -> dict:
    key_list = jax.random.split(jax.random.key(seed), 17)
    inputs = normal_values(key_list[0], (SEQS, LENGTH, D), 1.0, 6.0, ((0, 2), (1, 16)))
    first_gain = jnp.clip(1.0 + 0.1 * jax.random.normal(key_list[1], (D,), jnp.float32), 0.5, 1.5)
    first_shift = normal_values(key_list[2], (D,), 0.2, 1.0, (), jnp.float32)
    project_weight = normal_values(key_list[3], (3, D, D), D ** -0.5, 0.21875, ((2, 4),))
    project_bias = normal_values(key_list[4], (2, D), 0.3, 1.5, ((1, 4),), jnp.float32)
    attend_weight = normal_values(key_list[5], (D, D), (D // 48 + 4) ** -0.5, 1.25, ((0, 4),))
    attend_bias = normal_values(key_list[6], (D,), 0.3, 1.5, (), jnp.float32)
    second_gain = jnp.clip(1.0 + 0.1 * jax.random.normal(key_list[7], (D,), jnp.float32), 0.5, 1.5)
    second_shift = normal_values(key_list[8], (D,), 0.2, 1.0, (), jnp.float32)
    expand_weight = normal_values(key_list[9], (D, FF), D ** -0.5, 0.21875, ((1, 4),))
    expand_bias = normal_values(key_list[10], (FF,), 0.3, 1.5, ((0, 4),), jnp.float32)
    shrink_weight = normal_values(key_list[11], (FF, D), FF ** -0.5, 0.109375, ((0, 4),))
    shrink_bias = normal_values(key_list[12], (D,), 0.3, 1.5, (), jnp.float32)
    segments = jax.vmap(lambda own: jnp.searchsorted(jnp.cumsum(ragged_sizes(own, DOCS, LENGTH, MOST, 2)), jnp.arange(LENGTH), side="right"))(jax.random.split(key_list[13], SEQS)).reshape((SEQS, LENGTH)).astype(jnp.int32)
    block_order = jax.random.permutation(key_list[14], 2 * N_CONTEXT).astype(jnp.int32)
    cotangent = normal_values(key_list[15], (SEQS, LENGTH, D), 1.0, 6.0, ((0, 2), (1, 16)))
    return {"inputs": inputs, "first_gain": first_gain, "first_shift": first_shift, "project_weight": project_weight, "project_bias": project_bias, "attend_weight": attend_weight, "attend_bias": attend_bias, "second_gain": second_gain, "second_shift": second_shift, "expand_weight": expand_weight, "expand_bias": expand_bias, "shrink_weight": shrink_weight, "shrink_bias": shrink_bias, "segments": segments, "block_order": block_order, "cotangent": cotangent}


@jax.custom_vjp
def low(v):
    return lax.optimization_barrier(v.astype(jnp.bfloat16)).astype(jnp.float32)

@jax.custom_vjp
def low_back(v):
    return v

def low_keep(v):
    return (low(v), None)

def low_pass(kept, grad):
    return (grad,)

def back_keep(v):
    return (v, None)

def back_low(kept, grad):
    return (low(grad),)
low.defvjp(low_keep, low_pass)
low_back.defvjp(back_keep, back_low)
NEG_FILL = -1e+30
NORM_EPS = 1e-05
HIGHEST = lax.Precision.HIGHEST

def layer_norm(values):
    centre = lax.optimization_barrier(jnp.mean(values, axis=-1, keepdims=True))
    shifted = values - centre
    spread = lax.optimization_barrier(jnp.mean(shifted * shifted, axis=-1, keepdims=True))
    return shifted * lax.rsqrt(spread + NORM_EPS)

def affine_norm(values, gain, shift):
    return layer_norm(values) * gain + shift

def stored_places(order, half_rows, seq_len):
    index = jnp.arange(seq_len, dtype=jnp.int32)
    slots = jnp.arange(order.shape[0], dtype=jnp.int32)
    chosen = lax.optimization_barrier(jnp.sum(jnp.where((index // half_rows)[:, None] == slots[None, :], order[None, :], 0), axis=1))
    return (chosen.astype(jnp.int32) * half_rows + index % half_rows).astype(jnp.int32)

def allowed_pairs(query_place, query_seg, key_place, key_seg):
    return (query_seg[:, None] == key_seg[None, :]) & (key_place[None, :] <= query_place[:, None])

def attend_block(items, key_heads, value_heads, key_place, key_seg):
    query_heads, query_place, query_seg = items
    scores = jnp.einsum('qhe,khe->qhk', query_heads, key_heads, precision=HIGHEST) * HEAD_DIM ** (-0.5)
    allowed = allowed_pairs(query_place, query_seg, key_place, key_seg)
    scores = low_back(jnp.where(allowed[:, None, :], scores, NEG_FILL))
    weights = jax.nn.softmax(scores, axis=-1)
    return jnp.einsum('qhk,khe->qhe', low(weights), value_heads, precision=HIGHEST)

def block_layer(tokens_in, first_gain, first_shift, project_weight, project_bias, attend_weight, attend_bias, second_gain, second_shift, expand_weight, expand_bias, shrink_weight, shrink_bias, places, seg_stored):
    seq_len = tokens_in.shape[0]
    head_count = project_weight.shape[2] // HEAD_DIM
    hidden1 = low(affine_norm(tokens_in, first_gain, first_shift))
    projected = jnp.einsum('rd,kde->kre', hidden1, project_weight, precision=HIGHEST)
    query_rows = low_back(low(projected[0] + project_bias[0]))
    key_rows = low_back(low(projected[1]))
    value_rows = low_back(low(projected[2] + project_bias[1]))
    blk_rows = math.gcd(seq_len, 512)
    blk_count = seq_len // blk_rows
    key_heads = key_rows.reshape(seq_len, head_count, HEAD_DIM)
    value_heads = value_rows.reshape(seq_len, head_count, HEAD_DIM)

    def one_block(items):
        return attend_block(items, key_heads, value_heads, places, seg_stored)
    attended = lax.map(jax.checkpoint(one_block), (query_rows.reshape(blk_count, blk_rows, head_count, HEAD_DIM), places.reshape(blk_count, blk_rows), seg_stored.reshape(blk_count, blk_rows)))
    attended = low_back(low(attended.reshape(seq_len, head_count * HEAD_DIM)))
    branch = low_back(jnp.dot(attended, attend_weight, precision=HIGHEST) + attend_bias)
    middle = tokens_in + branch
    hidden2 = low(affine_norm(middle, second_gain, second_shift))
    pre_act = low_back(jnp.dot(hidden2, expand_weight, precision=HIGHEST) + expand_bias)
    activ = low(jax.nn.gelu(pre_act, approximate=True))
    return middle + jnp.dot(activ, shrink_weight, precision=HIGHEST) + shrink_bias

def reference(inputs, first_gain, first_shift, project_weight, project_bias, attend_weight, attend_bias, second_gain, second_shift, expand_weight, expand_bias, shrink_weight, shrink_bias, segments, block_order, cotangent):
    params = (first_gain.astype(jnp.float32), first_shift.astype(jnp.float32), project_weight.astype(jnp.float32), project_bias.astype(jnp.float32), attend_weight.astype(jnp.float32), attend_bias.astype(jnp.float32), second_gain.astype(jnp.float32), second_shift.astype(jnp.float32), expand_weight.astype(jnp.float32), expand_bias.astype(jnp.float32), shrink_weight.astype(jnp.float32), shrink_bias.astype(jnp.float32))
    places = stored_places(block_order, TOK_DEV // 2, LENGTH)

    def one_sequence(totals, item):
        tokens_in, seg_row, grad_out = item
        seg_stored = jnp.take(seg_row, places).astype(jnp.int32)

        def forward(tokens_val, *weights):
            return block_layer(tokens_val, *weights, places, seg_stored)
        result, pull = jax.vjp(forward, tokens_in.astype(jnp.float32), *params)
        grads = pull(grad_out.astype(jnp.float32))
        totals = tuple((first + second for first, second in zip(totals, grads[1:])))
        return (totals, (result.astype(jnp.bfloat16), grads[0].astype(jnp.bfloat16)))
    start_totals = tuple((jnp.zeros_like(param) for param in params))
    totals, (results, grad_rows) = lax.scan(one_sequence, start_totals, (inputs, segments, cotangent))
    return (results, grad_rows, totals[0], totals[1], totals[2], totals[3], totals[4], totals[5], totals[6], totals[7], totals[8], totals[9], totals[10], totals[11])
```

```python
import functools

import jax
import jax.numpy as jnp
from jax import lax
from jax.experimental import pallas as pl
from jax.experimental.pallas import tpu as pltpu
from jax.sharding import PartitionSpec as P

HEAD_DIM = 64
NEG_FILL = -1e30
NORM_EPS = 1e-05
DOC_LIMIT = 16
MESH = pl.DeviceIdType.MESH
VM = pl.BlockSpec(memory_space=pltpu.VMEM)
SM = pl.BlockSpec(memory_space=pltpu.SMEM)
DMA = pltpu.SemaphoreType.DMA


def remote_params(collective_id):
    return pltpu.CompilerParams(
        collective_id=collective_id, has_side_effects=True, vmem_limit_bytes=48 << 20
    )


def line_barrier(me, n):
    bar = pltpu.get_barrier_semaphore()

    @pl.when(me > 0)
    def _():
        pl.semaphore_signal(bar, inc=1, device_id={"tensor": me - 1}, device_id_type=MESH)

    @pl.when(me < n - 1)
    def _():
        pl.semaphore_signal(bar, inc=1, device_id={"tensor": me + 1}, device_id_type=MESH)

    pl.semaphore_wait(bar, jnp.where(me > 0, 1, 0) + jnp.where(me < n - 1, 1, 0))


def gather_kernel(n, x_ref, o_ref, send, recv, loc):
    me = lax.axis_index("tensor")
    line_barrier(me, n)
    own = pltpu.make_async_copy(x_ref, o_ref.at[me], loc)
    own.start()

    def copy(d, s):
        shard = jnp.clip(me - s if d == 0 else me + s, 0, n - 1)
        return pltpu.make_async_remote_copy(
            src_ref=x_ref if s == 0 else o_ref.at[shard],
            dst_ref=o_ref.at[shard],
            send_sem=send.at[d, s],
            recv_sem=recv.at[d, s],
            device_id={"tensor": jnp.clip(me + 1 if d == 0 else me - 1, 0, n - 1)},
            device_id_type=MESH,
        )

    def sends(d, s):
        return (me - s >= 0) & (me < n - 1) if d == 0 else (me + s < n) & (me > 0)

    def gets(d, s):
        return me - 1 - s >= 0 if d == 0 else me + 1 + s < n

    def landed(d, s):
        shard = jnp.clip(me - 1 - s if d == 0 else me + 1 + s, 0, n - 1)
        return pltpu.make_async_copy(o_ref.at[shard], o_ref.at[shard], recv.at[d, s])

    for s in range(n - 1):
        for d in range(2):
            if s > 0:

                @pl.when(gets(d, s - 1))
                def _():
                    landed(d, s - 1).wait()

            @pl.when(sends(d, s))
            def _():
                copy(d, s).start()

    for d in range(2):

        @pl.when(gets(d, n - 2))
        def _():
            landed(d, n - 2).wait()

        for s in range(n - 1):

            @pl.when(sends(d, s))
            def _():
                copy(d, s).wait_send()

    own.wait()


def gather_rows(x, n, collective_id):
    rows, cols = x.shape
    return pl.pallas_call(
        functools.partial(gather_kernel, n),
        out_shape=jax.ShapeDtypeStruct((n, rows, cols), x.dtype),
        in_specs=[VM],
        out_specs=VM,
        scratch_shapes=[DMA((2, n - 1)), DMA((2, n - 1)), DMA],
        compiler_params=remote_params(collective_id),
    )(x).reshape(n * rows, cols)


def scatter_kernel(n, x_ref, o_ref, buf, tmp, send, recv):
    me = lax.axis_index("tensor")
    line_barrier(me, n)

    def term(d, k):
        return n - 1 - k if d == 0 else k

    def sends(d, k):
        return me < n - 1 - k if d == 0 else me > k

    def behind(d):
        return me > 0 if d == 0 else me < n - 1

    def copy(d, k, first):
        return pltpu.make_async_remote_copy(
            src_ref=x_ref.at[term(d, k)] if first else tmp.at[d, k],
            dst_ref=buf.at[d, k],
            send_sem=send.at[d, k],
            recv_sem=recv.at[d, k],
            device_id={"tensor": jnp.clip(me + 1 if d == 0 else me - 1, 0, n - 1)},
            device_id_type=MESH,
        )

    def landed(d, k):
        return pltpu.make_async_copy(buf.at[d, k], buf.at[d, k], recv.at[d, k])

    for d in range(2):

        @pl.when(jnp.logical_not(behind(d)))
        def _():
            for k in range(n - 1):
                copy(d, k, True).start()

    for k in range(n - 1):
        for d in range(2):

            @pl.when(behind(d) & sends(d, k))
            def _():
                landed(d, k).wait()
                both = buf[d, k].astype(jnp.float32) + x_ref[term(d, k)].astype(jnp.float32)
                tmp[d, k] = both.astype(tmp.dtype)
                copy(d, k, False).start()

    o_ref[...] = x_ref[me].astype(jnp.float32)
    for d in range(2):
        for k in range(n - 1):

            @pl.when(behind(d) & (me == term(d, k)))
            def _():
                landed(d, k).wait()
                o_ref[...] += buf[d, k].astype(jnp.float32)

    for d in range(2):
        for k in range(n - 1):

            @pl.when(sends(d, k))
            def _():
                copy(d, k, False).wait_send()


def scatter_rows(x, n, collective_id):
    rows, cols = x.shape
    own = rows // n
    return pl.pallas_call(
        functools.partial(scatter_kernel, n),
        out_shape=jax.ShapeDtypeStruct((own, cols), jnp.float32),
        in_specs=[VM],
        out_specs=VM,
        scratch_shapes=[
            pltpu.VMEM((2, n - 1, own, cols), x.dtype),
            pltpu.VMEM((2, n - 1, own, cols), x.dtype),
            DMA((2, n - 1)),
            DMA((2, n - 1)),
        ],
        compiler_params=remote_params(collective_id),
    )(x.reshape(n, own, cols))


def group_barrier(axes, sizes):
    mine = [lax.axis_index(name) for name in axes]
    place = sum_index(mine, sizes)
    total = 1
    for size in sizes:
        total *= size
    bar = pltpu.get_barrier_semaphore()
    for shift in range(1, total):
        other = lax.rem(place + shift, total)
        pl.semaphore_signal(bar, inc=1, device_id=spread(other, axes, sizes), device_id_type=MESH)
    pl.semaphore_wait(bar, total - 1)
    return place, total


def sum_index(mine, sizes):
    place = 0
    for at, size in zip(mine, sizes):
        place = place * size + at
    return place


def spread(place, axes, sizes):
    found = {}
    for name, size in reversed(tuple(zip(axes, sizes))):
        found[name] = lax.rem(place, size)
        place = lax.div(place, size)
    return found


def to_heads_kernel(nc, heads, x_ref, o_ref, send, recv, loc):
    me, _ = group_barrier(("context",), (nc,))

    def copy(shift):
        other = lax.rem(me + shift, nc)
        return other, pltpu.make_async_remote_copy(
            src_ref=x_ref.at[jnp.minimum(other, heads - 1)],
            dst_ref=o_ref.at[me],
            send_sem=send.at[shift],
            recv_sem=recv.at[shift],
            device_id={"context": other},
            device_id_type=MESH,
        )

    for shift in range(1, nc):
        other, item = copy(shift)

        @pl.when(other < heads)
        def _():
            item.start()

    own = pltpu.make_async_copy(x_ref.at[jnp.minimum(me, heads - 1)], o_ref.at[me], loc)
    own.start()
    own.wait()

    @pl.when(me < heads)
    def _():
        for shift in range(1, nc):
            source = lax.rem(me + nc - shift, nc)
            pltpu.make_async_copy(o_ref.at[source], o_ref.at[source], recv.at[shift]).wait()

    for shift in range(1, nc):
        other, item = copy(shift)

        @pl.when(other < heads)
        def _():
            item.wait_send()


def to_heads(x, nc, collective_id):
    heads = x.shape[0]
    return pl.pallas_call(
        functools.partial(to_heads_kernel, nc, heads),
        out_shape=jax.ShapeDtypeStruct((nc,) + x.shape[1:], x.dtype),
        in_specs=[VM],
        out_specs=VM,
        scratch_shapes=[DMA((nc,)), DMA((nc,)), DMA],
        compiler_params=remote_params(collective_id),
    )(x)


def from_heads_kernel(nc, heads, x_ref, o_ref, send, recv, loc):
    me, _ = group_barrier(("context",), (nc,))

    def copy(shift):
        other = lax.rem(me + shift, nc)
        return pltpu.make_async_remote_copy(
            src_ref=x_ref.at[other],
            dst_ref=o_ref.at[jnp.minimum(me, heads - 1)],
            send_sem=send.at[shift],
            recv_sem=recv.at[shift],
            device_id={"context": other},
            device_id_type=MESH,
        )

    @pl.when(me < heads)
    def _():
        for shift in range(1, nc):
            copy(shift).start()
        own = pltpu.make_async_copy(x_ref.at[me], o_ref.at[me], loc)
        own.start()
        own.wait()

    for shift in range(1, nc):
        source = lax.rem(me + nc - shift, nc)

        @pl.when(source < heads)
        def _():
            at = jnp.minimum(source, heads - 1)
            pltpu.make_async_copy(o_ref.at[at], o_ref.at[at], recv.at[shift]).wait()

    @pl.when(me < heads)
    def _():
        for shift in range(1, nc):
            copy(shift).wait_send()


def from_heads(x, nc, heads, collective_id):
    return pl.pallas_call(
        functools.partial(from_heads_kernel, nc, heads),
        out_shape=jax.ShapeDtypeStruct((heads,) + x.shape[1:], x.dtype),
        in_specs=[VM],
        out_specs=VM,
        scratch_shapes=[DMA((nc,)), DMA((nc,)), DMA],
        compiler_params=remote_params(collective_id),
    )(x)


AXES = ("context", "tensor")


def rows_kernel(nc, nt, heads, x_ref, o_ref, send, recv, loc):
    me, total = group_barrier(AXES, (nc, nt))
    my_ctx, my_ten = lax.axis_index("context"), lax.axis_index("tensor")
    my_head = my_ten * heads + jnp.minimum(my_ctx, heads - 1)

    def copy(shift):
        other = lax.rem(me + shift, total)
        return pltpu.make_async_remote_copy(
            src_ref=x_ref.at[other],
            dst_ref=o_ref.at[my_head],
            send_sem=send.at[shift],
            recv_sem=recv.at[shift],
            device_id=spread(other, AXES, (nc, nt)),
            device_id_type=MESH,
        )

    @pl.when(my_ctx < heads)
    def _():
        for shift in range(1, total):
            copy(shift).start()
        own = pltpu.make_async_copy(x_ref.at[me], o_ref.at[my_head], loc)
        own.start()
        own.wait()

    for shift in range(1, total):
        source = lax.rem(me + total - shift, total)
        ctx, ten = lax.div(source, nt), lax.rem(source, nt)

        @pl.when(ctx < heads)
        def _():
            at = ten * heads + jnp.minimum(ctx, heads - 1)
            pltpu.make_async_copy(o_ref.at[at], o_ref.at[at], recv.at[shift]).wait()

    @pl.when(my_ctx < heads)
    def _():
        for shift in range(1, total):
            copy(shift).wait_send()


def to_rows(x, nc, nt, heads, collective_id):
    total = nc * nt
    return pl.pallas_call(
        functools.partial(rows_kernel, nc, nt, heads),
        out_shape=jax.ShapeDtypeStruct((nt * heads,) + x.shape[1:], x.dtype),
        in_specs=[VM],
        out_specs=VM,
        scratch_shapes=[DMA((total,)), DMA((total,)), DMA],
        compiler_params=remote_params(collective_id),
    )(x)


def rows_back_kernel(nc, nt, heads, x_ref, o_ref, send, recv, loc):
    me, total = group_barrier(AXES, (nc, nt))
    my_ctx, my_ten = lax.axis_index("context"), lax.axis_index("tensor")

    def copy(shift):
        other = lax.rem(me + shift, total)
        ctx, ten = lax.div(other, nt), lax.rem(other, nt)
        return ctx < heads, pltpu.make_async_remote_copy(
            src_ref=x_ref.at[ten * heads + jnp.minimum(ctx, heads - 1)],
            dst_ref=o_ref.at[me],
            send_sem=send.at[shift],
            recv_sem=recv.at[shift],
            device_id={"context": ctx, "tensor": ten},
            device_id_type=MESH,
        )

    for shift in range(1, total):
        goes, item = copy(shift)

        @pl.when(goes)
        def _():
            item.start()

    own = pltpu.make_async_copy(
        x_ref.at[my_ten * heads + jnp.minimum(my_ctx, heads - 1)], o_ref.at[me], loc
    )
    own.start()
    own.wait()

    @pl.when(my_ctx < heads)
    def _():
        for shift in range(1, total):
            source = lax.rem(me + total - shift, total)
            pltpu.make_async_copy(o_ref.at[source], o_ref.at[source], recv.at[shift]).wait()

    for shift in range(1, total):
        goes, item = copy(shift)

        @pl.when(goes)
        def _():
            item.wait_send()


def rows_back(x, nc, nt, heads, collective_id):
    total = nc * nt
    return pl.pallas_call(
        functools.partial(rows_back_kernel, nc, nt, heads),
        out_shape=jax.ShapeDtypeStruct((total,) + x.shape[1:], x.dtype),
        in_specs=[VM],
        out_specs=VM,
        scratch_shapes=[DMA((total,)), DMA((total,)), DMA],
        compiler_params=remote_params(collective_id),
    )(x)


def vectors_kernel(names, sizes, shared, x_ref, o_ref, now, *rest):
    bufs, sems = rest[: len(names)], rest[len(names) :]
    bar = pltpu.get_barrier_semaphore()
    for name, size in zip(names, sizes):
        me = lax.axis_index(name)
        for shift in range(1, size):
            pl.semaphore_signal(
                bar, inc=1, device_id={name: lax.rem(me + shift, size)}, device_id_type=MESH
            )
    pl.semaphore_wait(bar, sum(sizes) - len(sizes))
    for stage, (name, size) in enumerate(zip(names, sizes)):
        buf, send, recv = bufs[stage], sems[2 * stage], sems[2 * stage + 1]
        me = lax.axis_index(name)

        def copy(shift):
            return pltpu.make_async_remote_copy(
                src_ref=now.at[stage] if stage else x_ref.at[0],
                dst_ref=buf.at[me],
                send_sem=send.at[shift],
                recv_sem=recv.at[shift],
                device_id={name: lax.rem(me + shift, size)},
                device_id_type=MESH,
            )

        for shift in range(1, size):
            copy(shift).start()
        buf[me] = now[stage] if stage else x_ref[0]
        for shift in range(1, size):
            source = lax.rem(me + size - shift, size)
            pltpu.make_async_copy(buf.at[source], buf.at[source], recv.at[shift]).wait()
        total = buf[0]
        for at in range(1, size):
            total = total + buf[at]
        if stage == 0:
            row = lax.broadcasted_iota(jnp.int32, total.shape, 0)
            total = jnp.where(row < shared, total, x_ref[0])
        if stage + 1 < len(names):
            now[stage + 1] = total
        else:
            o_ref[...] = total
        for shift in range(1, size):
            copy(shift).wait_send()


def sum_vectors(rows, shared, mesh_sizes, collective_id):
    names = ("tensor", "context", "dp")
    sizes = tuple(mesh_sizes[name] for name in names)
    shape = rows.shape
    return pl.pallas_call(
        functools.partial(vectors_kernel, names, sizes, shared),
        out_shape=jax.ShapeDtypeStruct(shape, jnp.float32),
        in_specs=[VM],
        out_specs=VM,
        scratch_shapes=[pltpu.VMEM((len(names),) + shape, jnp.float32)]
        + [pltpu.VMEM((size,) + shape, jnp.float32) for size in sizes]
        + [DMA((size,)) for size in sizes for _ in range(2)],
        compiler_params=remote_params(collective_id),
    )(rows[None])


def dot(left, right, dims):
    return lax.dot_general(left, right, ((dims[0], dims[1]), ((), ())), preferred_element_type=jnp.float32)


def key_positions(first, keys, queries):
    return first + lax.broadcasted_iota(jnp.int32, (keys, queries), 0)


def load_rows(qkv_ref, rows, nb, half, qs, kt, ks, vs):
    for block in range(nb):
        part = slice(block % 2 * half, block % 2 * half + half)
        item = qkv_ref[block // 2, :, part]
        qs[block] = item[:HEAD_DIM] * jnp.asarray(HEAD_DIM**-0.5, item.dtype)
        if kt is not None:
            kt[block] = item[HEAD_DIM : 2 * HEAD_DIM]
        ks[block] = item[HEAD_DIM : 2 * HEAD_DIM].T
        if vs is not None:
            vs[block] = item[2 * HEAD_DIM :].T


def forward_kernel(half, slot_ref, low_ref, on_ref, qkv_ref, start_ref, o_ref, full_ref, lse_ref, qs, ks):
    nb = full_ref.shape[0]

    @pl.when(on_ref[0] > 0)
    def _():
        load_rows(qkv_ref, None, nb, half, qs, None, ks, None)

        @pl.loop(0, nb)
        def _(nq):
            slot = slot_ref[nq]
            query = qs[slot]
            start = start_ref[nq]
            here = nq * half + lax.broadcasted_iota(jnp.int32, (1, half), 1)

            def step(nk, state):
                top, total, acc = state
                at = slot_ref[nk]
                score = dot(ks[at], query, ((1,), (0,)))
                place = key_positions(nk * half, half, half)
                score = jnp.where((place >= start) & (place <= here), score, NEG_FILL)
                new_top = jnp.maximum(top, jnp.max(score, axis=0, keepdims=True))
                factor = jnp.exp(top - new_top)
                weight = jnp.exp(score - new_top)
                total = total * factor + jnp.sum(weight, axis=0, keepdims=True)
                value = qkv_ref[at // 2, 2 * HEAD_DIM :, pl.ds(pl.multiple_of(at % 2 * half, 128), half)]
                acc = acc * factor + dot(value, weight.astype(jnp.bfloat16), ((1,), (0,)))
                return new_top, total, acc

            top, total, acc = lax.fori_loop(
                low_ref[nq],
                nq + 1,
                step,
                (
                    jnp.full((1, half), NEG_FILL, jnp.float32),
                    jnp.zeros((1, half), jnp.float32),
                    jnp.zeros((HEAD_DIM, half), jnp.float32),
                ),
            )
            result = acc / total
            full_ref[slot] = result
            lse_ref[slot] = top + jnp.log(total)
            low = result.astype(jnp.bfloat16)
            o_ref[2 * slot] = low[:, : half // 2]
            o_ref[2 * slot + 1] = low[:, half // 2 :]


def attend_forward(qkv, tables, half):
    nc = qkv.shape[0]
    nb = 2 * nc
    return pl.pallas_call(
        functools.partial(forward_kernel, half),
        out_shape=(
            jax.ShapeDtypeStruct((2 * nb, HEAD_DIM, half // 2), jnp.bfloat16),
            jax.ShapeDtypeStruct((nb, HEAD_DIM, half), jnp.float32),
            jax.ShapeDtypeStruct((nb, 1, half), jnp.float32),
        ),
        in_specs=[SM, SM, SM, VM, VM],
        out_specs=(VM, VM, VM),
        scratch_shapes=[
            pltpu.VMEM((nb, HEAD_DIM, half), jnp.bfloat16),
            pltpu.VMEM((nb, half, HEAD_DIM), jnp.bfloat16),
        ],
        compiler_params=pltpu.CompilerParams(vmem_limit_bytes=48 << 20),
    )(tables["slot"], tables["low"], tables["on"], qkv, tables["start"])


def backward_kernel(
    half, slot_ref, high_ref, on_ref, qkv_ref, start_ref, full_ref, lse_ref, grad_ref, o_ref, qs, kt, ks, vs, gs, ds, dq
):
    nb = full_ref.shape[0]

    @pl.when(on_ref[0] > 0)
    def _():
        load_rows(qkv_ref, None, nb, half, qs, kt, ks, vs)
        for block in range(nb):
            both = jnp.concatenate([grad_ref[2 * block], grad_ref[2 * block + 1]], axis=1)
            gs[block] = both
            ds[block] = jnp.sum(both.astype(jnp.float32) * full_ref[block], axis=0, keepdims=True)
            dq[block] = jnp.zeros((HEAD_DIM, half), jnp.float32)

        @pl.loop(0, nb)
        def _(nk):
            at = slot_ref[nk]
            place = key_positions(nk * half, half, half)

            def step(nq, state):
                grad_key, grad_value = state
                slot = slot_ref[nq]
                query, grad = qs[slot], gs[slot]
                here = nq * half + lax.broadcasted_iota(jnp.int32, (1, half), 1)
                score = dot(ks[at], query, ((1,), (0,)))
                score = jnp.where((place >= start_ref[nq]) & (place <= here), score, NEG_FILL)
                weight = jnp.exp(score - lse_ref[slot])
                grad_weight = dot(vs[at], grad, ((1,), (0,)))
                grad_score = (weight * (grad_weight - ds[slot])).astype(jnp.bfloat16)
                grad_value = grad_value + dot(grad, weight.astype(jnp.bfloat16), ((1,), (1,)))
                grad_key = grad_key + dot(query, grad_score, ((1,), (1,)))
                dq[slot] += dot(kt[at], grad_score, ((1,), (0,)))
                return grad_key, grad_value

            zero = jnp.zeros((HEAD_DIM, half), jnp.float32)
            grad_key, grad_value = lax.fori_loop(nk, high_ref[nk], step, (zero, zero))
            columns = pl.ds(pl.multiple_of(at % 2 * half, 128), half)
            o_ref[at // 2, HEAD_DIM : 2 * HEAD_DIM, columns] = grad_key.astype(jnp.bfloat16)
            o_ref[at // 2, 2 * HEAD_DIM :, columns] = grad_value.astype(jnp.bfloat16)

        for block in range(nb):
            part = slice(block % 2 * half, block % 2 * half + half)
            o_ref[block // 2, :HEAD_DIM, part] = (dq[block] * HEAD_DIM**-0.5).astype(jnp.bfloat16)


def attend_backward(qkv, tables, full, lse, grad, half):
    nc = qkv.shape[0]
    nb = 2 * nc
    low = jnp.bfloat16
    return pl.pallas_call(
        functools.partial(backward_kernel, half),
        out_shape=jax.ShapeDtypeStruct(qkv.shape, low),
        in_specs=[SM, SM, SM, VM, VM, VM, VM, VM],
        out_specs=VM,
        scratch_shapes=[
            pltpu.VMEM((nb, HEAD_DIM, half), low),
            pltpu.VMEM((nb, HEAD_DIM, half), low),
            pltpu.VMEM((nb, half, HEAD_DIM), low),
            pltpu.VMEM((nb, half, HEAD_DIM), low),
            pltpu.VMEM((nb, HEAD_DIM, half), low),
            pltpu.VMEM((nb, 1, half), jnp.float32),
            pltpu.VMEM((nb, HEAD_DIM, half), jnp.float32),
        ],
        compiler_params=pltpu.CompilerParams(vmem_limit_bytes=48 << 20),
    )(tables["slot"], tables["high"], tables["on"], qkv, tables["start"], full, lse, grad)


def block_tables(segments, order, half, heads):
    nb = order.shape[0]
    counts = jnp.arange(nb, dtype=jnp.int32)
    slot = jnp.sum(jnp.where(order[None, :] == counts[:, None], counts[None, :], 0), axis=1)
    docs = jnp.arange(DOC_LIMIT, dtype=jnp.int32)
    before = jnp.sum((segments[None, :] < docs[:, None]).astype(jnp.int32), axis=1)
    start = jnp.sum(jnp.where(segments[None, :] == docs[:, None], before[:, None], 0), axis=0)
    blocks = segments.reshape(nb, half)
    first, last = blocks[:, 0], blocks[:, -1]
    low = jnp.sum((last[None, :] < first[:, None]).astype(jnp.int32), axis=1)
    high = jnp.sum((first[None, :] <= last[:, None]).astype(jnp.int32), axis=1)
    on = (lax.axis_index("context") < heads).astype(jnp.int32).reshape(1)
    return {"slot": slot, "low": low, "high": high, "on": on, "start": start.reshape(nb, 1, half)}


def norm_parts(values):
    centre = jnp.mean(values, axis=-1, keepdims=True)
    shifted = values - centre
    spread_ = jnp.mean(shifted * shifted, axis=-1, keepdims=True)
    scale = lax.rsqrt(spread_ + NORM_EPS)
    return shifted * scale, scale


def norm_backward(grad, normed, scale, gain):
    e = grad * gain
    mean_e = jnp.mean(e, axis=-1, keepdims=True)
    mean_en = jnp.mean(e * normed, axis=-1, keepdims=True)
    return (e - mean_e - normed * mean_en) * scale


def gelu_tanh(values):
    return jax.nn.gelu(values, approximate=True)


def cross_rows(left, right):
    return lax.dot_general(
        left, right, (((0,), (0,)), ((), ())), preferred_element_type=jnp.float32
    )


def after(value, done):
    return lax.optimization_barrier((value, done))[0]


def per_device(
    mesh_sizes,
    inputs,
    first_gain,
    first_shift,
    project_weight,
    project_bias,
    attend_weight,
    attend_bias,
    second_gain,
    second_shift,
    expand_weight,
    expand_bias,
    shrink_weight,
    shrink_bias,
    segments,
    block_order,
    cotangent,
):
    nt, nc = mesh_sizes["tensor"], mesh_sizes["context"]
    own_rows, width = inputs.shape[1], inputs.shape[2]
    local_width = project_weight.shape[2]
    heads = local_width // HEAD_DIM
    block_rows = own_rows * nt
    half = block_rows // 2
    low = jnp.bfloat16
    tables = block_tables(segments[0], block_order, half, heads)

    tokens_own = inputs[0].astype(jnp.float32)
    grad_out = cotangent[0]
    normed1, scale1 = norm_parts(tokens_own)
    hidden1 = (normed1 * first_gain + first_shift).astype(low)
    hidden1_full = gather_rows(hidden1, nt, 0)

    attend_full = lax.all_gather(after(attend_weight, hidden1_full), "tensor", axis=0, tiled=True)
    grad_full = lax.all_gather(after(grad_out, attend_full), "tensor", axis=0, tiled=True)

    by_head = project_weight.reshape(3, width, heads, HEAD_DIM)
    bias = jnp.stack([project_bias[0], jnp.zeros_like(project_bias[0]), project_bias[1]])
    bias = bias.reshape(3, heads, HEAD_DIM).transpose(1, 0, 2).reshape(-1, 1)
    weight_rows = by_head.transpose(2, 0, 3, 1).reshape(3 * local_width, width)
    projected = dot(weight_rows, hidden1_full, ((1,), (1,))) + bias
    qkv = to_heads(projected.astype(low).reshape(heads, 3 * HEAD_DIM, block_rows), nc, 1)
    pieces, attended_full, lse = attend_forward(qkv, tables, half)
    attended = to_rows(pieces, nc, nt, heads, 2).reshape(width, own_rows)

    middle = tokens_own + cross_rows(attended, attend_full) + attend_bias
    normed2, scale2 = norm_parts(middle)
    hidden2 = (normed2 * second_gain + second_shift).astype(low)
    hidden2_full = gather_rows(hidden2, nt, 3)
    pre_act = jnp.dot(hidden2_full, expand_weight, preferred_element_type=jnp.float32) + expand_bias
    activ = gelu_tanh(pre_act).astype(low)
    grad_act = dot(grad_full, shrink_weight, ((1,), (1,)))
    grad_pre = jax.vjp(gelu_tanh, pre_act)[1](grad_act)[0].astype(low)
    grad_hidden2 = scatter_rows(dot(grad_pre, expand_weight, ((1,), (1,))).astype(low), nt, 4)

    feed = jnp.dot(activ, shrink_weight, preferred_element_type=jnp.float32).astype(low)
    feed_sum = lax.psum_scatter(
        after(feed, grad_hidden2), "tensor", scatter_dimension=0, tiled=True
    ).astype(jnp.float32)
    outputs = (middle + feed_sum + shrink_bias).astype(low)[None]

    grad_shrink = cross_rows(activ, grad_full).astype(low)
    grad_expand = cross_rows(hidden2_full, grad_pre).astype(low)
    grad_expand_bias = jnp.sum(grad_pre.astype(jnp.float32), axis=0)
    grad_shrink_bias = jnp.sum(grad_out.astype(jnp.float32), axis=0)
    grad_shrink, grad_expand = lax.psum((grad_shrink, grad_expand), ("context", "dp"))

    grad_second_gain = jnp.sum(grad_hidden2 * normed2, axis=0)
    grad_second_shift = jnp.sum(grad_hidden2, axis=0)
    grad_middle = grad_out.astype(jnp.float32) + norm_backward(
        grad_hidden2, normed2, scale2, second_gain
    )
    grad_middle_low = grad_middle.astype(low)
    grad_attend_bias = jnp.sum(grad_middle_low.astype(jnp.float32), axis=0)
    grad_attended = dot(attend_full, grad_middle_low, ((1,), (1,))).astype(low)
    grad_heads = rows_back(
        grad_attended.reshape(nt * heads, HEAD_DIM, own_rows), nc, nt, heads, 5
    )
    grad_attend = jnp.dot(attended, grad_middle_low, preferred_element_type=jnp.float32).astype(low)
    grad_attend = lax.psum_scatter(grad_attend, "tensor", scatter_dimension=0, tiled=True)
    grad_attend = lax.psum(grad_attend, ("context", "dp"))

    grad_qkv = attend_backward(qkv, tables, attended_full, lse, grad_heads, half)
    grad_rows = from_heads(grad_qkv, nc, heads, 6).reshape(3 * local_width, block_rows)
    grad_hidden1 = scatter_rows(cross_rows(grad_rows, weight_rows).astype(low), nt, 7)
    grad_project = dot(hidden1_full, grad_rows, ((0,), (1,))).astype(low)
    grad_project = lax.psum(grad_project, ("context", "dp"))
    grad_project = (
        grad_project.reshape(width, heads, 3, HEAD_DIM).transpose(2, 0, 1, 3).reshape(3, width, local_width)
    )
    row_sums = jnp.sum(grad_rows.astype(jnp.float32), axis=1).reshape(heads, 3, HEAD_DIM)
    grad_project_bias = jnp.concatenate([row_sums[:, 0].reshape(-1), row_sums[:, 2].reshape(-1)])

    grad_first_gain = jnp.sum(grad_hidden1 * normed1, axis=0)
    grad_first_shift = jnp.sum(grad_hidden1, axis=0)
    grad_inputs = (grad_middle + norm_backward(grad_hidden1, normed1, scale1, first_gain)).astype(low)[None]

    spare = -grad_project_bias.shape[0] % width
    vectors = jnp.concatenate(
        [
            grad_first_gain,
            grad_first_shift,
            grad_attend_bias,
            grad_second_gain,
            grad_second_shift,
            grad_shrink_bias,
            grad_expand_bias,
            jnp.pad(grad_project_bias, (0, spare)),
        ]
    ).reshape(-1, width)
    summed = sum_vectors(vectors, 6, mesh_sizes, 8)
    tail = summed[6:].reshape(-1)
    wide = grad_expand_bias.shape[0]
    f32 = lambda value: value.astype(jnp.float32)
    return (
        outputs,
        grad_inputs,
        summed[0],
        summed[1],
        f32(grad_project),
        tail[wide : wide + 2 * local_width].reshape(2, local_width),
        f32(grad_attend),
        summed[2],
        summed[3],
        summed[4],
        f32(grad_expand),
        tail[:wide],
        f32(grad_shrink),
        summed[5],
    )


def solution(mesh):
    rows = P("dp", ("context", "tensor"), None)
    in_specs = (
        rows,
        P(),
        P(),
        P(None, None, "tensor"),
        P(None, "tensor"),
        P("tensor", None),
        P(),
        P(),
        P(),
        P(None, "tensor"),
        P("tensor"),
        P("tensor", None),
        P(),
        P("dp", None),
        P(),
        rows,
    )
    out_specs = (
        rows,
        rows,
        P(),
        P(),
        P(None, None, "tensor"),
        P(None, "tensor"),
        P("tensor", None),
        P(),
        P(),
        P(),
        P(None, "tensor"),
        P("tensor"),
        P("tensor", None),
        P(),
    )
    return jax.shard_map(
        functools.partial(per_device, dict(mesh.shape)),
        mesh=mesh,
        in_specs=in_specs,
        out_specs=out_specs,
        check_vma=False,
    )
```

```python
import functools

import jax
import jax.numpy as jnp
from jax import lax
from jax.experimental import pallas as pl
from jax.experimental.pallas import tpu as pltpu
from jax.sharding import PartitionSpec as P

HEAD_DIM = 64
NEG_FILL = -1e30
NORM_EPS = 1e-05
DOC_LIMIT = 16
MESH = pl.DeviceIdType.MESH
VM = pl.BlockSpec(memory_space=pltpu.VMEM)
SM = pl.BlockSpec(memory_space=pltpu.SMEM)
DMA = pltpu.SemaphoreType.DMA


def remote_params(collective_id):
    return pltpu.CompilerParams(
        collective_id=collective_id, has_side_effects=True, vmem_limit_bytes=48 << 20
    )


def line_barrier(me, n):
    bar = pltpu.get_barrier_semaphore()

    @pl.when(me > 0)
    def _():
        pl.semaphore_signal(bar, inc=1, device_id={"tensor": me - 1}, device_id_type=MESH)

    @pl.when(me < n - 1)
    def _():
        pl.semaphore_signal(bar, inc=1, device_id={"tensor": me + 1}, device_id_type=MESH)

    pl.semaphore_wait(bar, jnp.where(me > 0, 1, 0) + jnp.where(me < n - 1, 1, 0))


def gather_kernel(n, x_ref, o_ref, send, recv, loc):
    me = lax.axis_index("tensor")
    line_barrier(me, n)
    own = pltpu.make_async_copy(x_ref, o_ref.at[me], loc)
    own.start()

    def copy(d, s):
        shard = jnp.clip(me - s if d == 0 else me + s, 0, n - 1)
        return pltpu.make_async_remote_copy(
            src_ref=x_ref if s == 0 else o_ref.at[shard],
            dst_ref=o_ref.at[shard],
            send_sem=send.at[d, s],
            recv_sem=recv.at[d, s],
            device_id={"tensor": jnp.clip(me + 1 if d == 0 else me - 1, 0, n - 1)},
            device_id_type=MESH,
        )

    def sends(d, s):
        return (me - s >= 0) & (me < n - 1) if d == 0 else (me + s < n) & (me > 0)

    def gets(d, s):
        return me - 1 - s >= 0 if d == 0 else me + 1 + s < n

    def landed(d, s):
        shard = jnp.clip(me - 1 - s if d == 0 else me + 1 + s, 0, n - 1)
        return pltpu.make_async_copy(o_ref.at[shard], o_ref.at[shard], recv.at[d, s])

    for s in range(n - 1):
        for d in range(2):
            if s > 0:

                @pl.when(gets(d, s - 1))
                def _():
                    landed(d, s - 1).wait()

            @pl.when(sends(d, s))
            def _():
                copy(d, s).start()

    for d in range(2):

        @pl.when(gets(d, n - 2))
        def _():
            landed(d, n - 2).wait()

        for s in range(n - 1):

            @pl.when(sends(d, s))
            def _():
                copy(d, s).wait_send()

    own.wait()


def gather_rows(x, n, collective_id):
    rows, cols = x.shape
    return pl.pallas_call(
        functools.partial(gather_kernel, n),
        out_shape=jax.ShapeDtypeStruct((n, rows, cols), x.dtype),
        in_specs=[VM],
        out_specs=VM,
        scratch_shapes=[DMA((2, n - 1)), DMA((2, n - 1)), DMA],
        compiler_params=remote_params(collective_id),
    )(x).reshape(n * rows, cols)


def scatter_kernel(n, x_ref, o_ref, buf, tmp, send, recv):
    me = lax.axis_index("tensor")
    line_barrier(me, n)

    def term(d, k):
        return n - 1 - k if d == 0 else k

    def sends(d, k):
        return me < n - 1 - k if d == 0 else me > k

    def behind(d):
        return me > 0 if d == 0 else me < n - 1

    def copy(d, k, first):
        return pltpu.make_async_remote_copy(
            src_ref=x_ref.at[term(d, k)] if first else tmp.at[d, k],
            dst_ref=buf.at[d, k],
            send_sem=send.at[d, k],
            recv_sem=recv.at[d, k],
            device_id={"tensor": jnp.clip(me + 1 if d == 0 else me - 1, 0, n - 1)},
            device_id_type=MESH,
        )

    def landed(d, k):
        return pltpu.make_async_copy(buf.at[d, k], buf.at[d, k], recv.at[d, k])

    for d in range(2):

        @pl.when(jnp.logical_not(behind(d)))
        def _():
            for k in range(n - 1):
                copy(d, k, True).start()

    for k in range(n - 1):
        for d in range(2):

            @pl.when(behind(d) & sends(d, k))
            def _():
                landed(d, k).wait()
                both = buf[d, k].astype(jnp.float32) + x_ref[term(d, k)].astype(jnp.float32)
                tmp[d, k] = both.astype(tmp.dtype)
                copy(d, k, False).start()

    o_ref[...] = x_ref[me].astype(jnp.float32)
    for d in range(2):
        for k in range(n - 1):

            @pl.when(behind(d) & (me == term(d, k)))
            def _():
                landed(d, k).wait()
                o_ref[...] += buf[d, k].astype(jnp.float32)

    for d in range(2):
        for k in range(n - 1):

            @pl.when(sends(d, k))
            def _():
                copy(d, k, False).wait_send()


def scatter_rows(x, n, collective_id):
    rows, cols = x.shape
    own = rows // n
    return pl.pallas_call(
        functools.partial(scatter_kernel, n),
        out_shape=jax.ShapeDtypeStruct((own, cols), jnp.float32),
        in_specs=[VM],
        out_specs=VM,
        scratch_shapes=[
            pltpu.VMEM((2, n - 1, own, cols), x.dtype),
            pltpu.VMEM((2, n - 1, own, cols), x.dtype),
            DMA((2, n - 1)),
            DMA((2, n - 1)),
        ],
        compiler_params=remote_params(collective_id),
    )(x.reshape(n, own, cols))


def group_barrier(axes, sizes):
    mine = [lax.axis_index(name) for name in axes]
    place = sum_index(mine, sizes)
    total = 1
    for size in sizes:
        total *= size
    bar = pltpu.get_barrier_semaphore()
    for shift in range(1, total):
        other = lax.rem(place + shift, total)
        pl.semaphore_signal(bar, inc=1, device_id=spread(other, axes, sizes), device_id_type=MESH)
    pl.semaphore_wait(bar, total - 1)
    return place, total


def sum_index(mine, sizes):
    place = 0
    for at, size in zip(mine, sizes):
        place = place * size + at
    return place


def spread(place, axes, sizes):
    found = {}
    for name, size in reversed(tuple(zip(axes, sizes))):
        found[name] = lax.rem(place, size)
        place = lax.div(place, size)
    return found


def to_heads_kernel(nc, heads, x_ref, o_ref, send, recv, loc):
    me, _ = group_barrier(("context",), (nc,))

    def copy(shift):
        other = lax.rem(me + shift, nc)
        return other, pltpu.make_async_remote_copy(
            src_ref=x_ref.at[jnp.minimum(other, heads - 1)],
            dst_ref=o_ref.at[me],
            send_sem=send.at[shift],
            recv_sem=recv.at[shift],
            device_id={"context": other},
            device_id_type=MESH,
        )

    for shift in range(1, nc):
        other, item = copy(shift)

        @pl.when(other < heads)
        def _():
            item.start()

    own = pltpu.make_async_copy(x_ref.at[jnp.minimum(me, heads - 1)], o_ref.at[me], loc)
    own.start()
    own.wait()

    @pl.when(me < heads)
    def _():
        for shift in range(1, nc):
            source = lax.rem(me + nc - shift, nc)
            pltpu.make_async_copy(o_ref.at[source], o_ref.at[source], recv.at[shift]).wait()

    for shift in range(1, nc):
        other, item = copy(shift)

        @pl.when(other < heads)
        def _():
            item.wait_send()


def to_heads(x, nc, collective_id):
    heads = x.shape[0]
    return pl.pallas_call(
        functools.partial(to_heads_kernel, nc, heads),
        out_shape=jax.ShapeDtypeStruct((nc,) + x.shape[1:], x.dtype),
        in_specs=[VM],
        out_specs=VM,
        scratch_shapes=[DMA((nc,)), DMA((nc,)), DMA],
        compiler_params=remote_params(collective_id),
    )(x)


def from_heads_kernel(nc, heads, x_ref, o_ref, send, recv, loc):
    me, _ = group_barrier(("context",), (nc,))

    def copy(shift):
        other = lax.rem(me + shift, nc)
        return pltpu.make_async_remote_copy(
            src_ref=x_ref.at[other],
            dst_ref=o_ref.at[jnp.minimum(me, heads - 1)],
            send_sem=send.at[shift],
            recv_sem=recv.at[shift],
            device_id={"context": other},
            device_id_type=MESH,
        )

    @pl.when(me < heads)
    def _():
        for shift in range(1, nc):
            copy(shift).start()
        own = pltpu.make_async_copy(x_ref.at[me], o_ref.at[me], loc)
        own.start()
        own.wait()

    for shift in range(1, nc):
        source = lax.rem(me + nc - shift, nc)

        @pl.when(source < heads)
        def _():
            at = jnp.minimum(source, heads - 1)
            pltpu.make_async_copy(o_ref.at[at], o_ref.at[at], recv.at[shift]).wait()

    @pl.when(me < heads)
    def _():
        for shift in range(1, nc):
            copy(shift).wait_send()


def from_heads(x, nc, heads, collective_id):
    return pl.pallas_call(
        functools.partial(from_heads_kernel, nc, heads),
        out_shape=jax.ShapeDtypeStruct((heads,) + x.shape[1:], x.dtype),
        in_specs=[VM],
        out_specs=VM,
        scratch_shapes=[DMA((nc,)), DMA((nc,)), DMA],
        compiler_params=remote_params(collective_id),
    )(x)


AXES = ("context", "tensor")


def rows_kernel(nc, nt, heads, x_ref, o_ref, send, recv, loc):
    me, total = group_barrier(AXES, (nc, nt))
    my_ctx, my_ten = lax.axis_index("context"), lax.axis_index("tensor")
    my_head = my_ten * heads + jnp.minimum(my_ctx, heads - 1)

    def copy(shift):
        other = lax.rem(me + shift, total)
        return pltpu.make_async_remote_copy(
            src_ref=x_ref.at[other],
            dst_ref=o_ref.at[my_head],
            send_sem=send.at[shift],
            recv_sem=recv.at[shift],
            device_id=spread(other, AXES, (nc, nt)),
            device_id_type=MESH,
        )

    @pl.when(my_ctx < heads)
    def _():
        for shift in range(1, total):
            copy(shift).start()
        own = pltpu.make_async_copy(x_ref.at[me], o_ref.at[my_head], loc)
        own.start()
        own.wait()

    for shift in range(1, total):
        source = lax.rem(me + total - shift, total)
        ctx, ten = lax.div(source, nt), lax.rem(source, nt)

        @pl.when(ctx < heads)
        def _():
            at = ten * heads + jnp.minimum(ctx, heads - 1)
            pltpu.make_async_copy(o_ref.at[at], o_ref.at[at], recv.at[shift]).wait()

    @pl.when(my_ctx < heads)
    def _():
        for shift in range(1, total):
            copy(shift).wait_send()


def to_rows(x, nc, nt, heads, collective_id):
    total = nc * nt
    return pl.pallas_call(
        functools.partial(rows_kernel, nc, nt, heads),
        out_shape=jax.ShapeDtypeStruct((nt * heads,) + x.shape[1:], x.dtype),
        in_specs=[VM],
        out_specs=VM,
        scratch_shapes=[DMA((total,)), DMA((total,)), DMA],
        compiler_params=remote_params(collective_id),
    )(x)


def rows_back_kernel(nc, nt, heads, x_ref, o_ref, send, recv, loc):
    me, total = group_barrier(AXES, (nc, nt))
    my_ctx, my_ten = lax.axis_index("context"), lax.axis_index("tensor")

    def copy(shift):
        other = lax.rem(me + shift, total)
        ctx, ten = lax.div(other, nt), lax.rem(other, nt)
        return ctx < heads, pltpu.make_async_remote_copy(
            src_ref=x_ref.at[ten * heads + jnp.minimum(ctx, heads - 1)],
            dst_ref=o_ref.at[me],
            send_sem=send.at[shift],
            recv_sem=recv.at[shift],
            device_id={"context": ctx, "tensor": ten},
            device_id_type=MESH,
        )

    for shift in range(1, total):
        goes, item = copy(shift)

        @pl.when(goes)
        def _():
            item.start()

    own = pltpu.make_async_copy(
        x_ref.at[my_ten * heads + jnp.minimum(my_ctx, heads - 1)], o_ref.at[me], loc
    )
    own.start()
    own.wait()

    @pl.when(my_ctx < heads)
    def _():
        for shift in range(1, total):
            source = lax.rem(me + total - shift, total)
            pltpu.make_async_copy(o_ref.at[source], o_ref.at[source], recv.at[shift]).wait()

    for shift in range(1, total):
        goes, item = copy(shift)

        @pl.when(goes)
        def _():
            item.wait_send()


def rows_back(x, nc, nt, heads, collective_id):
    total = nc * nt
    return pl.pallas_call(
        functools.partial(rows_back_kernel, nc, nt, heads),
        out_shape=jax.ShapeDtypeStruct((total,) + x.shape[1:], x.dtype),
        in_specs=[VM],
        out_specs=VM,
        scratch_shapes=[DMA((total,)), DMA((total,)), DMA],
        compiler_params=remote_params(collective_id),
    )(x)


def vectors_kernel(names, sizes, shared, x_ref, o_ref, now, *rest):
    bufs, sems = rest[: len(names)], rest[len(names) :]
    bar = pltpu.get_barrier_semaphore()
    for name, size in zip(names, sizes):
        me = lax.axis_index(name)
        for shift in range(1, size):
            pl.semaphore_signal(
                bar, inc=1, device_id={name: lax.rem(me + shift, size)}, device_id_type=MESH
            )
    pl.semaphore_wait(bar, sum(sizes) - len(sizes))
    for stage, (name, size) in enumerate(zip(names, sizes)):
        buf, send, recv = bufs[stage], sems[2 * stage], sems[2 * stage + 1]
        me = lax.axis_index(name)

        def copy(shift):
            return pltpu.make_async_remote_copy(
                src_ref=now.at[stage] if stage else x_ref.at[0],
                dst_ref=buf.at[me],
                send_sem=send.at[shift],
                recv_sem=recv.at[shift],
                device_id={name: lax.rem(me + shift, size)},
                device_id_type=MESH,
            )

        for shift in range(1, size):
            copy(shift).start()
        buf[me] = now[stage] if stage else x_ref[0]
        for shift in range(1, size):
            source = lax.rem(me + size - shift, size)
            pltpu.make_async_copy(buf.at[source], buf.at[source], recv.at[shift]).wait()
        total = buf[0]
        for at in range(1, size):
            total = total + buf[at]
        if stage == 0:
            row = lax.broadcasted_iota(jnp.int32, total.shape, 0)
            total = jnp.where(row < shared, total, x_ref[0])
        if stage + 1 < len(names):
            now[stage + 1] = total
        else:
            o_ref[...] = total
        for shift in range(1, size):
            copy(shift).wait_send()


def sum_vectors(rows, shared, mesh_sizes, collective_id):
    names = ("tensor", "context", "dp")
    sizes = tuple(mesh_sizes[name] for name in names)
    shape = rows.shape
    return pl.pallas_call(
        functools.partial(vectors_kernel, names, sizes, shared),
        out_shape=jax.ShapeDtypeStruct(shape, jnp.float32),
        in_specs=[VM],
        out_specs=VM,
        scratch_shapes=[pltpu.VMEM((len(names),) + shape, jnp.float32)]
        + [pltpu.VMEM((size,) + shape, jnp.float32) for size in sizes]
        + [DMA((size,)) for size in sizes for _ in range(2)],
        compiler_params=remote_params(collective_id),
    )(rows[None])


class PlaneSum:
    slots = 7

    def __init__(self, u, o, bufs, send, recv):
        self.u, self.o, self.send, self.recv = u, o, send, recv
        self.rc, self.s1, self.ra, self.rb, self.sa, self.sb, self.ta, self.tb = bufs
        ctx, self.x = lax.axis_index("context"), lax.axis_index("dp")
        self.core, self.y = lax.rem(ctx, 2), lax.div(ctx, 2)
        self.chip_peer = {"context": ctx + 1 - 2 * self.core}
        self.y_peer = {"context": lax.rem(ctx + 2, 4)}
        self.x_peer = {"dp": 1 - self.x}

    @staticmethod
    def scratch(shape, dtype):
        tail = tuple(shape[1:])
        return [pltpu.VMEM((count,) + tail, dtype) for count in (8, 8, 2, 2, 2, 2, 1, 1)] + [
            DMA((10,)),
            DMA((10,)),
        ]

    @staticmethod
    def greet(bar):
        ctx, x = lax.axis_index("context"), lax.axis_index("dp")
        for peer in (
            {"context": ctx + 1 - 2 * lax.rem(ctx, 2)},
            {"context": lax.rem(ctx + 2, 4)},
            {"dp": 1 - x},
        ):
            pl.semaphore_signal(bar, inc=1, device_id=peer, device_id_type=MESH)
        return 3

    def copy(self, at, src, dst, peer):
        return pltpu.make_async_remote_copy(
            src_ref=src,
            dst_ref=dst,
            send_sem=self.send.at[at],
            recv_sem=self.recv.at[at],
            device_id=peer,
            device_id_type=MESH,
        )

    def got(self, at, ref):
        pltpu.make_async_copy(ref, ref, self.recv.at[at]).wait()

    def add(self, out, left, right):
        f32 = jnp.float32
        out[...] = (left[...].astype(f32) + right[...].astype(f32)).astype(out.dtype)

    def hop(self, at):
        x, y, core = self.x, self.y, self.core
        o = self.o
        mine_a, mine_b = core * 8 + 2 * x + y, core * 8 + 4 + 2 * y + x
        pair_a, pair_b = pl.ds(core * 8 + 2 * x, 2), pl.ds(core * 8 + 4 + 2 * y, 2)
        all_mine = pl.ds(core * 8, 8)
        one = lambda at: pl.ds(at, 1)
        return [
            lambda: self.copy(0, self.u.at[pl.ds(8 - core * 8, 8)], self.rc, self.chip_peer),
            lambda: self.copy(1, self.s1.at[pl.ds(2 - 2 * x, 2)], self.ra, self.x_peer),
            lambda: self.copy(2, self.s1.at[pl.ds(6 - 2 * y, 2)], self.rb, self.y_peer),
            lambda: self.copy(3, self.sa.at[one(1 - y)], self.ta, self.y_peer),
            lambda: self.copy(4, self.sb.at[one(1 - x)], self.tb, self.x_peer),
            lambda: self.copy(5, o.at[one(mine_a)], o.at[one(mine_a)], self.y_peer),
            lambda: self.copy(6, o.at[one(mine_b)], o.at[one(mine_b)], self.x_peer),
            lambda: self.copy(7, o.at[pair_a], o.at[pair_a], self.x_peer),
            lambda: self.copy(8, o.at[pair_b], o.at[pair_b], self.y_peer),
            lambda: self.copy(9, o.at[all_mine], o.at[all_mine], self.chip_peer),
        ][at]()

    def begin(self):
        self.hop(0).start()

    def first(self):
        self.got(0, self.rc)
        self.add(self.s1, self.u.at[pl.ds(self.core * 8, 8)], self.rc)
        self.hop(1).start()
        self.hop(2).start()

    def second(self):
        self.got(1, self.ra)
        self.add(self.sa, self.s1.at[pl.ds(2 * self.x, 2)], self.ra)
        self.hop(3).start()
        self.got(2, self.rb)
        self.add(self.sb, self.s1.at[pl.ds(4 + 2 * self.y, 2)], self.rb)
        self.hop(4).start()

    def third(self, out_a, out_b):
        self.got(3, self.ta)
        self.add(out_a, self.sa.at[pl.ds(self.y, 1)], self.ta)
        self.got(4, self.tb)
        self.add(out_b, self.sb.at[pl.ds(self.x, 1)], self.tb)

    def own(self):
        return (
            self.o.at[pl.ds(self.core * 8 + 2 * self.x + self.y, 1)],
            self.o.at[pl.ds(self.core * 8 + 4 + 2 * self.y + self.x, 1)],
        )

    def spread1(self):
        self.hop(5).start()
        self.hop(6).start()

    def spread2(self):
        x, y, core = self.x, self.y, self.core
        self.got(5, self.o.at[pl.ds(core * 8 + 2 * x + 1 - y, 1)])
        self.hop(7).start()
        self.got(6, self.o.at[pl.ds(core * 8 + 4 + 2 * y + 1 - x, 1)])
        self.hop(8).start()

    def spread3(self):
        x, y, core = self.x, self.y, self.core
        self.got(7, self.o.at[pl.ds(core * 8 + 2 - 2 * x, 2)])
        self.got(8, self.o.at[pl.ds(core * 8 + 6 - 2 * y, 2)])
        self.hop(9).start()

    def finish(self, which=range(10)):
        if 9 in which:
            self.got(9, self.o.at[pl.ds(8 - self.core * 8, 8)])
        for at in which:
            self.hop(at).wait_send()


def line_greet(bar, me, n):
    @pl.when(me > 0)
    def _():
        pl.semaphore_signal(bar, inc=1, device_id={"tensor": me - 1}, device_id_type=MESH)

    @pl.when(me < n - 1)
    def _():
        pl.semaphore_signal(bar, inc=1, device_id={"tensor": me + 1}, device_id_type=MESH)

    return jnp.where(me > 0, 1, 0) + jnp.where(me < n - 1, 1, 0)


class LineScatter:
    def __init__(self, n, x, o, buf, tmp, send, recv):
        self.n, self.x, self.o, self.buf, self.tmp, self.send, self.recv = n, x, o, buf, tmp, send, recv
        self.me = lax.axis_index("tensor")

    @staticmethod
    def scratch(n, own, cols, dtype):
        return [
            pltpu.VMEM((2, n - 1, own, cols), dtype),
            pltpu.VMEM((2, n - 1, own, cols), dtype),
            DMA((2, n - 1)),
            DMA((2, n - 1)),
        ]

    def term(self, d, k):
        return self.n - 1 - k if d == 0 else k

    def sends(self, d, k):
        return self.me < self.n - 1 - k if d == 0 else self.me > k

    def behind(self, d):
        return self.me > 0 if d == 0 else self.me < self.n - 1

    def copy(self, d, k, first):
        return pltpu.make_async_remote_copy(
            src_ref=self.x.at[self.term(d, k)] if first else self.tmp.at[d, k],
            dst_ref=self.buf.at[d, k],
            send_sem=self.send.at[d, k],
            recv_sem=self.recv.at[d, k],
            device_id={"tensor": jnp.clip(self.me + 1 if d == 0 else self.me - 1, 0, self.n - 1)},
            device_id_type=MESH,
        )

    def landed(self, d, k):
        return pltpu.make_async_copy(self.buf.at[d, k], self.buf.at[d, k], self.recv.at[d, k])

    def begin(self):
        for d in range(2):

            @pl.when(jnp.logical_not(self.behind(d)))
            def _():
                for k in range(self.n - 1):
                    self.copy(d, k, True).start()

    def step(self, k):
        for d in range(2):

            @pl.when(self.behind(d) & self.sends(d, k))
            def _():
                self.landed(d, k).wait()
                at = self.term(d, k)
                both = self.buf[d, k].astype(jnp.float32) + self.x[at].astype(jnp.float32)
                self.tmp[d, k] = both.astype(self.tmp.dtype)
                self.copy(d, k, False).start()

    def end(self):
        self.o[...] = self.x[self.me].astype(jnp.float32)
        for d in range(2):
            for k in range(self.n - 1):

                @pl.when(self.behind(d) & (self.me == self.term(d, k)))
                def _():
                    self.landed(d, k).wait()
                    self.o[...] += self.buf[d, k].astype(jnp.float32)

        for d in range(2):
            for k in range(self.n - 1):

                @pl.when(self.sends(d, k))
                def _():
                    self.copy(d, k, False).wait_send()


def scatter_and_sum_kernel(n, count, x_ref, *rest):
    us, rest = rest[:count], rest[count:]
    o_ref, outs, rest = rest[0], rest[1 : 1 + count], rest[1 + count :]
    line = LineScatter(n, x_ref, o_ref, *rest[:4])
    rest = rest[4:]
    sums = [
        PlaneSum(us[i], outs[i], rest[10 * i : 10 * i + 8], rest[10 * i + 8], rest[10 * i + 9])
        for i in range(count)
    ]
    bar = pltpu.get_barrier_semaphore()
    met = line_greet(bar, line.me, n) + PlaneSum.greet(bar)
    pl.semaphore_wait(bar, met)
    line.begin()
    for item in sums:
        item.begin()
    for item in sums:
        item.first()
    line.step(0)
    for item in sums:
        item.second()
    for k in range(1, n - 1):
        line.step(k)
    for item in sums:
        item.third(*item.own())
        item.spread1()
    for item in sums:
        item.spread2()
    line.end()
    for item in sums:
        item.spread3()
    for item in sums:
        item.finish()


def scatter_and_sum(x, units, n, collective_id):
    rows, cols = x.shape
    own = rows // n
    result = pl.pallas_call(
        functools.partial(scatter_and_sum_kernel, n, len(units)),
        out_shape=(jax.ShapeDtypeStruct((own, cols), jnp.float32),)
        + tuple(jax.ShapeDtypeStruct(unit.shape, unit.dtype) for unit in units),
        in_specs=[VM] * (1 + len(units)),
        out_specs=(VM,) * (1 + len(units)),
        scratch_shapes=LineScatter.scratch(n, own, cols, x.dtype)
        + [item for unit in units for item in PlaneSum.scratch(unit.shape, unit.dtype)],
        compiler_params=remote_params(collective_id),
    )(x.reshape(n, own, cols), *units)
    return result[0], result[1:]


def rows_back_sum_kernel(nc, nt, heads, x_ref, u_ref, o_ref, a_ref, send, recv, loc, za, zb, pa, pb, zsend, zrecv, *rest):
    total = nc * nt
    my_ctx, my_ten = lax.axis_index("context"), lax.axis_index("tensor")
    me = my_ctx * nt + my_ten
    bar = pltpu.get_barrier_semaphore()
    for shift in range(1, total):
        other = lax.rem(me + shift, total)
        pl.semaphore_signal(bar, inc=1, device_id=spread(other, AXES, (nc, nt)), device_id_type=MESH)
    x = lax.axis_index("dp")
    pl.semaphore_signal(bar, inc=1, device_id={"dp": 1 - x}, device_id_type=MESH)
    pl.semaphore_wait(bar, total)

    unit = PlaneSum(u_ref, a_ref, rest[:8], rest[8], rest[9])

    def copy(shift):
        other = lax.rem(me + shift, total)
        ctx, ten = lax.div(other, nt), lax.rem(other, nt)
        return ctx < heads, pltpu.make_async_remote_copy(
            src_ref=x_ref.at[ten * heads + jnp.minimum(ctx, heads - 1)],
            dst_ref=o_ref.at[me],
            send_sem=send.at[shift],
            recv_sem=recv.at[shift],
            device_id={"context": ctx, "tensor": ten},
            device_id_type=MESH,
        )

    for shift in range(1, total):
        goes, item = copy(shift)

        @pl.when(goes)
        def _():
            item.start()

    unit.begin()
    own = pltpu.make_async_copy(
        x_ref.at[my_ten * heads + jnp.minimum(my_ctx, heads - 1)], o_ref.at[me], loc
    )
    own.start()
    own.wait()
    unit.first()
    unit.second()
    unit.third(pa, pb)

    def across(half, shift):
        other = lax.rem(my_ten + shift, nt)
        part, land = ((pa, za), (pb, zb))[half]
        return pltpu.make_async_remote_copy(
            src_ref=part.at[0, other],
            dst_ref=land.at[my_ten],
            send_sem=zsend.at[half, shift],
            recv_sem=zrecv.at[half, shift],
            device_id={"tensor": other},
            device_id_type=MESH,
        )

    for half in range(2):
        for shift in range(1, nt):
            across(half, shift).start()
    for half, (part, land, done) in enumerate(zip((pa, pb), (za, zb), unit.own())):
        land[my_ten] = part[0, my_ten]
        for shift in range(1, nt):
            source = lax.rem(my_ten + nt - shift, nt)
            pltpu.make_async_copy(land.at[source], land.at[source], zrecv.at[half, shift]).wait()
        value = land[0].astype(jnp.float32)
        for at in range(1, nt):
            value = value + land[at].astype(jnp.float32)
        done[0] = value.astype(done.dtype)
    unit.spread1()
    unit.spread2()

    @pl.when(my_ctx < heads)
    def _():
        for shift in range(1, total):
            source = lax.rem(me + total - shift, total)
            pltpu.make_async_copy(o_ref.at[source], o_ref.at[source], recv.at[shift]).wait()

    unit.spread3()
    unit.finish()
    for half in range(2):
        for shift in range(1, nt):
            across(half, shift).wait_send()
    for shift in range(1, total):
        goes, item = copy(shift)

        @pl.when(goes)
        def _():
            item.wait_send()


def rows_back_sum(x, unit, nc, nt, heads, collective_id):
    total = nc * nt
    piece = unit.shape[2:]
    low = unit.dtype
    return pl.pallas_call(
        functools.partial(rows_back_sum_kernel, nc, nt, heads),
        out_shape=(
            jax.ShapeDtypeStruct((total,) + x.shape[1:], x.dtype),
            jax.ShapeDtypeStruct((16,) + piece, low),
        ),
        in_specs=[VM, VM],
        out_specs=(VM, VM),
        scratch_shapes=[
            DMA((total,)),
            DMA((total,)),
            DMA,
            pltpu.VMEM((nt,) + piece, low),
            pltpu.VMEM((nt,) + piece, low),
            pltpu.VMEM((1, nt) + piece, low),
            pltpu.VMEM((1, nt) + piece, low),
            DMA((2, nt)),
            DMA((2, nt)),
        ]
        + PlaneSum.scratch(unit.shape, low),
        compiler_params=remote_params(collective_id),
    )(x, unit)


class LineGather:
    def __init__(self, n, x, o, send, recv):
        self.n, self.x, self.o, self.send, self.recv = n, x, o, send, recv
        self.me = lax.axis_index("tensor")

    def copy(self, d, s):
        me, n = self.me, self.n
        shard = jnp.clip(me - s if d == 0 else me + s, 0, n - 1)
        return pltpu.make_async_remote_copy(
            src_ref=self.x if s == 0 else self.o.at[shard],
            dst_ref=self.o.at[shard],
            send_sem=self.send.at[d, s],
            recv_sem=self.recv.at[d, s],
            device_id={"tensor": jnp.clip(me + 1 if d == 0 else me - 1, 0, n - 1)},
            device_id_type=MESH,
        )

    def sends(self, d, s):
        me, n = self.me, self.n
        return (me - s >= 0) & (me < n - 1) if d == 0 else (me + s < n) & (me > 0)

    def wait(self, d, s):
        me, n = self.me, self.n

        @pl.when(me - 1 - s >= 0 if d == 0 else me + 1 + s < n)
        def _():
            shard = jnp.clip(me - 1 - s if d == 0 else me + 1 + s, 0, n - 1)
            pltpu.make_async_copy(self.o.at[shard], self.o.at[shard], self.recv.at[d, s]).wait()

    def step(self, s):
        for d in range(2):
            if s > 0:
                self.wait(d, s - 1)

            @pl.when(self.sends(d, s))
            def _():
                self.copy(d, s).start()

    def last(self):
        for d in range(2):
            self.wait(d, self.n - 2)

    def finish(self):
        for d in range(2):
            for s in range(self.n - 1):

                @pl.when(self.sends(d, s))
                def _():
                    self.copy(d, s).wait_send()


def gather_pieces_kernel(n, x_ref, w_ref, o_ref, f_ref, held, s1, r1, s2, r2, s3, r3, loc):
    me, ctx, x = lax.axis_index("tensor"), lax.axis_index("context"), lax.axis_index("dp")
    place = ctx * 2 + x
    bar = pltpu.get_barrier_semaphore()
    met = line_greet(bar, me, n)
    for shift in range(1, 8):
        other = lax.rem(place + shift, 8)
        pl.semaphore_signal(
            bar, inc=1, device_id={"context": lax.div(other, 2), "dp": lax.rem(other, 2)}, device_id_type=MESH
        )
    pl.semaphore_wait(bar, met + 7)
    small = LineGather(n, w_ref, held, s1, r1)
    large = LineGather(n, x_ref, o_ref, s2, r2)
    small.step(0)
    large.step(0)
    own = pltpu.make_async_copy(x_ref, o_ref.at[me], loc.at[0])
    own.start()
    piece = pltpu.make_async_copy(w_ref, held.at[me], loc.at[1])
    piece.start()
    piece.wait()
    for s in range(1, n - 1):
        small.step(s)
    small.last()

    def there(at):
        ctx_, x_ = lax.div(at, 2), lax.rem(at, 2)
        rows = pl.ds(pl.multiple_of((lax.div(ctx_, 2) * 2 + x_) * w_ref.shape[0], 16), w_ref.shape[0])
        cols = pl.ds(pl.multiple_of(lax.rem(ctx_, 2) * w_ref.shape[1], 128), w_ref.shape[1])
        return f_ref.at[:, rows, cols]

    def push(shift):
        other = lax.rem(place + shift, 8)
        return pltpu.make_async_remote_copy(
            src_ref=held,
            dst_ref=there(place),
            send_sem=s3.at[shift],
            recv_sem=r3.at[shift],
            device_id={"context": lax.div(other, 2), "dp": lax.rem(other, 2)},
            device_id_type=MESH,
        )

    for shift in range(1, 8):
        push(shift).start()
    kept = pltpu.make_async_copy(held, there(place), loc.at[2])
    kept.start()
    for s in range(1, n - 1):
        large.step(s)
    large.last()
    for shift in range(1, 8):
        source = there(lax.rem(place + 8 - shift, 8))
        pltpu.make_async_copy(source, source, r3.at[shift]).wait()
    kept.wait()
    own.wait()
    small.finish()
    large.finish()
    for shift in range(1, 8):
        push(shift).wait_send()


def gather_pieces(x, w, n, collective_id):
    rows, cols = x.shape
    wide, deep = w.shape
    ctx, dp = lax.axis_index("context"), lax.axis_index("dp")
    piece = lax.dynamic_slice(
        w,
        ((lax.div(ctx, 2) * 2 + dp) * (wide // 4), lax.rem(ctx, 2) * (deep // 2)),
        (wide // 4, deep // 2),
    )
    full, weight = pl.pallas_call(
        functools.partial(gather_pieces_kernel, n),
        out_shape=(
            jax.ShapeDtypeStruct((n, rows, cols), x.dtype),
            jax.ShapeDtypeStruct((n, wide, deep), w.dtype),
        ),
        in_specs=[VM, VM],
        out_specs=(VM, VM),
        scratch_shapes=[pltpu.VMEM((n,) + piece.shape, w.dtype)]
        + [DMA((2, n - 1)) for _ in range(4)]
        + [DMA((8,)), DMA((8,)), DMA((3,))],
        compiler_params=remote_params(collective_id),
    )(x, piece)
    return full.reshape(n * rows, cols), weight.reshape(n * wide, deep)


def dot(left, right, dims):
    return lax.dot_general(left, right, ((dims[0], dims[1]), ((), ())), preferred_element_type=jnp.float32)


def key_positions(first, keys, queries):
    return first + lax.broadcasted_iota(jnp.int32, (keys, queries), 0)


def load_rows(qkv_ref, rows, nb, half, qs, kt, ks, vs):
    for block in range(nb):
        part = slice(block % 2 * half, block % 2 * half + half)
        item = qkv_ref[block // 2, :, part]
        qs[block] = item[:HEAD_DIM] * jnp.asarray(HEAD_DIM**-0.5, item.dtype)
        if kt is not None:
            kt[block] = item[HEAD_DIM : 2 * HEAD_DIM]
        ks[block] = item[HEAD_DIM : 2 * HEAD_DIM].T
        if vs is not None:
            vs[block] = item[2 * HEAD_DIM :].T


def forward_kernel(half, slot_ref, low_ref, on_ref, qkv_ref, start_ref, o_ref, full_ref, lse_ref, qs, ks):
    nb = full_ref.shape[0]

    @pl.when(on_ref[0] > 0)
    def _():
        load_rows(qkv_ref, None, nb, half, qs, None, ks, None)

        @pl.loop(0, nb)
        def _(nq):
            slot = slot_ref[nq]
            query = qs[slot]
            start = start_ref[nq]
            here = nq * half + lax.broadcasted_iota(jnp.int32, (1, half), 1)

            def step(nk, state):
                top, total, acc = state
                at = slot_ref[nk]
                score = dot(ks[at], query, ((1,), (0,)))
                place = key_positions(nk * half, half, half)
                score = jnp.where((place >= start) & (place <= here), score, NEG_FILL)
                new_top = jnp.maximum(top, jnp.max(score, axis=0, keepdims=True))
                factor = jnp.exp(top - new_top)
                weight = jnp.exp(score - new_top)
                total = total * factor + jnp.sum(weight, axis=0, keepdims=True)
                value = qkv_ref[at // 2, 2 * HEAD_DIM :, pl.ds(pl.multiple_of(at % 2 * half, 128), half)]
                acc = acc * factor + dot(value, weight.astype(jnp.bfloat16), ((1,), (0,)))
                return new_top, total, acc

            top, total, acc = lax.fori_loop(
                low_ref[nq],
                nq + 1,
                step,
                (
                    jnp.full((1, half), NEG_FILL, jnp.float32),
                    jnp.zeros((1, half), jnp.float32),
                    jnp.zeros((HEAD_DIM, half), jnp.float32),
                ),
            )
            result = acc / total
            full_ref[slot] = result
            lse_ref[slot] = top + jnp.log(total)
            low = result.astype(jnp.bfloat16)
            o_ref[2 * slot] = low[:, : half // 2]
            o_ref[2 * slot + 1] = low[:, half // 2 :]


def attend_forward(qkv, tables, half):
    nc = qkv.shape[0]
    nb = 2 * nc
    return pl.pallas_call(
        functools.partial(forward_kernel, half),
        out_shape=(
            jax.ShapeDtypeStruct((2 * nb, HEAD_DIM, half // 2), jnp.bfloat16),
            jax.ShapeDtypeStruct((nb, HEAD_DIM, half), jnp.float32),
            jax.ShapeDtypeStruct((nb, 1, half), jnp.float32),
        ),
        in_specs=[SM, SM, SM, VM, VM],
        out_specs=(VM, VM, VM),
        scratch_shapes=[
            pltpu.VMEM((nb, HEAD_DIM, half), jnp.bfloat16),
            pltpu.VMEM((nb, half, HEAD_DIM), jnp.bfloat16),
        ],
        compiler_params=pltpu.CompilerParams(vmem_limit_bytes=48 << 20),
    )(tables["slot"], tables["low"], tables["on"], qkv, tables["start"])


def backward_kernel(
    half, slot_ref, high_ref, on_ref, qkv_ref, start_ref, full_ref, lse_ref, grad_ref, o_ref, qs, kt, ks, vs, gs, ds, dq
):
    nb = full_ref.shape[0]

    @pl.when(on_ref[0] > 0)
    def _():
        load_rows(qkv_ref, None, nb, half, qs, kt, ks, vs)
        for block in range(nb):
            both = jnp.concatenate([grad_ref[2 * block], grad_ref[2 * block + 1]], axis=1)
            gs[block] = both
            ds[block] = jnp.sum(both.astype(jnp.float32) * full_ref[block], axis=0, keepdims=True)
            dq[block] = jnp.zeros((HEAD_DIM, half), jnp.float32)

        @pl.loop(0, nb)
        def _(nk):
            at = slot_ref[nk]
            place = key_positions(nk * half, half, half)

            def step(nq, state):
                grad_key, grad_value = state
                slot = slot_ref[nq]
                query, grad = qs[slot], gs[slot]
                here = nq * half + lax.broadcasted_iota(jnp.int32, (1, half), 1)
                score = dot(ks[at], query, ((1,), (0,)))
                score = jnp.where((place >= start_ref[nq]) & (place <= here), score, NEG_FILL)
                weight = jnp.exp(score - lse_ref[slot])
                grad_weight = dot(vs[at], grad, ((1,), (0,)))
                grad_score = (weight * (grad_weight - ds[slot])).astype(jnp.bfloat16)
                grad_value = grad_value + dot(grad, weight.astype(jnp.bfloat16), ((1,), (1,)))
                grad_key = grad_key + dot(query, grad_score, ((1,), (1,)))
                dq[slot] += dot(kt[at], grad_score, ((1,), (0,)))
                return grad_key, grad_value

            zero = jnp.zeros((HEAD_DIM, half), jnp.float32)
            grad_key, grad_value = lax.fori_loop(nk, high_ref[nk], step, (zero, zero))
            columns = pl.ds(pl.multiple_of(at % 2 * half, 128), half)
            o_ref[at // 2, HEAD_DIM : 2 * HEAD_DIM, columns] = grad_key.astype(jnp.bfloat16)
            o_ref[at // 2, 2 * HEAD_DIM :, columns] = grad_value.astype(jnp.bfloat16)

        for block in range(nb):
            part = slice(block % 2 * half, block % 2 * half + half)
            o_ref[block // 2, :HEAD_DIM, part] = (dq[block] * HEAD_DIM**-0.5).astype(jnp.bfloat16)


def attend_backward(qkv, tables, full, lse, grad, half):
    nc = qkv.shape[0]
    nb = 2 * nc
    low = jnp.bfloat16
    return pl.pallas_call(
        functools.partial(backward_kernel, half),
        out_shape=jax.ShapeDtypeStruct(qkv.shape, low),
        in_specs=[SM, SM, SM, VM, VM, VM, VM, VM],
        out_specs=VM,
        scratch_shapes=[
            pltpu.VMEM((nb, HEAD_DIM, half), low),
            pltpu.VMEM((nb, HEAD_DIM, half), low),
            pltpu.VMEM((nb, half, HEAD_DIM), low),
            pltpu.VMEM((nb, half, HEAD_DIM), low),
            pltpu.VMEM((nb, HEAD_DIM, half), low),
            pltpu.VMEM((nb, 1, half), jnp.float32),
            pltpu.VMEM((nb, HEAD_DIM, half), jnp.float32),
        ],
        compiler_params=pltpu.CompilerParams(vmem_limit_bytes=48 << 20),
    )(tables["slot"], tables["high"], tables["on"], qkv, tables["start"], full, lse, grad)


def block_tables(segments, order, half, heads):
    nb = order.shape[0]
    counts = jnp.arange(nb, dtype=jnp.int32)
    slot = jnp.sum(jnp.where(order[None, :] == counts[:, None], counts[None, :], 0), axis=1)
    docs = jnp.arange(DOC_LIMIT, dtype=jnp.int32)
    before = jnp.sum((segments[None, :] < docs[:, None]).astype(jnp.int32), axis=1)
    start = jnp.sum(jnp.where(segments[None, :] == docs[:, None], before[:, None], 0), axis=0)
    blocks = segments.reshape(nb, half)
    first, last = blocks[:, 0], blocks[:, -1]
    low = jnp.sum((last[None, :] < first[:, None]).astype(jnp.int32), axis=1)
    high = jnp.sum((first[None, :] <= last[:, None]).astype(jnp.int32), axis=1)
    on = (lax.axis_index("context") < heads).astype(jnp.int32).reshape(1)
    return {"slot": slot, "low": low, "high": high, "on": on, "start": start.reshape(nb, 1, half)}


def norm_parts(values):
    centre = jnp.mean(values, axis=-1, keepdims=True)
    shifted = values - centre
    spread_ = jnp.mean(shifted * shifted, axis=-1, keepdims=True)
    scale = lax.rsqrt(spread_ + NORM_EPS)
    return shifted * scale, scale


def norm_backward(grad, normed, scale, gain):
    e = grad * gain
    mean_e = jnp.mean(e, axis=-1, keepdims=True)
    mean_en = jnp.mean(e * normed, axis=-1, keepdims=True)
    return (e - mean_e - normed * mean_en) * scale


def gelu_tanh(values):
    return jax.nn.gelu(values, approximate=True)


def cross_rows(left, right):
    return lax.dot_general(
        left, right, (((0,), (0,)), ((), ())), preferred_element_type=jnp.float32
    )


def after(value, done):
    return lax.optimization_barrier((value, done))[0]


def per_device(
    mesh_sizes,
    inputs,
    first_gain,
    first_shift,
    project_weight,
    project_bias,
    attend_weight,
    attend_bias,
    second_gain,
    second_shift,
    expand_weight,
    expand_bias,
    shrink_weight,
    shrink_bias,
    segments,
    block_order,
    cotangent,
):
    nt, nc = mesh_sizes["tensor"], mesh_sizes["context"]
    own_rows, width = inputs.shape[1], inputs.shape[2]
    local_width = project_weight.shape[2]
    heads = local_width // HEAD_DIM
    block_rows = own_rows * nt
    half = block_rows // 2
    low = jnp.bfloat16
    tables = block_tables(segments[0], block_order, half, heads)

    tokens_own = inputs[0].astype(jnp.float32)
    grad_out = cotangent[0]
    normed1, scale1 = norm_parts(tokens_own)
    hidden1 = (normed1 * first_gain + first_shift).astype(low)
    square = nc == 4 and mesh_sizes["dp"] == 2
    plane = ("context", "dp")
    if square:
        hidden1_full, attend_full = gather_pieces(hidden1, attend_weight, nt, 0)
    else:
        hidden1_full = gather_rows(hidden1, nt, 0)
        attend_full = lax.all_gather(attend_weight, "tensor", axis=0, tiled=True)
    grad_full = lax.all_gather(after(grad_out, hidden1_full), "tensor", axis=0, tiled=True)

    by_head = project_weight.reshape(3, width, heads, HEAD_DIM)
    bias = jnp.stack([project_bias[0], jnp.zeros_like(project_bias[0]), project_bias[1]])
    bias = bias.reshape(3, heads, HEAD_DIM).transpose(1, 0, 2).reshape(-1, 1)
    weight_rows = by_head.transpose(2, 0, 3, 1).reshape(3 * local_width, width)
    projected = dot(weight_rows, hidden1_full, ((1,), (1,))) + bias
    qkv = to_heads(projected.astype(low).reshape(heads, 3 * HEAD_DIM, block_rows), nc, 1)
    pieces, attended_full, lse = attend_forward(qkv, tables, half)
    attended = to_rows(pieces, nc, nt, heads, 2).reshape(width, own_rows)

    middle = tokens_own + cross_rows(attended, attend_full) + attend_bias
    normed2, scale2 = norm_parts(middle)
    hidden2 = (normed2 * second_gain + second_shift).astype(low)
    hidden2_full = gather_rows(hidden2, nt, 3)
    pre_act = jnp.dot(hidden2_full, expand_weight, preferred_element_type=jnp.float32) + expand_bias
    activ = gelu_tanh(pre_act).astype(low)
    grad_act = dot(grad_full, shrink_weight, ((1,), (1,)))
    grad_pre = jax.vjp(gelu_tanh, pre_act)[1](grad_act)[0].astype(low)
    grad_shrink = cross_rows(activ, grad_full).astype(low)
    grad_expand = cross_rows(hidden2_full, grad_pre).astype(low)
    grad_hidden2 = dot(grad_pre, expand_weight, ((1,), (1,))).astype(low)
    if square:
        units = [item.reshape((16, -1) + item.shape[1:]) for item in (grad_shrink, grad_expand)]
        grad_hidden2, units = scatter_and_sum(grad_hidden2, units, nt, 4)
        grad_shrink, grad_expand = (
            unit.reshape(item.shape) for unit, item in zip(units, (grad_shrink, grad_expand))
        )
    else:
        grad_hidden2 = scatter_rows(grad_hidden2, nt, 4)
        grad_shrink, grad_expand = lax.psum((grad_shrink, grad_expand), plane)
    grad_expand_bias = jnp.sum(grad_pre.astype(jnp.float32), axis=0)
    grad_shrink_bias = jnp.sum(grad_out.astype(jnp.float32), axis=0)
    feed = jnp.dot(activ, shrink_weight, preferred_element_type=jnp.float32).astype(low)

    grad_second_gain = jnp.sum(grad_hidden2 * normed2, axis=0)
    grad_second_shift = jnp.sum(grad_hidden2, axis=0)
    grad_middle = grad_out.astype(jnp.float32) + norm_backward(
        grad_hidden2, normed2, scale2, second_gain
    )
    grad_middle_low = grad_middle.astype(low)
    grad_attend_bias = jnp.sum(grad_middle_low.astype(jnp.float32), axis=0)
    grad_attended = dot(attend_full, grad_middle_low, ((1,), (1,))).astype(low)
    grad_attend = jnp.dot(attended, grad_middle_low, preferred_element_type=jnp.float32).astype(low)
    grad_attended = grad_attended.reshape(nt * heads, HEAD_DIM, own_rows)
    if square:
        unit = grad_attend.reshape(nt, 16, -1, width).transpose(1, 0, 2, 3)
        grad_heads, grad_attend = rows_back_sum(grad_attended, unit, nc, nt, heads, 5)
        grad_attend = grad_attend.reshape(local_width, width)
    else:
        grad_heads = rows_back(grad_attended, nc, nt, heads, 5)
        grad_attend = lax.psum_scatter(grad_attend, "tensor", scatter_dimension=0, tiled=True)
        grad_attend = lax.psum(grad_attend, plane)

    feed_sum = lax.psum_scatter(after(feed, grad_heads), "tensor", scatter_dimension=0, tiled=True)

    grad_qkv = attend_backward(qkv, tables, attended_full, lse, grad_heads, half)
    grad_rows = from_heads(grad_qkv, nc, heads, 6).reshape(3 * local_width, block_rows)
    grad_project = dot(hidden1_full, grad_rows, ((0,), (1,))).astype(low)
    grad_hidden1 = cross_rows(grad_rows, weight_rows).astype(low)
    if square:
        unit = grad_project.reshape(16, -1, 3 * local_width)
        grad_hidden1, (unit,) = scatter_and_sum(grad_hidden1, [unit], nt, 7)
        grad_project = unit.reshape(grad_project.shape)
    else:
        grad_hidden1 = scatter_rows(grad_hidden1, nt, 7)
        grad_project = lax.psum(grad_project, plane)
    feed_sum = after(feed_sum, grad_hidden1).astype(jnp.float32)
    outputs = (middle + feed_sum + shrink_bias).astype(low)[None]
    grad_project = (
        grad_project.reshape(width, heads, 3, HEAD_DIM).transpose(2, 0, 1, 3).reshape(3, width, local_width)
    )
    row_sums = jnp.sum(grad_rows.astype(jnp.float32), axis=1).reshape(heads, 3, HEAD_DIM)
    grad_project_bias = jnp.concatenate([row_sums[:, 0].reshape(-1), row_sums[:, 2].reshape(-1)])

    grad_first_gain = jnp.sum(grad_hidden1 * normed1, axis=0)
    grad_first_shift = jnp.sum(grad_hidden1, axis=0)
    grad_inputs = (grad_middle + norm_backward(grad_hidden1, normed1, scale1, first_gain)).astype(low)[None]

    spare = -grad_project_bias.shape[0] % width
    vectors = jnp.concatenate(
        [
            grad_first_gain,
            grad_first_shift,
            grad_attend_bias,
            grad_second_gain,
            grad_second_shift,
            grad_shrink_bias,
            grad_expand_bias,
            jnp.pad(grad_project_bias, (0, spare)),
        ]
    ).reshape(-1, width)
    summed = sum_vectors(vectors, 6, mesh_sizes, 8)
    tail = summed[6:].reshape(-1)
    wide = grad_expand_bias.shape[0]
    f32 = lambda value: value.astype(jnp.float32)
    return (
        outputs,
        grad_inputs,
        summed[0],
        summed[1],
        f32(grad_project),
        tail[wide : wide + 2 * local_width].reshape(2, local_width),
        f32(grad_attend),
        summed[2],
        summed[3],
        summed[4],
        f32(grad_expand),
        tail[:wide],
        f32(grad_shrink),
        summed[5],
    )


def solution(mesh):
    rows = P("dp", ("context", "tensor"), None)
    in_specs = (
        rows,
        P(),
        P(),
        P(None, None, "tensor"),
        P(None, "tensor"),
        P("tensor", None),
        P(),
        P(),
        P(),
        P(None, "tensor"),
        P("tensor"),
        P("tensor", None),
        P(),
        P("dp", None),
        P(),
        rows,
    )
    out_specs = (
        rows,
        rows,
        P(),
        P(),
        P(None, None, "tensor"),
        P(None, "tensor"),
        P("tensor", None),
        P(),
        P(),
        P(),
        P(None, "tensor"),
        P("tensor"),
        P("tensor", None),
        P(),
    )
    return jax.shard_map(
        functools.partial(per_device, dict(mesh.shape)),
        mesh=mesh,
        in_specs=in_specs,
        out_specs=out_specs,
        check_vma=False,
    )
```

```python
import functools

import jax
import jax.numpy as jnp
from jax import lax
from jax.experimental import pallas as pl
from jax.experimental.pallas import tpu as pltpu
from jax.sharding import PartitionSpec as P

HEAD_DIM = 64
NEG_FILL = -1e30
NORM_EPS = 1e-05
DOC_LIMIT = 16
MESH = pl.DeviceIdType.MESH
VM = pl.BlockSpec(memory_space=pltpu.VMEM)
SM = pl.BlockSpec(memory_space=pltpu.SMEM)
DMA = pltpu.SemaphoreType.DMA


def remote_params(collective_id):
    return pltpu.CompilerParams(
        collective_id=collective_id, has_side_effects=True, vmem_limit_bytes=48 << 20
    )


def line_barrier(me, n):
    bar = pltpu.get_barrier_semaphore()

    @pl.when(me > 0)
    def _():
        pl.semaphore_signal(bar, inc=1, device_id={"tensor": me - 1}, device_id_type=MESH)

    @pl.when(me < n - 1)
    def _():
        pl.semaphore_signal(bar, inc=1, device_id={"tensor": me + 1}, device_id_type=MESH)

    pl.semaphore_wait(bar, jnp.where(me > 0, 1, 0) + jnp.where(me < n - 1, 1, 0))


def gather_kernel(n, x_ref, o_ref, send, recv, loc):
    me = lax.axis_index("tensor")
    line_barrier(me, n)
    own = pltpu.make_async_copy(x_ref, o_ref.at[me], loc)
    own.start()

    def copy(d, s):
        shard = jnp.clip(me - s if d == 0 else me + s, 0, n - 1)
        return pltpu.make_async_remote_copy(
            src_ref=x_ref if s == 0 else o_ref.at[shard],
            dst_ref=o_ref.at[shard],
            send_sem=send.at[d, s],
            recv_sem=recv.at[d, s],
            device_id={"tensor": jnp.clip(me + 1 if d == 0 else me - 1, 0, n - 1)},
            device_id_type=MESH,
        )

    def sends(d, s):
        return (me - s >= 0) & (me < n - 1) if d == 0 else (me + s < n) & (me > 0)

    def gets(d, s):
        return me - 1 - s >= 0 if d == 0 else me + 1 + s < n

    def landed(d, s):
        shard = jnp.clip(me - 1 - s if d == 0 else me + 1 + s, 0, n - 1)
        return pltpu.make_async_copy(o_ref.at[shard], o_ref.at[shard], recv.at[d, s])

    for s in range(n - 1):
        for d in range(2):
            if s > 0:

                @pl.when(gets(d, s - 1))
                def _():
                    landed(d, s - 1).wait()

            @pl.when(sends(d, s))
            def _():
                copy(d, s).start()

    for d in range(2):

        @pl.when(gets(d, n - 2))
        def _():
            landed(d, n - 2).wait()

        for s in range(n - 1):

            @pl.when(sends(d, s))
            def _():
                copy(d, s).wait_send()

    own.wait()


def gather_rows(x, n, collective_id):
    rows, cols = x.shape
    return pl.pallas_call(
        functools.partial(gather_kernel, n),
        out_shape=jax.ShapeDtypeStruct((n, rows, cols), x.dtype),
        in_specs=[VM],
        out_specs=VM,
        scratch_shapes=[DMA((2, n - 1)), DMA((2, n - 1)), DMA],
        compiler_params=remote_params(collective_id),
    )(x).reshape(n * rows, cols)


def scatter_kernel(n, x_ref, o_ref, buf, tmp, send, recv):
    me = lax.axis_index("tensor")
    line_barrier(me, n)

    def term(d, k):
        return n - 1 - k if d == 0 else k

    def sends(d, k):
        return me < n - 1 - k if d == 0 else me > k

    def behind(d):
        return me > 0 if d == 0 else me < n - 1

    def copy(d, k, first):
        return pltpu.make_async_remote_copy(
            src_ref=x_ref.at[term(d, k)] if first else tmp.at[d, k],
            dst_ref=buf.at[d, k],
            send_sem=send.at[d, k],
            recv_sem=recv.at[d, k],
            device_id={"tensor": jnp.clip(me + 1 if d == 0 else me - 1, 0, n - 1)},
            device_id_type=MESH,
        )

    def landed(d, k):
        return pltpu.make_async_copy(buf.at[d, k], buf.at[d, k], recv.at[d, k])

    for d in range(2):

        @pl.when(jnp.logical_not(behind(d)))
        def _():
            for k in range(n - 1):
                copy(d, k, True).start()

    for k in range(n - 1):
        for d in range(2):

            @pl.when(behind(d) & sends(d, k))
            def _():
                landed(d, k).wait()
                both = buf[d, k].astype(jnp.float32) + x_ref[term(d, k)].astype(jnp.float32)
                tmp[d, k] = both.astype(tmp.dtype)
                copy(d, k, False).start()

    o_ref[...] = x_ref[me].astype(jnp.float32)
    for d in range(2):
        for k in range(n - 1):

            @pl.when(behind(d) & (me == term(d, k)))
            def _():
                landed(d, k).wait()
                o_ref[...] += buf[d, k].astype(jnp.float32)

    for d in range(2):
        for k in range(n - 1):

            @pl.when(sends(d, k))
            def _():
                copy(d, k, False).wait_send()


def scatter_rows(x, n, collective_id):
    rows, cols = x.shape
    own = rows // n
    return pl.pallas_call(
        functools.partial(scatter_kernel, n),
        out_shape=jax.ShapeDtypeStruct((own, cols), jnp.float32),
        in_specs=[VM],
        out_specs=VM,
        scratch_shapes=[
            pltpu.VMEM((2, n - 1, own, cols), x.dtype),
            pltpu.VMEM((2, n - 1, own, cols), x.dtype),
            DMA((2, n - 1)),
            DMA((2, n - 1)),
        ],
        compiler_params=remote_params(collective_id),
    )(x.reshape(n, own, cols))


def group_barrier(axes, sizes):
    mine = [lax.axis_index(name) for name in axes]
    place = sum_index(mine, sizes)
    total = 1
    for size in sizes:
        total *= size
    bar = pltpu.get_barrier_semaphore()
    for shift in range(1, total):
        other = lax.rem(place + shift, total)
        pl.semaphore_signal(bar, inc=1, device_id=spread(other, axes, sizes), device_id_type=MESH)
    pl.semaphore_wait(bar, total - 1)
    return place, total


def sum_index(mine, sizes):
    place = 0
    for at, size in zip(mine, sizes):
        place = place * size + at
    return place


def spread(place, axes, sizes):
    found = {}
    for name, size in reversed(tuple(zip(axes, sizes))):
        found[name] = lax.rem(place, size)
        place = lax.div(place, size)
    return found


def to_heads_kernel(nc, heads, x_ref, o_ref, send, recv, loc):
    me, _ = group_barrier(("context",), (nc,))

    def copy(shift):
        other = lax.rem(me + shift, nc)
        return other, pltpu.make_async_remote_copy(
            src_ref=x_ref.at[:, jnp.minimum(other, heads - 1)],
            dst_ref=o_ref.at[me],
            send_sem=send.at[shift],
            recv_sem=recv.at[shift],
            device_id={"context": other},
            device_id_type=MESH,
        )

    for shift in range(1, nc):
        other, item = copy(shift)

        @pl.when(other < heads)
        def _():
            item.start()

    own = pltpu.make_async_copy(x_ref.at[:, jnp.minimum(me, heads - 1)], o_ref.at[me], loc)
    own.start()
    own.wait()

    @pl.when(me < heads)
    def _():
        for shift in range(1, nc):
            source = lax.rem(me + nc - shift, nc)
            pltpu.make_async_copy(o_ref.at[source], o_ref.at[source], recv.at[shift]).wait()

    for shift in range(1, nc):
        other, item = copy(shift)

        @pl.when(other < heads)
        def _():
            item.wait_send()


def to_heads(x, nc, collective_id):
    heads = x.shape[1]
    return pl.pallas_call(
        functools.partial(to_heads_kernel, nc, heads),
        out_shape=jax.ShapeDtypeStruct((nc, x.shape[0]) + x.shape[2:], x.dtype),
        in_specs=[VM],
        out_specs=VM,
        scratch_shapes=[DMA((nc,)), DMA((nc,)), DMA],
        compiler_params=remote_params(collective_id),
    )(x)


def from_heads_kernel(nc, nt, heads, extra, x_ref, *rest):
    if extra:
        p_ref, o_ref, s_ref, send, recv, loc, land, zsend, zrecv = rest
    else:
        o_ref, send, recv, loc = rest
    me, ten = lax.axis_index("context"), lax.axis_index("tensor")
    bar = pltpu.get_barrier_semaphore()
    for shift in range(1, nc):
        pl.semaphore_signal(bar, inc=1, device_id={"context": lax.rem(me + shift, nc)}, device_id_type=MESH)
    if extra:
        for shift in range(1, nt):
            pl.semaphore_signal(bar, inc=1, device_id={"tensor": lax.rem(ten + shift, nt)}, device_id_type=MESH)
    pl.semaphore_wait(bar, nc - 1 + (nt - 1 if extra else 0))

    def copy(shift):
        other = lax.rem(me + shift, nc)
        return pltpu.make_async_remote_copy(
            src_ref=x_ref.at[other],
            dst_ref=o_ref.at[:, jnp.minimum(me, heads - 1)],
            send_sem=send.at[shift],
            recv_sem=recv.at[shift],
            device_id={"context": other},
            device_id_type=MESH,
        )

    def across(shift):
        other = lax.rem(ten + shift, nt)
        return pltpu.make_async_remote_copy(
            src_ref=p_ref.at[lax.div(other, 2), lax.rem(other, 2)],
            dst_ref=land.at[ten],
            send_sem=zsend.at[shift],
            recv_sem=zrecv.at[shift],
            device_id={"tensor": other},
            device_id_type=MESH,
        )

    if extra:
        for shift in range(1, nt):
            across(shift).start()

    @pl.when(me < heads)
    def _():
        for shift in range(1, nc):
            copy(shift).start()
        own = pltpu.make_async_copy(x_ref.at[me], o_ref.at[:, me], loc)
        own.start()
        own.wait()

    if extra:
        land[ten] = p_ref[lax.div(ten, 2), lax.rem(ten, 2)]
        for shift in range(1, nt):
            source = lax.rem(ten + nt - shift, nt)
            pltpu.make_async_copy(land.at[source], land.at[source], zrecv.at[shift]).wait()
        value = land[0].astype(jnp.float32)
        for at in range(1, nt):
            value = value + land[at].astype(jnp.float32)
        s_ref[...] = value.astype(s_ref.dtype)
        for shift in range(1, nt):
            across(shift).wait_send()

    for shift in range(1, nc):
        source = lax.rem(me + nc - shift, nc)

        @pl.when(source < heads)
        def _():
            at = jnp.minimum(source, heads - 1)
            pltpu.make_async_copy(o_ref.at[:, at], o_ref.at[:, at], recv.at[shift]).wait()

    @pl.when(me < heads)
    def _():
        for shift in range(1, nc):
            copy(shift).wait_send()


def from_heads(x, pieces, nc, nt, heads, collective_id):
    extra = pieces is not None
    out = jax.ShapeDtypeStruct((x.shape[1], heads) + x.shape[2:], x.dtype)
    scratch = [DMA((nc,)), DMA((nc,)), DMA]
    if extra:
        piece = pieces.shape[2:]
        scratch += [pltpu.VMEM((nt,) + piece, pieces.dtype), DMA((nt,)), DMA((nt,))]
        out = (out, jax.ShapeDtypeStruct(piece, pieces.dtype))
    return pl.pallas_call(
        functools.partial(from_heads_kernel, nc, nt, heads, extra),
        out_shape=out,
        in_specs=[VM] * (1 + extra),
        out_specs=(VM, VM) if extra else VM,
        scratch_shapes=scratch,
        compiler_params=remote_params(collective_id),
    )(*((x, pieces) if extra else (x,)))


AXES = ("context", "tensor")


def rows_kernel(nc, nt, heads, x_ref, o_ref, send, recv, loc):
    me, total = group_barrier(AXES, (nc, nt))
    my_ctx, my_ten = lax.axis_index("context"), lax.axis_index("tensor")
    my_head = my_ten * heads + jnp.minimum(my_ctx, heads - 1)

    def copy(shift):
        other = lax.rem(me + shift, total)
        return pltpu.make_async_remote_copy(
            src_ref=x_ref.at[other],
            dst_ref=o_ref.at[my_head],
            send_sem=send.at[shift],
            recv_sem=recv.at[shift],
            device_id=spread(other, AXES, (nc, nt)),
            device_id_type=MESH,
        )

    @pl.when(my_ctx < heads)
    def _():
        for shift in range(1, total):
            copy(shift).start()
        own = pltpu.make_async_copy(x_ref.at[me], o_ref.at[my_head], loc)
        own.start()
        own.wait()

    for shift in range(1, total):
        source = lax.rem(me + total - shift, total)
        ctx, ten = lax.div(source, nt), lax.rem(source, nt)

        @pl.when(ctx < heads)
        def _():
            at = ten * heads + jnp.minimum(ctx, heads - 1)
            pltpu.make_async_copy(o_ref.at[at], o_ref.at[at], recv.at[shift]).wait()

    @pl.when(my_ctx < heads)
    def _():
        for shift in range(1, total):
            copy(shift).wait_send()


def to_rows(x, nc, nt, heads, collective_id):
    total = nc * nt
    return pl.pallas_call(
        functools.partial(rows_kernel, nc, nt, heads),
        out_shape=jax.ShapeDtypeStruct((nt * heads,) + x.shape[1:], x.dtype),
        in_specs=[VM],
        out_specs=VM,
        scratch_shapes=[DMA((total,)), DMA((total,)), DMA],
        compiler_params=remote_params(collective_id),
    )(x)


def rows_back_kernel(nc, nt, heads, x_ref, o_ref, send, recv, loc):
    me, total = group_barrier(AXES, (nc, nt))
    my_ctx, my_ten = lax.axis_index("context"), lax.axis_index("tensor")

    def copy(shift):
        other = lax.rem(me + shift, total)
        ctx, ten = lax.div(other, nt), lax.rem(other, nt)
        return ctx < heads, pltpu.make_async_remote_copy(
            src_ref=x_ref.at[ten * heads + jnp.minimum(ctx, heads - 1)],
            dst_ref=o_ref.at[me],
            send_sem=send.at[shift],
            recv_sem=recv.at[shift],
            device_id={"context": ctx, "tensor": ten},
            device_id_type=MESH,
        )

    for shift in range(1, total):
        goes, item = copy(shift)

        @pl.when(goes)
        def _():
            item.start()

    own = pltpu.make_async_copy(
        x_ref.at[my_ten * heads + jnp.minimum(my_ctx, heads - 1)], o_ref.at[me], loc
    )
    own.start()
    own.wait()

    @pl.when(my_ctx < heads)
    def _():
        for shift in range(1, total):
            source = lax.rem(me + total - shift, total)
            pltpu.make_async_copy(o_ref.at[source], o_ref.at[source], recv.at[shift]).wait()

    for shift in range(1, total):
        goes, item = copy(shift)

        @pl.when(goes)
        def _():
            item.wait_send()


def rows_back(x, nc, nt, heads, collective_id):
    total = nc * nt
    return pl.pallas_call(
        functools.partial(rows_back_kernel, nc, nt, heads),
        out_shape=jax.ShapeDtypeStruct((total,) + x.shape[1:], x.dtype),
        in_specs=[VM],
        out_specs=VM,
        scratch_shapes=[DMA((total,)), DMA((total,)), DMA],
        compiler_params=remote_params(collective_id),
    )(x)


def vectors_kernel(names, sizes, shared, x_ref, o_ref, now, *rest):
    bufs, sems = rest[: len(names)], rest[len(names) :]
    bar = pltpu.get_barrier_semaphore()
    for name, size in zip(names, sizes):
        me = lax.axis_index(name)
        for shift in range(1, size):
            pl.semaphore_signal(
                bar, inc=1, device_id={name: lax.rem(me + shift, size)}, device_id_type=MESH
            )
    pl.semaphore_wait(bar, sum(sizes) - len(sizes))
    for stage, (name, size) in enumerate(zip(names, sizes)):
        buf, send, recv = bufs[stage], sems[2 * stage], sems[2 * stage + 1]
        me = lax.axis_index(name)

        def copy(shift):
            return pltpu.make_async_remote_copy(
                src_ref=now.at[stage] if stage else x_ref.at[0],
                dst_ref=buf.at[me],
                send_sem=send.at[shift],
                recv_sem=recv.at[shift],
                device_id={name: lax.rem(me + shift, size)},
                device_id_type=MESH,
            )

        for shift in range(1, size):
            copy(shift).start()
        buf[me] = now[stage] if stage else x_ref[0]
        for shift in range(1, size):
            source = lax.rem(me + size - shift, size)
            pltpu.make_async_copy(buf.at[source], buf.at[source], recv.at[shift]).wait()
        total = buf[0]
        for at in range(1, size):
            total = total + buf[at]
        if stage == 0:
            row = lax.broadcasted_iota(jnp.int32, total.shape, 0)
            total = jnp.where(row < shared, total, x_ref[0])
        if stage + 1 < len(names):
            now[stage + 1] = total
        else:
            o_ref[...] = total
        for shift in range(1, size):
            copy(shift).wait_send()


def sum_vectors(rows, shared, mesh_sizes, collective_id):
    names = ("tensor", "context", "dp")
    sizes = tuple(mesh_sizes[name] for name in names)
    shape = rows.shape
    return pl.pallas_call(
        functools.partial(vectors_kernel, names, sizes, shared),
        out_shape=jax.ShapeDtypeStruct(shape, jnp.float32),
        in_specs=[VM],
        out_specs=VM,
        scratch_shapes=[pltpu.VMEM((len(names),) + shape, jnp.float32)]
        + [pltpu.VMEM((size,) + shape, jnp.float32) for size in sizes]
        + [DMA((size,)) for size in sizes for _ in range(2)],
        compiler_params=remote_params(collective_id),
    )(rows[None])


class PlaneSum:
    def __init__(self, u, p, o, bufs=None, spread=None):
        self.u, self.p, self.o = u, p, o
        if bufs is not None:
            self.rc, self.s1, self.ra, self.rb, self.sa, self.sb, self.ta, self.tb = bufs[:8]
            self.send1, self.recv1 = bufs[8:]
        if spread is not None:
            self.send2, self.recv2, self.loc = spread
        ctx, self.x = lax.axis_index("context"), lax.axis_index("dp")
        self.core, self.y = lax.rem(ctx, 2), lax.div(ctx, 2)
        self.chip_peer = {"context": ctx + 1 - 2 * self.core}
        self.y_peer = {"context": lax.rem(ctx + 2, 4)}
        self.x_peer = {"dp": 1 - self.x}

    @staticmethod
    def reduce_scratch(shape, dtype):
        tail = tuple(shape[1:])
        bufs = [pltpu.VMEM((count,) + tail, dtype) for count in (8, 8, 2, 2, 2, 2, 1, 1)]
        return bufs + [DMA((5,)), DMA((5,))]

    @staticmethod
    def spread_scratch():
        return [DMA((5,)), DMA((5,)), DMA((2,))]

    @staticmethod
    def greet(bar):
        ctx, x = lax.axis_index("context"), lax.axis_index("dp")
        for peer in (
            {"context": ctx + 1 - 2 * lax.rem(ctx, 2)},
            {"context": lax.rem(ctx + 2, 4)},
            {"dp": 1 - x},
        ):
            pl.semaphore_signal(bar, inc=1, device_id=peer, device_id_type=MESH)
        return 3

    def copy(self, at, src, dst, peer):
        send, recv = (self.send1, self.recv1) if at < 5 else (self.send2, self.recv2)
        return pltpu.make_async_remote_copy(
            src_ref=src,
            dst_ref=dst,
            send_sem=send.at[at % 5],
            recv_sem=recv.at[at % 5],
            device_id=peer,
            device_id_type=MESH,
        )

    def got(self, at, ref):
        recv = self.recv1 if at < 5 else self.recv2
        pltpu.make_async_copy(ref, ref, recv.at[at % 5]).wait()

    def add(self, out, left, right):
        f32 = jnp.float32
        out[...] = (left[...].astype(f32) + right[...].astype(f32)).astype(out.dtype)

    def mine(self, half):
        if half == 0:
            return pl.ds(self.core * 8 + 2 * self.x + self.y, 1)
        return pl.ds(self.core * 8 + 4 + 2 * self.y + self.x, 1)

    def hop(self, at):
        x, y, core = self.x, self.y, self.core
        u, o, p = self.u, self.o, self.p
        pair_a, pair_b = pl.ds(core * 8 + 2 * x, 2), pl.ds(core * 8 + 4 + 2 * y, 2)
        one = lambda at: pl.ds(at, 1)
        return [
            lambda: self.copy(0, u.at[pl.ds(8 - core * 8, 8)], self.rc, self.chip_peer),
            lambda: self.copy(1, self.s1.at[pl.ds(2 - 2 * x, 2)], self.ra, self.x_peer),
            lambda: self.copy(2, self.s1.at[pl.ds(6 - 2 * y, 2)], self.rb, self.y_peer),
            lambda: self.copy(3, self.sa.at[one(1 - y)], self.ta, self.y_peer),
            lambda: self.copy(4, self.sb.at[one(1 - x)], self.tb, self.x_peer),
            lambda: self.copy(5, p.at[one(0)], o.at[self.mine(0)], self.y_peer),
            lambda: self.copy(6, p.at[one(1)], o.at[self.mine(1)], self.x_peer),
            lambda: self.copy(7, o.at[pair_a], o.at[pair_a], self.x_peer),
            lambda: self.copy(8, o.at[pair_b], o.at[pair_b], self.y_peer),
            lambda: self.copy(9, o.at[pl.ds(core * 8, 8)], o.at[pl.ds(core * 8, 8)], self.chip_peer),
        ][at]()

    def begin(self):
        self.hop(0).start()

    def first(self):
        self.got(0, self.rc)
        self.add(self.s1, self.u.at[pl.ds(self.core * 8, 8)], self.rc)
        self.hop(1).start()
        self.hop(2).start()

    def second(self):
        self.got(1, self.ra)
        self.add(self.sa, self.s1.at[pl.ds(2 * self.x, 2)], self.ra)
        self.hop(3).start()
        self.got(2, self.rb)
        self.add(self.sb, self.s1.at[pl.ds(4 + 2 * self.y, 2)], self.rb)
        self.hop(4).start()

    def third(self):
        self.got(3, self.ta)
        self.add(self.p.at[pl.ds(0, 1)], self.sa.at[pl.ds(self.y, 1)], self.ta)
        self.got(4, self.tb)
        self.add(self.p.at[pl.ds(1, 1)], self.sb.at[pl.ds(self.x, 1)], self.tb)

    def reduced(self):
        for at in range(5):
            self.hop(at).wait_send()

    def kept(self, half):
        return pltpu.make_async_copy(self.p.at[pl.ds(half, 1)], self.o.at[self.mine(half)], self.loc.at[half])

    def spread1(self):
        self.hop(5).start()
        self.hop(6).start()
        self.kept(0).start()
        self.kept(1).start()

    def spread2(self):
        x, y, core = self.x, self.y, self.core
        self.kept(0).wait()
        self.got(5, self.o.at[pl.ds(core * 8 + 2 * x + 1 - y, 1)])
        self.hop(7).start()
        self.kept(1).wait()
        self.got(6, self.o.at[pl.ds(core * 8 + 4 + 2 * y + 1 - x, 1)])
        self.hop(8).start()

    def spread3(self):
        x, y, core = self.x, self.y, self.core
        self.got(7, self.o.at[pl.ds(core * 8 + 2 - 2 * x, 2)])
        self.got(8, self.o.at[pl.ds(core * 8 + 6 - 2 * y, 2)])
        self.hop(9).start()

    def everywhere(self):
        self.got(9, self.o.at[pl.ds(8 - self.core * 8, 8)])
        for at in range(5, 10):
            self.hop(at).wait_send()


def unit_pieces(unit):
    return jax.ShapeDtypeStruct((2,) + unit.shape[1:], unit.dtype)


def line_greet(bar, me, n):
    @pl.when(me > 0)
    def _():
        pl.semaphore_signal(bar, inc=1, device_id={"tensor": me - 1}, device_id_type=MESH)

    @pl.when(me < n - 1)
    def _():
        pl.semaphore_signal(bar, inc=1, device_id={"tensor": me + 1}, device_id_type=MESH)

    return jnp.where(me > 0, 1, 0) + jnp.where(me < n - 1, 1, 0)


class LineScatter:
    def __init__(self, n, x, o, buf, tmp, send, recv):
        self.n, self.x, self.o, self.buf, self.tmp, self.send, self.recv = n, x, o, buf, tmp, send, recv
        self.me = lax.axis_index("tensor")

    @staticmethod
    def scratch(n, own, cols, dtype):
        return [
            pltpu.VMEM((2, n - 1, own, cols), dtype),
            pltpu.VMEM((2, n - 1, own, cols), dtype),
            DMA((2, n - 1)),
            DMA((2, n - 1)),
        ]

    def term(self, d, k):
        return self.n - 1 - k if d == 0 else k

    def sends(self, d, k):
        return self.me < self.n - 1 - k if d == 0 else self.me > k

    def behind(self, d):
        return self.me > 0 if d == 0 else self.me < self.n - 1

    def copy(self, d, k, first):
        return pltpu.make_async_remote_copy(
            src_ref=self.x.at[self.term(d, k)] if first else self.tmp.at[d, k],
            dst_ref=self.buf.at[d, k],
            send_sem=self.send.at[d, k],
            recv_sem=self.recv.at[d, k],
            device_id={"tensor": jnp.clip(self.me + 1 if d == 0 else self.me - 1, 0, self.n - 1)},
            device_id_type=MESH,
        )

    def landed(self, d, k):
        return pltpu.make_async_copy(self.buf.at[d, k], self.buf.at[d, k], self.recv.at[d, k])

    def begin(self):
        for d in range(2):

            @pl.when(jnp.logical_not(self.behind(d)))
            def _():
                for k in range(self.n - 1):
                    self.copy(d, k, True).start()

    def step(self, k):
        for d in range(2):

            @pl.when(self.behind(d) & self.sends(d, k))
            def _():
                self.landed(d, k).wait()
                at = self.term(d, k)
                both = self.buf[d, k].astype(jnp.float32) + self.x[at].astype(jnp.float32)
                self.tmp[d, k] = both.astype(self.tmp.dtype)
                self.copy(d, k, False).start()

    def end(self):
        self.o[...] = self.x[self.me].astype(jnp.float32)
        for d in range(2):
            for k in range(self.n - 1):

                @pl.when(self.behind(d) & (self.me == self.term(d, k)))
                def _():
                    self.landed(d, k).wait()
                    self.o[...] += self.buf[d, k].astype(jnp.float32)

        for d in range(2):
            for k in range(self.n - 1):

                @pl.when(self.sends(d, k))
                def _():
                    self.copy(d, k, False).wait_send()


def scatter_reduce_kernel(n, count, x_ref, *rest):
    us, rest = rest[:count], rest[count:]
    o_ref, ps, rest = rest[0], rest[1 : 1 + count], rest[1 + count :]
    line = LineScatter(n, x_ref, o_ref, *rest[:4])
    rest = rest[4:]
    sums = [PlaneSum(us[i], ps[i], None, rest[10 * i : 10 * i + 10]) for i in range(count)]
    bar = pltpu.get_barrier_semaphore()
    met = line_greet(bar, line.me, n) + PlaneSum.greet(bar)
    pl.semaphore_wait(bar, met)
    line.begin()
    for item in sums:
        item.begin()
    for item in sums:
        item.first()
    line.step(0)
    for item in sums:
        item.second()
    for k in range(1, n - 1):
        line.step(k)
    for item in sums:
        item.third()
    line.end()
    for item in sums:
        item.reduced()


def scatter_reduce(x, units, n, collective_id):
    rows, cols = x.shape
    own = rows // n
    result = pl.pallas_call(
        functools.partial(scatter_reduce_kernel, n, len(units)),
        out_shape=(jax.ShapeDtypeStruct((own, cols), jnp.float32),) + tuple(unit_pieces(unit) for unit in units),
        in_specs=[VM] * (1 + len(units)),
        out_specs=(VM,) * (1 + len(units)),
        scratch_shapes=LineScatter.scratch(n, own, cols, x.dtype)
        + [item for unit in units for item in PlaneSum.reduce_scratch(unit.shape, unit.dtype)],
        compiler_params=remote_params(collective_id),
    )(x.reshape(n, own, cols), *units)
    return result[0], result[1:]


def last_kernel(n, shared, count, x_ref, u_ref, a_ref, *rest):
    ps, rest = rest[:count], rest[count:]
    token_ref, gain_ref, middle_ref, vec_ref, rest = rest[0], rest[1], rest[2], rest[3], rest[4:]
    g_ref, v_ref, po_ref, ao_ref, rest = rest[0], rest[1], rest[2], rest[3], rest[4:]
    outs, rest = rest[:count], rest[count:]
    sum_ref, piece, rest = rest[0], rest[1], rest[2:]
    line = LineScatter(n, x_ref, sum_ref, *rest[:4])
    project = PlaneSum(u_ref, piece, po_ref, rest[4:14], rest[14:17])
    rest = rest[17:]
    feeds = [PlaneSum(None, ps[i], outs[i], None, rest[3 * i : 3 * i + 3]) for i in range(count)]
    rest = rest[3 * count :]
    asend, arecv, aloc, now, rest = rest[0], rest[1], rest[2], rest[3], rest[4:]
    names, sizes = ("tensor", "context", "dp"), (n, 4, 2)
    bufs, sems = rest[:3], rest[3:]

    ten, ctx, x = (lax.axis_index(name) for name in names)
    place = ctx * 2 + x
    bar = pltpu.get_barrier_semaphore()
    for shift in range(1, n):
        pl.semaphore_signal(bar, inc=1, device_id={"tensor": lax.rem(ten + shift, n)}, device_id_type=MESH)
    for shift in range(1, 8):
        other = lax.rem(place + shift, 8)
        pl.semaphore_signal(
            bar, inc=1, device_id={"context": lax.div(other, 2), "dp": lax.rem(other, 2)}, device_id_type=MESH
        )
    pl.semaphore_wait(bar, n + 6)

    def there(at):
        ctx_, x_ = lax.div(at, 2), lax.rem(at, 2)
        y_ = lax.div(ctx_, 2)
        row = jnp.where(ten < n // 2, 2 * x_ + y_, 2 * y_ + x_)
        rows = pl.ds(pl.multiple_of(row * a_ref.shape[0], 16), a_ref.shape[0])
        cols = pl.ds(pl.multiple_of(lax.rem(ctx_, 2) * a_ref.shape[1], 128), a_ref.shape[1])
        return ao_ref.at[rows, cols]

    def push(shift):
        other = lax.rem(place + shift, 8)
        return pltpu.make_async_remote_copy(
            src_ref=a_ref,
            dst_ref=there(place),
            send_sem=asend.at[shift],
            recv_sem=arecv.at[shift],
            device_id={"context": lax.div(other, 2), "dp": lax.rem(other, 2)},
            device_id_type=MESH,
        )

    line.begin()
    project.begin()
    for item in feeds:
        item.spread1()
    for shift in range(1, 8):
        push(shift).start()
    kept = pltpu.make_async_copy(a_ref, there(place), aloc)
    kept.start()
    normed, scale = norm_parts(token_ref[...].astype(jnp.float32))
    project.first()
    line.step(0)
    for item in feeds:
        item.spread2()
    project.second()
    for k in range(1, n - 1):
        line.step(k)
    for item in feeds:
        item.spread3()
    project.third()
    project.spread1()
    line.end()
    grad = sum_ref[...]
    now[0] = vec_ref[...]
    now[0, 0:1] = jnp.sum(grad * normed, axis=0, keepdims=True)
    now[0, 1:2] = jnp.sum(grad, axis=0, keepdims=True)

    def stage_copy(stage, shift):
        name, size = names[stage], sizes[stage]
        me = lax.axis_index(name)
        return pltpu.make_async_remote_copy(
            src_ref=now.at[stage],
            dst_ref=bufs[stage].at[me],
            send_sem=sems[2 * stage].at[shift],
            recv_sem=sems[2 * stage + 1].at[shift],
            device_id={name: lax.rem(me + shift, size)},
            device_id_type=MESH,
        )

    def stage_start(stage):
        for shift in range(1, sizes[stage]):
            stage_copy(stage, shift).start()
        bufs[stage][lax.axis_index(names[stage])] = now[stage]

    def stage_end(stage):
        buf, size = bufs[stage], sizes[stage]
        me = lax.axis_index(names[stage])
        for shift in range(1, size):
            source = lax.rem(me + size - shift, size)
            pltpu.make_async_copy(buf.at[source], buf.at[source], sems[2 * stage + 1].at[shift]).wait()
        total = buf[0]
        for at in range(1, size):
            total = total + buf[at]
        if stage == 0:
            row = lax.broadcasted_iota(jnp.int32, total.shape, 0)
            total = jnp.where(row < shared, total, vec_ref[...])
        if stage < 2:
            now[stage + 1] = total
        else:
            v_ref[...] = total

    stage_start(0)
    back = norm_backward(grad, normed, scale, gain_ref[...])
    g_ref[...] = (middle_ref[...] + back).astype(g_ref.dtype)
    project.spread2()
    stage_end(0)
    stage_start(1)
    project.spread3()
    stage_end(1)
    stage_start(2)
    kept.wait()
    for shift in range(1, 8):
        source = there(lax.rem(place + 8 - shift, 8))
        pltpu.make_async_copy(source, source, arecv.at[shift]).wait()
    for item in feeds:
        item.everywhere()
    stage_end(2)
    project.everywhere()
    project.reduced()
    for shift in range(1, 8):
        push(shift).wait_send()
    for stage in range(3):
        for shift in range(1, sizes[stage]):
            stage_copy(stage, shift).wait_send()


def last_part(x, unit, attend_piece, pieces, tokens, gain, grad_middle, vectors, shared, n, collective_id):
    rows, cols = x.shape
    own = rows // n
    count = len(pieces)
    f32, low = jnp.float32, x.dtype
    whole = lambda item: jax.ShapeDtypeStruct((16,) + item.shape[1:], item.dtype)
    wide, deep = attend_piece.shape
    result = pl.pallas_call(
        functools.partial(last_kernel, n, shared, count),
        out_shape=(
            jax.ShapeDtypeStruct((own, cols), low),
            jax.ShapeDtypeStruct(vectors.shape, f32),
            whole(unit),
            jax.ShapeDtypeStruct((4 * wide, 2 * deep), low),
        )
        + tuple(whole(item) for item in pieces),
        in_specs=[VM] * (7 + count),
        out_specs=(VM,) * (4 + count),
        scratch_shapes=[pltpu.VMEM((own, cols), f32), pltpu.VMEM((2,) + unit.shape[1:], low)]
        + LineScatter.scratch(n, own, cols, low)
        + PlaneSum.reduce_scratch(unit.shape, low)
        + PlaneSum.spread_scratch()
        + [item for _ in pieces for item in PlaneSum.spread_scratch()]
        + [DMA((8,)), DMA((8,)), DMA, pltpu.VMEM((3,) + vectors.shape, f32)]
        + [pltpu.VMEM((size,) + vectors.shape, f32) for size in (n, 4, 2)]
        + [DMA((size,)) for size in (n, 4, 2) for _ in range(2)],
        compiler_params=remote_params(collective_id),
    )(x.reshape(n, own, cols), unit, attend_piece, *pieces, tokens, gain, grad_middle, vectors)
    return result[0], result[1], result[2], result[3], result[4:]


def rows_back_sum_kernel(nc, nt, heads, x_ref, u_ref, o_ref, p_ref, send, recv, loc, *rest):
    total = nc * nt
    my_ctx, my_ten = lax.axis_index("context"), lax.axis_index("tensor")
    me = my_ctx * nt + my_ten
    bar = pltpu.get_barrier_semaphore()
    for shift in range(1, total):
        other = lax.rem(me + shift, total)
        pl.semaphore_signal(bar, inc=1, device_id=spread(other, AXES, (nc, nt)), device_id_type=MESH)
    x = lax.axis_index("dp")
    pl.semaphore_signal(bar, inc=1, device_id={"dp": 1 - x}, device_id_type=MESH)
    pl.semaphore_wait(bar, total)

    unit = PlaneSum(u_ref, p_ref, None, rest)

    def copy(shift):
        other = lax.rem(me + shift, total)
        ctx, ten = lax.div(other, nt), lax.rem(other, nt)
        return ctx < heads, pltpu.make_async_remote_copy(
            src_ref=x_ref.at[ten * heads + jnp.minimum(ctx, heads - 1)],
            dst_ref=o_ref.at[me],
            send_sem=send.at[shift],
            recv_sem=recv.at[shift],
            device_id={"context": ctx, "tensor": ten},
            device_id_type=MESH,
        )

    for shift in range(1, total):
        goes, item = copy(shift)

        @pl.when(goes)
        def _():
            item.start()

    unit.begin()
    own = pltpu.make_async_copy(
        x_ref.at[my_ten * heads + jnp.minimum(my_ctx, heads - 1)], o_ref.at[me], loc
    )
    own.start()
    own.wait()
    unit.first()
    unit.second()
    unit.third()

    @pl.when(my_ctx < heads)
    def _():
        for shift in range(1, total):
            source = lax.rem(me + total - shift, total)
            pltpu.make_async_copy(o_ref.at[source], o_ref.at[source], recv.at[shift]).wait()

    unit.reduced()
    for shift in range(1, total):
        goes, item = copy(shift)

        @pl.when(goes)
        def _():
            item.wait_send()


def rows_back_sum(x, unit, nc, nt, heads, collective_id):
    total = nc * nt
    return pl.pallas_call(
        functools.partial(rows_back_sum_kernel, nc, nt, heads),
        out_shape=(jax.ShapeDtypeStruct((total,) + x.shape[1:], x.dtype), unit_pieces(unit)),
        in_specs=[VM, VM],
        out_specs=(VM, VM),
        scratch_shapes=[DMA((total,)), DMA((total,)), DMA] + PlaneSum.reduce_scratch(unit.shape, unit.dtype),
        compiler_params=remote_params(collective_id),
    )(x, unit)


class LineGather:
    def __init__(self, n, x, o, send, recv):
        self.n, self.x, self.o, self.send, self.recv = n, x, o, send, recv
        self.me = lax.axis_index("tensor")

    def copy(self, d, s):
        me, n = self.me, self.n
        shard = jnp.clip(me - s if d == 0 else me + s, 0, n - 1)
        return pltpu.make_async_remote_copy(
            src_ref=self.x if s == 0 else self.o.at[shard],
            dst_ref=self.o.at[shard],
            send_sem=self.send.at[d, s],
            recv_sem=self.recv.at[d, s],
            device_id={"tensor": jnp.clip(me + 1 if d == 0 else me - 1, 0, n - 1)},
            device_id_type=MESH,
        )

    def sends(self, d, s):
        me, n = self.me, self.n
        return (me - s >= 0) & (me < n - 1) if d == 0 else (me + s < n) & (me > 0)

    def wait(self, d, s):
        me, n = self.me, self.n

        @pl.when(me - 1 - s >= 0 if d == 0 else me + 1 + s < n)
        def _():
            shard = jnp.clip(me - 1 - s if d == 0 else me + 1 + s, 0, n - 1)
            pltpu.make_async_copy(self.o.at[shard], self.o.at[shard], self.recv.at[d, s]).wait()

    def step(self, s):
        for d in range(2):
            if s > 0:
                self.wait(d, s - 1)

            @pl.when(self.sends(d, s))
            def _():
                self.copy(d, s).start()

    def last(self):
        for d in range(2):
            self.wait(d, self.n - 2)

    def finish(self):
        for d in range(2):
            for s in range(self.n - 1):

                @pl.when(self.sends(d, s))
                def _():
                    self.copy(d, s).wait_send()


def gather_pieces_kernel(n, t_ref, gain_ref, shift_ref, full_ref, o_ref, f_ref, x_ref, held, s1, r1, s2, r2, s3, r3, loc):
    me, ctx, x = lax.axis_index("tensor"), lax.axis_index("context"), lax.axis_index("dp")
    place = ctx * 2 + x
    bar = pltpu.get_barrier_semaphore()
    met = line_greet(bar, me, n)
    for shift in range(1, 8):
        other = lax.rem(place + shift, 8)
        pl.semaphore_signal(
            bar, inc=1, device_id={"context": lax.div(other, 2), "dp": lax.rem(other, 2)}, device_id_type=MESH
        )
    normed, _ = norm_parts(t_ref[...].astype(jnp.float32))
    x_ref[...] = (normed * gain_ref[...] + shift_ref[...]).astype(x_ref.dtype)
    pl.semaphore_wait(bar, met + 7)
    tall, deep = held.shape[1:]
    w_ref = full_ref.at[
        pl.ds(pl.multiple_of((lax.div(ctx, 2) * 2 + x) * tall, 16), tall),
        pl.ds(pl.multiple_of(lax.rem(ctx, 2) * deep, 128), deep),
    ]
    small = LineGather(n, w_ref, held, s1, r1)
    large = LineGather(n, x_ref, o_ref, s2, r2)
    small.step(0)
    large.step(0)
    own = pltpu.make_async_copy(x_ref, o_ref.at[me], loc.at[0])
    own.start()
    piece = pltpu.make_async_copy(w_ref, held.at[me], loc.at[1])
    piece.start()
    piece.wait()
    for s in range(1, n - 1):
        small.step(s)
    small.last()

    def there(at):
        ctx_, x_ = lax.div(at, 2), lax.rem(at, 2)
        rows = pl.ds(pl.multiple_of((lax.div(ctx_, 2) * 2 + x_) * tall, 16), tall)
        cols = pl.ds(pl.multiple_of(lax.rem(ctx_, 2) * deep, 128), deep)
        return f_ref.at[:, rows, cols]

    def push(shift):
        other = lax.rem(place + shift, 8)
        return pltpu.make_async_remote_copy(
            src_ref=held,
            dst_ref=there(place),
            send_sem=s3.at[shift],
            recv_sem=r3.at[shift],
            device_id={"context": lax.div(other, 2), "dp": lax.rem(other, 2)},
            device_id_type=MESH,
        )

    for shift in range(1, 8):
        push(shift).start()
    kept = pltpu.make_async_copy(held, there(place), loc.at[2])
    kept.start()
    for s in range(1, n - 1):
        large.step(s)
    large.last()
    for shift in range(1, 8):
        source = there(lax.rem(place + 8 - shift, 8))
        pltpu.make_async_copy(source, source, r3.at[shift]).wait()
    kept.wait()
    own.wait()
    small.finish()
    large.finish()
    for shift in range(1, 8):
        push(shift).wait_send()


def gather_pieces(tokens, gain, shift, w, n, collective_id):
    rows, cols = tokens.shape
    wide, deep = w.shape
    full, weight = pl.pallas_call(
        functools.partial(gather_pieces_kernel, n),
        out_shape=(
            jax.ShapeDtypeStruct((n, rows, cols), jnp.bfloat16),
            jax.ShapeDtypeStruct((n, wide, deep), w.dtype),
        ),
        in_specs=[VM] * 4,
        out_specs=(VM, VM),
        scratch_shapes=[
            pltpu.VMEM((rows, cols), jnp.bfloat16),
            pltpu.VMEM((n, wide // 4, deep // 2), w.dtype),
        ]
        + [DMA((2, n - 1)) for _ in range(4)]
        + [DMA((8,)), DMA((8,)), DMA((3,))],
        compiler_params=remote_params(collective_id),
    )(tokens, gain[None], shift[None], w)
    return full.reshape(n * rows, cols), weight.reshape(n * wide, deep)


def dot(left, right, dims):
    return lax.dot_general(left, right, ((dims[0], dims[1]), ((), ())), preferred_element_type=jnp.float32)


def key_positions(first, keys, queries):
    return first + lax.broadcasted_iota(jnp.int32, (keys, queries), 0)


def load_rows(qkv_ref, nb, half, qs, kt, ks, vs):
    for block in range(nb):
        part = slice(block % 2 * half, block % 2 * half + half)
        at = block // 2
        qs[block] = qkv_ref[at, 0, :, part] * jnp.asarray(HEAD_DIM**-0.5, qs.dtype)
        item = qkv_ref[at, 1, :, part]
        if kt is not None:
            kt[block] = item
        ks[block] = item.T
        if vs is not None:
            vs[block] = qkv_ref[at, 2, :, part].T


def fill_tables(nb, half, seg_ref, order_ref, slot_ref, low_ref, high_ref):
    for block in range(nb):
        slot_ref[order_ref[block]] = jnp.int32(block)
    first = [seg_ref[0, block * half] for block in range(nb)]
    last = [seg_ref[0, block * half + half - 1] for block in range(nb)]
    for block in range(nb):
        if low_ref is not None:
            low_ref[block] = sum(jnp.where(item < first[block], 1, 0) for item in last)
        if high_ref is not None:
            high_ref[block] = sum(jnp.where(item <= last[block], 1, 0) for item in first)


def forward_kernel(half, heads, seg_s, order_ref, seg_ref, qkv_ref, o_ref, full_ref, lse_ref, start_ref, qs, ks, slot_ref, low_ref):
    nb = full_ref.shape[0]

    @pl.when(lax.axis_index("context") < heads)
    def _():
        load_rows(qkv_ref, nb, half, qs, None, ks, None)
        fill_tables(nb, half, seg_s, order_ref, slot_ref, low_ref, None)
        seg = seg_ref[...]
        start = jnp.zeros(seg.shape, jnp.float32)
        for doc in range(1, DOC_LIMIT):
            before = jnp.sum(jnp.where(seg < doc, 1.0, 0.0), axis=1, keepdims=True)
            start = jnp.where(seg == doc, before, start)
        start_ref[...] = start.astype(jnp.int32)

        @pl.loop(0, nb)
        def _(nq):
            slot = slot_ref[nq]
            query = qs[slot]
            begin = start_ref[:, pl.ds(pl.multiple_of(nq * half, 128), half)]
            here = nq * half + lax.broadcasted_iota(jnp.int32, (1, half), 1)

            def step(nk, state):
                top, total, acc = state
                at = slot_ref[nk]
                score = dot(ks[at], query, ((1,), (0,)))
                place = key_positions(nk * half, half, half)
                score = jnp.where((place >= begin) & (place <= here), score, NEG_FILL)
                new_top = jnp.maximum(top, jnp.max(score, axis=0, keepdims=True))
                factor = jnp.exp(top - new_top)
                weight = jnp.exp(score - new_top)
                total = total * factor + jnp.sum(weight, axis=0, keepdims=True)
                value = qkv_ref[at // 2, 2, :, pl.ds(pl.multiple_of(at % 2 * half, 128), half)]
                acc = acc * factor + dot(value, weight.astype(jnp.bfloat16), ((1,), (0,)))
                return new_top, total, acc

            top, total, acc = lax.fori_loop(
                low_ref[nq],
                nq + 1,
                step,
                (
                    jnp.full((1, half), NEG_FILL, jnp.float32),
                    jnp.zeros((1, half), jnp.float32),
                    jnp.zeros((HEAD_DIM, half), jnp.float32),
                ),
            )
            result = acc / total
            full_ref[slot] = result
            lse_ref[slot] = top + jnp.log(total)
            low = result.astype(jnp.bfloat16)
            o_ref[2 * slot] = low[:, : half // 2]
            o_ref[2 * slot + 1] = low[:, half // 2 :]


def attend_forward(qkv, segments, order, half, heads):
    nc = qkv.shape[0]
    nb = 2 * nc
    return pl.pallas_call(
        functools.partial(forward_kernel, half, heads),
        out_shape=(
            jax.ShapeDtypeStruct((2 * nb, HEAD_DIM, half // 2), jnp.bfloat16),
            jax.ShapeDtypeStruct((nb, HEAD_DIM, half), jnp.float32),
            jax.ShapeDtypeStruct((nb, 1, half), jnp.float32),
            jax.ShapeDtypeStruct(segments.shape, jnp.int32),
        ),
        in_specs=[SM, SM, VM, VM],
        out_specs=(VM, VM, VM, VM),
        scratch_shapes=[
            pltpu.VMEM((nb, HEAD_DIM, half), jnp.bfloat16),
            pltpu.VMEM((nb, half, HEAD_DIM), jnp.bfloat16),
            pltpu.SMEM((nb,), jnp.int32),
            pltpu.SMEM((nb,), jnp.int32),
        ],
        compiler_params=pltpu.CompilerParams(vmem_limit_bytes=48 << 20),
    )(segments, order, segments, qkv)


def backward_kernel(
    half, heads, seg_s, order_ref, start_ref, qkv_ref, full_ref, lse_ref, grad_ref, o_ref,
    qs, kt, ks, vs, gs, ds, dq, slot_ref, high_ref,
):
    nb = full_ref.shape[0]

    @pl.when(lax.axis_index("context") < heads)
    def _():
        load_rows(qkv_ref, nb, half, qs, kt, ks, vs)
        fill_tables(nb, half, seg_s, order_ref, slot_ref, None, high_ref)
        for block in range(nb):
            both = jnp.concatenate([grad_ref[2 * block], grad_ref[2 * block + 1]], axis=1)
            gs[block] = both
            ds[block] = jnp.sum(both.astype(jnp.float32) * full_ref[block], axis=0, keepdims=True)
            dq[block] = jnp.zeros((HEAD_DIM, half), jnp.float32)

        @pl.loop(0, nb)
        def _(nk):
            at = slot_ref[nk]
            place = key_positions(nk * half, half, half)

            def step(nq, state):
                grad_key, grad_value = state
                slot = slot_ref[nq]
                query, grad = qs[slot], gs[slot]
                begin = start_ref[:, pl.ds(pl.multiple_of(nq * half, 128), half)]
                here = nq * half + lax.broadcasted_iota(jnp.int32, (1, half), 1)
                score = dot(ks[at], query, ((1,), (0,)))
                score = jnp.where((place >= begin) & (place <= here), score, NEG_FILL)
                weight = jnp.exp(score - lse_ref[slot])
                grad_weight = dot(vs[at], grad, ((1,), (0,)))
                grad_score = (weight * (grad_weight - ds[slot])).astype(jnp.bfloat16)
                grad_value = grad_value + dot(grad, weight.astype(jnp.bfloat16), ((1,), (1,)))
                grad_key = grad_key + dot(query, grad_score, ((1,), (1,)))
                dq[slot] += dot(kt[at], grad_score, ((1,), (0,)))
                return grad_key, grad_value

            zero = jnp.zeros((HEAD_DIM, half), jnp.float32)
            grad_key, grad_value = lax.fori_loop(nk, high_ref[nk], step, (zero, zero))
            columns = pl.ds(pl.multiple_of(at % 2 * half, 128), half)
            o_ref[at // 2, 1, :, columns] = grad_key.astype(jnp.bfloat16)
            o_ref[at // 2, 2, :, columns] = grad_value.astype(jnp.bfloat16)

        for block in range(nb):
            part = slice(block % 2 * half, block % 2 * half + half)
            o_ref[block // 2, 0, :, part] = (dq[block] * HEAD_DIM**-0.5).astype(jnp.bfloat16)


def attend_backward(qkv, segments, order, start, full, lse, grad, half, heads):
    nc = qkv.shape[0]
    nb = 2 * nc
    low = jnp.bfloat16
    return pl.pallas_call(
        functools.partial(backward_kernel, half, heads),
        out_shape=jax.ShapeDtypeStruct(qkv.shape, low),
        in_specs=[SM, SM, VM, VM, VM, VM, VM],
        out_specs=VM,
        scratch_shapes=[
            pltpu.VMEM((nb, HEAD_DIM, half), low),
            pltpu.VMEM((nb, HEAD_DIM, half), low),
            pltpu.VMEM((nb, half, HEAD_DIM), low),
            pltpu.VMEM((nb, half, HEAD_DIM), low),
            pltpu.VMEM((nb, HEAD_DIM, half), low),
            pltpu.VMEM((nb, 1, half), jnp.float32),
            pltpu.VMEM((nb, HEAD_DIM, half), jnp.float32),
            pltpu.SMEM((nb,), jnp.int32),
            pltpu.SMEM((nb,), jnp.int32),
        ],
        compiler_params=pltpu.CompilerParams(vmem_limit_bytes=48 << 20),
    )(segments, order, start, qkv, full, lse, grad)


def norm_parts(values):
    centre = jnp.mean(values, axis=-1, keepdims=True)
    shifted = values - centre
    spread_ = jnp.mean(shifted * shifted, axis=-1, keepdims=True)
    scale = lax.rsqrt(spread_ + NORM_EPS)
    return shifted * scale, scale


def norm_backward(grad, normed, scale, gain):
    e = grad * gain
    mean_e = jnp.mean(e, axis=-1, keepdims=True)
    mean_en = jnp.mean(e * normed, axis=-1, keepdims=True)
    return (e - mean_e - normed * mean_en) * scale


def gelu_tanh(values):
    return jax.nn.gelu(values, approximate=True)


def cross_rows(left, right):
    return lax.dot_general(
        left, right, (((0,), (0,)), ((), ())), preferred_element_type=jnp.float32
    )


def after(value, done):
    return lax.optimization_barrier((value, done))[0]


def per_device(
    mesh_sizes,
    inputs,
    first_gain,
    first_shift,
    project_weight,
    project_bias,
    attend_weight,
    attend_bias,
    second_gain,
    second_shift,
    expand_weight,
    expand_bias,
    shrink_weight,
    shrink_bias,
    segments,
    block_order,
    cotangent,
):
    nt, nc = mesh_sizes["tensor"], mesh_sizes["context"]
    own_rows, width = inputs.shape[1], inputs.shape[2]
    local_width = project_weight.shape[2]
    heads = local_width // HEAD_DIM
    block_rows = own_rows * nt
    half = block_rows // 2
    low = jnp.bfloat16
    f32 = lambda value: value.astype(jnp.float32)
    square = nt == 4 and nc == 4 and mesh_sizes["dp"] == 2
    plane = ("context", "dp")

    tokens_own = f32(inputs[0])
    grad_out = cotangent[0]
    if square:
        hidden1_full, attend_full = gather_pieces(inputs[0], first_gain, first_shift, attend_weight, nt, 0)
    else:
        hidden1 = norm_parts(tokens_own)[0] * first_gain + first_shift
        hidden1_full = gather_rows(hidden1.astype(low), nt, 0)
        attend_full = lax.all_gather(attend_weight, "tensor", axis=0, tiled=True)
    grad_full = lax.all_gather(after(grad_out, hidden1_full), "tensor", axis=0, tiled=True)

    bias = jnp.stack([project_bias[0], jnp.zeros_like(project_bias[0]), project_bias[1]])[:, :, None]
    projected = jnp.einsum(
        "kde,rd->ker", project_weight, hidden1_full, preferred_element_type=jnp.float32
    )
    projected = (projected + bias).astype(low).reshape(3, heads, HEAD_DIM, block_rows)
    qkv = to_heads(projected, nc, 1)
    pieces, attended_full, lse, start = attend_forward(qkv, segments, block_order, half, heads)
    attended = to_rows(pieces, nc, nt, heads, 2).reshape(width, own_rows)

    middle = tokens_own + cross_rows(attended, attend_full) + attend_bias
    normed2, scale2 = norm_parts(middle)
    hidden2 = (normed2 * second_gain + second_shift).astype(low)
    hidden2_full = gather_rows(hidden2, nt, 3)
    pre_act = jnp.dot(hidden2_full, expand_weight, preferred_element_type=jnp.float32) + expand_bias
    activ = gelu_tanh(pre_act).astype(low)
    grad_act = dot(grad_full, shrink_weight, ((1,), (1,)))
    grad_pre = jax.vjp(gelu_tanh, pre_act)[1](grad_act)[0].astype(low)
    grad_shrink = cross_rows(activ, grad_full).astype(low)
    grad_expand = cross_rows(hidden2_full, grad_pre).astype(low)
    grad_hidden2 = dot(grad_pre, expand_weight, ((1,), (1,))).astype(low)
    if square:
        units = [item.reshape((16, -1) + item.shape[1:]) for item in (grad_shrink, grad_expand)]
        grad_hidden2, feed_pieces = scatter_reduce(grad_hidden2, units, nt, 4)
    else:
        grad_hidden2 = scatter_rows(grad_hidden2, nt, 4)
    grad_expand_bias = jnp.sum(f32(grad_pre), axis=0)
    grad_shrink_bias = jnp.sum(f32(grad_out), axis=0)
    feed = jnp.dot(activ, shrink_weight, preferred_element_type=jnp.float32).astype(low)

    grad_second_gain = jnp.sum(grad_hidden2 * normed2, axis=0)
    grad_second_shift = jnp.sum(grad_hidden2, axis=0)
    grad_middle = f32(grad_out) + norm_backward(grad_hidden2, normed2, scale2, second_gain)
    grad_middle_low = grad_middle.astype(low)
    grad_attend_bias = jnp.sum(f32(grad_middle_low), axis=0)
    grad_attended = dot(attend_full, grad_middle_low, ((1,), (1,))).astype(low)
    grad_attended = grad_attended.reshape(nt * heads, HEAD_DIM, own_rows)
    grad_attend = jnp.dot(attended, grad_middle_low, preferred_element_type=jnp.float32).astype(low)
    if square:
        unit = grad_attend.reshape(2, 2, 4, own_rows // 4, 2, width // 2).transpose(4, 0, 2, 1, 3, 5)
        unit = unit.reshape(16, 2, own_rows // 4, width // 2)
        grad_heads, attend_pieces = rows_back_sum(grad_attended, unit, nc, nt, heads, 5)
    else:
        grad_heads = rows_back(grad_attended, nc, nt, heads, 5)
        attend_pieces = None
    feed_sum = lax.psum_scatter(after(feed, grad_heads), "tensor", scatter_dimension=0, tiled=True)

    grad_qkv = attend_backward(qkv, segments, block_order, start, attended_full, lse, grad_heads, half, heads)
    grad_rows = from_heads(grad_qkv, attend_pieces, nc, nt, heads, 6)
    if square:
        grad_rows, attend_piece = grad_rows
    grad_rows = grad_rows.reshape(3 * local_width, block_rows)
    grad_project = dot(hidden1_full, grad_rows, ((0,), (1,))).astype(low)
    grad_hidden1 = lax.dot_general(
        grad_rows.reshape(3, local_width, block_rows),
        project_weight,
        (((0, 1), (0, 2)), ((), ())),
        preferred_element_type=jnp.float32,
    ).astype(low)
    row_sums = jnp.sum(f32(grad_rows), axis=1)
    grad_project_bias = jnp.concatenate([row_sums[:local_width], row_sums[2 * local_width :]])

    wide = grad_expand_bias.shape[0]
    spare = -(wide + 2 * local_width) % width
    others = [
        grad_attend_bias,
        grad_second_gain,
        grad_second_shift,
        grad_shrink_bias,
        grad_expand_bias,
        jnp.pad(grad_project_bias, (0, spare)),
    ]
    if square:
        empty = jnp.zeros((2 * width,), jnp.float32)
        vectors = jnp.concatenate([empty] + others).reshape(-1, width)
        grad_inputs, summed, grad_project, grad_attend, feeds = last_part(
            grad_hidden1,
            grad_project.reshape(16, -1, 3 * local_width),
            attend_piece,
            feed_pieces,
            inputs[0],
            first_gain[None],
            grad_middle,
            vectors,
            6,
            nt,
            7,
        )
        grad_project = grad_project.reshape(width, 3 * local_width)
        grad_shrink, grad_expand = feeds[0].reshape(-1, width), feeds[1].reshape(width, -1)
    else:
        grad_hidden1 = scatter_rows(grad_hidden1, nt, 7)
        normed1, scale1 = norm_parts(tokens_own)
        back = norm_backward(grad_hidden1, normed1, scale1, first_gain)
        grad_inputs = (grad_middle + back).astype(low)
        both = [jnp.sum(grad_hidden1 * normed1, axis=0), jnp.sum(grad_hidden1, axis=0)]
        vectors = jnp.concatenate(both + others).reshape(-1, width)
        summed = sum_vectors(vectors, 6, mesh_sizes, 8)
        grad_attend = lax.psum_scatter(grad_attend, "tensor", scatter_dimension=0, tiled=True)
        grad_project, grad_attend, grad_shrink, grad_expand = lax.psum(
            (grad_project, grad_attend, grad_shrink, grad_expand), plane
        )
    feed_sum = f32(after(feed_sum, summed))
    outputs = (middle + feed_sum + shrink_bias).astype(low)[None]
    grad_project = jnp.stack(
        [grad_project[:, at * local_width : (at + 1) * local_width] for at in range(3)]
    )
    tail = summed[6:].reshape(-1)
    return (
        outputs,
        grad_inputs[None],
        summed[0],
        summed[1],
        f32(grad_project),
        tail[wide : wide + 2 * local_width].reshape(2, local_width),
        f32(grad_attend),
        summed[2],
        summed[3],
        summed[4],
        f32(grad_expand),
        tail[:wide],
        f32(grad_shrink),
        summed[5],
    )


def solution(mesh):
    rows = P("dp", ("context", "tensor"), None)
    in_specs = (
        rows,
        P(),
        P(),
        P(None, None, "tensor"),
        P(None, "tensor"),
        P("tensor", None),
        P(),
        P(),
        P(),
        P(None, "tensor"),
        P("tensor"),
        P("tensor", None),
        P(),
        P("dp", None),
        P(),
        rows,
    )
    out_specs = (
        rows,
        rows,
        P(),
        P(),
        P(None, None, "tensor"),
        P(None, "tensor"),
        P("tensor", None),
        P(),
        P(),
        P(),
        P(None, "tensor"),
        P("tensor"),
        P("tensor", None),
        P(),
    )
    return jax.shard_map(
        functools.partial(per_device, dict(mesh.shape)),
        mesh=mesh,
        in_specs=in_specs,
        out_specs=out_specs,
        check_vma=False,
    )
```

```python
import functools

import jax
import jax.numpy as jnp
from jax import lax
from jax.experimental import pallas as pl
from jax.experimental.pallas import tpu as pltpu
from jax.sharding import PartitionSpec as P

HEAD_DIM = 64
NEG_FILL = -1e30
NORM_EPS = 1e-05
DOC_LIMIT = 16
MESH = pl.DeviceIdType.MESH
VM = pl.BlockSpec(memory_space=pltpu.VMEM)
SM = pl.BlockSpec(memory_space=pltpu.SMEM)
DMA = pltpu.SemaphoreType.DMA


def remote_params(collective_id):
    return pltpu.CompilerParams(
        collective_id=collective_id, has_side_effects=True, vmem_limit_bytes=48 << 20
    )


def line_barrier(me, n):
    bar = pltpu.get_barrier_semaphore()

    @pl.when(me > 0)
    def _():
        pl.semaphore_signal(bar, inc=1, device_id={"tensor": me - 1}, device_id_type=MESH)

    @pl.when(me < n - 1)
    def _():
        pl.semaphore_signal(bar, inc=1, device_id={"tensor": me + 1}, device_id_type=MESH)

    pl.semaphore_wait(bar, jnp.where(me > 0, 1, 0) + jnp.where(me < n - 1, 1, 0))


def gather_kernel(n, x_ref, o_ref, send, recv, loc):
    me = lax.axis_index("tensor")
    line_barrier(me, n)
    own = pltpu.make_async_copy(x_ref, o_ref.at[me], loc)
    own.start()

    def copy(d, s):
        shard = jnp.clip(me - s if d == 0 else me + s, 0, n - 1)
        return pltpu.make_async_remote_copy(
            src_ref=x_ref if s == 0 else o_ref.at[shard],
            dst_ref=o_ref.at[shard],
            send_sem=send.at[d, s],
            recv_sem=recv.at[d, s],
            device_id={"tensor": jnp.clip(me + 1 if d == 0 else me - 1, 0, n - 1)},
            device_id_type=MESH,
        )

    def sends(d, s):
        return (me - s >= 0) & (me < n - 1) if d == 0 else (me + s < n) & (me > 0)

    def gets(d, s):
        return me - 1 - s >= 0 if d == 0 else me + 1 + s < n

    def landed(d, s):
        shard = jnp.clip(me - 1 - s if d == 0 else me + 1 + s, 0, n - 1)
        return pltpu.make_async_copy(o_ref.at[shard], o_ref.at[shard], recv.at[d, s])

    for s in range(n - 1):
        for d in range(2):
            if s > 0:

                @pl.when(gets(d, s - 1))
                def _():
                    landed(d, s - 1).wait()

            @pl.when(sends(d, s))
            def _():
                copy(d, s).start()

    for d in range(2):

        @pl.when(gets(d, n - 2))
        def _():
            landed(d, n - 2).wait()

        for s in range(n - 1):

            @pl.when(sends(d, s))
            def _():
                copy(d, s).wait_send()

    own.wait()


def gather_rows(x, n, collective_id):
    rows, cols = x.shape
    return pl.pallas_call(
        functools.partial(gather_kernel, n),
        out_shape=jax.ShapeDtypeStruct((n, rows, cols), x.dtype),
        in_specs=[VM],
        out_specs=VM,
        scratch_shapes=[DMA((2, n - 1)), DMA((2, n - 1)), DMA],
        compiler_params=remote_params(collective_id),
    )(x).reshape(n * rows, cols)


def scatter_kernel(n, x_ref, o_ref, buf, tmp, send, recv):
    me = lax.axis_index("tensor")
    line_barrier(me, n)

    def term(d, k):
        return n - 1 - k if d == 0 else k

    def sends(d, k):
        return me < n - 1 - k if d == 0 else me > k

    def behind(d):
        return me > 0 if d == 0 else me < n - 1

    def copy(d, k, first):
        return pltpu.make_async_remote_copy(
            src_ref=x_ref.at[term(d, k)] if first else tmp.at[d, k],
            dst_ref=buf.at[d, k],
            send_sem=send.at[d, k],
            recv_sem=recv.at[d, k],
            device_id={"tensor": jnp.clip(me + 1 if d == 0 else me - 1, 0, n - 1)},
            device_id_type=MESH,
        )

    def landed(d, k):
        return pltpu.make_async_copy(buf.at[d, k], buf.at[d, k], recv.at[d, k])

    for d in range(2):

        @pl.when(jnp.logical_not(behind(d)))
        def _():
            for k in range(n - 1):
                copy(d, k, True).start()

    for k in range(n - 1):
        for d in range(2):

            @pl.when(behind(d) & sends(d, k))
            def _():
                landed(d, k).wait()
                both = buf[d, k].astype(jnp.float32) + x_ref[term(d, k)].astype(jnp.float32)
                tmp[d, k] = both.astype(tmp.dtype)
                copy(d, k, False).start()

    o_ref[...] = x_ref[me].astype(jnp.float32)
    for d in range(2):
        for k in range(n - 1):

            @pl.when(behind(d) & (me == term(d, k)))
            def _():
                landed(d, k).wait()
                o_ref[...] += buf[d, k].astype(jnp.float32)

    for d in range(2):
        for k in range(n - 1):

            @pl.when(sends(d, k))
            def _():
                copy(d, k, False).wait_send()


def scatter_rows(x, n, collective_id):
    rows, cols = x.shape
    own = rows // n
    return pl.pallas_call(
        functools.partial(scatter_kernel, n),
        out_shape=jax.ShapeDtypeStruct((own, cols), jnp.float32),
        in_specs=[VM],
        out_specs=VM,
        scratch_shapes=[
            pltpu.VMEM((2, n - 1, own, cols), x.dtype),
            pltpu.VMEM((2, n - 1, own, cols), x.dtype),
            DMA((2, n - 1)),
            DMA((2, n - 1)),
        ],
        compiler_params=remote_params(collective_id),
    )(x.reshape(n, own, cols))


def group_barrier(axes, sizes):
    mine = [lax.axis_index(name) for name in axes]
    place = sum_index(mine, sizes)
    total = 1
    for size in sizes:
        total *= size
    bar = pltpu.get_barrier_semaphore()
    for shift in range(1, total):
        other = lax.rem(place + shift, total)
        pl.semaphore_signal(bar, inc=1, device_id=spread(other, axes, sizes), device_id_type=MESH)
    pl.semaphore_wait(bar, total - 1)
    return place, total


def sum_index(mine, sizes):
    place = 0
    for at, size in zip(mine, sizes):
        place = place * size + at
    return place


def spread(place, axes, sizes):
    found = {}
    for name, size in reversed(tuple(zip(axes, sizes))):
        found[name] = lax.rem(place, size)
        place = lax.div(place, size)
    return found


def to_heads_kernel(nc, heads, x_ref, o_ref, send, recv, loc):
    me, _ = group_barrier(("context",), (nc,))

    def copy(shift):
        other = lax.rem(me + shift, nc)
        return other, pltpu.make_async_remote_copy(
            src_ref=x_ref.at[:, jnp.minimum(other, heads - 1)],
            dst_ref=o_ref.at[me],
            send_sem=send.at[shift],
            recv_sem=recv.at[shift],
            device_id={"context": other},
            device_id_type=MESH,
        )

    for shift in range(1, nc):
        other, item = copy(shift)

        @pl.when(other < heads)
        def _():
            item.start()

    own = pltpu.make_async_copy(x_ref.at[:, jnp.minimum(me, heads - 1)], o_ref.at[me], loc)
    own.start()
    own.wait()

    @pl.when(me < heads)
    def _():
        for shift in range(1, nc):
            source = lax.rem(me + nc - shift, nc)
            pltpu.make_async_copy(o_ref.at[source], o_ref.at[source], recv.at[shift]).wait()

    for shift in range(1, nc):
        other, item = copy(shift)

        @pl.when(other < heads)
        def _():
            item.wait_send()


def to_heads(x, nc, collective_id):
    heads = x.shape[1]
    return pl.pallas_call(
        functools.partial(to_heads_kernel, nc, heads),
        out_shape=jax.ShapeDtypeStruct((nc, x.shape[0]) + x.shape[2:], x.dtype),
        in_specs=[VM],
        out_specs=VM,
        scratch_shapes=[DMA((nc,)), DMA((nc,)), DMA],
        compiler_params=remote_params(collective_id),
    )(x)


def from_heads_kernel(nc, nt, heads, extra, x_ref, *rest):
    if extra:
        p_ref, o_ref, s_ref, send, recv, loc, land, zsend, zrecv = rest
    else:
        o_ref, send, recv, loc = rest
    me, ten = lax.axis_index("context"), lax.axis_index("tensor")
    bar = pltpu.get_barrier_semaphore()
    for shift in range(1, nc):
        pl.semaphore_signal(bar, inc=1, device_id={"context": lax.rem(me + shift, nc)}, device_id_type=MESH)
    if extra:
        for shift in range(1, nt):
            pl.semaphore_signal(bar, inc=1, device_id={"tensor": lax.rem(ten + shift, nt)}, device_id_type=MESH)
    pl.semaphore_wait(bar, nc - 1 + (nt - 1 if extra else 0))

    def copy(shift):
        other = lax.rem(me + shift, nc)
        return pltpu.make_async_remote_copy(
            src_ref=x_ref.at[other],
            dst_ref=o_ref.at[:, jnp.minimum(me, heads - 1)],
            send_sem=send.at[shift],
            recv_sem=recv.at[shift],
            device_id={"context": other},
            device_id_type=MESH,
        )

    def across(shift):
        other = lax.rem(ten + shift, nt)
        return pltpu.make_async_remote_copy(
            src_ref=p_ref.at[lax.div(other, 2), lax.rem(other, 2)],
            dst_ref=land.at[ten],
            send_sem=zsend.at[shift],
            recv_sem=zrecv.at[shift],
            device_id={"tensor": other},
            device_id_type=MESH,
        )

    if extra:
        for shift in range(1, nt):
            across(shift).start()

    @pl.when(me < heads)
    def _():
        for shift in range(1, nc):
            copy(shift).start()
        own = pltpu.make_async_copy(x_ref.at[me], o_ref.at[:, me], loc)
        own.start()
        own.wait()

    if extra:
        land[ten] = p_ref[lax.div(ten, 2), lax.rem(ten, 2)]
        for shift in range(1, nt):
            source = lax.rem(ten + nt - shift, nt)
            pltpu.make_async_copy(land.at[source], land.at[source], zrecv.at[shift]).wait()
        value = land[0].astype(jnp.float32)
        for at in range(1, nt):
            value = value + land[at].astype(jnp.float32)
        s_ref[...] = value.astype(s_ref.dtype)
        for shift in range(1, nt):
            across(shift).wait_send()

    for shift in range(1, nc):
        source = lax.rem(me + nc - shift, nc)

        @pl.when(source < heads)
        def _():
            at = jnp.minimum(source, heads - 1)
            pltpu.make_async_copy(o_ref.at[:, at], o_ref.at[:, at], recv.at[shift]).wait()

    @pl.when(me < heads)
    def _():
        for shift in range(1, nc):
            copy(shift).wait_send()


def from_heads(x, pieces, nc, nt, heads, collective_id):
    extra = pieces is not None
    out = jax.ShapeDtypeStruct((x.shape[1], heads) + x.shape[2:], x.dtype)
    scratch = [DMA((nc,)), DMA((nc,)), DMA]
    if extra:
        piece = pieces.shape[2:]
        scratch += [pltpu.VMEM((nt,) + piece, pieces.dtype), DMA((nt,)), DMA((nt,))]
        out = (out, jax.ShapeDtypeStruct(piece, pieces.dtype))
    return pl.pallas_call(
        functools.partial(from_heads_kernel, nc, nt, heads, extra),
        out_shape=out,
        in_specs=[VM] * (1 + extra),
        out_specs=(VM, VM) if extra else VM,
        scratch_shapes=scratch,
        compiler_params=remote_params(collective_id),
    )(*((x, pieces) if extra else (x,)))


AXES = ("context", "tensor")


def rows_kernel(nc, nt, heads, x_ref, o_ref, send, recv, loc):
    me, total = group_barrier(AXES, (nc, nt))
    my_ctx, my_ten = lax.axis_index("context"), lax.axis_index("tensor")
    my_head = my_ten * heads + jnp.minimum(my_ctx, heads - 1)

    def copy(shift):
        other = lax.rem(me + shift, total)
        return pltpu.make_async_remote_copy(
            src_ref=x_ref.at[other],
            dst_ref=o_ref.at[my_head],
            send_sem=send.at[shift],
            recv_sem=recv.at[shift],
            device_id=spread(other, AXES, (nc, nt)),
            device_id_type=MESH,
        )

    @pl.when(my_ctx < heads)
    def _():
        for shift in range(1, total):
            copy(shift).start()
        own = pltpu.make_async_copy(x_ref.at[me], o_ref.at[my_head], loc)
        own.start()
        own.wait()

    for shift in range(1, total):
        source = lax.rem(me + total - shift, total)
        ctx, ten = lax.div(source, nt), lax.rem(source, nt)

        @pl.when(ctx < heads)
        def _():
            at = ten * heads + jnp.minimum(ctx, heads - 1)
            pltpu.make_async_copy(o_ref.at[at], o_ref.at[at], recv.at[shift]).wait()

    @pl.when(my_ctx < heads)
    def _():
        for shift in range(1, total):
            copy(shift).wait_send()


def to_rows(x, nc, nt, heads, collective_id):
    total = nc * nt
    return pl.pallas_call(
        functools.partial(rows_kernel, nc, nt, heads),
        out_shape=jax.ShapeDtypeStruct((nt * heads,) + x.shape[1:], x.dtype),
        in_specs=[VM],
        out_specs=VM,
        scratch_shapes=[DMA((total,)), DMA((total,)), DMA],
        compiler_params=remote_params(collective_id),
    )(x)


def rows_back_kernel(nc, nt, heads, x_ref, o_ref, send, recv, loc):
    me, total = group_barrier(AXES, (nc, nt))
    my_ctx, my_ten = lax.axis_index("context"), lax.axis_index("tensor")

    def copy(shift):
        other = lax.rem(me + shift, total)
        ctx, ten = lax.div(other, nt), lax.rem(other, nt)
        return ctx < heads, pltpu.make_async_remote_copy(
            src_ref=x_ref.at[ten * heads + jnp.minimum(ctx, heads - 1)],
            dst_ref=o_ref.at[me],
            send_sem=send.at[shift],
            recv_sem=recv.at[shift],
            device_id={"context": ctx, "tensor": ten},
            device_id_type=MESH,
        )

    for shift in range(1, total):
        goes, item = copy(shift)

        @pl.when(goes)
        def _():
            item.start()

    own = pltpu.make_async_copy(
        x_ref.at[my_ten * heads + jnp.minimum(my_ctx, heads - 1)], o_ref.at[me], loc
    )
    own.start()
    own.wait()

    @pl.when(my_ctx < heads)
    def _():
        for shift in range(1, total):
            source = lax.rem(me + total - shift, total)
            pltpu.make_async_copy(o_ref.at[source], o_ref.at[source], recv.at[shift]).wait()

    for shift in range(1, total):
        goes, item = copy(shift)

        @pl.when(goes)
        def _():
            item.wait_send()


def rows_back(x, nc, nt, heads, collective_id):
    total = nc * nt
    return pl.pallas_call(
        functools.partial(rows_back_kernel, nc, nt, heads),
        out_shape=jax.ShapeDtypeStruct((total,) + x.shape[1:], x.dtype),
        in_specs=[VM],
        out_specs=VM,
        scratch_shapes=[DMA((total,)), DMA((total,)), DMA],
        compiler_params=remote_params(collective_id),
    )(x)


def vectors_kernel(names, sizes, shared, x_ref, o_ref, now, *rest):
    bufs, sems = rest[: len(names)], rest[len(names) :]
    bar = pltpu.get_barrier_semaphore()
    for name, size in zip(names, sizes):
        me = lax.axis_index(name)
        for shift in range(1, size):
            pl.semaphore_signal(
                bar, inc=1, device_id={name: lax.rem(me + shift, size)}, device_id_type=MESH
            )
    pl.semaphore_wait(bar, sum(sizes) - len(sizes))
    for stage, (name, size) in enumerate(zip(names, sizes)):
        buf, send, recv = bufs[stage], sems[2 * stage], sems[2 * stage + 1]
        me = lax.axis_index(name)

        def copy(shift):
            return pltpu.make_async_remote_copy(
                src_ref=now.at[stage] if stage else x_ref.at[0],
                dst_ref=buf.at[me],
                send_sem=send.at[shift],
                recv_sem=recv.at[shift],
                device_id={name: lax.rem(me + shift, size)},
                device_id_type=MESH,
            )

        for shift in range(1, size):
            copy(shift).start()
        buf[me] = now[stage] if stage else x_ref[0]
        for shift in range(1, size):
            source = lax.rem(me + size - shift, size)
            pltpu.make_async_copy(buf.at[source], buf.at[source], recv.at[shift]).wait()
        total = buf[0]
        for at in range(1, size):
            total = total + buf[at]
        if stage == 0:
            row = lax.broadcasted_iota(jnp.int32, total.shape, 0)
            total = jnp.where(row < shared, total, x_ref[0])
        if stage + 1 < len(names):
            now[stage + 1] = total
        else:
            o_ref[...] = total
        for shift in range(1, size):
            copy(shift).wait_send()


def sum_vectors(rows, shared, mesh_sizes, collective_id):
    names = ("tensor", "context", "dp")
    sizes = tuple(mesh_sizes[name] for name in names)
    shape = rows.shape
    return pl.pallas_call(
        functools.partial(vectors_kernel, names, sizes, shared),
        out_shape=jax.ShapeDtypeStruct(shape, jnp.float32),
        in_specs=[VM],
        out_specs=VM,
        scratch_shapes=[pltpu.VMEM((len(names),) + shape, jnp.float32)]
        + [pltpu.VMEM((size,) + shape, jnp.float32) for size in sizes]
        + [DMA((size,)) for size in sizes for _ in range(2)],
        compiler_params=remote_params(collective_id),
    )(rows[None])


class PlaneSum:
    def __init__(self, u, p, o, bufs=None, spread=None):
        self.u, self.p, self.o = u, p, o
        if bufs is not None:
            self.rc, self.s1, self.ra, self.rb, self.sa, self.sb, self.ta, self.tb = bufs[:8]
            self.send1, self.recv1 = bufs[8:]
        if spread is not None:
            self.send2, self.recv2, self.loc = spread
        ctx, self.x = lax.axis_index("context"), lax.axis_index("dp")
        self.core, self.y = lax.rem(ctx, 2), lax.div(ctx, 2)
        self.chip_peer = {"context": ctx + 1 - 2 * self.core}
        self.y_peer = {"context": lax.rem(ctx + 2, 4)}
        self.x_peer = {"dp": 1 - self.x}

    @staticmethod
    def reduce_scratch(shape, dtype):
        tail = tuple(shape[1:])
        bufs = [pltpu.VMEM((count,) + tail, dtype) for count in (8, 8, 2, 2, 2, 2, 1, 1)]
        return bufs + [DMA((5,)), DMA((5,))]

    @staticmethod
    def spread_scratch():
        return [DMA((5,)), DMA((5,)), DMA((2,))]

    @staticmethod
    def greet(bar):
        ctx, x = lax.axis_index("context"), lax.axis_index("dp")
        for peer in (
            {"context": ctx + 1 - 2 * lax.rem(ctx, 2)},
            {"context": lax.rem(ctx + 2, 4)},
            {"dp": 1 - x},
        ):
            pl.semaphore_signal(bar, inc=1, device_id=peer, device_id_type=MESH)
        return 3

    def copy(self, at, src, dst, peer):
        send, recv = (self.send1, self.recv1) if at < 5 else (self.send2, self.recv2)
        return pltpu.make_async_remote_copy(
            src_ref=src,
            dst_ref=dst,
            send_sem=send.at[at % 5],
            recv_sem=recv.at[at % 5],
            device_id=peer,
            device_id_type=MESH,
        )

    def got(self, at, ref):
        recv = self.recv1 if at < 5 else self.recv2
        pltpu.make_async_copy(ref, ref, recv.at[at % 5]).wait()

    def add(self, out, left, right):
        f32 = jnp.float32
        out[...] = (left[...].astype(f32) + right[...].astype(f32)).astype(out.dtype)

    def mine(self, half):
        if half == 0:
            return pl.ds(self.core * 8 + 2 * self.x + self.y, 1)
        return pl.ds(self.core * 8 + 4 + 2 * self.y + self.x, 1)

    def hop(self, at):
        x, y, core = self.x, self.y, self.core
        o, p = self.o, self.p
        pair_a, pair_b = pl.ds(core * 8 + 2 * x, 2), pl.ds(core * 8 + 4 + 2 * y, 2)
        one = lambda at: pl.ds(at, 1)
        return [
            lambda: self.copy(0, self.by_core(1 - core), self.rc, self.chip_peer),
            lambda: self.copy(1, self.quarter(0, 1 - x), self.ra, self.x_peer),
            lambda: self.copy(2, self.quarter(1, 1 - y), self.rb, self.y_peer),
            lambda: self.copy(3, self.eighth(0, 1 - y), self.ta, self.y_peer),
            lambda: self.copy(4, self.eighth(1, 1 - x), self.tb, self.x_peer),
            lambda: self.copy(5, p.at[one(0)], o.at[self.mine(0)], self.y_peer),
            lambda: self.copy(6, p.at[one(1)], o.at[self.mine(1)], self.x_peer),
            lambda: self.copy(7, o.at[pair_a], o.at[pair_a], self.x_peer),
            lambda: self.copy(8, o.at[pair_b], o.at[pair_b], self.y_peer),
            lambda: self.copy(9, o.at[pl.ds(core * 8, 8)], o.at[pl.ds(core * 8, 8)], self.chip_peer),
        ][at]()

    def begin(self):
        self.hop(0).start()

    def by_core(self, core):
        return self.u.at[pl.ds(core * 8, 8)]

    def quarter(self, half, at):
        return self.s1.at[pl.ds(4 * half + 2 * at, 2)]

    def eighth(self, half, at):
        return (self.sa, self.sb)[half].at[pl.ds(at, 1)]

    def result(self, half):
        return self.p.at[pl.ds(half, 1)]

    def first(self):
        self.got(0, self.rc)
        self.add(self.s1, self.by_core(self.core), self.rc)
        self.hop(1).start()
        self.hop(2).start()

    def second(self):
        self.got(1, self.ra)
        self.add(self.sa, self.quarter(0, self.x), self.ra)
        self.hop(3).start()
        self.got(2, self.rb)
        self.add(self.sb, self.quarter(1, self.y), self.rb)
        self.hop(4).start()

    def third(self):
        self.got(3, self.ta)
        self.add(self.result(0), self.eighth(0, self.y), self.ta)
        self.got(4, self.tb)
        self.add(self.result(1), self.eighth(1, self.x), self.tb)

    def reduced(self):
        for at in range(5):
            self.hop(at).wait_send()

    def kept(self, half):
        return pltpu.make_async_copy(self.p.at[pl.ds(half, 1)], self.o.at[self.mine(half)], self.loc.at[half])

    def spread1(self):
        self.hop(5).start()
        self.hop(6).start()
        self.kept(0).start()
        self.kept(1).start()

    def spread2(self):
        x, y, core = self.x, self.y, self.core
        self.kept(0).wait()
        self.got(5, self.o.at[pl.ds(core * 8 + 2 * x + 1 - y, 1)])
        self.hop(7).start()
        self.kept(1).wait()
        self.got(6, self.o.at[pl.ds(core * 8 + 4 + 2 * y + 1 - x, 1)])
        self.hop(8).start()

    def spread3(self):
        x, y, core = self.x, self.y, self.core
        self.got(7, self.o.at[pl.ds(core * 8 + 2 - 2 * x, 2)])
        self.got(8, self.o.at[pl.ds(core * 8 + 6 - 2 * y, 2)])
        self.hop(9).start()

    def everywhere(self):
        self.got(9, self.o.at[pl.ds(8 - self.core * 8, 8)])
        for at in range(5, 10):
            self.hop(at).wait_send()


class StripSum(PlaneSum):
    @staticmethod
    def reduce_scratch(shape, dtype):
        _, rows, cols = shape
        shapes = [(4, rows)] * 2 + [(2, rows // 2)] * 4 + [(2, rows // 4)] * 2
        return [pltpu.VMEM(item + (cols // 2,), dtype) for item in shapes] + [DMA((5,)), DMA((5,))]

    def by_core(self, core):
        size = self.u.shape[2] // 2
        return self.u.at[:, :, pl.ds(pl.multiple_of(core * size, 128), size)]

    def quarter(self, half, at):
        size = self.s1.shape[1] // 2
        return self.s1.at[pl.ds(2 * half, 2), pl.ds(pl.multiple_of(at * size, 16), size)]

    def eighth(self, half, at):
        size = self.sa.shape[1] // 2
        return (self.sa, self.sb)[half].at[:, pl.ds(pl.multiple_of(at * size, 16), size)]

    def result(self, half):
        return self.p.at[half]


def unit_pieces(unit):
    return jax.ShapeDtypeStruct((2,) + unit.shape[1:], unit.dtype)


def line_greet(bar, me, n):
    @pl.when(me > 0)
    def _():
        pl.semaphore_signal(bar, inc=1, device_id={"tensor": me - 1}, device_id_type=MESH)

    @pl.when(me < n - 1)
    def _():
        pl.semaphore_signal(bar, inc=1, device_id={"tensor": me + 1}, device_id_type=MESH)

    return jnp.where(me > 0, 1, 0) + jnp.where(me < n - 1, 1, 0)


class LineScatter:
    def __init__(self, n, x, o, buf, tmp, send, recv):
        self.n, self.x, self.o, self.buf, self.tmp, self.send, self.recv = n, x, o, buf, tmp, send, recv
        self.me = lax.axis_index("tensor")

    @staticmethod
    def scratch(n, own, cols, dtype):
        return [
            pltpu.VMEM((2, n - 1, own, cols), dtype),
            pltpu.VMEM((2, n - 1, own, cols), dtype),
            DMA((2, n - 1)),
            DMA((2, n - 1)),
        ]

    def term(self, d, k):
        return self.n - 1 - k if d == 0 else k

    def sends(self, d, k):
        return self.me < self.n - 1 - k if d == 0 else self.me > k

    def behind(self, d):
        return self.me > 0 if d == 0 else self.me < self.n - 1

    def copy(self, d, k, first):
        return pltpu.make_async_remote_copy(
            src_ref=self.x.at[self.term(d, k)] if first else self.tmp.at[d, k],
            dst_ref=self.buf.at[d, k],
            send_sem=self.send.at[d, k],
            recv_sem=self.recv.at[d, k],
            device_id={"tensor": jnp.clip(self.me + 1 if d == 0 else self.me - 1, 0, self.n - 1)},
            device_id_type=MESH,
        )

    def landed(self, d, k):
        return pltpu.make_async_copy(self.buf.at[d, k], self.buf.at[d, k], self.recv.at[d, k])

    def begin(self):
        for d in range(2):

            @pl.when(jnp.logical_not(self.behind(d)))
            def _():
                for k in range(self.n - 1):
                    self.copy(d, k, True).start()

    def step(self, k):
        for d in range(2):

            @pl.when(self.behind(d) & self.sends(d, k))
            def _():
                self.landed(d, k).wait()
                at = self.term(d, k)
                both = self.buf[d, k].astype(jnp.float32) + self.x[at].astype(jnp.float32)
                self.tmp[d, k] = both.astype(self.tmp.dtype)
                self.copy(d, k, False).start()

    def end(self):
        self.o[...] = self.x[self.me].astype(jnp.float32)
        for d in range(2):
            for k in range(self.n - 1):

                @pl.when(self.behind(d) & (self.me == self.term(d, k)))
                def _():
                    self.landed(d, k).wait()
                    self.o[...] += self.buf[d, k].astype(jnp.float32)

        for d in range(2):
            for k in range(self.n - 1):

                @pl.when(self.sends(d, k))
                def _():
                    self.copy(d, k, False).wait_send()


GELU_SCALE = 0.7978845608028654
GELU_CUBE = 0.044715


def feed_kernel(n, chunks, x_ref, up_ref, down_ref, bias_ref, grad_ref, *rest):
    (o_ref, feed_ref, sum_ref, p1_ref, p2_ref), rest = rest[:5], rest[5:]
    (held, act, gp, part, acc, buf, tmp, u1, u2), rest = rest[:9], rest[9:]
    (gsend, grecv, loc, ssend, srecv), rest = rest[:5], rest[5:]
    plane = [PlaneSum(u1, p1_ref, None, rest[:10]), PlaneSum(u2, p2_ref, None, rest[10:20])]
    me = lax.axis_index("tensor")
    rows, width = x_ref.shape
    wide = up_ref.shape[1]
    few = rows // chunks
    f32, low = jnp.float32, jnp.bfloat16
    bar = pltpu.get_barrier_semaphore()
    pl.semaphore_wait(bar, line_greet(bar, me, n) + PlaneSum.greet(bar))

    def rows_of(block):
        return pl.ds(pl.multiple_of(block * rows, rows), rows)

    def neighbour(d):
        return {"tensor": jnp.clip(jnp.where(d == 0, me + 1, me - 1), 0, n - 1)}

    def onward(d):
        return jnp.where(d == 0, me, n - 1 - me) < n - 1

    def hand_on(d, s, block, first):
        return pltpu.make_async_remote_copy(
            src_ref=x_ref if first else held.at[rows_of(block)],
            dst_ref=held.at[rows_of(block)],
            send_sem=gsend.at[d, s],
            recv_sem=grecv.at[d, s],
            device_id=neighbour(d),
            device_id_type=MESH,
        )

    def chunk(block, c):
        return pl.ds(pl.multiple_of(block * rows + c * few, few), few)

    def back(d, block, c, first):
        at = chunk(block, c)
        return pltpu.make_async_remote_copy(
            src_ref=part.at[at] if first else tmp.at[at],
            dst_ref=buf.at[d, at],
            send_sem=ssend.at[block, c],
            recv_sem=srecv.at[d, block, c],
            device_id=neighbour(d),
            device_id_type=MESH,
        )

    for d in range(2):

        @pl.when(onward(d))
        def _():
            hand_on(d, 0, me, True).start()

    own = pltpu.make_async_copy(x_ref, held.at[rows_of(me)], loc)
    own.start()
    sum_ref[...] = jnp.zeros_like(sum_ref)
    own.wait()
    columns = 256

    def work(block):
        here = rows_of(block)
        acc[...] = jnp.zeros_like(acc)

        @pl.loop(0, wide // columns)
        def _(j):
            at = pl.ds(pl.multiple_of(j * columns, columns), columns)
            pre = dot(held[here, :], up_ref[:, at], ((1,), (0,))) + bias_ref[:, at]
            square = pre * pre
            tanh = jnp.tanh(GELU_SCALE * pre * (1.0 + GELU_CUBE * square))
            act[here, at] = (0.5 * pre * (1.0 + tanh)).astype(low)
            slope = 0.5 * (1.0 + tanh) + 0.5 * pre * (1.0 - tanh * tanh) * (
                GELU_SCALE * (1.0 + 3.0 * GELU_CUBE * square)
            )
            grad = (dot(grad_ref[here, :], down_ref[at, :], ((1,), (1,))) * slope).astype(low)
            gp[here, at] = grad
            acc[...] += dot(grad, up_ref[:, at], ((1,), (1,)))

        part[here, :] = acc[...].astype(low)
        sum_ref[...] += jnp.sum(gp[here, :].astype(f32), axis=0, keepdims=True)

    near = jnp.minimum(me, n - 1 - me)
    toward = jnp.where(2 * me < n - 1, -1, 1)

    @pl.loop(0, n)
    def _(slot):
        paired = slot <= 2 * near
        distance = jnp.where(paired, lax.div(slot + 1, 2), slot - near)
        side = jnp.where(paired & (lax.rem(slot, 2) == 1), toward, -toward)
        block = me + side * distance
        d = jnp.where(block < me, 0, 1)
        s = jnp.maximum(distance - 1, 0)

        @pl.when(slot > 0)
        def _():
            landed = held.at[rows_of(block)]
            pltpu.make_async_copy(landed, landed, grecv.at[d, s]).wait()

            @pl.when(onward(d))
            def _():
                hand_on(d, jnp.minimum(s + 1, n - 2), block, False).start()

        work(block)

        @pl.when((slot > 0) & ((me == 0) | (me == n - 1)))
        def _():
            for c in range(chunks):
                back(1 - d, block, c, True).start()

    def weights(left, right, unit):
        half = wide // 2

        @pl.loop(0, 2)
        def _(j):
            at = pl.ds(pl.multiple_of(j * half, 128), half)
            total = dot(left[:, at], right[...], ((0,), (0,)))
            unit[pl.ds(8 * j, 8)] = total.astype(low).reshape((8,) + unit.shape[1:])

    weights(act, grad_ref, u1)
    plane[0].begin()
    weights(held, gp, u2)
    plane[1].begin()

    def relay(way, block):
        d = jnp.where(way > 0, 0, 1)

        @pl.when((me > 0) & (me < n - 1) & (block >= 0) & (block < n))
        def _():
            for c in range(chunks):
                at = chunk(block, c)
                landed = buf.at[d, at]
                pltpu.make_async_copy(landed, landed, srecv.at[d, block, c]).wait()
                tmp[at, :] = (buf[d, at, :].astype(f32) + part[at, :].astype(f32)).astype(low)
                back(d, block, c, False).start()

    plane[0].first()
    for j in range(1, n):
        relay(-toward, me - toward * j)
        if j == 1:
            plane[1].first()

    @pl.loop(0, n)
    def _(block):
        here = rows_of(block)
        feed_ref[here, :] = dot(act[here, :], down_ref[...], ((1,), (0,))).astype(low)

    plane[0].second()
    plane[1].second()
    for j in range(1, n):
        relay(toward, me + toward * j)
    for item in plane:
        item.third()
    for c in range(chunks):
        at = chunk(me, c)
        mine = pl.ds(c * few, few)
        o_ref[mine, :] = part[at, :].astype(f32)
        for d in range(2):

            @pl.when(me > 0 if d == 0 else me < n - 1)
            def _():
                landed = buf.at[d, at]
                pltpu.make_async_copy(landed, landed, srecv.at[d, me, c]).wait()
                o_ref[mine, :] += buf[d, at, :].astype(f32)

    for d in range(2):
        for s in range(n - 1):
            block = me - s if d == 0 else me + s

            @pl.when(onward(d) & (block >= 0) & (block < n))
            def _():
                hand_on(d, s, me, True).wait_send()

    for block in range(n):

        @pl.when(me != block)
        def _():
            for c in range(chunks):
                back(jnp.where(me < block, 0, 1), block, c, True).wait_send()

    for item in plane:
        item.reduced()


def feed_part(x, up, down, bias, grad, n, collective_id):
    rows, width = x.shape
    wide = up.shape[1]
    chunks = 2
    total = n * rows
    low, f32 = jnp.bfloat16, jnp.float32
    unit = (16, wide // 16, width)
    piece = jax.ShapeDtypeStruct((2,) + unit[1:], low)
    return pl.pallas_call(
        functools.partial(feed_kernel, n, chunks),
        out_shape=(
            jax.ShapeDtypeStruct((rows, width), f32),
            jax.ShapeDtypeStruct((total, width), low),
            jax.ShapeDtypeStruct((1, wide), f32),
            piece,
            piece,
        ),
        in_specs=[VM] * 5,
        out_specs=(VM,) * 5,
        scratch_shapes=[
            pltpu.VMEM((total, width), low),
            pltpu.VMEM((total, wide), low),
            pltpu.VMEM((total, wide), low),
            pltpu.VMEM((total, width), low),
            pltpu.VMEM((rows, width), f32),
            pltpu.VMEM((2, total, width), low),
            pltpu.VMEM((total, width), low),
            pltpu.VMEM(unit, low),
            pltpu.VMEM(unit, low),
            DMA((2, n - 1)),
            DMA((2, n - 1)),
            DMA,
            DMA((n, chunks)),
            DMA((2, n, chunks)),
        ]
        + PlaneSum.reduce_scratch(unit, low) * 2,
        compiler_params=remote_params(collective_id),
    )(x, up, down, bias[None], grad)


def last_kernel(n, shared, count, x_ref, u_ref, a_ref, *rest):
    ps, rest = rest[:count], rest[count:]
    token_ref, gain_ref, middle_ref, vec_ref, rest = rest[0], rest[1], rest[2], rest[3], rest[4:]
    g_ref, v_ref, po_ref, ao_ref, rest = rest[0], rest[1], rest[2], rest[3], rest[4:]
    outs, rest = rest[:count], rest[count:]
    sum_ref, piece, rest = rest[0], rest[1], rest[2:]
    line = LineScatter(n, x_ref, sum_ref, *rest[:4])
    project = PlaneSum(u_ref, piece, po_ref, rest[4:14], rest[14:17])
    rest = rest[17:]
    feeds = [PlaneSum(None, ps[i], outs[i], None, rest[3 * i : 3 * i + 3]) for i in range(count)]
    rest = rest[3 * count :]
    asend, arecv, aloc, now, rest = rest[0], rest[1], rest[2], rest[3], rest[4:]
    names, sizes = ("tensor", "context", "dp"), (n, 4, 2)
    bufs, sems = rest[:3], rest[3:]

    ten, ctx, x = (lax.axis_index(name) for name in names)
    place = ctx * 2 + x
    bar = pltpu.get_barrier_semaphore()
    for shift in range(1, n):
        pl.semaphore_signal(bar, inc=1, device_id={"tensor": lax.rem(ten + shift, n)}, device_id_type=MESH)
    for shift in range(1, 8):
        other = lax.rem(place + shift, 8)
        pl.semaphore_signal(
            bar, inc=1, device_id={"context": lax.div(other, 2), "dp": lax.rem(other, 2)}, device_id_type=MESH
        )
    pl.semaphore_wait(bar, n + 6)

    def there(at):
        ctx_, x_ = lax.div(at, 2), lax.rem(at, 2)
        y_ = lax.div(ctx_, 2)
        row = jnp.where(ten < n // 2, 2 * x_ + y_, 2 * y_ + x_)
        rows = pl.ds(pl.multiple_of(row * a_ref.shape[0], 16), a_ref.shape[0])
        cols = pl.ds(pl.multiple_of(lax.rem(ctx_, 2) * a_ref.shape[1], 128), a_ref.shape[1])
        return ao_ref.at[rows, cols]

    def push(shift):
        other = lax.rem(place + shift, 8)
        return pltpu.make_async_remote_copy(
            src_ref=a_ref,
            dst_ref=there(place),
            send_sem=asend.at[shift],
            recv_sem=arecv.at[shift],
            device_id={"context": lax.div(other, 2), "dp": lax.rem(other, 2)},
            device_id_type=MESH,
        )

    line.begin()
    project.begin()
    for item in feeds:
        item.spread1()
    for shift in range(1, 8):
        push(shift).start()
    kept = pltpu.make_async_copy(a_ref, there(place), aloc)
    kept.start()
    normed, scale = norm_parts(token_ref[...].astype(jnp.float32))
    project.first()
    line.step(0)
    for item in feeds:
        item.spread2()
    project.second()
    for k in range(1, n - 1):
        line.step(k)
    for item in feeds:
        item.spread3()
    project.third()
    project.spread1()
    line.end()
    grad = sum_ref[...]
    now[0] = vec_ref[...]
    now[0, 0:1] = jnp.sum(grad * normed, axis=0, keepdims=True)
    now[0, 1:2] = jnp.sum(grad, axis=0, keepdims=True)

    def stage_copy(stage, shift):
        name, size = names[stage], sizes[stage]
        me = lax.axis_index(name)
        return pltpu.make_async_remote_copy(
            src_ref=now.at[stage],
            dst_ref=bufs[stage].at[me],
            send_sem=sems[2 * stage].at[shift],
            recv_sem=sems[2 * stage + 1].at[shift],
            device_id={name: lax.rem(me + shift, size)},
            device_id_type=MESH,
        )

    def stage_start(stage):
        for shift in range(1, sizes[stage]):
            stage_copy(stage, shift).start()
        bufs[stage][lax.axis_index(names[stage])] = now[stage]

    def stage_end(stage):
        buf, size = bufs[stage], sizes[stage]
        me = lax.axis_index(names[stage])
        for shift in range(1, size):
            source = lax.rem(me + size - shift, size)
            pltpu.make_async_copy(buf.at[source], buf.at[source], sems[2 * stage + 1].at[shift]).wait()
        total = buf[0]
        for at in range(1, size):
            total = total + buf[at]
        if stage == 0:
            row = lax.broadcasted_iota(jnp.int32, total.shape, 0)
            total = jnp.where(row < shared, total, vec_ref[...])
        if stage < 2:
            now[stage + 1] = total
        else:
            v_ref[...] = total

    stage_start(0)
    back = norm_backward(grad, normed, scale, gain_ref[...])
    g_ref[...] = (middle_ref[...] + back).astype(g_ref.dtype)
    project.spread2()
    stage_end(0)
    stage_start(1)
    project.spread3()
    stage_end(1)
    stage_start(2)
    kept.wait()
    for shift in range(1, 8):
        source = there(lax.rem(place + 8 - shift, 8))
        pltpu.make_async_copy(source, source, arecv.at[shift]).wait()
    for item in feeds:
        item.everywhere()
    stage_end(2)
    project.everywhere()
    project.reduced()
    for shift in range(1, 8):
        push(shift).wait_send()
    for stage in range(3):
        for shift in range(1, sizes[stage]):
            stage_copy(stage, shift).wait_send()


def last_part(x, unit, attend_piece, pieces, tokens, gain, grad_middle, vectors, shared, n, collective_id):
    rows, cols = x.shape
    own = rows // n
    count = len(pieces)
    f32, low = jnp.float32, x.dtype
    whole = lambda item: jax.ShapeDtypeStruct((16,) + item.shape[1:], item.dtype)
    wide, deep = attend_piece.shape
    result = pl.pallas_call(
        functools.partial(last_kernel, n, shared, count),
        out_shape=(
            jax.ShapeDtypeStruct((own, cols), low),
            jax.ShapeDtypeStruct(vectors.shape, f32),
            whole(unit),
            jax.ShapeDtypeStruct((4 * wide, 2 * deep), low),
        )
        + tuple(whole(item) for item in pieces),
        in_specs=[VM] * (7 + count),
        out_specs=(VM,) * (4 + count),
        scratch_shapes=[pltpu.VMEM((own, cols), f32), pltpu.VMEM((2,) + unit.shape[1:], low)]
        + LineScatter.scratch(n, own, cols, low)
        + PlaneSum.reduce_scratch(unit.shape, low)
        + PlaneSum.spread_scratch()
        + [item for _ in pieces for item in PlaneSum.spread_scratch()]
        + [DMA((8,)), DMA((8,)), DMA, pltpu.VMEM((3,) + vectors.shape, f32)]
        + [pltpu.VMEM((size,) + vectors.shape, f32) for size in (n, 4, 2)]
        + [DMA((size,)) for size in (n, 4, 2) for _ in range(2)],
        compiler_params=remote_params(collective_id),
    )(x.reshape(n, own, cols), unit, attend_piece, *pieces, tokens, gain, grad_middle, vectors)
    return result[0], result[1], result[2], result[3], result[4:]


def rows_back_sum_kernel(nc, nt, heads, x_ref, u_ref, o_ref, p_ref, send, recv, loc, *rest):
    total = nc * nt
    my_ctx, my_ten = lax.axis_index("context"), lax.axis_index("tensor")
    me = my_ctx * nt + my_ten
    bar = pltpu.get_barrier_semaphore()
    for shift in range(1, total):
        other = lax.rem(me + shift, total)
        pl.semaphore_signal(bar, inc=1, device_id=spread(other, AXES, (nc, nt)), device_id_type=MESH)
    x = lax.axis_index("dp")
    pl.semaphore_signal(bar, inc=1, device_id={"dp": 1 - x}, device_id_type=MESH)
    pl.semaphore_wait(bar, total)

    unit = StripSum(u_ref, p_ref, None, rest)

    def copy(shift):
        other = lax.rem(me + shift, total)
        ctx, ten = lax.div(other, nt), lax.rem(other, nt)
        return ctx < heads, pltpu.make_async_remote_copy(
            src_ref=x_ref.at[ten * heads + jnp.minimum(ctx, heads - 1)],
            dst_ref=o_ref.at[me],
            send_sem=send.at[shift],
            recv_sem=recv.at[shift],
            device_id={"context": ctx, "tensor": ten},
            device_id_type=MESH,
        )

    for shift in range(1, total):
        goes, item = copy(shift)

        @pl.when(goes)
        def _():
            item.start()

    unit.begin()
    own = pltpu.make_async_copy(
        x_ref.at[my_ten * heads + jnp.minimum(my_ctx, heads - 1)], o_ref.at[me], loc
    )
    own.start()
    own.wait()
    unit.first()
    unit.second()
    unit.third()

    @pl.when(my_ctx < heads)
    def _():
        for shift in range(1, total):
            source = lax.rem(me + total - shift, total)
            pltpu.make_async_copy(o_ref.at[source], o_ref.at[source], recv.at[shift]).wait()

    unit.reduced()
    for shift in range(1, total):
        goes, item = copy(shift)

        @pl.when(goes)
        def _():
            item.wait_send()


def rows_back_sum(x, unit, nc, nt, heads, collective_id):
    total = nc * nt
    return pl.pallas_call(
        functools.partial(rows_back_sum_kernel, nc, nt, heads),
        out_shape=(
            jax.ShapeDtypeStruct((total,) + x.shape[1:], x.dtype),
            jax.ShapeDtypeStruct((2, 2, unit.shape[1] // 4, unit.shape[2] // 2), unit.dtype),
        ),
        in_specs=[VM, VM],
        out_specs=(VM, VM),
        scratch_shapes=[DMA((total,)), DMA((total,)), DMA] + StripSum.reduce_scratch(unit.shape, unit.dtype),
        compiler_params=remote_params(collective_id),
    )(x, unit)


class LineGather:
    def __init__(self, n, x, o, send, recv):
        self.n, self.x, self.o, self.send, self.recv = n, x, o, send, recv
        self.me = lax.axis_index("tensor")

    def copy(self, d, s):
        me, n = self.me, self.n
        shard = jnp.clip(me - s if d == 0 else me + s, 0, n - 1)
        return pltpu.make_async_remote_copy(
            src_ref=self.x if s == 0 else self.o.at[shard],
            dst_ref=self.o.at[shard],
            send_sem=self.send.at[d, s],
            recv_sem=self.recv.at[d, s],
            device_id={"tensor": jnp.clip(me + 1 if d == 0 else me - 1, 0, n - 1)},
            device_id_type=MESH,
        )

    def sends(self, d, s):
        me, n = self.me, self.n
        return (me - s >= 0) & (me < n - 1) if d == 0 else (me + s < n) & (me > 0)

    def wait(self, d, s):
        me, n = self.me, self.n

        @pl.when(me - 1 - s >= 0 if d == 0 else me + 1 + s < n)
        def _():
            shard = jnp.clip(me - 1 - s if d == 0 else me + 1 + s, 0, n - 1)
            pltpu.make_async_copy(self.o.at[shard], self.o.at[shard], self.recv.at[d, s]).wait()

    def step(self, s):
        for d in range(2):
            if s > 0:
                self.wait(d, s - 1)

            @pl.when(self.sends(d, s))
            def _():
                self.copy(d, s).start()

    def last(self):
        for d in range(2):
            self.wait(d, self.n - 2)

    def finish(self):
        for d in range(2):
            for s in range(self.n - 1):

                @pl.when(self.sends(d, s))
                def _():
                    self.copy(d, s).wait_send()


def gather_pieces_kernel(n, t_ref, gain_ref, shift_ref, full_ref, o_ref, f_ref, x_ref, held, s1, r1, s2, r2, s3, r3, loc):
    me, ctx, x = lax.axis_index("tensor"), lax.axis_index("context"), lax.axis_index("dp")
    place = ctx * 2 + x
    bar = pltpu.get_barrier_semaphore()
    met = line_greet(bar, me, n)
    for shift in range(1, 8):
        other = lax.rem(place + shift, 8)
        pl.semaphore_signal(
            bar, inc=1, device_id={"context": lax.div(other, 2), "dp": lax.rem(other, 2)}, device_id_type=MESH
        )
    normed, _ = norm_parts(t_ref[...].astype(jnp.float32))
    x_ref[...] = (normed * gain_ref[...] + shift_ref[...]).astype(x_ref.dtype)
    pl.semaphore_wait(bar, met + 7)
    tall, deep = held.shape[1:]
    w_ref = full_ref.at[
        pl.ds(pl.multiple_of((lax.div(ctx, 2) * 2 + x) * tall, 16), tall),
        pl.ds(pl.multiple_of(lax.rem(ctx, 2) * deep, 128), deep),
    ]
    small = LineGather(n, w_ref, held, s1, r1)
    large = LineGather(n, x_ref, o_ref, s2, r2)
    small.step(0)
    large.step(0)
    own = pltpu.make_async_copy(x_ref, o_ref.at[me], loc.at[0])
    own.start()
    piece = pltpu.make_async_copy(w_ref, held.at[me], loc.at[1])
    piece.start()
    piece.wait()
    for s in range(1, n - 1):
        small.step(s)
    small.last()

    def there(at):
        ctx_, x_ = lax.div(at, 2), lax.rem(at, 2)
        rows = pl.ds(pl.multiple_of((lax.div(ctx_, 2) * 2 + x_) * tall, 16), tall)
        cols = pl.ds(pl.multiple_of(lax.rem(ctx_, 2) * deep, 128), deep)
        return f_ref.at[:, rows, cols]

    def push(shift):
        other = lax.rem(place + shift, 8)
        return pltpu.make_async_remote_copy(
            src_ref=held,
            dst_ref=there(place),
            send_sem=s3.at[shift],
            recv_sem=r3.at[shift],
            device_id={"context": lax.div(other, 2), "dp": lax.rem(other, 2)},
            device_id_type=MESH,
        )

    for shift in range(1, 8):
        push(shift).start()
    kept = pltpu.make_async_copy(held, there(place), loc.at[2])
    kept.start()
    for s in range(1, n - 1):
        large.step(s)
    large.last()
    for shift in range(1, 8):
        source = there(lax.rem(place + 8 - shift, 8))
        pltpu.make_async_copy(source, source, r3.at[shift]).wait()
    kept.wait()
    own.wait()
    small.finish()
    large.finish()
    for shift in range(1, 8):
        push(shift).wait_send()


def gather_pieces(tokens, gain, shift, w, n, collective_id):
    rows, cols = tokens.shape
    wide, deep = w.shape
    full, weight = pl.pallas_call(
        functools.partial(gather_pieces_kernel, n),
        out_shape=(
            jax.ShapeDtypeStruct((n, rows, cols), jnp.bfloat16),
            jax.ShapeDtypeStruct((n, wide, deep), w.dtype),
        ),
        in_specs=[VM] * 4,
        out_specs=(VM, VM),
        scratch_shapes=[
            pltpu.VMEM((rows, cols), jnp.bfloat16),
            pltpu.VMEM((n, wide // 4, deep // 2), w.dtype),
        ]
        + [DMA((2, n - 1)) for _ in range(4)]
        + [DMA((8,)), DMA((8,)), DMA((3,))],
        compiler_params=remote_params(collective_id),
    )(tokens, gain[None], shift[None], w)
    return full.reshape(n * rows, cols), weight.reshape(n * wide, deep)


def dot(left, right, dims):
    return lax.dot_general(left, right, ((dims[0], dims[1]), ((), ())), preferred_element_type=jnp.float32)


def key_positions(first, keys, queries):
    return first + lax.broadcasted_iota(jnp.int32, (keys, queries), 0)


def load_rows(qkv_ref, nb, half, qs, kt, ks, vs):
    for block in range(nb):
        part = slice(block % 2 * half, block % 2 * half + half)
        at = block // 2
        qs[block] = qkv_ref[at, 0, :, part] * jnp.asarray(HEAD_DIM**-0.5, qs.dtype)
        item = qkv_ref[at, 1, :, part]
        if kt is not None:
            kt[block] = item
        ks[block] = item.T
        if vs is not None:
            vs[block] = qkv_ref[at, 2, :, part].T


def fill_tables(nb, half, seg_ref, order_ref, slot_ref, low_ref, high_ref):
    for block in range(nb):
        slot_ref[order_ref[block]] = jnp.int32(block)
    first = [seg_ref[0, block * half] for block in range(nb)]
    last = [seg_ref[0, block * half + half - 1] for block in range(nb)]
    for block in range(nb):
        if low_ref is not None:
            low_ref[block] = sum(jnp.where(item < first[block], 1, 0) for item in last)
        if high_ref is not None:
            high_ref[block] = sum(jnp.where(item <= last[block], 1, 0) for item in first)


def forward_kernel(half, heads, seg_s, order_ref, seg_ref, qkv_ref, o_ref, full_ref, lse_ref, start_ref, qs, ks, slot_ref, low_ref):
    nb = full_ref.shape[0]

    @pl.when(lax.axis_index("context") < heads)
    def _():
        load_rows(qkv_ref, nb, half, qs, None, ks, None)
        fill_tables(nb, half, seg_s, order_ref, slot_ref, low_ref, None)
        seg = seg_ref[...]
        start = jnp.zeros(seg.shape, jnp.float32)
        for doc in range(1, DOC_LIMIT):
            before = jnp.sum(jnp.where(seg < doc, 1.0, 0.0), axis=1, keepdims=True)
            start = jnp.where(seg == doc, before, start)
        start_ref[...] = start.astype(jnp.int32)

        @pl.loop(0, nb)
        def _(nq):
            slot = slot_ref[nq]
            query = qs[slot]
            begin = start_ref[:, pl.ds(pl.multiple_of(nq * half, 128), half)]
            here = nq * half + lax.broadcasted_iota(jnp.int32, (1, half), 1)

            def step(nk, state):
                top, total, acc = state
                at = slot_ref[nk]
                score = dot(ks[at], query, ((1,), (0,)))
                place = key_positions(nk * half, half, half)
                score = jnp.where((place >= begin) & (place <= here), score, NEG_FILL)
                new_top = jnp.maximum(top, jnp.max(score, axis=0, keepdims=True))
                factor = jnp.exp(top - new_top)
                weight = jnp.exp(score - new_top)
                total = total * factor + jnp.sum(weight, axis=0, keepdims=True)
                value = qkv_ref[at // 2, 2, :, pl.ds(pl.multiple_of(at % 2 * half, 128), half)]
                acc = acc * factor + dot(value, weight.astype(jnp.bfloat16), ((1,), (0,)))
                return new_top, total, acc

            top, total, acc = lax.fori_loop(
                low_ref[nq],
                nq + 1,
                step,
                (
                    jnp.full((1, half), NEG_FILL, jnp.float32),
                    jnp.zeros((1, half), jnp.float32),
                    jnp.zeros((HEAD_DIM, half), jnp.float32),
                ),
            )
            result = acc / total
            full_ref[slot] = result
            lse_ref[slot] = top + jnp.log(total)
            low = result.astype(jnp.bfloat16)
            o_ref[2 * slot] = low[:, : half // 2]
            o_ref[2 * slot + 1] = low[:, half // 2 :]


def attend_forward(qkv, segments, order, half, heads):
    nc = qkv.shape[0]
    nb = 2 * nc
    return pl.pallas_call(
        functools.partial(forward_kernel, half, heads),
        out_shape=(
            jax.ShapeDtypeStruct((2 * nb, HEAD_DIM, half // 2), jnp.bfloat16),
            jax.ShapeDtypeStruct((nb, HEAD_DIM, half), jnp.float32),
            jax.ShapeDtypeStruct((nb, 1, half), jnp.float32),
            jax.ShapeDtypeStruct(segments.shape, jnp.int32),
        ),
        in_specs=[SM, SM, VM, VM],
        out_specs=(VM, VM, VM, VM),
        scratch_shapes=[
            pltpu.VMEM((nb, HEAD_DIM, half), jnp.bfloat16),
            pltpu.VMEM((nb, half, HEAD_DIM), jnp.bfloat16),
            pltpu.SMEM((nb,), jnp.int32),
            pltpu.SMEM((nb,), jnp.int32),
        ],
        compiler_params=pltpu.CompilerParams(vmem_limit_bytes=48 << 20),
    )(segments, order, segments, qkv)


def backward_kernel(
    half, heads, seg_s, order_ref, start_ref, qkv_ref, full_ref, lse_ref, grad_ref, o_ref,
    qs, kt, ks, vs, gs, ds, dq, slot_ref, high_ref,
):
    nb = full_ref.shape[0]

    @pl.when(lax.axis_index("context") < heads)
    def _():
        load_rows(qkv_ref, nb, half, qs, kt, ks, vs)
        fill_tables(nb, half, seg_s, order_ref, slot_ref, None, high_ref)
        for block in range(nb):
            both = jnp.concatenate([grad_ref[2 * block], grad_ref[2 * block + 1]], axis=1)
            gs[block] = both
            ds[block] = jnp.sum(both.astype(jnp.float32) * full_ref[block], axis=0, keepdims=True)
            dq[block] = jnp.zeros((HEAD_DIM, half), jnp.float32)

        @pl.loop(0, nb)
        def _(nk):
            at = slot_ref[nk]
            place = key_positions(nk * half, half, half)

            def step(nq, state):
                grad_key, grad_value = state
                slot = slot_ref[nq]
                query, grad = qs[slot], gs[slot]
                begin = start_ref[:, pl.ds(pl.multiple_of(nq * half, 128), half)]
                here = nq * half + lax.broadcasted_iota(jnp.int32, (1, half), 1)
                score = dot(ks[at], query, ((1,), (0,)))
                score = jnp.where((place >= begin) & (place <= here), score, NEG_FILL)
                weight = jnp.exp(score - lse_ref[slot])
                grad_weight = dot(vs[at], grad, ((1,), (0,)))
                grad_score = (weight * (grad_weight - ds[slot])).astype(jnp.bfloat16)
                grad_value = grad_value + dot(grad, weight.astype(jnp.bfloat16), ((1,), (1,)))
                grad_key = grad_key + dot(query, grad_score, ((1,), (1,)))
                dq[slot] += dot(kt[at], grad_score, ((1,), (0,)))
                return grad_key, grad_value

            zero = jnp.zeros((HEAD_DIM, half), jnp.float32)
            grad_key, grad_value = lax.fori_loop(nk, high_ref[nk], step, (zero, zero))
            columns = pl.ds(pl.multiple_of(at % 2 * half, 128), half)
            o_ref[at // 2, 1, :, columns] = grad_key.astype(jnp.bfloat16)
            o_ref[at // 2, 2, :, columns] = grad_value.astype(jnp.bfloat16)

        for block in range(nb):
            part = slice(block % 2 * half, block % 2 * half + half)
            o_ref[block // 2, 0, :, part] = (dq[block] * HEAD_DIM**-0.5).astype(jnp.bfloat16)


def attend_backward(qkv, segments, order, start, full, lse, grad, half, heads):
    nc = qkv.shape[0]
    nb = 2 * nc
    low = jnp.bfloat16
    return pl.pallas_call(
        functools.partial(backward_kernel, half, heads),
        out_shape=jax.ShapeDtypeStruct(qkv.shape, low),
        in_specs=[SM, SM, VM, VM, VM, VM, VM],
        out_specs=VM,
        scratch_shapes=[
            pltpu.VMEM((nb, HEAD_DIM, half), low),
            pltpu.VMEM((nb, HEAD_DIM, half), low),
            pltpu.VMEM((nb, half, HEAD_DIM), low),
            pltpu.VMEM((nb, half, HEAD_DIM), low),
            pltpu.VMEM((nb, HEAD_DIM, half), low),
            pltpu.VMEM((nb, 1, half), jnp.float32),
            pltpu.VMEM((nb, HEAD_DIM, half), jnp.float32),
            pltpu.SMEM((nb,), jnp.int32),
            pltpu.SMEM((nb,), jnp.int32),
        ],
        compiler_params=pltpu.CompilerParams(vmem_limit_bytes=48 << 20),
    )(segments, order, start, qkv, full, lse, grad)


def norm_parts(values):
    centre = jnp.mean(values, axis=-1, keepdims=True)
    shifted = values - centre
    spread_ = jnp.mean(shifted * shifted, axis=-1, keepdims=True)
    scale = lax.rsqrt(spread_ + NORM_EPS)
    return shifted * scale, scale


def norm_backward(grad, normed, scale, gain):
    e = grad * gain
    mean_e = jnp.mean(e, axis=-1, keepdims=True)
    mean_en = jnp.mean(e * normed, axis=-1, keepdims=True)
    return (e - mean_e - normed * mean_en) * scale


def gelu_tanh(values):
    return jax.nn.gelu(values, approximate=True)


def cross_rows(left, right):
    return lax.dot_general(
        left, right, (((0,), (0,)), ((), ())), preferred_element_type=jnp.float32
    )


def after(value, done):
    return lax.optimization_barrier((value, done))[0]


def per_device(
    mesh_sizes,
    inputs,
    first_gain,
    first_shift,
    project_weight,
    project_bias,
    attend_weight,
    attend_bias,
    second_gain,
    second_shift,
    expand_weight,
    expand_bias,
    shrink_weight,
    shrink_bias,
    segments,
    block_order,
    cotangent,
):
    nt, nc = mesh_sizes["tensor"], mesh_sizes["context"]
    own_rows, width = inputs.shape[1], inputs.shape[2]
    local_width = project_weight.shape[2]
    heads = local_width // HEAD_DIM
    block_rows = own_rows * nt
    half = block_rows // 2
    low = jnp.bfloat16
    f32 = lambda value: value.astype(jnp.float32)
    square = nt == 4 and nc == 4 and mesh_sizes["dp"] == 2
    plane = ("context", "dp")

    tokens_own = f32(inputs[0])
    grad_out = cotangent[0]
    if square:
        hidden1_full, attend_full = gather_pieces(inputs[0], first_gain, first_shift, attend_weight, nt, 0)
    else:
        hidden1 = norm_parts(tokens_own)[0] * first_gain + first_shift
        hidden1_full = gather_rows(hidden1.astype(low), nt, 0)
        attend_full = lax.all_gather(attend_weight, "tensor", axis=0, tiled=True)
    grad_full = lax.all_gather(after(grad_out, hidden1_full), "tensor", axis=0, tiled=True)

    bias = jnp.stack([project_bias[0], jnp.zeros_like(project_bias[0]), project_bias[1]])[:, :, None]
    projected = jnp.einsum(
        "kde,rd->ker", project_weight, hidden1_full, preferred_element_type=jnp.float32
    )
    projected = (projected + bias).astype(low).reshape(3, heads, HEAD_DIM, block_rows)
    qkv = to_heads(projected, nc, 1)
    pieces, attended_full, lse, start = attend_forward(qkv, segments, block_order, half, heads)
    attended = to_rows(pieces, nc, nt, heads, 2).reshape(width, own_rows)

    middle = tokens_own + cross_rows(attended, attend_full) + attend_bias
    normed2, scale2 = norm_parts(middle)
    hidden2 = (normed2 * second_gain + second_shift).astype(low)
    grad_shrink_bias = jnp.sum(f32(grad_out), axis=0)
    if square:
        grad_hidden2, feed, grad_expand_bias, *feed_pieces = feed_part(
            hidden2, expand_weight, shrink_weight, expand_bias, grad_full, nt, 3
        )
        grad_expand_bias = grad_expand_bias[0]
    else:
        hidden2_full = gather_rows(hidden2, nt, 3)
        pre_act = jnp.dot(hidden2_full, expand_weight, preferred_element_type=jnp.float32) + expand_bias
        activ = gelu_tanh(pre_act).astype(low)
        grad_act = dot(grad_full, shrink_weight, ((1,), (1,)))
        grad_pre = jax.vjp(gelu_tanh, pre_act)[1](grad_act)[0].astype(low)
        grad_shrink = cross_rows(activ, grad_full).astype(low)
        grad_expand = cross_rows(hidden2_full, grad_pre).astype(low)
        grad_hidden2 = scatter_rows(dot(grad_pre, expand_weight, ((1,), (1,))).astype(low), nt, 4)
        grad_expand_bias = jnp.sum(f32(grad_pre), axis=0)
        feed = jnp.dot(activ, shrink_weight, preferred_element_type=jnp.float32).astype(low)

    grad_second_gain = jnp.sum(grad_hidden2 * normed2, axis=0)
    grad_second_shift = jnp.sum(grad_hidden2, axis=0)
    grad_middle = f32(grad_out) + norm_backward(grad_hidden2, normed2, scale2, second_gain)
    grad_middle_low = grad_middle.astype(low)
    grad_attend_bias = jnp.sum(f32(grad_middle_low), axis=0)
    grad_attended = dot(attend_full, grad_middle_low, ((1,), (1,))).astype(low)
    grad_attended = grad_attended.reshape(nt * heads, HEAD_DIM, own_rows)
    grad_attend = jnp.dot(attended, grad_middle_low, preferred_element_type=jnp.float32).astype(low)
    if square:
        unit = grad_attend.reshape(nt, local_width, width)
        grad_heads, attend_pieces = rows_back_sum(grad_attended, unit, nc, nt, heads, 5)
    else:
        grad_heads = rows_back(grad_attended, nc, nt, heads, 5)
        attend_pieces = None
    feed_sum = lax.psum_scatter(after(feed, grad_heads), "tensor", scatter_dimension=0, tiled=True)

    grad_qkv = attend_backward(qkv, segments, block_order, start, attended_full, lse, grad_heads, half, heads)
    grad_rows = from_heads(grad_qkv, attend_pieces, nc, nt, heads, 6)
    if square:
        grad_rows, attend_piece = grad_rows
    grad_rows = grad_rows.reshape(3 * local_width, block_rows)
    grad_project = dot(hidden1_full, grad_rows, ((0,), (1,))).astype(low)
    grad_hidden1 = lax.dot_general(
        grad_rows.reshape(3, local_width, block_rows),
        project_weight,
        (((0, 1), (0, 2)), ((), ())),
        preferred_element_type=jnp.float32,
    ).astype(low)
    row_sums = jnp.sum(f32(grad_rows), axis=1)
    grad_project_bias = jnp.concatenate([row_sums[:local_width], row_sums[2 * local_width :]])

    wide = grad_expand_bias.shape[0]
    spare = -(wide + 2 * local_width) % width
    others = [
        grad_attend_bias,
        grad_second_gain,
        grad_second_shift,
        grad_shrink_bias,
        grad_expand_bias,
        jnp.pad(grad_project_bias, (0, spare)),
    ]
    if square:
        empty = jnp.zeros((2 * width,), jnp.float32)
        vectors = jnp.concatenate([empty] + others).reshape(-1, width)
        grad_inputs, summed, grad_project, grad_attend, feeds = last_part(
            grad_hidden1,
            grad_project.reshape(16, -1, 3 * local_width),
            attend_piece,
            feed_pieces,
            inputs[0],
            first_gain[None],
            grad_middle,
            vectors,
            6,
            nt,
            7,
        )
        grad_project = grad_project.reshape(width, 3 * local_width)
        grad_shrink, grad_expand = feeds[0].reshape(-1, width), feeds[1].reshape(width, -1)
    else:
        grad_hidden1 = scatter_rows(grad_hidden1, nt, 7)
        normed1, scale1 = norm_parts(tokens_own)
        back = norm_backward(grad_hidden1, normed1, scale1, first_gain)
        grad_inputs = (grad_middle + back).astype(low)
        both = [jnp.sum(grad_hidden1 * normed1, axis=0), jnp.sum(grad_hidden1, axis=0)]
        vectors = jnp.concatenate(both + others).reshape(-1, width)
        summed = sum_vectors(vectors, 6, mesh_sizes, 8)
        grad_attend = lax.psum_scatter(grad_attend, "tensor", scatter_dimension=0, tiled=True)
        grad_project, grad_attend, grad_shrink, grad_expand = lax.psum(
            (grad_project, grad_attend, grad_shrink, grad_expand), plane
        )
    feed_sum = f32(after(feed_sum, summed))
    outputs = (middle + feed_sum + shrink_bias).astype(low)[None]
    grad_project = jnp.stack(
        [grad_project[:, at * local_width : (at + 1) * local_width] for at in range(3)]
    )
    tail = summed[6:].reshape(-1)
    return (
        outputs,
        grad_inputs[None],
        summed[0],
        summed[1],
        f32(grad_project),
        tail[wide : wide + 2 * local_width].reshape(2, local_width),
        f32(grad_attend),
        summed[2],
        summed[3],
        summed[4],
        f32(grad_expand),
        tail[:wide],
        f32(grad_shrink),
        summed[5],
    )


def solution(mesh):
    rows = P("dp", ("context", "tensor"), None)
    in_specs = (
        rows,
        P(),
        P(),
        P(None, None, "tensor"),
        P(None, "tensor"),
        P("tensor", None),
        P(),
        P(),
        P(),
        P(None, "tensor"),
        P("tensor"),
        P("tensor", None),
        P(),
        P("dp", None),
        P(),
        rows,
    )
    out_specs = (
        rows,
        rows,
        P(),
        P(),
        P(None, None, "tensor"),
        P(None, "tensor"),
        P("tensor", None),
        P(),
        P(),
        P(),
        P(None, "tensor"),
        P("tensor"),
        P("tensor", None),
        P(),
    )
    return jax.shard_map(
        functools.partial(per_device, dict(mesh.shape)),
        mesh=mesh,
        in_specs=in_specs,
        out_specs=out_specs,
        check_vma=False,
    )
```

```python
import functools

import jax
import jax.numpy as jnp
from jax import lax
from jax.experimental import pallas as pl
from jax.experimental.pallas import tpu as pltpu
from jax.sharding import PartitionSpec as P

HEAD_DIM = 64
NEG_FILL = -1e30
NORM_EPS = 1e-05
DOC_LIMIT = 16
MESH = pl.DeviceIdType.MESH
VM = pl.BlockSpec(memory_space=pltpu.VMEM)
SM = pl.BlockSpec(memory_space=pltpu.SMEM)
DMA = pltpu.SemaphoreType.DMA


def remote_params(collective_id):
    return pltpu.CompilerParams(
        collective_id=collective_id, has_side_effects=True, vmem_limit_bytes=48 << 20
    )


def line_barrier(me, n):
    bar = pltpu.get_barrier_semaphore()

    @pl.when(me > 0)
    def _():
        pl.semaphore_signal(bar, inc=1, device_id={"tensor": me - 1}, device_id_type=MESH)

    @pl.when(me < n - 1)
    def _():
        pl.semaphore_signal(bar, inc=1, device_id={"tensor": me + 1}, device_id_type=MESH)

    pl.semaphore_wait(bar, jnp.where(me > 0, 1, 0) + jnp.where(me < n - 1, 1, 0))


def gather_kernel(n, x_ref, o_ref, send, recv, loc):
    me = lax.axis_index("tensor")
    line_barrier(me, n)
    own = pltpu.make_async_copy(x_ref, o_ref.at[me], loc)
    own.start()

    def copy(d, s):
        shard = jnp.clip(me - s if d == 0 else me + s, 0, n - 1)
        return pltpu.make_async_remote_copy(
            src_ref=x_ref if s == 0 else o_ref.at[shard],
            dst_ref=o_ref.at[shard],
            send_sem=send.at[d, s],
            recv_sem=recv.at[d, s],
            device_id={"tensor": jnp.clip(me + 1 if d == 0 else me - 1, 0, n - 1)},
            device_id_type=MESH,
        )

    def sends(d, s):
        return (me - s >= 0) & (me < n - 1) if d == 0 else (me + s < n) & (me > 0)

    def gets(d, s):
        return me - 1 - s >= 0 if d == 0 else me + 1 + s < n

    def landed(d, s):
        shard = jnp.clip(me - 1 - s if d == 0 else me + 1 + s, 0, n - 1)
        return pltpu.make_async_copy(o_ref.at[shard], o_ref.at[shard], recv.at[d, s])

    for s in range(n - 1):
        for d in range(2):
            if s > 0:

                @pl.when(gets(d, s - 1))
                def _():
                    landed(d, s - 1).wait()

            @pl.when(sends(d, s))
            def _():
                copy(d, s).start()

    for d in range(2):

        @pl.when(gets(d, n - 2))
        def _():
            landed(d, n - 2).wait()

        for s in range(n - 1):

            @pl.when(sends(d, s))
            def _():
                copy(d, s).wait_send()

    own.wait()


def gather_rows(x, n, collective_id):
    rows, cols = x.shape
    return pl.pallas_call(
        functools.partial(gather_kernel, n),
        out_shape=jax.ShapeDtypeStruct((n, rows, cols), x.dtype),
        in_specs=[VM],
        out_specs=VM,
        scratch_shapes=[DMA((2, n - 1)), DMA((2, n - 1)), DMA],
        compiler_params=remote_params(collective_id),
    )(x).reshape(n * rows, cols)


def scatter_kernel(n, x_ref, o_ref, buf, tmp, send, recv):
    me = lax.axis_index("tensor")
    line_barrier(me, n)

    def term(d, k):
        return n - 1 - k if d == 0 else k

    def sends(d, k):
        return me < n - 1 - k if d == 0 else me > k

    def behind(d):
        return me > 0 if d == 0 else me < n - 1

    def copy(d, k, first):
        return pltpu.make_async_remote_copy(
            src_ref=x_ref.at[term(d, k)] if first else tmp.at[d, k],
            dst_ref=buf.at[d, k],
            send_sem=send.at[d, k],
            recv_sem=recv.at[d, k],
            device_id={"tensor": jnp.clip(me + 1 if d == 0 else me - 1, 0, n - 1)},
            device_id_type=MESH,
        )

    def landed(d, k):
        return pltpu.make_async_copy(buf.at[d, k], buf.at[d, k], recv.at[d, k])

    for d in range(2):

        @pl.when(jnp.logical_not(behind(d)))
        def _():
            for k in range(n - 1):
                copy(d, k, True).start()

    for k in range(n - 1):
        for d in range(2):

            @pl.when(behind(d) & sends(d, k))
            def _():
                landed(d, k).wait()
                both = buf[d, k].astype(jnp.float32) + x_ref[term(d, k)].astype(jnp.float32)
                tmp[d, k] = both.astype(tmp.dtype)
                copy(d, k, False).start()

    o_ref[...] = x_ref[me].astype(jnp.float32)
    for d in range(2):
        for k in range(n - 1):

            @pl.when(behind(d) & (me == term(d, k)))
            def _():
                landed(d, k).wait()
                o_ref[...] += buf[d, k].astype(jnp.float32)

    for d in range(2):
        for k in range(n - 1):

            @pl.when(sends(d, k))
            def _():
                copy(d, k, False).wait_send()


def scatter_rows(x, n, collective_id):
    rows, cols = x.shape
    own = rows // n
    return pl.pallas_call(
        functools.partial(scatter_kernel, n),
        out_shape=jax.ShapeDtypeStruct((own, cols), jnp.float32),
        in_specs=[VM],
        out_specs=VM,
        scratch_shapes=[
            pltpu.VMEM((2, n - 1, own, cols), x.dtype),
            pltpu.VMEM((2, n - 1, own, cols), x.dtype),
            DMA((2, n - 1)),
            DMA((2, n - 1)),
        ],
        compiler_params=remote_params(collective_id),
    )(x.reshape(n, own, cols))


def group_barrier(axes, sizes):
    mine = [lax.axis_index(name) for name in axes]
    place = sum_index(mine, sizes)
    total = 1
    for size in sizes:
        total *= size
    bar = pltpu.get_barrier_semaphore()
    for shift in range(1, total):
        other = lax.rem(place + shift, total)
        pl.semaphore_signal(bar, inc=1, device_id=spread(other, axes, sizes), device_id_type=MESH)
    pl.semaphore_wait(bar, total - 1)
    return place, total


def sum_index(mine, sizes):
    place = 0
    for at, size in zip(mine, sizes):
        place = place * size + at
    return place


def spread(place, axes, sizes):
    found = {}
    for name, size in reversed(tuple(zip(axes, sizes))):
        found[name] = lax.rem(place, size)
        place = lax.div(place, size)
    return found


def to_heads_kernel(nc, heads, x_ref, o_ref, send, recv, loc):
    me, _ = group_barrier(("context",), (nc,))

    def copy(shift):
        other = lax.rem(me + shift, nc)
        return other, pltpu.make_async_remote_copy(
            src_ref=x_ref.at[:, jnp.minimum(other, heads - 1)],
            dst_ref=o_ref.at[me],
            send_sem=send.at[shift],
            recv_sem=recv.at[shift],
            device_id={"context": other},
            device_id_type=MESH,
        )

    for shift in range(1, nc):
        other, item = copy(shift)

        @pl.when(other < heads)
        def _():
            item.start()

    own = pltpu.make_async_copy(x_ref.at[:, jnp.minimum(me, heads - 1)], o_ref.at[me], loc)
    own.start()
    own.wait()

    @pl.when(me < heads)
    def _():
        for shift in range(1, nc):
            source = lax.rem(me + nc - shift, nc)
            pltpu.make_async_copy(o_ref.at[source], o_ref.at[source], recv.at[shift]).wait()

    for shift in range(1, nc):
        other, item = copy(shift)

        @pl.when(other < heads)
        def _():
            item.wait_send()


def to_heads(x, nc, collective_id):
    heads = x.shape[1]
    return pl.pallas_call(
        functools.partial(to_heads_kernel, nc, heads),
        out_shape=jax.ShapeDtypeStruct((nc, x.shape[0]) + x.shape[2:], x.dtype),
        in_specs=[VM],
        out_specs=VM,
        scratch_shapes=[DMA((nc,)), DMA((nc,)), DMA],
        compiler_params=remote_params(collective_id),
    )(x)


def from_heads_kernel(nc, nt, heads, extra, x_ref, *rest):
    if extra:
        p_ref, o_ref, s_ref, send, recv, loc, land, zsend, zrecv = rest
    else:
        o_ref, send, recv, loc = rest
    me, ten = lax.axis_index("context"), lax.axis_index("tensor")
    bar = pltpu.get_barrier_semaphore()
    for shift in range(1, nc):
        pl.semaphore_signal(bar, inc=1, device_id={"context": lax.rem(me + shift, nc)}, device_id_type=MESH)
    if extra:
        for shift in range(1, nt):
            pl.semaphore_signal(bar, inc=1, device_id={"tensor": lax.rem(ten + shift, nt)}, device_id_type=MESH)
    pl.semaphore_wait(bar, nc - 1 + (nt - 1 if extra else 0))

    def copy(shift):
        other = lax.rem(me + shift, nc)
        return pltpu.make_async_remote_copy(
            src_ref=x_ref.at[other],
            dst_ref=o_ref.at[:, jnp.minimum(me, heads - 1)],
            send_sem=send.at[shift],
            recv_sem=recv.at[shift],
            device_id={"context": other},
            device_id_type=MESH,
        )

    def across(shift):
        other = lax.rem(ten + shift, nt)
        return pltpu.make_async_remote_copy(
            src_ref=p_ref.at[lax.div(other, 2), lax.rem(other, 2)],
            dst_ref=land.at[ten],
            send_sem=zsend.at[shift],
            recv_sem=zrecv.at[shift],
            device_id={"tensor": other},
            device_id_type=MESH,
        )

    if extra:
        for shift in range(1, nt):
            across(shift).start()

    @pl.when(me < heads)
    def _():
        for shift in range(1, nc):
            copy(shift).start()
        own = pltpu.make_async_copy(x_ref.at[me], o_ref.at[:, me], loc)
        own.start()
        own.wait()

    if extra:
        land[ten] = p_ref[lax.div(ten, 2), lax.rem(ten, 2)]
        for shift in range(1, nt):
            source = lax.rem(ten + nt - shift, nt)
            pltpu.make_async_copy(land.at[source], land.at[source], zrecv.at[shift]).wait()
        value = land[0].astype(jnp.float32)
        for at in range(1, nt):
            value = value + land[at].astype(jnp.float32)
        s_ref[...] = value.astype(s_ref.dtype)
        for shift in range(1, nt):
            across(shift).wait_send()

    for shift in range(1, nc):
        source = lax.rem(me + nc - shift, nc)

        @pl.when(source < heads)
        def _():
            at = jnp.minimum(source, heads - 1)
            pltpu.make_async_copy(o_ref.at[:, at], o_ref.at[:, at], recv.at[shift]).wait()

    @pl.when(me < heads)
    def _():
        for shift in range(1, nc):
            copy(shift).wait_send()


def from_heads(x, pieces, nc, nt, heads, collective_id):
    extra = pieces is not None
    out = jax.ShapeDtypeStruct((x.shape[1], heads) + x.shape[2:], x.dtype)
    scratch = [DMA((nc,)), DMA((nc,)), DMA]
    if extra:
        piece = pieces.shape[2:]
        scratch += [pltpu.VMEM((nt,) + piece, pieces.dtype), DMA((nt,)), DMA((nt,))]
        out = (out, jax.ShapeDtypeStruct(piece, pieces.dtype))
    return pl.pallas_call(
        functools.partial(from_heads_kernel, nc, nt, heads, extra),
        out_shape=out,
        in_specs=[VM] * (1 + extra),
        out_specs=(VM, VM) if extra else VM,
        scratch_shapes=scratch,
        compiler_params=remote_params(collective_id),
    )(*((x, pieces) if extra else (x,)))


AXES = ("context", "tensor")


def rows_kernel(nc, nt, heads, x_ref, o_ref, send, recv, loc):
    me, total = group_barrier(AXES, (nc, nt))
    my_ctx, my_ten = lax.axis_index("context"), lax.axis_index("tensor")
    my_head = my_ten * heads + jnp.minimum(my_ctx, heads - 1)

    def copy(shift):
        other = lax.rem(me + shift, total)
        return pltpu.make_async_remote_copy(
            src_ref=x_ref.at[other],
            dst_ref=o_ref.at[my_head],
            send_sem=send.at[shift],
            recv_sem=recv.at[shift],
            device_id=spread(other, AXES, (nc, nt)),
            device_id_type=MESH,
        )

    @pl.when(my_ctx < heads)
    def _():
        for shift in range(1, total):
            copy(shift).start()
        own = pltpu.make_async_copy(x_ref.at[me], o_ref.at[my_head], loc)
        own.start()
        own.wait()

    for shift in range(1, total):
        source = lax.rem(me + total - shift, total)
        ctx, ten = lax.div(source, nt), lax.rem(source, nt)

        @pl.when(ctx < heads)
        def _():
            at = ten * heads + jnp.minimum(ctx, heads - 1)
            pltpu.make_async_copy(o_ref.at[at], o_ref.at[at], recv.at[shift]).wait()

    @pl.when(my_ctx < heads)
    def _():
        for shift in range(1, total):
            copy(shift).wait_send()


def to_rows(x, nc, nt, heads, collective_id):
    total = nc * nt
    return pl.pallas_call(
        functools.partial(rows_kernel, nc, nt, heads),
        out_shape=jax.ShapeDtypeStruct((nt * heads,) + x.shape[1:], x.dtype),
        in_specs=[VM],
        out_specs=VM,
        scratch_shapes=[DMA((total,)), DMA((total,)), DMA],
        compiler_params=remote_params(collective_id),
    )(x)


def rows_back_kernel(nc, nt, heads, x_ref, o_ref, send, recv, loc):
    me, total = group_barrier(AXES, (nc, nt))
    my_ctx, my_ten = lax.axis_index("context"), lax.axis_index("tensor")

    def copy(shift):
        other = lax.rem(me + shift, total)
        ctx, ten = lax.div(other, nt), lax.rem(other, nt)
        return ctx < heads, pltpu.make_async_remote_copy(
            src_ref=x_ref.at[ten * heads + jnp.minimum(ctx, heads - 1)],
            dst_ref=o_ref.at[me],
            send_sem=send.at[shift],
            recv_sem=recv.at[shift],
            device_id={"context": ctx, "tensor": ten},
            device_id_type=MESH,
        )

    for shift in range(1, total):
        goes, item = copy(shift)

        @pl.when(goes)
        def _():
            item.start()

    own = pltpu.make_async_copy(
        x_ref.at[my_ten * heads + jnp.minimum(my_ctx, heads - 1)], o_ref.at[me], loc
    )
    own.start()
    own.wait()

    @pl.when(my_ctx < heads)
    def _():
        for shift in range(1, total):
            source = lax.rem(me + total - shift, total)
            pltpu.make_async_copy(o_ref.at[source], o_ref.at[source], recv.at[shift]).wait()

    for shift in range(1, total):
        goes, item = copy(shift)

        @pl.when(goes)
        def _():
            item.wait_send()


def rows_back(x, nc, nt, heads, collective_id):
    total = nc * nt
    return pl.pallas_call(
        functools.partial(rows_back_kernel, nc, nt, heads),
        out_shape=jax.ShapeDtypeStruct((total,) + x.shape[1:], x.dtype),
        in_specs=[VM],
        out_specs=VM,
        scratch_shapes=[DMA((total,)), DMA((total,)), DMA],
        compiler_params=remote_params(collective_id),
    )(x)


def vectors_kernel(names, sizes, shared, x_ref, o_ref, now, *rest):
    bufs, sems = rest[: len(names)], rest[len(names) :]
    bar = pltpu.get_barrier_semaphore()
    for name, size in zip(names, sizes):
        me = lax.axis_index(name)
        for shift in range(1, size):
            pl.semaphore_signal(
                bar, inc=1, device_id={name: lax.rem(me + shift, size)}, device_id_type=MESH
            )
    pl.semaphore_wait(bar, sum(sizes) - len(sizes))
    for stage, (name, size) in enumerate(zip(names, sizes)):
        buf, send, recv = bufs[stage], sems[2 * stage], sems[2 * stage + 1]
        me = lax.axis_index(name)

        def copy(shift):
            return pltpu.make_async_remote_copy(
                src_ref=now.at[stage] if stage else x_ref.at[0],
                dst_ref=buf.at[me],
                send_sem=send.at[shift],
                recv_sem=recv.at[shift],
                device_id={name: lax.rem(me + shift, size)},
                device_id_type=MESH,
            )

        for shift in range(1, size):
            copy(shift).start()
        buf[me] = now[stage] if stage else x_ref[0]
        for shift in range(1, size):
            source = lax.rem(me + size - shift, size)
            pltpu.make_async_copy(buf.at[source], buf.at[source], recv.at[shift]).wait()
        total = buf[0]
        for at in range(1, size):
            total = total + buf[at]
        if stage == 0:
            row = lax.broadcasted_iota(jnp.int32, total.shape, 0)
            total = jnp.where(row < shared, total, x_ref[0])
        if stage + 1 < len(names):
            now[stage + 1] = total
        else:
            o_ref[...] = total
        for shift in range(1, size):
            copy(shift).wait_send()


def sum_vectors(rows, shared, mesh_sizes, collective_id):
    names = ("tensor", "context", "dp")
    sizes = tuple(mesh_sizes[name] for name in names)
    shape = rows.shape
    return pl.pallas_call(
        functools.partial(vectors_kernel, names, sizes, shared),
        out_shape=jax.ShapeDtypeStruct(shape, jnp.float32),
        in_specs=[VM],
        out_specs=VM,
        scratch_shapes=[pltpu.VMEM((len(names),) + shape, jnp.float32)]
        + [pltpu.VMEM((size,) + shape, jnp.float32) for size in sizes]
        + [DMA((size,)) for size in sizes for _ in range(2)],
        compiler_params=remote_params(collective_id),
    )(rows[None])


class PlaneSum:
    def __init__(self, u, p, o, bufs=None, spread=None):
        self.u, self.p, self.o = u, p, o
        if bufs is not None:
            self.rc, self.s1, self.ra, self.rb, self.sa, self.sb, self.ta, self.tb = bufs[:8]
            self.send1, self.recv1 = bufs[8:]
        if spread is not None:
            self.send2, self.recv2, self.loc = spread
        ctx, self.x = lax.axis_index("context"), lax.axis_index("dp")
        self.core, self.y = lax.rem(ctx, 2), lax.div(ctx, 2)
        self.chip_peer = {"context": ctx + 1 - 2 * self.core}
        self.y_peer = {"context": lax.rem(ctx + 2, 4)}
        self.x_peer = {"dp": 1 - self.x}

    @staticmethod
    def reduce_scratch(shape, dtype):
        tail = tuple(shape[1:])
        bufs = [pltpu.VMEM((count,) + tail, dtype) for count in (8, 8, 2, 2, 2, 2, 1, 1)]
        return bufs + [DMA((5,)), DMA((5,))]

    @staticmethod
    def spread_scratch():
        return [DMA((5,)), DMA((5,)), DMA((2,))]

    @staticmethod
    def greet(bar):
        ctx, x = lax.axis_index("context"), lax.axis_index("dp")
        for peer in (
            {"context": ctx + 1 - 2 * lax.rem(ctx, 2)},
            {"context": lax.rem(ctx + 2, 4)},
            {"dp": 1 - x},
        ):
            pl.semaphore_signal(bar, inc=1, device_id=peer, device_id_type=MESH)
        return 3

    def copy(self, at, src, dst, peer):
        send, recv = (self.send1, self.recv1) if at < 5 else (self.send2, self.recv2)
        return pltpu.make_async_remote_copy(
            src_ref=src,
            dst_ref=dst,
            send_sem=send.at[at % 5],
            recv_sem=recv.at[at % 5],
            device_id=peer,
            device_id_type=MESH,
        )

    def got(self, at, ref):
        recv = self.recv1 if at < 5 else self.recv2
        pltpu.make_async_copy(ref, ref, recv.at[at % 5]).wait()

    def add(self, out, left, right):
        f32 = jnp.float32
        out[...] = (left[...].astype(f32) + right[...].astype(f32)).astype(out.dtype)

    def mine(self, half):
        if half == 0:
            return pl.ds(self.core * 8 + 2 * self.x + self.y, 1)
        return pl.ds(self.core * 8 + 4 + 2 * self.y + self.x, 1)

    def hop(self, at):
        x, y, core = self.x, self.y, self.core
        o, p = self.o, self.p
        pair_a, pair_b = pl.ds(core * 8 + 2 * x, 2), pl.ds(core * 8 + 4 + 2 * y, 2)
        one = lambda at: pl.ds(at, 1)
        return [
            lambda: self.copy(0, self.by_core(1 - core), self.rc, self.chip_peer),
            lambda: self.copy(1, self.quarter(0, 1 - x), self.ra, self.x_peer),
            lambda: self.copy(2, self.quarter(1, 1 - y), self.rb, self.y_peer),
            lambda: self.copy(3, self.eighth(0, 1 - y), self.ta, self.y_peer),
            lambda: self.copy(4, self.eighth(1, 1 - x), self.tb, self.x_peer),
            lambda: self.copy(5, p.at[one(0)], o.at[self.mine(0)], self.y_peer),
            lambda: self.copy(6, p.at[one(1)], o.at[self.mine(1)], self.x_peer),
            lambda: self.copy(7, o.at[pair_a], o.at[pair_a], self.x_peer),
            lambda: self.copy(8, o.at[pair_b], o.at[pair_b], self.y_peer),
            lambda: self.copy(9, o.at[pl.ds(core * 8, 8)], o.at[pl.ds(core * 8, 8)], self.chip_peer),
        ][at]()

    def begin(self):
        self.hop(0).start()

    def by_core(self, core):
        return self.u.at[pl.ds(core * 8, 8)]

    def quarter(self, half, at):
        return self.s1.at[pl.ds(4 * half + 2 * at, 2)]

    def eighth(self, half, at):
        return (self.sa, self.sb)[half].at[pl.ds(at, 1)]

    def result(self, half):
        return self.p.at[pl.ds(half, 1)]

    def first(self):
        self.got(0, self.rc)
        self.add(self.s1, self.by_core(self.core), self.rc)
        self.hop(1).start()
        self.hop(2).start()

    def second(self):
        self.got(1, self.ra)
        self.add(self.sa, self.quarter(0, self.x), self.ra)
        self.hop(3).start()
        self.got(2, self.rb)
        self.add(self.sb, self.quarter(1, self.y), self.rb)
        self.hop(4).start()

    def third(self):
        self.got(3, self.ta)
        self.add(self.result(0), self.eighth(0, self.y), self.ta)
        self.got(4, self.tb)
        self.add(self.result(1), self.eighth(1, self.x), self.tb)

    def reduced(self):
        for at in range(5):
            self.hop(at).wait_send()

    def kept(self, half):
        return pltpu.make_async_copy(self.p.at[pl.ds(half, 1)], self.o.at[self.mine(half)], self.loc.at[half])

    def spread1(self):
        self.hop(5).start()
        self.hop(6).start()
        self.kept(0).start()
        self.kept(1).start()

    def spread2(self):
        x, y, core = self.x, self.y, self.core
        self.kept(0).wait()
        self.got(5, self.o.at[pl.ds(core * 8 + 2 * x + 1 - y, 1)])
        self.hop(7).start()
        self.kept(1).wait()
        self.got(6, self.o.at[pl.ds(core * 8 + 4 + 2 * y + 1 - x, 1)])
        self.hop(8).start()

    def spread3(self):
        x, y, core = self.x, self.y, self.core
        self.got(7, self.o.at[pl.ds(core * 8 + 2 - 2 * x, 2)])
        self.got(8, self.o.at[pl.ds(core * 8 + 6 - 2 * y, 2)])
        self.hop(9).start()

    def everywhere(self):
        self.got(9, self.o.at[pl.ds(8 - self.core * 8, 8)])
        for at in range(5, 10):
            self.hop(at).wait_send()


class StripSum(PlaneSum):
    @staticmethod
    def reduce_scratch(shape, dtype):
        _, rows, cols = shape
        shapes = [(4, rows)] * 2 + [(2, rows // 2)] * 4 + [(2, rows // 4)] * 2
        return [pltpu.VMEM(item + (cols // 2,), dtype) for item in shapes] + [DMA((5,)), DMA((5,))]

    def by_core(self, core):
        size = self.u.shape[2] // 2
        return self.u.at[:, :, pl.ds(pl.multiple_of(core * size, 128), size)]

    def quarter(self, half, at):
        size = self.s1.shape[1] // 2
        return self.s1.at[pl.ds(2 * half, 2), pl.ds(pl.multiple_of(at * size, 16), size)]

    def eighth(self, half, at):
        size = self.sa.shape[1] // 2
        return (self.sa, self.sb)[half].at[:, pl.ds(pl.multiple_of(at * size, 16), size)]

    def result(self, half):
        return self.p.at[half]


def unit_pieces(unit):
    return jax.ShapeDtypeStruct((2,) + unit.shape[1:], unit.dtype)


def line_greet(bar, me, n):
    @pl.when(me > 0)
    def _():
        pl.semaphore_signal(bar, inc=1, device_id={"tensor": me - 1}, device_id_type=MESH)

    @pl.when(me < n - 1)
    def _():
        pl.semaphore_signal(bar, inc=1, device_id={"tensor": me + 1}, device_id_type=MESH)

    return jnp.where(me > 0, 1, 0) + jnp.where(me < n - 1, 1, 0)


class LineScatter:
    def __init__(self, n, x, o, buf, tmp, send, recv):
        self.n, self.x, self.o, self.buf, self.tmp, self.send, self.recv = n, x, o, buf, tmp, send, recv
        self.me = lax.axis_index("tensor")

    @staticmethod
    def scratch(n, own, cols, dtype):
        return [
            pltpu.VMEM((2, n - 1, own, cols), dtype),
            pltpu.VMEM((2, n - 1, own, cols), dtype),
            DMA((2, n - 1)),
            DMA((2, n - 1)),
        ]

    def term(self, d, k):
        return self.n - 1 - k if d == 0 else k

    def sends(self, d, k):
        return self.me < self.n - 1 - k if d == 0 else self.me > k

    def behind(self, d):
        return self.me > 0 if d == 0 else self.me < self.n - 1

    def copy(self, d, k, first):
        return pltpu.make_async_remote_copy(
            src_ref=self.x.at[self.term(d, k)] if first else self.tmp.at[d, k],
            dst_ref=self.buf.at[d, k],
            send_sem=self.send.at[d, k],
            recv_sem=self.recv.at[d, k],
            device_id={"tensor": jnp.clip(self.me + 1 if d == 0 else self.me - 1, 0, self.n - 1)},
            device_id_type=MESH,
        )

    def landed(self, d, k):
        return pltpu.make_async_copy(self.buf.at[d, k], self.buf.at[d, k], self.recv.at[d, k])

    def begin(self):
        for d in range(2):

            @pl.when(jnp.logical_not(self.behind(d)))
            def _():
                for k in range(self.n - 1):
                    self.copy(d, k, True).start()

    def step(self, k):
        for d in range(2):

            @pl.when(self.behind(d) & self.sends(d, k))
            def _():
                self.landed(d, k).wait()
                at = self.term(d, k)
                both = self.buf[d, k].astype(jnp.float32) + self.x[at].astype(jnp.float32)
                self.tmp[d, k] = both.astype(self.tmp.dtype)
                self.copy(d, k, False).start()

    def end(self):
        self.o[...] = self.x[self.me].astype(jnp.float32)
        for d in range(2):
            for k in range(self.n - 1):

                @pl.when(self.behind(d) & (self.me == self.term(d, k)))
                def _():
                    self.landed(d, k).wait()
                    self.o[...] += self.buf[d, k].astype(jnp.float32)

        for d in range(2):
            for k in range(self.n - 1):

                @pl.when(self.sends(d, k))
                def _():
                    self.copy(d, k, False).wait_send()


GELU_SCALE = 0.7978845608028654
GELU_CUBE = 0.044715


def feed_kernel(n, nc, heads, chunks, piece_ref, *rest):
    (token_ref, out_ref, abias_ref, gain_ref, shift_ref, up_hbm, down_hbm, bias_ref, grad_hbm), rest = rest[:9], rest[9:]
    (o_ref, feed_ref, sum_ref, p1_ref, p2_ref, middle_ref, att_ref), rest = rest[:7], rest[7:]
    (x_ref, up_ref, down_ref, grad_ref, wsem, asend, arecv, aloc), rest = rest[:8], rest[8:]
    (held, act, gp, part, acc, buf, tmp, u1, u2), rest = rest[:9], rest[9:]
    (gsend, grecv, loc, ssend, srecv), rest = rest[:5], rest[5:]
    plane = [PlaneSum(u1, p1_ref, None, rest[:10]), PlaneSum(u2, p2_ref, None, rest[10:20])]
    me = lax.axis_index("tensor")
    rows, width = token_ref.shape
    wide = up_ref.shape[1]
    few = rows // chunks
    f32, low = jnp.float32, jnp.bfloat16
    ctx, dp = lax.axis_index("context"), lax.axis_index("dp")
    place, total = ctx * n + me, nc * n
    my_head = me * heads + jnp.minimum(ctx, heads - 1)
    bar = pltpu.get_barrier_semaphore()
    for shift in range(1, total):
        other = lax.rem(place + shift, total)
        pl.semaphore_signal(bar, inc=1, device_id=spread(other, AXES, (nc, n)), device_id_type=MESH)
    pl.semaphore_signal(bar, inc=1, device_id={"dp": 1 - dp}, device_id_type=MESH)
    weights_in = [
        pltpu.make_async_copy(src, dst, wsem.at[at])
        for at, (src, dst) in enumerate(((up_hbm, up_ref), (down_hbm, down_ref), (grad_hbm, grad_ref)))
    ]
    for item in weights_in:
        item.start()
    pl.semaphore_wait(bar, total)

    def to_place(shift):
        other = lax.rem(place + shift, total)
        return pltpu.make_async_remote_copy(
            src_ref=piece_ref.at[other],
            dst_ref=att_ref.at[my_head],
            send_sem=asend.at[shift],
            recv_sem=arecv.at[shift],
            device_id=spread(other, AXES, (nc, n)),
            device_id_type=MESH,
        )

    @pl.when(ctx < heads)
    def _():
        for shift in range(1, total):
            to_place(shift).start()
        stay = pltpu.make_async_copy(piece_ref.at[place], att_ref.at[my_head], aloc)
        stay.start()
        stay.wait()

    for shift in range(1, total):
        source = lax.rem(place + total - shift, total)
        at_ctx, at_ten = lax.div(source, n), lax.rem(source, n)

        @pl.when(at_ctx < heads)
        def _():
            landed = att_ref.at[at_ten * heads + jnp.minimum(at_ctx, heads - 1)]
            pltpu.make_async_copy(landed, landed, arecv.at[shift]).wait()

    attended = att_ref[...].reshape(width, rows)
    middle = token_ref[...].astype(f32) + dot(attended, out_ref[...], ((0,), (0,))) + abias_ref[...]
    middle_ref[...] = middle
    x_ref[...] = (norm_parts(middle)[0] * gain_ref[...] + shift_ref[...]).astype(low)

    @pl.when(ctx < heads)
    def _():
        for shift in range(1, total):
            to_place(shift).wait_send()

    def rows_of(block):
        return pl.ds(pl.multiple_of(block * rows, rows), rows)

    def neighbour(d):
        return {"tensor": jnp.clip(jnp.where(d == 0, me + 1, me - 1), 0, n - 1)}

    def onward(d):
        return jnp.where(d == 0, me, n - 1 - me) < n - 1

    def hand_on(d, s, block, first):
        return pltpu.make_async_remote_copy(
            src_ref=x_ref if first else held.at[rows_of(block)],
            dst_ref=held.at[rows_of(block)],
            send_sem=gsend.at[d, s],
            recv_sem=grecv.at[d, s],
            device_id=neighbour(d),
            device_id_type=MESH,
        )

    def chunk(block, c):
        return pl.ds(pl.multiple_of(block * rows + c * few, few), few)

    def back(d, block, c, first):
        at = chunk(block, c)
        return pltpu.make_async_remote_copy(
            src_ref=part.at[at] if first else tmp.at[at],
            dst_ref=buf.at[d, at],
            send_sem=ssend.at[block, c],
            recv_sem=srecv.at[d, block, c],
            device_id=neighbour(d),
            device_id_type=MESH,
        )

    for d in range(2):

        @pl.when(onward(d))
        def _():
            hand_on(d, 0, me, True).start()

    own = pltpu.make_async_copy(x_ref, held.at[rows_of(me)], loc)
    own.start()
    sum_ref[...] = jnp.zeros_like(sum_ref)
    own.wait()
    for item in weights_in:
        item.wait()
    columns = 256

    def work(block):
        here = rows_of(block)
        acc[...] = jnp.zeros_like(acc)

        @pl.loop(0, wide // columns)
        def _(j):
            at = pl.ds(pl.multiple_of(j * columns, columns), columns)
            pre = dot(held[here, :], up_ref[:, at], ((1,), (0,))) + bias_ref[:, at]
            square = pre * pre
            tanh = jnp.tanh(GELU_SCALE * pre * (1.0 + GELU_CUBE * square))
            act[here, at] = (0.5 * pre * (1.0 + tanh)).astype(low)
            slope = 0.5 * (1.0 + tanh) + 0.5 * pre * (1.0 - tanh * tanh) * (
                GELU_SCALE * (1.0 + 3.0 * GELU_CUBE * square)
            )
            grad = (dot(grad_ref[here, :], down_ref[at, :], ((1,), (1,))) * slope).astype(low)
            gp[here, at] = grad
            acc[...] += dot(grad, up_ref[:, at], ((1,), (1,)))

        part[here, :] = acc[...].astype(low)
        sum_ref[...] += jnp.sum(gp[here, :].astype(f32), axis=0, keepdims=True)

    near = jnp.minimum(me, n - 1 - me)
    toward = jnp.where(2 * me < n - 1, -1, 1)

    @pl.loop(0, n)
    def _(slot):
        paired = slot <= 2 * near
        distance = jnp.where(paired, lax.div(slot + 1, 2), slot - near)
        side = jnp.where(paired & (lax.rem(slot, 2) == 1), toward, -toward)
        block = me + side * distance
        d = jnp.where(block < me, 0, 1)
        s = jnp.maximum(distance - 1, 0)

        @pl.when(slot > 0)
        def _():
            landed = held.at[rows_of(block)]
            pltpu.make_async_copy(landed, landed, grecv.at[d, s]).wait()

            @pl.when(onward(d))
            def _():
                hand_on(d, jnp.minimum(s + 1, n - 2), block, False).start()

        work(block)

        @pl.when((slot > 0) & ((me == 0) | (me == n - 1)))
        def _():
            for c in range(chunks):
                back(1 - d, block, c, True).start()

    def weights(left, right, unit):
        half = wide // 2

        @pl.loop(0, 2)
        def _(j):
            at = pl.ds(pl.multiple_of(j * half, 128), half)
            total = dot(left[:, at], right[...], ((0,), (0,)))
            unit[pl.ds(8 * j, 8)] = total.astype(low).reshape((8,) + unit.shape[1:])

    weights(act, grad_ref, u1)
    plane[0].begin()
    weights(held, gp, u2)
    plane[1].begin()

    def relay(way, block):
        d = jnp.where(way > 0, 0, 1)

        @pl.when((me > 0) & (me < n - 1) & (block >= 0) & (block < n))
        def _():
            for c in range(chunks):
                at = chunk(block, c)
                landed = buf.at[d, at]
                pltpu.make_async_copy(landed, landed, srecv.at[d, block, c]).wait()
                tmp[at, :] = (buf[d, at, :].astype(f32) + part[at, :].astype(f32)).astype(low)
                back(d, block, c, False).start()

    plane[0].first()
    for j in range(1, n):
        relay(-toward, me - toward * j)
        if j == 1:
            plane[1].first()

    @pl.loop(0, n)
    def _(block):
        here = rows_of(block)
        feed_ref[here, :] = dot(act[here, :], down_ref[...], ((1,), (0,))).astype(low)

    plane[0].second()
    plane[1].second()
    for j in range(1, n):
        relay(toward, me + toward * j)
    for item in plane:
        item.third()
    for c in range(chunks):
        at = chunk(me, c)
        mine = pl.ds(c * few, few)
        o_ref[mine, :] = part[at, :].astype(f32)
        for d in range(2):

            @pl.when(me > 0 if d == 0 else me < n - 1)
            def _():
                landed = buf.at[d, at]
                pltpu.make_async_copy(landed, landed, srecv.at[d, me, c]).wait()
                o_ref[mine, :] += buf[d, at, :].astype(f32)

    for d in range(2):
        for s in range(n - 1):
            block = me - s if d == 0 else me + s

            @pl.when(onward(d) & (block >= 0) & (block < n))
            def _():
                hand_on(d, s, me, True).wait_send()

    for block in range(n):

        @pl.when(me != block)
        def _():
            for c in range(chunks):
                back(jnp.where(me < block, 0, 1), block, c, True).wait_send()

    for item in plane:
        item.reduced()


def feed_part(pieces, tokens, out_weight, vectors, up, down, bias, grad, n, nc, heads, collective_id):
    rows, width = tokens.shape
    wide = up.shape[1]
    chunks = 2
    total = n * rows
    low, f32 = jnp.bfloat16, jnp.float32
    unit = (16, wide // 16, width)
    piece = jax.ShapeDtypeStruct((2,) + unit[1:], low)
    anywhere = pl.BlockSpec(memory_space=pl.ANY)
    return pl.pallas_call(
        functools.partial(feed_kernel, n, nc, heads, chunks),
        out_shape=(
            jax.ShapeDtypeStruct((rows, width), f32),
            jax.ShapeDtypeStruct((total, width), low),
            jax.ShapeDtypeStruct((1, wide), f32),
            piece,
            piece,
            jax.ShapeDtypeStruct((rows, width), f32),
            jax.ShapeDtypeStruct((n * heads,) + pieces.shape[1:], low),
        ),
        in_specs=[VM] * 6 + [anywhere, anywhere, VM, anywhere],
        out_specs=(VM,) * 7,
        scratch_shapes=[
            pltpu.VMEM((rows, width), low),
            pltpu.VMEM(up.shape, low),
            pltpu.VMEM(down.shape, low),
            pltpu.VMEM(grad.shape, low),
            DMA((3,)),
            DMA((nc * n,)),
            DMA((nc * n,)),
            DMA,
            pltpu.VMEM((total, width), low),
            pltpu.VMEM((total, wide), low),
            pltpu.VMEM((total, wide), low),
            pltpu.VMEM((total, width), low),
            pltpu.VMEM((rows, width), f32),
            pltpu.VMEM((2, total, width), low),
            pltpu.VMEM((total, width), low),
            pltpu.VMEM(unit, low),
            pltpu.VMEM(unit, low),
            DMA((2, n - 1)),
            DMA((2, n - 1)),
            DMA,
            DMA((n, chunks)),
            DMA((2, n, chunks)),
        ]
        + PlaneSum.reduce_scratch(unit, low) * 2,
        compiler_params=remote_params(collective_id),
    )(pieces, tokens, out_weight, *(item[None] for item in vectors), up, down, bias[None], grad)


def last_kernel(n, shared, count, x_ref, u_ref, a_ref, *rest):
    ps, rest = rest[:count], rest[count:]
    token_ref, gain_ref, middle_ref, vec_ref, rest = rest[0], rest[1], rest[2], rest[3], rest[4:]
    g_ref, v_ref, po_ref, ao_ref, rest = rest[0], rest[1], rest[2], rest[3], rest[4:]
    outs, rest = rest[:count], rest[count:]
    sum_ref, piece, rest = rest[0], rest[1], rest[2:]
    line = LineScatter(n, x_ref, sum_ref, *rest[:4])
    project = PlaneSum(u_ref, piece, po_ref, rest[4:14], rest[14:17])
    rest = rest[17:]
    feeds = [PlaneSum(None, ps[i], outs[i], None, rest[3 * i : 3 * i + 3]) for i in range(count)]
    rest = rest[3 * count :]
    asend, arecv, aloc, now, rest = rest[0], rest[1], rest[2], rest[3], rest[4:]
    names, sizes = ("tensor", "context", "dp"), (n, 4, 2)
    bufs, sems = rest[:3], rest[3:]

    ten, ctx, x = (lax.axis_index(name) for name in names)
    place = ctx * 2 + x
    bar = pltpu.get_barrier_semaphore()
    for shift in range(1, n):
        pl.semaphore_signal(bar, inc=1, device_id={"tensor": lax.rem(ten + shift, n)}, device_id_type=MESH)
    for shift in range(1, 8):
        other = lax.rem(place + shift, 8)
        pl.semaphore_signal(
            bar, inc=1, device_id={"context": lax.div(other, 2), "dp": lax.rem(other, 2)}, device_id_type=MESH
        )
    pl.semaphore_wait(bar, n + 6)

    def there(at):
        ctx_, x_ = lax.div(at, 2), lax.rem(at, 2)
        y_ = lax.div(ctx_, 2)
        row = jnp.where(ten < n // 2, 2 * x_ + y_, 2 * y_ + x_)
        rows = pl.ds(pl.multiple_of(row * a_ref.shape[0], 16), a_ref.shape[0])
        cols = pl.ds(pl.multiple_of(lax.rem(ctx_, 2) * a_ref.shape[1], 128), a_ref.shape[1])
        return ao_ref.at[rows, cols]

    def push(shift):
        other = lax.rem(place + shift, 8)
        return pltpu.make_async_remote_copy(
            src_ref=a_ref,
            dst_ref=there(place),
            send_sem=asend.at[shift],
            recv_sem=arecv.at[shift],
            device_id={"context": lax.div(other, 2), "dp": lax.rem(other, 2)},
            device_id_type=MESH,
        )

    line.begin()
    project.begin()
    for item in feeds:
        item.spread1()
    for shift in range(1, 8):
        push(shift).start()
    kept = pltpu.make_async_copy(a_ref, there(place), aloc)
    kept.start()
    normed, scale = norm_parts(token_ref[...].astype(jnp.float32))
    project.first()
    line.step(0)
    for item in feeds:
        item.spread2()
    project.second()
    for k in range(1, n - 1):
        line.step(k)
    for item in feeds:
        item.spread3()
    project.third()
    project.spread1()
    line.end()
    grad = sum_ref[...]
    now[0] = vec_ref[...]
    now[0, 0:1] = jnp.sum(grad * normed, axis=0, keepdims=True)
    now[0, 1:2] = jnp.sum(grad, axis=0, keepdims=True)

    def stage_copy(stage, shift):
        name, size = names[stage], sizes[stage]
        me = lax.axis_index(name)
        return pltpu.make_async_remote_copy(
            src_ref=now.at[stage],
            dst_ref=bufs[stage].at[me],
            send_sem=sems[2 * stage].at[shift],
            recv_sem=sems[2 * stage + 1].at[shift],
            device_id={name: lax.rem(me + shift, size)},
            device_id_type=MESH,
        )

    def stage_start(stage):
        for shift in range(1, sizes[stage]):
            stage_copy(stage, shift).start()
        bufs[stage][lax.axis_index(names[stage])] = now[stage]

    def stage_end(stage):
        buf, size = bufs[stage], sizes[stage]
        me = lax.axis_index(names[stage])
        for shift in range(1, size):
            source = lax.rem(me + size - shift, size)
            pltpu.make_async_copy(buf.at[source], buf.at[source], sems[2 * stage + 1].at[shift]).wait()
        total = buf[0]
        for at in range(1, size):
            total = total + buf[at]
        if stage == 0:
            row = lax.broadcasted_iota(jnp.int32, total.shape, 0)
            total = jnp.where(row < shared, total, vec_ref[...])
        if stage < 2:
            now[stage + 1] = total
        else:
            v_ref[...] = total

    stage_start(0)
    back = norm_backward(grad, normed, scale, gain_ref[...])
    g_ref[...] = (middle_ref[...] + back).astype(g_ref.dtype)
    project.spread2()
    stage_end(0)
    stage_start(1)
    project.spread3()
    stage_end(1)
    stage_start(2)
    kept.wait()
    for shift in range(1, 8):
        source = there(lax.rem(place + 8 - shift, 8))
        pltpu.make_async_copy(source, source, arecv.at[shift]).wait()
    for item in feeds:
        item.everywhere()
    stage_end(2)
    project.everywhere()
    project.reduced()
    for shift in range(1, 8):
        push(shift).wait_send()
    for stage in range(3):
        for shift in range(1, sizes[stage]):
            stage_copy(stage, shift).wait_send()


def last_part(x, unit, attend_piece, pieces, tokens, gain, grad_middle, vectors, shared, n, collective_id):
    rows, cols = x.shape
    own = rows // n
    count = len(pieces)
    f32, low = jnp.float32, x.dtype
    whole = lambda item: jax.ShapeDtypeStruct((16,) + item.shape[1:], item.dtype)
    wide, deep = attend_piece.shape
    result = pl.pallas_call(
        functools.partial(last_kernel, n, shared, count),
        out_shape=(
            jax.ShapeDtypeStruct((own, cols), low),
            jax.ShapeDtypeStruct(vectors.shape, f32),
            whole(unit),
            jax.ShapeDtypeStruct((4 * wide, 2 * deep), low),
        )
        + tuple(whole(item) for item in pieces),
        in_specs=[VM] * (7 + count),
        out_specs=(VM,) * (4 + count),
        scratch_shapes=[pltpu.VMEM((own, cols), f32), pltpu.VMEM((2,) + unit.shape[1:], low)]
        + LineScatter.scratch(n, own, cols, low)
        + PlaneSum.reduce_scratch(unit.shape, low)
        + PlaneSum.spread_scratch()
        + [item for _ in pieces for item in PlaneSum.spread_scratch()]
        + [DMA((8,)), DMA((8,)), DMA, pltpu.VMEM((3,) + vectors.shape, f32)]
        + [pltpu.VMEM((size,) + vectors.shape, f32) for size in (n, 4, 2)]
        + [DMA((size,)) for size in (n, 4, 2) for _ in range(2)],
        compiler_params=remote_params(collective_id),
    )(x.reshape(n, own, cols), unit, attend_piece, *pieces, tokens, gain, grad_middle, vectors)
    return result[0], result[1], result[2], result[3], result[4:]


def rows_back_sum_kernel(nc, nt, heads, x_ref, u_ref, o_ref, p_ref, send, recv, loc, *rest):
    total = nc * nt
    my_ctx, my_ten = lax.axis_index("context"), lax.axis_index("tensor")
    me = my_ctx * nt + my_ten
    bar = pltpu.get_barrier_semaphore()
    for shift in range(1, total):
        other = lax.rem(me + shift, total)
        pl.semaphore_signal(bar, inc=1, device_id=spread(other, AXES, (nc, nt)), device_id_type=MESH)
    x = lax.axis_index("dp")
    pl.semaphore_signal(bar, inc=1, device_id={"dp": 1 - x}, device_id_type=MESH)
    pl.semaphore_wait(bar, total)

    unit = StripSum(u_ref, p_ref, None, rest)

    def copy(shift):
        other = lax.rem(me + shift, total)
        ctx, ten = lax.div(other, nt), lax.rem(other, nt)
        return ctx < heads, pltpu.make_async_remote_copy(
            src_ref=x_ref.at[ten * heads + jnp.minimum(ctx, heads - 1)],
            dst_ref=o_ref.at[me],
            send_sem=send.at[shift],
            recv_sem=recv.at[shift],
            device_id={"context": ctx, "tensor": ten},
            device_id_type=MESH,
        )

    for shift in range(1, total):
        goes, item = copy(shift)

        @pl.when(goes)
        def _():
            item.start()

    unit.begin()
    own = pltpu.make_async_copy(
        x_ref.at[my_ten * heads + jnp.minimum(my_ctx, heads - 1)], o_ref.at[me], loc
    )
    own.start()
    own.wait()
    unit.first()
    unit.second()
    unit.third()

    @pl.when(my_ctx < heads)
    def _():
        for shift in range(1, total):
            source = lax.rem(me + total - shift, total)
            pltpu.make_async_copy(o_ref.at[source], o_ref.at[source], recv.at[shift]).wait()

    unit.reduced()
    for shift in range(1, total):
        goes, item = copy(shift)

        @pl.when(goes)
        def _():
            item.wait_send()


def rows_back_sum(x, unit, nc, nt, heads, collective_id):
    total = nc * nt
    return pl.pallas_call(
        functools.partial(rows_back_sum_kernel, nc, nt, heads),
        out_shape=(
            jax.ShapeDtypeStruct((total,) + x.shape[1:], x.dtype),
            jax.ShapeDtypeStruct((2, 2, unit.shape[1] // 4, unit.shape[2] // 2), unit.dtype),
        ),
        in_specs=[VM, VM],
        out_specs=(VM, VM),
        scratch_shapes=[DMA((total,)), DMA((total,)), DMA] + StripSum.reduce_scratch(unit.shape, unit.dtype),
        compiler_params=remote_params(collective_id),
    )(x, unit)


class LineGather:
    def __init__(self, n, x, o, send, recv):
        self.n, self.x, self.o, self.send, self.recv = n, x, o, send, recv
        self.me = lax.axis_index("tensor")

    def copy(self, d, s):
        me, n = self.me, self.n
        shard = jnp.clip(me - s if d == 0 else me + s, 0, n - 1)
        return pltpu.make_async_remote_copy(
            src_ref=self.x if s == 0 else self.o.at[shard],
            dst_ref=self.o.at[shard],
            send_sem=self.send.at[d, s],
            recv_sem=self.recv.at[d, s],
            device_id={"tensor": jnp.clip(me + 1 if d == 0 else me - 1, 0, n - 1)},
            device_id_type=MESH,
        )

    def sends(self, d, s):
        me, n = self.me, self.n
        return (me - s >= 0) & (me < n - 1) if d == 0 else (me + s < n) & (me > 0)

    def wait(self, d, s):
        me, n = self.me, self.n

        @pl.when(me - 1 - s >= 0 if d == 0 else me + 1 + s < n)
        def _():
            shard = jnp.clip(me - 1 - s if d == 0 else me + 1 + s, 0, n - 1)
            pltpu.make_async_copy(self.o.at[shard], self.o.at[shard], self.recv.at[d, s]).wait()

    def step(self, s):
        for d in range(2):
            if s > 0:
                self.wait(d, s - 1)

            @pl.when(self.sends(d, s))
            def _():
                self.copy(d, s).start()

    def last(self):
        for d in range(2):
            self.wait(d, self.n - 2)

    def finish(self):
        for d in range(2):
            for s in range(self.n - 1):

                @pl.when(self.sends(d, s))
                def _():
                    self.copy(d, s).wait_send()


def start_kernel(n, nc, heads, t_ref, gain_ref, shift_ref, full_ref, w_ref, b_ref, o_ref, f_ref, q_ref, *rest):
    (x_ref, held, proj), rest = rest[:3], rest[3:]
    s1, r1, s2, r2, s3, r3, s4, r4, loc = rest
    me, ctx, x = lax.axis_index("tensor"), lax.axis_index("context"), lax.axis_index("dp")
    core, y = lax.rem(ctx, 2), lax.div(ctx, 2)
    rows, width = t_ref.shape
    half = 2 * rows
    bar = pltpu.get_barrier_semaphore()
    met = line_greet(bar, me, n)
    for shift in range(1, nc):
        pl.semaphore_signal(bar, inc=1, device_id={"context": lax.rem(ctx + shift, nc)}, device_id_type=MESH)
    pl.semaphore_signal(bar, inc=1, device_id={"dp": 1 - x}, device_id_type=MESH)
    normed, _ = norm_parts(t_ref[...].astype(jnp.float32))
    x_ref[...] = (normed * gain_ref[...] + shift_ref[...]).astype(x_ref.dtype)
    pl.semaphore_wait(bar, met + nc)

    tall, deep = held.shape[1:]
    strip = pl.ds(pl.multiple_of(core * deep, 128), deep)
    piece = full_ref.at[pl.ds(pl.multiple_of((2 * y + x) * tall, 16), tall), strip]
    small = LineGather(n, piece, held, s1, r1)
    large = LineGather(n, x_ref, o_ref, s2, r2)
    small.step(0)
    large.step(0)
    own = pltpu.make_async_copy(x_ref, o_ref.at[me], loc.at[0])
    own.start()
    mine = pltpu.make_async_copy(piece, held.at[me], loc.at[1])
    mine.start()
    mine.wait()
    own.wait()
    for s in range(1, n - 1):
        small.step(s)
    small.last()

    def there(y_, x_):
        return f_ref.at[:, pl.ds(pl.multiple_of((2 * y_ + x_) * tall, 16), tall), strip]

    x_peer, y_peer = {"dp": 1 - x}, {"context": lax.rem(ctx + 2, 4)}

    def hop(at):
        src, dst, peer = [
            (held, there(y, x), x_peer),
            (held, there(y, x), y_peer),
            (there(y, 1 - x), there(y, 1 - x), y_peer),
            (f_ref.at[:, :, strip], f_ref.at[:, :, strip], {"context": ctx + 1 - 2 * core}),
        ][at]
        return pltpu.make_async_remote_copy(
            src_ref=src,
            dst_ref=dst,
            send_sem=s3.at[at],
            recv_sem=r3.at[at],
            device_id=peer,
            device_id_type=MESH,
        )

    def got(at):
        other = pl.ds(pl.multiple_of((1 - core) * deep, 128), deep)
        ref = [there(y, 1 - x), there(1 - y, x), there(1 - y, 1 - x), f_ref.at[:, :, other]][at]
        pltpu.make_async_copy(ref, ref, r3.at[at]).wait()

    hop(0).start()
    kept = pltpu.make_async_copy(held, there(y, x), loc.at[2])
    kept.start()

    def columns(pair):
        return pl.ds(pl.multiple_of(pair * half, 128), half)

    def project(pair):
        token = jnp.concatenate([o_ref[2 * pair], o_ref[2 * pair + 1]], axis=0)
        for kind in range(3):
            value = dot(w_ref[kind], token, ((0,), (1,))) + b_ref[kind]
            proj[kind, :, :, columns(pair)] = value.astype(proj.dtype).reshape(heads, HEAD_DIM, half)

    def ship(index, pair, shift):
        other = lax.rem(ctx + shift, nc)
        return other, pltpu.make_async_remote_copy(
            src_ref=proj.at[:, jnp.minimum(other, heads - 1), :, columns(pair)],
            dst_ref=q_ref.at[ctx, :, :, columns(pair)],
            send_sem=s4.at[index, shift],
            recv_sem=r4.at[index, shift],
            device_id={"context": other},
            device_id_type=MESH,
        )

    def ship_all(index, pair):
        for shift in range(1, nc):
            other, item = ship(index, pair, shift)

            @pl.when(other < heads)
            def _():
                item.start()

    near = lax.div(me, 2)
    large.step(1)
    project(near)
    ship_all(0, near)
    hop(1).start()
    for s in range(2, n - 1):
        large.step(s)
    got(0)
    hop(2).start()
    large.last()
    project(1 - near)
    ship_all(1, 1 - near)
    stay = pltpu.make_async_copy(proj.at[:, jnp.minimum(ctx, heads - 1)], q_ref.at[ctx], loc.at[3])
    stay.start()
    kept.wait()
    got(1)
    got(2)
    hop(3).start()
    stay.wait()

    @pl.when(ctx < heads)
    def _():
        for index in range(2):
            for shift in range(1, nc):
                source = lax.rem(ctx + nc - shift, nc)
                pair = near if index == 0 else 1 - near
                ref = q_ref.at[source, :, :, columns(pair)]
                pltpu.make_async_copy(ref, ref, r4.at[index, shift]).wait()

    got(3)
    small.finish()
    large.finish()
    for at in range(4):
        hop(at).wait_send()
    for index in range(2):
        for shift in range(1, nc):
            other, item = ship(index, near if index == 0 else 1 - near, shift)

            @pl.when(other < heads)
            def _():
                item.wait_send()


def start_part(tokens, gain, shift, w, project_weight, bias, n, nc, heads, collective_id):
    rows, cols = tokens.shape
    wide, deep = w.shape
    low = jnp.bfloat16
    full, weight, qkv = pl.pallas_call(
        functools.partial(start_kernel, n, nc, heads),
        out_shape=(
            jax.ShapeDtypeStruct((n, rows, cols), low),
            jax.ShapeDtypeStruct((n, wide, deep), w.dtype),
            jax.ShapeDtypeStruct((nc, 3, HEAD_DIM, n * rows), low),
        ),
        in_specs=[VM] * 6,
        out_specs=(VM, VM, VM),
        scratch_shapes=[
            pltpu.VMEM((rows, cols), low),
            pltpu.VMEM((n, wide // 4, deep // 2), w.dtype),
            pltpu.VMEM((3, heads, HEAD_DIM, n * rows), low),
        ]
        + [DMA((2, n - 1)) for _ in range(4)]
        + [DMA((4,)), DMA((4,)), DMA((2, nc)), DMA((2, nc)), DMA((4,))],
        compiler_params=remote_params(collective_id),
    )(tokens, gain[None], shift[None], w, project_weight, bias)
    return full.reshape(n * rows, cols), weight.reshape(n * wide, deep), qkv


def dot(left, right, dims):
    return lax.dot_general(left, right, ((dims[0], dims[1]), ((), ())), preferred_element_type=jnp.float32)


def key_positions(first, keys, queries):
    return first + lax.broadcasted_iota(jnp.int32, (keys, queries), 0)


def load_rows(qkv_ref, nb, half, qs, kt, ks, vs):
    for block in range(nb):
        part = slice(block % 2 * half, block % 2 * half + half)
        at = block // 2
        qs[block] = qkv_ref[at, 0, :, part] * jnp.asarray(HEAD_DIM**-0.5, qs.dtype)
        item = qkv_ref[at, 1, :, part]
        if kt is not None:
            kt[block] = item
        ks[block] = item.T
        if vs is not None:
            vs[block] = qkv_ref[at, 2, :, part].T


def fill_tables(nb, half, seg_ref, order_ref, slot_ref, low_ref, high_ref):
    for block in range(nb):
        slot_ref[order_ref[block]] = jnp.int32(block)
    first = [seg_ref[0, block * half] for block in range(nb)]
    last = [seg_ref[0, block * half + half - 1] for block in range(nb)]
    for block in range(nb):
        if low_ref is not None:
            low_ref[block] = sum(jnp.where(item < first[block], 1, 0) for item in last)
        if high_ref is not None:
            high_ref[block] = sum(jnp.where(item <= last[block], 1, 0) for item in first)


def forward_kernel(half, heads, seg_s, order_ref, seg_ref, qkv_ref, o_ref, full_ref, lse_ref, start_ref, qs, ks, slot_ref, low_ref):
    nb = full_ref.shape[0]

    @pl.when(lax.axis_index("context") < heads)
    def _():
        load_rows(qkv_ref, nb, half, qs, None, ks, None)
        fill_tables(nb, half, seg_s, order_ref, slot_ref, low_ref, None)
        seg = seg_ref[...]
        start = jnp.zeros(seg.shape, jnp.float32)
        for doc in range(1, DOC_LIMIT):
            before = jnp.sum(jnp.where(seg < doc, 1.0, 0.0), axis=1, keepdims=True)
            start = jnp.where(seg == doc, before, start)
        start_ref[...] = start.astype(jnp.int32)

        @pl.loop(0, nb)
        def _(nq):
            slot = slot_ref[nq]
            query = qs[slot]
            begin = start_ref[:, pl.ds(pl.multiple_of(nq * half, 128), half)]
            here = nq * half + lax.broadcasted_iota(jnp.int32, (1, half), 1)

            def step(nk, state):
                top, total, acc = state
                at = slot_ref[nk]
                score = dot(ks[at], query, ((1,), (0,)))
                place = key_positions(nk * half, half, half)
                score = jnp.where((place >= begin) & (place <= here), score, NEG_FILL)
                new_top = jnp.maximum(top, jnp.max(score, axis=0, keepdims=True))
                factor = jnp.exp(top - new_top)
                weight = jnp.exp(score - new_top)
                total = total * factor + jnp.sum(weight, axis=0, keepdims=True)
                value = qkv_ref[at // 2, 2, :, pl.ds(pl.multiple_of(at % 2 * half, 128), half)]
                acc = acc * factor + dot(value, weight.astype(jnp.bfloat16), ((1,), (0,)))
                return new_top, total, acc

            top, total, acc = lax.fori_loop(
                low_ref[nq],
                nq + 1,
                step,
                (
                    jnp.full((1, half), NEG_FILL, jnp.float32),
                    jnp.zeros((1, half), jnp.float32),
                    jnp.zeros((HEAD_DIM, half), jnp.float32),
                ),
            )
            result = acc / total
            full_ref[slot] = result
            lse_ref[slot] = top + jnp.log(total)
            low = result.astype(jnp.bfloat16)
            o_ref[2 * slot] = low[:, : half // 2]
            o_ref[2 * slot + 1] = low[:, half // 2 :]


def attend_forward(qkv, segments, order, half, heads):
    nc = qkv.shape[0]
    nb = 2 * nc
    return pl.pallas_call(
        functools.partial(forward_kernel, half, heads),
        out_shape=(
            jax.ShapeDtypeStruct((2 * nb, HEAD_DIM, half // 2), jnp.bfloat16),
            jax.ShapeDtypeStruct((nb, HEAD_DIM, half), jnp.float32),
            jax.ShapeDtypeStruct((nb, 1, half), jnp.float32),
            jax.ShapeDtypeStruct(segments.shape, jnp.int32),
        ),
        in_specs=[SM, SM, VM, VM],
        out_specs=(VM, VM, VM, VM),
        scratch_shapes=[
            pltpu.VMEM((nb, HEAD_DIM, half), jnp.bfloat16),
            pltpu.VMEM((nb, half, HEAD_DIM), jnp.bfloat16),
            pltpu.SMEM((nb,), jnp.int32),
            pltpu.SMEM((nb,), jnp.int32),
        ],
        compiler_params=pltpu.CompilerParams(vmem_limit_bytes=48 << 20),
    )(segments, order, segments, qkv)


def backward_kernel(
    half, heads, seg_s, order_ref, start_ref, qkv_ref, full_ref, lse_ref, grad_ref, o_ref,
    qs, kt, ks, vs, gs, ds, dq, slot_ref, high_ref,
):
    nb = full_ref.shape[0]

    @pl.when(lax.axis_index("context") < heads)
    def _():
        load_rows(qkv_ref, nb, half, qs, kt, ks, vs)
        fill_tables(nb, half, seg_s, order_ref, slot_ref, None, high_ref)
        for block in range(nb):
            both = jnp.concatenate([grad_ref[2 * block], grad_ref[2 * block + 1]], axis=1)
            gs[block] = both
            ds[block] = jnp.sum(both.astype(jnp.float32) * full_ref[block], axis=0, keepdims=True)
            dq[block] = jnp.zeros((HEAD_DIM, half), jnp.float32)

        @pl.loop(0, nb)
        def _(nk):
            at = slot_ref[nk]
            place = key_positions(nk * half, half, half)

            def step(nq, state):
                grad_key, grad_value = state
                slot = slot_ref[nq]
                query, grad = qs[slot], gs[slot]
                begin = start_ref[:, pl.ds(pl.multiple_of(nq * half, 128), half)]
                here = nq * half + lax.broadcasted_iota(jnp.int32, (1, half), 1)
                score = dot(ks[at], query, ((1,), (0,)))
                score = jnp.where((place >= begin) & (place <= here), score, NEG_FILL)
                weight = jnp.exp(score - lse_ref[slot])
                grad_weight = dot(vs[at], grad, ((1,), (0,)))
                grad_score = (weight * (grad_weight - ds[slot])).astype(jnp.bfloat16)
                grad_value = grad_value + dot(grad, weight.astype(jnp.bfloat16), ((1,), (1,)))
                grad_key = grad_key + dot(query, grad_score, ((1,), (1,)))
                dq[slot] += dot(kt[at], grad_score, ((1,), (0,)))
                return grad_key, grad_value

            zero = jnp.zeros((HEAD_DIM, half), jnp.float32)
            grad_key, grad_value = lax.fori_loop(nk, high_ref[nk], step, (zero, zero))
            columns = pl.ds(pl.multiple_of(at % 2 * half, 128), half)
            o_ref[at // 2, 1, :, columns] = grad_key.astype(jnp.bfloat16)
            o_ref[at // 2, 2, :, columns] = grad_value.astype(jnp.bfloat16)

        for block in range(nb):
            part = slice(block % 2 * half, block % 2 * half + half)
            o_ref[block // 2, 0, :, part] = (dq[block] * HEAD_DIM**-0.5).astype(jnp.bfloat16)


def attend_backward(qkv, segments, order, start, full, lse, grad, half, heads):
    nc = qkv.shape[0]
    nb = 2 * nc
    low = jnp.bfloat16
    return pl.pallas_call(
        functools.partial(backward_kernel, half, heads),
        out_shape=jax.ShapeDtypeStruct(qkv.shape, low),
        in_specs=[SM, SM, VM, VM, VM, VM, VM],
        out_specs=VM,
        scratch_shapes=[
            pltpu.VMEM((nb, HEAD_DIM, half), low),
            pltpu.VMEM((nb, HEAD_DIM, half), low),
            pltpu.VMEM((nb, half, HEAD_DIM), low),
            pltpu.VMEM((nb, half, HEAD_DIM), low),
            pltpu.VMEM((nb, HEAD_DIM, half), low),
            pltpu.VMEM((nb, 1, half), jnp.float32),
            pltpu.VMEM((nb, HEAD_DIM, half), jnp.float32),
            pltpu.SMEM((nb,), jnp.int32),
            pltpu.SMEM((nb,), jnp.int32),
        ],
        compiler_params=pltpu.CompilerParams(vmem_limit_bytes=48 << 20),
    )(segments, order, start, qkv, full, lse, grad)


def norm_parts(values):
    centre = jnp.mean(values, axis=-1, keepdims=True)
    shifted = values - centre
    spread_ = jnp.mean(shifted * shifted, axis=-1, keepdims=True)
    scale = lax.rsqrt(spread_ + NORM_EPS)
    return shifted * scale, scale


def norm_backward(grad, normed, scale, gain):
    e = grad * gain
    mean_e = jnp.mean(e, axis=-1, keepdims=True)
    mean_en = jnp.mean(e * normed, axis=-1, keepdims=True)
    return (e - mean_e - normed * mean_en) * scale


def gelu_tanh(values):
    return jax.nn.gelu(values, approximate=True)


def cross_rows(left, right):
    return lax.dot_general(
        left, right, (((0,), (0,)), ((), ())), preferred_element_type=jnp.float32
    )


def after(value, done):
    return lax.optimization_barrier((value, done))[0]


def per_device(
    mesh_sizes,
    inputs,
    first_gain,
    first_shift,
    project_weight,
    project_bias,
    attend_weight,
    attend_bias,
    second_gain,
    second_shift,
    expand_weight,
    expand_bias,
    shrink_weight,
    shrink_bias,
    segments,
    block_order,
    cotangent,
):
    nt, nc = mesh_sizes["tensor"], mesh_sizes["context"]
    own_rows, width = inputs.shape[1], inputs.shape[2]
    local_width = project_weight.shape[2]
    heads = local_width // HEAD_DIM
    block_rows = own_rows * nt
    half = block_rows // 2
    low = jnp.bfloat16
    f32 = lambda value: value.astype(jnp.float32)
    square = nt == 4 and nc == 4 and mesh_sizes["dp"] == 2
    plane = ("context", "dp")

    tokens_own = f32(inputs[0])
    grad_out = cotangent[0]
    bias = jnp.stack([project_bias[0], jnp.zeros_like(project_bias[0]), project_bias[1]])[:, :, None]
    if square:
        hidden1_full, attend_full, qkv = start_part(
            inputs[0], first_gain, first_shift, attend_weight, project_weight, bias, nt, nc, heads, 0
        )
    else:
        hidden1 = norm_parts(tokens_own)[0] * first_gain + first_shift
        hidden1_full = gather_rows(hidden1.astype(low), nt, 0)
        attend_full = lax.all_gather(attend_weight, "tensor", axis=0, tiled=True)
        projected = jnp.einsum(
            "kde,rd->ker", project_weight, hidden1_full, preferred_element_type=jnp.float32
        )
        projected = (projected + bias).astype(low).reshape(3, heads, HEAD_DIM, block_rows)
        qkv = to_heads(projected, nc, 1)
    grad_full = lax.all_gather(after(grad_out, hidden1_full), "tensor", axis=0, tiled=True)
    pieces, attended_full, lse, start = attend_forward(qkv, segments, block_order, half, heads)
    grad_shrink_bias = jnp.sum(f32(grad_out), axis=0)

    if square:
        grad_hidden2, feed, grad_expand_bias, *feed_pieces, middle, attended = feed_part(
            pieces,
            inputs[0],
            attend_full,
            (attend_bias, second_gain, second_shift),
            expand_weight,
            shrink_weight,
            expand_bias,
            grad_full,
            nt,
            nc,
            heads,
            3,
        )
        attended = attended.reshape(width, own_rows)
        grad_expand_bias = grad_expand_bias[0]
        normed2, scale2 = norm_parts(middle)
    else:
        attended = to_rows(pieces, nc, nt, heads, 2).reshape(width, own_rows)
        middle = tokens_own + cross_rows(attended, attend_full) + attend_bias
        normed2, scale2 = norm_parts(middle)
        hidden2 = (normed2 * second_gain + second_shift).astype(low)
        hidden2_full = gather_rows(hidden2, nt, 3)
        pre_act = jnp.dot(hidden2_full, expand_weight, preferred_element_type=jnp.float32) + expand_bias
        activ = gelu_tanh(pre_act).astype(low)
        grad_act = dot(grad_full, shrink_weight, ((1,), (1,)))
        grad_pre = jax.vjp(gelu_tanh, pre_act)[1](grad_act)[0].astype(low)
        grad_shrink = cross_rows(activ, grad_full).astype(low)
        grad_expand = cross_rows(hidden2_full, grad_pre).astype(low)
        grad_hidden2 = scatter_rows(dot(grad_pre, expand_weight, ((1,), (1,))).astype(low), nt, 4)
        grad_expand_bias = jnp.sum(f32(grad_pre), axis=0)
        feed = jnp.dot(activ, shrink_weight, preferred_element_type=jnp.float32).astype(low)

    grad_second_gain = jnp.sum(grad_hidden2 * normed2, axis=0)
    grad_second_shift = jnp.sum(grad_hidden2, axis=0)
    grad_middle = f32(grad_out) + norm_backward(grad_hidden2, normed2, scale2, second_gain)
    grad_middle_low = grad_middle.astype(low)
    grad_attend_bias = jnp.sum(f32(grad_middle_low), axis=0)
    grad_attended = dot(attend_full, grad_middle_low, ((1,), (1,))).astype(low)
    grad_attended = grad_attended.reshape(nt * heads, HEAD_DIM, own_rows)
    grad_attend = jnp.dot(attended, grad_middle_low, preferred_element_type=jnp.float32).astype(low)
    if square:
        unit = grad_attend.reshape(nt, local_width, width)
        grad_heads, attend_pieces = rows_back_sum(grad_attended, unit, nc, nt, heads, 5)
    else:
        grad_heads = rows_back(grad_attended, nc, nt, heads, 5)
        attend_pieces = None
    feed_sum = lax.psum_scatter(after(feed, grad_heads), "tensor", scatter_dimension=0, tiled=True)

    grad_qkv = attend_backward(qkv, segments, block_order, start, attended_full, lse, grad_heads, half, heads)
    grad_rows = from_heads(grad_qkv, attend_pieces, nc, nt, heads, 6)
    if square:
        grad_rows, attend_piece = grad_rows
    grad_rows = grad_rows.reshape(3 * local_width, block_rows)
    grad_project = dot(hidden1_full, grad_rows, ((0,), (1,))).astype(low)
    grad_hidden1 = lax.dot_general(
        grad_rows.reshape(3, local_width, block_rows),
        project_weight,
        (((0, 1), (0, 2)), ((), ())),
        preferred_element_type=jnp.float32,
    ).astype(low)
    row_sums = jnp.sum(f32(grad_rows), axis=1)
    grad_project_bias = jnp.concatenate([row_sums[:local_width], row_sums[2 * local_width :]])

    wide = grad_expand_bias.shape[0]
    spare = -(wide + 2 * local_width) % width
    others = [
        grad_attend_bias,
        grad_second_gain,
        grad_second_shift,
        grad_shrink_bias,
        grad_expand_bias,
        jnp.pad(grad_project_bias, (0, spare)),
    ]
    if square:
        empty = jnp.zeros((2 * width,), jnp.float32)
        vectors = jnp.concatenate([empty] + others).reshape(-1, width)
        grad_inputs, summed, grad_project, grad_attend, feeds = last_part(
            grad_hidden1,
            grad_project.reshape(16, -1, 3 * local_width),
            attend_piece,
            feed_pieces,
            inputs[0],
            first_gain[None],
            grad_middle,
            vectors,
            6,
            nt,
            7,
        )
        grad_project = grad_project.reshape(width, 3 * local_width)
        grad_shrink, grad_expand = feeds[0].reshape(-1, width), feeds[1].reshape(width, -1)
    else:
        grad_hidden1 = scatter_rows(grad_hidden1, nt, 7)
        normed1, scale1 = norm_parts(tokens_own)
        back = norm_backward(grad_hidden1, normed1, scale1, first_gain)
        grad_inputs = (grad_middle + back).astype(low)
        both = [jnp.sum(grad_hidden1 * normed1, axis=0), jnp.sum(grad_hidden1, axis=0)]
        vectors = jnp.concatenate(both + others).reshape(-1, width)
        summed = sum_vectors(vectors, 6, mesh_sizes, 8)
        grad_attend = lax.psum_scatter(grad_attend, "tensor", scatter_dimension=0, tiled=True)
        grad_project, grad_attend, grad_shrink, grad_expand = lax.psum(
            (grad_project, grad_attend, grad_shrink, grad_expand), plane
        )
    feed_sum = f32(after(feed_sum, summed))
    outputs = (middle + feed_sum + shrink_bias).astype(low)[None]
    grad_project = jnp.stack(
        [grad_project[:, at * local_width : (at + 1) * local_width] for at in range(3)]
    )
    tail = summed[6:].reshape(-1)
    return (
        outputs,
        grad_inputs[None],
        summed[0],
        summed[1],
        f32(grad_project),
        tail[wide : wide + 2 * local_width].reshape(2, local_width),
        f32(grad_attend),
        summed[2],
        summed[3],
        summed[4],
        f32(grad_expand),
        tail[:wide],
        f32(grad_shrink),
        summed[5],
    )


def solution(mesh):
    rows = P("dp", ("context", "tensor"), None)
    in_specs = (
        rows,
        P(),
        P(),
        P(None, None, "tensor"),
        P(None, "tensor"),
        P("tensor", None),
        P(),
        P(),
        P(),
        P(None, "tensor"),
        P("tensor"),
        P("tensor", None),
        P(),
        P("dp", None),
        P(),
        rows,
    )
    out_specs = (
        rows,
        rows,
        P(),
        P(),
        P(None, None, "tensor"),
        P(None, "tensor"),
        P("tensor", None),
        P(),
        P(),
        P(),
        P(None, "tensor"),
        P("tensor"),
        P("tensor", None),
        P(),
    )
    return jax.shard_map(
        functools.partial(per_device, dict(mesh.shape)),
        mesh=mesh,
        in_specs=in_specs,
        out_specs=out_specs,
        check_vma=False,
    )
```

```python
import functools

import jax
import jax.numpy as jnp
from jax import lax
from jax.experimental import pallas as pl
from jax.experimental.pallas import tpu as pltpu
from jax.sharding import PartitionSpec as P

HEAD_DIM = 64
NEG_FILL = -1e30
NORM_EPS = 1e-05
DOC_LIMIT = 16
MESH = pl.DeviceIdType.MESH
VM = pl.BlockSpec(memory_space=pltpu.VMEM)
SM = pl.BlockSpec(memory_space=pltpu.SMEM)
DMA = pltpu.SemaphoreType.DMA


def remote_params(collective_id, mib=16):
    return pltpu.CompilerParams(
        collective_id=collective_id, has_side_effects=True, vmem_limit_bytes=mib << 20
    )


ANY = pl.BlockSpec(memory_space=pl.ANY)


def row(ref):
    return ref[...].reshape(1, -1)


def line_barrier(me, n):
    bar = pltpu.get_barrier_semaphore()

    @pl.when(me > 0)
    def _():
        pl.semaphore_signal(bar, inc=1, device_id={"tensor": me - 1}, device_id_type=MESH)

    @pl.when(me < n - 1)
    def _():
        pl.semaphore_signal(bar, inc=1, device_id={"tensor": me + 1}, device_id_type=MESH)

    pl.semaphore_wait(bar, jnp.where(me > 0, 1, 0) + jnp.where(me < n - 1, 1, 0))


def gather_kernel(n, x_ref, o_ref, send, recv, loc):
    me = lax.axis_index("tensor")
    line_barrier(me, n)
    own = pltpu.make_async_copy(x_ref, o_ref.at[me], loc)
    own.start()

    def copy(d, s):
        shard = jnp.clip(me - s if d == 0 else me + s, 0, n - 1)
        return pltpu.make_async_remote_copy(
            src_ref=x_ref if s == 0 else o_ref.at[shard],
            dst_ref=o_ref.at[shard],
            send_sem=send.at[d, s],
            recv_sem=recv.at[d, s],
            device_id={"tensor": jnp.clip(me + 1 if d == 0 else me - 1, 0, n - 1)},
            device_id_type=MESH,
        )

    def sends(d, s):
        return (me - s >= 0) & (me < n - 1) if d == 0 else (me + s < n) & (me > 0)

    def gets(d, s):
        return me - 1 - s >= 0 if d == 0 else me + 1 + s < n

    def landed(d, s):
        shard = jnp.clip(me - 1 - s if d == 0 else me + 1 + s, 0, n - 1)
        return pltpu.make_async_copy(o_ref.at[shard], o_ref.at[shard], recv.at[d, s])

    for s in range(n - 1):
        for d in range(2):
            if s > 0:

                @pl.when(gets(d, s - 1))
                def _():
                    landed(d, s - 1).wait()

            @pl.when(sends(d, s))
            def _():
                copy(d, s).start()

    for d in range(2):

        @pl.when(gets(d, n - 2))
        def _():
            landed(d, n - 2).wait()

        for s in range(n - 1):

            @pl.when(sends(d, s))
            def _():
                copy(d, s).wait_send()

    own.wait()


def gather_rows(x, n, collective_id):
    rows, cols = x.shape
    return pl.pallas_call(
        functools.partial(gather_kernel, n),
        out_shape=jax.ShapeDtypeStruct((n, rows, cols), x.dtype),
        in_specs=[VM],
        out_specs=VM,
        scratch_shapes=[DMA((2, n - 1)), DMA((2, n - 1)), DMA],
        compiler_params=remote_params(collective_id),
    )(x).reshape(n * rows, cols)


def scatter_kernel(n, x_ref, o_ref, buf, tmp, send, recv):
    me = lax.axis_index("tensor")
    line_barrier(me, n)

    def term(d, k):
        return n - 1 - k if d == 0 else k

    def sends(d, k):
        return me < n - 1 - k if d == 0 else me > k

    def behind(d):
        return me > 0 if d == 0 else me < n - 1

    def copy(d, k, first):
        return pltpu.make_async_remote_copy(
            src_ref=x_ref.at[term(d, k)] if first else tmp.at[d, k],
            dst_ref=buf.at[d, k],
            send_sem=send.at[d, k],
            recv_sem=recv.at[d, k],
            device_id={"tensor": jnp.clip(me + 1 if d == 0 else me - 1, 0, n - 1)},
            device_id_type=MESH,
        )

    def landed(d, k):
        return pltpu.make_async_copy(buf.at[d, k], buf.at[d, k], recv.at[d, k])

    for d in range(2):

        @pl.when(jnp.logical_not(behind(d)))
        def _():
            for k in range(n - 1):
                copy(d, k, True).start()

    for k in range(n - 1):
        for d in range(2):

            @pl.when(behind(d) & sends(d, k))
            def _():
                landed(d, k).wait()
                both = buf[d, k].astype(jnp.float32) + x_ref[term(d, k)].astype(jnp.float32)
                tmp[d, k] = both.astype(tmp.dtype)
                copy(d, k, False).start()

    o_ref[...] = x_ref[me].astype(jnp.float32)
    for d in range(2):
        for k in range(n - 1):

            @pl.when(behind(d) & (me == term(d, k)))
            def _():
                landed(d, k).wait()
                o_ref[...] += buf[d, k].astype(jnp.float32)

    for d in range(2):
        for k in range(n - 1):

            @pl.when(sends(d, k))
            def _():
                copy(d, k, False).wait_send()


def scatter_rows(x, n, collective_id):
    rows, cols = x.shape
    own = rows // n
    return pl.pallas_call(
        functools.partial(scatter_kernel, n),
        out_shape=jax.ShapeDtypeStruct((own, cols), jnp.float32),
        in_specs=[VM],
        out_specs=VM,
        scratch_shapes=[
            pltpu.VMEM((2, n - 1, own, cols), x.dtype),
            pltpu.VMEM((2, n - 1, own, cols), x.dtype),
            DMA((2, n - 1)),
            DMA((2, n - 1)),
        ],
        compiler_params=remote_params(collective_id),
    )(x.reshape(n, own, cols))


def group_barrier(axes, sizes):
    mine = [lax.axis_index(name) for name in axes]
    place = sum_index(mine, sizes)
    total = 1
    for size in sizes:
        total *= size
    bar = pltpu.get_barrier_semaphore()
    for shift in range(1, total):
        other = lax.rem(place + shift, total)
        pl.semaphore_signal(bar, inc=1, device_id=spread(other, axes, sizes), device_id_type=MESH)
    pl.semaphore_wait(bar, total - 1)
    return place, total


def sum_index(mine, sizes):
    place = 0
    for at, size in zip(mine, sizes):
        place = place * size + at
    return place


def spread(place, axes, sizes):
    found = {}
    for name, size in reversed(tuple(zip(axes, sizes))):
        found[name] = lax.rem(place, size)
        place = lax.div(place, size)
    return found


def to_heads_kernel(nc, heads, x_ref, o_ref, send, recv, loc):
    me, _ = group_barrier(("context",), (nc,))

    def copy(shift):
        other = lax.rem(me + shift, nc)
        return other, pltpu.make_async_remote_copy(
            src_ref=x_ref.at[:, jnp.minimum(other, heads - 1)],
            dst_ref=o_ref.at[me],
            send_sem=send.at[shift],
            recv_sem=recv.at[shift],
            device_id={"context": other},
            device_id_type=MESH,
        )

    for shift in range(1, nc):
        other, item = copy(shift)

        @pl.when(other < heads)
        def _():
            item.start()

    own = pltpu.make_async_copy(x_ref.at[:, jnp.minimum(me, heads - 1)], o_ref.at[me], loc)
    own.start()
    own.wait()

    @pl.when(me < heads)
    def _():
        for shift in range(1, nc):
            source = lax.rem(me + nc - shift, nc)
            pltpu.make_async_copy(o_ref.at[source], o_ref.at[source], recv.at[shift]).wait()

    for shift in range(1, nc):
        other, item = copy(shift)

        @pl.when(other < heads)
        def _():
            item.wait_send()


def to_heads(x, nc, collective_id):
    heads = x.shape[1]
    return pl.pallas_call(
        functools.partial(to_heads_kernel, nc, heads),
        out_shape=jax.ShapeDtypeStruct((nc, x.shape[0]) + x.shape[2:], x.dtype),
        in_specs=[VM],
        out_specs=VM,
        scratch_shapes=[DMA((nc,)), DMA((nc,)), DMA],
        compiler_params=remote_params(collective_id),
    )(x)


def from_heads_kernel(nc, nt, heads, extra, x_ref, *rest):
    if extra:
        p_ref, o_ref, s_ref, send, recv, loc, land, zsend, zrecv = rest
    else:
        o_ref, send, recv, loc = rest
    me, ten = lax.axis_index("context"), lax.axis_index("tensor")
    bar = pltpu.get_barrier_semaphore()
    for shift in range(1, nc):
        pl.semaphore_signal(bar, inc=1, device_id={"context": lax.rem(me + shift, nc)}, device_id_type=MESH)
    if extra:
        for shift in range(1, nt):
            pl.semaphore_signal(bar, inc=1, device_id={"tensor": lax.rem(ten + shift, nt)}, device_id_type=MESH)
    pl.semaphore_wait(bar, nc - 1 + (nt - 1 if extra else 0))

    def copy(shift):
        other = lax.rem(me + shift, nc)
        return pltpu.make_async_remote_copy(
            src_ref=x_ref.at[other],
            dst_ref=o_ref.at[:, jnp.minimum(me, heads - 1)],
            send_sem=send.at[shift],
            recv_sem=recv.at[shift],
            device_id={"context": other},
            device_id_type=MESH,
        )

    def across(shift):
        other = lax.rem(ten + shift, nt)
        return pltpu.make_async_remote_copy(
            src_ref=p_ref.at[lax.div(other, 2), lax.rem(other, 2)],
            dst_ref=land.at[ten],
            send_sem=zsend.at[shift],
            recv_sem=zrecv.at[shift],
            device_id={"tensor": other},
            device_id_type=MESH,
        )

    if extra:
        for shift in range(1, nt):
            across(shift).start()

    @pl.when(me < heads)
    def _():
        for shift in range(1, nc):
            copy(shift).start()
        own = pltpu.make_async_copy(x_ref.at[me], o_ref.at[:, me], loc)
        own.start()
        own.wait()

    if extra:
        land[ten] = p_ref[lax.div(ten, 2), lax.rem(ten, 2)]
        for shift in range(1, nt):
            source = lax.rem(ten + nt - shift, nt)
            pltpu.make_async_copy(land.at[source], land.at[source], zrecv.at[shift]).wait()
        value = land[0].astype(jnp.float32)
        for at in range(1, nt):
            value = value + land[at].astype(jnp.float32)
        s_ref[...] = value.astype(s_ref.dtype)
        for shift in range(1, nt):
            across(shift).wait_send()

    for shift in range(1, nc):
        source = lax.rem(me + nc - shift, nc)

        @pl.when(source < heads)
        def _():
            at = jnp.minimum(source, heads - 1)
            pltpu.make_async_copy(o_ref.at[:, at], o_ref.at[:, at], recv.at[shift]).wait()

    @pl.when(me < heads)
    def _():
        for shift in range(1, nc):
            copy(shift).wait_send()


def from_heads(x, pieces, nc, nt, heads, collective_id):
    extra = pieces is not None
    out = jax.ShapeDtypeStruct((x.shape[1], heads) + x.shape[2:], x.dtype)
    scratch = [DMA((nc,)), DMA((nc,)), DMA]
    if extra:
        piece = pieces.shape[2:]
        scratch += [pltpu.VMEM((nt,) + piece, pieces.dtype), DMA((nt,)), DMA((nt,))]
        out = (out, jax.ShapeDtypeStruct(piece, pieces.dtype))
    return pl.pallas_call(
        functools.partial(from_heads_kernel, nc, nt, heads, extra),
        out_shape=out,
        in_specs=[VM] * (1 + extra),
        out_specs=(VM, VM) if extra else VM,
        scratch_shapes=scratch,
        compiler_params=remote_params(collective_id),
    )(*((x, pieces) if extra else (x,)))


AXES = ("context", "tensor")


def rows_kernel(nc, nt, heads, x_ref, o_ref, send, recv, loc):
    me, total = group_barrier(AXES, (nc, nt))
    my_ctx, my_ten = lax.axis_index("context"), lax.axis_index("tensor")
    my_head = my_ten * heads + jnp.minimum(my_ctx, heads - 1)

    def copy(shift):
        other = lax.rem(me + shift, total)
        return pltpu.make_async_remote_copy(
            src_ref=x_ref.at[other],
            dst_ref=o_ref.at[my_head],
            send_sem=send.at[shift],
            recv_sem=recv.at[shift],
            device_id=spread(other, AXES, (nc, nt)),
            device_id_type=MESH,
        )

    @pl.when(my_ctx < heads)
    def _():
        for shift in range(1, total):
            copy(shift).start()
        own = pltpu.make_async_copy(x_ref.at[me], o_ref.at[my_head], loc)
        own.start()
        own.wait()

    for shift in range(1, total):
        source = lax.rem(me + total - shift, total)
        ctx, ten = lax.div(source, nt), lax.rem(source, nt)

        @pl.when(ctx < heads)
        def _():
            at = ten * heads + jnp.minimum(ctx, heads - 1)
            pltpu.make_async_copy(o_ref.at[at], o_ref.at[at], recv.at[shift]).wait()

    @pl.when(my_ctx < heads)
    def _():
        for shift in range(1, total):
            copy(shift).wait_send()


def to_rows(x, nc, nt, heads, collective_id):
    total = nc * nt
    return pl.pallas_call(
        functools.partial(rows_kernel, nc, nt, heads),
        out_shape=jax.ShapeDtypeStruct((nt * heads,) + x.shape[1:], x.dtype),
        in_specs=[VM],
        out_specs=VM,
        scratch_shapes=[DMA((total,)), DMA((total,)), DMA],
        compiler_params=remote_params(collective_id),
    )(x)


def rows_back_kernel(nc, nt, heads, x_ref, o_ref, send, recv, loc):
    me, total = group_barrier(AXES, (nc, nt))
    my_ctx, my_ten = lax.axis_index("context"), lax.axis_index("tensor")

    def copy(shift):
        other = lax.rem(me + shift, total)
        ctx, ten = lax.div(other, nt), lax.rem(other, nt)
        return ctx < heads, pltpu.make_async_remote_copy(
            src_ref=x_ref.at[ten * heads + jnp.minimum(ctx, heads - 1)],
            dst_ref=o_ref.at[me],
            send_sem=send.at[shift],
            recv_sem=recv.at[shift],
            device_id={"context": ctx, "tensor": ten},
            device_id_type=MESH,
        )

    for shift in range(1, total):
        goes, item = copy(shift)

        @pl.when(goes)
        def _():
            item.start()

    own = pltpu.make_async_copy(
        x_ref.at[my_ten * heads + jnp.minimum(my_ctx, heads - 1)], o_ref.at[me], loc
    )
    own.start()
    own.wait()

    @pl.when(my_ctx < heads)
    def _():
        for shift in range(1, total):
            source = lax.rem(me + total - shift, total)
            pltpu.make_async_copy(o_ref.at[source], o_ref.at[source], recv.at[shift]).wait()

    for shift in range(1, total):
        goes, item = copy(shift)

        @pl.when(goes)
        def _():
            item.wait_send()


def rows_back(x, nc, nt, heads, collective_id):
    total = nc * nt
    return pl.pallas_call(
        functools.partial(rows_back_kernel, nc, nt, heads),
        out_shape=jax.ShapeDtypeStruct((total,) + x.shape[1:], x.dtype),
        in_specs=[VM],
        out_specs=VM,
        scratch_shapes=[DMA((total,)), DMA((total,)), DMA],
        compiler_params=remote_params(collective_id),
    )(x)


def vectors_kernel(names, sizes, shared, x_ref, o_ref, now, *rest):
    bufs, sems = rest[: len(names)], rest[len(names) :]
    bar = pltpu.get_barrier_semaphore()
    for name, size in zip(names, sizes):
        me = lax.axis_index(name)
        for shift in range(1, size):
            pl.semaphore_signal(
                bar, inc=1, device_id={name: lax.rem(me + shift, size)}, device_id_type=MESH
            )
    pl.semaphore_wait(bar, sum(sizes) - len(sizes))
    for stage, (name, size) in enumerate(zip(names, sizes)):
        buf, send, recv = bufs[stage], sems[2 * stage], sems[2 * stage + 1]
        me = lax.axis_index(name)

        def copy(shift):
            return pltpu.make_async_remote_copy(
                src_ref=now.at[stage] if stage else x_ref.at[0],
                dst_ref=buf.at[me],
                send_sem=send.at[shift],
                recv_sem=recv.at[shift],
                device_id={name: lax.rem(me + shift, size)},
                device_id_type=MESH,
            )

        for shift in range(1, size):
            copy(shift).start()
        buf[me] = now[stage] if stage else x_ref[0]
        for shift in range(1, size):
            source = lax.rem(me + size - shift, size)
            pltpu.make_async_copy(buf.at[source], buf.at[source], recv.at[shift]).wait()
        total = buf[0]
        for at in range(1, size):
            total = total + buf[at]
        if stage == 0:
            row = lax.broadcasted_iota(jnp.int32, total.shape, 0)
            total = jnp.where(row < shared, total, x_ref[0])
        if stage + 1 < len(names):
            now[stage + 1] = total
        else:
            o_ref[...] = total
        for shift in range(1, size):
            copy(shift).wait_send()


def sum_vectors(rows, shared, mesh_sizes, collective_id):
    names = ("tensor", "context", "dp")
    sizes = tuple(mesh_sizes[name] for name in names)
    shape = rows.shape
    return pl.pallas_call(
        functools.partial(vectors_kernel, names, sizes, shared),
        out_shape=jax.ShapeDtypeStruct(shape, jnp.float32),
        in_specs=[VM],
        out_specs=VM,
        scratch_shapes=[pltpu.VMEM((len(names),) + shape, jnp.float32)]
        + [pltpu.VMEM((size,) + shape, jnp.float32) for size in sizes]
        + [DMA((size,)) for size in sizes for _ in range(2)],
        compiler_params=remote_params(collective_id),
    )(rows[None])


class PlaneSum:
    def __init__(self, u, p, o, bufs=None, spread=None):
        self.u, self.p, self.o = u, p, o
        if bufs is not None:
            self.rc, self.s1, self.ra, self.rb, self.sa, self.sb, self.ta, self.tb = bufs[:8]
            self.send1, self.recv1 = bufs[8:]
        if spread is not None:
            self.send2, self.recv2, self.loc = spread
        ctx, self.x = lax.axis_index("context"), lax.axis_index("dp")
        self.core, self.y = lax.rem(ctx, 2), lax.div(ctx, 2)
        self.chip_peer = {"context": ctx + 1 - 2 * self.core}
        self.y_peer = {"context": lax.rem(ctx + 2, 4)}
        self.x_peer = {"dp": 1 - self.x}

    @staticmethod
    def reduce_scratch(shape, dtype):
        tail = tuple(shape[1:])
        bufs = [pltpu.VMEM((count,) + tail, dtype) for count in (8, 8, 2, 2, 2, 2, 1, 1)]
        return bufs + [DMA((5,)), DMA((5,))]

    @staticmethod
    def spread_scratch():
        return [DMA((5,)), DMA((5,)), DMA((2,))]

    @staticmethod
    def greet(bar):
        ctx, x = lax.axis_index("context"), lax.axis_index("dp")
        for peer in (
            {"context": ctx + 1 - 2 * lax.rem(ctx, 2)},
            {"context": lax.rem(ctx + 2, 4)},
            {"dp": 1 - x},
        ):
            pl.semaphore_signal(bar, inc=1, device_id=peer, device_id_type=MESH)
        return 3

    def copy(self, at, src, dst, peer):
        send, recv = (self.send1, self.recv1) if at < 5 else (self.send2, self.recv2)
        return pltpu.make_async_remote_copy(
            src_ref=src,
            dst_ref=dst,
            send_sem=send.at[at % 5],
            recv_sem=recv.at[at % 5],
            device_id=peer,
            device_id_type=MESH,
        )

    def got(self, at, ref):
        recv = self.recv1 if at < 5 else self.recv2
        pltpu.make_async_copy(ref, ref, recv.at[at % 5]).wait()

    def add(self, out, left, right):
        f32 = jnp.float32
        out[...] = (left[...].astype(f32) + right[...].astype(f32)).astype(out.dtype)

    def mine(self, half):
        if half == 0:
            return pl.ds(self.core * 8 + 2 * self.x + self.y, 1)
        return pl.ds(self.core * 8 + 4 + 2 * self.y + self.x, 1)

    def hop(self, at):
        x, y, core = self.x, self.y, self.core
        o, p = self.o, self.p
        pair_a, pair_b = pl.ds(core * 8 + 2 * x, 2), pl.ds(core * 8 + 4 + 2 * y, 2)
        one = lambda at: pl.ds(at, 1)
        return [
            lambda: self.copy(0, self.by_core(1 - core), self.rc, self.chip_peer),
            lambda: self.copy(1, self.quarter(0, 1 - x), self.ra, self.x_peer),
            lambda: self.copy(2, self.quarter(1, 1 - y), self.rb, self.y_peer),
            lambda: self.copy(3, self.eighth(0, 1 - y), self.ta, self.y_peer),
            lambda: self.copy(4, self.eighth(1, 1 - x), self.tb, self.x_peer),
            lambda: self.copy(5, p.at[one(0)], o.at[self.mine(0)], self.y_peer),
            lambda: self.copy(6, p.at[one(1)], o.at[self.mine(1)], self.x_peer),
            lambda: self.copy(7, o.at[pair_a], o.at[pair_a], self.x_peer),
            lambda: self.copy(8, o.at[pair_b], o.at[pair_b], self.y_peer),
            lambda: self.copy(9, o.at[pl.ds(core * 8, 8)], o.at[pl.ds(core * 8, 8)], self.chip_peer),
        ][at]()

    def begin(self):
        self.hop(0).start()

    def by_core(self, core):
        return self.u.at[pl.ds(core * 8, 8)]

    def quarter(self, half, at):
        return self.s1.at[pl.ds(4 * half + 2 * at, 2)]

    def eighth(self, half, at):
        return (self.sa, self.sb)[half].at[pl.ds(at, 1)]

    def result(self, half):
        return self.p.at[pl.ds(half, 1)]

    def first(self):
        self.got(0, self.rc)
        self.add(self.s1, self.by_core(self.core), self.rc)
        self.hop(1).start()
        self.hop(2).start()

    def second(self):
        self.got(1, self.ra)
        self.add(self.sa, self.quarter(0, self.x), self.ra)
        self.hop(3).start()
        self.got(2, self.rb)
        self.add(self.sb, self.quarter(1, self.y), self.rb)
        self.hop(4).start()

    def third(self):
        self.got(3, self.ta)
        self.add(self.result(0), self.eighth(0, self.y), self.ta)
        self.got(4, self.tb)
        self.add(self.result(1), self.eighth(1, self.x), self.tb)

    def reduced(self):
        for at in range(5):
            self.hop(at).wait_send()

    def kept(self, half):
        return pltpu.make_async_copy(self.p.at[pl.ds(half, 1)], self.o.at[self.mine(half)], self.loc.at[half])

    def spread1(self):
        self.hop(5).start()
        self.hop(6).start()
        self.kept(0).start()
        self.kept(1).start()

    def spread2(self):
        x, y, core = self.x, self.y, self.core
        self.kept(0).wait()
        self.got(5, self.o.at[pl.ds(core * 8 + 2 * x + 1 - y, 1)])
        self.hop(7).start()
        self.kept(1).wait()
        self.got(6, self.o.at[pl.ds(core * 8 + 4 + 2 * y + 1 - x, 1)])
        self.hop(8).start()

    def spread3(self):
        x, y, core = self.x, self.y, self.core
        self.got(7, self.o.at[pl.ds(core * 8 + 2 - 2 * x, 2)])
        self.got(8, self.o.at[pl.ds(core * 8 + 6 - 2 * y, 2)])
        self.hop(9).start()

    def everywhere(self):
        self.got(9, self.o.at[pl.ds(8 - self.core * 8, 8)])
        for at in range(5, 10):
            self.hop(at).wait_send()


class StripSum(PlaneSum):
    @staticmethod
    def reduce_scratch(shape, dtype):
        _, rows, cols = shape
        shapes = [(4, rows)] * 2 + [(2, rows // 2)] * 4 + [(2, rows // 4)] * 2
        return [pltpu.VMEM(item + (cols // 2,), dtype) for item in shapes] + [DMA((5,)), DMA((5,))]

    def by_core(self, core):
        size = self.u.shape[2] // 2
        return self.u.at[:, :, pl.ds(pl.multiple_of(core * size, 128), size)]

    def quarter(self, half, at):
        size = self.s1.shape[1] // 2
        return self.s1.at[pl.ds(2 * half, 2), pl.ds(pl.multiple_of(at * size, 16), size)]

    def eighth(self, half, at):
        size = self.sa.shape[1] // 2
        return (self.sa, self.sb)[half].at[:, pl.ds(pl.multiple_of(at * size, 16), size)]

    def result(self, half):
        return self.p.at[half]


def unit_pieces(unit):
    return jax.ShapeDtypeStruct((2,) + unit.shape[1:], unit.dtype)


def line_greet(bar, me, n):
    @pl.when(me > 0)
    def _():
        pl.semaphore_signal(bar, inc=1, device_id={"tensor": me - 1}, device_id_type=MESH)

    @pl.when(me < n - 1)
    def _():
        pl.semaphore_signal(bar, inc=1, device_id={"tensor": me + 1}, device_id_type=MESH)

    return jnp.where(me > 0, 1, 0) + jnp.where(me < n - 1, 1, 0)


class LineScatter:
    def __init__(self, n, x, o, buf, tmp, send, recv):
        self.n, self.x, self.o, self.buf, self.tmp, self.send, self.recv = n, x, o, buf, tmp, send, recv
        self.me = lax.axis_index("tensor")

    @staticmethod
    def scratch(n, own, cols, dtype):
        return [
            pltpu.VMEM((2, n - 1, own, cols), dtype),
            pltpu.VMEM((2, n - 1, own, cols), dtype),
            DMA((2, n - 1)),
            DMA((2, n - 1)),
        ]

    def term(self, d, k):
        return self.n - 1 - k if d == 0 else k

    def sends(self, d, k):
        return self.me < self.n - 1 - k if d == 0 else self.me > k

    def behind(self, d):
        return self.me > 0 if d == 0 else self.me < self.n - 1

    def copy(self, d, k, first):
        return pltpu.make_async_remote_copy(
            src_ref=self.x.at[self.term(d, k)] if first else self.tmp.at[d, k],
            dst_ref=self.buf.at[d, k],
            send_sem=self.send.at[d, k],
            recv_sem=self.recv.at[d, k],
            device_id={"tensor": jnp.clip(self.me + 1 if d == 0 else self.me - 1, 0, self.n - 1)},
            device_id_type=MESH,
        )

    def landed(self, d, k):
        return pltpu.make_async_copy(self.buf.at[d, k], self.buf.at[d, k], self.recv.at[d, k])

    def begin(self):
        for d in range(2):

            @pl.when(jnp.logical_not(self.behind(d)))
            def _():
                for k in range(self.n - 1):
                    self.copy(d, k, True).start()

    def step(self, k):
        for d in range(2):

            @pl.when(self.behind(d) & self.sends(d, k))
            def _():
                self.landed(d, k).wait()
                at = self.term(d, k)
                both = self.buf[d, k].astype(jnp.float32) + self.x[at].astype(jnp.float32)
                self.tmp[d, k] = both.astype(self.tmp.dtype)
                self.copy(d, k, False).start()

    def end(self):
        self.o[...] = self.x[self.me].astype(jnp.float32)
        for d in range(2):
            for k in range(self.n - 1):

                @pl.when(self.behind(d) & (self.me == self.term(d, k)))
                def _():
                    self.landed(d, k).wait()
                    self.o[...] += self.buf[d, k].astype(jnp.float32)

        for d in range(2):
            for k in range(self.n - 1):

                @pl.when(self.sends(d, k))
                def _():
                    self.copy(d, k, False).wait_send()


GELU_SCALE = 0.7978845608028654
GELU_CUBE = 0.044715


def feed_kernel(n, nc, heads, chunks, piece_ref, *rest):
    (token_ref, out_ref, abias_ref, gain_ref, shift_ref, up_hbm, down_hbm, bias_ref, near_ref, cot_ref), rest = rest[:10], rest[10:]
    (o_ref, feed_ref, sum_ref, p1_ref, p2_ref, middle_ref, att_ref), rest = rest[:7], rest[7:]
    (x_ref, up_ref, down_ref, grad_ref, wsem, asend, arecv, aloc, csend, crecv, cloc), rest = rest[:11], rest[11:]
    (held, act, gp, part, acc, buf, tmp, u1, u2), rest = rest[:9], rest[9:]
    (gsend, grecv, loc, ssend, srecv), rest = rest[:5], rest[5:]
    plane = [PlaneSum(u1, p1_ref, None, rest[:10]), PlaneSum(u2, p2_ref, None, rest[10:20])]
    me = lax.axis_index("tensor")
    rows, width = token_ref.shape
    wide = up_ref.shape[1]
    few = rows // chunks
    f32, low = jnp.float32, jnp.bfloat16
    ctx, dp = lax.axis_index("context"), lax.axis_index("dp")
    place, total = ctx * n + me, nc * n
    my_head = me * heads + jnp.minimum(ctx, heads - 1)
    bar = pltpu.get_barrier_semaphore()
    for shift in range(1, total):
        other = lax.rem(place + shift, total)
        pl.semaphore_signal(bar, inc=1, device_id=spread(other, AXES, (nc, n)), device_id_type=MESH)
    pl.semaphore_signal(bar, inc=1, device_id={"dp": 1 - dp}, device_id_type=MESH)
    weights_in = [
        pltpu.make_async_copy(src, dst, wsem.at[at])
        for at, (src, dst) in enumerate(((up_hbm, up_ref), (down_hbm, down_ref)))
    ]
    for item in weights_in:
        item.start()

    def grad_rows(block):
        return grad_ref.at[pl.ds(pl.multiple_of(block * rows, rows), rows)]

    def grad_on(d, s):
        block = jnp.clip(me - s if d == 0 else me + s, 0, n - 1)
        return pltpu.make_async_remote_copy(
            src_ref=near_ref.at[block] if s == 1 else grad_rows(block),
            dst_ref=grad_rows(block),
            send_sem=csend.at[d, s],
            recv_sem=crecv.at[d, s],
            device_id={"tensor": jnp.clip(me + 1 if d == 0 else me - 1, 0, n - 1)},
            device_id_type=MESH,
        )

    def grad_sends(d, s):
        return (me - s >= 0) & (me < n - 1) if d == 0 else (me + s < n) & (me > 0)

    def grad_near(d):
        block = jnp.clip(me - 1 if d == 0 else me + 1, 0, n - 1)
        return pltpu.make_async_copy(near_ref.at[block], grad_rows(block), cloc.at[d])

    def grad_own():
        return pltpu.make_async_copy(cot_ref, grad_rows(me), cloc.at[2])

    def beside(d):
        return me > 0 if d == 0 else me < n - 1

    grad_own().start()
    for d in range(2):

        @pl.when(beside(d))
        def _():
            grad_near(d).start()

    pl.semaphore_wait(bar, total)
    for d in range(2):

        @pl.when(grad_sends(d, 1))
        def _():
            grad_on(d, 1).start()

    def to_place(shift):
        other = lax.rem(place + shift, total)
        return pltpu.make_async_remote_copy(
            src_ref=piece_ref.at[other],
            dst_ref=att_ref.at[my_head],
            send_sem=asend.at[shift],
            recv_sem=arecv.at[shift],
            device_id=spread(other, AXES, (nc, n)),
            device_id_type=MESH,
        )

    @pl.when(ctx < heads)
    def _():
        for shift in range(1, total):
            to_place(shift).start()
        stay = pltpu.make_async_copy(piece_ref.at[place], att_ref.at[my_head], aloc)
        stay.start()
        stay.wait()

    for shift in range(1, total):
        source = lax.rem(place + total - shift, total)
        at_ctx, at_ten = lax.div(source, n), lax.rem(source, n)

        @pl.when(at_ctx < heads)
        def _():
            landed = att_ref.at[at_ten * heads + jnp.minimum(at_ctx, heads - 1)]
            pltpu.make_async_copy(landed, landed, arecv.at[shift]).wait()

    attended = att_ref[...].reshape(width, rows)
    middle = token_ref[...].astype(f32) + dot(attended, out_ref[...], ((0,), (0,))) + row(abias_ref)
    middle_ref[...] = middle
    x_ref[...] = (norm_parts(middle)[0] * row(gain_ref) + row(shift_ref)).astype(low)

    @pl.when(ctx < heads)
    def _():
        for shift in range(1, total):
            to_place(shift).wait_send()

    def rows_of(block):
        return pl.ds(pl.multiple_of(block * rows, rows), rows)

    def neighbour(d):
        return {"tensor": jnp.clip(jnp.where(d == 0, me + 1, me - 1), 0, n - 1)}

    def onward(d):
        return jnp.where(d == 0, me, n - 1 - me) < n - 1

    def hand_on(d, s, block, first):
        return pltpu.make_async_remote_copy(
            src_ref=x_ref if first else held.at[rows_of(block)],
            dst_ref=held.at[rows_of(block)],
            send_sem=gsend.at[d, s],
            recv_sem=grecv.at[d, s],
            device_id=neighbour(d),
            device_id_type=MESH,
        )

    def chunk(block, c):
        return pl.ds(pl.multiple_of(block * rows + c * few, few), few)

    def back(d, block, c, first):
        at = chunk(block, c)
        return pltpu.make_async_remote_copy(
            src_ref=part.at[at] if first else tmp.at[at],
            dst_ref=buf.at[d, at],
            send_sem=ssend.at[block, c],
            recv_sem=srecv.at[d, block, c],
            device_id=neighbour(d),
            device_id_type=MESH,
        )

    for d in range(2):

        @pl.when(onward(d))
        def _():
            hand_on(d, 0, me, True).start()

    own = pltpu.make_async_copy(x_ref, held.at[rows_of(me)], loc)
    own.start()
    sum_ref[...] = jnp.zeros_like(sum_ref)
    own.wait()
    for item in weights_in:
        item.wait()
    grad_own().wait()
    for d in range(2):

        @pl.when(beside(d))
        def _():
            grad_near(d).wait()

    for s in range(1, n - 1):
        for d in range(2):
            block = me - 1 - s if d == 0 else me + 1 + s

            @pl.when((block >= 0) & (block < n))
            def _():
                landed = grad_rows(jnp.clip(block, 0, n - 1))
                pltpu.make_async_copy(landed, landed, crecv.at[d, s]).wait()

            if s + 1 < n - 1:

                @pl.when(grad_sends(d, s + 1))
                def _():
                    grad_on(d, s + 1).start()

        if s == n - 3:
            break
    columns = 256

    def work(block):
        here = rows_of(block)
        acc[...] = jnp.zeros_like(acc)

        @pl.loop(0, wide // columns)
        def _(j):
            at = pl.ds(pl.multiple_of(j * columns, columns), columns)
            pre = dot(held[here, :], up_ref[:, at], ((1,), (0,))) + bias_ref[at].reshape(1, -1)
            square = pre * pre
            tanh = jnp.tanh(GELU_SCALE * pre * (1.0 + GELU_CUBE * square))
            act[here, at] = (0.5 * pre * (1.0 + tanh)).astype(low)
            slope = 0.5 * (1.0 + tanh) + 0.5 * pre * (1.0 - tanh * tanh) * (
                GELU_SCALE * (1.0 + 3.0 * GELU_CUBE * square)
            )
            grad = (dot(grad_ref[here, :], down_ref[at, :], ((1,), (1,))) * slope).astype(low)
            gp[here, at] = grad
            acc[...] += dot(grad, up_ref[:, at], ((1,), (1,)))

        part[here, :] = acc[...].astype(low)
        sum_ref[...] += jnp.sum(gp[here, :].astype(f32), axis=0, keepdims=True)

    near = jnp.minimum(me, n - 1 - me)
    toward = jnp.where(2 * me < n - 1, -1, 1)

    @pl.loop(0, n)
    def _(slot):
        paired = slot <= 2 * near
        distance = jnp.where(paired, lax.div(slot + 1, 2), slot - near)
        side = jnp.where(paired & (lax.rem(slot, 2) == 1), toward, -toward)
        block = me + side * distance
        d = jnp.where(block < me, 0, 1)
        s = jnp.maximum(distance - 1, 0)

        @pl.when(slot > 0)
        def _():
            landed = held.at[rows_of(block)]
            pltpu.make_async_copy(landed, landed, grecv.at[d, s]).wait()

            @pl.when(onward(d))
            def _():
                hand_on(d, jnp.minimum(s + 1, n - 2), block, False).start()

        @pl.when(distance == n - 1)
        def _():
            landed = grad_rows(block)
            pltpu.make_async_copy(landed, landed, crecv.at[d, n - 2]).wait()

        work(block)

        @pl.when((slot > 0) & ((me == 0) | (me == n - 1)))
        def _():
            for c in range(chunks):
                back(1 - d, block, c, True).start()

    def weights(left, right, unit):
        half = wide // 2

        @pl.loop(0, 2)
        def _(j):
            at = pl.ds(pl.multiple_of(j * half, 128), half)
            total = dot(left[:, at], right[...], ((0,), (0,)))
            unit[pl.ds(8 * j, 8)] = total.astype(low).reshape((8,) + unit.shape[1:])

    weights(act, grad_ref, u1)
    plane[0].begin()
    weights(held, gp, u2)
    plane[1].begin()

    def relay(way, block):
        d = jnp.where(way > 0, 0, 1)

        @pl.when((me > 0) & (me < n - 1) & (block >= 0) & (block < n))
        def _():
            for c in range(chunks):
                at = chunk(block, c)
                landed = buf.at[d, at]
                pltpu.make_async_copy(landed, landed, srecv.at[d, block, c]).wait()
                tmp[at, :] = (buf[d, at, :].astype(f32) + part[at, :].astype(f32)).astype(low)
                back(d, block, c, False).start()

    plane[0].first()
    for j in range(1, n):
        relay(-toward, me - toward * j)
        if j == 1:
            plane[1].first()

    @pl.loop(0, n)
    def _(block):
        here = rows_of(block)
        feed_ref[here, :] = dot(act[here, :], down_ref[...], ((1,), (0,))).astype(low)

    plane[0].second()
    plane[1].second()
    for j in range(1, n):
        relay(toward, me + toward * j)
    for item in plane:
        item.third()
    for c in range(chunks):
        at = chunk(me, c)
        mine = pl.ds(c * few, few)
        o_ref[mine, :] = part[at, :].astype(f32)
        for d in range(2):

            @pl.when(me > 0 if d == 0 else me < n - 1)
            def _():
                landed = buf.at[d, at]
                pltpu.make_async_copy(landed, landed, srecv.at[d, me, c]).wait()
                o_ref[mine, :] += buf[d, at, :].astype(f32)

    for d in range(2):
        for s in range(n - 1):
            block = me - s if d == 0 else me + s

            @pl.when(onward(d) & (block >= 0) & (block < n))
            def _():
                hand_on(d, s, me, True).wait_send()

    for block in range(n):

        @pl.when(me != block)
        def _():
            for c in range(chunks):
                back(jnp.where(me < block, 0, 1), block, c, True).wait_send()

    for d in range(2):
        for s in range(1, n - 1):

            @pl.when(grad_sends(d, s))
            def _():
                grad_on(d, s).wait_send()

    for item in plane:
        item.reduced()


def feed_part(pieces, tokens, out_weight, vectors, up, down, bias, near, cotangent, n, nc, heads, collective_id):
    rows, width = tokens.shape
    wide = up.shape[1]
    chunks = 2
    total = n * rows
    low, f32 = jnp.bfloat16, jnp.float32
    unit = (16, wide // 16, width)
    piece = jax.ShapeDtypeStruct((2,) + unit[1:], low)
    return pl.pallas_call(
        functools.partial(feed_kernel, n, nc, heads, chunks),
        out_shape=(
            jax.ShapeDtypeStruct((rows, width), f32),
            jax.ShapeDtypeStruct((total, width), low),
            jax.ShapeDtypeStruct((1, wide), f32),
            piece,
            piece,
            jax.ShapeDtypeStruct((rows, width), f32),
            jax.ShapeDtypeStruct((n * heads,) + pieces.shape[1:], low),
        ),
        in_specs=[VM] * 6 + [ANY, ANY, VM, ANY, ANY],
        out_specs=(VM,) * 7,
        scratch_shapes=[
            pltpu.VMEM((rows, width), low),
            pltpu.VMEM(up.shape, low),
            pltpu.VMEM(down.shape, low),
            pltpu.VMEM((total, width), low),
            DMA((2,)),
            DMA((nc * n,)),
            DMA((nc * n,)),
            DMA,
            DMA((2, n - 1)),
            DMA((2, n - 1)),
            DMA((3,)),
            pltpu.VMEM((total, width), low),
            pltpu.VMEM((total, wide), low),
            pltpu.VMEM((total, wide), low),
            pltpu.VMEM((total, width), low),
            pltpu.VMEM((rows, width), f32),
            pltpu.VMEM((2, total, width), low),
            pltpu.VMEM((total, width), low),
            pltpu.VMEM(unit, low),
            pltpu.VMEM(unit, low),
            DMA((2, n - 1)),
            DMA((2, n - 1)),
            DMA,
            DMA((n, chunks)),
            DMA((2, n, chunks)),
        ]
        + PlaneSum.reduce_scratch(unit, low) * 2,
        compiler_params=remote_params(collective_id, 32),
    )(pieces, tokens, out_weight, *vectors, up, down, bias, near, cotangent)


def last_kernel(n, shared, count, x_ref, u_ref, a_ref, *rest):
    ps, rest = rest[:count], rest[count:]
    token_ref, gain_ref, middle_ref, vec_ref, rest = rest[0], rest[1], rest[2], rest[3], rest[4:]
    g_ref, v_ref, po_ref, ao_ref, rest = rest[0], rest[1], rest[2], rest[3], rest[4:]
    outs, rest = rest[:count], rest[count:]
    sum_ref, piece, rest = rest[0], rest[1], rest[2:]
    line = LineScatter(n, x_ref, sum_ref, *rest[:4])
    project = PlaneSum(u_ref, piece, po_ref, rest[4:14], rest[14:17])
    rest = rest[17:]
    feeds = [PlaneSum(None, ps[i], outs[i], None, rest[3 * i : 3 * i + 3]) for i in range(count)]
    rest = rest[3 * count :]
    asend, arecv, aloc, now, rest = rest[0], rest[1], rest[2], rest[3], rest[4:]
    names, sizes = ("tensor", "context", "dp"), (n, 4, 2)
    bufs, sems = rest[:3], rest[3:]

    ten, ctx, x = (lax.axis_index(name) for name in names)
    place = ctx * 2 + x
    bar = pltpu.get_barrier_semaphore()
    for shift in range(1, n):
        pl.semaphore_signal(bar, inc=1, device_id={"tensor": lax.rem(ten + shift, n)}, device_id_type=MESH)
    for shift in range(1, 8):
        other = lax.rem(place + shift, 8)
        pl.semaphore_signal(
            bar, inc=1, device_id={"context": lax.div(other, 2), "dp": lax.rem(other, 2)}, device_id_type=MESH
        )
    pl.semaphore_wait(bar, n + 6)

    def there(at):
        ctx_, x_ = lax.div(at, 2), lax.rem(at, 2)
        y_ = lax.div(ctx_, 2)
        row = jnp.where(ten < n // 2, 2 * x_ + y_, 2 * y_ + x_)
        rows = pl.ds(pl.multiple_of(row * a_ref.shape[0], 16), a_ref.shape[0])
        cols = pl.ds(pl.multiple_of(lax.rem(ctx_, 2) * a_ref.shape[1], 128), a_ref.shape[1])
        return ao_ref.at[rows, cols]

    def push(shift):
        other = lax.rem(place + shift, 8)
        return pltpu.make_async_remote_copy(
            src_ref=a_ref,
            dst_ref=there(place),
            send_sem=asend.at[shift],
            recv_sem=arecv.at[shift],
            device_id={"context": lax.div(other, 2), "dp": lax.rem(other, 2)},
            device_id_type=MESH,
        )

    line.begin()
    project.begin()
    for item in feeds:
        item.spread1()
    for shift in range(1, 8):
        push(shift).start()
    kept = pltpu.make_async_copy(a_ref, there(place), aloc)
    kept.start()
    normed, scale = norm_parts(token_ref[...].astype(jnp.float32))
    project.first()
    line.step(0)
    for item in feeds:
        item.spread2()
    project.second()
    for k in range(1, n - 1):
        line.step(k)
    for item in feeds:
        item.spread3()
    project.third()
    project.spread1()
    line.end()
    grad = sum_ref[...]
    now[0] = vec_ref[...]
    now[0, 0:1] = jnp.sum(grad * normed, axis=0, keepdims=True)
    now[0, 1:2] = jnp.sum(grad, axis=0, keepdims=True)

    def stage_copy(stage, shift):
        name, size = names[stage], sizes[stage]
        me = lax.axis_index(name)
        return pltpu.make_async_remote_copy(
            src_ref=now.at[stage],
            dst_ref=bufs[stage].at[me],
            send_sem=sems[2 * stage].at[shift],
            recv_sem=sems[2 * stage + 1].at[shift],
            device_id={name: lax.rem(me + shift, size)},
            device_id_type=MESH,
        )

    def stage_start(stage):
        for shift in range(1, sizes[stage]):
            stage_copy(stage, shift).start()
        bufs[stage][lax.axis_index(names[stage])] = now[stage]

    def stage_end(stage):
        buf, size = bufs[stage], sizes[stage]
        me = lax.axis_index(names[stage])
        for shift in range(1, size):
            source = lax.rem(me + size - shift, size)
            pltpu.make_async_copy(buf.at[source], buf.at[source], sems[2 * stage + 1].at[shift]).wait()
        total = buf[0]
        for at in range(1, size):
            total = total + buf[at]
        if stage == 0:
            row = lax.broadcasted_iota(jnp.int32, total.shape, 0)
            total = jnp.where(row < shared, total, vec_ref[...])
        if stage < 2:
            now[stage + 1] = total
        else:
            v_ref[...] = total

    stage_start(0)
    back = norm_backward(grad, normed, scale, row(gain_ref))
    g_ref[...] = (middle_ref[...] + back).astype(g_ref.dtype)
    project.spread2()
    stage_end(0)
    stage_start(1)
    project.spread3()
    stage_end(1)
    stage_start(2)
    kept.wait()
    for shift in range(1, 8):
        source = there(lax.rem(place + 8 - shift, 8))
        pltpu.make_async_copy(source, source, arecv.at[shift]).wait()
    for item in feeds:
        item.everywhere()
    stage_end(2)
    project.everywhere()
    project.reduced()
    for shift in range(1, 8):
        push(shift).wait_send()
    for stage in range(3):
        for shift in range(1, sizes[stage]):
            stage_copy(stage, shift).wait_send()


def last_part(x, unit, attend_piece, pieces, tokens, gain, grad_middle, vectors, shared, n, collective_id):
    rows, cols = x.shape
    own = rows // n
    count = len(pieces)
    f32, low = jnp.float32, x.dtype
    whole = lambda item: jax.ShapeDtypeStruct((16,) + item.shape[1:], item.dtype)
    wide, deep = attend_piece.shape
    result = pl.pallas_call(
        functools.partial(last_kernel, n, shared, count),
        out_shape=(
            jax.ShapeDtypeStruct((own, cols), low),
            jax.ShapeDtypeStruct(vectors.shape, f32),
            whole(unit),
            jax.ShapeDtypeStruct((4 * wide, 2 * deep), low),
        )
        + tuple(whole(item) for item in pieces),
        in_specs=[VM] * (7 + count),
        out_specs=(VM,) * (4 + count),
        scratch_shapes=[pltpu.VMEM((own, cols), f32), pltpu.VMEM((2,) + unit.shape[1:], low)]
        + LineScatter.scratch(n, own, cols, low)
        + PlaneSum.reduce_scratch(unit.shape, low)
        + PlaneSum.spread_scratch()
        + [item for _ in pieces for item in PlaneSum.spread_scratch()]
        + [DMA((8,)), DMA((8,)), DMA, pltpu.VMEM((3,) + vectors.shape, f32)]
        + [pltpu.VMEM((size,) + vectors.shape, f32) for size in (n, 4, 2)]
        + [DMA((size,)) for size in (n, 4, 2) for _ in range(2)],
        compiler_params=remote_params(collective_id),
    )(x.reshape(n, own, cols), unit, attend_piece, *pieces, tokens, gain, grad_middle, vectors)
    return result[0], result[1], result[2], result[3], result[4:]


def rows_back_sum_kernel(nc, nt, heads, x_ref, u_ref, o_ref, p_ref, send, recv, loc, *rest):
    total = nc * nt
    my_ctx, my_ten = lax.axis_index("context"), lax.axis_index("tensor")
    me = my_ctx * nt + my_ten
    bar = pltpu.get_barrier_semaphore()
    for shift in range(1, total):
        other = lax.rem(me + shift, total)
        pl.semaphore_signal(bar, inc=1, device_id=spread(other, AXES, (nc, nt)), device_id_type=MESH)
    x = lax.axis_index("dp")
    pl.semaphore_signal(bar, inc=1, device_id={"dp": 1 - x}, device_id_type=MESH)
    pl.semaphore_wait(bar, total)

    unit = StripSum(u_ref, p_ref, None, rest)

    def copy(shift):
        other = lax.rem(me + shift, total)
        ctx, ten = lax.div(other, nt), lax.rem(other, nt)
        return ctx < heads, pltpu.make_async_remote_copy(
            src_ref=x_ref.at[ten * heads + jnp.minimum(ctx, heads - 1)],
            dst_ref=o_ref.at[me],
            send_sem=send.at[shift],
            recv_sem=recv.at[shift],
            device_id={"context": ctx, "tensor": ten},
            device_id_type=MESH,
        )

    for shift in range(1, total):
        goes, item = copy(shift)

        @pl.when(goes)
        def _():
            item.start()

    unit.begin()
    own = pltpu.make_async_copy(
        x_ref.at[my_ten * heads + jnp.minimum(my_ctx, heads - 1)], o_ref.at[me], loc
    )
    own.start()
    own.wait()
    unit.first()
    unit.second()
    unit.third()

    @pl.when(my_ctx < heads)
    def _():
        for shift in range(1, total):
            source = lax.rem(me + total - shift, total)
            pltpu.make_async_copy(o_ref.at[source], o_ref.at[source], recv.at[shift]).wait()

    unit.reduced()
    for shift in range(1, total):
        goes, item = copy(shift)

        @pl.when(goes)
        def _():
            item.wait_send()


def rows_back_sum(x, unit, nc, nt, heads, collective_id):
    total = nc * nt
    return pl.pallas_call(
        functools.partial(rows_back_sum_kernel, nc, nt, heads),
        out_shape=(
            jax.ShapeDtypeStruct((total,) + x.shape[1:], x.dtype),
            jax.ShapeDtypeStruct((2, 2, unit.shape[1] // 4, unit.shape[2] // 2), unit.dtype),
        ),
        in_specs=[VM, VM],
        out_specs=(VM, VM),
        scratch_shapes=[DMA((total,)), DMA((total,)), DMA] + StripSum.reduce_scratch(unit.shape, unit.dtype),
        compiler_params=remote_params(collective_id),
    )(x, unit)


class LineGather:
    def __init__(self, n, x, o, send, recv):
        self.n, self.x, self.o, self.send, self.recv = n, x, o, send, recv
        self.me = lax.axis_index("tensor")

    def copy(self, d, s):
        me, n = self.me, self.n
        shard = jnp.clip(me - s if d == 0 else me + s, 0, n - 1)
        return pltpu.make_async_remote_copy(
            src_ref=self.x if s == 0 else self.o.at[shard],
            dst_ref=self.o.at[shard],
            send_sem=self.send.at[d, s],
            recv_sem=self.recv.at[d, s],
            device_id={"tensor": jnp.clip(me + 1 if d == 0 else me - 1, 0, n - 1)},
            device_id_type=MESH,
        )

    def sends(self, d, s):
        me, n = self.me, self.n
        return (me - s >= 0) & (me < n - 1) if d == 0 else (me + s < n) & (me > 0)

    def wait(self, d, s):
        me, n = self.me, self.n

        @pl.when(me - 1 - s >= 0 if d == 0 else me + 1 + s < n)
        def _():
            shard = jnp.clip(me - 1 - s if d == 0 else me + 1 + s, 0, n - 1)
            pltpu.make_async_copy(self.o.at[shard], self.o.at[shard], self.recv.at[d, s]).wait()

    def step(self, s):
        for d in range(2):
            if s > 0:
                self.wait(d, s - 1)

            @pl.when(self.sends(d, s))
            def _():
                self.copy(d, s).start()

    def last(self):
        for d in range(2):
            self.wait(d, self.n - 2)

    def finish(self, steps=None):
        for d in range(2):
            for s in range(steps or self.n - 1):

                @pl.when(self.sends(d, s))
                def _():
                    self.copy(d, s).wait_send()


def start_kernel(n, nc, heads, t_ref, gain_ref, shift_ref, full_ref, w_hbm, b_ref, c_ref, o_ref, f_ref, q_ref, g_ref, *rest):
    (x_ref, held, proj, w_ref), rest = rest[:4], rest[4:]
    s1, r1, s2, r2, s5, r5, s3, r3, s4, r4, loc = rest
    me, ctx, x = lax.axis_index("tensor"), lax.axis_index("context"), lax.axis_index("dp")
    core, y = lax.rem(ctx, 2), lax.div(ctx, 2)
    rows, width = t_ref.shape
    half = 2 * rows
    bar = pltpu.get_barrier_semaphore()
    met = line_greet(bar, me, n)
    for shift in range(1, nc):
        pl.semaphore_signal(bar, inc=1, device_id={"context": lax.rem(ctx + shift, nc)}, device_id_type=MESH)
    pl.semaphore_signal(bar, inc=1, device_id={"dp": 1 - x}, device_id_type=MESH)
    weight_in = pltpu.make_async_copy(w_hbm, w_ref, loc.at[4])
    weight_in.start()
    normed, _ = norm_parts(t_ref[...].astype(jnp.float32))
    x_ref[...] = (normed * row(gain_ref) + row(shift_ref)).astype(x_ref.dtype)
    pl.semaphore_wait(bar, met + nc)

    tall, deep = held.shape[1:]
    strip = pl.ds(pl.multiple_of(core * deep, 128), deep)
    piece = full_ref.at[pl.ds(pl.multiple_of((2 * y + x) * tall, 16), tall), strip]
    small = LineGather(n, piece, held, s1, r1)
    large = LineGather(n, x_ref, o_ref, s2, r2)
    grads = LineGather(n, c_ref, g_ref, s5, r5)
    small.step(0)
    large.step(0)
    own = pltpu.make_async_copy(x_ref, o_ref.at[me], loc.at[0])
    own.start()
    mine = pltpu.make_async_copy(piece, held.at[me], loc.at[1])
    mine.start()
    mine.wait()
    own.wait()
    for s in range(1, n - 1):
        small.step(s)
    small.last()

    def there(y_, x_):
        return f_ref.at[:, pl.ds(pl.multiple_of((2 * y_ + x_) * tall, 16), tall), strip]

    x_peer, y_peer = {"dp": 1 - x}, {"context": lax.rem(ctx + 2, 4)}

    def hop(at):
        src, dst, peer = [
            (held, there(y, x), x_peer),
            (held, there(y, x), y_peer),
            (there(y, 1 - x), there(y, 1 - x), y_peer),
            (f_ref.at[:, :, strip], f_ref.at[:, :, strip], {"context": ctx + 1 - 2 * core}),
        ][at]
        return pltpu.make_async_remote_copy(
            src_ref=src,
            dst_ref=dst,
            send_sem=s3.at[at],
            recv_sem=r3.at[at],
            device_id=peer,
            device_id_type=MESH,
        )

    def got(at):
        other = pl.ds(pl.multiple_of((1 - core) * deep, 128), deep)
        ref = [there(y, 1 - x), there(1 - y, x), there(1 - y, 1 - x), f_ref.at[:, :, other]][at]
        pltpu.make_async_copy(ref, ref, r3.at[at]).wait()

    hop(0).start()
    kept = pltpu.make_async_copy(held, there(y, x), loc.at[2])
    kept.start()

    def columns(pair):
        return pl.ds(pl.multiple_of(pair * half, 128), half)

    def project(pair):
        token = jnp.concatenate([o_ref[2 * pair], o_ref[2 * pair + 1]], axis=0)
        for kind in range(3):
            value = dot(w_ref[kind], token, ((0,), (1,))) + b_ref[kind]
            proj[kind, :, :, columns(pair)] = value.astype(proj.dtype).reshape(heads, HEAD_DIM, half)

    def ship(index, pair, shift):
        other = lax.rem(ctx + shift, nc)
        return other, pltpu.make_async_remote_copy(
            src_ref=proj.at[:, jnp.minimum(other, heads - 1), :, columns(pair)],
            dst_ref=q_ref.at[ctx, :, :, columns(pair)],
            send_sem=s4.at[index, shift],
            recv_sem=r4.at[index, shift],
            device_id={"context": other},
            device_id_type=MESH,
        )

    def ship_all(index, pair):
        for shift in range(1, nc):
            other, item = ship(index, pair, shift)

            @pl.when(other < heads)
            def _():
                item.start()

    near = lax.div(me, 2)
    large.step(1)
    weight_in.wait()
    project(near)
    ship_all(0, near)
    hop(1).start()
    for s in range(2, n - 1):
        large.step(s)
    grads.step(0)
    got(0)
    hop(2).start()
    large.last()
    project(1 - near)
    ship_all(1, 1 - near)
    stay = pltpu.make_async_copy(proj.at[:, jnp.minimum(ctx, heads - 1)], q_ref.at[ctx], loc.at[3])
    stay.start()
    kept.wait()
    got(1)
    got(2)
    hop(3).start()
    stay.wait()

    @pl.when(ctx < heads)
    def _():
        for index in range(2):
            for shift in range(1, nc):
                source = lax.rem(ctx + nc - shift, nc)
                pair = near if index == 0 else 1 - near
                ref = q_ref.at[source, :, :, columns(pair)]
                pltpu.make_async_copy(ref, ref, r4.at[index, shift]).wait()

    got(3)
    for d in range(2):
        grads.wait(d, 0)
    small.finish()
    large.finish()
    grads.finish(1)
    for at in range(4):
        hop(at).wait_send()
    for index in range(2):
        for shift in range(1, nc):
            other, item = ship(index, near if index == 0 else 1 - near, shift)

            @pl.when(other < heads)
            def _():
                item.wait_send()


def start_part(tokens, gain, shift, w, project_weight, bias, cotangent, n, nc, heads, collective_id):
    rows, cols = tokens.shape
    wide, deep = w.shape
    low = jnp.bfloat16
    full, weight, qkv, grads = pl.pallas_call(
        functools.partial(start_kernel, n, nc, heads),
        out_shape=(
            jax.ShapeDtypeStruct((n, rows, cols), low),
            jax.ShapeDtypeStruct((n, wide, deep), w.dtype),
            jax.ShapeDtypeStruct((nc, 3, HEAD_DIM, n * rows), low),
            jax.ShapeDtypeStruct((n, rows, cols), low),
        ),
        in_specs=[VM, VM, VM, ANY, ANY, VM, ANY],
        out_specs=(VM,) * 4,
        scratch_shapes=[
            pltpu.VMEM((rows, cols), low),
            pltpu.VMEM((n, wide // 4, deep // 2), w.dtype),
            pltpu.VMEM((3, heads, HEAD_DIM, n * rows), low),
            pltpu.VMEM(project_weight.shape, low),
        ]
        + [DMA((2, n - 1)) for _ in range(6)]
        + [DMA((4,)), DMA((4,)), DMA((2, nc)), DMA((2, nc)), DMA((5,))],
        compiler_params=remote_params(collective_id),
    )(tokens, gain, shift, w, project_weight, bias, cotangent)
    return full.reshape(n * rows, cols), weight.reshape(n * wide, deep), qkv, grads


def dot(left, right, dims):
    return lax.dot_general(left, right, ((dims[0], dims[1]), ((), ())), preferred_element_type=jnp.float32)


def key_positions(first, keys, queries):
    return first + lax.broadcasted_iota(jnp.int32, (keys, queries), 0)


def load_rows(qkv_ref, nb, half, qs, kt, ks, vs):
    for block in range(nb):
        part = slice(block % 2 * half, block % 2 * half + half)
        at = block // 2
        qs[block] = qkv_ref[at, 0, :, part] * jnp.asarray(HEAD_DIM**-0.5, qs.dtype)
        item = qkv_ref[at, 1, :, part]
        if kt is not None:
            kt[block] = item
        ks[block] = item.T
        if vs is not None:
            vs[block] = qkv_ref[at, 2, :, part].T


def fill_tables(nb, half, seg_ref, order_ref, slot_ref, low_ref, high_ref):
    for block in range(nb):
        slot_ref[order_ref[block]] = jnp.int32(block)
    first = [seg_ref[0, block * half] for block in range(nb)]
    last = [seg_ref[0, block * half + half - 1] for block in range(nb)]
    for block in range(nb):
        if low_ref is not None:
            low_ref[block] = sum(jnp.where(item < first[block], 1, 0) for item in last)
        if high_ref is not None:
            high_ref[block] = sum(jnp.where(item <= last[block], 1, 0) for item in first)


def forward_kernel(half, heads, seg_s, order_ref, seg_ref, qkv_ref, o_ref, full_ref, lse_ref, start_ref, qs, ks, slot_ref, low_ref):
    nb = full_ref.shape[0]

    @pl.when(lax.axis_index("context") < heads)
    def _():
        load_rows(qkv_ref, nb, half, qs, None, ks, None)
        fill_tables(nb, half, seg_s, order_ref, slot_ref, low_ref, None)
        seg = seg_ref[...]
        start = jnp.zeros(seg.shape, jnp.float32)
        for doc in range(1, DOC_LIMIT):
            before = jnp.sum(jnp.where(seg < doc, 1.0, 0.0), axis=1, keepdims=True)
            start = jnp.where(seg == doc, before, start)
        start_ref[...] = start.astype(jnp.int32)

        @pl.loop(0, nb)
        def _(nq):
            slot = slot_ref[nq]
            query = qs[slot]
            begin = start_ref[:, pl.ds(pl.multiple_of(nq * half, 128), half)]
            here = nq * half + lax.broadcasted_iota(jnp.int32, (1, half), 1)

            def step(nk, state):
                top, total, acc = state
                at = slot_ref[nk]
                score = dot(ks[at], query, ((1,), (0,)))
                place = key_positions(nk * half, half, half)
                score = jnp.where((place >= begin) & (place <= here), score, NEG_FILL)
                new_top = jnp.maximum(top, jnp.max(score, axis=0, keepdims=True))
                factor = jnp.exp(top - new_top)
                weight = jnp.exp(score - new_top)
                total = total * factor + jnp.sum(weight, axis=0, keepdims=True)
                value = qkv_ref[at // 2, 2, :, pl.ds(pl.multiple_of(at % 2 * half, 128), half)]
                acc = acc * factor + dot(value, weight.astype(jnp.bfloat16), ((1,), (0,)))
                return new_top, total, acc

            top, total, acc = lax.fori_loop(
                low_ref[nq],
                nq + 1,
                step,
                (
                    jnp.full((1, half), NEG_FILL, jnp.float32),
                    jnp.zeros((1, half), jnp.float32),
                    jnp.zeros((HEAD_DIM, half), jnp.float32),
                ),
            )
            result = acc / total
            full_ref[slot] = result
            lse_ref[slot] = top + jnp.log(total)
            low = result.astype(jnp.bfloat16)
            o_ref[2 * slot] = low[:, : half // 2]
            o_ref[2 * slot + 1] = low[:, half // 2 :]


def attend_forward(qkv, segments, order, half, heads):
    nc = qkv.shape[0]
    nb = 2 * nc
    return pl.pallas_call(
        functools.partial(forward_kernel, half, heads),
        out_shape=(
            jax.ShapeDtypeStruct((2 * nb, HEAD_DIM, half // 2), jnp.bfloat16),
            jax.ShapeDtypeStruct((nb, HEAD_DIM, half), jnp.float32),
            jax.ShapeDtypeStruct((nb, 1, half), jnp.float32),
            jax.ShapeDtypeStruct(segments.shape, jnp.int32),
        ),
        in_specs=[SM, SM, VM, VM],
        out_specs=(VM, VM, VM, VM),
        scratch_shapes=[
            pltpu.VMEM((nb, HEAD_DIM, half), jnp.bfloat16),
            pltpu.VMEM((nb, half, HEAD_DIM), jnp.bfloat16),
            pltpu.SMEM((nb,), jnp.int32),
            pltpu.SMEM((nb,), jnp.int32),
        ],
        compiler_params=pltpu.CompilerParams(vmem_limit_bytes=24 << 20),
    )(segments, order, segments, qkv)


def backward_kernel(
    half, heads, seg_s, order_ref, start_ref, qkv_ref, full_ref, lse_ref, grad_ref, o_ref,
    qs, kt, ks, vs, gs, ds, dq, slot_ref, high_ref,
):
    nb = full_ref.shape[0]

    @pl.when(lax.axis_index("context") < heads)
    def _():
        load_rows(qkv_ref, nb, half, qs, kt, ks, vs)
        fill_tables(nb, half, seg_s, order_ref, slot_ref, None, high_ref)
        for block in range(nb):
            both = jnp.concatenate([grad_ref[2 * block], grad_ref[2 * block + 1]], axis=1)
            gs[block] = both
            ds[block] = jnp.sum(both.astype(jnp.float32) * full_ref[block], axis=0, keepdims=True)
            dq[block] = jnp.zeros((HEAD_DIM, half), jnp.float32)

        @pl.loop(0, nb)
        def _(nk):
            at = slot_ref[nk]
            place = key_positions(nk * half, half, half)

            def step(nq, state):
                grad_key, grad_value = state
                slot = slot_ref[nq]
                query, grad = qs[slot], gs[slot]
                begin = start_ref[:, pl.ds(pl.multiple_of(nq * half, 128), half)]
                here = nq * half + lax.broadcasted_iota(jnp.int32, (1, half), 1)
                score = dot(ks[at], query, ((1,), (0,)))
                score = jnp.where((place >= begin) & (place <= here), score, NEG_FILL)
                weight = jnp.exp(score - lse_ref[slot])
                grad_weight = dot(vs[at], grad, ((1,), (0,)))
                grad_score = (weight * (grad_weight - ds[slot])).astype(jnp.bfloat16)
                grad_value = grad_value + dot(grad, weight.astype(jnp.bfloat16), ((1,), (1,)))
                grad_key = grad_key + dot(query, grad_score, ((1,), (1,)))
                dq[slot] += dot(kt[at], grad_score, ((1,), (0,)))
                return grad_key, grad_value

            zero = jnp.zeros((HEAD_DIM, half), jnp.float32)
            grad_key, grad_value = lax.fori_loop(nk, high_ref[nk], step, (zero, zero))
            columns = pl.ds(pl.multiple_of(at % 2 * half, 128), half)
            o_ref[at // 2, 1, :, columns] = grad_key.astype(jnp.bfloat16)
            o_ref[at // 2, 2, :, columns] = grad_value.astype(jnp.bfloat16)

        for block in range(nb):
            part = slice(block % 2 * half, block % 2 * half + half)
            o_ref[block // 2, 0, :, part] = (dq[block] * HEAD_DIM**-0.5).astype(jnp.bfloat16)


def attend_backward(qkv, segments, order, start, full, lse, grad, half, heads):
    nc = qkv.shape[0]
    nb = 2 * nc
    low = jnp.bfloat16
    return pl.pallas_call(
        functools.partial(backward_kernel, half, heads),
        out_shape=jax.ShapeDtypeStruct(qkv.shape, low),
        in_specs=[SM, SM, VM, VM, VM, VM, VM],
        out_specs=VM,
        scratch_shapes=[
            pltpu.VMEM((nb, HEAD_DIM, half), low),
            pltpu.VMEM((nb, HEAD_DIM, half), low),
            pltpu.VMEM((nb, half, HEAD_DIM), low),
            pltpu.VMEM((nb, half, HEAD_DIM), low),
            pltpu.VMEM((nb, HEAD_DIM, half), low),
            pltpu.VMEM((nb, 1, half), jnp.float32),
            pltpu.VMEM((nb, HEAD_DIM, half), jnp.float32),
            pltpu.SMEM((nb,), jnp.int32),
            pltpu.SMEM((nb,), jnp.int32),
        ],
        compiler_params=pltpu.CompilerParams(vmem_limit_bytes=24 << 20),
    )(segments, order, start, qkv, full, lse, grad)


def norm_parts(values):
    centre = jnp.mean(values, axis=-1, keepdims=True)
    shifted = values - centre
    spread_ = jnp.mean(shifted * shifted, axis=-1, keepdims=True)
    scale = lax.rsqrt(spread_ + NORM_EPS)
    return shifted * scale, scale


def norm_backward(grad, normed, scale, gain):
    e = grad * gain
    mean_e = jnp.mean(e, axis=-1, keepdims=True)
    mean_en = jnp.mean(e * normed, axis=-1, keepdims=True)
    return (e - mean_e - normed * mean_en) * scale


def gelu_tanh(values):
    return jax.nn.gelu(values, approximate=True)


def cross_rows(left, right):
    return lax.dot_general(
        left, right, (((0,), (0,)), ((), ())), preferred_element_type=jnp.float32
    )


def after(value, done):
    return lax.optimization_barrier((value, done))[0]


def per_device(
    mesh_sizes,
    inputs,
    first_gain,
    first_shift,
    project_weight,
    project_bias,
    attend_weight,
    attend_bias,
    second_gain,
    second_shift,
    expand_weight,
    expand_bias,
    shrink_weight,
    shrink_bias,
    segments,
    block_order,
    cotangent,
):
    nt, nc = mesh_sizes["tensor"], mesh_sizes["context"]
    own_rows, width = inputs.shape[1], inputs.shape[2]
    local_width = project_weight.shape[2]
    heads = local_width // HEAD_DIM
    block_rows = own_rows * nt
    half = block_rows // 2
    low = jnp.bfloat16
    f32 = lambda value: value.astype(jnp.float32)
    square = nt == 4 and nc == 4 and mesh_sizes["dp"] == 2
    plane = ("context", "dp")

    tokens_own = f32(inputs[0])
    grad_out = cotangent[0]
    bias = jnp.stack([project_bias[0], jnp.zeros_like(project_bias[0]), project_bias[1]])[:, :, None]
    if square:
        hidden1_full, attend_full, qkv, grads_near = start_part(
            inputs[0], first_gain, first_shift, attend_weight, project_weight, bias, grad_out, nt, nc, heads, 0
        )
    else:
        hidden1 = norm_parts(tokens_own)[0] * first_gain + first_shift
        hidden1_full = gather_rows(hidden1.astype(low), nt, 0)
        attend_full = lax.all_gather(attend_weight, "tensor", axis=0, tiled=True)
        projected = jnp.einsum(
            "kde,rd->ker", project_weight, hidden1_full, preferred_element_type=jnp.float32
        )
        projected = (projected + bias).astype(low).reshape(3, heads, HEAD_DIM, block_rows)
        qkv = to_heads(projected, nc, 1)
    pieces, attended_full, lse, start = attend_forward(qkv, segments, block_order, half, heads)
    grad_shrink_bias = jnp.sum(f32(grad_out), axis=0)

    if square:
        grad_hidden2, feed, grad_expand_bias, *feed_pieces, middle, attended = feed_part(
            pieces,
            inputs[0],
            attend_full,
            (attend_bias, second_gain, second_shift),
            expand_weight,
            shrink_weight,
            expand_bias,
            grads_near,
            grad_out,
            nt,
            nc,
            heads,
            3,
        )
        attended = attended.reshape(width, own_rows)
        grad_expand_bias = grad_expand_bias[0]
        normed2, scale2 = norm_parts(middle)
    else:
        grad_full = lax.all_gather(grad_out, "tensor", axis=0, tiled=True)
        attended = to_rows(pieces, nc, nt, heads, 2).reshape(width, own_rows)
        middle = tokens_own + cross_rows(attended, attend_full) + attend_bias
        normed2, scale2 = norm_parts(middle)
        hidden2 = (normed2 * second_gain + second_shift).astype(low)
        hidden2_full = gather_rows(hidden2, nt, 3)
        pre_act = jnp.dot(hidden2_full, expand_weight, preferred_element_type=jnp.float32) + expand_bias
        activ = gelu_tanh(pre_act).astype(low)
        grad_act = dot(grad_full, shrink_weight, ((1,), (1,)))
        grad_pre = jax.vjp(gelu_tanh, pre_act)[1](grad_act)[0].astype(low)
        grad_shrink = cross_rows(activ, grad_full).astype(low)
        grad_expand = cross_rows(hidden2_full, grad_pre).astype(low)
        grad_hidden2 = scatter_rows(dot(grad_pre, expand_weight, ((1,), (1,))).astype(low), nt, 4)
        grad_expand_bias = jnp.sum(f32(grad_pre), axis=0)
        feed = jnp.dot(activ, shrink_weight, preferred_element_type=jnp.float32).astype(low)

    grad_second_gain = jnp.sum(grad_hidden2 * normed2, axis=0)
    grad_second_shift = jnp.sum(grad_hidden2, axis=0)
    grad_middle = f32(grad_out) + norm_backward(grad_hidden2, normed2, scale2, second_gain)
    grad_middle_low = grad_middle.astype(low)
    grad_attend_bias = jnp.sum(f32(grad_middle_low), axis=0)
    grad_attended = dot(attend_full, grad_middle_low, ((1,), (1,))).astype(low)
    grad_attended = grad_attended.reshape(nt * heads, HEAD_DIM, own_rows)
    grad_attend = jnp.dot(attended, grad_middle_low, preferred_element_type=jnp.float32).astype(low)
    if square:
        unit = grad_attend.reshape(nt, local_width, width)
        grad_heads, attend_pieces = rows_back_sum(grad_attended, unit, nc, nt, heads, 5)
    else:
        grad_heads = rows_back(grad_attended, nc, nt, heads, 5)
        attend_pieces = None
    feed_sum = lax.psum_scatter(after(feed, grad_heads), "tensor", scatter_dimension=0, tiled=True)

    grad_qkv = attend_backward(qkv, segments, block_order, start, attended_full, lse, grad_heads, half, heads)
    grad_rows = from_heads(grad_qkv, attend_pieces, nc, nt, heads, 6)
    if square:
        grad_rows, attend_piece = grad_rows
    grad_rows = grad_rows.reshape(3 * local_width, block_rows)
    grad_project = dot(hidden1_full, grad_rows, ((0,), (1,))).astype(low)
    grad_hidden1 = lax.dot_general(
        grad_rows.reshape(3, local_width, block_rows),
        project_weight,
        (((0, 1), (0, 2)), ((), ())),
        preferred_element_type=jnp.float32,
    ).astype(low)
    row_sums = jnp.sum(f32(grad_rows), axis=1)
    grad_project_bias = jnp.concatenate([row_sums[:local_width], row_sums[2 * local_width :]])

    wide = grad_expand_bias.shape[0]
    spare = -(wide + 2 * local_width) % width
    others = [
        grad_attend_bias,
        grad_second_gain,
        grad_second_shift,
        grad_shrink_bias,
        grad_expand_bias,
        jnp.pad(grad_project_bias, (0, spare)),
    ]
    if square:
        empty = jnp.zeros((2 * width,), jnp.float32)
        vectors = jnp.concatenate([empty] + others).reshape(-1, width)
        grad_inputs, summed, grad_project, grad_attend, feeds = last_part(
            grad_hidden1,
            grad_project.reshape(16, -1, 3 * local_width),
            attend_piece,
            feed_pieces,
            inputs[0],
            first_gain,
            grad_middle,
            vectors,
            6,
            nt,
            7,
        )
        grad_project = grad_project.reshape(width, 3 * local_width)
        grad_shrink, grad_expand = feeds[0].reshape(-1, width), feeds[1].reshape(width, -1)
    else:
        grad_hidden1 = scatter_rows(grad_hidden1, nt, 7)
        normed1, scale1 = norm_parts(tokens_own)
        back = norm_backward(grad_hidden1, normed1, scale1, first_gain)
        grad_inputs = (grad_middle + back).astype(low)
        both = [jnp.sum(grad_hidden1 * normed1, axis=0), jnp.sum(grad_hidden1, axis=0)]
        vectors = jnp.concatenate(both + others).reshape(-1, width)
        summed = sum_vectors(vectors, 6, mesh_sizes, 8)
        grad_attend = lax.psum_scatter(grad_attend, "tensor", scatter_dimension=0, tiled=True)
        grad_project, grad_attend, grad_shrink, grad_expand = lax.psum(
            (grad_project, grad_attend, grad_shrink, grad_expand), plane
        )
    feed_sum = f32(after(feed_sum, summed))
    outputs = (middle + feed_sum + shrink_bias).astype(low)[None]
    grad_project = jnp.stack(
        [grad_project[:, at * local_width : (at + 1) * local_width] for at in range(3)]
    )
    tail = summed[6:].reshape(-1)
    return (
        outputs,
        grad_inputs[None],
        summed[0],
        summed[1],
        f32(grad_project),
        tail[wide : wide + 2 * local_width].reshape(2, local_width),
        f32(grad_attend),
        summed[2],
        summed[3],
        summed[4],
        f32(grad_expand),
        tail[:wide],
        f32(grad_shrink),
        summed[5],
    )


def solution(mesh):
    rows = P("dp", ("context", "tensor"), None)
    in_specs = (
        rows,
        P(),
        P(),
        P(None, None, "tensor"),
        P(None, "tensor"),
        P("tensor", None),
        P(),
        P(),
        P(),
        P(None, "tensor"),
        P("tensor"),
        P("tensor", None),
        P(),
        P("dp", None),
        P(),
        rows,
    )
    out_specs = (
        rows,
        rows,
        P(),
        P(),
        P(None, None, "tensor"),
        P(None, "tensor"),
        P("tensor", None),
        P(),
        P(),
        P(),
        P(None, "tensor"),
        P("tensor"),
        P("tensor", None),
        P(),
    )
    return jax.shard_map(
        functools.partial(per_device, dict(mesh.shape)),
        mesh=mesh,
        in_specs=in_specs,
        out_specs=out_specs,
        check_vma=False,
    )
```

```python
import functools

import jax
import jax.numpy as jnp
from jax import lax
from jax.experimental import pallas as pl
from jax.experimental.pallas import tpu as pltpu
from jax.sharding import PartitionSpec as P

HEAD_DIM = 64
NEG_FILL = -1e30
NORM_EPS = 1e-05
DOC_LIMIT = 16
MESH = pl.DeviceIdType.MESH
VM = pl.BlockSpec(memory_space=pltpu.VMEM)
SM = pl.BlockSpec(memory_space=pltpu.SMEM)
DMA = pltpu.SemaphoreType.DMA


def remote_params(collective_id, mib=16):
    return pltpu.CompilerParams(
        collective_id=collective_id, has_side_effects=True, vmem_limit_bytes=mib << 20
    )


ANY = pl.BlockSpec(memory_space=pl.ANY)


def row(ref):
    return ref[...].reshape(1, -1)


def line_barrier(me, n):
    bar = pltpu.get_barrier_semaphore()

    @pl.when(me > 0)
    def _():
        pl.semaphore_signal(bar, inc=1, device_id={"tensor": me - 1}, device_id_type=MESH)

    @pl.when(me < n - 1)
    def _():
        pl.semaphore_signal(bar, inc=1, device_id={"tensor": me + 1}, device_id_type=MESH)

    pl.semaphore_wait(bar, jnp.where(me > 0, 1, 0) + jnp.where(me < n - 1, 1, 0))


def gather_kernel(n, x_ref, o_ref, send, recv, loc):
    me = lax.axis_index("tensor")
    line_barrier(me, n)
    own = pltpu.make_async_copy(x_ref, o_ref.at[me], loc)
    own.start()

    def copy(d, s):
        shard = jnp.clip(me - s if d == 0 else me + s, 0, n - 1)
        return pltpu.make_async_remote_copy(
            src_ref=x_ref if s == 0 else o_ref.at[shard],
            dst_ref=o_ref.at[shard],
            send_sem=send.at[d, s],
            recv_sem=recv.at[d, s],
            device_id={"tensor": jnp.clip(me + 1 if d == 0 else me - 1, 0, n - 1)},
            device_id_type=MESH,
        )

    def sends(d, s):
        return (me - s >= 0) & (me < n - 1) if d == 0 else (me + s < n) & (me > 0)

    def gets(d, s):
        return me - 1 - s >= 0 if d == 0 else me + 1 + s < n

    def landed(d, s):
        shard = jnp.clip(me - 1 - s if d == 0 else me + 1 + s, 0, n - 1)
        return pltpu.make_async_copy(o_ref.at[shard], o_ref.at[shard], recv.at[d, s])

    for s in range(n - 1):
        for d in range(2):
            if s > 0:

                @pl.when(gets(d, s - 1))
                def _():
                    landed(d, s - 1).wait()

            @pl.when(sends(d, s))
            def _():
                copy(d, s).start()

    for d in range(2):

        @pl.when(gets(d, n - 2))
        def _():
            landed(d, n - 2).wait()

        for s in range(n - 1):

            @pl.when(sends(d, s))
            def _():
                copy(d, s).wait_send()

    own.wait()


def gather_rows(x, n, collective_id):
    rows, cols = x.shape
    return pl.pallas_call(
        functools.partial(gather_kernel, n),
        out_shape=jax.ShapeDtypeStruct((n, rows, cols), x.dtype),
        in_specs=[VM],
        out_specs=VM,
        scratch_shapes=[DMA((2, n - 1)), DMA((2, n - 1)), DMA],
        compiler_params=remote_params(collective_id),
    )(x).reshape(n * rows, cols)


def scatter_kernel(n, x_ref, o_ref, buf, tmp, send, recv):
    me = lax.axis_index("tensor")
    line_barrier(me, n)

    def term(d, k):
        return n - 1 - k if d == 0 else k

    def sends(d, k):
        return me < n - 1 - k if d == 0 else me > k

    def behind(d):
        return me > 0 if d == 0 else me < n - 1

    def copy(d, k, first):
        return pltpu.make_async_remote_copy(
            src_ref=x_ref.at[term(d, k)] if first else tmp.at[d, k],
            dst_ref=buf.at[d, k],
            send_sem=send.at[d, k],
            recv_sem=recv.at[d, k],
            device_id={"tensor": jnp.clip(me + 1 if d == 0 else me - 1, 0, n - 1)},
            device_id_type=MESH,
        )

    def landed(d, k):
        return pltpu.make_async_copy(buf.at[d, k], buf.at[d, k], recv.at[d, k])

    for d in range(2):

        @pl.when(jnp.logical_not(behind(d)))
        def _():
            for k in range(n - 1):
                copy(d, k, True).start()

    for k in range(n - 1):
        for d in range(2):

            @pl.when(behind(d) & sends(d, k))
            def _():
                landed(d, k).wait()
                both = buf[d, k].astype(jnp.float32) + x_ref[term(d, k)].astype(jnp.float32)
                tmp[d, k] = both.astype(tmp.dtype)
                copy(d, k, False).start()

    o_ref[...] = x_ref[me].astype(jnp.float32)
    for d in range(2):
        for k in range(n - 1):

            @pl.when(behind(d) & (me == term(d, k)))
            def _():
                landed(d, k).wait()
                o_ref[...] += buf[d, k].astype(jnp.float32)

    for d in range(2):
        for k in range(n - 1):

            @pl.when(sends(d, k))
            def _():
                copy(d, k, False).wait_send()


def scatter_rows(x, n, collective_id):
    rows, cols = x.shape
    own = rows // n
    return pl.pallas_call(
        functools.partial(scatter_kernel, n),
        out_shape=jax.ShapeDtypeStruct((own, cols), jnp.float32),
        in_specs=[VM],
        out_specs=VM,
        scratch_shapes=[
            pltpu.VMEM((2, n - 1, own, cols), x.dtype),
            pltpu.VMEM((2, n - 1, own, cols), x.dtype),
            DMA((2, n - 1)),
            DMA((2, n - 1)),
        ],
        compiler_params=remote_params(collective_id),
    )(x.reshape(n, own, cols))


def group_barrier(axes, sizes):
    mine = [lax.axis_index(name) for name in axes]
    place = sum_index(mine, sizes)
    total = 1
    for size in sizes:
        total *= size
    bar = pltpu.get_barrier_semaphore()
    for shift in range(1, total):
        other = lax.rem(place + shift, total)
        pl.semaphore_signal(bar, inc=1, device_id=spread(other, axes, sizes), device_id_type=MESH)
    pl.semaphore_wait(bar, total - 1)
    return place, total


def sum_index(mine, sizes):
    place = 0
    for at, size in zip(mine, sizes):
        place = place * size + at
    return place


def spread(place, axes, sizes):
    found = {}
    for name, size in reversed(tuple(zip(axes, sizes))):
        found[name] = lax.rem(place, size)
        place = lax.div(place, size)
    return found


def to_heads_kernel(nc, heads, x_ref, o_ref, send, recv, loc):
    me, _ = group_barrier(("context",), (nc,))

    def copy(shift):
        other = lax.rem(me + shift, nc)
        return other, pltpu.make_async_remote_copy(
            src_ref=x_ref.at[:, jnp.minimum(other, heads - 1)],
            dst_ref=o_ref.at[me],
            send_sem=send.at[shift],
            recv_sem=recv.at[shift],
            device_id={"context": other},
            device_id_type=MESH,
        )

    for shift in range(1, nc):
        other, item = copy(shift)

        @pl.when(other < heads)
        def _():
            item.start()

    own = pltpu.make_async_copy(x_ref.at[:, jnp.minimum(me, heads - 1)], o_ref.at[me], loc)
    own.start()
    own.wait()

    @pl.when(me < heads)
    def _():
        for shift in range(1, nc):
            source = lax.rem(me + nc - shift, nc)
            pltpu.make_async_copy(o_ref.at[source], o_ref.at[source], recv.at[shift]).wait()

    for shift in range(1, nc):
        other, item = copy(shift)

        @pl.when(other < heads)
        def _():
            item.wait_send()


def to_heads(x, nc, collective_id):
    heads = x.shape[1]
    return pl.pallas_call(
        functools.partial(to_heads_kernel, nc, heads),
        out_shape=jax.ShapeDtypeStruct((nc, x.shape[0]) + x.shape[2:], x.dtype),
        in_specs=[VM],
        out_specs=VM,
        scratch_shapes=[DMA((nc,)), DMA((nc,)), DMA],
        compiler_params=remote_params(collective_id),
    )(x)


def from_heads_kernel(nc, heads, x_ref, o_ref, send, recv, loc):
    me, _ = group_barrier(("context",), (nc,))

    def copy(shift):
        other = lax.rem(me + shift, nc)
        return pltpu.make_async_remote_copy(
            src_ref=x_ref.at[other],
            dst_ref=o_ref.at[:, jnp.minimum(me, heads - 1)],
            send_sem=send.at[shift],
            recv_sem=recv.at[shift],
            device_id={"context": other},
            device_id_type=MESH,
        )

    @pl.when(me < heads)
    def _():
        for shift in range(1, nc):
            copy(shift).start()
        own = pltpu.make_async_copy(x_ref.at[me], o_ref.at[:, me], loc)
        own.start()
        own.wait()

    for shift in range(1, nc):
        source = lax.rem(me + nc - shift, nc)

        @pl.when(source < heads)
        def _():
            at = jnp.minimum(source, heads - 1)
            pltpu.make_async_copy(o_ref.at[:, at], o_ref.at[:, at], recv.at[shift]).wait()

    @pl.when(me < heads)
    def _():
        for shift in range(1, nc):
            copy(shift).wait_send()


def from_heads(x, nc, heads, collective_id):
    return pl.pallas_call(
        functools.partial(from_heads_kernel, nc, heads),
        out_shape=jax.ShapeDtypeStruct((x.shape[1], heads) + x.shape[2:], x.dtype),
        in_specs=[VM],
        out_specs=VM,
        scratch_shapes=[DMA((nc,)), DMA((nc,)), DMA],
        compiler_params=remote_params(collective_id),
    )(x)


AXES = ("context", "tensor")


def rows_kernel(nc, nt, heads, x_ref, o_ref, send, recv, loc):
    me, total = group_barrier(AXES, (nc, nt))
    my_ctx, my_ten = lax.axis_index("context"), lax.axis_index("tensor")
    my_head = my_ten * heads + jnp.minimum(my_ctx, heads - 1)

    def copy(shift):
        other = lax.rem(me + shift, total)
        return pltpu.make_async_remote_copy(
            src_ref=x_ref.at[other],
            dst_ref=o_ref.at[my_head],
            send_sem=send.at[shift],
            recv_sem=recv.at[shift],
            device_id=spread(other, AXES, (nc, nt)),
            device_id_type=MESH,
        )

    @pl.when(my_ctx < heads)
    def _():
        for shift in range(1, total):
            copy(shift).start()
        own = pltpu.make_async_copy(x_ref.at[me], o_ref.at[my_head], loc)
        own.start()
        own.wait()

    for shift in range(1, total):
        source = lax.rem(me + total - shift, total)
        ctx, ten = lax.div(source, nt), lax.rem(source, nt)

        @pl.when(ctx < heads)
        def _():
            at = ten * heads + jnp.minimum(ctx, heads - 1)
            pltpu.make_async_copy(o_ref.at[at], o_ref.at[at], recv.at[shift]).wait()

    @pl.when(my_ctx < heads)
    def _():
        for shift in range(1, total):
            copy(shift).wait_send()


def to_rows(x, nc, nt, heads, collective_id):
    total = nc * nt
    return pl.pallas_call(
        functools.partial(rows_kernel, nc, nt, heads),
        out_shape=jax.ShapeDtypeStruct((nt * heads,) + x.shape[1:], x.dtype),
        in_specs=[VM],
        out_specs=VM,
        scratch_shapes=[DMA((total,)), DMA((total,)), DMA],
        compiler_params=remote_params(collective_id),
    )(x)


def rows_back_kernel(nc, nt, heads, x_ref, o_ref, send, recv, loc):
    me, total = group_barrier(AXES, (nc, nt))
    my_ctx, my_ten = lax.axis_index("context"), lax.axis_index("tensor")

    def copy(shift):
        other = lax.rem(me + shift, total)
        ctx, ten = lax.div(other, nt), lax.rem(other, nt)
        return ctx < heads, pltpu.make_async_remote_copy(
            src_ref=x_ref.at[ten * heads + jnp.minimum(ctx, heads - 1)],
            dst_ref=o_ref.at[me],
            send_sem=send.at[shift],
            recv_sem=recv.at[shift],
            device_id={"context": ctx, "tensor": ten},
            device_id_type=MESH,
        )

    for shift in range(1, total):
        goes, item = copy(shift)

        @pl.when(goes)
        def _():
            item.start()

    own = pltpu.make_async_copy(
        x_ref.at[my_ten * heads + jnp.minimum(my_ctx, heads - 1)], o_ref.at[me], loc
    )
    own.start()
    own.wait()

    @pl.when(my_ctx < heads)
    def _():
        for shift in range(1, total):
            source = lax.rem(me + total - shift, total)
            pltpu.make_async_copy(o_ref.at[source], o_ref.at[source], recv.at[shift]).wait()

    for shift in range(1, total):
        goes, item = copy(shift)

        @pl.when(goes)
        def _():
            item.wait_send()


def rows_back(x, nc, nt, heads, collective_id):
    total = nc * nt
    return pl.pallas_call(
        functools.partial(rows_back_kernel, nc, nt, heads),
        out_shape=jax.ShapeDtypeStruct((total,) + x.shape[1:], x.dtype),
        in_specs=[VM],
        out_specs=VM,
        scratch_shapes=[DMA((total,)), DMA((total,)), DMA],
        compiler_params=remote_params(collective_id),
    )(x)


def vectors_kernel(names, sizes, shared, x_ref, o_ref, now, *rest):
    bufs, sems = rest[: len(names)], rest[len(names) :]
    bar = pltpu.get_barrier_semaphore()
    for name, size in zip(names, sizes):
        me = lax.axis_index(name)
        for shift in range(1, size):
            pl.semaphore_signal(
                bar, inc=1, device_id={name: lax.rem(me + shift, size)}, device_id_type=MESH
            )
    pl.semaphore_wait(bar, sum(sizes) - len(sizes))
    for stage, (name, size) in enumerate(zip(names, sizes)):
        buf, send, recv = bufs[stage], sems[2 * stage], sems[2 * stage + 1]
        me = lax.axis_index(name)

        def copy(shift):
            return pltpu.make_async_remote_copy(
                src_ref=now.at[stage] if stage else x_ref.at[0],
                dst_ref=buf.at[me],
                send_sem=send.at[shift],
                recv_sem=recv.at[shift],
                device_id={name: lax.rem(me + shift, size)},
                device_id_type=MESH,
            )

        for shift in range(1, size):
            copy(shift).start()
        buf[me] = now[stage] if stage else x_ref[0]
        for shift in range(1, size):
            source = lax.rem(me + size - shift, size)
            pltpu.make_async_copy(buf.at[source], buf.at[source], recv.at[shift]).wait()
        total = buf[0]
        for at in range(1, size):
            total = total + buf[at]
        if stage == 0:
            row = lax.broadcasted_iota(jnp.int32, total.shape, 0)
            total = jnp.where(row < shared, total, x_ref[0])
        if stage + 1 < len(names):
            now[stage + 1] = total
        else:
            o_ref[...] = total
        for shift in range(1, size):
            copy(shift).wait_send()


def sum_vectors(rows, shared, mesh_sizes, collective_id):
    names = ("tensor", "context", "dp")
    sizes = tuple(mesh_sizes[name] for name in names)
    shape = rows.shape
    return pl.pallas_call(
        functools.partial(vectors_kernel, names, sizes, shared),
        out_shape=jax.ShapeDtypeStruct(shape, jnp.float32),
        in_specs=[VM],
        out_specs=VM,
        scratch_shapes=[pltpu.VMEM((len(names),) + shape, jnp.float32)]
        + [pltpu.VMEM((size,) + shape, jnp.float32) for size in sizes]
        + [DMA((size,)) for size in sizes for _ in range(2)],
        compiler_params=remote_params(collective_id),
    )(rows[None])


class PlaneSum:
    def __init__(self, u, p, o, bufs=None, spread=None):
        self.u, self.p, self.o = u, p, o
        if bufs is not None:
            self.rc, self.s1, self.ra, self.rb, self.sa, self.sb, self.ta, self.tb = bufs[:8]
            self.send1, self.recv1 = bufs[8:]
        if spread is not None:
            self.send2, self.recv2, self.loc = spread
        ctx, self.x = lax.axis_index("context"), lax.axis_index("dp")
        self.core, self.y = lax.rem(ctx, 2), lax.div(ctx, 2)
        self.chip_peer = {"context": ctx + 1 - 2 * self.core}
        self.y_peer = {"context": lax.rem(ctx + 2, 4)}
        self.x_peer = {"dp": 1 - self.x}

    @staticmethod
    def reduce_scratch(shape, dtype):
        tail = tuple(shape[1:])
        bufs = [pltpu.VMEM((count,) + tail, dtype) for count in (8, 8, 2, 2, 2, 2, 1, 1)]
        return bufs + [DMA((5,)), DMA((5,))]

    @staticmethod
    def spread_scratch():
        return [DMA((5,)), DMA((5,)), DMA((2,))]

    @staticmethod
    def greet(bar):
        ctx, x = lax.axis_index("context"), lax.axis_index("dp")
        for peer in (
            {"context": ctx + 1 - 2 * lax.rem(ctx, 2)},
            {"context": lax.rem(ctx + 2, 4)},
            {"dp": 1 - x},
        ):
            pl.semaphore_signal(bar, inc=1, device_id=peer, device_id_type=MESH)
        return 3

    def copy(self, at, src, dst, peer):
        send, recv = (self.send1, self.recv1) if at < 5 else (self.send2, self.recv2)
        return pltpu.make_async_remote_copy(
            src_ref=src,
            dst_ref=dst,
            send_sem=send.at[at % 5],
            recv_sem=recv.at[at % 5],
            device_id=peer,
            device_id_type=MESH,
        )

    def got(self, at, ref):
        recv = self.recv1 if at < 5 else self.recv2
        pltpu.make_async_copy(ref, ref, recv.at[at % 5]).wait()

    def add(self, out, left, right):
        f32 = jnp.float32
        out[...] = (left[...].astype(f32) + right[...].astype(f32)).astype(out.dtype)

    def mine(self, half):
        if half == 0:
            return pl.ds(self.core * 8 + 2 * self.x + self.y, 1)
        return pl.ds(self.core * 8 + 4 + 2 * self.y + self.x, 1)

    def hop(self, at):
        x, y, core = self.x, self.y, self.core
        o, p = self.o, self.p
        pair_a, pair_b = pl.ds(core * 8 + 2 * x, 2), pl.ds(core * 8 + 4 + 2 * y, 2)
        one = lambda at: pl.ds(at, 1)
        return [
            lambda: self.copy(0, self.by_core(1 - core), self.rc, self.chip_peer),
            lambda: self.copy(1, self.quarter(0, 1 - x), self.ra, self.x_peer),
            lambda: self.copy(2, self.quarter(1, 1 - y), self.rb, self.y_peer),
            lambda: self.copy(3, self.eighth(0, 1 - y), self.ta, self.y_peer),
            lambda: self.copy(4, self.eighth(1, 1 - x), self.tb, self.x_peer),
            lambda: self.copy(5, p.at[one(0)], o.at[self.mine(0)], self.y_peer),
            lambda: self.copy(6, p.at[one(1)], o.at[self.mine(1)], self.x_peer),
            lambda: self.copy(7, o.at[pair_a], o.at[pair_a], self.x_peer),
            lambda: self.copy(8, o.at[pair_b], o.at[pair_b], self.y_peer),
            lambda: self.copy(9, o.at[pl.ds(core * 8, 8)], o.at[pl.ds(core * 8, 8)], self.chip_peer),
        ][at]()

    def begin(self):
        self.hop(0).start()

    def by_core(self, core):
        return self.u.at[pl.ds(core * 8, 8)]

    def quarter(self, half, at):
        return self.s1.at[pl.ds(4 * half + 2 * at, 2)]

    def eighth(self, half, at):
        return (self.sa, self.sb)[half].at[pl.ds(at, 1)]

    def result(self, half):
        return self.p.at[pl.ds(half, 1)]

    def first(self):
        self.got(0, self.rc)
        self.add(self.s1, self.by_core(self.core), self.rc)
        self.hop(1).start()
        self.hop(2).start()

    def second(self):
        self.got(1, self.ra)
        self.add(self.sa, self.quarter(0, self.x), self.ra)
        self.hop(3).start()
        self.got(2, self.rb)
        self.add(self.sb, self.quarter(1, self.y), self.rb)
        self.hop(4).start()

    def third(self):
        self.got(3, self.ta)
        self.add(self.result(0), self.eighth(0, self.y), self.ta)
        self.got(4, self.tb)
        self.add(self.result(1), self.eighth(1, self.x), self.tb)

    def reduced(self):
        for at in range(5):
            self.hop(at).wait_send()

    def kept(self, half):
        return pltpu.make_async_copy(self.p.at[pl.ds(half, 1)], self.o.at[self.mine(half)], self.loc.at[half])

    def spread1(self):
        self.hop(5).start()
        self.hop(6).start()
        self.kept(0).start()
        self.kept(1).start()

    def spread2(self):
        x, y, core = self.x, self.y, self.core
        self.kept(0).wait()
        self.got(5, self.o.at[pl.ds(core * 8 + 2 * x + 1 - y, 1)])
        self.hop(7).start()
        self.kept(1).wait()
        self.got(6, self.o.at[pl.ds(core * 8 + 4 + 2 * y + 1 - x, 1)])
        self.hop(8).start()

    def spread3(self):
        x, y, core = self.x, self.y, self.core
        self.got(7, self.o.at[pl.ds(core * 8 + 2 - 2 * x, 2)])
        self.got(8, self.o.at[pl.ds(core * 8 + 6 - 2 * y, 2)])
        self.hop(9).start()

    def everywhere(self):
        self.got(9, self.o.at[pl.ds(8 - self.core * 8, 8)])
        for at in range(5, 10):
            self.hop(at).wait_send()


class StripSum(PlaneSum):
    @staticmethod
    def reduce_scratch(shape, dtype):
        lead, rows, cols = shape
        rest = lead - 2
        shapes = [(lead, rows)] * 2
        shapes += [(count, rows // 2) for count in (2, rest, 2, rest)] + [(count, rows // 4) for count in (2, rest)]
        return [pltpu.VMEM(item + (cols // 2,), dtype) for item in shapes] + [DMA((5,)), DMA((5,))]

    def lead(self, half):
        whole = (self.u if self.u is not None else self.o).shape[0]
        return pl.ds(0, 2) if half == 0 else pl.ds(2, whole - 2)

    def strip(self, core):
        size = (self.u if self.u is not None else self.o).shape[2] // 2
        return pl.ds(pl.multiple_of(core * size, 128), size)

    def rows(self, at, parts):
        size = (self.u if self.u is not None else self.o).shape[1] // parts
        return pl.ds(pl.multiple_of(at * size, 16), size)

    def by_core(self, core):
        return self.u.at[:, :, self.strip(core)]

    def quarter(self, half, at):
        return self.s1.at[self.lead(half), self.rows(at, 2)]

    def eighth(self, half, at):
        return (self.sa, self.sb)[half].at[:, self.rows(at, 4)]

    def result(self, half):
        return self.p.at[half, pl.ds(0, 2 if half == 0 else self.u.shape[0] - 2)]

    def hop(self, at):
        if at < 5:
            return super().hop(at)
        o, x, y = self.o, self.x, self.y
        mine = lambda half: o.at[
            self.lead(half), self.rows(2 * x + y if half == 0 else 2 * y + x, 4), self.strip(self.core)
        ]
        pair = lambda half: o.at[self.lead(half), self.rows(x if half == 0 else y, 2), self.strip(self.core)]
        both = o.at[:, :, self.strip(self.core)]
        return [
            lambda: self.copy(5, self.result(0), mine(0), self.y_peer),
            lambda: self.copy(6, self.result(1), mine(1), self.x_peer),
            lambda: self.copy(7, pair(0), pair(0), self.x_peer),
            lambda: self.copy(8, pair(1), pair(1), self.y_peer),
            lambda: self.copy(9, both, both, self.chip_peer),
        ][at - 5]()

    def kept(self, half):
        x, y = self.x, self.y
        mine = self.o.at[
            self.lead(half), self.rows(2 * x + y if half == 0 else 2 * y + x, 4), self.strip(self.core)
        ]
        return pltpu.make_async_copy(self.result(half), mine, self.loc.at[half])

    def spread2(self):
        x, y, mine = self.x, self.y, self.strip(self.core)
        self.kept(0).wait()
        self.got(5, self.o.at[self.lead(0), self.rows(2 * x + 1 - y, 4), mine])
        self.hop(7).start()
        self.kept(1).wait()
        self.got(6, self.o.at[self.lead(1), self.rows(2 * y + 1 - x, 4), mine])
        self.hop(8).start()

    def spread3(self):
        mine = self.strip(self.core)
        self.got(7, self.o.at[self.lead(0), self.rows(1 - self.x, 2), mine])
        self.got(8, self.o.at[self.lead(1), self.rows(1 - self.y, 2), mine])
        self.hop(9).start()

    def everywhere(self):
        self.got(9, self.o.at[:, :, self.strip(1 - self.core)])
        for at in range(5, 10):
            self.hop(at).wait_send()


def unit_pieces(unit):
    return jax.ShapeDtypeStruct((2,) + unit.shape[1:], unit.dtype)


def line_greet(bar, me, n):
    @pl.when(me > 0)
    def _():
        pl.semaphore_signal(bar, inc=1, device_id={"tensor": me - 1}, device_id_type=MESH)

    @pl.when(me < n - 1)
    def _():
        pl.semaphore_signal(bar, inc=1, device_id={"tensor": me + 1}, device_id_type=MESH)

    return jnp.where(me > 0, 1, 0) + jnp.where(me < n - 1, 1, 0)


class LineScatter:
    def __init__(self, n, x, o, buf, tmp, send, recv):
        self.n, self.x, self.o, self.buf, self.tmp, self.send, self.recv = n, x, o, buf, tmp, send, recv
        self.me = lax.axis_index("tensor")

    @staticmethod
    def scratch(n, own, cols, dtype):
        return [
            pltpu.VMEM((2, n - 1, own, cols), dtype),
            pltpu.VMEM((2, n - 1, own, cols), dtype),
            DMA((2, n - 1)),
            DMA((2, n - 1)),
        ]

    def term(self, d, k):
        return self.n - 1 - k if d == 0 else k

    def sends(self, d, k):
        return self.me < self.n - 1 - k if d == 0 else self.me > k

    def behind(self, d):
        return self.me > 0 if d == 0 else self.me < self.n - 1

    def copy(self, d, k, first):
        return pltpu.make_async_remote_copy(
            src_ref=self.x.at[self.term(d, k)] if first else self.tmp.at[d, k],
            dst_ref=self.buf.at[d, k],
            send_sem=self.send.at[d, k],
            recv_sem=self.recv.at[d, k],
            device_id={"tensor": jnp.clip(self.me + 1 if d == 0 else self.me - 1, 0, self.n - 1)},
            device_id_type=MESH,
        )

    def landed(self, d, k):
        return pltpu.make_async_copy(self.buf.at[d, k], self.buf.at[d, k], self.recv.at[d, k])

    def begin(self, ks):
        for d in range(2):

            @pl.when(jnp.logical_not(self.behind(d)))
            def _():
                for k in ks:
                    self.copy(d, k, True).start()

    def step(self, k, which=None):
        for d in range(2):
            now = self.behind(d) & self.sends(d, k)

            @pl.when(now if which is None else now & which(d))
            def _():
                self.landed(d, k).wait()
                at = self.term(d, k)
                both = self.buf[d, k].astype(jnp.float32) + self.x[at].astype(jnp.float32)
                self.tmp[d, k] = both.astype(self.tmp.dtype)
                self.copy(d, k, False).start()

    def end(self):
        self.o[...] = self.x[self.me].astype(jnp.float32)
        for d in range(2):
            for k in range(self.n - 1):

                @pl.when(self.behind(d) & (self.me == self.term(d, k)))
                def _():
                    self.landed(d, k).wait()
                    self.o[...] += self.buf[d, k].astype(jnp.float32)

        for d in range(2):
            for k in range(self.n - 1):

                @pl.when(self.sends(d, k))
                def _():
                    self.copy(d, k, False).wait_send()


GELU_SCALE = 0.7978845608028654
GELU_CUBE = 0.044715


def feed_kernel(n, nc, heads, chunks, piece_ref, *rest):
    (token_ref, out_ref, abias_ref, gain_ref, shift_ref, up_hbm, down_hbm, bias_ref, near_ref, cot_ref), rest = rest[:10], rest[10:]
    (feed_ref, p1_ref, p2_ref, middle_ref, gm_ref, vec_ref, heads_ref, p3_ref), rest = rest[:8], rest[8:]
    (o_ref, sum_ref, att_ref, gpiece, u3, bsend, brecv, bloc), rest = rest[:8], rest[8:]
    (x_ref, up_ref, down_ref, grad_ref, wsem, asend, arecv, aloc, csend, crecv, cloc), rest = rest[:11], rest[11:]
    (held, act, gp, part, acc, buf, tmp, u1, u2), rest = rest[:9], rest[9:]
    (gsend, grecv, loc, ssend, srecv), rest = rest[:5], rest[5:]
    plane = [PlaneSum(u1, p1_ref, None, rest[:10]), PlaneSum(u2, p2_ref, None, rest[10:20])]
    out_sum = StripSum(u3, p3_ref, None, rest[20:30])
    me = lax.axis_index("tensor")
    rows, width = token_ref.shape
    wide = up_ref.shape[1]
    few = rows // chunks
    f32, low = jnp.float32, jnp.bfloat16
    ctx, dp = lax.axis_index("context"), lax.axis_index("dp")
    place, total = ctx * n + me, nc * n
    my_head = me * heads + jnp.minimum(ctx, heads - 1)
    bar = pltpu.get_barrier_semaphore()
    for shift in range(1, total):
        other = lax.rem(place + shift, total)
        pl.semaphore_signal(bar, inc=1, device_id=spread(other, AXES, (nc, n)), device_id_type=MESH)
    pl.semaphore_signal(bar, inc=1, device_id={"dp": 1 - dp}, device_id_type=MESH)
    weights_in = [
        pltpu.make_async_copy(src, dst, wsem.at[at])
        for at, (src, dst) in enumerate(((up_hbm, up_ref), (down_hbm, down_ref)))
    ]
    for item in weights_in:
        item.start()

    def grad_rows(block):
        return grad_ref.at[pl.ds(pl.multiple_of(block * rows, rows), rows)]

    def grad_on(d, s):
        block = jnp.clip(me - s if d == 0 else me + s, 0, n - 1)
        return pltpu.make_async_remote_copy(
            src_ref=near_ref.at[block] if s == 1 else grad_rows(block),
            dst_ref=grad_rows(block),
            send_sem=csend.at[d, s],
            recv_sem=crecv.at[d, s],
            device_id={"tensor": jnp.clip(me + 1 if d == 0 else me - 1, 0, n - 1)},
            device_id_type=MESH,
        )

    def grad_sends(d, s):
        return (me - s >= 0) & (me < n - 1) if d == 0 else (me + s < n) & (me > 0)

    def grad_near(d):
        block = jnp.clip(me - 1 if d == 0 else me + 1, 0, n - 1)
        return pltpu.make_async_copy(near_ref.at[block], grad_rows(block), cloc.at[d])

    def grad_own():
        return pltpu.make_async_copy(cot_ref, grad_rows(me), cloc.at[2])

    def beside(d):
        return me > 0 if d == 0 else me < n - 1

    grad_own().start()
    for d in range(2):

        @pl.when(beside(d))
        def _():
            grad_near(d).start()

    pl.semaphore_wait(bar, total)
    for d in range(2):

        @pl.when(grad_sends(d, 1))
        def _():
            grad_on(d, 1).start()

    def to_place(shift):
        other = lax.rem(place + shift, total)
        return pltpu.make_async_remote_copy(
            src_ref=piece_ref.at[other],
            dst_ref=att_ref.at[my_head],
            send_sem=asend.at[shift],
            recv_sem=arecv.at[shift],
            device_id=spread(other, AXES, (nc, n)),
            device_id_type=MESH,
        )

    @pl.when(ctx < heads)
    def _():
        for shift in range(1, total):
            to_place(shift).start()
        stay = pltpu.make_async_copy(piece_ref.at[place], att_ref.at[my_head], aloc)
        stay.start()
        stay.wait()

    for shift in range(1, total):
        source = lax.rem(place + total - shift, total)
        at_ctx, at_ten = lax.div(source, n), lax.rem(source, n)

        @pl.when(at_ctx < heads)
        def _():
            landed = att_ref.at[at_ten * heads + jnp.minimum(at_ctx, heads - 1)]
            pltpu.make_async_copy(landed, landed, arecv.at[shift]).wait()

    attended = att_ref[...].reshape(width, rows)
    middle = token_ref[...].astype(f32) + dot(attended, out_ref[...], ((0,), (0,))) + row(abias_ref)
    middle_ref[...] = middle
    x_ref[...] = (norm_parts(middle)[0] * row(gain_ref) + row(shift_ref)).astype(low)

    @pl.when(ctx < heads)
    def _():
        for shift in range(1, total):
            to_place(shift).wait_send()

    def rows_of(block):
        return pl.ds(pl.multiple_of(block * rows, rows), rows)

    def neighbour(d):
        return {"tensor": jnp.clip(jnp.where(d == 0, me + 1, me - 1), 0, n - 1)}

    def onward(d):
        return jnp.where(d == 0, me, n - 1 - me) < n - 1

    def hand_on(d, s, block, first):
        return pltpu.make_async_remote_copy(
            src_ref=x_ref if first else held.at[rows_of(block)],
            dst_ref=held.at[rows_of(block)],
            send_sem=gsend.at[d, s],
            recv_sem=grecv.at[d, s],
            device_id=neighbour(d),
            device_id_type=MESH,
        )

    def chunk(block, c):
        return pl.ds(pl.multiple_of(block * rows + c * few, few), few)

    def back(d, block, c, first):
        at = chunk(block, c)
        return pltpu.make_async_remote_copy(
            src_ref=part.at[at] if first else tmp.at[at],
            dst_ref=buf.at[d, at],
            send_sem=ssend.at[block, c],
            recv_sem=srecv.at[d, block, c],
            device_id=neighbour(d),
            device_id_type=MESH,
        )

    for d in range(2):

        @pl.when(onward(d))
        def _():
            hand_on(d, 0, me, True).start()

    own = pltpu.make_async_copy(x_ref, held.at[rows_of(me)], loc)
    own.start()
    sum_ref[...] = jnp.zeros_like(sum_ref)
    own.wait()
    for item in weights_in:
        item.wait()
    grad_own().wait()
    for d in range(2):

        @pl.when(beside(d))
        def _():
            grad_near(d).wait()

    for s in range(1, n - 1):
        for d in range(2):
            block = me - 1 - s if d == 0 else me + 1 + s

            @pl.when((block >= 0) & (block < n))
            def _():
                landed = grad_rows(jnp.clip(block, 0, n - 1))
                pltpu.make_async_copy(landed, landed, crecv.at[d, s]).wait()

            if s + 1 < n - 1:

                @pl.when(grad_sends(d, s + 1))
                def _():
                    grad_on(d, s + 1).start()

        if s == n - 3:
            break
    columns = 256

    def work(block):
        here = rows_of(block)
        acc[...] = jnp.zeros_like(acc)

        @pl.loop(0, wide // columns)
        def _(j):
            at = pl.ds(pl.multiple_of(j * columns, columns), columns)
            pre = dot(held[here, :], up_ref[:, at], ((1,), (0,))) + bias_ref[at].reshape(1, -1)
            square = pre * pre
            tanh = jnp.tanh(GELU_SCALE * pre * (1.0 + GELU_CUBE * square))
            act[here, at] = (0.5 * pre * (1.0 + tanh)).astype(low)
            slope = 0.5 * (1.0 + tanh) + 0.5 * pre * (1.0 - tanh * tanh) * (
                GELU_SCALE * (1.0 + 3.0 * GELU_CUBE * square)
            )
            grad = (dot(grad_ref[here, :], down_ref[at, :], ((1,), (1,))) * slope).astype(low)
            gp[here, at] = grad
            acc[...] += dot(grad, up_ref[:, at], ((1,), (1,)))

        part[here, :] = acc[...].astype(low)
        sum_ref[...] += jnp.sum(gp[here, :].astype(f32), axis=0, keepdims=True)

    near = jnp.minimum(me, n - 1 - me)
    toward = jnp.where(2 * me < n - 1, -1, 1)

    @pl.loop(0, n)
    def _(slot):
        paired = slot <= 2 * near
        distance = jnp.where(paired, lax.div(slot + 1, 2), slot - near)
        side = jnp.where(paired & (lax.rem(slot, 2) == 1), toward, -toward)
        block = me + side * distance
        d = jnp.where(block < me, 0, 1)
        s = jnp.maximum(distance - 1, 0)

        @pl.when(slot > 0)
        def _():
            landed = held.at[rows_of(block)]
            pltpu.make_async_copy(landed, landed, grecv.at[d, s]).wait()

            @pl.when(onward(d))
            def _():
                hand_on(d, jnp.minimum(s + 1, n - 2), block, False).start()

        @pl.when(distance == n - 1)
        def _():
            landed = grad_rows(block)
            pltpu.make_async_copy(landed, landed, crecv.at[d, n - 2]).wait()

        work(block)

        @pl.when((slot > 0) & ((me == 0) | (me == n - 1)))
        def _():
            for c in range(chunks):
                back(1 - d, block, c, True).start()

    def weights(left, right, unit):
        half = wide // 2

        @pl.loop(0, 2)
        def _(j):
            at = pl.ds(pl.multiple_of(j * half, 128), half)
            total = dot(left[:, at], right[...], ((0,), (0,)))
            unit[pl.ds(8 * j, 8)] = total.astype(low).reshape((8,) + unit.shape[1:])

    weights(act, grad_ref, u1)
    plane[0].begin()
    weights(held, gp, u2)
    plane[1].begin()

    def relay(way, block):
        d = jnp.where(way > 0, 0, 1)

        @pl.when((me > 0) & (me < n - 1) & (block >= 0) & (block < n))
        def _():
            for c in range(chunks):
                at = chunk(block, c)
                landed = buf.at[d, at]
                pltpu.make_async_copy(landed, landed, srecv.at[d, block, c]).wait()
                tmp[at, :] = (buf[d, at, :].astype(f32) + part[at, :].astype(f32)).astype(low)
                back(d, block, c, False).start()

    plane[0].first()
    for j in range(1, n):
        relay(-toward, me - toward * j)
        if j == 1:
            plane[1].first()

    @pl.loop(0, n)
    def _(block):
        here = rows_of(block)
        feed_ref[here, :] = dot(act[here, :], down_ref[...], ((1,), (0,))).astype(low)

    plane[0].second()
    plane[1].second()
    for j in range(1, n):
        relay(toward, me + toward * j)
    for item in plane:
        item.third()
    for c in range(chunks):
        at = chunk(me, c)
        mine = pl.ds(c * few, few)
        o_ref[mine, :] = part[at, :].astype(f32)
        for d in range(2):

            @pl.when(me > 0 if d == 0 else me < n - 1)
            def _():
                landed = buf.at[d, at]
                pltpu.make_async_copy(landed, landed, srecv.at[d, me, c]).wait()
                o_ref[mine, :] += buf[d, at, :].astype(f32)

    grad = o_ref[...]
    normed, scale = norm_parts(middle_ref[...])
    above = grad_ref[rows_of(me), :].astype(f32)
    grad_middle = above + norm_backward(grad, normed, scale, row(gain_ref))
    gm_ref[...] = grad_middle
    gm_low = grad_middle.astype(low)
    back_out = dot(out_ref[...], gm_low, ((1,), (1,))).astype(low)
    gpiece[...] = back_out.reshape(gpiece.shape)
    vec_ref[...] = jnp.zeros_like(vec_ref)
    vec_ref[2:3, :] = jnp.sum(gm_low.astype(f32), axis=0, keepdims=True)

    def to_head(shift):
        other = lax.rem(place + shift, total)
        at_ctx, at_ten = lax.div(other, n), lax.rem(other, n)
        return at_ctx < heads, pltpu.make_async_remote_copy(
            src_ref=gpiece.at[at_ten * heads + jnp.minimum(at_ctx, heads - 1)],
            dst_ref=heads_ref.at[place],
            send_sem=bsend.at[shift],
            recv_sem=brecv.at[shift],
            device_id={"context": at_ctx, "tensor": at_ten},
            device_id_type=MESH,
        )

    for shift in range(1, total):
        goes, item = to_head(shift)

        @pl.when(goes)
        def _():
            item.start()

    stay = pltpu.make_async_copy(gpiece.at[my_head], heads_ref.at[place], bloc)
    stay.start()
    u3[...] = dot(att_ref[...].reshape(width, rows), gm_low, ((1,), (0,))).astype(low).reshape(u3.shape)
    out_sum.begin()
    vec_ref[3:4, :] = jnp.sum(grad * normed, axis=0, keepdims=True)
    vec_ref[4:5, :] = jnp.sum(grad, axis=0, keepdims=True)
    vec_ref[5:6, :] = jnp.sum(above, axis=0, keepdims=True)
    vec_ref[6:7, :] = sum_ref[...]
    out_sum.first()
    out_sum.second()
    out_sum.third()
    stay.wait()

    @pl.when(ctx < heads)
    def _():
        for shift in range(1, total):
            source = lax.rem(place + total - shift, total)
            landed = heads_ref.at[source]
            pltpu.make_async_copy(landed, landed, brecv.at[shift]).wait()

    for shift in range(1, total):
        goes, item = to_head(shift)

        @pl.when(goes)
        def _():
            item.wait_send()

    out_sum.reduced()
    for d in range(2):
        for s in range(n - 1):
            block = me - s if d == 0 else me + s

            @pl.when(onward(d) & (block >= 0) & (block < n))
            def _():
                hand_on(d, s, me, True).wait_send()

    for block in range(n):

        @pl.when(me != block)
        def _():
            for c in range(chunks):
                back(jnp.where(me < block, 0, 1), block, c, True).wait_send()

    for d in range(2):
        for s in range(1, n - 1):

            @pl.when(grad_sends(d, s))
            def _():
                grad_on(d, s).wait_send()

    for item in plane:
        item.reduced()


def feed_part(pieces, tokens, out_weight, vectors, up, down, bias, near, cotangent, n, nc, heads, collective_id):
    rows, width = tokens.shape
    wide = up.shape[1]
    chunks = 2
    total = n * rows
    low, f32 = jnp.bfloat16, jnp.float32
    unit = (16, wide // 16, width)
    piece = jax.ShapeDtypeStruct((2,) + unit[1:], low)
    return pl.pallas_call(
        functools.partial(feed_kernel, n, nc, heads, chunks),
        out_shape=(
            jax.ShapeDtypeStruct((total, width), low),
            piece,
            piece,
            jax.ShapeDtypeStruct((rows, width), f32),
            jax.ShapeDtypeStruct((rows, width), f32),
            jax.ShapeDtypeStruct((8, width), f32),
            jax.ShapeDtypeStruct(pieces.shape, low),
            jax.ShapeDtypeStruct((2, 2, rows // 4, width // 2), low),
        ),
        in_specs=[VM] * 6 + [ANY, ANY, VM, ANY, ANY],
        out_specs=(VM,) * 8,
        scratch_shapes=[
            pltpu.VMEM((rows, width), f32),
            pltpu.VMEM((1, wide), f32),
            pltpu.VMEM((n * heads,) + pieces.shape[1:], low),
            pltpu.VMEM((n * heads,) + pieces.shape[1:], low),
            pltpu.VMEM((n, width // n, width), low),
            DMA((nc * n,)),
            DMA((nc * n,)),
            DMA,
            pltpu.VMEM((rows, width), low),
            pltpu.VMEM(up.shape, low),
            pltpu.VMEM(down.shape, low),
            pltpu.VMEM((total, width), low),
            DMA((2,)),
            DMA((nc * n,)),
            DMA((nc * n,)),
            DMA,
            DMA((2, n - 1)),
            DMA((2, n - 1)),
            DMA((3,)),
            pltpu.VMEM((total, width), low),
            pltpu.VMEM((total, wide), low),
            pltpu.VMEM((total, wide), low),
            pltpu.VMEM((total, width), low),
            pltpu.VMEM((rows, width), f32),
            pltpu.VMEM((2, total, width), low),
            pltpu.VMEM((total, width), low),
            pltpu.VMEM(unit, low),
            pltpu.VMEM(unit, low),
            DMA((2, n - 1)),
            DMA((2, n - 1)),
            DMA,
            DMA((n, chunks)),
            DMA((2, n, chunks)),
        ]
        + PlaneSum.reduce_scratch(unit, low) * 2
        + StripSum.reduce_scratch((n, width // n, width), low),
        compiler_params=remote_params(collective_id, 40),
    )(pieces, tokens, out_weight, *vectors, up, down, bias, near, cotangent)


def last_kernel(n, nc, heads, shared, count, x_ref, w_hbm, h_hbm, a_hbm, *rest):
    ps, rest = rest[:count], rest[count:]
    (token_hbm, gain_ref, middle_hbm, vec_ref), rest = rest[:4], rest[4:]
    (g_ref, v_ref, po_ref, ao_ref), rest = rest[:4], rest[4:]
    outs, rest = rest[:count], rest[count:]
    (rows_ref, w_ref, h_ref, token_ref, middle_ref, part, sum_ref, u_ref, piece), rest = rest[:9], rest[9:]
    (hsend, hrecv, hloc, win), rest = rest[:4], rest[4:]
    chunks = 2
    own = token_ref.shape[0]
    few = own // chunks
    lines = [
        LineScatter(n, part.at[:, pl.ds(c * few, few)], sum_ref.at[pl.ds(c * few, few)], *rest[4 * c : 4 * c + 4])
        for c in range(chunks)
    ]
    rest = rest[4 * chunks :]
    project = StripSum(u_ref, piece, po_ref, rest[:10], rest[10:13])
    rest = rest[13:]
    feeds = [PlaneSum(None, ps[i], outs[i], None, rest[3 * i : 3 * i + 3]) for i in range(count)]
    rest = rest[3 * count :]
    (land, zsend, zrecv, zloc, a_ref), rest = rest[:5], rest[5:]
    (asend, arecv, aloc, now), rest = rest[:4], rest[4:]
    names, sizes = ("tensor", "context", "dp"), (n, nc, 2)
    bufs, sems = rest[:3], rest[3:]
    f32, low = jnp.float32, jnp.bfloat16

    ten, ctx, x = (lax.axis_index(name) for name in names)
    place = ctx * 2 + x
    bar = pltpu.get_barrier_semaphore()
    for shift in range(1, n):
        pl.semaphore_signal(bar, inc=1, device_id={"tensor": lax.rem(ten + shift, n)}, device_id_type=MESH)
    for shift in range(1, 8):
        other = lax.rem(place + shift, 8)
        pl.semaphore_signal(
            bar, inc=1, device_id={"context": lax.div(other, 2), "dp": lax.rem(other, 2)}, device_id_type=MESH
        )
    copies_in = [
        pltpu.make_async_copy(src, dst, win.at[at])
        for at, (src, dst) in enumerate(
            ((token_hbm, token_ref), (middle_hbm, middle_ref), (w_hbm, w_ref), (h_hbm, h_ref))
        )
    ]
    for item in copies_in:
        item.start()
    pl.semaphore_wait(bar, n + 6)

    half = 2 * own
    far = 1 - lax.div(ten, 2)
    pairs = (far, 1 - far)

    def columns(pair):
        return pl.ds(pl.multiple_of(pair * half, 128), half)

    def ship(index, shift):
        other = lax.rem(ctx + shift, nc)
        return pltpu.make_async_remote_copy(
            src_ref=x_ref.at[other, :, :, columns(pairs[index])],
            dst_ref=rows_ref.at[:, jnp.minimum(ctx, heads - 1), :, columns(pairs[index])],
            send_sem=hsend.at[index, shift],
            recv_sem=hrecv.at[index, shift],
            device_id={"context": other},
            device_id_type=MESH,
        )

    @pl.when(ctx < heads)
    def _():
        for index in range(2):
            for shift in range(1, nc):
                ship(index, shift).start()
        stay = pltpu.make_async_copy(x_ref.at[ctx], rows_ref.at[:, ctx], hloc)
        stay.start()
        stay.wait()

    def across(shift):
        other = lax.rem(ten + shift, n)
        return pltpu.make_async_remote_copy(
            src_ref=a_hbm.at[lax.div(other, 2), lax.rem(other, 2)],
            dst_ref=land.at[ten],
            send_sem=zsend.at[shift],
            recv_sem=zrecv.at[shift],
            device_id={"tensor": other},
            device_id_type=MESH,
        )

    for shift in range(1, n):
        across(shift).start()
    mine = pltpu.make_async_copy(a_hbm.at[lax.div(ten, 2), lax.rem(ten, 2)], land.at[ten], zloc)
    mine.start()
    for item in feeds:
        item.spread1()

    def there(at):
        ctx_, x_ = lax.div(at, 2), lax.rem(at, 2)
        y_ = lax.div(ctx_, 2)
        row_ = jnp.where(ten < n // 2, 2 * x_ + y_, 2 * y_ + x_)
        rows = pl.ds(pl.multiple_of(row_ * a_ref.shape[0], 16), a_ref.shape[0])
        cols = pl.ds(pl.multiple_of(lax.rem(ctx_, 2) * a_ref.shape[1], 128), a_ref.shape[1])
        return ao_ref.at[rows, cols]

    def push(shift):
        other = lax.rem(place + shift, 8)
        return pltpu.make_async_remote_copy(
            src_ref=a_ref,
            dst_ref=there(place),
            send_sem=asend.at[shift],
            recv_sem=arecv.at[shift],
            device_id={"context": lax.div(other, 2), "dp": lax.rem(other, 2)},
            device_id_type=MESH,
        )

    for item in copies_in[:2]:
        item.wait()
    normed, scale = norm_parts(token_ref[...].astype(f32))
    mine.wait()
    for shift in range(1, n):
        source = lax.rem(ten + n - shift, n)
        pltpu.make_async_copy(land.at[source], land.at[source], zrecv.at[shift]).wait()
    value = land[0].astype(f32)
    for at in range(1, n):
        value = value + land[at].astype(f32)
    a_ref[...] = value.astype(low)
    for item in copies_in[2:]:
        item.wait()
    for shift in range(1, 8):
        push(shift).start()
    kept = pltpu.make_async_copy(a_ref, there(place), aloc)
    kept.start()

    def partials(index):
        at = columns(pairs[index])
        for shift in range(1, nc):
            source = lax.rem(ctx + nc - shift, nc)

            @pl.when(source < heads)
            def _():
                ref = rows_ref.at[:, jnp.minimum(source, heads - 1), :, at]
                pltpu.make_async_copy(ref, ref, hrecv.at[index, shift]).wait()

        total = 0.0
        for kind in range(3):
            grads = rows_ref[kind, :, :, at].reshape(heads * HEAD_DIM, half)
            total = total + dot(grads, w_ref[kind], ((0,), (0,)))
        part[pl.ds(2 * pairs[index], 2)] = total.astype(low).reshape(2, own, total.shape[1])

    first = lambda d: (ten < n // 2) if d == 0 else (ten >= n // 2)
    second = lambda d: (ten >= n // 2) if d == 0 else (ten < n // 2)
    partials(0)
    for line in lines:
        line.begin((0, 1))
    partials(1)
    for line in lines:
        line.begin((2,))
    for item in feeds:
        item.spread2()
    for line in lines:
        line.step(0, first)
    for kind in range(3):
        grads = rows_ref[kind].reshape(heads * HEAD_DIM, n * own)
        u_ref[kind] = dot(grads, h_ref[...], ((1,), (0,))).astype(low)
    project.begin()
    for line in lines:
        line.step(1, first)
    now[0] = vec_ref[...]
    ends = jnp.concatenate(
        [rows_ref[kind].reshape(heads * HEAD_DIM, n * own) for kind in (0, 2)], axis=0
    )
    bias = dot(jnp.ones((8, n * own), low), ends, ((1,), (1,)))
    now[0, 7:8, 0 : bias.shape[1]] = bias[0:1]
    project.first()
    for item in feeds:
        item.spread3()
    project.second()
    for k in range(n - 1):
        for line in lines:
            line.step(k, second)
    project.third()
    project.spread1()
    for line in lines:
        line.end()
    grad = sum_ref[...]
    now[0, 0:1] = jnp.sum(grad * normed, axis=0, keepdims=True)
    now[0, 1:2] = jnp.sum(grad, axis=0, keepdims=True)
    alone = now[0]

    def stage_copy(stage, shift):
        name, size = names[stage], sizes[stage]
        me = lax.axis_index(name)
        return pltpu.make_async_remote_copy(
            src_ref=now.at[stage],
            dst_ref=bufs[stage].at[me],
            send_sem=sems[2 * stage].at[shift],
            recv_sem=sems[2 * stage + 1].at[shift],
            device_id={name: lax.rem(me + shift, size)},
            device_id_type=MESH,
        )

    def stage_start(stage):
        for shift in range(1, sizes[stage]):
            stage_copy(stage, shift).start()
        bufs[stage][lax.axis_index(names[stage])] = now[stage]

    def stage_end(stage):
        buf, size = bufs[stage], sizes[stage]
        me = lax.axis_index(names[stage])
        for shift in range(1, size):
            source = lax.rem(me + size - shift, size)
            pltpu.make_async_copy(buf.at[source], buf.at[source], sems[2 * stage + 1].at[shift]).wait()
        total = buf[0]
        for at in range(1, size):
            total = total + buf[at]
        if stage == 0:
            line_ = lax.broadcasted_iota(jnp.int32, total.shape, 0)
            total = jnp.where(line_ < shared, total, alone)
        if stage < 2:
            now[stage + 1] = total
        else:
            v_ref[...] = total

    stage_start(0)
    back = norm_backward(grad, normed, scale, row(gain_ref))
    g_ref[...] = (middle_ref[...] + back).astype(g_ref.dtype)
    project.spread2()
    stage_end(0)
    stage_start(1)
    project.spread3()
    stage_end(1)
    stage_start(2)
    kept.wait()
    for shift in range(1, 8):
        source = there(lax.rem(place + 8 - shift, 8))
        pltpu.make_async_copy(source, source, arecv.at[shift]).wait()
    for item in feeds:
        item.everywhere()
    stage_end(2)
    project.everywhere()
    project.reduced()

    @pl.when(ctx < heads)
    def _():
        for index in range(2):
            for shift in range(1, nc):
                ship(index, shift).wait_send()

    for shift in range(1, n):
        across(shift).wait_send()
    for shift in range(1, 8):
        push(shift).wait_send()
    for stage in range(3):
        for shift in range(1, sizes[stage]):
            stage_copy(stage, shift).wait_send()


def last_part(x, weight, hidden, attend_pieces, pieces, tokens, gain, grad_middle, vectors, shared, n, heads, collective_id):
    nc = x.shape[0]
    own, cols = tokens.shape
    count = len(pieces)
    f32, low = jnp.float32, jnp.bfloat16
    whole = lambda item: jax.ShapeDtypeStruct((16,) + item.shape[1:], item.dtype)
    wide, deep = attend_pieces.shape[2:]
    unit = (3, heads * HEAD_DIM, cols)
    result = pl.pallas_call(
        functools.partial(last_kernel, n, nc, heads, shared, count),
        out_shape=(
            jax.ShapeDtypeStruct((own, cols), low),
            jax.ShapeDtypeStruct(vectors.shape, f32),
            jax.ShapeDtypeStruct(unit, low),
            jax.ShapeDtypeStruct((4 * wide, 2 * deep), low),
        )
        + tuple(whole(item) for item in pieces),
        in_specs=[VM, ANY, ANY, ANY] + [ANY] * count + [ANY, VM, ANY, VM],
        out_specs=(VM,) * (4 + count),
        scratch_shapes=[
            pltpu.VMEM((3, heads, HEAD_DIM, n * own), low),
            pltpu.VMEM(weight.shape, low),
            pltpu.VMEM(hidden.shape, low),
            pltpu.VMEM(tokens.shape, low),
            pltpu.VMEM((own, cols), f32),
            pltpu.VMEM((n, own, cols), low),
            pltpu.VMEM((own, cols), f32),
            pltpu.VMEM(unit, low),
            pltpu.VMEM((2, 2, unit[1] // 4, cols // 2), low),
            DMA((2, nc)),
            DMA((2, nc)),
            DMA,
            DMA((4,)),
        ]
        + LineScatter.scratch(n, own // 2, cols, low) * 2
        + StripSum.reduce_scratch(unit, low)
        + PlaneSum.spread_scratch()
        + [item for _ in pieces for item in PlaneSum.spread_scratch()]
        + [pltpu.VMEM((n, wide, deep), low), DMA((n,)), DMA((n,)), DMA, pltpu.VMEM((wide, deep), low)]
        + [DMA((8,)), DMA((8,)), DMA, pltpu.VMEM((3,) + vectors.shape, f32)]
        + [pltpu.VMEM((size,) + vectors.shape, f32) for size in (n, nc, 2)]
        + [DMA((size,)) for size in (n, nc, 2) for _ in range(2)],
        compiler_params=remote_params(collective_id, 32),
    )(x, weight, hidden, attend_pieces, *pieces, tokens, gain, grad_middle, vectors)
    return result[0], result[1], result[2], result[3], result[4:]


class LineGather:
    def __init__(self, n, x, o, send, recv):
        self.n, self.x, self.o, self.send, self.recv = n, x, o, send, recv
        self.me = lax.axis_index("tensor")

    def copy(self, d, s):
        me, n = self.me, self.n
        shard = jnp.clip(me - s if d == 0 else me + s, 0, n - 1)
        return pltpu.make_async_remote_copy(
            src_ref=self.x if s == 0 else self.o.at[shard],
            dst_ref=self.o.at[shard],
            send_sem=self.send.at[d, s],
            recv_sem=self.recv.at[d, s],
            device_id={"tensor": jnp.clip(me + 1 if d == 0 else me - 1, 0, n - 1)},
            device_id_type=MESH,
        )

    def sends(self, d, s):
        me, n = self.me, self.n
        return (me - s >= 0) & (me < n - 1) if d == 0 else (me + s < n) & (me > 0)

    def wait(self, d, s):
        me, n = self.me, self.n

        @pl.when(me - 1 - s >= 0 if d == 0 else me + 1 + s < n)
        def _():
            shard = jnp.clip(me - 1 - s if d == 0 else me + 1 + s, 0, n - 1)
            pltpu.make_async_copy(self.o.at[shard], self.o.at[shard], self.recv.at[d, s]).wait()

    def step(self, s):
        for d in range(2):
            if s > 0:
                self.wait(d, s - 1)

            @pl.when(self.sends(d, s))
            def _():
                self.copy(d, s).start()

    def last(self):
        for d in range(2):
            self.wait(d, self.n - 2)

    def finish(self, steps=None):
        for d in range(2):
            for s in range(steps or self.n - 1):

                @pl.when(self.sends(d, s))
                def _():
                    self.copy(d, s).wait_send()


def start_kernel(n, nc, heads, t_ref, gain_ref, shift_ref, full_ref, w_hbm, b_ref, c_ref, o_ref, f_ref, q_ref, g_ref, *rest):
    (x_ref, held, proj, w_ref), rest = rest[:4], rest[4:]
    s1, r1, s2, r2, s5, r5, s3, r3, s4, r4, loc = rest
    me, ctx, x = lax.axis_index("tensor"), lax.axis_index("context"), lax.axis_index("dp")
    core, y = lax.rem(ctx, 2), lax.div(ctx, 2)
    rows, width = t_ref.shape
    half = 2 * rows
    bar = pltpu.get_barrier_semaphore()
    met = line_greet(bar, me, n)
    for shift in range(1, nc):
        pl.semaphore_signal(bar, inc=1, device_id={"context": lax.rem(ctx + shift, nc)}, device_id_type=MESH)
    pl.semaphore_signal(bar, inc=1, device_id={"dp": 1 - x}, device_id_type=MESH)
    weight_in = pltpu.make_async_copy(w_hbm, w_ref, loc.at[4])
    weight_in.start()
    normed, _ = norm_parts(t_ref[...].astype(jnp.float32))
    x_ref[...] = (normed * row(gain_ref) + row(shift_ref)).astype(x_ref.dtype)
    pl.semaphore_wait(bar, met + nc)

    tall, deep = held.shape[1:]
    strip = pl.ds(pl.multiple_of(core * deep, 128), deep)
    piece = full_ref.at[pl.ds(pl.multiple_of((2 * y + x) * tall, 16), tall), strip]
    small = LineGather(n, piece, held, s1, r1)
    large = LineGather(n, x_ref, o_ref, s2, r2)
    grads = LineGather(n, c_ref, g_ref, s5, r5)
    small.step(0)
    large.step(0)
    own = pltpu.make_async_copy(x_ref, o_ref.at[me], loc.at[0])
    own.start()
    mine = pltpu.make_async_copy(piece, held.at[me], loc.at[1])
    mine.start()
    mine.wait()
    own.wait()
    for s in range(1, n - 1):
        small.step(s)
    small.last()

    def there(y_, x_):
        return f_ref.at[:, pl.ds(pl.multiple_of((2 * y_ + x_) * tall, 16), tall), strip]

    x_peer, y_peer = {"dp": 1 - x}, {"context": lax.rem(ctx + 2, 4)}

    def hop(at):
        src, dst, peer = [
            (held, there(y, x), x_peer),
            (held, there(y, x), y_peer),
            (there(y, 1 - x), there(y, 1 - x), y_peer),
            (f_ref.at[:, :, strip], f_ref.at[:, :, strip], {"context": ctx + 1 - 2 * core}),
        ][at]
        return pltpu.make_async_remote_copy(
            src_ref=src,
            dst_ref=dst,
            send_sem=s3.at[at],
            recv_sem=r3.at[at],
            device_id=peer,
            device_id_type=MESH,
        )

    def got(at):
        other = pl.ds(pl.multiple_of((1 - core) * deep, 128), deep)
        ref = [there(y, 1 - x), there(1 - y, x), there(1 - y, 1 - x), f_ref.at[:, :, other]][at]
        pltpu.make_async_copy(ref, ref, r3.at[at]).wait()

    hop(0).start()
    kept = pltpu.make_async_copy(held, there(y, x), loc.at[2])
    kept.start()

    def columns(pair):
        return pl.ds(pl.multiple_of(pair * half, 128), half)

    def project(pair):
        token = jnp.concatenate([o_ref[2 * pair], o_ref[2 * pair + 1]], axis=0)
        for kind in range(3):
            value = dot(w_ref[kind], token, ((1,), (1,))) + b_ref[kind]
            proj[kind, :, :, columns(pair)] = value.astype(proj.dtype).reshape(heads, HEAD_DIM, half)

    def ship(index, pair, shift):
        other = lax.rem(ctx + shift, nc)
        return other, pltpu.make_async_remote_copy(
            src_ref=proj.at[:, jnp.minimum(other, heads - 1), :, columns(pair)],
            dst_ref=q_ref.at[ctx, :, :, columns(pair)],
            send_sem=s4.at[index, shift],
            recv_sem=r4.at[index, shift],
            device_id={"context": other},
            device_id_type=MESH,
        )

    def ship_all(index, pair):
        for shift in range(1, nc):
            other, item = ship(index, pair, shift)

            @pl.when(other < heads)
            def _():
                item.start()

    near = lax.div(me, 2)
    large.step(1)
    weight_in.wait()
    project(near)
    ship_all(0, near)
    hop(1).start()
    for s in range(2, n - 1):
        large.step(s)
    grads.step(0)
    got(0)
    hop(2).start()
    large.last()
    project(1 - near)
    ship_all(1, 1 - near)
    stay = pltpu.make_async_copy(proj.at[:, jnp.minimum(ctx, heads - 1)], q_ref.at[ctx], loc.at[3])
    stay.start()
    kept.wait()
    got(1)
    got(2)
    hop(3).start()
    stay.wait()

    @pl.when(ctx < heads)
    def _():
        for index in range(2):
            for shift in range(1, nc):
                source = lax.rem(ctx + nc - shift, nc)
                pair = near if index == 0 else 1 - near
                ref = q_ref.at[source, :, :, columns(pair)]
                pltpu.make_async_copy(ref, ref, r4.at[index, shift]).wait()

    got(3)
    for d in range(2):
        grads.wait(d, 0)
    small.finish()
    large.finish()
    grads.finish(1)
    for at in range(4):
        hop(at).wait_send()
    for index in range(2):
        for shift in range(1, nc):
            other, item = ship(index, near if index == 0 else 1 - near, shift)

            @pl.when(other < heads)
            def _():
                item.wait_send()


def start_part(tokens, gain, shift, w, project_weight, bias, cotangent, n, nc, heads, collective_id):
    rows, cols = tokens.shape
    wide, deep = w.shape
    low = jnp.bfloat16
    full, weight, qkv, grads = pl.pallas_call(
        functools.partial(start_kernel, n, nc, heads),
        out_shape=(
            jax.ShapeDtypeStruct((n, rows, cols), low),
            jax.ShapeDtypeStruct((n, wide, deep), w.dtype),
            jax.ShapeDtypeStruct((nc, 3, HEAD_DIM, n * rows), low),
            jax.ShapeDtypeStruct((n, rows, cols), low),
        ),
        in_specs=[VM, VM, VM, ANY, ANY, VM, ANY],
        out_specs=(VM,) * 4,
        scratch_shapes=[
            pltpu.VMEM((rows, cols), low),
            pltpu.VMEM((n, wide // 4, deep // 2), w.dtype),
            pltpu.VMEM((3, heads, HEAD_DIM, n * rows), low),
            pltpu.VMEM(project_weight.shape, low),
        ]
        + [DMA((2, n - 1)) for _ in range(6)]
        + [DMA((4,)), DMA((4,)), DMA((2, nc)), DMA((2, nc)), DMA((5,))],
        compiler_params=remote_params(collective_id),
    )(tokens, gain, shift, w, project_weight, bias, cotangent)
    return full.reshape(n * rows, cols), weight.reshape(n * wide, deep), qkv, grads


def dot(left, right, dims):
    return lax.dot_general(left, right, ((dims[0], dims[1]), ((), ())), preferred_element_type=jnp.float32)


def key_positions(first, keys, queries):
    return first + lax.broadcasted_iota(jnp.int32, (keys, queries), 0)


def load_rows(qkv_ref, nb, half, qs, kt, ks, vs):
    for block in range(nb):
        part = slice(block % 2 * half, block % 2 * half + half)
        at = block // 2
        qs[block] = qkv_ref[at, 0, :, part] * jnp.asarray(HEAD_DIM**-0.5, qs.dtype)
        item = qkv_ref[at, 1, :, part]
        if kt is not None:
            kt[block] = item
        ks[block] = item.T
        if vs is not None:
            vs[block] = qkv_ref[at, 2, :, part].T


def fill_tables(nb, half, seg_ref, order_ref, slot_ref, low_ref, high_ref):
    for block in range(nb):
        slot_ref[order_ref[block]] = jnp.int32(block)
    first = [seg_ref[0, block * half] for block in range(nb)]
    last = [seg_ref[0, block * half + half - 1] for block in range(nb)]
    for block in range(nb):
        if low_ref is not None:
            low_ref[block] = sum(jnp.where(item < first[block], 1, 0) for item in last)
        if high_ref is not None:
            high_ref[block] = sum(jnp.where(item <= last[block], 1, 0) for item in first)


def forward_kernel(half, heads, seg_s, order_ref, seg_ref, qkv_ref, o_ref, full_ref, lse_ref, start_ref, qs, ks, slot_ref, low_ref):
    nb = full_ref.shape[0]

    @pl.when(lax.axis_index("context") < heads)
    def _():
        load_rows(qkv_ref, nb, half, qs, None, ks, None)
        fill_tables(nb, half, seg_s, order_ref, slot_ref, low_ref, None)
        seg = seg_ref[...]
        start = jnp.zeros(seg.shape, jnp.float32)
        for doc in range(1, DOC_LIMIT):
            before = jnp.sum(jnp.where(seg < doc, 1.0, 0.0), axis=1, keepdims=True)
            start = jnp.where(seg == doc, before, start)
        start_ref[...] = start.astype(jnp.int32)

        @pl.loop(0, nb)
        def _(nq):
            slot = slot_ref[nq]
            query = qs[slot]
            begin = start_ref[:, pl.ds(pl.multiple_of(nq * half, 128), half)]
            here = nq * half + lax.broadcasted_iota(jnp.int32, (1, half), 1)

            def step(nk, state):
                top, total, acc = state
                at = slot_ref[nk]
                score = dot(ks[at], query, ((1,), (0,)))
                place = key_positions(nk * half, half, half)
                score = jnp.where((place >= begin) & (place <= here), score, NEG_FILL)
                new_top = jnp.maximum(top, jnp.max(score, axis=0, keepdims=True))
                factor = jnp.exp(top - new_top)
                weight = jnp.exp(score - new_top)
                total = total * factor + jnp.sum(weight, axis=0, keepdims=True)
                value = qkv_ref[at // 2, 2, :, pl.ds(pl.multiple_of(at % 2 * half, 128), half)]
                acc = acc * factor + dot(value, weight.astype(jnp.bfloat16), ((1,), (0,)))
                return new_top, total, acc

            top, total, acc = lax.fori_loop(
                low_ref[nq],
                nq + 1,
                step,
                (
                    jnp.full((1, half), NEG_FILL, jnp.float32),
                    jnp.zeros((1, half), jnp.float32),
                    jnp.zeros((HEAD_DIM, half), jnp.float32),
                ),
            )
            result = acc / total
            full_ref[slot] = result
            lse_ref[slot] = top + jnp.log(total)
            low = result.astype(jnp.bfloat16)
            o_ref[2 * slot] = low[:, : half // 2]
            o_ref[2 * slot + 1] = low[:, half // 2 :]


def attend_forward(qkv, segments, order, half, heads):
    nc = qkv.shape[0]
    nb = 2 * nc
    return pl.pallas_call(
        functools.partial(forward_kernel, half, heads),
        out_shape=(
            jax.ShapeDtypeStruct((2 * nb, HEAD_DIM, half // 2), jnp.bfloat16),
            jax.ShapeDtypeStruct((nb, HEAD_DIM, half), jnp.float32),
            jax.ShapeDtypeStruct((nb, 1, half), jnp.float32),
            jax.ShapeDtypeStruct(segments.shape, jnp.int32),
        ),
        in_specs=[SM, SM, VM, VM],
        out_specs=(VM, VM, VM, VM),
        scratch_shapes=[
            pltpu.VMEM((nb, HEAD_DIM, half), jnp.bfloat16),
            pltpu.VMEM((nb, half, HEAD_DIM), jnp.bfloat16),
            pltpu.SMEM((nb,), jnp.int32),
            pltpu.SMEM((nb,), jnp.int32),
        ],
        compiler_params=pltpu.CompilerParams(vmem_limit_bytes=24 << 20),
    )(segments, order, segments, qkv)


def backward_kernel(
    half, heads, seg_s, order_ref, start_ref, qkv_ref, full_ref, lse_ref, grad_ref, o_ref,
    qs, kt, ks, vs, gs, ds, dq, slot_ref, high_ref,
):
    nb = full_ref.shape[0]

    @pl.when(lax.axis_index("context") < heads)
    def _():
        load_rows(qkv_ref, nb, half, qs, kt, ks, vs)
        fill_tables(nb, half, seg_s, order_ref, slot_ref, None, high_ref)
        for block in range(nb):
            both = jnp.concatenate([grad_ref[2 * block], grad_ref[2 * block + 1]], axis=1)
            gs[block] = both
            ds[block] = jnp.sum(both.astype(jnp.float32) * full_ref[block], axis=0, keepdims=True)
            dq[block] = jnp.zeros((HEAD_DIM, half), jnp.float32)

        @pl.loop(0, nb)
        def _(nk):
            at = slot_ref[nk]
            place = key_positions(nk * half, half, half)

            def step(nq, state):
                grad_key, grad_value = state
                slot = slot_ref[nq]
                query, grad = qs[slot], gs[slot]
                begin = start_ref[:, pl.ds(pl.multiple_of(nq * half, 128), half)]
                here = nq * half + lax.broadcasted_iota(jnp.int32, (1, half), 1)
                score = dot(ks[at], query, ((1,), (0,)))
                score = jnp.where((place >= begin) & (place <= here), score, NEG_FILL)
                weight = jnp.exp(score - lse_ref[slot])
                grad_weight = dot(vs[at], grad, ((1,), (0,)))
                grad_score = (weight * (grad_weight - ds[slot])).astype(jnp.bfloat16)
                grad_value = grad_value + dot(grad, weight.astype(jnp.bfloat16), ((1,), (1,)))
                grad_key = grad_key + dot(query, grad_score, ((1,), (1,)))
                dq[slot] += dot(kt[at], grad_score, ((1,), (0,)))
                return grad_key, grad_value

            zero = jnp.zeros((HEAD_DIM, half), jnp.float32)
            grad_key, grad_value = lax.fori_loop(nk, high_ref[nk], step, (zero, zero))
            columns = pl.ds(pl.multiple_of(at % 2 * half, 128), half)
            o_ref[at // 2, 1, :, columns] = grad_key.astype(jnp.bfloat16)
            o_ref[at // 2, 2, :, columns] = grad_value.astype(jnp.bfloat16)

        for block in range(nb):
            part = slice(block % 2 * half, block % 2 * half + half)
            o_ref[block // 2, 0, :, part] = (dq[block] * HEAD_DIM**-0.5).astype(jnp.bfloat16)


def attend_backward(qkv, segments, order, start, full, lse, grad, half, heads):
    nc = qkv.shape[0]
    nb = 2 * nc
    low = jnp.bfloat16
    return pl.pallas_call(
        functools.partial(backward_kernel, half, heads),
        out_shape=jax.ShapeDtypeStruct(qkv.shape, low),
        in_specs=[SM, SM, VM, VM, VM, VM, VM],
        out_specs=VM,
        scratch_shapes=[
            pltpu.VMEM((nb, HEAD_DIM, half), low),
            pltpu.VMEM((nb, HEAD_DIM, half), low),
            pltpu.VMEM((nb, half, HEAD_DIM), low),
            pltpu.VMEM((nb, half, HEAD_DIM), low),
            pltpu.VMEM((nb, HEAD_DIM, half), low),
            pltpu.VMEM((nb, 1, half), jnp.float32),
            pltpu.VMEM((nb, HEAD_DIM, half), jnp.float32),
            pltpu.SMEM((nb,), jnp.int32),
            pltpu.SMEM((nb,), jnp.int32),
        ],
        compiler_params=pltpu.CompilerParams(vmem_limit_bytes=24 << 20),
    )(segments, order, start, qkv, full, lse, grad)


def norm_parts(values):
    centre = jnp.mean(values, axis=-1, keepdims=True)
    shifted = values - centre
    spread_ = jnp.mean(shifted * shifted, axis=-1, keepdims=True)
    scale = lax.rsqrt(spread_ + NORM_EPS)
    return shifted * scale, scale


def norm_backward(grad, normed, scale, gain):
    e = grad * gain
    mean_e = jnp.mean(e, axis=-1, keepdims=True)
    mean_en = jnp.mean(e * normed, axis=-1, keepdims=True)
    return (e - mean_e - normed * mean_en) * scale


def gelu_tanh(values):
    return jax.nn.gelu(values, approximate=True)


def cross_rows(left, right):
    return lax.dot_general(
        left, right, (((0,), (0,)), ((), ())), preferred_element_type=jnp.float32
    )


def after(value, done):
    return lax.optimization_barrier((value, done))[0]


def per_device(
    mesh_sizes,
    inputs,
    first_gain,
    first_shift,
    project_weight,
    project_bias,
    attend_weight,
    attend_bias,
    second_gain,
    second_shift,
    expand_weight,
    expand_bias,
    shrink_weight,
    shrink_bias,
    segments,
    block_order,
    cotangent,
):
    nt, nc = mesh_sizes["tensor"], mesh_sizes["context"]
    own_rows, width = inputs.shape[1], inputs.shape[2]
    local_width = project_weight.shape[2]
    heads = local_width // HEAD_DIM
    block_rows = own_rows * nt
    half = block_rows // 2
    low = jnp.bfloat16
    f32 = lambda value: value.astype(jnp.float32)
    square = nt == 4 and nc == 4 and mesh_sizes["dp"] == 2
    plane = ("context", "dp")

    tokens_own = f32(inputs[0])
    grad_out = cotangent[0]
    bias = jnp.stack([project_bias[0], jnp.zeros_like(project_bias[0]), project_bias[1]])[:, :, None]
    weight_rows = project_weight.transpose(0, 2, 1)
    if square:
        hidden1_full, attend_full, qkv, grads_near = start_part(
            inputs[0], first_gain, first_shift, attend_weight, weight_rows, bias, grad_out, nt, nc, heads, 0
        )
        pieces, attended_full, lse, start = attend_forward(qkv, segments, block_order, half, heads)
        feed, *feed_pieces, middle, grad_middle, vectors, grad_heads, attend_pieces = feed_part(
            pieces,
            inputs[0],
            attend_full,
            (attend_bias, second_gain, second_shift),
            expand_weight,
            shrink_weight,
            expand_bias,
            grads_near,
            grad_out,
            nt,
            nc,
            heads,
            3,
        )
        feed_sum = lax.psum_scatter(after(feed, grad_heads), "tensor", scatter_dimension=0, tiled=True)
        grad_qkv = attend_backward(
            qkv, segments, block_order, start, attended_full, lse, grad_heads, half, heads
        )
        grad_inputs, summed, grad_project, grad_attend, feeds = last_part(
            grad_qkv,
            weight_rows,
            hidden1_full,
            attend_pieces,
            feed_pieces,
            inputs[0],
            first_gain,
            grad_middle,
            vectors,
            6,
            nt,
            heads,
            7,
        )
        grad_project = grad_project.transpose(0, 2, 1)
        grad_shrink, grad_expand = feeds[0].reshape(-1, width), feeds[1].reshape(width, -1)
        wide = expand_bias.shape[0]
    else:
        hidden1 = norm_parts(tokens_own)[0] * first_gain + first_shift
        hidden1_full = gather_rows(hidden1.astype(low), nt, 0)
        attend_full = lax.all_gather(attend_weight, "tensor", axis=0, tiled=True)
        projected = jnp.einsum(
            "ked,rd->ker", weight_rows, hidden1_full, preferred_element_type=jnp.float32
        )
        projected = (projected + bias).astype(low).reshape(3, heads, HEAD_DIM, block_rows)
        qkv = to_heads(projected, nc, 1)
        pieces, attended_full, lse, start = attend_forward(qkv, segments, block_order, half, heads)
        grad_full = lax.all_gather(grad_out, "tensor", axis=0, tiled=True)
        attended = to_rows(pieces, nc, nt, heads, 2).reshape(width, own_rows)
        middle = tokens_own + cross_rows(attended, attend_full) + attend_bias
        normed2, scale2 = norm_parts(middle)
        hidden2 = (normed2 * second_gain + second_shift).astype(low)
        hidden2_full = gather_rows(hidden2, nt, 3)
        pre_act = jnp.dot(hidden2_full, expand_weight, preferred_element_type=jnp.float32) + expand_bias
        activ = gelu_tanh(pre_act).astype(low)
        grad_act = dot(grad_full, shrink_weight, ((1,), (1,)))
        grad_pre = jax.vjp(gelu_tanh, pre_act)[1](grad_act)[0].astype(low)
        grad_shrink = cross_rows(activ, grad_full).astype(low)
        grad_expand = cross_rows(hidden2_full, grad_pre).astype(low)
        grad_hidden2 = scatter_rows(dot(grad_pre, expand_weight, ((1,), (1,))).astype(low), nt, 4)
        grad_expand_bias = jnp.sum(f32(grad_pre), axis=0)
        feed = jnp.dot(activ, shrink_weight, preferred_element_type=jnp.float32).astype(low)

        grad_shrink_bias = jnp.sum(f32(grad_out), axis=0)
        grad_second_gain = jnp.sum(grad_hidden2 * normed2, axis=0)
        grad_second_shift = jnp.sum(grad_hidden2, axis=0)
        grad_middle = f32(grad_out) + norm_backward(grad_hidden2, normed2, scale2, second_gain)
        grad_middle_low = grad_middle.astype(low)
        grad_attend_bias = jnp.sum(f32(grad_middle_low), axis=0)
        grad_attended = dot(attend_full, grad_middle_low, ((1,), (1,))).astype(low)
        grad_attended = grad_attended.reshape(nt * heads, HEAD_DIM, own_rows)
        grad_attend = jnp.dot(attended, grad_middle_low, preferred_element_type=jnp.float32).astype(low)
        grad_heads = rows_back(grad_attended, nc, nt, heads, 5)
        feed_sum = lax.psum_scatter(after(feed, grad_heads), "tensor", scatter_dimension=0, tiled=True)

        grad_qkv = attend_backward(
            qkv, segments, block_order, start, attended_full, lse, grad_heads, half, heads
        )
        grad_rows = from_heads(grad_qkv, nc, heads, 6).reshape(3 * local_width, block_rows)
        grad_project = dot(hidden1_full, grad_rows, ((0,), (1,))).astype(low)
        grad_hidden1 = cross_rows(grad_rows, weight_rows.reshape(3 * local_width, width)).astype(low)
        row_sums = jnp.sum(f32(grad_rows), axis=1)
        grad_project_bias = jnp.concatenate([row_sums[:local_width], row_sums[2 * local_width :]])
        grad_hidden1 = scatter_rows(grad_hidden1, nt, 7)
        normed1, scale1 = norm_parts(tokens_own)
        back = norm_backward(grad_hidden1, normed1, scale1, first_gain)
        grad_inputs = (grad_middle + back).astype(low)
        wide = grad_expand_bias.shape[0]
        vectors = jnp.concatenate(
            [
                jnp.sum(grad_hidden1 * normed1, axis=0),
                jnp.sum(grad_hidden1, axis=0),
                grad_attend_bias,
                grad_second_gain,
                grad_second_shift,
                grad_shrink_bias,
                grad_expand_bias,
                jnp.pad(grad_project_bias, (0, -(wide + 2 * local_width) % width)),
            ]
        ).reshape(-1, width)
        summed = sum_vectors(vectors, 6, mesh_sizes, 8)
        grad_attend = lax.psum_scatter(grad_attend, "tensor", scatter_dimension=0, tiled=True)
        grad_project, grad_attend, grad_shrink, grad_expand = lax.psum(
            (grad_project, grad_attend, grad_shrink, grad_expand), plane
        )
        grad_project = jnp.stack(
            [grad_project[:, at * local_width : (at + 1) * local_width] for at in range(3)]
        )
    feed_sum = f32(after(feed_sum, summed))
    outputs = (middle + feed_sum + shrink_bias).astype(low)[None]
    tail = summed[6:].reshape(-1)
    return (
        outputs,
        grad_inputs[None],
        summed[0],
        summed[1],
        f32(grad_project),
        tail[wide : wide + 2 * local_width].reshape(2, local_width),
        f32(grad_attend),
        summed[2],
        summed[3],
        summed[4],
        f32(grad_expand),
        tail[:wide],
        f32(grad_shrink),
        summed[5],
    )


def solution(mesh):
    rows = P("dp", ("context", "tensor"), None)
    in_specs = (
        rows,
        P(),
        P(),
        P(None, None, "tensor"),
        P(None, "tensor"),
        P("tensor", None),
        P(),
        P(),
        P(),
        P(None, "tensor"),
        P("tensor"),
        P("tensor", None),
        P(),
        P("dp", None),
        P(),
        rows,
    )
    out_specs = (
        rows,
        rows,
        P(),
        P(),
        P(None, None, "tensor"),
        P(None, "tensor"),
        P("tensor", None),
        P(),
        P(),
        P(),
        P(None, "tensor"),
        P("tensor"),
        P("tensor", None),
        P(),
    )
    return jax.shard_map(
        functools.partial(per_device, dict(mesh.shape)),
        mesh=mesh,
        in_specs=in_specs,
        out_specs=out_specs,
        check_vma=False,
    )
```

```python
import functools

import jax
import jax.numpy as jnp
from jax import lax
from jax.experimental import pallas as pl
from jax.experimental.pallas import tpu as pltpu
from jax.sharding import PartitionSpec as P

HEAD_DIM = 64
NEG_FILL = -1e30
NORM_EPS = 1e-05
DOC_LIMIT = 16
MESH = pl.DeviceIdType.MESH
VM = pl.BlockSpec(memory_space=pltpu.VMEM)
SM = pl.BlockSpec(memory_space=pltpu.SMEM)
DMA = pltpu.SemaphoreType.DMA


def remote_params(collective_id, mib=16):
    return pltpu.CompilerParams(
        collective_id=collective_id, has_side_effects=True, vmem_limit_bytes=mib << 20
    )


HB = pl.BlockSpec(memory_space=pltpu.HBM)


def copies(pairs, sems):
    return [pltpu.make_async_copy(src, dst, sems.at[at]) for at, (src, dst) in enumerate(pairs)]


def row(ref):
    return ref[...].reshape(1, -1)


def line_barrier(me, n):
    bar = pltpu.get_barrier_semaphore()

    @pl.when(me > 0)
    def _():
        pl.semaphore_signal(bar, inc=1, device_id={"tensor": me - 1}, device_id_type=MESH)

    @pl.when(me < n - 1)
    def _():
        pl.semaphore_signal(bar, inc=1, device_id={"tensor": me + 1}, device_id_type=MESH)

    pl.semaphore_wait(bar, jnp.where(me > 0, 1, 0) + jnp.where(me < n - 1, 1, 0))


def gather_kernel(n, x_ref, o_ref, send, recv, loc):
    me = lax.axis_index("tensor")
    line_barrier(me, n)
    own = pltpu.make_async_copy(x_ref, o_ref.at[me], loc)
    own.start()

    def copy(d, s):
        shard = jnp.clip(me - s if d == 0 else me + s, 0, n - 1)
        return pltpu.make_async_remote_copy(
            src_ref=x_ref if s == 0 else o_ref.at[shard],
            dst_ref=o_ref.at[shard],
            send_sem=send.at[d, s],
            recv_sem=recv.at[d, s],
            device_id={"tensor": jnp.clip(me + 1 if d == 0 else me - 1, 0, n - 1)},
            device_id_type=MESH,
        )

    def sends(d, s):
        return (me - s >= 0) & (me < n - 1) if d == 0 else (me + s < n) & (me > 0)

    def gets(d, s):
        return me - 1 - s >= 0 if d == 0 else me + 1 + s < n

    def landed(d, s):
        shard = jnp.clip(me - 1 - s if d == 0 else me + 1 + s, 0, n - 1)
        return pltpu.make_async_copy(o_ref.at[shard], o_ref.at[shard], recv.at[d, s])

    for s in range(n - 1):
        for d in range(2):
            if s > 0:

                @pl.when(gets(d, s - 1))
                def _():
                    landed(d, s - 1).wait()

            @pl.when(sends(d, s))
            def _():
                copy(d, s).start()

    for d in range(2):

        @pl.when(gets(d, n - 2))
        def _():
            landed(d, n - 2).wait()

        for s in range(n - 1):

            @pl.when(sends(d, s))
            def _():
                copy(d, s).wait_send()

    own.wait()


def gather_rows(x, n, collective_id):
    rows, cols = x.shape
    return pl.pallas_call(
        functools.partial(gather_kernel, n),
        out_shape=jax.ShapeDtypeStruct((n, rows, cols), x.dtype),
        in_specs=[VM],
        out_specs=VM,
        scratch_shapes=[DMA((2, n - 1)), DMA((2, n - 1)), DMA],
        compiler_params=remote_params(collective_id),
    )(x).reshape(n * rows, cols)


def scatter_kernel(n, x_ref, o_ref, buf, tmp, send, recv):
    me = lax.axis_index("tensor")
    line_barrier(me, n)

    def term(d, k):
        return n - 1 - k if d == 0 else k

    def sends(d, k):
        return me < n - 1 - k if d == 0 else me > k

    def behind(d):
        return me > 0 if d == 0 else me < n - 1

    def copy(d, k, first):
        return pltpu.make_async_remote_copy(
            src_ref=x_ref.at[term(d, k)] if first else tmp.at[d, k],
            dst_ref=buf.at[d, k],
            send_sem=send.at[d, k],
            recv_sem=recv.at[d, k],
            device_id={"tensor": jnp.clip(me + 1 if d == 0 else me - 1, 0, n - 1)},
            device_id_type=MESH,
        )

    def landed(d, k):
        return pltpu.make_async_copy(buf.at[d, k], buf.at[d, k], recv.at[d, k])

    for d in range(2):

        @pl.when(jnp.logical_not(behind(d)))
        def _():
            for k in range(n - 1):
                copy(d, k, True).start()

    for k in range(n - 1):
        for d in range(2):

            @pl.when(behind(d) & sends(d, k))
            def _():
                landed(d, k).wait()
                both = buf[d, k].astype(jnp.float32) + x_ref[term(d, k)].astype(jnp.float32)
                tmp[d, k] = both.astype(tmp.dtype)
                copy(d, k, False).start()

    o_ref[...] = x_ref[me].astype(jnp.float32)
    for d in range(2):
        for k in range(n - 1):

            @pl.when(behind(d) & (me == term(d, k)))
            def _():
                landed(d, k).wait()
                o_ref[...] += buf[d, k].astype(jnp.float32)

    for d in range(2):
        for k in range(n - 1):

            @pl.when(sends(d, k))
            def _():
                copy(d, k, False).wait_send()


def scatter_rows(x, n, collective_id):
    rows, cols = x.shape
    own = rows // n
    return pl.pallas_call(
        functools.partial(scatter_kernel, n),
        out_shape=jax.ShapeDtypeStruct((own, cols), jnp.float32),
        in_specs=[VM],
        out_specs=VM,
        scratch_shapes=[
            pltpu.VMEM((2, n - 1, own, cols), x.dtype),
            pltpu.VMEM((2, n - 1, own, cols), x.dtype),
            DMA((2, n - 1)),
            DMA((2, n - 1)),
        ],
        compiler_params=remote_params(collective_id),
    )(x.reshape(n, own, cols))


def group_barrier(axes, sizes):
    mine = [lax.axis_index(name) for name in axes]
    place = sum_index(mine, sizes)
    total = 1
    for size in sizes:
        total *= size
    bar = pltpu.get_barrier_semaphore()
    for shift in range(1, total):
        other = lax.rem(place + shift, total)
        pl.semaphore_signal(bar, inc=1, device_id=spread(other, axes, sizes), device_id_type=MESH)
    pl.semaphore_wait(bar, total - 1)
    return place, total


def sum_index(mine, sizes):
    place = 0
    for at, size in zip(mine, sizes):
        place = place * size + at
    return place


def spread(place, axes, sizes):
    found = {}
    for name, size in reversed(tuple(zip(axes, sizes))):
        found[name] = lax.rem(place, size)
        place = lax.div(place, size)
    return found


def to_heads_kernel(nc, heads, x_ref, o_ref, send, recv, loc):
    me, _ = group_barrier(("context",), (nc,))

    def copy(shift):
        other = lax.rem(me + shift, nc)
        return other, pltpu.make_async_remote_copy(
            src_ref=x_ref.at[:, jnp.minimum(other, heads - 1)],
            dst_ref=o_ref.at[me],
            send_sem=send.at[shift],
            recv_sem=recv.at[shift],
            device_id={"context": other},
            device_id_type=MESH,
        )

    for shift in range(1, nc):
        other, item = copy(shift)

        @pl.when(other < heads)
        def _():
            item.start()

    own = pltpu.make_async_copy(x_ref.at[:, jnp.minimum(me, heads - 1)], o_ref.at[me], loc)
    own.start()
    own.wait()

    @pl.when(me < heads)
    def _():
        for shift in range(1, nc):
            source = lax.rem(me + nc - shift, nc)
            pltpu.make_async_copy(o_ref.at[source], o_ref.at[source], recv.at[shift]).wait()

    for shift in range(1, nc):
        other, item = copy(shift)

        @pl.when(other < heads)
        def _():
            item.wait_send()


def to_heads(x, nc, collective_id):
    heads = x.shape[1]
    return pl.pallas_call(
        functools.partial(to_heads_kernel, nc, heads),
        out_shape=jax.ShapeDtypeStruct((nc, x.shape[0]) + x.shape[2:], x.dtype),
        in_specs=[VM],
        out_specs=VM,
        scratch_shapes=[DMA((nc,)), DMA((nc,)), DMA],
        compiler_params=remote_params(collective_id),
    )(x)


def from_heads_kernel(nc, heads, x_ref, o_ref, send, recv, loc):
    me, _ = group_barrier(("context",), (nc,))

    def copy(shift):
        other = lax.rem(me + shift, nc)
        return pltpu.make_async_remote_copy(
            src_ref=x_ref.at[other],
            dst_ref=o_ref.at[:, jnp.minimum(me, heads - 1)],
            send_sem=send.at[shift],
            recv_sem=recv.at[shift],
            device_id={"context": other},
            device_id_type=MESH,
        )

    @pl.when(me < heads)
    def _():
        for shift in range(1, nc):
            copy(shift).start()
        own = pltpu.make_async_copy(x_ref.at[me], o_ref.at[:, me], loc)
        own.start()
        own.wait()

    for shift in range(1, nc):
        source = lax.rem(me + nc - shift, nc)

        @pl.when(source < heads)
        def _():
            at = jnp.minimum(source, heads - 1)
            pltpu.make_async_copy(o_ref.at[:, at], o_ref.at[:, at], recv.at[shift]).wait()

    @pl.when(me < heads)
    def _():
        for shift in range(1, nc):
            copy(shift).wait_send()


def from_heads(x, nc, heads, collective_id):
    return pl.pallas_call(
        functools.partial(from_heads_kernel, nc, heads),
        out_shape=jax.ShapeDtypeStruct((x.shape[1], heads) + x.shape[2:], x.dtype),
        in_specs=[VM],
        out_specs=VM,
        scratch_shapes=[DMA((nc,)), DMA((nc,)), DMA],
        compiler_params=remote_params(collective_id),
    )(x)


AXES = ("context", "tensor")


def rows_kernel(nc, nt, heads, x_ref, o_ref, send, recv, loc):
    me, total = group_barrier(AXES, (nc, nt))
    my_ctx, my_ten = lax.axis_index("context"), lax.axis_index("tensor")
    my_head = my_ten * heads + jnp.minimum(my_ctx, heads - 1)

    def copy(shift):
        other = lax.rem(me + shift, total)
        return pltpu.make_async_remote_copy(
            src_ref=x_ref.at[other],
            dst_ref=o_ref.at[my_head],
            send_sem=send.at[shift],
            recv_sem=recv.at[shift],
            device_id=spread(other, AXES, (nc, nt)),
            device_id_type=MESH,
        )

    @pl.when(my_ctx < heads)
    def _():
        for shift in range(1, total):
            copy(shift).start()
        own = pltpu.make_async_copy(x_ref.at[me], o_ref.at[my_head], loc)
        own.start()
        own.wait()

    for shift in range(1, total):
        source = lax.rem(me + total - shift, total)
        ctx, ten = lax.div(source, nt), lax.rem(source, nt)

        @pl.when(ctx < heads)
        def _():
            at = ten * heads + jnp.minimum(ctx, heads - 1)
            pltpu.make_async_copy(o_ref.at[at], o_ref.at[at], recv.at[shift]).wait()

    @pl.when(my_ctx < heads)
    def _():
        for shift in range(1, total):
            copy(shift).wait_send()


def to_rows(x, nc, nt, heads, collective_id):
    total = nc * nt
    return pl.pallas_call(
        functools.partial(rows_kernel, nc, nt, heads),
        out_shape=jax.ShapeDtypeStruct((nt * heads,) + x.shape[1:], x.dtype),
        in_specs=[VM],
        out_specs=VM,
        scratch_shapes=[DMA((total,)), DMA((total,)), DMA],
        compiler_params=remote_params(collective_id),
    )(x)


def rows_back_kernel(nc, nt, heads, x_ref, o_ref, send, recv, loc):
    me, total = group_barrier(AXES, (nc, nt))
    my_ctx, my_ten = lax.axis_index("context"), lax.axis_index("tensor")

    def copy(shift):
        other = lax.rem(me + shift, total)
        ctx, ten = lax.div(other, nt), lax.rem(other, nt)
        return ctx < heads, pltpu.make_async_remote_copy(
            src_ref=x_ref.at[ten * heads + jnp.minimum(ctx, heads - 1)],
            dst_ref=o_ref.at[me],
            send_sem=send.at[shift],
            recv_sem=recv.at[shift],
            device_id={"context": ctx, "tensor": ten},
            device_id_type=MESH,
        )

    for shift in range(1, total):
        goes, item = copy(shift)

        @pl.when(goes)
        def _():
            item.start()

    own = pltpu.make_async_copy(
        x_ref.at[my_ten * heads + jnp.minimum(my_ctx, heads - 1)], o_ref.at[me], loc
    )
    own.start()
    own.wait()

    @pl.when(my_ctx < heads)
    def _():
        for shift in range(1, total):
            source = lax.rem(me + total - shift, total)
            pltpu.make_async_copy(o_ref.at[source], o_ref.at[source], recv.at[shift]).wait()

    for shift in range(1, total):
        goes, item = copy(shift)

        @pl.when(goes)
        def _():
            item.wait_send()


def rows_back(x, nc, nt, heads, collective_id):
    total = nc * nt
    return pl.pallas_call(
        functools.partial(rows_back_kernel, nc, nt, heads),
        out_shape=jax.ShapeDtypeStruct((total,) + x.shape[1:], x.dtype),
        in_specs=[VM],
        out_specs=VM,
        scratch_shapes=[DMA((total,)), DMA((total,)), DMA],
        compiler_params=remote_params(collective_id),
    )(x)


def vectors_kernel(names, sizes, shared, x_ref, o_ref, now, *rest):
    bufs, sems = rest[: len(names)], rest[len(names) :]
    bar = pltpu.get_barrier_semaphore()
    for name, size in zip(names, sizes):
        me = lax.axis_index(name)
        for shift in range(1, size):
            pl.semaphore_signal(
                bar, inc=1, device_id={name: lax.rem(me + shift, size)}, device_id_type=MESH
            )
    pl.semaphore_wait(bar, sum(sizes) - len(sizes))
    for stage, (name, size) in enumerate(zip(names, sizes)):
        buf, send, recv = bufs[stage], sems[2 * stage], sems[2 * stage + 1]
        me = lax.axis_index(name)

        def copy(shift):
            return pltpu.make_async_remote_copy(
                src_ref=now.at[stage] if stage else x_ref.at[0],
                dst_ref=buf.at[me],
                send_sem=send.at[shift],
                recv_sem=recv.at[shift],
                device_id={name: lax.rem(me + shift, size)},
                device_id_type=MESH,
            )

        for shift in range(1, size):
            copy(shift).start()
        buf[me] = now[stage] if stage else x_ref[0]
        for shift in range(1, size):
            source = lax.rem(me + size - shift, size)
            pltpu.make_async_copy(buf.at[source], buf.at[source], recv.at[shift]).wait()
        total = buf[0]
        for at in range(1, size):
            total = total + buf[at]
        if stage == 0:
            row = lax.broadcasted_iota(jnp.int32, total.shape, 0)
            total = jnp.where(row < shared, total, x_ref[0])
        if stage + 1 < len(names):
            now[stage + 1] = total
        else:
            o_ref[...] = total
        for shift in range(1, size):
            copy(shift).wait_send()


def sum_vectors(rows, shared, mesh_sizes, collective_id):
    names = ("tensor", "context", "dp")
    sizes = tuple(mesh_sizes[name] for name in names)
    shape = rows.shape
    return pl.pallas_call(
        functools.partial(vectors_kernel, names, sizes, shared),
        out_shape=jax.ShapeDtypeStruct(shape, jnp.float32),
        in_specs=[VM],
        out_specs=VM,
        scratch_shapes=[pltpu.VMEM((len(names),) + shape, jnp.float32)]
        + [pltpu.VMEM((size,) + shape, jnp.float32) for size in sizes]
        + [DMA((size,)) for size in sizes for _ in range(2)],
        compiler_params=remote_params(collective_id),
    )(rows[None])


class PlaneSum:
    def __init__(self, u, p, o, bufs=None, spread=None):
        self.u, self.p, self.o = u, p, o
        if bufs is not None:
            self.rc, self.s1, self.ra, self.rb, self.sa, self.sb, self.ta, self.tb = bufs[:8]
            self.send1, self.recv1 = bufs[8:]
        if spread is not None:
            self.send2, self.recv2, self.loc = spread
        ctx, self.x = lax.axis_index("context"), lax.axis_index("dp")
        self.core, self.y = lax.rem(ctx, 2), lax.div(ctx, 2)
        self.chip_peer = {"context": ctx + 1 - 2 * self.core}
        self.y_peer = {"context": lax.rem(ctx + 2, 4)}
        self.x_peer = {"dp": 1 - self.x}

    @staticmethod
    def reduce_scratch(shape, dtype):
        tail = tuple(shape[1:])
        bufs = [pltpu.VMEM((count,) + tail, dtype) for count in (8, 8, 2, 2, 2, 2, 1, 1)]
        return bufs + [DMA((5,)), DMA((5,))]

    @staticmethod
    def spread_scratch():
        return [DMA((5,)), DMA((5,)), DMA((2,))]

    @staticmethod
    def greet(bar):
        ctx, x = lax.axis_index("context"), lax.axis_index("dp")
        for peer in (
            {"context": ctx + 1 - 2 * lax.rem(ctx, 2)},
            {"context": lax.rem(ctx + 2, 4)},
            {"dp": 1 - x},
        ):
            pl.semaphore_signal(bar, inc=1, device_id=peer, device_id_type=MESH)
        return 3

    def copy(self, at, src, dst, peer):
        send, recv = (self.send1, self.recv1) if at < 5 else (self.send2, self.recv2)
        return pltpu.make_async_remote_copy(
            src_ref=src,
            dst_ref=dst,
            send_sem=send.at[at % 5],
            recv_sem=recv.at[at % 5],
            device_id=peer,
            device_id_type=MESH,
        )

    def got(self, at, ref):
        recv = self.recv1 if at < 5 else self.recv2
        pltpu.make_async_copy(ref, ref, recv.at[at % 5]).wait()

    def add(self, out, left, right):
        f32 = jnp.float32
        out[...] = (left[...].astype(f32) + right[...].astype(f32)).astype(out.dtype)

    def mine(self, half):
        if half == 0:
            return pl.ds(self.core * 8 + 2 * self.x + self.y, 1)
        return pl.ds(self.core * 8 + 4 + 2 * self.y + self.x, 1)

    def hop(self, at):
        x, y, core = self.x, self.y, self.core
        o, p = self.o, self.p
        pair_a, pair_b = pl.ds(core * 8 + 2 * x, 2), pl.ds(core * 8 + 4 + 2 * y, 2)
        one = lambda at: pl.ds(at, 1)
        return [
            lambda: self.copy(0, self.by_core(1 - core), self.rc, self.chip_peer),
            lambda: self.copy(1, self.quarter(0, 1 - x), self.ra, self.x_peer),
            lambda: self.copy(2, self.quarter(1, 1 - y), self.rb, self.y_peer),
            lambda: self.copy(3, self.eighth(0, 1 - y), self.ta, self.y_peer),
            lambda: self.copy(4, self.eighth(1, 1 - x), self.tb, self.x_peer),
            lambda: self.copy(5, p.at[one(0)], o.at[self.mine(0)], self.y_peer),
            lambda: self.copy(6, p.at[one(1)], o.at[self.mine(1)], self.x_peer),
            lambda: self.copy(7, o.at[pair_a], o.at[pair_a], self.x_peer),
            lambda: self.copy(8, o.at[pair_b], o.at[pair_b], self.y_peer),
            lambda: self.copy(9, o.at[pl.ds(core * 8, 8)], o.at[pl.ds(core * 8, 8)], self.chip_peer),
        ][at]()

    def begin(self):
        self.hop(0).start()

    def by_core(self, core):
        return self.u.at[pl.ds(core * 8, 8)]

    def quarter(self, half, at):
        return self.s1.at[pl.ds(4 * half + 2 * at, 2)]

    def eighth(self, half, at):
        return (self.sa, self.sb)[half].at[pl.ds(at, 1)]

    def result(self, half):
        return self.p.at[pl.ds(half, 1)]

    def first(self):
        self.got(0, self.rc)
        self.add(self.s1, self.by_core(self.core), self.rc)
        self.hop(1).start()
        self.hop(2).start()

    def second(self):
        self.got(1, self.ra)
        self.add(self.sa, self.quarter(0, self.x), self.ra)
        self.hop(3).start()
        self.got(2, self.rb)
        self.add(self.sb, self.quarter(1, self.y), self.rb)
        self.hop(4).start()

    def third(self):
        self.got(3, self.ta)
        self.add(self.result(0), self.eighth(0, self.y), self.ta)
        self.got(4, self.tb)
        self.add(self.result(1), self.eighth(1, self.x), self.tb)

    def reduced(self):
        for at in range(5):
            self.hop(at).wait_send()

    def kept(self, half):
        return pltpu.make_async_copy(self.p.at[pl.ds(half, 1)], self.o.at[self.mine(half)], self.loc.at[half])

    def spread1(self):
        self.hop(5).start()
        self.hop(6).start()
        self.kept(0).start()
        self.kept(1).start()

    def spread2(self):
        x, y, core = self.x, self.y, self.core
        self.kept(0).wait()
        self.got(5, self.o.at[pl.ds(core * 8 + 2 * x + 1 - y, 1)])
        self.hop(7).start()
        self.kept(1).wait()
        self.got(6, self.o.at[pl.ds(core * 8 + 4 + 2 * y + 1 - x, 1)])
        self.hop(8).start()

    def spread3(self):
        x, y, core = self.x, self.y, self.core
        self.got(7, self.o.at[pl.ds(core * 8 + 2 - 2 * x, 2)])
        self.got(8, self.o.at[pl.ds(core * 8 + 6 - 2 * y, 2)])
        self.hop(9).start()

    def everywhere(self):
        self.got(9, self.o.at[pl.ds(8 - self.core * 8, 8)])
        for at in range(5, 10):
            self.hop(at).wait_send()


class StripSum(PlaneSum):
    @staticmethod
    def reduce_scratch(shape, dtype):
        lead, rows, cols = shape
        rest = lead - 2
        shapes = [(lead, rows)] * 2
        shapes += [(count, rows // 2) for count in (2, rest, 2, rest)] + [(count, rows // 4) for count in (2, rest)]
        return [pltpu.VMEM(item + (cols // 2,), dtype) for item in shapes] + [DMA((5,)), DMA((5,))]

    def lead(self, half):
        whole = (self.u if self.u is not None else self.o).shape[0]
        return pl.ds(0, 2) if half == 0 else pl.ds(2, whole - 2)

    def strip(self, core):
        size = (self.u if self.u is not None else self.o).shape[2] // 2
        return pl.ds(pl.multiple_of(core * size, 128), size)

    def rows(self, at, parts):
        size = (self.u if self.u is not None else self.o).shape[1] // parts
        return pl.ds(pl.multiple_of(at * size, 16), size)

    def by_core(self, core):
        return self.u.at[:, :, self.strip(core)]

    def quarter(self, half, at):
        return self.s1.at[self.lead(half), self.rows(at, 2)]

    def eighth(self, half, at):
        return (self.sa, self.sb)[half].at[:, self.rows(at, 4)]

    def result(self, half):
        return self.p.at[half, pl.ds(0, 2 if half == 0 else self.u.shape[0] - 2)]

    def hop(self, at):
        if at < 5:
            return super().hop(at)
        o, x, y = self.o, self.x, self.y
        mine = lambda half: o.at[
            self.lead(half), self.rows(2 * x + y if half == 0 else 2 * y + x, 4), self.strip(self.core)
        ]
        pair = lambda half: o.at[self.lead(half), self.rows(x if half == 0 else y, 2), self.strip(self.core)]
        both = o.at[:, :, self.strip(self.core)]
        return [
            lambda: self.copy(5, self.result(0), mine(0), self.y_peer),
            lambda: self.copy(6, self.result(1), mine(1), self.x_peer),
            lambda: self.copy(7, pair(0), pair(0), self.x_peer),
            lambda: self.copy(8, pair(1), pair(1), self.y_peer),
            lambda: self.copy(9, both, both, self.chip_peer),
        ][at - 5]()

    def kept(self, half):
        x, y = self.x, self.y
        mine = self.o.at[
            self.lead(half), self.rows(2 * x + y if half == 0 else 2 * y + x, 4), self.strip(self.core)
        ]
        return pltpu.make_async_copy(self.result(half), mine, self.loc.at[half])

    def spread2(self):
        x, y, mine = self.x, self.y, self.strip(self.core)
        self.kept(0).wait()
        self.got(5, self.o.at[self.lead(0), self.rows(2 * x + 1 - y, 4), mine])
        self.hop(7).start()
        self.kept(1).wait()
        self.got(6, self.o.at[self.lead(1), self.rows(2 * y + 1 - x, 4), mine])
        self.hop(8).start()

    def spread3(self):
        mine = self.strip(self.core)
        self.got(7, self.o.at[self.lead(0), self.rows(1 - self.x, 2), mine])
        self.got(8, self.o.at[self.lead(1), self.rows(1 - self.y, 2), mine])
        self.hop(9).start()

    def everywhere(self):
        self.got(9, self.o.at[:, :, self.strip(1 - self.core)])
        for at in range(5, 10):
            self.hop(at).wait_send()


def unit_pieces(unit):
    return jax.ShapeDtypeStruct((2,) + unit.shape[1:], unit.dtype)


def line_greet(bar, me, n):
    @pl.when(me > 0)
    def _():
        pl.semaphore_signal(bar, inc=1, device_id={"tensor": me - 1}, device_id_type=MESH)

    @pl.when(me < n - 1)
    def _():
        pl.semaphore_signal(bar, inc=1, device_id={"tensor": me + 1}, device_id_type=MESH)

    return jnp.where(me > 0, 1, 0) + jnp.where(me < n - 1, 1, 0)


class LineScatter:
    def __init__(self, n, x, o, buf, tmp, send, recv):
        self.n, self.x, self.o, self.buf, self.tmp, self.send, self.recv = n, x, o, buf, tmp, send, recv
        self.me = lax.axis_index("tensor")

    @staticmethod
    def scratch(n, own, cols, dtype):
        return [
            pltpu.VMEM((2, n - 1, own, cols), dtype),
            pltpu.VMEM((2, n - 1, own, cols), dtype),
            DMA((2, n - 1)),
            DMA((2, n - 1)),
        ]

    def term(self, d, k):
        return self.n - 1 - k if d == 0 else k

    def sends(self, d, k):
        return self.me < self.n - 1 - k if d == 0 else self.me > k

    def behind(self, d):
        return self.me > 0 if d == 0 else self.me < self.n - 1

    def copy(self, d, k, first):
        return pltpu.make_async_remote_copy(
            src_ref=self.x.at[self.term(d, k)] if first else self.tmp.at[d, k],
            dst_ref=self.buf.at[d, k],
            send_sem=self.send.at[d, k],
            recv_sem=self.recv.at[d, k],
            device_id={"tensor": jnp.clip(self.me + 1 if d == 0 else self.me - 1, 0, self.n - 1)},
            device_id_type=MESH,
        )

    def landed(self, d, k):
        return pltpu.make_async_copy(self.buf.at[d, k], self.buf.at[d, k], self.recv.at[d, k])

    def begin(self, ks):
        for d in range(2):

            @pl.when(jnp.logical_not(self.behind(d)))
            def _():
                for k in ks:
                    self.copy(d, k, True).start()

    def step(self, k, which=None):
        for d in range(2):
            now = self.behind(d) & self.sends(d, k)

            @pl.when(now if which is None else now & which(d))
            def _():
                self.landed(d, k).wait()
                at = self.term(d, k)
                both = self.buf[d, k].astype(jnp.float32) + self.x[at].astype(jnp.float32)
                self.tmp[d, k] = both.astype(self.tmp.dtype)
                self.copy(d, k, False).start()

    def end(self):
        self.o[...] = self.x[self.me].astype(jnp.float32)
        for d in range(2):
            for k in range(self.n - 1):

                @pl.when(self.behind(d) & (self.me == self.term(d, k)))
                def _():
                    self.landed(d, k).wait()
                    self.o[...] += self.buf[d, k].astype(jnp.float32)

        for d in range(2):
            for k in range(self.n - 1):

                @pl.when(self.sends(d, k))
                def _():
                    self.copy(d, k, False).wait_send()


GELU_SCALE = 0.7978845608028654
GELU_CUBE = 0.044715


def feed_kernel(n, nc, heads, chunks, piece_ref, *rest):
    (token_hbm, out_ref, abias_hbm, gain_hbm, shift_hbm, up_hbm, down_hbm, bias_hbm, near_ref, cot_ref), rest = rest[:10], rest[10:]
    outs, heads_ref, rest = rest[:7], rest[7], rest[8:]
    kept_refs, rest = rest[:7], rest[7:]
    feed_ref, p1_ref, p2_ref, middle_ref, gm_ref, vec_ref, p3_ref = kept_refs
    (token_ref, abias_ref, gain_ref, shift_ref, bias_ref, osem), rest = rest[:6], rest[6:]
    leave = copies(tuple(zip(kept_refs, outs)), osem)
    (o_ref, sum_ref, att_ref, gpiece, u3, bsend, brecv, bloc), rest = rest[:8], rest[8:]
    (x_ref, up_ref, down_ref, grad_ref, wsem, asend, arecv, aloc, csend, crecv, cloc), rest = rest[:11], rest[11:]
    (held, act, gp, part, acc, buf, tmp, u1, u2), rest = rest[:9], rest[9:]
    (gsend, grecv, loc, ssend, srecv), rest = rest[:5], rest[5:]
    plane = [PlaneSum(u1, p1_ref, None, rest[:10]), PlaneSum(u2, p2_ref, None, rest[10:20])]
    out_sum = StripSum(u3, p3_ref, None, rest[20:30])
    me = lax.axis_index("tensor")
    rows, width = token_ref.shape
    wide = up_ref.shape[1]
    few = rows // chunks
    f32, low = jnp.float32, jnp.bfloat16
    ctx, dp = lax.axis_index("context"), lax.axis_index("dp")
    place, total = ctx * n + me, nc * n
    my_head = me * heads + jnp.minimum(ctx, heads - 1)
    bar = pltpu.get_barrier_semaphore()
    for shift in range(1, total):
        other = lax.rem(place + shift, total)
        pl.semaphore_signal(bar, inc=1, device_id=spread(other, AXES, (nc, n)), device_id_type=MESH)
    pl.semaphore_signal(bar, inc=1, device_id={"dp": 1 - dp}, device_id_type=MESH)
    weights_in = copies(
        (
            (token_hbm, token_ref),
            (abias_hbm, abias_ref),
            (gain_hbm, gain_ref),
            (shift_hbm, shift_ref),
            (bias_hbm, bias_ref),
            (up_hbm, up_ref),
            (down_hbm, down_ref),
        ),
        wsem,
    )
    for item in weights_in:
        item.start()

    def grad_rows(block):
        return grad_ref.at[pl.ds(pl.multiple_of(block * rows, rows), rows)]

    def grad_on(d, s):
        block = jnp.clip(me - s if d == 0 else me + s, 0, n - 1)
        return pltpu.make_async_remote_copy(
            src_ref=near_ref.at[block] if s == 1 else grad_rows(block),
            dst_ref=grad_rows(block),
            send_sem=csend.at[d, s],
            recv_sem=crecv.at[d, s],
            device_id={"tensor": jnp.clip(me + 1 if d == 0 else me - 1, 0, n - 1)},
            device_id_type=MESH,
        )

    def grad_sends(d, s):
        return (me - s >= 0) & (me < n - 1) if d == 0 else (me + s < n) & (me > 0)

    def grad_near(d):
        block = jnp.clip(me - 1 if d == 0 else me + 1, 0, n - 1)
        return pltpu.make_async_copy(near_ref.at[block], grad_rows(block), cloc.at[d])

    def grad_own():
        return pltpu.make_async_copy(cot_ref, grad_rows(me), cloc.at[2])

    def beside(d):
        return me > 0 if d == 0 else me < n - 1

    grad_own().start()
    for d in range(2):

        @pl.when(beside(d))
        def _():
            grad_near(d).start()

    pl.semaphore_wait(bar, total)
    for d in range(2):

        @pl.when(grad_sends(d, 1))
        def _():
            grad_on(d, 1).start()

    def to_place(shift):
        other = lax.rem(place + shift, total)
        return pltpu.make_async_remote_copy(
            src_ref=piece_ref.at[other],
            dst_ref=att_ref.at[my_head],
            send_sem=asend.at[shift],
            recv_sem=arecv.at[shift],
            device_id=spread(other, AXES, (nc, n)),
            device_id_type=MESH,
        )

    @pl.when(ctx < heads)
    def _():
        for shift in range(1, total):
            to_place(shift).start()
        stay = pltpu.make_async_copy(piece_ref.at[place], att_ref.at[my_head], aloc)
        stay.start()
        stay.wait()

    for shift in range(1, total):
        source = lax.rem(place + total - shift, total)
        at_ctx, at_ten = lax.div(source, n), lax.rem(source, n)

        @pl.when(at_ctx < heads)
        def _():
            landed = att_ref.at[at_ten * heads + jnp.minimum(at_ctx, heads - 1)]
            pltpu.make_async_copy(landed, landed, arecv.at[shift]).wait()

    for item in weights_in[:4]:
        item.wait()
    attended = att_ref[...].reshape(width, rows)
    middle = token_ref[...].astype(f32) + dot(attended, out_ref[...], ((0,), (0,))) + row(abias_ref)
    middle_ref[...] = middle
    leave[3].start()
    x_ref[...] = (norm_parts(middle)[0] * row(gain_ref) + row(shift_ref)).astype(low)

    @pl.when(ctx < heads)
    def _():
        for shift in range(1, total):
            to_place(shift).wait_send()

    def rows_of(block):
        return pl.ds(pl.multiple_of(block * rows, rows), rows)

    def neighbour(d):
        return {"tensor": jnp.clip(jnp.where(d == 0, me + 1, me - 1), 0, n - 1)}

    def onward(d):
        return jnp.where(d == 0, me, n - 1 - me) < n - 1

    def hand_on(d, s, block, first):
        return pltpu.make_async_remote_copy(
            src_ref=x_ref if first else held.at[rows_of(block)],
            dst_ref=held.at[rows_of(block)],
            send_sem=gsend.at[d, s],
            recv_sem=grecv.at[d, s],
            device_id=neighbour(d),
            device_id_type=MESH,
        )

    def chunk(block, c):
        return pl.ds(pl.multiple_of(block * rows + c * few, few), few)

    def back(d, block, c, first):
        at = chunk(block, c)
        return pltpu.make_async_remote_copy(
            src_ref=part.at[at] if first else tmp.at[at],
            dst_ref=buf.at[d, at],
            send_sem=ssend.at[block, c],
            recv_sem=srecv.at[d, block, c],
            device_id=neighbour(d),
            device_id_type=MESH,
        )

    for d in range(2):

        @pl.when(onward(d))
        def _():
            hand_on(d, 0, me, True).start()

    own = pltpu.make_async_copy(x_ref, held.at[rows_of(me)], loc)
    own.start()
    sum_ref[...] = jnp.zeros_like(sum_ref)
    own.wait()
    for item in weights_in[4:]:
        item.wait()
    grad_own().wait()
    for d in range(2):

        @pl.when(beside(d))
        def _():
            grad_near(d).wait()

    for s in range(1, n - 1):
        for d in range(2):
            block = me - 1 - s if d == 0 else me + 1 + s

            @pl.when((block >= 0) & (block < n))
            def _():
                landed = grad_rows(jnp.clip(block, 0, n - 1))
                pltpu.make_async_copy(landed, landed, crecv.at[d, s]).wait()

            if s + 1 < n - 1:

                @pl.when(grad_sends(d, s + 1))
                def _():
                    grad_on(d, s + 1).start()

        if s == n - 3:
            break
    columns = 256

    def work(block):
        here = rows_of(block)
        acc[...] = jnp.zeros_like(acc)

        @pl.loop(0, wide // columns)
        def _(j):
            at = pl.ds(pl.multiple_of(j * columns, columns), columns)
            pre = dot(held[here, :], up_ref[:, at], ((1,), (0,))) + bias_ref[at].reshape(1, -1)
            square = pre * pre
            tanh = jnp.tanh(GELU_SCALE * pre * (1.0 + GELU_CUBE * square))
            act[here, at] = (0.5 * pre * (1.0 + tanh)).astype(low)
            slope = 0.5 * (1.0 + tanh) + 0.5 * pre * (1.0 - tanh * tanh) * (
                GELU_SCALE * (1.0 + 3.0 * GELU_CUBE * square)
            )
            grad = (dot(grad_ref[here, :], down_ref[at, :], ((1,), (1,))) * slope).astype(low)
            gp[here, at] = grad
            acc[...] += dot(grad, up_ref[:, at], ((1,), (1,)))

        part[here, :] = acc[...].astype(low)
        sum_ref[...] += jnp.sum(gp[here, :].astype(f32), axis=0, keepdims=True)

    near = jnp.minimum(me, n - 1 - me)
    toward = jnp.where(2 * me < n - 1, -1, 1)

    @pl.loop(0, n)
    def _(slot):
        paired = slot <= 2 * near
        distance = jnp.where(paired, lax.div(slot + 1, 2), slot - near)
        side = jnp.where(paired & (lax.rem(slot, 2) == 1), toward, -toward)
        block = me + side * distance
        d = jnp.where(block < me, 0, 1)
        s = jnp.maximum(distance - 1, 0)

        @pl.when(slot > 0)
        def _():
            landed = held.at[rows_of(block)]
            pltpu.make_async_copy(landed, landed, grecv.at[d, s]).wait()

            @pl.when(onward(d))
            def _():
                hand_on(d, jnp.minimum(s + 1, n - 2), block, False).start()

        @pl.when(distance == n - 1)
        def _():
            landed = grad_rows(block)
            pltpu.make_async_copy(landed, landed, crecv.at[d, n - 2]).wait()

        work(block)

        @pl.when((slot > 0) & ((me == 0) | (me == n - 1)))
        def _():
            for c in range(chunks):
                back(1 - d, block, c, True).start()

    def weights(left, right, unit):
        half = wide // 2

        @pl.loop(0, 2)
        def _(j):
            at = pl.ds(pl.multiple_of(j * half, 128), half)
            total = dot(left[:, at], right[...], ((0,), (0,)))
            unit[pl.ds(8 * j, 8)] = total.astype(low).reshape((8,) + unit.shape[1:])

    weights(act, grad_ref, u1)
    plane[0].begin()
    weights(held, gp, u2)
    plane[1].begin()

    def relay(way, block):
        d = jnp.where(way > 0, 0, 1)

        @pl.when((me > 0) & (me < n - 1) & (block >= 0) & (block < n))
        def _():
            for c in range(chunks):
                at = chunk(block, c)
                landed = buf.at[d, at]
                pltpu.make_async_copy(landed, landed, srecv.at[d, block, c]).wait()
                tmp[at, :] = (buf[d, at, :].astype(f32) + part[at, :].astype(f32)).astype(low)
                back(d, block, c, False).start()

    plane[0].first()
    for j in range(1, n):
        relay(-toward, me - toward * j)
        if j == 1:
            plane[1].first()

    @pl.loop(0, n)
    def _(block):
        here = rows_of(block)
        feed_ref[here, :] = dot(act[here, :], down_ref[...], ((1,), (0,))).astype(low)

    leave[0].start()

    plane[0].second()
    plane[1].second()
    for j in range(1, n):
        relay(toward, me + toward * j)
    for item in plane:
        item.third()
    for c in range(chunks):
        at = chunk(me, c)
        mine = pl.ds(c * few, few)
        o_ref[mine, :] = part[at, :].astype(f32)
        for d in range(2):

            @pl.when(me > 0 if d == 0 else me < n - 1)
            def _():
                landed = buf.at[d, at]
                pltpu.make_async_copy(landed, landed, srecv.at[d, me, c]).wait()
                o_ref[mine, :] += buf[d, at, :].astype(f32)

    grad = o_ref[...]
    normed, scale = norm_parts(middle_ref[...])
    above = grad_ref[rows_of(me), :].astype(f32)
    grad_middle = above + norm_backward(grad, normed, scale, row(gain_ref))
    gm_ref[...] = grad_middle
    for at in (1, 2, 4):
        leave[at].start()
    gm_low = grad_middle.astype(low)
    back_out = dot(out_ref[...], gm_low, ((1,), (1,))).astype(low)
    gpiece[...] = back_out.reshape(gpiece.shape)
    vec_ref[...] = jnp.zeros_like(vec_ref)
    vec_ref[2:3, :] = jnp.sum(gm_low.astype(f32), axis=0, keepdims=True)

    def to_head(shift):
        other = lax.rem(place + shift, total)
        at_ctx, at_ten = lax.div(other, n), lax.rem(other, n)
        return at_ctx < heads, pltpu.make_async_remote_copy(
            src_ref=gpiece.at[at_ten * heads + jnp.minimum(at_ctx, heads - 1)],
            dst_ref=heads_ref.at[place],
            send_sem=bsend.at[shift],
            recv_sem=brecv.at[shift],
            device_id={"context": at_ctx, "tensor": at_ten},
            device_id_type=MESH,
        )

    for shift in range(1, total):
        goes, item = to_head(shift)

        @pl.when(goes)
        def _():
            item.start()

    stay = pltpu.make_async_copy(gpiece.at[my_head], heads_ref.at[place], bloc)
    stay.start()
    u3[...] = dot(att_ref[...].reshape(width, rows), gm_low, ((1,), (0,))).astype(low).reshape(u3.shape)
    out_sum.begin()
    vec_ref[3:4, :] = jnp.sum(grad * normed, axis=0, keepdims=True)
    vec_ref[4:5, :] = jnp.sum(grad, axis=0, keepdims=True)
    vec_ref[5:6, :] = jnp.sum(above, axis=0, keepdims=True)
    vec_ref[6:7, :] = sum_ref[...]
    out_sum.first()
    out_sum.second()
    out_sum.third()
    leave[5].start()
    leave[6].start()
    stay.wait()

    @pl.when(ctx < heads)
    def _():
        for shift in range(1, total):
            source = lax.rem(place + total - shift, total)
            landed = heads_ref.at[source]
            pltpu.make_async_copy(landed, landed, brecv.at[shift]).wait()

    for shift in range(1, total):
        goes, item = to_head(shift)

        @pl.when(goes)
        def _():
            item.wait_send()

    out_sum.reduced()
    for item in leave:
        item.wait()
    for d in range(2):
        for s in range(n - 1):
            block = me - s if d == 0 else me + s

            @pl.when(onward(d) & (block >= 0) & (block < n))
            def _():
                hand_on(d, s, me, True).wait_send()

    for block in range(n):

        @pl.when(me != block)
        def _():
            for c in range(chunks):
                back(jnp.where(me < block, 0, 1), block, c, True).wait_send()

    for d in range(2):
        for s in range(1, n - 1):

            @pl.when(grad_sends(d, s))
            def _():
                grad_on(d, s).wait_send()

    for item in plane:
        item.reduced()


def feed_part(pieces, tokens, out_weight, vectors, up, down, bias, near, cotangent, n, nc, heads, collective_id):
    rows, width = tokens.shape
    wide = up.shape[1]
    chunks = 2
    total = n * rows
    low, f32 = jnp.bfloat16, jnp.float32
    unit = (16, wide // 16, width)
    piece = jax.ShapeDtypeStruct((2,) + unit[1:], low)
    return pl.pallas_call(
        functools.partial(feed_kernel, n, nc, heads, chunks),
        out_shape=(
            jax.ShapeDtypeStruct((total, width), low),
            piece,
            piece,
            jax.ShapeDtypeStruct((rows, width), f32),
            jax.ShapeDtypeStruct((rows, width), f32),
            jax.ShapeDtypeStruct((8, width), f32),
            jax.ShapeDtypeStruct((2, 2, rows // 4, width // 2), low),
            jax.ShapeDtypeStruct(pieces.shape, low),
        ),
        in_specs=[VM, HB, VM, HB, HB, HB, HB, HB, HB, VM, HB],
        out_specs=(HB,) * 7 + (VM,),
        scratch_shapes=[
            pltpu.VMEM((total, width), low),
            pltpu.VMEM(piece.shape, low),
            pltpu.VMEM(piece.shape, low),
            pltpu.VMEM((rows, width), f32),
            pltpu.VMEM((rows, width), f32),
            pltpu.VMEM((8, width), f32),
            pltpu.VMEM((2, 2, rows // 4, width // 2), low),
            pltpu.VMEM(tokens.shape, tokens.dtype),
            pltpu.VMEM((width,), f32),
            pltpu.VMEM((width,), f32),
            pltpu.VMEM((width,), f32),
            pltpu.VMEM((wide,), f32),
            DMA((7,)),
            pltpu.VMEM((rows, width), f32),
            pltpu.VMEM((1, wide), f32),
            pltpu.VMEM((n * heads,) + pieces.shape[1:], low),
            pltpu.VMEM((n * heads,) + pieces.shape[1:], low),
            pltpu.VMEM((n, width // n, width), low),
            DMA((nc * n,)),
            DMA((nc * n,)),
            DMA,
            pltpu.VMEM((rows, width), low),
            pltpu.VMEM(up.shape, low),
            pltpu.VMEM(down.shape, low),
            pltpu.VMEM((total, width), low),
            DMA((7,)),
            DMA((nc * n,)),
            DMA((nc * n,)),
            DMA,
            DMA((2, n - 1)),
            DMA((2, n - 1)),
            DMA((3,)),
            pltpu.VMEM((total, width), low),
            pltpu.VMEM((total, wide), low),
            pltpu.VMEM((total, wide), low),
            pltpu.VMEM((total, width), low),
            pltpu.VMEM((rows, width), f32),
            pltpu.VMEM((2, total, width), low),
            pltpu.VMEM((total, width), low),
            pltpu.VMEM(unit, low),
            pltpu.VMEM(unit, low),
            DMA((2, n - 1)),
            DMA((2, n - 1)),
            DMA,
            DMA((n, chunks)),
            DMA((2, n, chunks)),
        ]
        + PlaneSum.reduce_scratch(unit, low) * 2
        + StripSum.reduce_scratch((n, width // n, width), low),
        compiler_params=remote_params(collective_id, 40),
    )(pieces, tokens, out_weight, *vectors, up, down, bias, near, cotangent)


def last_kernel(n, nc, heads, shared, count, x_ref, w_hbm, h_hbm, a_hbm, feed_hbm, mid_hbm, bias_hbm, *rest):
    ps, rest = rest[:count], rest[count:]
    (token_hbm, gain_hbm, middle_hbm, vec_hbm), rest = rest[:4], rest[4:]
    (out_ref, g_ref, v_ref, po_ref, ao_ref), rest = rest[:5], rest[5:]
    outs, rest = rest[:count], rest[count:]
    (rows_ref, w_ref, h_ref, token_ref, middle_ref, part, sum_ref, u_ref, piece), rest = rest[:9], rest[9:]
    (hsend, hrecv, hloc, win), rest = rest[:4], rest[4:]
    (feed_ref, fsum_ref, mid_ref, bias_ref, gain_ref, vec_ref), rest = rest[:6], rest[6:]
    feed_line = LineScatter(n, feed_ref, fsum_ref, *rest[:4])
    rest = rest[4:]
    chunks = 2
    own = token_ref.shape[0]
    few = own // chunks
    lines = [
        LineScatter(n, part.at[:, pl.ds(c * few, few)], sum_ref.at[pl.ds(c * few, few)], *rest[4 * c : 4 * c + 4])
        for c in range(chunks)
    ]
    rest = rest[4 * chunks :]
    project = StripSum(u_ref, piece, po_ref, rest[:10], rest[10:13])
    rest = rest[13:]
    feeds = [PlaneSum(None, ps[i], outs[i], None, rest[3 * i : 3 * i + 3]) for i in range(count)]
    rest = rest[3 * count :]
    (land, zsend, zrecv, zloc, a_ref), rest = rest[:5], rest[5:]
    (asend, arecv, aloc, now), rest = rest[:4], rest[4:]
    sizes = (n, 2 * nc)
    bufs, sems = rest[:2], rest[2:]
    f32, low = jnp.float32, jnp.bfloat16

    ten, ctx, x = (lax.axis_index(name) for name in ("tensor", "context", "dp"))
    place = ctx * 2 + x
    bar = pltpu.get_barrier_semaphore()
    for shift in range(1, n):
        pl.semaphore_signal(bar, inc=1, device_id={"tensor": lax.rem(ten + shift, n)}, device_id_type=MESH)
    for shift in range(1, 8):
        other = lax.rem(place + shift, 8)
        pl.semaphore_signal(
            bar, inc=1, device_id={"context": lax.div(other, 2), "dp": lax.rem(other, 2)}, device_id_type=MESH
        )
    copies_in = copies(
        (
            (feed_hbm, feed_ref),
            (token_hbm, token_ref),
            (w_hbm, w_ref),
            (h_hbm, h_ref),
            (middle_hbm, middle_ref),
            (mid_hbm, mid_ref),
            (bias_hbm, bias_ref),
            (gain_hbm, gain_ref),
            (vec_hbm, vec_ref),
        ),
        win,
    )
    for item in copies_in:
        item.start()
    pl.semaphore_wait(bar, n + 6)

    half = 2 * own
    far = 1 - lax.div(ten, 2)
    pairs = (far, 1 - far)

    def columns(pair):
        return pl.ds(pl.multiple_of(pair * half, 128), half)

    def ship(index, shift):
        other = lax.rem(ctx + shift, nc)
        return pltpu.make_async_remote_copy(
            src_ref=x_ref.at[other, :, :, columns(pairs[index])],
            dst_ref=rows_ref.at[:, jnp.minimum(ctx, heads - 1), :, columns(pairs[index])],
            send_sem=hsend.at[index, shift],
            recv_sem=hrecv.at[index, shift],
            device_id={"context": other},
            device_id_type=MESH,
        )

    @pl.when(ctx < heads)
    def _():
        for index in range(2):
            for shift in range(1, nc):
                ship(index, shift).start()
        stay = pltpu.make_async_copy(x_ref.at[ctx], rows_ref.at[:, ctx], hloc)
        stay.start()
        stay.wait()

    def across(shift):
        other = lax.rem(ten + shift, n)
        return pltpu.make_async_remote_copy(
            src_ref=a_hbm.at[lax.div(other, 2), lax.rem(other, 2)],
            dst_ref=land.at[ten],
            send_sem=zsend.at[shift],
            recv_sem=zrecv.at[shift],
            device_id={"tensor": other},
            device_id_type=MESH,
        )

    copies_in[0].wait()
    feed_line.begin((0, 1))
    for shift in range(1, n):
        across(shift).start()
    mine = pltpu.make_async_copy(a_hbm.at[lax.div(ten, 2), lax.rem(ten, 2)], land.at[ten], zloc)
    mine.start()
    for item in feeds:
        item.spread1()

    def there(at):
        ctx_, x_ = lax.div(at, 2), lax.rem(at, 2)
        y_ = lax.div(ctx_, 2)
        row_ = jnp.where(ten < n // 2, 2 * x_ + y_, 2 * y_ + x_)
        rows = pl.ds(pl.multiple_of(row_ * a_ref.shape[0], 16), a_ref.shape[0])
        cols = pl.ds(pl.multiple_of(lax.rem(ctx_, 2) * a_ref.shape[1], 128), a_ref.shape[1])
        return ao_ref.at[rows, cols]

    def push(shift):
        other = lax.rem(place + shift, 8)
        return pltpu.make_async_remote_copy(
            src_ref=a_ref,
            dst_ref=there(place),
            send_sem=asend.at[shift],
            recv_sem=arecv.at[shift],
            device_id={"context": lax.div(other, 2), "dp": lax.rem(other, 2)},
            device_id_type=MESH,
        )

    copies_in[1].wait()
    normed, scale = norm_parts(token_ref[...].astype(f32))
    mine.wait()
    for shift in range(1, n):
        source = lax.rem(ten + n - shift, n)
        pltpu.make_async_copy(land.at[source], land.at[source], zrecv.at[shift]).wait()
    value = land[0].astype(f32)
    for at in range(1, n):
        value = value + land[at].astype(f32)
    a_ref[...] = value.astype(low)
    for item in copies_in[2:]:
        item.wait()
    now[0] = vec_ref[...]
    for shift in range(1, 8):
        push(shift).start()
    kept = pltpu.make_async_copy(a_ref, there(place), aloc)
    kept.start()

    def partials(index):
        at = columns(pairs[index])
        for shift in range(1, nc):
            source = lax.rem(ctx + nc - shift, nc)

            @pl.when(source < heads)
            def _():
                ref = rows_ref.at[:, jnp.minimum(source, heads - 1), :, at]
                pltpu.make_async_copy(ref, ref, hrecv.at[index, shift]).wait()

        total = 0.0
        for kind in range(3):
            grads = rows_ref[kind, :, :, at].reshape(heads * HEAD_DIM, half)
            total = total + dot(grads, w_ref[kind], ((0,), (0,)))
        part[pl.ds(2 * pairs[index], 2)] = total.astype(low).reshape(2, own, total.shape[1])

    first = lambda d: (ten < n // 2) if d == 0 else (ten >= n // 2)
    second = lambda d: (ten >= n // 2) if d == 0 else (ten < n // 2)
    feed_line.step(0, first)
    partials(0)
    for line in lines:
        line.begin((0, 1))
    partials(1)
    for line in lines:
        line.begin((2,))
    feed_line.begin((2,))
    for item in feeds:
        item.spread2()
    for line in lines:
        line.step(0, first)
    feed_line.step(1, first)
    feed_line.step(0, second)
    for kind in range(3):
        grads = rows_ref[kind].reshape(heads * HEAD_DIM, n * own)
        u_ref[kind] = dot(grads, h_ref[...], ((1,), (0,))).astype(low)
    project.begin()
    for line in lines:
        line.step(1, first)
    ends = jnp.concatenate(
        [rows_ref[kind].reshape(heads * HEAD_DIM, n * own) for kind in (0, 2)], axis=0
    )
    bias = dot(jnp.ones((8, n * own), low), ends, ((1,), (1,)))
    now[0, 7:8, 0 : bias.shape[1]] = bias[0:1]
    project.first()
    for item in feeds:
        item.spread3()
    project.second()
    for k in range(n - 1):
        for line in lines:
            line.step(k, second)
    feed_line.step(1, second)
    project.third()
    project.spread1()
    for line in lines:
        line.end()
    grad = sum_ref[...]
    now[0, 0:1] = jnp.sum(grad * normed, axis=0, keepdims=True)
    now[0, 1:2] = jnp.sum(grad, axis=0, keepdims=True)
    alone = now[0]

    def where(stage):
        return ten if stage == 0 else place

    def stage_copy(stage, shift):
        other = lax.rem(where(stage) + shift, sizes[stage])
        peer = {"tensor": other} if stage == 0 else {"context": lax.div(other, 2), "dp": lax.rem(other, 2)}
        return pltpu.make_async_remote_copy(
            src_ref=now.at[stage],
            dst_ref=bufs[stage].at[where(stage)],
            send_sem=sems[2 * stage].at[shift],
            recv_sem=sems[2 * stage + 1].at[shift],
            device_id=peer,
            device_id_type=MESH,
        )

    def stage_start(stage):
        for shift in range(1, sizes[stage]):
            stage_copy(stage, shift).start()
        bufs[stage][where(stage)] = now[stage]

    def stage_end(stage):
        buf, size = bufs[stage], sizes[stage]
        for shift in range(1, size):
            source = lax.rem(where(stage) + size - shift, size)
            pltpu.make_async_copy(buf.at[source], buf.at[source], sems[2 * stage + 1].at[shift]).wait()
        total = buf[0]
        for at in range(1, size):
            total = total + buf[at]
        if stage == 0:
            line_ = lax.broadcasted_iota(jnp.int32, total.shape, 0)
            now[1] = jnp.where(line_ < shared, total, alone)
        else:
            v_ref[...] = total

    stage_start(0)
    back = norm_backward(grad, normed, scale, row(gain_ref))
    g_ref[...] = (middle_ref[...] + back).astype(g_ref.dtype)
    project.spread2()
    stage_end(0)
    stage_start(1)
    project.spread3()
    feed_line.end()
    out_ref[...] = (mid_ref[...] + fsum_ref[...] + row(bias_ref)).astype(low)
    kept.wait()
    for shift in range(1, 8):
        source = there(lax.rem(place + 8 - shift, 8))
        pltpu.make_async_copy(source, source, arecv.at[shift]).wait()
    for item in feeds:
        item.everywhere()
    stage_end(1)
    project.everywhere()
    project.reduced()

    @pl.when(ctx < heads)
    def _():
        for index in range(2):
            for shift in range(1, nc):
                ship(index, shift).wait_send()

    for shift in range(1, n):
        across(shift).wait_send()
    for shift in range(1, 8):
        push(shift).wait_send()
    for stage in range(2):
        for shift in range(1, sizes[stage]):
            stage_copy(stage, shift).wait_send()


def last_part(x, weight, hidden, attend_pieces, feed, middle, bias, pieces, tokens, gain, grad_middle, vectors, shared, n, heads, collective_id):
    nc = x.shape[0]
    own, cols = tokens.shape
    count = len(pieces)
    f32, low = jnp.float32, jnp.bfloat16
    whole = lambda item: jax.ShapeDtypeStruct((16,) + item.shape[1:], item.dtype)
    wide, deep = attend_pieces.shape[2:]
    unit = (3, heads * HEAD_DIM, cols)
    result = pl.pallas_call(
        functools.partial(last_kernel, n, nc, heads, shared, count),
        out_shape=(
            jax.ShapeDtypeStruct((own, cols), low),
            jax.ShapeDtypeStruct((own, cols), low),
            jax.ShapeDtypeStruct(vectors.shape, f32),
            jax.ShapeDtypeStruct(unit, low),
            jax.ShapeDtypeStruct((4 * wide, 2 * deep), low),
        )
        + tuple(whole(item) for item in pieces),
        in_specs=[VM] + [HB] * (10 + count),
        out_specs=(VM,) * (5 + count),
        scratch_shapes=[
            pltpu.VMEM((3, heads, HEAD_DIM, n * own), low),
            pltpu.VMEM(weight.shape, low),
            pltpu.VMEM(hidden.shape, low),
            pltpu.VMEM(tokens.shape, low),
            pltpu.VMEM((own, cols), f32),
            pltpu.VMEM((n, own, cols), low),
            pltpu.VMEM((own, cols), f32),
            pltpu.VMEM(unit, low),
            pltpu.VMEM((2, 2, unit[1] // 4, cols // 2), low),
            DMA((2, nc)),
            DMA((2, nc)),
            DMA,
            DMA((9,)),
            pltpu.VMEM((n, own, cols), low),
            pltpu.VMEM((own, cols), f32),
            pltpu.VMEM((own, cols), f32),
            pltpu.VMEM((cols,), f32),
            pltpu.VMEM((cols,), f32),
            pltpu.VMEM(vectors.shape, f32),
        ]
        + LineScatter.scratch(n, own, cols, low)
        + LineScatter.scratch(n, own // 2, cols, low) * 2
        + StripSum.reduce_scratch(unit, low)
        + PlaneSum.spread_scratch()
        + [item for _ in pieces for item in PlaneSum.spread_scratch()]
        + [pltpu.VMEM((n, wide, deep), low), DMA((n,)), DMA((n,)), DMA, pltpu.VMEM((wide, deep), low)]
        + [DMA((8,)), DMA((8,)), DMA, pltpu.VMEM((2,) + vectors.shape, f32)]
        + [pltpu.VMEM((size,) + vectors.shape, f32) for size in (n, 2 * nc)]
        + [DMA((size,)) for size in (n, 2 * nc) for _ in range(2)],
        compiler_params=remote_params(collective_id, 32),
    )(
        x, weight, hidden, attend_pieces, feed.reshape(n, own, cols), middle, bias,
        *pieces, tokens, gain, grad_middle, vectors,
    )
    return result[:5] + (result[5:],)


class LineGather:
    def __init__(self, n, x, o, send, recv):
        self.n, self.x, self.o, self.send, self.recv = n, x, o, send, recv
        self.me = lax.axis_index("tensor")

    def copy(self, d, s):
        me, n = self.me, self.n
        shard = jnp.clip(me - s if d == 0 else me + s, 0, n - 1)
        return pltpu.make_async_remote_copy(
            src_ref=self.x if s == 0 else self.o.at[shard],
            dst_ref=self.o.at[shard],
            send_sem=self.send.at[d, s],
            recv_sem=self.recv.at[d, s],
            device_id={"tensor": jnp.clip(me + 1 if d == 0 else me - 1, 0, n - 1)},
            device_id_type=MESH,
        )

    def sends(self, d, s):
        me, n = self.me, self.n
        return (me - s >= 0) & (me < n - 1) if d == 0 else (me + s < n) & (me > 0)

    def wait(self, d, s):
        me, n = self.me, self.n

        @pl.when(me - 1 - s >= 0 if d == 0 else me + 1 + s < n)
        def _():
            shard = jnp.clip(me - 1 - s if d == 0 else me + 1 + s, 0, n - 1)
            pltpu.make_async_copy(self.o.at[shard], self.o.at[shard], self.recv.at[d, s]).wait()

    def step(self, s):
        for d in range(2):
            if s > 0:
                self.wait(d, s - 1)

            @pl.when(self.sends(d, s))
            def _():
                self.copy(d, s).start()

    def last(self):
        for d in range(2):
            self.wait(d, self.n - 2)

    def finish(self, steps=None):
        for d in range(2):
            for s in range(steps or self.n - 1):

                @pl.when(self.sends(d, s))
                def _():
                    self.copy(d, s).wait_send()


def start_kernel(n, nc, heads, t_hbm, gain_hbm, shift_hbm, full_ref, w_hbm, b_hbm, c_ref, o_hbm, f_ref, q_ref, g_ref, *rest):
    (x_ref, held, proj, w_ref, o_ref, t_ref, gain_ref, shift_ref, b_ref, win), rest = rest[:10], rest[10:]
    arrive = copies(((t_hbm, t_ref), (gain_hbm, gain_ref), (shift_hbm, shift_ref), (b_hbm, b_ref)), win)
    for item in arrive:
        item.start()
    s1, r1, s2, r2, s5, r5, s3, r3, s4, r4, loc = rest
    me, ctx, x = lax.axis_index("tensor"), lax.axis_index("context"), lax.axis_index("dp")
    core, y = lax.rem(ctx, 2), lax.div(ctx, 2)
    rows, width = t_ref.shape
    half = 2 * rows
    bar = pltpu.get_barrier_semaphore()
    met = line_greet(bar, me, n)
    for shift in range(1, nc):
        pl.semaphore_signal(bar, inc=1, device_id={"context": lax.rem(ctx + shift, nc)}, device_id_type=MESH)
    pl.semaphore_signal(bar, inc=1, device_id={"dp": 1 - x}, device_id_type=MESH)
    weight_in = pltpu.make_async_copy(w_hbm, w_ref, loc.at[4])
    weight_in.start()
    for item in arrive:
        item.wait()
    normed, _ = norm_parts(t_ref[...].astype(jnp.float32))
    x_ref[...] = (normed * row(gain_ref) + row(shift_ref)).astype(x_ref.dtype)
    pl.semaphore_wait(bar, met + nc)

    tall, deep = held.shape[1:]
    strip = pl.ds(pl.multiple_of(core * deep, 128), deep)
    piece = full_ref.at[pl.ds(pl.multiple_of((2 * y + x) * tall, 16), tall), strip]
    small = LineGather(n, piece, held, s1, r1)
    large = LineGather(n, x_ref, o_ref, s2, r2)
    grads = LineGather(n, c_ref, g_ref, s5, r5)
    small.step(0)
    large.step(0)
    own = pltpu.make_async_copy(x_ref, o_ref.at[me], loc.at[0])
    own.start()
    mine = pltpu.make_async_copy(piece, held.at[me], loc.at[1])
    mine.start()
    mine.wait()
    own.wait()
    for s in range(1, n - 1):
        small.step(s)
    small.last()

    def there(y_, x_):
        return f_ref.at[:, pl.ds(pl.multiple_of((2 * y_ + x_) * tall, 16), tall), strip]

    x_peer, y_peer = {"dp": 1 - x}, {"context": lax.rem(ctx + 2, 4)}

    def hop(at):
        src, dst, peer = [
            (held, there(y, x), x_peer),
            (held, there(y, x), y_peer),
            (there(y, 1 - x), there(y, 1 - x), y_peer),
            (f_ref.at[:, :, strip], f_ref.at[:, :, strip], {"context": ctx + 1 - 2 * core}),
        ][at]
        return pltpu.make_async_remote_copy(
            src_ref=src,
            dst_ref=dst,
            send_sem=s3.at[at],
            recv_sem=r3.at[at],
            device_id=peer,
            device_id_type=MESH,
        )

    def got(at):
        other = pl.ds(pl.multiple_of((1 - core) * deep, 128), deep)
        ref = [there(y, 1 - x), there(1 - y, x), there(1 - y, 1 - x), f_ref.at[:, :, other]][at]
        pltpu.make_async_copy(ref, ref, r3.at[at]).wait()

    hop(0).start()
    kept = pltpu.make_async_copy(held, there(y, x), loc.at[2])
    kept.start()

    def columns(pair):
        return pl.ds(pl.multiple_of(pair * half, 128), half)

    def project(pair):
        token = jnp.concatenate([o_ref[2 * pair], o_ref[2 * pair + 1]], axis=0)
        for kind in range(3):
            value = dot(w_ref[kind], token, ((1,), (1,))) + b_ref[kind]
            proj[kind, :, :, columns(pair)] = value.astype(proj.dtype).reshape(heads, HEAD_DIM, half)

    def ship(index, pair, shift):
        other = lax.rem(ctx + shift, nc)
        return other, pltpu.make_async_remote_copy(
            src_ref=proj.at[:, jnp.minimum(other, heads - 1), :, columns(pair)],
            dst_ref=q_ref.at[ctx, :, :, columns(pair)],
            send_sem=s4.at[index, shift],
            recv_sem=r4.at[index, shift],
            device_id={"context": other},
            device_id_type=MESH,
        )

    def ship_all(index, pair):
        for shift in range(1, nc):
            other, item = ship(index, pair, shift)

            @pl.when(other < heads)
            def _():
                item.start()

    near = lax.div(me, 2)
    large.step(1)
    weight_in.wait()
    project(near)
    ship_all(0, near)
    hop(1).start()
    for s in range(2, n - 1):
        large.step(s)
    grads.step(0)
    got(0)
    hop(2).start()
    large.last()
    project(1 - near)
    ship_all(1, 1 - near)
    result = pltpu.make_async_copy(o_ref, o_hbm, loc.at[5])
    result.start()
    stay = pltpu.make_async_copy(proj.at[:, jnp.minimum(ctx, heads - 1)], q_ref.at[ctx], loc.at[3])
    stay.start()
    kept.wait()
    got(1)
    got(2)
    hop(3).start()
    stay.wait()

    @pl.when(ctx < heads)
    def _():
        for index in range(2):
            for shift in range(1, nc):
                source = lax.rem(ctx + nc - shift, nc)
                pair = near if index == 0 else 1 - near
                ref = q_ref.at[source, :, :, columns(pair)]
                pltpu.make_async_copy(ref, ref, r4.at[index, shift]).wait()

    got(3)
    for d in range(2):
        grads.wait(d, 0)
    result.wait()
    small.finish()
    large.finish()
    grads.finish(1)
    for at in range(4):
        hop(at).wait_send()
    for index in range(2):
        for shift in range(1, nc):
            other, item = ship(index, near if index == 0 else 1 - near, shift)

            @pl.when(other < heads)
            def _():
                item.wait_send()


def start_part(tokens, gain, shift, w, project_weight, bias, cotangent, n, nc, heads, collective_id):
    rows, cols = tokens.shape
    wide, deep = w.shape
    low = jnp.bfloat16
    full, weight, qkv, grads = pl.pallas_call(
        functools.partial(start_kernel, n, nc, heads),
        out_shape=(
            jax.ShapeDtypeStruct((n, rows, cols), low),
            jax.ShapeDtypeStruct((n, wide, deep), w.dtype),
            jax.ShapeDtypeStruct((nc, 3, HEAD_DIM, n * rows), low),
            jax.ShapeDtypeStruct((n, rows, cols), low),
        ),
        in_specs=[HB] * 7,
        out_specs=(HB, VM, VM, VM),
        scratch_shapes=[
            pltpu.VMEM((rows, cols), low),
            pltpu.VMEM((n, wide // 4, deep // 2), w.dtype),
            pltpu.VMEM((3, heads, HEAD_DIM, n * rows), low),
            pltpu.VMEM(project_weight.shape, low),
            pltpu.VMEM((n, rows, cols), low),
            pltpu.VMEM((rows, cols), tokens.dtype),
            pltpu.VMEM(gain.shape, jnp.float32),
            pltpu.VMEM(shift.shape, jnp.float32),
            pltpu.VMEM(bias.shape, jnp.float32),
            DMA((4,)),
        ]
        + [DMA((2, n - 1)) for _ in range(6)]
        + [DMA((4,)), DMA((4,)), DMA((2, nc)), DMA((2, nc)), DMA((6,))],
        compiler_params=remote_params(collective_id),
    )(tokens, gain, shift, w, project_weight, bias, cotangent)
    return full.reshape(n * rows, cols), weight.reshape(n * wide, deep), qkv, grads


def dot(left, right, dims):
    return lax.dot_general(left, right, ((dims[0], dims[1]), ((), ())), preferred_element_type=jnp.float32)


def key_positions(first, keys, queries):
    return first + lax.broadcasted_iota(jnp.int32, (keys, queries), 0)


def load_rows(qkv_ref, nb, half, qs, kt, ks, vs):
    for block in range(nb):
        part = slice(block % 2 * half, block % 2 * half + half)
        at = block // 2
        qs[block] = qkv_ref[at, 0, :, part] * jnp.asarray(HEAD_DIM**-0.5, qs.dtype)
        item = qkv_ref[at, 1, :, part]
        if kt is not None:
            kt[block] = item
        ks[block] = item.T
        if vs is not None:
            vs[block] = qkv_ref[at, 2, :, part].T


def fill_tables(nb, half, seg_ref, order_ref, slot_ref, low_ref, high_ref):
    for block in range(nb):
        slot_ref[order_ref[block]] = jnp.int32(block)
    first = [seg_ref[0, block * half] for block in range(nb)]
    last = [seg_ref[0, block * half + half - 1] for block in range(nb)]
    for block in range(nb):
        if low_ref is not None:
            low_ref[block] = sum(jnp.where(item < first[block], 1, 0) for item in last)
        if high_ref is not None:
            high_ref[block] = sum(jnp.where(item <= last[block], 1, 0) for item in first)


def forward_kernel(half, heads, seg_s, order_ref, seg_ref, qkv_ref, o_ref, full_ref, lse_ref, start_ref, qs, ks, slot_ref, low_ref):
    nb = full_ref.shape[0]

    @pl.when(lax.axis_index("context") < heads)
    def _():
        load_rows(qkv_ref, nb, half, qs, None, ks, None)
        fill_tables(nb, half, seg_s, order_ref, slot_ref, low_ref, None)
        seg = seg_ref[...]
        start = jnp.zeros(seg.shape, jnp.float32)
        for doc in range(1, DOC_LIMIT):
            before = jnp.sum(jnp.where(seg < doc, 1.0, 0.0), axis=1, keepdims=True)
            start = jnp.where(seg == doc, before, start)
        start_ref[...] = start.astype(jnp.int32)

        @pl.loop(0, nb)
        def _(nq):
            slot = slot_ref[nq]
            query = qs[slot]
            begin = start_ref[:, pl.ds(pl.multiple_of(nq * half, 128), half)]
            here = nq * half + lax.broadcasted_iota(jnp.int32, (1, half), 1)

            def step(nk, state):
                top, total, acc = state
                at = slot_ref[nk]
                score = dot(ks[at], query, ((1,), (0,)))
                place = key_positions(nk * half, half, half)
                score = jnp.where((place >= begin) & (place <= here), score, NEG_FILL)
                new_top = jnp.maximum(top, jnp.max(score, axis=0, keepdims=True))
                factor = jnp.exp(top - new_top)
                weight = jnp.exp(score - new_top)
                total = total * factor + jnp.sum(weight, axis=0, keepdims=True)
                value = qkv_ref[at // 2, 2, :, pl.ds(pl.multiple_of(at % 2 * half, 128), half)]
                acc = acc * factor + dot(value, weight.astype(jnp.bfloat16), ((1,), (0,)))
                return new_top, total, acc

            top, total, acc = lax.fori_loop(
                low_ref[nq],
                nq + 1,
                step,
                (
                    jnp.full((1, half), NEG_FILL, jnp.float32),
                    jnp.zeros((1, half), jnp.float32),
                    jnp.zeros((HEAD_DIM, half), jnp.float32),
                ),
            )
            result = acc / total
            full_ref[slot] = result
            lse_ref[slot] = top + jnp.log(total)
            low = result.astype(jnp.bfloat16)
            o_ref[2 * slot] = low[:, : half // 2]
            o_ref[2 * slot + 1] = low[:, half // 2 :]


def attend_forward(qkv, segments, order, half, heads):
    nc = qkv.shape[0]
    nb = 2 * nc
    return pl.pallas_call(
        functools.partial(forward_kernel, half, heads),
        out_shape=(
            jax.ShapeDtypeStruct((2 * nb, HEAD_DIM, half // 2), jnp.bfloat16),
            jax.ShapeDtypeStruct((nb, HEAD_DIM, half), jnp.float32),
            jax.ShapeDtypeStruct((nb, 1, half), jnp.float32),
            jax.ShapeDtypeStruct(segments.shape, jnp.int32),
        ),
        in_specs=[SM, SM, VM, VM],
        out_specs=(VM, VM, VM, VM),
        scratch_shapes=[
            pltpu.VMEM((nb, HEAD_DIM, half), jnp.bfloat16),
            pltpu.VMEM((nb, half, HEAD_DIM), jnp.bfloat16),
            pltpu.SMEM((nb,), jnp.int32),
            pltpu.SMEM((nb,), jnp.int32),
        ],
        compiler_params=pltpu.CompilerParams(vmem_limit_bytes=24 << 20),
    )(segments, order, segments, qkv)


def backward_kernel(
    half, heads, seg_s, order_ref, start_ref, qkv_ref, full_ref, lse_ref, grad_ref, o_ref,
    qs, kt, ks, vs, gs, ds, dq, slot_ref, high_ref,
):
    nb = full_ref.shape[0]

    @pl.when(lax.axis_index("context") < heads)
    def _():
        load_rows(qkv_ref, nb, half, qs, kt, ks, vs)
        fill_tables(nb, half, seg_s, order_ref, slot_ref, None, high_ref)
        for block in range(nb):
            both = jnp.concatenate([grad_ref[2 * block], grad_ref[2 * block + 1]], axis=1)
            gs[block] = both
            ds[block] = jnp.sum(both.astype(jnp.float32) * full_ref[block], axis=0, keepdims=True)
            dq[block] = jnp.zeros((HEAD_DIM, half), jnp.float32)

        @pl.loop(0, nb)
        def _(nk):
            at = slot_ref[nk]
            place = key_positions(nk * half, half, half)

            def step(nq, state):
                grad_key, grad_value = state
                slot = slot_ref[nq]
                query, grad = qs[slot], gs[slot]
                begin = start_ref[:, pl.ds(pl.multiple_of(nq * half, 128), half)]
                here = nq * half + lax.broadcasted_iota(jnp.int32, (1, half), 1)
                score = dot(ks[at], query, ((1,), (0,)))
                score = jnp.where((place >= begin) & (place <= here), score, NEG_FILL)
                weight = jnp.exp(score - lse_ref[slot])
                grad_weight = dot(vs[at], grad, ((1,), (0,)))
                grad_score = (weight * (grad_weight - ds[slot])).astype(jnp.bfloat16)
                grad_value = grad_value + dot(grad, weight.astype(jnp.bfloat16), ((1,), (1,)))
                grad_key = grad_key + dot(query, grad_score, ((1,), (1,)))
                dq[slot] += dot(kt[at], grad_score, ((1,), (0,)))
                return grad_key, grad_value

            zero = jnp.zeros((HEAD_DIM, half), jnp.float32)
            grad_key, grad_value = lax.fori_loop(nk, high_ref[nk], step, (zero, zero))
            columns = pl.ds(pl.multiple_of(at % 2 * half, 128), half)
            o_ref[at // 2, 1, :, columns] = grad_key.astype(jnp.bfloat16)
            o_ref[at // 2, 2, :, columns] = grad_value.astype(jnp.bfloat16)

        for block in range(nb):
            part = slice(block % 2 * half, block % 2 * half + half)
            o_ref[block // 2, 0, :, part] = (dq[block] * HEAD_DIM**-0.5).astype(jnp.bfloat16)


def attend_backward(qkv, segments, order, start, full, lse, grad, half, heads):
    nc = qkv.shape[0]
    nb = 2 * nc
    low = jnp.bfloat16
    return pl.pallas_call(
        functools.partial(backward_kernel, half, heads),
        out_shape=jax.ShapeDtypeStruct(qkv.shape, low),
        in_specs=[SM, SM, VM, VM, VM, VM, VM],
        out_specs=VM,
        scratch_shapes=[
            pltpu.VMEM((nb, HEAD_DIM, half), low),
            pltpu.VMEM((nb, HEAD_DIM, half), low),
            pltpu.VMEM((nb, half, HEAD_DIM), low),
            pltpu.VMEM((nb, half, HEAD_DIM), low),
            pltpu.VMEM((nb, HEAD_DIM, half), low),
            pltpu.VMEM((nb, 1, half), jnp.float32),
            pltpu.VMEM((nb, HEAD_DIM, half), jnp.float32),
            pltpu.SMEM((nb,), jnp.int32),
            pltpu.SMEM((nb,), jnp.int32),
        ],
        compiler_params=pltpu.CompilerParams(vmem_limit_bytes=24 << 20),
    )(segments, order, start, qkv, full, lse, grad)


def norm_parts(values):
    centre = jnp.mean(values, axis=-1, keepdims=True)
    shifted = values - centre
    spread_ = jnp.mean(shifted * shifted, axis=-1, keepdims=True)
    scale = lax.rsqrt(spread_ + NORM_EPS)
    return shifted * scale, scale


def norm_backward(grad, normed, scale, gain):
    e = grad * gain
    mean_e = jnp.mean(e, axis=-1, keepdims=True)
    mean_en = jnp.mean(e * normed, axis=-1, keepdims=True)
    return (e - mean_e - normed * mean_en) * scale


def gelu_tanh(values):
    return jax.nn.gelu(values, approximate=True)


def cross_rows(left, right):
    return lax.dot_general(
        left, right, (((0,), (0,)), ((), ())), preferred_element_type=jnp.float32
    )


def after(value, done):
    return lax.optimization_barrier((value, done))[0]


def per_device(
    mesh_sizes,
    inputs,
    first_gain,
    first_shift,
    project_weight,
    project_bias,
    attend_weight,
    attend_bias,
    second_gain,
    second_shift,
    expand_weight,
    expand_bias,
    shrink_weight,
    shrink_bias,
    segments,
    block_order,
    cotangent,
):
    nt, nc = mesh_sizes["tensor"], mesh_sizes["context"]
    own_rows, width = inputs.shape[1], inputs.shape[2]
    local_width = project_weight.shape[2]
    heads = local_width // HEAD_DIM
    block_rows = own_rows * nt
    half = block_rows // 2
    low = jnp.bfloat16
    f32 = lambda value: value.astype(jnp.float32)
    square = nt == 4 and nc == 4 and mesh_sizes["dp"] == 2
    plane = ("context", "dp")

    tokens_own = f32(inputs[0])
    grad_out = cotangent[0]
    bias = jnp.stack([project_bias[0], jnp.zeros_like(project_bias[0]), project_bias[1]])[:, :, None]
    weight_rows = project_weight.transpose(0, 2, 1)
    if square:
        hidden1_full, attend_full, qkv, grads_near = start_part(
            inputs[0], first_gain, first_shift, attend_weight, weight_rows, bias, grad_out, nt, nc, heads, 0
        )
        pieces, attended_full, lse, start = attend_forward(qkv, segments, block_order, half, heads)
        feed, *feed_pieces, middle, grad_middle, vectors, attend_pieces, grad_heads = feed_part(
            pieces,
            inputs[0],
            attend_full,
            (attend_bias, second_gain, second_shift),
            expand_weight,
            shrink_weight,
            expand_bias,
            grads_near,
            grad_out,
            nt,
            nc,
            heads,
            3,
        )
        grad_qkv = attend_backward(
            qkv, segments, block_order, start, attended_full, lse, grad_heads, half, heads
        )
        outputs, grad_inputs, summed, grad_project, grad_attend, feeds = last_part(
            grad_qkv,
            weight_rows,
            hidden1_full,
            attend_pieces,
            feed,
            middle,
            shrink_bias,
            feed_pieces,
            inputs[0],
            first_gain,
            grad_middle,
            vectors,
            6,
            nt,
            heads,
            7,
        )
        grad_project = grad_project.transpose(0, 2, 1)
        grad_shrink, grad_expand = feeds[0].reshape(-1, width), feeds[1].reshape(width, -1)
        wide = expand_bias.shape[0]
    else:
        hidden1 = norm_parts(tokens_own)[0] * first_gain + first_shift
        hidden1_full = gather_rows(hidden1.astype(low), nt, 0)
        attend_full = lax.all_gather(attend_weight, "tensor", axis=0, tiled=True)
        projected = jnp.einsum(
            "ked,rd->ker", weight_rows, hidden1_full, preferred_element_type=jnp.float32
        )
        projected = (projected + bias).astype(low).reshape(3, heads, HEAD_DIM, block_rows)
        qkv = to_heads(projected, nc, 1)
        pieces, attended_full, lse, start = attend_forward(qkv, segments, block_order, half, heads)
        grad_full = lax.all_gather(grad_out, "tensor", axis=0, tiled=True)
        attended = to_rows(pieces, nc, nt, heads, 2).reshape(width, own_rows)
        middle = tokens_own + cross_rows(attended, attend_full) + attend_bias
        normed2, scale2 = norm_parts(middle)
        hidden2 = (normed2 * second_gain + second_shift).astype(low)
        hidden2_full = gather_rows(hidden2, nt, 3)
        pre_act = jnp.dot(hidden2_full, expand_weight, preferred_element_type=jnp.float32) + expand_bias
        activ = gelu_tanh(pre_act).astype(low)
        grad_act = dot(grad_full, shrink_weight, ((1,), (1,)))
        grad_pre = jax.vjp(gelu_tanh, pre_act)[1](grad_act)[0].astype(low)
        grad_shrink = cross_rows(activ, grad_full).astype(low)
        grad_expand = cross_rows(hidden2_full, grad_pre).astype(low)
        grad_hidden2 = scatter_rows(dot(grad_pre, expand_weight, ((1,), (1,))).astype(low), nt, 4)
        grad_expand_bias = jnp.sum(f32(grad_pre), axis=0)
        feed = jnp.dot(activ, shrink_weight, preferred_element_type=jnp.float32).astype(low)

        grad_shrink_bias = jnp.sum(f32(grad_out), axis=0)
        grad_second_gain = jnp.sum(grad_hidden2 * normed2, axis=0)
        grad_second_shift = jnp.sum(grad_hidden2, axis=0)
        grad_middle = f32(grad_out) + norm_backward(grad_hidden2, normed2, scale2, second_gain)
        grad_middle_low = grad_middle.astype(low)
        grad_attend_bias = jnp.sum(f32(grad_middle_low), axis=0)
        grad_attended = dot(attend_full, grad_middle_low, ((1,), (1,))).astype(low)
        grad_attended = grad_attended.reshape(nt * heads, HEAD_DIM, own_rows)
        grad_attend = jnp.dot(attended, grad_middle_low, preferred_element_type=jnp.float32).astype(low)
        grad_heads = rows_back(grad_attended, nc, nt, heads, 5)
        feed_sum = lax.psum_scatter(after(feed, grad_heads), "tensor", scatter_dimension=0, tiled=True)

        grad_qkv = attend_backward(
            qkv, segments, block_order, start, attended_full, lse, grad_heads, half, heads
        )
        grad_rows = from_heads(grad_qkv, nc, heads, 6).reshape(3 * local_width, block_rows)
        grad_project = dot(hidden1_full, grad_rows, ((0,), (1,))).astype(low)
        grad_hidden1 = cross_rows(grad_rows, weight_rows.reshape(3 * local_width, width)).astype(low)
        row_sums = jnp.sum(f32(grad_rows), axis=1)
        grad_project_bias = jnp.concatenate([row_sums[:local_width], row_sums[2 * local_width :]])
        grad_hidden1 = scatter_rows(grad_hidden1, nt, 7)
        normed1, scale1 = norm_parts(tokens_own)
        back = norm_backward(grad_hidden1, normed1, scale1, first_gain)
        grad_inputs = (grad_middle + back).astype(low)
        wide = grad_expand_bias.shape[0]
        vectors = jnp.concatenate(
            [
                jnp.sum(grad_hidden1 * normed1, axis=0),
                jnp.sum(grad_hidden1, axis=0),
                grad_attend_bias,
                grad_second_gain,
                grad_second_shift,
                grad_shrink_bias,
                grad_expand_bias,
                jnp.pad(grad_project_bias, (0, -(wide + 2 * local_width) % width)),
            ]
        ).reshape(-1, width)
        summed = sum_vectors(vectors, 6, mesh_sizes, 8)
        grad_attend = lax.psum_scatter(grad_attend, "tensor", scatter_dimension=0, tiled=True)
        grad_project, grad_attend, grad_shrink, grad_expand = lax.psum(
            (grad_project, grad_attend, grad_shrink, grad_expand), plane
        )
        grad_project = jnp.stack(
            [grad_project[:, at * local_width : (at + 1) * local_width] for at in range(3)]
        )
        outputs = (middle + f32(feed_sum) + shrink_bias).astype(low)
    tail = summed[6:].reshape(-1)
    return (
        outputs[None],
        grad_inputs[None],
        summed[0],
        summed[1],
        f32(grad_project),
        tail[wide : wide + 2 * local_width].reshape(2, local_width),
        f32(grad_attend),
        summed[2],
        summed[3],
        summed[4],
        f32(grad_expand),
        tail[:wide],
        f32(grad_shrink),
        summed[5],
    )


def solution(mesh):
    rows = P("dp", ("context", "tensor"), None)
    in_specs = (
        rows,
        P(),
        P(),
        P(None, None, "tensor"),
        P(None, "tensor"),
        P("tensor", None),
        P(),
        P(),
        P(),
        P(None, "tensor"),
        P("tensor"),
        P("tensor", None),
        P(),
        P("dp", None),
        P(),
        rows,
    )
    out_specs = (
        rows,
        rows,
        P(),
        P(),
        P(None, None, "tensor"),
        P(None, "tensor"),
        P("tensor", None),
        P(),
        P(),
        P(),
        P(None, "tensor"),
        P("tensor"),
        P("tensor", None),
        P(),
    )
    return jax.shard_map(
        functools.partial(per_device, dict(mesh.shape)),
        mesh=mesh,
        in_specs=in_specs,
        out_specs=out_specs,
        check_vma=False,
    )
```

```python
import functools

import jax
import jax.numpy as jnp
from jax import lax
from jax.experimental import pallas as pl
from jax.experimental.pallas import tpu as pltpu
from jax.sharding import PartitionSpec as P

HEAD_DIM = 64
NEG_FILL = -1e30
NORM_EPS = 1e-05
DOC_LIMIT = 16
MESH = pl.DeviceIdType.MESH
VM = pl.BlockSpec(memory_space=pltpu.VMEM)
SM = pl.BlockSpec(memory_space=pltpu.SMEM)
DMA = pltpu.SemaphoreType.DMA


def remote_params(collective_id, mib=16):
    return pltpu.CompilerParams(
        collective_id=collective_id, has_side_effects=True, vmem_limit_bytes=mib << 20
    )


HB = pl.BlockSpec(memory_space=pltpu.HBM)


def copies(pairs, sems):
    return [pltpu.make_async_copy(src, dst, sems.at[at]) for at, (src, dst) in enumerate(pairs)]


def row(ref):
    return ref[...].reshape(1, -1)


def line_barrier(me, n):
    bar = pltpu.get_barrier_semaphore()

    @pl.when(me > 0)
    def _():
        pl.semaphore_signal(bar, inc=1, device_id={"tensor": me - 1}, device_id_type=MESH)

    @pl.when(me < n - 1)
    def _():
        pl.semaphore_signal(bar, inc=1, device_id={"tensor": me + 1}, device_id_type=MESH)

    pl.semaphore_wait(bar, jnp.where(me > 0, 1, 0) + jnp.where(me < n - 1, 1, 0))


def gather_kernel(n, x_ref, o_ref, send, recv, loc):
    me = lax.axis_index("tensor")
    line_barrier(me, n)
    own = pltpu.make_async_copy(x_ref, o_ref.at[me], loc)
    own.start()

    def copy(d, s):
        shard = jnp.clip(me - s if d == 0 else me + s, 0, n - 1)
        return pltpu.make_async_remote_copy(
            src_ref=x_ref if s == 0 else o_ref.at[shard],
            dst_ref=o_ref.at[shard],
            send_sem=send.at[d, s],
            recv_sem=recv.at[d, s],
            device_id={"tensor": jnp.clip(me + 1 if d == 0 else me - 1, 0, n - 1)},
            device_id_type=MESH,
        )

    def sends(d, s):
        return (me - s >= 0) & (me < n - 1) if d == 0 else (me + s < n) & (me > 0)

    def gets(d, s):
        return me - 1 - s >= 0 if d == 0 else me + 1 + s < n

    def landed(d, s):
        shard = jnp.clip(me - 1 - s if d == 0 else me + 1 + s, 0, n - 1)
        return pltpu.make_async_copy(o_ref.at[shard], o_ref.at[shard], recv.at[d, s])

    for s in range(n - 1):
        for d in range(2):
            if s > 0:

                @pl.when(gets(d, s - 1))
                def _():
                    landed(d, s - 1).wait()

            @pl.when(sends(d, s))
            def _():
                copy(d, s).start()

    for d in range(2):

        @pl.when(gets(d, n - 2))
        def _():
            landed(d, n - 2).wait()

        for s in range(n - 1):

            @pl.when(sends(d, s))
            def _():
                copy(d, s).wait_send()

    own.wait()


def gather_rows(x, n, collective_id):
    rows, cols = x.shape
    return pl.pallas_call(
        functools.partial(gather_kernel, n),
        out_shape=jax.ShapeDtypeStruct((n, rows, cols), x.dtype),
        in_specs=[VM],
        out_specs=VM,
        scratch_shapes=[DMA((2, n - 1)), DMA((2, n - 1)), DMA],
        compiler_params=remote_params(collective_id),
    )(x).reshape(n * rows, cols)


def scatter_kernel(n, x_ref, o_ref, buf, tmp, send, recv):
    me = lax.axis_index("tensor")
    line_barrier(me, n)

    def term(d, k):
        return n - 1 - k if d == 0 else k

    def sends(d, k):
        return me < n - 1 - k if d == 0 else me > k

    def behind(d):
        return me > 0 if d == 0 else me < n - 1

    def copy(d, k, first):
        return pltpu.make_async_remote_copy(
            src_ref=x_ref.at[term(d, k)] if first else tmp.at[d, k],
            dst_ref=buf.at[d, k],
            send_sem=send.at[d, k],
            recv_sem=recv.at[d, k],
            device_id={"tensor": jnp.clip(me + 1 if d == 0 else me - 1, 0, n - 1)},
            device_id_type=MESH,
        )

    def landed(d, k):
        return pltpu.make_async_copy(buf.at[d, k], buf.at[d, k], recv.at[d, k])

    for d in range(2):

        @pl.when(jnp.logical_not(behind(d)))
        def _():
            for k in range(n - 1):
                copy(d, k, True).start()

    for k in range(n - 1):
        for d in range(2):

            @pl.when(behind(d) & sends(d, k))
            def _():
                landed(d, k).wait()
                both = buf[d, k].astype(jnp.float32) + x_ref[term(d, k)].astype(jnp.float32)
                tmp[d, k] = both.astype(tmp.dtype)
                copy(d, k, False).start()

    o_ref[...] = x_ref[me].astype(jnp.float32)
    for d in range(2):
        for k in range(n - 1):

            @pl.when(behind(d) & (me == term(d, k)))
            def _():
                landed(d, k).wait()
                o_ref[...] += buf[d, k].astype(jnp.float32)

    for d in range(2):
        for k in range(n - 1):

            @pl.when(sends(d, k))
            def _():
                copy(d, k, False).wait_send()


def scatter_rows(x, n, collective_id):
    rows, cols = x.shape
    own = rows // n
    return pl.pallas_call(
        functools.partial(scatter_kernel, n),
        out_shape=jax.ShapeDtypeStruct((own, cols), jnp.float32),
        in_specs=[VM],
        out_specs=VM,
        scratch_shapes=[
            pltpu.VMEM((2, n - 1, own, cols), x.dtype),
            pltpu.VMEM((2, n - 1, own, cols), x.dtype),
            DMA((2, n - 1)),
            DMA((2, n - 1)),
        ],
        compiler_params=remote_params(collective_id),
    )(x.reshape(n, own, cols))


def group_barrier(axes, sizes):
    mine = [lax.axis_index(name) for name in axes]
    place = sum_index(mine, sizes)
    total = 1
    for size in sizes:
        total *= size
    bar = pltpu.get_barrier_semaphore()
    for shift in range(1, total):
        other = lax.rem(place + shift, total)
        pl.semaphore_signal(bar, inc=1, device_id=spread(other, axes, sizes), device_id_type=MESH)
    pl.semaphore_wait(bar, total - 1)
    return place, total


def sum_index(mine, sizes):
    place = 0
    for at, size in zip(mine, sizes):
        place = place * size + at
    return place


def spread(place, axes, sizes):
    found = {}
    for name, size in reversed(tuple(zip(axes, sizes))):
        found[name] = lax.rem(place, size)
        place = lax.div(place, size)
    return found


def to_heads_kernel(nc, heads, x_ref, o_ref, send, recv, loc):
    me, _ = group_barrier(("context",), (nc,))

    def copy(shift):
        other = lax.rem(me + shift, nc)
        return other, pltpu.make_async_remote_copy(
            src_ref=x_ref.at[:, jnp.minimum(other, heads - 1)],
            dst_ref=o_ref.at[me],
            send_sem=send.at[shift],
            recv_sem=recv.at[shift],
            device_id={"context": other},
            device_id_type=MESH,
        )

    for shift in range(1, nc):
        other, item = copy(shift)

        @pl.when(other < heads)
        def _():
            item.start()

    own = pltpu.make_async_copy(x_ref.at[:, jnp.minimum(me, heads - 1)], o_ref.at[me], loc)
    own.start()
    own.wait()

    @pl.when(me < heads)
    def _():
        for shift in range(1, nc):
            source = lax.rem(me + nc - shift, nc)
            pltpu.make_async_copy(o_ref.at[source], o_ref.at[source], recv.at[shift]).wait()

    for shift in range(1, nc):
        other, item = copy(shift)

        @pl.when(other < heads)
        def _():
            item.wait_send()


def to_heads(x, nc, collective_id):
    heads = x.shape[1]
    return pl.pallas_call(
        functools.partial(to_heads_kernel, nc, heads),
        out_shape=jax.ShapeDtypeStruct((nc, x.shape[0]) + x.shape[2:], x.dtype),
        in_specs=[VM],
        out_specs=VM,
        scratch_shapes=[DMA((nc,)), DMA((nc,)), DMA],
        compiler_params=remote_params(collective_id),
    )(x)


def from_heads_kernel(nc, heads, x_ref, o_ref, send, recv, loc):
    me, _ = group_barrier(("context",), (nc,))

    def copy(shift):
        other = lax.rem(me + shift, nc)
        return pltpu.make_async_remote_copy(
            src_ref=x_ref.at[other],
            dst_ref=o_ref.at[:, jnp.minimum(me, heads - 1)],
            send_sem=send.at[shift],
            recv_sem=recv.at[shift],
            device_id={"context": other},
            device_id_type=MESH,
        )

    @pl.when(me < heads)
    def _():
        for shift in range(1, nc):
            copy(shift).start()
        own = pltpu.make_async_copy(x_ref.at[me], o_ref.at[:, me], loc)
        own.start()
        own.wait()

    for shift in range(1, nc):
        source = lax.rem(me + nc - shift, nc)

        @pl.when(source < heads)
        def _():
            at = jnp.minimum(source, heads - 1)
            pltpu.make_async_copy(o_ref.at[:, at], o_ref.at[:, at], recv.at[shift]).wait()

    @pl.when(me < heads)
    def _():
        for shift in range(1, nc):
            copy(shift).wait_send()


def from_heads(x, nc, heads, collective_id):
    return pl.pallas_call(
        functools.partial(from_heads_kernel, nc, heads),
        out_shape=jax.ShapeDtypeStruct((x.shape[1], heads) + x.shape[2:], x.dtype),
        in_specs=[VM],
        out_specs=VM,
        scratch_shapes=[DMA((nc,)), DMA((nc,)), DMA],
        compiler_params=remote_params(collective_id),
    )(x)


AXES = ("context", "tensor")


def rows_kernel(nc, nt, heads, x_ref, o_ref, send, recv, loc):
    me, total = group_barrier(AXES, (nc, nt))
    my_ctx, my_ten = lax.axis_index("context"), lax.axis_index("tensor")
    my_head = my_ten * heads + jnp.minimum(my_ctx, heads - 1)

    def copy(shift):
        other = lax.rem(me + shift, total)
        return pltpu.make_async_remote_copy(
            src_ref=x_ref.at[other],
            dst_ref=o_ref.at[my_head],
            send_sem=send.at[shift],
            recv_sem=recv.at[shift],
            device_id=spread(other, AXES, (nc, nt)),
            device_id_type=MESH,
        )

    @pl.when(my_ctx < heads)
    def _():
        for shift in range(1, total):
            copy(shift).start()
        own = pltpu.make_async_copy(x_ref.at[me], o_ref.at[my_head], loc)
        own.start()
        own.wait()

    for shift in range(1, total):
        source = lax.rem(me + total - shift, total)
        ctx, ten = lax.div(source, nt), lax.rem(source, nt)

        @pl.when(ctx < heads)
        def _():
            at = ten * heads + jnp.minimum(ctx, heads - 1)
            pltpu.make_async_copy(o_ref.at[at], o_ref.at[at], recv.at[shift]).wait()

    @pl.when(my_ctx < heads)
    def _():
        for shift in range(1, total):
            copy(shift).wait_send()


def to_rows(x, nc, nt, heads, collective_id):
    total = nc * nt
    return pl.pallas_call(
        functools.partial(rows_kernel, nc, nt, heads),
        out_shape=jax.ShapeDtypeStruct((nt * heads,) + x.shape[1:], x.dtype),
        in_specs=[VM],
        out_specs=VM,
        scratch_shapes=[DMA((total,)), DMA((total,)), DMA],
        compiler_params=remote_params(collective_id),
    )(x)


def rows_back_kernel(nc, nt, heads, x_ref, o_ref, send, recv, loc):
    me, total = group_barrier(AXES, (nc, nt))
    my_ctx, my_ten = lax.axis_index("context"), lax.axis_index("tensor")

    def copy(shift):
        other = lax.rem(me + shift, total)
        ctx, ten = lax.div(other, nt), lax.rem(other, nt)
        return ctx < heads, pltpu.make_async_remote_copy(
            src_ref=x_ref.at[ten * heads + jnp.minimum(ctx, heads - 1)],
            dst_ref=o_ref.at[me],
            send_sem=send.at[shift],
            recv_sem=recv.at[shift],
            device_id={"context": ctx, "tensor": ten},
            device_id_type=MESH,
        )

    for shift in range(1, total):
        goes, item = copy(shift)

        @pl.when(goes)
        def _():
            item.start()

    own = pltpu.make_async_copy(
        x_ref.at[my_ten * heads + jnp.minimum(my_ctx, heads - 1)], o_ref.at[me], loc
    )
    own.start()
    own.wait()

    @pl.when(my_ctx < heads)
    def _():
        for shift in range(1, total):
            source = lax.rem(me + total - shift, total)
            pltpu.make_async_copy(o_ref.at[source], o_ref.at[source], recv.at[shift]).wait()

    for shift in range(1, total):
        goes, item = copy(shift)

        @pl.when(goes)
        def _():
            item.wait_send()


def rows_back(x, nc, nt, heads, collective_id):
    total = nc * nt
    return pl.pallas_call(
        functools.partial(rows_back_kernel, nc, nt, heads),
        out_shape=jax.ShapeDtypeStruct((total,) + x.shape[1:], x.dtype),
        in_specs=[VM],
        out_specs=VM,
        scratch_shapes=[DMA((total,)), DMA((total,)), DMA],
        compiler_params=remote_params(collective_id),
    )(x)


def vectors_kernel(names, sizes, shared, x_ref, o_ref, now, *rest):
    bufs, sems = rest[: len(names)], rest[len(names) :]
    bar = pltpu.get_barrier_semaphore()
    for name, size in zip(names, sizes):
        me = lax.axis_index(name)
        for shift in range(1, size):
            pl.semaphore_signal(
                bar, inc=1, device_id={name: lax.rem(me + shift, size)}, device_id_type=MESH
            )
    pl.semaphore_wait(bar, sum(sizes) - len(sizes))
    for stage, (name, size) in enumerate(zip(names, sizes)):
        buf, send, recv = bufs[stage], sems[2 * stage], sems[2 * stage + 1]
        me = lax.axis_index(name)

        def copy(shift):
            return pltpu.make_async_remote_copy(
                src_ref=now.at[stage] if stage else x_ref.at[0],
                dst_ref=buf.at[me],
                send_sem=send.at[shift],
                recv_sem=recv.at[shift],
                device_id={name: lax.rem(me + shift, size)},
                device_id_type=MESH,
            )

        for shift in range(1, size):
            copy(shift).start()
        buf[me] = now[stage] if stage else x_ref[0]
        for shift in range(1, size):
            source = lax.rem(me + size - shift, size)
            pltpu.make_async_copy(buf.at[source], buf.at[source], recv.at[shift]).wait()
        total = buf[0]
        for at in range(1, size):
            total = total + buf[at]
        if stage == 0:
            row = lax.broadcasted_iota(jnp.int32, total.shape, 0)
            total = jnp.where(row < shared, total, x_ref[0])
        if stage + 1 < len(names):
            now[stage + 1] = total
        else:
            o_ref[...] = total
        for shift in range(1, size):
            copy(shift).wait_send()


def sum_vectors(rows, shared, mesh_sizes, collective_id):
    names = ("tensor", "context", "dp")
    sizes = tuple(mesh_sizes[name] for name in names)
    shape = rows.shape
    return pl.pallas_call(
        functools.partial(vectors_kernel, names, sizes, shared),
        out_shape=jax.ShapeDtypeStruct(shape, jnp.float32),
        in_specs=[VM],
        out_specs=VM,
        scratch_shapes=[pltpu.VMEM((len(names),) + shape, jnp.float32)]
        + [pltpu.VMEM((size,) + shape, jnp.float32) for size in sizes]
        + [DMA((size,)) for size in sizes for _ in range(2)],
        compiler_params=remote_params(collective_id),
    )(rows[None])


class PlaneSum:
    def __init__(self, u, p, o, bufs=None, spread=None):
        self.u, self.p, self.o = u, p, o
        if bufs is not None:
            self.rc, self.s1, self.ra, self.rb, self.sa, self.sb, self.ta, self.tb = bufs[:8]
            self.send1, self.recv1 = bufs[8:]
        if spread is not None:
            self.send2, self.recv2, self.loc = spread
        ctx, self.x = lax.axis_index("context"), lax.axis_index("dp")
        self.core, self.y = lax.rem(ctx, 2), lax.div(ctx, 2)
        self.chip_peer = {"context": ctx + 1 - 2 * self.core}
        self.y_peer = {"context": lax.rem(ctx + 2, 4)}
        self.x_peer = {"dp": 1 - self.x}

    @staticmethod
    def reduce_scratch(shape, dtype):
        tail = tuple(shape[1:])
        bufs = [pltpu.VMEM((count,) + tail, dtype) for count in (8, 8, 2, 2, 2, 2, 1, 1)]
        return bufs + [DMA((5,)), DMA((5,))]

    @staticmethod
    def spread_scratch():
        return [DMA((5,)), DMA((5,)), DMA((2,))]

    @staticmethod
    def greet(bar):
        ctx, x = lax.axis_index("context"), lax.axis_index("dp")
        for peer in (
            {"context": ctx + 1 - 2 * lax.rem(ctx, 2)},
            {"context": lax.rem(ctx + 2, 4)},
            {"dp": 1 - x},
        ):
            pl.semaphore_signal(bar, inc=1, device_id=peer, device_id_type=MESH)
        return 3

    def copy(self, at, src, dst, peer):
        send, recv = (self.send1, self.recv1) if at < 5 else (self.send2, self.recv2)
        return pltpu.make_async_remote_copy(
            src_ref=src,
            dst_ref=dst,
            send_sem=send.at[at % 5],
            recv_sem=recv.at[at % 5],
            device_id=peer,
            device_id_type=MESH,
        )

    def got(self, at, ref):
        recv = self.recv1 if at < 5 else self.recv2
        pltpu.make_async_copy(ref, ref, recv.at[at % 5]).wait()

    def add(self, out, left, right):
        f32 = jnp.float32
        out[...] = (left[...].astype(f32) + right[...].astype(f32)).astype(out.dtype)

    def mine(self, half):
        if half == 0:
            return pl.ds(self.core * 8 + 2 * self.x + self.y, 1)
        return pl.ds(self.core * 8 + 4 + 2 * self.y + self.x, 1)

    def hop(self, at):
        x, y, core = self.x, self.y, self.core
        o, p = self.o, self.p
        pair_a, pair_b = pl.ds(core * 8 + 2 * x, 2), pl.ds(core * 8 + 4 + 2 * y, 2)
        one = lambda at: pl.ds(at, 1)
        return [
            lambda: self.copy(0, self.by_core(1 - core), self.rc, self.chip_peer),
            lambda: self.copy(1, self.quarter(0, 1 - x), self.ra, self.x_peer),
            lambda: self.copy(2, self.quarter(1, 1 - y), self.rb, self.y_peer),
            lambda: self.copy(3, self.eighth(0, 1 - y), self.ta, self.y_peer),
            lambda: self.copy(4, self.eighth(1, 1 - x), self.tb, self.x_peer),
            lambda: self.copy(5, p.at[one(0)], o.at[self.mine(0)], self.y_peer),
            lambda: self.copy(6, p.at[one(1)], o.at[self.mine(1)], self.x_peer),
            lambda: self.copy(7, o.at[pair_a], o.at[pair_a], self.x_peer),
            lambda: self.copy(8, o.at[pair_b], o.at[pair_b], self.y_peer),
            lambda: self.copy(9, o.at[pl.ds(core * 8, 8)], o.at[pl.ds(core * 8, 8)], self.chip_peer),
        ][at]()

    def begin(self):
        self.hop(0).start()

    def by_core(self, core):
        return self.u.at[pl.ds(core * 8, 8)]

    def quarter(self, half, at):
        return self.s1.at[pl.ds(4 * half + 2 * at, 2)]

    def eighth(self, half, at):
        return (self.sa, self.sb)[half].at[pl.ds(at, 1)]

    def result(self, half):
        return self.p.at[pl.ds(half, 1)]

    def first(self):
        self.got(0, self.rc)
        self.add(self.s1, self.by_core(self.core), self.rc)
        self.hop(1).start()
        self.hop(2).start()

    def second(self):
        self.got(1, self.ra)
        self.add(self.sa, self.quarter(0, self.x), self.ra)
        self.hop(3).start()
        self.got(2, self.rb)
        self.add(self.sb, self.quarter(1, self.y), self.rb)
        self.hop(4).start()

    def third(self):
        self.got(3, self.ta)
        self.add(self.result(0), self.eighth(0, self.y), self.ta)
        self.got(4, self.tb)
        self.add(self.result(1), self.eighth(1, self.x), self.tb)

    def reduced(self):
        for at in range(5):
            self.hop(at).wait_send()

    def kept(self, half):
        return pltpu.make_async_copy(self.p.at[pl.ds(half, 1)], self.o.at[self.mine(half)], self.loc.at[half])

    def spread1(self):
        self.hop(5).start()
        self.hop(6).start()
        self.kept(0).start()
        self.kept(1).start()

    def spread2(self):
        x, y, core = self.x, self.y, self.core
        self.kept(0).wait()
        self.got(5, self.o.at[pl.ds(core * 8 + 2 * x + 1 - y, 1)])
        self.hop(7).start()
        self.kept(1).wait()
        self.got(6, self.o.at[pl.ds(core * 8 + 4 + 2 * y + 1 - x, 1)])
        self.hop(8).start()

    def spread3(self):
        x, y, core = self.x, self.y, self.core
        self.got(7, self.o.at[pl.ds(core * 8 + 2 - 2 * x, 2)])
        self.got(8, self.o.at[pl.ds(core * 8 + 6 - 2 * y, 2)])
        self.hop(9).start()

    def everywhere(self):
        self.got(9, self.o.at[pl.ds(8 - self.core * 8, 8)])
        for at in range(5, 10):
            self.hop(at).wait_send()


class StripSum(PlaneSum):
    @staticmethod
    def reduce_scratch(shape, dtype):
        lead, rows, cols = shape
        rest = lead - 2
        shapes = [(lead, rows)] * 2
        shapes += [(count, rows // 2) for count in (2, rest, 2, rest)] + [(count, rows // 4) for count in (2, rest)]
        return [pltpu.VMEM(item + (cols // 2,), dtype) for item in shapes] + [DMA((5,)), DMA((5,))]

    def lead(self, half):
        whole = (self.u if self.u is not None else self.o).shape[0]
        return pl.ds(0, 2) if half == 0 else pl.ds(2, whole - 2)

    def strip(self, core):
        size = (self.u if self.u is not None else self.o).shape[2] // 2
        return pl.ds(pl.multiple_of(core * size, 128), size)

    def rows(self, at, parts):
        size = (self.u if self.u is not None else self.o).shape[1] // parts
        return pl.ds(pl.multiple_of(at * size, 16), size)

    def by_core(self, core):
        return self.u.at[:, :, self.strip(core)]

    def quarter(self, half, at):
        return self.s1.at[self.lead(half), self.rows(at, 2)]

    def eighth(self, half, at):
        return (self.sa, self.sb)[half].at[:, self.rows(at, 4)]

    def result(self, half):
        return self.p.at[half, pl.ds(0, 2 if half == 0 else self.u.shape[0] - 2)]

    def hop(self, at):
        if at < 5:
            return super().hop(at)
        o, x, y = self.o, self.x, self.y
        mine = lambda half: o.at[
            self.lead(half), self.rows(2 * x + y if half == 0 else 2 * y + x, 4), self.strip(self.core)
        ]
        pair = lambda half: o.at[self.lead(half), self.rows(x if half == 0 else y, 2), self.strip(self.core)]
        both = o.at[:, :, self.strip(self.core)]
        return [
            lambda: self.copy(5, self.result(0), mine(0), self.y_peer),
            lambda: self.copy(6, self.result(1), mine(1), self.x_peer),
            lambda: self.copy(7, pair(0), pair(0), self.x_peer),
            lambda: self.copy(8, pair(1), pair(1), self.y_peer),
            lambda: self.copy(9, both, both, self.chip_peer),
        ][at - 5]()

    def kept(self, half):
        x, y = self.x, self.y
        mine = self.o.at[
            self.lead(half), self.rows(2 * x + y if half == 0 else 2 * y + x, 4), self.strip(self.core)
        ]
        return pltpu.make_async_copy(self.result(half), mine, self.loc.at[half])

    def spread2(self):
        x, y, mine = self.x, self.y, self.strip(self.core)
        self.kept(0).wait()
        self.got(5, self.o.at[self.lead(0), self.rows(2 * x + 1 - y, 4), mine])
        self.hop(7).start()
        self.kept(1).wait()
        self.got(6, self.o.at[self.lead(1), self.rows(2 * y + 1 - x, 4), mine])
        self.hop(8).start()

    def spread3(self):
        mine = self.strip(self.core)
        self.got(7, self.o.at[self.lead(0), self.rows(1 - self.x, 2), mine])
        self.got(8, self.o.at[self.lead(1), self.rows(1 - self.y, 2), mine])
        self.hop(9).start()

    def everywhere(self):
        self.got(9, self.o.at[:, :, self.strip(1 - self.core)])
        for at in range(5, 10):
            self.hop(at).wait_send()


def unit_pieces(unit):
    return jax.ShapeDtypeStruct((2,) + unit.shape[1:], unit.dtype)


def line_greet(bar, me, n):
    @pl.when(me > 0)
    def _():
        pl.semaphore_signal(bar, inc=1, device_id={"tensor": me - 1}, device_id_type=MESH)

    @pl.when(me < n - 1)
    def _():
        pl.semaphore_signal(bar, inc=1, device_id={"tensor": me + 1}, device_id_type=MESH)

    return jnp.where(me > 0, 1, 0) + jnp.where(me < n - 1, 1, 0)


class LineScatter:
    def __init__(self, n, x, o, buf, tmp, send, recv):
        self.n, self.x, self.o, self.buf, self.tmp, self.send, self.recv = n, x, o, buf, tmp, send, recv
        self.me = lax.axis_index("tensor")

    @staticmethod
    def scratch(n, own, cols, dtype):
        return [
            pltpu.VMEM((2, n - 1, own, cols), dtype),
            pltpu.VMEM((2, n - 1, own, cols), dtype),
            DMA((2, n - 1)),
            DMA((2, n - 1)),
        ]

    def term(self, d, k):
        return self.n - 1 - k if d == 0 else k

    def sends(self, d, k):
        return self.me < self.n - 1 - k if d == 0 else self.me > k

    def behind(self, d):
        return self.me > 0 if d == 0 else self.me < self.n - 1

    def copy(self, d, k, first):
        return pltpu.make_async_remote_copy(
            src_ref=self.x.at[self.term(d, k)] if first else self.tmp.at[d, k],
            dst_ref=self.buf.at[d, k],
            send_sem=self.send.at[d, k],
            recv_sem=self.recv.at[d, k],
            device_id={"tensor": jnp.clip(self.me + 1 if d == 0 else self.me - 1, 0, self.n - 1)},
            device_id_type=MESH,
        )

    def landed(self, d, k):
        return pltpu.make_async_copy(self.buf.at[d, k], self.buf.at[d, k], self.recv.at[d, k])

    def begin(self, ks):
        for d in range(2):

            @pl.when(jnp.logical_not(self.behind(d)))
            def _():
                for k in ks:
                    self.copy(d, k, True).start()

    def step(self, k, which=None):
        for d in range(2):
            now = self.behind(d) & self.sends(d, k)

            @pl.when(now if which is None else now & which(d))
            def _():
                self.landed(d, k).wait()
                at = self.term(d, k)
                both = self.buf[d, k].astype(jnp.float32) + self.x[at].astype(jnp.float32)
                self.tmp[d, k] = both.astype(self.tmp.dtype)
                self.copy(d, k, False).start()

    def end(self):
        self.o[...] = self.x[self.me].astype(jnp.float32)
        for d in range(2):
            for k in range(self.n - 1):

                @pl.when(self.behind(d) & (self.me == self.term(d, k)))
                def _():
                    self.landed(d, k).wait()
                    self.o[...] += self.buf[d, k].astype(jnp.float32)

        for d in range(2):
            for k in range(self.n - 1):

                @pl.when(self.sends(d, k))
                def _():
                    self.copy(d, k, False).wait_send()


GELU_SCALE = 0.7978845608028654
GELU_CUBE = 0.044715


def feed_kernel(n, nc, heads, chunks, piece_ref, *rest):
    (token_hbm, out_hbm, abias_hbm, gain_hbm, shift_hbm, up_hbm, down_hbm, bias_hbm, near_ref, cot_ref), rest = rest[:10], rest[10:]
    outs, heads_ref, rest = rest[:7], rest[7], rest[8:]
    kept_refs, rest = rest[:7], rest[7:]
    feed_ref, p1_ref, p2_ref, middle_ref, gm_ref, vec_ref, p3_ref = kept_refs
    (token_ref, out_ref, abias_ref, gain_ref, shift_ref, bias_ref, osem), rest = rest[:7], rest[7:]
    leave = copies(tuple(zip(kept_refs, outs)), osem)
    (o_ref, sum_ref, att_ref, gpiece, u3, bsend, brecv, bloc), rest = rest[:8], rest[8:]
    (x_ref, up_ref, down_ref, grad_ref, wsem, asend, arecv, aloc, csend, crecv, cloc), rest = rest[:11], rest[11:]
    (held, act, gp, part, acc, buf, tmp, u1, u2), rest = rest[:9], rest[9:]
    (gsend, grecv, loc, ssend, srecv), rest = rest[:5], rest[5:]
    plane = [PlaneSum(u1, p1_ref, None, rest[:10]), PlaneSum(u2, p2_ref, None, rest[10:20])]
    out_sum = StripSum(u3, p3_ref, None, rest[20:30])
    me = lax.axis_index("tensor")
    rows, width = token_ref.shape
    wide = up_ref.shape[1]
    few = rows // chunks
    f32, low = jnp.float32, jnp.bfloat16
    ctx, dp = lax.axis_index("context"), lax.axis_index("dp")
    place, total = ctx * n + me, nc * n
    my_head = me * heads + jnp.minimum(ctx, heads - 1)
    bar = pltpu.get_barrier_semaphore()
    for shift in range(1, total):
        other = lax.rem(place + shift, total)
        pl.semaphore_signal(bar, inc=1, device_id=spread(other, AXES, (nc, n)), device_id_type=MESH)
    pl.semaphore_signal(bar, inc=1, device_id={"dp": 1 - dp}, device_id_type=MESH)
    weights_in = copies(
        (
            (token_hbm, token_ref),
            (abias_hbm, abias_ref),
            (gain_hbm, gain_ref),
            (shift_hbm, shift_ref),
            (out_hbm, out_ref),
            (bias_hbm, bias_ref),
            (up_hbm, up_ref),
            (down_hbm, down_ref),
        ),
        wsem,
    )
    for item in weights_in:
        item.start()

    def grad_rows(block):
        return grad_ref.at[pl.ds(pl.multiple_of(block * rows, rows), rows)]

    def grad_on(d, s):
        block = jnp.clip(me - s if d == 0 else me + s, 0, n - 1)
        return pltpu.make_async_remote_copy(
            src_ref=near_ref.at[block],
            dst_ref=grad_rows(block),
            send_sem=csend.at[d, s],
            recv_sem=crecv.at[d, s],
            device_id={"tensor": jnp.clip(me + 1 if d == 0 else me - 1, 0, n - 1)},
            device_id_type=MESH,
        )

    def grad_sends(d, s):
        return (me - s >= 0) & (me < n - 1) if d == 0 else (me + s < n) & (me > 0)

    def grad_near(d, s):
        block = jnp.clip(me - s if d == 0 else me + s, 0, n - 1)
        return pltpu.make_async_copy(near_ref.at[block], grad_rows(block), cloc.at[d, s])

    def grad_own():
        return pltpu.make_async_copy(cot_ref, grad_rows(me), cloc.at[0, 0])

    def beside(d, s):
        return me - s >= 0 if d == 0 else me + s < n

    grad_own().start()
    for d in range(2):
        for s in range(1, n - 1):

            @pl.when(beside(d, s))
            def _():
                grad_near(d, s).start()

    pl.semaphore_wait(bar, total)

    def to_place(shift):
        other = lax.rem(place + shift, total)
        return pltpu.make_async_remote_copy(
            src_ref=piece_ref.at[other],
            dst_ref=att_ref.at[my_head],
            send_sem=asend.at[shift],
            recv_sem=arecv.at[shift],
            device_id=spread(other, AXES, (nc, n)),
            device_id_type=MESH,
        )

    @pl.when(ctx < heads)
    def _():
        for shift in range(1, total):
            to_place(shift).start()
        stay = pltpu.make_async_copy(piece_ref.at[place], att_ref.at[my_head], aloc)
        stay.start()
        stay.wait()

    for d in range(2):

        @pl.when(grad_sends(d, n - 2))
        def _():
            grad_on(d, n - 2).start()

    for shift in range(1, total):
        source = lax.rem(place + total - shift, total)
        at_ctx, at_ten = lax.div(source, n), lax.rem(source, n)

        @pl.when(at_ctx < heads)
        def _():
            landed = att_ref.at[at_ten * heads + jnp.minimum(at_ctx, heads - 1)]
            pltpu.make_async_copy(landed, landed, arecv.at[shift]).wait()

    for item in weights_in[:5]:
        item.wait()
    attended = att_ref[...].reshape(width, rows)
    middle = token_ref[...].astype(f32) + dot(attended, out_ref[...], ((0,), (0,))) + row(abias_ref)
    middle_ref[...] = middle
    leave[3].start()
    x_ref[...] = (norm_parts(middle)[0] * row(gain_ref) + row(shift_ref)).astype(low)

    @pl.when(ctx < heads)
    def _():
        for shift in range(1, total):
            to_place(shift).wait_send()

    def rows_of(block):
        return pl.ds(pl.multiple_of(block * rows, rows), rows)

    def neighbour(d):
        return {"tensor": jnp.clip(jnp.where(d == 0, me + 1, me - 1), 0, n - 1)}

    def onward(d):
        return jnp.where(d == 0, me, n - 1 - me) < n - 1

    def hand_on(d, s, block, first):
        return pltpu.make_async_remote_copy(
            src_ref=x_ref if first else held.at[rows_of(block)],
            dst_ref=held.at[rows_of(block)],
            send_sem=gsend.at[d, s],
            recv_sem=grecv.at[d, s],
            device_id=neighbour(d),
            device_id_type=MESH,
        )

    def chunk(block, c):
        return pl.ds(pl.multiple_of(block * rows + c * few, few), few)

    def back(d, block, c, first):
        at = chunk(block, c)
        return pltpu.make_async_remote_copy(
            src_ref=part.at[at] if first else tmp.at[at],
            dst_ref=buf.at[d, at],
            send_sem=ssend.at[block, c],
            recv_sem=srecv.at[d, block, c],
            device_id=neighbour(d),
            device_id_type=MESH,
        )

    for d in range(2):

        @pl.when(onward(d))
        def _():
            hand_on(d, 0, me, True).start()

    own = pltpu.make_async_copy(x_ref, held.at[rows_of(me)], loc)
    own.start()
    sum_ref[...] = jnp.zeros_like(sum_ref)
    own.wait()
    for item in weights_in[5:]:
        item.wait()
    grad_own().wait()
    for d in range(2):
        for s in range(1, n - 1):

            @pl.when(beside(d, s))
            def _():
                grad_near(d, s).wait()

    columns = 256

    def work(block):
        here = rows_of(block)
        acc[...] = jnp.zeros_like(acc)

        @pl.loop(0, wide // columns)
        def _(j):
            at = pl.ds(pl.multiple_of(j * columns, columns), columns)
            pre = dot(held[here, :], up_ref[:, at], ((1,), (0,))) + bias_ref[at].reshape(1, -1)
            square = pre * pre
            tanh = jnp.tanh(GELU_SCALE * pre * (1.0 + GELU_CUBE * square))
            act[here, at] = (0.5 * pre * (1.0 + tanh)).astype(low)
            slope = 0.5 * (1.0 + tanh) + 0.5 * pre * (1.0 - tanh * tanh) * (
                GELU_SCALE * (1.0 + 3.0 * GELU_CUBE * square)
            )
            grad = (dot(grad_ref[here, :], down_ref[at, :], ((1,), (1,))) * slope).astype(low)
            gp[here, at] = grad
            acc[...] += dot(grad, up_ref[:, at], ((1,), (1,)))

        part[here, :] = acc[...].astype(low)
        sum_ref[...] += jnp.sum(gp[here, :].astype(f32), axis=0, keepdims=True)

    near = jnp.minimum(me, n - 1 - me)
    toward = jnp.where(2 * me < n - 1, -1, 1)

    @pl.loop(0, n)
    def _(slot):
        paired = slot <= 2 * near
        distance = jnp.where(paired, lax.div(slot + 1, 2), slot - near)
        side = jnp.where(paired & (lax.rem(slot, 2) == 1), toward, -toward)
        block = me + side * distance
        d = jnp.where(block < me, 0, 1)
        s = jnp.maximum(distance - 1, 0)

        @pl.when(slot > 0)
        def _():
            landed = held.at[rows_of(block)]
            pltpu.make_async_copy(landed, landed, grecv.at[d, s]).wait()

            @pl.when(onward(d))
            def _():
                hand_on(d, jnp.minimum(s + 1, n - 2), block, False).start()

        @pl.when(distance == n - 1)
        def _():
            landed = grad_rows(block)
            pltpu.make_async_copy(landed, landed, crecv.at[d, n - 2]).wait()

        work(block)

        @pl.when((slot > 0) & ((me == 0) | (me == n - 1)))
        def _():
            for c in range(chunks):
                back(1 - d, block, c, True).start()

    def weights(left, right, unit):
        half = wide // 2

        @pl.loop(0, 2)
        def _(j):
            at = pl.ds(pl.multiple_of(j * half, 128), half)
            total = dot(left[:, at], right[...], ((0,), (0,)))
            unit[pl.ds(8 * j, 8)] = total.astype(low).reshape((8,) + unit.shape[1:])

    weights(act, grad_ref, u1)
    plane[0].begin()
    weights(held, gp, u2)
    plane[1].begin()

    def relay(way, block):
        d = jnp.where(way > 0, 0, 1)

        @pl.when((me > 0) & (me < n - 1) & (block >= 0) & (block < n))
        def _():
            for c in range(chunks):
                at = chunk(block, c)
                landed = buf.at[d, at]
                pltpu.make_async_copy(landed, landed, srecv.at[d, block, c]).wait()
                tmp[at, :] = (buf[d, at, :].astype(f32) + part[at, :].astype(f32)).astype(low)
                back(d, block, c, False).start()

    plane[0].first()
    for j in range(1, n):
        relay(-toward, me - toward * j)
        if j == 1:
            plane[1].first()

    @pl.loop(0, n)
    def _(block):
        here = rows_of(block)
        feed_ref[here, :] = dot(act[here, :], down_ref[...], ((1,), (0,))).astype(low)

    leave[0].start()

    plane[0].second()
    plane[1].second()
    for j in range(1, n):
        relay(toward, me + toward * j)
    for item in plane:
        item.third()
    for c in range(chunks):
        at = chunk(me, c)
        mine = pl.ds(c * few, few)
        o_ref[mine, :] = part[at, :].astype(f32)
        for d in range(2):

            @pl.when(me > 0 if d == 0 else me < n - 1)
            def _():
                landed = buf.at[d, at]
                pltpu.make_async_copy(landed, landed, srecv.at[d, me, c]).wait()
                o_ref[mine, :] += buf[d, at, :].astype(f32)

    grad = o_ref[...]
    normed, scale = norm_parts(middle_ref[...])
    above = grad_ref[rows_of(me), :].astype(f32)
    grad_middle = above + norm_backward(grad, normed, scale, row(gain_ref))
    gm_ref[...] = grad_middle
    for at in (1, 2, 4):
        leave[at].start()
    gm_low = grad_middle.astype(low)
    back_out = dot(out_ref[...], gm_low, ((1,), (1,))).astype(low)
    gpiece[...] = back_out.reshape(gpiece.shape)
    vec_ref[...] = jnp.zeros_like(vec_ref)
    vec_ref[2:3, :] = jnp.sum(gm_low.astype(f32), axis=0, keepdims=True)

    def to_head(shift):
        other = lax.rem(place + shift, total)
        at_ctx, at_ten = lax.div(other, n), lax.rem(other, n)
        return at_ctx < heads, pltpu.make_async_remote_copy(
            src_ref=gpiece.at[at_ten * heads + jnp.minimum(at_ctx, heads - 1)],
            dst_ref=heads_ref.at[place],
            send_sem=bsend.at[shift],
            recv_sem=brecv.at[shift],
            device_id={"context": at_ctx, "tensor": at_ten},
            device_id_type=MESH,
        )

    for shift in range(1, total):
        goes, item = to_head(shift)

        @pl.when(goes)
        def _():
            item.start()

    stay = pltpu.make_async_copy(gpiece.at[my_head], heads_ref.at[place], bloc)
    stay.start()
    u3[...] = dot(att_ref[...].reshape(width, rows), gm_low, ((1,), (0,))).astype(low).reshape(u3.shape)
    out_sum.begin()
    vec_ref[3:4, :] = jnp.sum(grad * normed, axis=0, keepdims=True)
    vec_ref[4:5, :] = jnp.sum(grad, axis=0, keepdims=True)
    vec_ref[5:6, :] = jnp.sum(above, axis=0, keepdims=True)
    vec_ref[6:7, :] = sum_ref[...]
    out_sum.first()
    out_sum.second()
    out_sum.third()
    leave[5].start()
    leave[6].start()
    stay.wait()

    @pl.when(ctx < heads)
    def _():
        for shift in range(1, total):
            source = lax.rem(place + total - shift, total)
            landed = heads_ref.at[source]
            pltpu.make_async_copy(landed, landed, brecv.at[shift]).wait()

    for shift in range(1, total):
        goes, item = to_head(shift)

        @pl.when(goes)
        def _():
            item.wait_send()

    out_sum.reduced()
    for item in leave:
        item.wait()
    for d in range(2):
        for s in range(n - 1):
            block = me - s if d == 0 else me + s

            @pl.when(onward(d) & (block >= 0) & (block < n))
            def _():
                hand_on(d, s, me, True).wait_send()

    for block in range(n):

        @pl.when(me != block)
        def _():
            for c in range(chunks):
                back(jnp.where(me < block, 0, 1), block, c, True).wait_send()

    for d in range(2):

        @pl.when(grad_sends(d, n - 2))
        def _():
            grad_on(d, n - 2).wait_send()

    for item in plane:
        item.reduced()


def feed_part(pieces, tokens, out_weight, vectors, up, down, bias, near, cotangent, n, nc, heads, collective_id):
    rows, width = tokens.shape
    wide = up.shape[1]
    chunks = 2
    total = n * rows
    low, f32 = jnp.bfloat16, jnp.float32
    unit = (16, wide // 16, width)
    piece = jax.ShapeDtypeStruct((2,) + unit[1:], low)
    return pl.pallas_call(
        functools.partial(feed_kernel, n, nc, heads, chunks),
        out_shape=(
            jax.ShapeDtypeStruct((total, width), low),
            piece,
            piece,
            jax.ShapeDtypeStruct((rows, width), f32),
            jax.ShapeDtypeStruct((rows, width), f32),
            jax.ShapeDtypeStruct((8, width), f32),
            jax.ShapeDtypeStruct((2, 2, rows // 4, width // 2), low),
            jax.ShapeDtypeStruct(pieces.shape, low),
        ),
        in_specs=[VM] + [HB] * 10,
        out_specs=(HB,) * 7 + (VM,),
        scratch_shapes=[
            pltpu.VMEM((total, width), low),
            pltpu.VMEM(piece.shape, low),
            pltpu.VMEM(piece.shape, low),
            pltpu.VMEM((rows, width), f32),
            pltpu.VMEM((rows, width), f32),
            pltpu.VMEM((8, width), f32),
            pltpu.VMEM((2, 2, rows // 4, width // 2), low),
            pltpu.VMEM(tokens.shape, tokens.dtype),
            pltpu.VMEM(out_weight.shape, low),
            pltpu.VMEM((width,), f32),
            pltpu.VMEM((width,), f32),
            pltpu.VMEM((width,), f32),
            pltpu.VMEM((wide,), f32),
            DMA((7,)),
            pltpu.VMEM((rows, width), f32),
            pltpu.VMEM((1, wide), f32),
            pltpu.VMEM((n * heads,) + pieces.shape[1:], low),
            pltpu.VMEM((n * heads,) + pieces.shape[1:], low),
            pltpu.VMEM((n, width // n, width), low),
            DMA((nc * n,)),
            DMA((nc * n,)),
            DMA,
            pltpu.VMEM((rows, width), low),
            pltpu.VMEM(up.shape, low),
            pltpu.VMEM(down.shape, low),
            pltpu.VMEM((total, width), low),
            DMA((8,)),
            DMA((nc * n,)),
            DMA((nc * n,)),
            DMA,
            DMA((2, n - 1)),
            DMA((2, n - 1)),
            DMA((2, n - 1)),
            pltpu.VMEM((total, width), low),
            pltpu.VMEM((total, wide), low),
            pltpu.VMEM((total, wide), low),
            pltpu.VMEM((total, width), low),
            pltpu.VMEM((rows, width), f32),
            pltpu.VMEM((2, total, width), low),
            pltpu.VMEM((total, width), low),
            pltpu.VMEM(unit, low),
            pltpu.VMEM(unit, low),
            DMA((2, n - 1)),
            DMA((2, n - 1)),
            DMA,
            DMA((n, chunks)),
            DMA((2, n, chunks)),
        ]
        + PlaneSum.reduce_scratch(unit, low) * 2
        + StripSum.reduce_scratch((n, width // n, width), low),
        compiler_params=remote_params(collective_id, 56),
    )(pieces, tokens, out_weight, *vectors, up, down, bias, near, cotangent)


def last_kernel(n, nc, heads, shared, count, x_ref, w_hbm, h_hbm, a_hbm, feed_hbm, mid_hbm, bias_hbm, *rest):
    ps, rest = rest[:count], rest[count:]
    (token_hbm, gain_hbm, middle_hbm, vec_hbm), rest = rest[:4], rest[4:]
    (out_ref, g_ref, v_ref, po_ref, ao_ref), rest = rest[:5], rest[5:]
    outs, rest = rest[:count], rest[count:]
    (rows_ref, w_ref, h_ref, token_ref, middle_ref, part, sum_ref, u_ref, piece), rest = rest[:9], rest[9:]
    (hsend, hrecv, hloc, win), rest = rest[:4], rest[4:]
    (feed_ref, fsum_ref, mid_ref, bias_ref, gain_ref, vec_ref), rest = rest[:6], rest[6:]
    feed_line = LineScatter(n, feed_ref, fsum_ref, *rest[:4])
    rest = rest[4:]
    chunks = 2
    own = token_ref.shape[0]
    few = own // chunks
    lines = [
        LineScatter(n, part.at[:, pl.ds(c * few, few)], sum_ref.at[pl.ds(c * few, few)], *rest[4 * c : 4 * c + 4])
        for c in range(chunks)
    ]
    rest = rest[4 * chunks :]
    project = StripSum(u_ref, piece, po_ref, rest[:10], rest[10:13])
    rest = rest[13:]
    feeds = [PlaneSum(None, ps[i], outs[i], None, rest[3 * i : 3 * i + 3]) for i in range(count)]
    rest = rest[3 * count :]
    (land, zsend, zrecv, zloc, a_ref), rest = rest[:5], rest[5:]
    (asend, arecv, aloc, now), rest = rest[:4], rest[4:]
    sizes = (n, 2 * nc)
    bufs, sems = rest[:2], rest[2:]
    f32, low = jnp.float32, jnp.bfloat16

    ten, ctx, x = (lax.axis_index(name) for name in ("tensor", "context", "dp"))
    place = ctx * 2 + x
    bar = pltpu.get_barrier_semaphore()
    for shift in range(1, n):
        pl.semaphore_signal(bar, inc=1, device_id={"tensor": lax.rem(ten + shift, n)}, device_id_type=MESH)
    for shift in range(1, 8):
        other = lax.rem(place + shift, 8)
        pl.semaphore_signal(
            bar, inc=1, device_id={"context": lax.div(other, 2), "dp": lax.rem(other, 2)}, device_id_type=MESH
        )
    copies_in = copies(
        (
            (feed_hbm, feed_ref),
            (token_hbm, token_ref),
            (w_hbm, w_ref),
            (h_hbm, h_ref),
            (middle_hbm, middle_ref),
            (mid_hbm, mid_ref),
            (bias_hbm, bias_ref),
            (gain_hbm, gain_ref),
            (vec_hbm, vec_ref),
        ),
        win,
    )
    for item in copies_in:
        item.start()
    pl.semaphore_wait(bar, n + 6)

    half = 2 * own
    far = 1 - lax.div(ten, 2)
    pairs = (far, 1 - far)

    def columns(pair):
        return pl.ds(pl.multiple_of(pair * half, 128), half)

    def ship(index, shift):
        other = lax.rem(ctx + shift, nc)
        return pltpu.make_async_remote_copy(
            src_ref=x_ref.at[other, :, :, columns(pairs[index])],
            dst_ref=rows_ref.at[:, jnp.minimum(ctx, heads - 1), :, columns(pairs[index])],
            send_sem=hsend.at[index, shift],
            recv_sem=hrecv.at[index, shift],
            device_id={"context": other},
            device_id_type=MESH,
        )

    @pl.when(ctx < heads)
    def _():
        for index in range(2):
            for shift in range(1, nc):
                ship(index, shift).start()
        stay = pltpu.make_async_copy(x_ref.at[ctx], rows_ref.at[:, ctx], hloc)
        stay.start()
        stay.wait()

    def across(shift):
        other = lax.rem(ten + shift, n)
        return pltpu.make_async_remote_copy(
            src_ref=a_hbm.at[lax.div(other, 2), lax.rem(other, 2)],
            dst_ref=land.at[ten],
            send_sem=zsend.at[shift],
            recv_sem=zrecv.at[shift],
            device_id={"tensor": other},
            device_id_type=MESH,
        )

    copies_in[0].wait()
    feed_line.begin((0,))
    for shift in range(1, n):
        across(shift).start()
    mine = pltpu.make_async_copy(a_hbm.at[lax.div(ten, 2), lax.rem(ten, 2)], land.at[ten], zloc)
    mine.start()
    for item in feeds:
        item.spread1()

    def there(at):
        ctx_, x_ = lax.div(at, 2), lax.rem(at, 2)
        y_ = lax.div(ctx_, 2)
        row_ = jnp.where(ten < n // 2, 2 * x_ + y_, 2 * y_ + x_)
        rows = pl.ds(pl.multiple_of(row_ * a_ref.shape[0], 16), a_ref.shape[0])
        cols = pl.ds(pl.multiple_of(lax.rem(ctx_, 2) * a_ref.shape[1], 128), a_ref.shape[1])
        return ao_ref.at[rows, cols]

    def push(shift):
        other = lax.rem(place + shift, 8)
        return pltpu.make_async_remote_copy(
            src_ref=a_ref,
            dst_ref=there(place),
            send_sem=asend.at[shift],
            recv_sem=arecv.at[shift],
            device_id={"context": lax.div(other, 2), "dp": lax.rem(other, 2)},
            device_id_type=MESH,
        )

    copies_in[1].wait()
    normed, scale = norm_parts(token_ref[...].astype(f32))
    mine.wait()
    for shift in range(1, n):
        source = lax.rem(ten + n - shift, n)
        pltpu.make_async_copy(land.at[source], land.at[source], zrecv.at[shift]).wait()
    value = land[0].astype(f32)
    for at in range(1, n):
        value = value + land[at].astype(f32)
    a_ref[...] = value.astype(low)
    for item in copies_in[2:]:
        item.wait()
    now[0] = vec_ref[...]
    for shift in range(1, 8):
        push(shift).start()
    kept = pltpu.make_async_copy(a_ref, there(place), aloc)
    kept.start()

    def partials(index):
        at = columns(pairs[index])
        for shift in range(1, nc):
            source = lax.rem(ctx + nc - shift, nc)

            @pl.when(source < heads)
            def _():
                ref = rows_ref.at[:, jnp.minimum(source, heads - 1), :, at]
                pltpu.make_async_copy(ref, ref, hrecv.at[index, shift]).wait()

        total = 0.0
        for kind in range(3):
            grads = rows_ref[kind, :, :, at].reshape(heads * HEAD_DIM, half)
            total = total + dot(grads, w_ref[kind], ((0,), (0,)))
        part[pl.ds(2 * pairs[index], 2)] = total.astype(low).reshape(2, own, total.shape[1])

    first = lambda d: (ten < n // 2) if d == 0 else (ten >= n // 2)
    second = lambda d: (ten >= n // 2) if d == 0 else (ten < n // 2)
    feed_line.step(0, first)
    partials(0)
    for line in lines:
        line.begin((0, 1))
    partials(1)
    for line in lines:
        line.begin((2,))
    feed_line.begin((1, 2))
    for item in feeds:
        item.spread2()
    for line in lines:
        line.step(0, first)
    for kind in range(3):
        grads = rows_ref[kind].reshape(heads * HEAD_DIM, n * own)
        u_ref[kind] = dot(grads, h_ref[...], ((1,), (0,))).astype(low)
    project.begin()
    for line in lines:
        line.step(1, first)
    feed_line.step(0, second)
    ends = jnp.concatenate(
        [rows_ref[kind].reshape(heads * HEAD_DIM, n * own) for kind in (0, 2)], axis=0
    )
    bias = dot(jnp.ones((8, n * own), low), ends, ((1,), (1,)))
    now[0, 7:8, 0 : bias.shape[1]] = bias[0:1]
    project.first()
    for item in feeds:
        item.spread3()
    project.second()
    for k in range(n - 1):
        for line in lines:
            line.step(k, second)
    project.third()
    project.spread1()
    for line in lines:
        line.end()
    grad = sum_ref[...]
    now[0, 0:1] = jnp.sum(grad * normed, axis=0, keepdims=True)
    now[0, 1:2] = jnp.sum(grad, axis=0, keepdims=True)
    alone = now[0]

    def where(stage):
        return ten if stage == 0 else place

    def stage_copy(stage, shift):
        other = lax.rem(where(stage) + shift, sizes[stage])
        peer = {"tensor": other} if stage == 0 else {"context": lax.div(other, 2), "dp": lax.rem(other, 2)}
        return pltpu.make_async_remote_copy(
            src_ref=now.at[stage],
            dst_ref=bufs[stage].at[where(stage)],
            send_sem=sems[2 * stage].at[shift],
            recv_sem=sems[2 * stage + 1].at[shift],
            device_id=peer,
            device_id_type=MESH,
        )

    def stage_start(stage):
        for shift in range(1, sizes[stage]):
            stage_copy(stage, shift).start()
        bufs[stage][where(stage)] = now[stage]

    def stage_end(stage):
        buf, size = bufs[stage], sizes[stage]
        for shift in range(1, size):
            source = lax.rem(where(stage) + size - shift, size)
            pltpu.make_async_copy(buf.at[source], buf.at[source], sems[2 * stage + 1].at[shift]).wait()
        total = buf[0]
        for at in range(1, size):
            total = total + buf[at]
        if stage == 0:
            line_ = lax.broadcasted_iota(jnp.int32, total.shape, 0)
            now[1] = jnp.where(line_ < shared, total, alone)
        else:
            v_ref[...] = total

    stage_start(0)
    back = norm_backward(grad, normed, scale, row(gain_ref))
    g_ref[...] = (middle_ref[...] + back).astype(g_ref.dtype)
    project.spread2()
    feed_line.step(1, first)
    stage_end(0)
    stage_start(1)
    project.spread3()
    feed_line.end()
    out_ref[...] = (mid_ref[...] + fsum_ref[...] + row(bias_ref)).astype(low)
    kept.wait()
    for shift in range(1, 8):
        source = there(lax.rem(place + 8 - shift, 8))
        pltpu.make_async_copy(source, source, arecv.at[shift]).wait()
    for item in feeds:
        item.everywhere()
    stage_end(1)
    project.everywhere()
    project.reduced()

    @pl.when(ctx < heads)
    def _():
        for index in range(2):
            for shift in range(1, nc):
                ship(index, shift).wait_send()

    for shift in range(1, n):
        across(shift).wait_send()
    for shift in range(1, 8):
        push(shift).wait_send()
    for stage in range(2):
        for shift in range(1, sizes[stage]):
            stage_copy(stage, shift).wait_send()


def last_part(x, weight, hidden, attend_pieces, feed, middle, bias, pieces, tokens, gain, grad_middle, vectors, shared, n, heads, collective_id):
    nc = x.shape[0]
    own, cols = tokens.shape
    count = len(pieces)
    f32, low = jnp.float32, jnp.bfloat16
    whole = lambda item: jax.ShapeDtypeStruct((16,) + item.shape[1:], item.dtype)
    wide, deep = attend_pieces.shape[2:]
    unit = (3, heads * HEAD_DIM, cols)
    result = pl.pallas_call(
        functools.partial(last_kernel, n, nc, heads, shared, count),
        out_shape=(
            jax.ShapeDtypeStruct((own, cols), low),
            jax.ShapeDtypeStruct((own, cols), low),
            jax.ShapeDtypeStruct(vectors.shape, f32),
            jax.ShapeDtypeStruct(unit, low),
            jax.ShapeDtypeStruct((4 * wide, 2 * deep), low),
        )
        + tuple(whole(item) for item in pieces),
        in_specs=[VM] + [HB] * (10 + count),
        out_specs=(VM,) * (5 + count),
        scratch_shapes=[
            pltpu.VMEM((3, heads, HEAD_DIM, n * own), low),
            pltpu.VMEM(weight.shape, low),
            pltpu.VMEM(hidden.shape, low),
            pltpu.VMEM(tokens.shape, low),
            pltpu.VMEM((own, cols), f32),
            pltpu.VMEM((n, own, cols), low),
            pltpu.VMEM((own, cols), f32),
            pltpu.VMEM(unit, low),
            pltpu.VMEM((2, 2, unit[1] // 4, cols // 2), low),
            DMA((2, nc)),
            DMA((2, nc)),
            DMA,
            DMA((9,)),
            pltpu.VMEM((n, own, cols), low),
            pltpu.VMEM((own, cols), f32),
            pltpu.VMEM((own, cols), f32),
            pltpu.VMEM((cols,), f32),
            pltpu.VMEM((cols,), f32),
            pltpu.VMEM(vectors.shape, f32),
        ]
        + LineScatter.scratch(n, own, cols, low)
        + LineScatter.scratch(n, own // 2, cols, low) * 2
        + StripSum.reduce_scratch(unit, low)
        + PlaneSum.spread_scratch()
        + [item for _ in pieces for item in PlaneSum.spread_scratch()]
        + [pltpu.VMEM((n, wide, deep), low), DMA((n,)), DMA((n,)), DMA, pltpu.VMEM((wide, deep), low)]
        + [DMA((8,)), DMA((8,)), DMA, pltpu.VMEM((2,) + vectors.shape, f32)]
        + [pltpu.VMEM((size,) + vectors.shape, f32) for size in (n, 2 * nc)]
        + [DMA((size,)) for size in (n, 2 * nc) for _ in range(2)],
        compiler_params=remote_params(collective_id, 32),
    )(
        x, weight, hidden, attend_pieces, feed.reshape(n, own, cols), middle, bias,
        *pieces, tokens, gain, grad_middle, vectors,
    )
    return result[:5] + (result[5:],)


class LineGather:
    def __init__(self, n, x, o, send, recv):
        self.n, self.x, self.o, self.send, self.recv = n, x, o, send, recv
        self.me = lax.axis_index("tensor")

    def copy(self, d, s):
        me, n = self.me, self.n
        shard = jnp.clip(me - s if d == 0 else me + s, 0, n - 1)
        return pltpu.make_async_remote_copy(
            src_ref=self.x if s == 0 else self.o.at[shard],
            dst_ref=self.o.at[shard],
            send_sem=self.send.at[d, s],
            recv_sem=self.recv.at[d, s],
            device_id={"tensor": jnp.clip(me + 1 if d == 0 else me - 1, 0, n - 1)},
            device_id_type=MESH,
        )

    def sends(self, d, s):
        me, n = self.me, self.n
        return (me - s >= 0) & (me < n - 1) if d == 0 else (me + s < n) & (me > 0)

    def wait(self, d, s):
        me, n = self.me, self.n

        @pl.when(me - 1 - s >= 0 if d == 0 else me + 1 + s < n)
        def _():
            shard = jnp.clip(me - 1 - s if d == 0 else me + 1 + s, 0, n - 1)
            pltpu.make_async_copy(self.o.at[shard], self.o.at[shard], self.recv.at[d, s]).wait()

    def step(self, s):
        for d in range(2):
            if s > 0:
                self.wait(d, s - 1)

            @pl.when(self.sends(d, s))
            def _():
                self.copy(d, s).start()

    def pass_on(self, d, s, now):
        @pl.when(self.sends(d, s) & now)
        def _():
            self.copy(d, s).start()

    def last(self):
        for d in range(2):
            self.wait(d, self.n - 2)

    def finish(self, steps=None):
        for d in range(2):
            for s in range(steps or self.n - 1):

                @pl.when(self.sends(d, s))
                def _():
                    self.copy(d, s).wait_send()


def start_kernel(n, nc, heads, t_hbm, gain_hbm, shift_hbm, full_ref, w_hbm, b_hbm, c_ref, o_hbm, f_ref, q_ref, g_ref, *rest):
    (x_ref, held, proj, w_ref, o_ref, t_ref, gain_ref, shift_ref, b_ref, win), rest = rest[:10], rest[10:]
    arrive = copies(((t_hbm, t_ref), (gain_hbm, gain_ref), (shift_hbm, shift_ref), (b_hbm, b_ref)), win)
    for item in arrive:
        item.start()
    s1, r1, s2, r2, s5, r5, s3, r3, s4, r4, loc = rest
    me, ctx, x = lax.axis_index("tensor"), lax.axis_index("context"), lax.axis_index("dp")
    core, y = lax.rem(ctx, 2), lax.div(ctx, 2)
    rows, width = t_ref.shape
    half = 2 * rows
    bar = pltpu.get_barrier_semaphore()
    met = line_greet(bar, me, n)
    for shift in range(1, nc):
        pl.semaphore_signal(bar, inc=1, device_id={"context": lax.rem(ctx + shift, nc)}, device_id_type=MESH)
    pl.semaphore_signal(bar, inc=1, device_id={"dp": 1 - x}, device_id_type=MESH)
    weight_in = pltpu.make_async_copy(w_hbm, w_ref, loc.at[4])
    weight_in.start()
    for item in arrive:
        item.wait()
    normed, _ = norm_parts(t_ref[...].astype(jnp.float32))
    x_ref[...] = (normed * row(gain_ref) + row(shift_ref)).astype(x_ref.dtype)
    pl.semaphore_wait(bar, met + nc)

    tall, deep = held.shape[1:]
    strip = pl.ds(pl.multiple_of(core * deep, 128), deep)
    piece = full_ref.at[pl.ds(pl.multiple_of((2 * y + x) * tall, 16), tall), strip]
    small = LineGather(n, piece, held, s1, r1)
    large = LineGather(n, x_ref, o_ref, s2, r2)
    grads = LineGather(n, c_ref, g_ref, s5, r5)
    def move(s):
        large.step(s)
        for d in range(2):
            grads.pass_on(d, 0, me == (s if d == 0 else n - 1 - s))

    small.step(0)
    move(0)
    own = pltpu.make_async_copy(x_ref, o_ref.at[me], loc.at[0])
    own.start()
    mine = pltpu.make_async_copy(piece, held.at[me], loc.at[1])
    mine.start()
    mine.wait()
    own.wait()
    for s in range(1, n - 1):
        small.step(s)
    small.last()

    def there(y_, x_):
        return f_ref.at[:, pl.ds(pl.multiple_of((2 * y_ + x_) * tall, 16), tall), strip]

    x_peer, y_peer = {"dp": 1 - x}, {"context": lax.rem(ctx + 2, 4)}

    def hop(at):
        src, dst, peer = [
            (held, there(y, x), x_peer),
            (held, there(y, x), y_peer),
            (there(y, 1 - x), there(y, 1 - x), y_peer),
            (f_ref.at[:, :, strip], f_ref.at[:, :, strip], {"context": ctx + 1 - 2 * core}),
        ][at]
        return pltpu.make_async_remote_copy(
            src_ref=src,
            dst_ref=dst,
            send_sem=s3.at[at],
            recv_sem=r3.at[at],
            device_id=peer,
            device_id_type=MESH,
        )

    def got(at):
        other = pl.ds(pl.multiple_of((1 - core) * deep, 128), deep)
        ref = [there(y, 1 - x), there(1 - y, x), there(1 - y, 1 - x), f_ref.at[:, :, other]][at]
        pltpu.make_async_copy(ref, ref, r3.at[at]).wait()

    hop(0).start()
    kept = pltpu.make_async_copy(held, there(y, x), loc.at[2])
    kept.start()

    def columns(pair):
        return pl.ds(pl.multiple_of(pair * half, 128), half)

    def project(pair):
        token = jnp.concatenate([o_ref[2 * pair], o_ref[2 * pair + 1]], axis=0)
        for kind in range(3):
            value = dot(w_ref[kind], token, ((1,), (1,))) + b_ref[kind]
            proj[kind, :, :, columns(pair)] = value.astype(proj.dtype).reshape(heads, HEAD_DIM, half)

    def ship(index, pair, shift):
        other = lax.rem(ctx + shift, nc)
        return other, pltpu.make_async_remote_copy(
            src_ref=proj.at[:, jnp.minimum(other, heads - 1), :, columns(pair)],
            dst_ref=q_ref.at[ctx, :, :, columns(pair)],
            send_sem=s4.at[index, shift],
            recv_sem=r4.at[index, shift],
            device_id={"context": other},
            device_id_type=MESH,
        )

    def ship_all(index, pair):
        for shift in range(1, nc):
            other, item = ship(index, pair, shift)

            @pl.when(other < heads)
            def _():
                item.start()

    near = lax.div(me, 2)
    move(1)
    weight_in.wait()
    project(near)
    ship_all(0, near)
    hop(1).start()
    for s in range(2, n - 1):
        move(s)
    got(0)
    hop(2).start()
    large.last()
    project(1 - near)
    ship_all(1, 1 - near)
    result = pltpu.make_async_copy(o_ref, o_hbm, loc.at[5])
    result.start()
    stay = pltpu.make_async_copy(proj.at[:, jnp.minimum(ctx, heads - 1)], q_ref.at[ctx], loc.at[3])
    stay.start()
    kept.wait()
    got(1)
    got(2)
    hop(3).start()
    for d in range(2):
        grads.wait(d, 0)
        grads.pass_on(d, 1, me >= 0)
    stay.wait()

    @pl.when(ctx < heads)
    def _():
        for index in range(2):
            for shift in range(1, nc):
                source = lax.rem(ctx + nc - shift, nc)
                pair = near if index == 0 else 1 - near
                ref = q_ref.at[source, :, :, columns(pair)]
                pltpu.make_async_copy(ref, ref, r4.at[index, shift]).wait()

    got(3)
    for d in range(2):
        grads.wait(d, 1)
    result.wait()
    small.finish()
    large.finish()
    grads.finish(2)
    for at in range(4):
        hop(at).wait_send()
    for index in range(2):
        for shift in range(1, nc):
            other, item = ship(index, near if index == 0 else 1 - near, shift)

            @pl.when(other < heads)
            def _():
                item.wait_send()


def start_part(tokens, gain, shift, w, project_weight, bias, cotangent, n, nc, heads, collective_id):
    rows, cols = tokens.shape
    wide, deep = w.shape
    low = jnp.bfloat16
    full, weight, qkv, grads = pl.pallas_call(
        functools.partial(start_kernel, n, nc, heads),
        out_shape=(
            jax.ShapeDtypeStruct((n, rows, cols), low),
            jax.ShapeDtypeStruct((n, wide, deep), w.dtype),
            jax.ShapeDtypeStruct((nc, 3, HEAD_DIM, n * rows), low),
            jax.ShapeDtypeStruct((n, rows, cols), low),
        ),
        in_specs=[HB] * 7,
        out_specs=(HB, VM, VM, VM),
        scratch_shapes=[
            pltpu.VMEM((rows, cols), low),
            pltpu.VMEM((n, wide // 4, deep // 2), w.dtype),
            pltpu.VMEM((3, heads, HEAD_DIM, n * rows), low),
            pltpu.VMEM(project_weight.shape, low),
            pltpu.VMEM((n, rows, cols), low),
            pltpu.VMEM((rows, cols), tokens.dtype),
            pltpu.VMEM(gain.shape, jnp.float32),
            pltpu.VMEM(shift.shape, jnp.float32),
            pltpu.VMEM(bias.shape, jnp.float32),
            DMA((4,)),
        ]
        + [DMA((2, n - 1)) for _ in range(6)]
        + [DMA((4,)), DMA((4,)), DMA((2, nc)), DMA((2, nc)), DMA((6,))],
        compiler_params=remote_params(collective_id, 56),
    )(tokens, gain, shift, w, project_weight, bias, cotangent)
    return full.reshape(n * rows, cols), weight.reshape(n * wide, deep), qkv, grads


def dot(left, right, dims):
    return lax.dot_general(left, right, ((dims[0], dims[1]), ((), ())), preferred_element_type=jnp.float32)


def key_positions(first, keys, queries):
    return first + lax.broadcasted_iota(jnp.int32, (keys, queries), 0)


def load_rows(qkv_ref, nb, half, qs, kt, ks, vs):
    for block in range(nb):
        part = slice(block % 2 * half, block % 2 * half + half)
        at = block // 2
        qs[block] = qkv_ref[at, 0, :, part] * jnp.asarray(HEAD_DIM**-0.5, qs.dtype)
        item = qkv_ref[at, 1, :, part]
        if kt is not None:
            kt[block] = item
        ks[block] = item.T
        if vs is not None:
            vs[block] = qkv_ref[at, 2, :, part].T


def fill_tables(nb, half, seg_ref, order_ref, slot_ref, low_ref, high_ref):
    for block in range(nb):
        slot_ref[order_ref[block]] = jnp.int32(block)
    first = [seg_ref[0, block * half] for block in range(nb)]
    last = [seg_ref[0, block * half + half - 1] for block in range(nb)]
    for block in range(nb):
        if low_ref is not None:
            low_ref[block] = sum(jnp.where(item < first[block], 1, 0) for item in last)
        if high_ref is not None:
            high_ref[block] = sum(jnp.where(item <= last[block], 1, 0) for item in first)


def forward_kernel(half, heads, seg_s, order_ref, seg_ref, qkv_ref, o_ref, full_ref, lse_ref, start_ref, qs, ks, slot_ref, low_ref):
    nb = full_ref.shape[0]

    @pl.when(lax.axis_index("context") < heads)
    def _():
        load_rows(qkv_ref, nb, half, qs, None, ks, None)
        fill_tables(nb, half, seg_s, order_ref, slot_ref, low_ref, None)
        seg = seg_ref[...]
        start = jnp.zeros(seg.shape, jnp.float32)
        for doc in range(1, DOC_LIMIT):
            before = jnp.sum(jnp.where(seg < doc, 1.0, 0.0), axis=1, keepdims=True)
            start = jnp.where(seg == doc, before, start)
        start_ref[...] = start.astype(jnp.int32)

        @pl.loop(0, nb)
        def _(nq):
            slot = slot_ref[nq]
            query = qs[slot]
            begin = start_ref[:, pl.ds(pl.multiple_of(nq * half, 128), half)]
            here = nq * half + lax.broadcasted_iota(jnp.int32, (1, half), 1)

            def step(nk, state):
                top, total, acc = state
                at = slot_ref[nk]
                score = dot(ks[at], query, ((1,), (0,)))
                place = key_positions(nk * half, half, half)
                score = jnp.where((place >= begin) & (place <= here), score, NEG_FILL)
                new_top = jnp.maximum(top, jnp.max(score, axis=0, keepdims=True))
                factor = jnp.exp(top - new_top)
                weight = jnp.exp(score - new_top)
                total = total * factor + jnp.sum(weight, axis=0, keepdims=True)
                value = qkv_ref[at // 2, 2, :, pl.ds(pl.multiple_of(at % 2 * half, 128), half)]
                acc = acc * factor + dot(value, weight.astype(jnp.bfloat16), ((1,), (0,)))
                return new_top, total, acc

            top, total, acc = lax.fori_loop(
                low_ref[nq],
                nq + 1,
                step,
                (
                    jnp.full((1, half), NEG_FILL, jnp.float32),
                    jnp.zeros((1, half), jnp.float32),
                    jnp.zeros((HEAD_DIM, half), jnp.float32),
                ),
            )
            result = acc / total
            full_ref[slot] = result
            lse_ref[slot] = top + jnp.log(total)
            low = result.astype(jnp.bfloat16)
            o_ref[2 * slot] = low[:, : half // 2]
            o_ref[2 * slot + 1] = low[:, half // 2 :]


def attend_forward(qkv, segments, order, half, heads):
    nc = qkv.shape[0]
    nb = 2 * nc
    return pl.pallas_call(
        functools.partial(forward_kernel, half, heads),
        out_shape=(
            jax.ShapeDtypeStruct((2 * nb, HEAD_DIM, half // 2), jnp.bfloat16),
            jax.ShapeDtypeStruct((nb, HEAD_DIM, half), jnp.float32),
            jax.ShapeDtypeStruct((nb, 1, half), jnp.float32),
            jax.ShapeDtypeStruct(segments.shape, jnp.int32),
        ),
        in_specs=[SM, SM, VM, VM],
        out_specs=(VM, VM, VM, VM),
        scratch_shapes=[
            pltpu.VMEM((nb, HEAD_DIM, half), jnp.bfloat16),
            pltpu.VMEM((nb, half, HEAD_DIM), jnp.bfloat16),
            pltpu.SMEM((nb,), jnp.int32),
            pltpu.SMEM((nb,), jnp.int32),
        ],
        compiler_params=pltpu.CompilerParams(vmem_limit_bytes=24 << 20),
    )(segments, order, segments, qkv)


def backward_kernel(
    half, heads, seg_s, order_ref, start_ref, qkv_ref, full_ref, lse_ref, grad_ref, o_ref,
    qs, kt, ks, vs, gs, ds, dq, slot_ref, high_ref,
):
    nb = full_ref.shape[0]

    @pl.when(lax.axis_index("context") < heads)
    def _():
        load_rows(qkv_ref, nb, half, qs, kt, ks, vs)
        fill_tables(nb, half, seg_s, order_ref, slot_ref, None, high_ref)
        for block in range(nb):
            both = jnp.concatenate([grad_ref[2 * block], grad_ref[2 * block + 1]], axis=1)
            gs[block] = both
            ds[block] = jnp.sum(both.astype(jnp.float32) * full_ref[block], axis=0, keepdims=True)
            dq[block] = jnp.zeros((HEAD_DIM, half), jnp.float32)

        @pl.loop(0, nb)
        def _(nk):
            at = slot_ref[nk]
            place = key_positions(nk * half, half, half)

            def step(nq, state):
                grad_key, grad_value = state
                slot = slot_ref[nq]
                query, grad = qs[slot], gs[slot]
                begin = start_ref[:, pl.ds(pl.multiple_of(nq * half, 128), half)]
                here = nq * half + lax.broadcasted_iota(jnp.int32, (1, half), 1)
                score = dot(ks[at], query, ((1,), (0,)))
                score = jnp.where((place >= begin) & (place <= here), score, NEG_FILL)
                weight = jnp.exp(score - lse_ref[slot])
                grad_weight = dot(vs[at], grad, ((1,), (0,)))
                grad_score = (weight * (grad_weight - ds[slot])).astype(jnp.bfloat16)
                grad_value = grad_value + dot(grad, weight.astype(jnp.bfloat16), ((1,), (1,)))
                grad_key = grad_key + dot(query, grad_score, ((1,), (1,)))
                dq[slot] += dot(kt[at], grad_score, ((1,), (0,)))
                return grad_key, grad_value

            zero = jnp.zeros((HEAD_DIM, half), jnp.float32)
            grad_key, grad_value = lax.fori_loop(nk, high_ref[nk], step, (zero, zero))
            columns = pl.ds(pl.multiple_of(at % 2 * half, 128), half)
            o_ref[at // 2, 1, :, columns] = grad_key.astype(jnp.bfloat16)
            o_ref[at // 2, 2, :, columns] = grad_value.astype(jnp.bfloat16)

        for block in range(nb):
            part = slice(block % 2 * half, block % 2 * half + half)
            o_ref[block // 2, 0, :, part] = (dq[block] * HEAD_DIM**-0.5).astype(jnp.bfloat16)


def attend_backward(qkv, segments, order, start, full, lse, grad, half, heads):
    nc = qkv.shape[0]
    nb = 2 * nc
    low = jnp.bfloat16
    return pl.pallas_call(
        functools.partial(backward_kernel, half, heads),
        out_shape=jax.ShapeDtypeStruct(qkv.shape, low),
        in_specs=[SM, SM, VM, VM, VM, VM, VM],
        out_specs=VM,
        scratch_shapes=[
            pltpu.VMEM((nb, HEAD_DIM, half), low),
            pltpu.VMEM((nb, HEAD_DIM, half), low),
            pltpu.VMEM((nb, half, HEAD_DIM), low),
            pltpu.VMEM((nb, half, HEAD_DIM), low),
            pltpu.VMEM((nb, HEAD_DIM, half), low),
            pltpu.VMEM((nb, 1, half), jnp.float32),
            pltpu.VMEM((nb, HEAD_DIM, half), jnp.float32),
            pltpu.SMEM((nb,), jnp.int32),
            pltpu.SMEM((nb,), jnp.int32),
        ],
        compiler_params=pltpu.CompilerParams(vmem_limit_bytes=24 << 20),
    )(segments, order, start, qkv, full, lse, grad)


def norm_parts(values):
    centre = jnp.mean(values, axis=-1, keepdims=True)
    shifted = values - centre
    spread_ = jnp.mean(shifted * shifted, axis=-1, keepdims=True)
    scale = lax.rsqrt(spread_ + NORM_EPS)
    return shifted * scale, scale


def norm_backward(grad, normed, scale, gain):
    e = grad * gain
    mean_e = jnp.mean(e, axis=-1, keepdims=True)
    mean_en = jnp.mean(e * normed, axis=-1, keepdims=True)
    return (e - mean_e - normed * mean_en) * scale


def gelu_tanh(values):
    return jax.nn.gelu(values, approximate=True)


def cross_rows(left, right):
    return lax.dot_general(
        left, right, (((0,), (0,)), ((), ())), preferred_element_type=jnp.float32
    )


def after(value, done):
    return lax.optimization_barrier((value, done))[0]


def per_device(
    mesh_sizes,
    inputs,
    first_gain,
    first_shift,
    project_weight,
    project_bias,
    attend_weight,
    attend_bias,
    second_gain,
    second_shift,
    expand_weight,
    expand_bias,
    shrink_weight,
    shrink_bias,
    segments,
    block_order,
    cotangent,
):
    nt, nc = mesh_sizes["tensor"], mesh_sizes["context"]
    own_rows, width = inputs.shape[1], inputs.shape[2]
    local_width = project_weight.shape[2]
    heads = local_width // HEAD_DIM
    block_rows = own_rows * nt
    half = block_rows // 2
    low = jnp.bfloat16
    f32 = lambda value: value.astype(jnp.float32)
    square = nt == 4 and nc == 4 and mesh_sizes["dp"] == 2
    plane = ("context", "dp")

    tokens_own = f32(inputs[0])
    grad_out = cotangent[0]
    bias = jnp.stack([project_bias[0], jnp.zeros_like(project_bias[0]), project_bias[1]])[:, :, None]
    weight_rows = project_weight.transpose(0, 2, 1)
    if square:
        hidden1_full, attend_full, qkv, grads_near = start_part(
            inputs[0], first_gain, first_shift, attend_weight, weight_rows, bias, grad_out, nt, nc, heads, 0
        )
        pieces, attended_full, lse, start = attend_forward(qkv, segments, block_order, half, heads)
        feed, *feed_pieces, middle, grad_middle, vectors, attend_pieces, grad_heads = feed_part(
            pieces,
            inputs[0],
            attend_full,
            (attend_bias, second_gain, second_shift),
            expand_weight,
            shrink_weight,
            expand_bias,
            grads_near,
            grad_out,
            nt,
            nc,
            heads,
            3,
        )
        grad_qkv = attend_backward(
            qkv, segments, block_order, start, attended_full, lse, grad_heads, half, heads
        )
        outputs, grad_inputs, summed, grad_project, grad_attend, feeds = last_part(
            grad_qkv,
            weight_rows,
            hidden1_full,
            attend_pieces,
            feed,
            middle,
            shrink_bias,
            feed_pieces,
            inputs[0],
            first_gain,
            grad_middle,
            vectors,
            6,
            nt,
            heads,
            7,
        )
        grad_project = grad_project.transpose(0, 2, 1)
        grad_shrink, grad_expand = feeds[0].reshape(-1, width), feeds[1].reshape(width, -1)
        wide = expand_bias.shape[0]
    else:
        hidden1 = norm_parts(tokens_own)[0] * first_gain + first_shift
        hidden1_full = gather_rows(hidden1.astype(low), nt, 0)
        attend_full = lax.all_gather(attend_weight, "tensor", axis=0, tiled=True)
        projected = jnp.einsum(
            "ked,rd->ker", weight_rows, hidden1_full, preferred_element_type=jnp.float32
        )
        projected = (projected + bias).astype(low).reshape(3, heads, HEAD_DIM, block_rows)
        qkv = to_heads(projected, nc, 1)
        pieces, attended_full, lse, start = attend_forward(qkv, segments, block_order, half, heads)
        grad_full = lax.all_gather(grad_out, "tensor", axis=0, tiled=True)
        attended = to_rows(pieces, nc, nt, heads, 2).reshape(width, own_rows)
        middle = tokens_own + cross_rows(attended, attend_full) + attend_bias
        normed2, scale2 = norm_parts(middle)
        hidden2 = (normed2 * second_gain + second_shift).astype(low)
        hidden2_full = gather_rows(hidden2, nt, 3)
        pre_act = jnp.dot(hidden2_full, expand_weight, preferred_element_type=jnp.float32) + expand_bias
        activ = gelu_tanh(pre_act).astype(low)
        grad_act = dot(grad_full, shrink_weight, ((1,), (1,)))
        grad_pre = jax.vjp(gelu_tanh, pre_act)[1](grad_act)[0].astype(low)
        grad_shrink = cross_rows(activ, grad_full).astype(low)
        grad_expand = cross_rows(hidden2_full, grad_pre).astype(low)
        grad_hidden2 = scatter_rows(dot(grad_pre, expand_weight, ((1,), (1,))).astype(low), nt, 4)
        grad_expand_bias = jnp.sum(f32(grad_pre), axis=0)
        feed = jnp.dot(activ, shrink_weight, preferred_element_type=jnp.float32).astype(low)

        grad_shrink_bias = jnp.sum(f32(grad_out), axis=0)
        grad_second_gain = jnp.sum(grad_hidden2 * normed2, axis=0)
        grad_second_shift = jnp.sum(grad_hidden2, axis=0)
        grad_middle = f32(grad_out) + norm_backward(grad_hidden2, normed2, scale2, second_gain)
        grad_middle_low = grad_middle.astype(low)
        grad_attend_bias = jnp.sum(f32(grad_middle_low), axis=0)
        grad_attended = dot(attend_full, grad_middle_low, ((1,), (1,))).astype(low)
        grad_attended = grad_attended.reshape(nt * heads, HEAD_DIM, own_rows)
        grad_attend = jnp.dot(attended, grad_middle_low, preferred_element_type=jnp.float32).astype(low)
        grad_heads = rows_back(grad_attended, nc, nt, heads, 5)
        feed_sum = lax.psum_scatter(after(feed, grad_heads), "tensor", scatter_dimension=0, tiled=True)

        grad_qkv = attend_backward(
            qkv, segments, block_order, start, attended_full, lse, grad_heads, half, heads
        )
        grad_rows = from_heads(grad_qkv, nc, heads, 6).reshape(3 * local_width, block_rows)
        grad_project = dot(hidden1_full, grad_rows, ((0,), (1,))).astype(low)
        grad_hidden1 = cross_rows(grad_rows, weight_rows.reshape(3 * local_width, width)).astype(low)
        row_sums = jnp.sum(f32(grad_rows), axis=1)
        grad_project_bias = jnp.concatenate([row_sums[:local_width], row_sums[2 * local_width :]])
        grad_hidden1 = scatter_rows(grad_hidden1, nt, 7)
        normed1, scale1 = norm_parts(tokens_own)
        back = norm_backward(grad_hidden1, normed1, scale1, first_gain)
        grad_inputs = (grad_middle + back).astype(low)
        wide = grad_expand_bias.shape[0]
        vectors = jnp.concatenate(
            [
                jnp.sum(grad_hidden1 * normed1, axis=0),
                jnp.sum(grad_hidden1, axis=0),
                grad_attend_bias,
                grad_second_gain,
                grad_second_shift,
                grad_shrink_bias,
                grad_expand_bias,
                jnp.pad(grad_project_bias, (0, -(wide + 2 * local_width) % width)),
            ]
        ).reshape(-1, width)
        summed = sum_vectors(vectors, 6, mesh_sizes, 8)
        grad_attend = lax.psum_scatter(grad_attend, "tensor", scatter_dimension=0, tiled=True)
        grad_project, grad_attend, grad_shrink, grad_expand = lax.psum(
            (grad_project, grad_attend, grad_shrink, grad_expand), plane
        )
        grad_project = jnp.stack(
            [grad_project[:, at * local_width : (at + 1) * local_width] for at in range(3)]
        )
        outputs = (middle + f32(feed_sum) + shrink_bias).astype(low)
    tail = summed[6:].reshape(-1)
    return (
        outputs[None],
        grad_inputs[None],
        summed[0],
        summed[1],
        f32(grad_project),
        tail[wide : wide + 2 * local_width].reshape(2, local_width),
        f32(grad_attend),
        summed[2],
        summed[3],
        summed[4],
        f32(grad_expand),
        tail[:wide],
        f32(grad_shrink),
        summed[5],
    )


def solution(mesh):
    rows = P("dp", ("context", "tensor"), None)
    in_specs = (
        rows,
        P(),
        P(),
        P(None, None, "tensor"),
        P(None, "tensor"),
        P("tensor", None),
        P(),
        P(),
        P(),
        P(None, "tensor"),
        P("tensor"),
        P("tensor", None),
        P(),
        P("dp", None),
        P(),
        rows,
    )
    out_specs = (
        rows,
        rows,
        P(),
        P(),
        P(None, None, "tensor"),
        P(None, "tensor"),
        P("tensor", None),
        P(),
        P(),
        P(),
        P(None, "tensor"),
        P("tensor"),
        P("tensor", None),
        P(),
    )
    return jax.shard_map(
        functools.partial(per_device, dict(mesh.shape)),
        mesh=mesh,
        in_specs=in_specs,
        out_specs=out_specs,
        check_vma=False,
    )
```

```python
import functools

import jax
import jax.numpy as jnp
from jax import lax
from jax.experimental import pallas as pl
from jax.experimental.pallas import tpu as pltpu
from jax.sharding import PartitionSpec as P

HEAD_DIM = 64
NEG_FILL = -1e30
NORM_EPS = 1e-05
DOC_LIMIT = 16
MESH = pl.DeviceIdType.MESH
VM = pl.BlockSpec(memory_space=pltpu.VMEM)
SM = pl.BlockSpec(memory_space=pltpu.SMEM)
DMA = pltpu.SemaphoreType.DMA


def remote_params(collective_id, mib=16):
    return pltpu.CompilerParams(
        collective_id=collective_id, has_side_effects=True, vmem_limit_bytes=mib << 20
    )


HB = pl.BlockSpec(memory_space=pltpu.HBM)


def copies(pairs, sems):
    return [pltpu.make_async_copy(src, dst, sems.at[at]) for at, (src, dst) in enumerate(pairs)]


def row(ref):
    return ref[...].reshape(1, -1)


def line_barrier(me, n):
    bar = pltpu.get_barrier_semaphore()

    @pl.when(me > 0)
    def _():
        pl.semaphore_signal(bar, inc=1, device_id={"tensor": me - 1}, device_id_type=MESH)

    @pl.when(me < n - 1)
    def _():
        pl.semaphore_signal(bar, inc=1, device_id={"tensor": me + 1}, device_id_type=MESH)

    pl.semaphore_wait(bar, jnp.where(me > 0, 1, 0) + jnp.where(me < n - 1, 1, 0))


def gather_kernel(n, x_ref, o_ref, send, recv, loc):
    me = lax.axis_index("tensor")
    line_barrier(me, n)
    own = pltpu.make_async_copy(x_ref, o_ref.at[me], loc)
    own.start()

    def copy(d, s):
        shard = jnp.clip(me - s if d == 0 else me + s, 0, n - 1)
        return pltpu.make_async_remote_copy(
            src_ref=x_ref if s == 0 else o_ref.at[shard],
            dst_ref=o_ref.at[shard],
            send_sem=send.at[d, s],
            recv_sem=recv.at[d, s],
            device_id={"tensor": jnp.clip(me + 1 if d == 0 else me - 1, 0, n - 1)},
            device_id_type=MESH,
        )

    def sends(d, s):
        return (me - s >= 0) & (me < n - 1) if d == 0 else (me + s < n) & (me > 0)

    def gets(d, s):
        return me - 1 - s >= 0 if d == 0 else me + 1 + s < n

    def landed(d, s):
        shard = jnp.clip(me - 1 - s if d == 0 else me + 1 + s, 0, n - 1)
        return pltpu.make_async_copy(o_ref.at[shard], o_ref.at[shard], recv.at[d, s])

    for s in range(n - 1):
        for d in range(2):
            if s > 0:

                @pl.when(gets(d, s - 1))
                def _():
                    landed(d, s - 1).wait()

            @pl.when(sends(d, s))
            def _():
                copy(d, s).start()

    for d in range(2):

        @pl.when(gets(d, n - 2))
        def _():
            landed(d, n - 2).wait()

        for s in range(n - 1):

            @pl.when(sends(d, s))
            def _():
                copy(d, s).wait_send()

    own.wait()


def gather_rows(x, n, collective_id):
    rows, cols = x.shape
    return pl.pallas_call(
        functools.partial(gather_kernel, n),
        out_shape=jax.ShapeDtypeStruct((n, rows, cols), x.dtype),
        in_specs=[VM],
        out_specs=VM,
        scratch_shapes=[DMA((2, n - 1)), DMA((2, n - 1)), DMA],
        compiler_params=remote_params(collective_id),
    )(x).reshape(n * rows, cols)


def scatter_kernel(n, x_ref, o_ref, buf, tmp, send, recv):
    me = lax.axis_index("tensor")
    line_barrier(me, n)

    def term(d, k):
        return n - 1 - k if d == 0 else k

    def sends(d, k):
        return me < n - 1 - k if d == 0 else me > k

    def behind(d):
        return me > 0 if d == 0 else me < n - 1

    def copy(d, k, first):
        return pltpu.make_async_remote_copy(
            src_ref=x_ref.at[term(d, k)] if first else tmp.at[d, k],
            dst_ref=buf.at[d, k],
            send_sem=send.at[d, k],
            recv_sem=recv.at[d, k],
            device_id={"tensor": jnp.clip(me + 1 if d == 0 else me - 1, 0, n - 1)},
            device_id_type=MESH,
        )

    def landed(d, k):
        return pltpu.make_async_copy(buf.at[d, k], buf.at[d, k], recv.at[d, k])

    for d in range(2):

        @pl.when(jnp.logical_not(behind(d)))
        def _():
            for k in range(n - 1):
                copy(d, k, True).start()

    for k in range(n - 1):
        for d in range(2):

            @pl.when(behind(d) & sends(d, k))
            def _():
                landed(d, k).wait()
                both = buf[d, k].astype(jnp.float32) + x_ref[term(d, k)].astype(jnp.float32)
                tmp[d, k] = both.astype(tmp.dtype)
                copy(d, k, False).start()

    o_ref[...] = x_ref[me].astype(jnp.float32)
    for d in range(2):
        for k in range(n - 1):

            @pl.when(behind(d) & (me == term(d, k)))
            def _():
                landed(d, k).wait()
                o_ref[...] += buf[d, k].astype(jnp.float32)

    for d in range(2):
        for k in range(n - 1):

            @pl.when(sends(d, k))
            def _():
                copy(d, k, False).wait_send()


def scatter_rows(x, n, collective_id):
    rows, cols = x.shape
    own = rows // n
    return pl.pallas_call(
        functools.partial(scatter_kernel, n),
        out_shape=jax.ShapeDtypeStruct((own, cols), jnp.float32),
        in_specs=[VM],
        out_specs=VM,
        scratch_shapes=[
            pltpu.VMEM((2, n - 1, own, cols), x.dtype),
            pltpu.VMEM((2, n - 1, own, cols), x.dtype),
            DMA((2, n - 1)),
            DMA((2, n - 1)),
        ],
        compiler_params=remote_params(collective_id),
    )(x.reshape(n, own, cols))


def group_barrier(axes, sizes):
    mine = [lax.axis_index(name) for name in axes]
    place = sum_index(mine, sizes)
    total = 1
    for size in sizes:
        total *= size
    bar = pltpu.get_barrier_semaphore()
    for shift in range(1, total):
        other = lax.rem(place + shift, total)
        pl.semaphore_signal(bar, inc=1, device_id=spread(other, axes, sizes), device_id_type=MESH)
    pl.semaphore_wait(bar, total - 1)
    return place, total


def sum_index(mine, sizes):
    place = 0
    for at, size in zip(mine, sizes):
        place = place * size + at
    return place


def spread(place, axes, sizes):
    found = {}
    for name, size in reversed(tuple(zip(axes, sizes))):
        found[name] = lax.rem(place, size)
        place = lax.div(place, size)
    return found


def to_heads_kernel(nc, heads, x_ref, o_ref, send, recv, loc):
    me, _ = group_barrier(("context",), (nc,))

    def copy(shift):
        other = lax.rem(me + shift, nc)
        return other, pltpu.make_async_remote_copy(
            src_ref=x_ref.at[:, jnp.minimum(other, heads - 1)],
            dst_ref=o_ref.at[me],
            send_sem=send.at[shift],
            recv_sem=recv.at[shift],
            device_id={"context": other},
            device_id_type=MESH,
        )

    for shift in range(1, nc):
        other, item = copy(shift)

        @pl.when(other < heads)
        def _():
            item.start()

    own = pltpu.make_async_copy(x_ref.at[:, jnp.minimum(me, heads - 1)], o_ref.at[me], loc)
    own.start()
    own.wait()

    @pl.when(me < heads)
    def _():
        for shift in range(1, nc):
            source = lax.rem(me + nc - shift, nc)
            pltpu.make_async_copy(o_ref.at[source], o_ref.at[source], recv.at[shift]).wait()

    for shift in range(1, nc):
        other, item = copy(shift)

        @pl.when(other < heads)
        def _():
            item.wait_send()


def to_heads(x, nc, collective_id):
    heads = x.shape[1]
    return pl.pallas_call(
        functools.partial(to_heads_kernel, nc, heads),
        out_shape=jax.ShapeDtypeStruct((nc, x.shape[0]) + x.shape[2:], x.dtype),
        in_specs=[VM],
        out_specs=VM,
        scratch_shapes=[DMA((nc,)), DMA((nc,)), DMA],
        compiler_params=remote_params(collective_id),
    )(x)


def from_heads_kernel(nc, heads, x_ref, o_ref, send, recv, loc):
    me, _ = group_barrier(("context",), (nc,))

    def copy(shift):
        other = lax.rem(me + shift, nc)
        return pltpu.make_async_remote_copy(
            src_ref=x_ref.at[other],
            dst_ref=o_ref.at[:, jnp.minimum(me, heads - 1)],
            send_sem=send.at[shift],
            recv_sem=recv.at[shift],
            device_id={"context": other},
            device_id_type=MESH,
        )

    @pl.when(me < heads)
    def _():
        for shift in range(1, nc):
            copy(shift).start()
        own = pltpu.make_async_copy(x_ref.at[me], o_ref.at[:, me], loc)
        own.start()
        own.wait()

    for shift in range(1, nc):
        source = lax.rem(me + nc - shift, nc)

        @pl.when(source < heads)
        def _():
            at = jnp.minimum(source, heads - 1)
            pltpu.make_async_copy(o_ref.at[:, at], o_ref.at[:, at], recv.at[shift]).wait()

    @pl.when(me < heads)
    def _():
        for shift in range(1, nc):
            copy(shift).wait_send()


def from_heads(x, nc, heads, collective_id):
    return pl.pallas_call(
        functools.partial(from_heads_kernel, nc, heads),
        out_shape=jax.ShapeDtypeStruct((x.shape[1], heads) + x.shape[2:], x.dtype),
        in_specs=[VM],
        out_specs=VM,
        scratch_shapes=[DMA((nc,)), DMA((nc,)), DMA],
        compiler_params=remote_params(collective_id),
    )(x)


AXES = ("context", "tensor")


def rows_kernel(nc, nt, heads, x_ref, o_ref, send, recv, loc):
    me, total = group_barrier(AXES, (nc, nt))
    my_ctx, my_ten = lax.axis_index("context"), lax.axis_index("tensor")
    my_head = my_ten * heads + jnp.minimum(my_ctx, heads - 1)

    def copy(shift):
        other = lax.rem(me + shift, total)
        return pltpu.make_async_remote_copy(
            src_ref=x_ref.at[other],
            dst_ref=o_ref.at[my_head],
            send_sem=send.at[shift],
            recv_sem=recv.at[shift],
            device_id=spread(other, AXES, (nc, nt)),
            device_id_type=MESH,
        )

    @pl.when(my_ctx < heads)
    def _():
        for shift in range(1, total):
            copy(shift).start()
        own = pltpu.make_async_copy(x_ref.at[me], o_ref.at[my_head], loc)
        own.start()
        own.wait()

    for shift in range(1, total):
        source = lax.rem(me + total - shift, total)
        ctx, ten = lax.div(source, nt), lax.rem(source, nt)

        @pl.when(ctx < heads)
        def _():
            at = ten * heads + jnp.minimum(ctx, heads - 1)
            pltpu.make_async_copy(o_ref.at[at], o_ref.at[at], recv.at[shift]).wait()

    @pl.when(my_ctx < heads)
    def _():
        for shift in range(1, total):
            copy(shift).wait_send()


def to_rows(x, nc, nt, heads, collective_id):
    total = nc * nt
    return pl.pallas_call(
        functools.partial(rows_kernel, nc, nt, heads),
        out_shape=jax.ShapeDtypeStruct((nt * heads,) + x.shape[1:], x.dtype),
        in_specs=[VM],
        out_specs=VM,
        scratch_shapes=[DMA((total,)), DMA((total,)), DMA],
        compiler_params=remote_params(collective_id),
    )(x)


def rows_back_kernel(nc, nt, heads, x_ref, o_ref, send, recv, loc):
    me, total = group_barrier(AXES, (nc, nt))
    my_ctx, my_ten = lax.axis_index("context"), lax.axis_index("tensor")

    def copy(shift):
        other = lax.rem(me + shift, total)
        ctx, ten = lax.div(other, nt), lax.rem(other, nt)
        return ctx < heads, pltpu.make_async_remote_copy(
            src_ref=x_ref.at[ten * heads + jnp.minimum(ctx, heads - 1)],
            dst_ref=o_ref.at[me],
            send_sem=send.at[shift],
            recv_sem=recv.at[shift],
            device_id={"context": ctx, "tensor": ten},
            device_id_type=MESH,
        )

    for shift in range(1, total):
        goes, item = copy(shift)

        @pl.when(goes)
        def _():
            item.start()

    own = pltpu.make_async_copy(
        x_ref.at[my_ten * heads + jnp.minimum(my_ctx, heads - 1)], o_ref.at[me], loc
    )
    own.start()
    own.wait()

    @pl.when(my_ctx < heads)
    def _():
        for shift in range(1, total):
            source = lax.rem(me + total - shift, total)
            pltpu.make_async_copy(o_ref.at[source], o_ref.at[source], recv.at[shift]).wait()

    for shift in range(1, total):
        goes, item = copy(shift)

        @pl.when(goes)
        def _():
            item.wait_send()


def rows_back(x, nc, nt, heads, collective_id):
    total = nc * nt
    return pl.pallas_call(
        functools.partial(rows_back_kernel, nc, nt, heads),
        out_shape=jax.ShapeDtypeStruct((total,) + x.shape[1:], x.dtype),
        in_specs=[VM],
        out_specs=VM,
        scratch_shapes=[DMA((total,)), DMA((total,)), DMA],
        compiler_params=remote_params(collective_id),
    )(x)


def vectors_kernel(names, sizes, shared, x_ref, o_ref, now, *rest):
    bufs, sems = rest[: len(names)], rest[len(names) :]
    bar = pltpu.get_barrier_semaphore()
    for name, size in zip(names, sizes):
        me = lax.axis_index(name)
        for shift in range(1, size):
            pl.semaphore_signal(
                bar, inc=1, device_id={name: lax.rem(me + shift, size)}, device_id_type=MESH
            )
    pl.semaphore_wait(bar, sum(sizes) - len(sizes))
    for stage, (name, size) in enumerate(zip(names, sizes)):
        buf, send, recv = bufs[stage], sems[2 * stage], sems[2 * stage + 1]
        me = lax.axis_index(name)

        def copy(shift):
            return pltpu.make_async_remote_copy(
                src_ref=now.at[stage] if stage else x_ref.at[0],
                dst_ref=buf.at[me],
                send_sem=send.at[shift],
                recv_sem=recv.at[shift],
                device_id={name: lax.rem(me + shift, size)},
                device_id_type=MESH,
            )

        for shift in range(1, size):
            copy(shift).start()
        buf[me] = now[stage] if stage else x_ref[0]
        for shift in range(1, size):
            source = lax.rem(me + size - shift, size)
            pltpu.make_async_copy(buf.at[source], buf.at[source], recv.at[shift]).wait()
        total = buf[0]
        for at in range(1, size):
            total = total + buf[at]
        if stage == 0:
            row = lax.broadcasted_iota(jnp.int32, total.shape, 0)
            total = jnp.where(row < shared, total, x_ref[0])
        if stage + 1 < len(names):
            now[stage + 1] = total
        else:
            o_ref[...] = total
        for shift in range(1, size):
            copy(shift).wait_send()


def sum_vectors(rows, shared, mesh_sizes, collective_id):
    names = ("tensor", "context", "dp")
    sizes = tuple(mesh_sizes[name] for name in names)
    shape = rows.shape
    return pl.pallas_call(
        functools.partial(vectors_kernel, names, sizes, shared),
        out_shape=jax.ShapeDtypeStruct(shape, jnp.float32),
        in_specs=[VM],
        out_specs=VM,
        scratch_shapes=[pltpu.VMEM((len(names),) + shape, jnp.float32)]
        + [pltpu.VMEM((size,) + shape, jnp.float32) for size in sizes]
        + [DMA((size,)) for size in sizes for _ in range(2)],
        compiler_params=remote_params(collective_id),
    )(rows[None])


class PlaneSum:
    def __init__(self, u, p, o, bufs=None, spread=None):
        self.u, self.p, self.o = u, p, o
        if bufs is not None:
            self.rc, self.s1, self.ra, self.rb, self.sa, self.sb, self.ta, self.tb = bufs[:8]
            self.send1, self.recv1 = bufs[8:]
        if spread is not None:
            self.send2, self.recv2, self.loc = spread
        ctx, self.x = lax.axis_index("context"), lax.axis_index("dp")
        self.core, self.y = lax.rem(ctx, 2), lax.div(ctx, 2)
        self.chip_peer = {"context": ctx + 1 - 2 * self.core}
        self.y_peer = {"context": lax.rem(ctx + 2, 4)}
        self.x_peer = {"dp": 1 - self.x}

    @staticmethod
    def reduce_scratch(shape, dtype):
        tail = tuple(shape[1:])
        bufs = [pltpu.VMEM((count,) + tail, dtype) for count in (8, 8, 2, 2, 2, 2, 1, 1)]
        return bufs + [DMA((5,)), DMA((5,))]

    @staticmethod
    def spread_scratch():
        return [DMA((5,)), DMA((5,)), DMA((2,))]

    @staticmethod
    def greet(bar):
        ctx, x = lax.axis_index("context"), lax.axis_index("dp")
        for peer in (
            {"context": ctx + 1 - 2 * lax.rem(ctx, 2)},
            {"context": lax.rem(ctx + 2, 4)},
            {"dp": 1 - x},
        ):
            pl.semaphore_signal(bar, inc=1, device_id=peer, device_id_type=MESH)
        return 3

    def copy(self, at, src, dst, peer):
        send, recv = (self.send1, self.recv1) if at < 5 else (self.send2, self.recv2)
        return pltpu.make_async_remote_copy(
            src_ref=src,
            dst_ref=dst,
            send_sem=send.at[at % 5],
            recv_sem=recv.at[at % 5],
            device_id=peer,
            device_id_type=MESH,
        )

    def got(self, at, ref):
        recv = self.recv1 if at < 5 else self.recv2
        pltpu.make_async_copy(ref, ref, recv.at[at % 5]).wait()

    def add(self, out, left, right):
        f32 = jnp.float32
        out[...] = (left[...].astype(f32) + right[...].astype(f32)).astype(out.dtype)

    def mine(self, half):
        if half == 0:
            return pl.ds(self.core * 8 + 2 * self.x + self.y, 1)
        return pl.ds(self.core * 8 + 4 + 2 * self.y + self.x, 1)

    def hop(self, at):
        x, y, core = self.x, self.y, self.core
        o, p = self.o, self.p
        pair_a, pair_b = pl.ds(core * 8 + 2 * x, 2), pl.ds(core * 8 + 4 + 2 * y, 2)
        one = lambda at: pl.ds(at, 1)
        return [
            lambda: self.copy(0, self.by_core(1 - core), self.rc, self.chip_peer),
            lambda: self.copy(1, self.quarter(0, 1 - x), self.ra, self.x_peer),
            lambda: self.copy(2, self.quarter(1, 1 - y), self.rb, self.y_peer),
            lambda: self.copy(3, self.eighth(0, 1 - y), self.ta, self.y_peer),
            lambda: self.copy(4, self.eighth(1, 1 - x), self.tb, self.x_peer),
            lambda: self.copy(5, p.at[one(0)], o.at[self.mine(0)], self.y_peer),
            lambda: self.copy(6, p.at[one(1)], o.at[self.mine(1)], self.x_peer),
            lambda: self.copy(7, o.at[pair_a], o.at[pair_a], self.x_peer),
            lambda: self.copy(8, o.at[pair_b], o.at[pair_b], self.y_peer),
            lambda: self.copy(9, o.at[pl.ds(core * 8, 8)], o.at[pl.ds(core * 8, 8)], self.chip_peer),
        ][at]()

    def begin(self):
        self.hop(0).start()

    def by_core(self, core):
        return self.u.at[pl.ds(core * 8, 8)]

    def quarter(self, half, at):
        return self.s1.at[pl.ds(4 * half + 2 * at, 2)]

    def eighth(self, half, at):
        return (self.sa, self.sb)[half].at[pl.ds(at, 1)]

    def result(self, half):
        return self.p.at[pl.ds(half, 1)]

    def first(self):
        self.got(0, self.rc)
        self.add(self.s1, self.by_core(self.core), self.rc)
        self.hop(1).start()
        self.hop(2).start()

    def second(self):
        self.got(1, self.ra)
        self.add(self.sa, self.quarter(0, self.x), self.ra)
        self.hop(3).start()
        self.got(2, self.rb)
        self.add(self.sb, self.quarter(1, self.y), self.rb)
        self.hop(4).start()

    def third(self):
        self.got(3, self.ta)
        self.add(self.result(0), self.eighth(0, self.y), self.ta)
        self.got(4, self.tb)
        self.add(self.result(1), self.eighth(1, self.x), self.tb)

    def reduced(self):
        for at in range(5):
            self.hop(at).wait_send()

    def kept(self, half):
        return pltpu.make_async_copy(self.p.at[pl.ds(half, 1)], self.o.at[self.mine(half)], self.loc.at[half])

    def spread1(self):
        self.hop(5).start()
        self.hop(6).start()
        self.kept(0).start()
        self.kept(1).start()

    def spread2(self):
        x, y, core = self.x, self.y, self.core
        self.kept(0).wait()
        self.got(5, self.o.at[pl.ds(core * 8 + 2 * x + 1 - y, 1)])
        self.hop(7).start()
        self.kept(1).wait()
        self.got(6, self.o.at[pl.ds(core * 8 + 4 + 2 * y + 1 - x, 1)])
        self.hop(8).start()

    def spread3(self):
        x, y, core = self.x, self.y, self.core
        self.got(7, self.o.at[pl.ds(core * 8 + 2 - 2 * x, 2)])
        self.got(8, self.o.at[pl.ds(core * 8 + 6 - 2 * y, 2)])
        self.hop(9).start()

    def everywhere(self):
        self.got(9, self.o.at[pl.ds(8 - self.core * 8, 8)])
        for at in range(5, 10):
            self.hop(at).wait_send()


class StripSum(PlaneSum):
    @staticmethod
    def reduce_scratch(shape, dtype):
        lead, rows, cols = shape
        rest = lead - 2
        shapes = [(lead, rows)] * 2
        shapes += [(count, rows // 2) for count in (2, rest, 2, rest)] + [(count, rows // 4) for count in (2, rest)]
        return [pltpu.VMEM(item + (cols // 2,), dtype) for item in shapes] + [DMA((5,)), DMA((5,))]

    def lead(self, half):
        whole = (self.u if self.u is not None else self.o).shape[0]
        return pl.ds(0, 2) if half == 0 else pl.ds(2, whole - 2)

    def strip(self, core):
        size = (self.u if self.u is not None else self.o).shape[2] // 2
        return pl.ds(pl.multiple_of(core * size, 128), size)

    def rows(self, at, parts):
        size = (self.u if self.u is not None else self.o).shape[1] // parts
        return pl.ds(pl.multiple_of(at * size, 16), size)

    def by_core(self, core):
        return self.u.at[:, :, self.strip(core)]

    def quarter(self, half, at):
        return self.s1.at[self.lead(half), self.rows(at, 2)]

    def eighth(self, half, at):
        return (self.sa, self.sb)[half].at[:, self.rows(at, 4)]

    def result(self, half):
        return self.p.at[half, pl.ds(0, 2 if half == 0 else self.u.shape[0] - 2)]

    def hop(self, at):
        if at < 5:
            return super().hop(at)
        o, x, y = self.o, self.x, self.y
        mine = lambda half: o.at[
            self.lead(half), self.rows(2 * x + y if half == 0 else 2 * y + x, 4), self.strip(self.core)
        ]
        pair = lambda half: o.at[self.lead(half), self.rows(x if half == 0 else y, 2), self.strip(self.core)]
        both = o.at[:, :, self.strip(self.core)]
        return [
            lambda: self.copy(5, self.result(0), mine(0), self.y_peer),
            lambda: self.copy(6, self.result(1), mine(1), self.x_peer),
            lambda: self.copy(7, pair(0), pair(0), self.x_peer),
            lambda: self.copy(8, pair(1), pair(1), self.y_peer),
            lambda: self.copy(9, both, both, self.chip_peer),
        ][at - 5]()

    def kept(self, half):
        x, y = self.x, self.y
        mine = self.o.at[
            self.lead(half), self.rows(2 * x + y if half == 0 else 2 * y + x, 4), self.strip(self.core)
        ]
        return pltpu.make_async_copy(self.result(half), mine, self.loc.at[half])

    def spread2(self):
        x, y, mine = self.x, self.y, self.strip(self.core)
        self.kept(0).wait()
        self.got(5, self.o.at[self.lead(0), self.rows(2 * x + 1 - y, 4), mine])
        self.hop(7).start()
        self.kept(1).wait()
        self.got(6, self.o.at[self.lead(1), self.rows(2 * y + 1 - x, 4), mine])
        self.hop(8).start()

    def spread3(self):
        mine = self.strip(self.core)
        self.got(7, self.o.at[self.lead(0), self.rows(1 - self.x, 2), mine])
        self.got(8, self.o.at[self.lead(1), self.rows(1 - self.y, 2), mine])
        self.hop(9).start()

    def everywhere(self):
        self.got(9, self.o.at[:, :, self.strip(1 - self.core)])
        for at in range(5, 10):
            self.hop(at).wait_send()


def unit_pieces(unit):
    return jax.ShapeDtypeStruct((2,) + unit.shape[1:], unit.dtype)


def line_greet(bar, me, n):
    @pl.when(me > 0)
    def _():
        pl.semaphore_signal(bar, inc=1, device_id={"tensor": me - 1}, device_id_type=MESH)

    @pl.when(me < n - 1)
    def _():
        pl.semaphore_signal(bar, inc=1, device_id={"tensor": me + 1}, device_id_type=MESH)

    return jnp.where(me > 0, 1, 0) + jnp.where(me < n - 1, 1, 0)


class LineScatter:
    def __init__(self, n, x, o, buf, tmp, send, recv):
        self.n, self.x, self.o, self.buf, self.tmp, self.send, self.recv = n, x, o, buf, tmp, send, recv
        self.me = lax.axis_index("tensor")

    @staticmethod
    def scratch(n, own, cols, dtype):
        return [
            pltpu.VMEM((2, n - 1, own, cols), dtype),
            pltpu.VMEM((2, n - 1, own, cols), dtype),
            DMA((2, n - 1)),
            DMA((2, n - 1)),
        ]

    def term(self, d, k):
        return self.n - 1 - k if d == 0 else k

    def sends(self, d, k):
        return self.me < self.n - 1 - k if d == 0 else self.me > k

    def behind(self, d):
        return self.me > 0 if d == 0 else self.me < self.n - 1

    def copy(self, d, k, first):
        return pltpu.make_async_remote_copy(
            src_ref=self.x.at[self.term(d, k)] if first else self.tmp.at[d, k],
            dst_ref=self.buf.at[d, k],
            send_sem=self.send.at[d, k],
            recv_sem=self.recv.at[d, k],
            device_id={"tensor": jnp.clip(self.me + 1 if d == 0 else self.me - 1, 0, self.n - 1)},
            device_id_type=MESH,
        )

    def landed(self, d, k):
        return pltpu.make_async_copy(self.buf.at[d, k], self.buf.at[d, k], self.recv.at[d, k])

    def begin(self, ks):
        for d in range(2):

            @pl.when(jnp.logical_not(self.behind(d)))
            def _():
                for k in ks:
                    self.copy(d, k, True).start()

    def step(self, k, which=None):
        for d in range(2):
            now = self.behind(d) & self.sends(d, k)

            @pl.when(now if which is None else now & which(d))
            def _():
                self.landed(d, k).wait()
                at = self.term(d, k)
                both = self.buf[d, k].astype(jnp.float32) + self.x[at].astype(jnp.float32)
                self.tmp[d, k] = both.astype(self.tmp.dtype)
                self.copy(d, k, False).start()

    def end(self):
        self.o[...] = self.x[self.me].astype(jnp.float32)
        for d in range(2):
            for k in range(self.n - 1):

                @pl.when(self.behind(d) & (self.me == self.term(d, k)))
                def _():
                    self.landed(d, k).wait()
                    self.o[...] += self.buf[d, k].astype(jnp.float32)

        for d in range(2):
            for k in range(self.n - 1):

                @pl.when(self.sends(d, k))
                def _():
                    self.copy(d, k, False).wait_send()


GELU_SCALE = 0.7978845608028654
GELU_CUBE = 0.044715


def feed_kernel(n, nc, heads, chunks, piece_ref, *rest):
    (token_hbm, out_ref, abias_hbm, gain_hbm, shift_hbm, up_hbm, down_hbm, bias_hbm, near_ref, cot_ref), rest = rest[:10], rest[10:]
    outs, heads_ref, rest = rest[:7], rest[7], rest[8:]
    kept_refs, rest = rest[:7], rest[7:]
    feed_ref, p1_ref, p2_ref, middle_ref, gm_ref, vec_ref, p3_ref = kept_refs
    (token_ref, abias_ref, gain_ref, shift_ref, bias_ref, osem), rest = rest[:6], rest[6:]
    leave = copies(tuple(zip(kept_refs, outs)), osem)
    (o_ref, sum_ref, att_ref, gpiece, u3, bsend, brecv, bloc), rest = rest[:8], rest[8:]
    (x_ref, up_ref, down_ref, grad_ref, wsem, asend, arecv, aloc, csend, crecv, cloc), rest = rest[:11], rest[11:]
    (held, act, gp, part, acc, buf, tmp, u1, u2), rest = rest[:9], rest[9:]
    (gsend, grecv, loc, ssend, srecv), rest = rest[:5], rest[5:]
    plane = [PlaneSum(u1, p1_ref, None, rest[:10]), PlaneSum(u2, p2_ref, None, rest[10:20])]
    out_sum = StripSum(u3, p3_ref, None, rest[20:30])
    me = lax.axis_index("tensor")
    rows, width = token_ref.shape
    wide = up_ref.shape[1]
    few = rows // chunks
    f32, low = jnp.float32, jnp.bfloat16
    ctx, dp = lax.axis_index("context"), lax.axis_index("dp")
    place, total = ctx * n + me, nc * n
    my_head = me * heads + jnp.minimum(ctx, heads - 1)
    bar = pltpu.get_barrier_semaphore()
    for shift in range(1, total):
        other = lax.rem(place + shift, total)
        pl.semaphore_signal(bar, inc=1, device_id=spread(other, AXES, (nc, n)), device_id_type=MESH)
    pl.semaphore_signal(bar, inc=1, device_id={"dp": 1 - dp}, device_id_type=MESH)
    weights_in = copies(
        (
            (token_hbm, token_ref),
            (abias_hbm, abias_ref),
            (gain_hbm, gain_ref),
            (shift_hbm, shift_ref),
            (bias_hbm, bias_ref),
            (up_hbm, up_ref),
            (down_hbm, down_ref),
        ),
        wsem,
    )
    for item in weights_in:
        item.start()

    def grad_rows(block):
        return grad_ref.at[pl.ds(pl.multiple_of(block * rows, rows), rows)]

    def grad_on(d, s):
        block = jnp.clip(me - s if d == 0 else me + s, 0, n - 1)
        return pltpu.make_async_remote_copy(
            src_ref=near_ref.at[block] if s == 1 else grad_rows(block),
            dst_ref=grad_rows(block),
            send_sem=csend.at[d, s],
            recv_sem=crecv.at[d, s],
            device_id={"tensor": jnp.clip(me + 1 if d == 0 else me - 1, 0, n - 1)},
            device_id_type=MESH,
        )

    def grad_sends(d, s):
        return (me - s >= 0) & (me < n - 1) if d == 0 else (me + s < n) & (me > 0)

    def grad_near(d):
        block = jnp.clip(me - 1 if d == 0 else me + 1, 0, n - 1)
        return pltpu.make_async_copy(near_ref.at[block], grad_rows(block), cloc.at[d])

    def grad_own():
        return pltpu.make_async_copy(cot_ref, grad_rows(me), cloc.at[2])

    def beside(d):
        return me > 0 if d == 0 else me < n - 1

    grad_own().start()
    for d in range(2):

        @pl.when(beside(d))
        def _():
            grad_near(d).start()

    pl.semaphore_wait(bar, total)

    def to_place(shift):
        other = lax.rem(place + shift, total)
        return pltpu.make_async_remote_copy(
            src_ref=piece_ref.at[other],
            dst_ref=att_ref.at[my_head],
            send_sem=asend.at[shift],
            recv_sem=arecv.at[shift],
            device_id=spread(other, AXES, (nc, n)),
            device_id_type=MESH,
        )

    @pl.when(ctx < heads)
    def _():
        for shift in range(1, total):
            to_place(shift).start()
        stay = pltpu.make_async_copy(piece_ref.at[place], att_ref.at[my_head], aloc)
        stay.start()
        stay.wait()

    for d in range(2):

        @pl.when(grad_sends(d, 1))
        def _():
            grad_on(d, 1).start()

    for shift in range(1, total):
        source = lax.rem(place + total - shift, total)
        at_ctx, at_ten = lax.div(source, n), lax.rem(source, n)

        @pl.when(at_ctx < heads)
        def _():
            landed = att_ref.at[at_ten * heads + jnp.minimum(at_ctx, heads - 1)]
            pltpu.make_async_copy(landed, landed, arecv.at[shift]).wait()

    for item in weights_in[:4]:
        item.wait()
    attended = att_ref[...].reshape(width, rows)
    middle = token_ref[...].astype(f32) + dot(attended, out_ref[...], ((0,), (0,))) + row(abias_ref)
    middle_ref[...] = middle
    leave[3].start()
    x_ref[...] = (norm_parts(middle)[0] * row(gain_ref) + row(shift_ref)).astype(low)

    @pl.when(ctx < heads)
    def _():
        for shift in range(1, total):
            to_place(shift).wait_send()

    def rows_of(block):
        return pl.ds(pl.multiple_of(block * rows, rows), rows)

    def neighbour(d):
        return {"tensor": jnp.clip(jnp.where(d == 0, me + 1, me - 1), 0, n - 1)}

    def onward(d):
        return jnp.where(d == 0, me, n - 1 - me) < n - 1

    def hand_on(d, s, block, first):
        return pltpu.make_async_remote_copy(
            src_ref=x_ref if first else held.at[rows_of(block)],
            dst_ref=held.at[rows_of(block)],
            send_sem=gsend.at[d, s],
            recv_sem=grecv.at[d, s],
            device_id=neighbour(d),
            device_id_type=MESH,
        )

    def chunk(block, c):
        return pl.ds(pl.multiple_of(block * rows + c * few, few), few)

    def back(d, block, c, first):
        at = chunk(block, c)
        return pltpu.make_async_remote_copy(
            src_ref=part.at[at] if first else tmp.at[at],
            dst_ref=buf.at[d, at],
            send_sem=ssend.at[block, c],
            recv_sem=srecv.at[d, block, c],
            device_id=neighbour(d),
            device_id_type=MESH,
        )

    for d in range(2):

        @pl.when(onward(d))
        def _():
            hand_on(d, 0, me, True).start()

    own = pltpu.make_async_copy(x_ref, held.at[rows_of(me)], loc)
    own.start()
    sum_ref[...] = jnp.zeros_like(sum_ref)
    own.wait()
    for item in weights_in[4:]:
        item.wait()
    grad_own().wait()
    for d in range(2):

        @pl.when(beside(d))
        def _():
            grad_near(d).wait()

    for s in range(1, n - 1):
        for d in range(2):
            block = me - 1 - s if d == 0 else me + 1 + s

            @pl.when((block >= 0) & (block < n))
            def _():
                landed = grad_rows(jnp.clip(block, 0, n - 1))
                pltpu.make_async_copy(landed, landed, crecv.at[d, s]).wait()

            if s + 1 < n - 1:

                @pl.when(grad_sends(d, s + 1))
                def _():
                    grad_on(d, s + 1).start()

        if s == n - 3:
            break
    columns = 256

    def work(block):
        here = rows_of(block)
        acc[...] = jnp.zeros_like(acc)

        @pl.loop(0, wide // columns)
        def _(j):
            at = pl.ds(pl.multiple_of(j * columns, columns), columns)
            pre = dot(held[here, :], up_ref[:, at], ((1,), (0,))) + bias_ref[at].reshape(1, -1)
            square = pre * pre
            tanh = jnp.tanh(GELU_SCALE * pre * (1.0 + GELU_CUBE * square))
            act[here, at] = (0.5 * pre * (1.0 + tanh)).astype(low)
            slope = 0.5 * (1.0 + tanh) + 0.5 * pre * (1.0 - tanh * tanh) * (
                GELU_SCALE * (1.0 + 3.0 * GELU_CUBE * square)
            )
            grad = (dot(grad_ref[here, :], down_ref[at, :], ((1,), (1,))) * slope).astype(low)
            gp[here, at] = grad
            acc[...] += dot(grad, up_ref[:, at], ((1,), (1,)))

        part[here, :] = acc[...].astype(low)
        sum_ref[...] += jnp.sum(gp[here, :].astype(f32), axis=0, keepdims=True)

    near = jnp.minimum(me, n - 1 - me)
    toward = jnp.where(2 * me < n - 1, -1, 1)

    @pl.loop(0, n)
    def _(slot):
        paired = slot <= 2 * near
        distance = jnp.where(paired, lax.div(slot + 1, 2), slot - near)
        side = jnp.where(paired & (lax.rem(slot, 2) == 1), toward, -toward)
        block = me + side * distance
        d = jnp.where(block < me, 0, 1)
        s = jnp.maximum(distance - 1, 0)

        @pl.when(slot > 0)
        def _():
            landed = held.at[rows_of(block)]
            pltpu.make_async_copy(landed, landed, grecv.at[d, s]).wait()

            @pl.when(onward(d))
            def _():
                hand_on(d, jnp.minimum(s + 1, n - 2), block, False).start()

        @pl.when(distance == n - 1)
        def _():
            landed = grad_rows(block)
            pltpu.make_async_copy(landed, landed, crecv.at[d, n - 2]).wait()

        work(block)

        @pl.when((slot > 0) & ((me == 0) | (me == n - 1)))
        def _():
            for c in range(chunks):
                back(1 - d, block, c, True).start()

    def weights(left, right, unit):
        half = wide // 2

        @pl.loop(0, 2)
        def _(j):
            at = pl.ds(pl.multiple_of(j * half, 128), half)
            total = dot(left[:, at], right[...], ((0,), (0,)))
            unit[pl.ds(8 * j, 8)] = total.astype(low).reshape((8,) + unit.shape[1:])

    weights(act, grad_ref, u1)
    plane[0].begin()
    weights(held, gp, u2)
    plane[1].begin()

    def relay(way, block):
        d = jnp.where(way > 0, 0, 1)

        @pl.when((me > 0) & (me < n - 1) & (block >= 0) & (block < n))
        def _():
            for c in range(chunks):
                at = chunk(block, c)
                landed = buf.at[d, at]
                pltpu.make_async_copy(landed, landed, srecv.at[d, block, c]).wait()
                tmp[at, :] = (buf[d, at, :].astype(f32) + part[at, :].astype(f32)).astype(low)
                back(d, block, c, False).start()

    plane[0].first()
    for j in range(1, n):
        relay(-toward, me - toward * j)
        if j == 1:
            plane[1].first()

    @pl.loop(0, n)
    def _(block):
        here = rows_of(block)
        feed_ref[here, :] = dot(act[here, :], down_ref[...], ((1,), (0,))).astype(low)

    leave[0].start()

    plane[0].second()
    plane[1].second()
    for j in range(1, n):
        relay(toward, me + toward * j)
    for item in plane:
        item.third()
    for c in range(chunks):
        at = chunk(me, c)
        mine = pl.ds(c * few, few)
        o_ref[mine, :] = part[at, :].astype(f32)
        for d in range(2):

            @pl.when(me > 0 if d == 0 else me < n - 1)
            def _():
                landed = buf.at[d, at]
                pltpu.make_async_copy(landed, landed, srecv.at[d, me, c]).wait()
                o_ref[mine, :] += buf[d, at, :].astype(f32)

    grad = o_ref[...]
    normed, scale = norm_parts(middle_ref[...])
    above = grad_ref[rows_of(me), :].astype(f32)
    grad_middle = above + norm_backward(grad, normed, scale, row(gain_ref))
    gm_ref[...] = grad_middle
    for at in (1, 2, 4):
        leave[at].start()
    gm_low = grad_middle.astype(low)
    back_out = dot(out_ref[...], gm_low, ((1,), (1,))).astype(low)
    gpiece[...] = back_out.reshape(gpiece.shape)
    vec_ref[...] = jnp.zeros_like(vec_ref)
    vec_ref[2:3, :] = jnp.sum(gm_low.astype(f32), axis=0, keepdims=True)

    def to_head(shift):
        other = lax.rem(place + shift, total)
        at_ctx, at_ten = lax.div(other, n), lax.rem(other, n)
        return at_ctx < heads, pltpu.make_async_remote_copy(
            src_ref=gpiece.at[at_ten * heads + jnp.minimum(at_ctx, heads - 1)],
            dst_ref=heads_ref.at[place],
            send_sem=bsend.at[shift],
            recv_sem=brecv.at[shift],
            device_id={"context": at_ctx, "tensor": at_ten},
            device_id_type=MESH,
        )

    for shift in range(1, total):
        goes, item = to_head(shift)

        @pl.when(goes)
        def _():
            item.start()

    stay = pltpu.make_async_copy(gpiece.at[my_head], heads_ref.at[place], bloc)
    stay.start()
    u3[...] = dot(att_ref[...].reshape(width, rows), gm_low, ((1,), (0,))).astype(low).reshape(u3.shape)
    out_sum.begin()
    vec_ref[3:4, :] = jnp.sum(grad * normed, axis=0, keepdims=True)
    vec_ref[4:5, :] = jnp.sum(grad, axis=0, keepdims=True)
    vec_ref[5:6, :] = jnp.sum(above, axis=0, keepdims=True)
    vec_ref[6:7, :] = sum_ref[...]
    out_sum.first()
    out_sum.second()
    out_sum.third()
    leave[5].start()
    leave[6].start()
    stay.wait()

    @pl.when(ctx < heads)
    def _():
        for shift in range(1, total):
            source = lax.rem(place + total - shift, total)
            landed = heads_ref.at[source]
            pltpu.make_async_copy(landed, landed, brecv.at[shift]).wait()

    for shift in range(1, total):
        goes, item = to_head(shift)

        @pl.when(goes)
        def _():
            item.wait_send()

    out_sum.reduced()
    for item in leave:
        item.wait()
    for d in range(2):
        for s in range(n - 1):
            block = me - s if d == 0 else me + s

            @pl.when(onward(d) & (block >= 0) & (block < n))
            def _():
                hand_on(d, s, me, True).wait_send()

    for block in range(n):

        @pl.when(me != block)
        def _():
            for c in range(chunks):
                back(jnp.where(me < block, 0, 1), block, c, True).wait_send()

    for d in range(2):
        for s in range(1, n - 1):

            @pl.when(grad_sends(d, s))
            def _():
                grad_on(d, s).wait_send()

    for item in plane:
        item.reduced()


def feed_part(pieces, tokens, out_weight, vectors, up, down, bias, near, cotangent, n, nc, heads, collective_id):
    rows, width = tokens.shape
    wide = up.shape[1]
    chunks = 2
    total = n * rows
    low, f32 = jnp.bfloat16, jnp.float32
    unit = (16, wide // 16, width)
    piece = jax.ShapeDtypeStruct((2,) + unit[1:], low)
    return pl.pallas_call(
        functools.partial(feed_kernel, n, nc, heads, chunks),
        out_shape=(
            jax.ShapeDtypeStruct((total, width), low),
            piece,
            piece,
            jax.ShapeDtypeStruct((rows, width), f32),
            jax.ShapeDtypeStruct((rows, width), f32),
            jax.ShapeDtypeStruct((8, width), f32),
            jax.ShapeDtypeStruct((2, 2, rows // 4, width // 2), low),
            jax.ShapeDtypeStruct(pieces.shape, low),
        ),
        in_specs=[VM, HB, VM, HB, HB, HB, HB, HB, HB, VM, HB],
        out_specs=(HB,) * 7 + (VM,),
        scratch_shapes=[
            pltpu.VMEM((total, width), low),
            pltpu.VMEM(piece.shape, low),
            pltpu.VMEM(piece.shape, low),
            pltpu.VMEM((rows, width), f32),
            pltpu.VMEM((rows, width), f32),
            pltpu.VMEM((8, width), f32),
            pltpu.VMEM((2, 2, rows // 4, width // 2), low),
            pltpu.VMEM(tokens.shape, tokens.dtype),
            pltpu.VMEM((width,), f32),
            pltpu.VMEM((width,), f32),
            pltpu.VMEM((width,), f32),
            pltpu.VMEM((wide,), f32),
            DMA((7,)),
            pltpu.VMEM((rows, width), f32),
            pltpu.VMEM((1, wide), f32),
            pltpu.VMEM((n * heads,) + pieces.shape[1:], low),
            pltpu.VMEM((n * heads,) + pieces.shape[1:], low),
            pltpu.VMEM((n, width // n, width), low),
            DMA((nc * n,)),
            DMA((nc * n,)),
            DMA,
            pltpu.VMEM((rows, width), low),
            pltpu.VMEM(up.shape, low),
            pltpu.VMEM(down.shape, low),
            pltpu.VMEM((total, width), low),
            DMA((7,)),
            DMA((nc * n,)),
            DMA((nc * n,)),
            DMA,
            DMA((2, n - 1)),
            DMA((2, n - 1)),
            DMA((3,)),
            pltpu.VMEM((total, width), low),
            pltpu.VMEM((total, wide), low),
            pltpu.VMEM((total, wide), low),
            pltpu.VMEM((total, width), low),
            pltpu.VMEM((rows, width), f32),
            pltpu.VMEM((2, total, width), low),
            pltpu.VMEM((total, width), low),
            pltpu.VMEM(unit, low),
            pltpu.VMEM(unit, low),
            DMA((2, n - 1)),
            DMA((2, n - 1)),
            DMA,
            DMA((n, chunks)),
            DMA((2, n, chunks)),
        ]
        + PlaneSum.reduce_scratch(unit, low) * 2
        + StripSum.reduce_scratch((n, width // n, width), low),
        compiler_params=remote_params(collective_id, 40),
    )(pieces, tokens, out_weight, *vectors, up, down, bias, near, cotangent)


def last_kernel(n, nc, heads, shared, count, x_ref, w_hbm, h_hbm, a_hbm, feed_hbm, mid_hbm, bias_hbm, *rest):
    ps, rest = rest[:count], rest[count:]
    (token_hbm, gain_hbm, middle_hbm, vec_hbm), rest = rest[:4], rest[4:]
    (out_ref, g_ref, v_ref, po_ref, ao_ref), rest = rest[:5], rest[5:]
    outs, rest = rest[:count], rest[count:]
    (rows_ref, w_ref, h_ref, token_ref, middle_ref, part, sum_ref, u_ref, piece), rest = rest[:9], rest[9:]
    (hsend, hrecv, hloc, win), rest = rest[:4], rest[4:]
    (feed_ref, fsum_ref, mid_ref, bias_ref, gain_ref, vec_ref), rest = rest[:6], rest[6:]
    feed_line = LineScatter(n, feed_ref, fsum_ref, *rest[:4])
    rest = rest[4:]
    chunks = 2
    own = token_ref.shape[0]
    few = own // chunks
    lines = [
        LineScatter(n, part.at[:, pl.ds(c * few, few)], sum_ref.at[pl.ds(c * few, few)], *rest[4 * c : 4 * c + 4])
        for c in range(chunks)
    ]
    rest = rest[4 * chunks :]
    project = StripSum(u_ref, piece, po_ref, rest[:10], rest[10:13])
    rest = rest[13:]
    feeds = [PlaneSum(None, ps[i], outs[i], None, rest[3 * i : 3 * i + 3]) for i in range(count)]
    rest = rest[3 * count :]
    (land, zsend, zrecv, zloc, a_ref), rest = rest[:5], rest[5:]
    (asend, arecv, aloc, now), rest = rest[:4], rest[4:]
    sizes = (n, 2 * nc)
    bufs, sems = rest[:2], rest[2:]
    f32, low = jnp.float32, jnp.bfloat16

    ten, ctx, x = (lax.axis_index(name) for name in ("tensor", "context", "dp"))
    place = ctx * 2 + x
    bar = pltpu.get_barrier_semaphore()
    for shift in range(1, n):
        pl.semaphore_signal(bar, inc=1, device_id={"tensor": lax.rem(ten + shift, n)}, device_id_type=MESH)
    for shift in range(1, 8):
        other = lax.rem(place + shift, 8)
        pl.semaphore_signal(
            bar, inc=1, device_id={"context": lax.div(other, 2), "dp": lax.rem(other, 2)}, device_id_type=MESH
        )
    copies_in = copies(
        (
            (feed_hbm, feed_ref),
            (token_hbm, token_ref),
            (w_hbm, w_ref),
            (h_hbm, h_ref),
            (middle_hbm, middle_ref),
            (mid_hbm, mid_ref),
            (bias_hbm, bias_ref),
            (gain_hbm, gain_ref),
            (vec_hbm, vec_ref),
        ),
        win,
    )
    for item in copies_in:
        item.start()
    pl.semaphore_wait(bar, n + 6)

    half = 2 * own
    far = 1 - lax.div(ten, 2)
    pairs = (far, 1 - far)

    def columns(pair):
        return pl.ds(pl.multiple_of(pair * half, 128), half)

    def ship(index, shift):
        other = lax.rem(ctx + shift, nc)
        return pltpu.make_async_remote_copy(
            src_ref=x_ref.at[other, :, :, columns(pairs[index])],
            dst_ref=rows_ref.at[:, jnp.minimum(ctx, heads - 1), :, columns(pairs[index])],
            send_sem=hsend.at[index, shift],
            recv_sem=hrecv.at[index, shift],
            device_id={"context": other},
            device_id_type=MESH,
        )

    @pl.when(ctx < heads)
    def _():
        for index in range(2):
            for shift in range(1, nc):
                ship(index, shift).start()
        stay = pltpu.make_async_copy(x_ref.at[ctx], rows_ref.at[:, ctx], hloc)
        stay.start()
        stay.wait()

    def across(shift):
        other = lax.rem(ten + shift, n)
        return pltpu.make_async_remote_copy(
            src_ref=a_hbm.at[lax.div(other, 2), lax.rem(other, 2)],
            dst_ref=land.at[ten],
            send_sem=zsend.at[shift],
            recv_sem=zrecv.at[shift],
            device_id={"tensor": other},
            device_id_type=MESH,
        )

    copies_in[0].wait()
    feed_line.begin((0,))
    for shift in range(1, n):
        across(shift).start()
    mine = pltpu.make_async_copy(a_hbm.at[lax.div(ten, 2), lax.rem(ten, 2)], land.at[ten], zloc)
    mine.start()
    for item in feeds:
        item.spread1()

    def there(at):
        ctx_, x_ = lax.div(at, 2), lax.rem(at, 2)
        y_ = lax.div(ctx_, 2)
        row_ = jnp.where(ten < n // 2, 2 * x_ + y_, 2 * y_ + x_)
        rows = pl.ds(pl.multiple_of(row_ * a_ref.shape[0], 16), a_ref.shape[0])
        cols = pl.ds(pl.multiple_of(lax.rem(ctx_, 2) * a_ref.shape[1], 128), a_ref.shape[1])
        return ao_ref.at[rows, cols]

    def push(shift):
        other = lax.rem(place + shift, 8)
        return pltpu.make_async_remote_copy(
            src_ref=a_ref,
            dst_ref=there(place),
            send_sem=asend.at[shift],
            recv_sem=arecv.at[shift],
            device_id={"context": lax.div(other, 2), "dp": lax.rem(other, 2)},
            device_id_type=MESH,
        )

    copies_in[1].wait()
    normed, scale = norm_parts(token_ref[...].astype(f32))
    mine.wait()
    for shift in range(1, n):
        source = lax.rem(ten + n - shift, n)
        pltpu.make_async_copy(land.at[source], land.at[source], zrecv.at[shift]).wait()
    value = land[0].astype(f32)
    for at in range(1, n):
        value = value + land[at].astype(f32)
    a_ref[...] = value.astype(low)
    for item in copies_in[2:]:
        item.wait()
    now[0] = vec_ref[...]
    for shift in range(1, 8):
        push(shift).start()
    kept = pltpu.make_async_copy(a_ref, there(place), aloc)
    kept.start()

    def partials(index):
        at = columns(pairs[index])
        for shift in range(1, nc):
            source = lax.rem(ctx + nc - shift, nc)

            @pl.when(source < heads)
            def _():
                ref = rows_ref.at[:, jnp.minimum(source, heads - 1), :, at]
                pltpu.make_async_copy(ref, ref, hrecv.at[index, shift]).wait()

        total = 0.0
        for kind in range(3):
            grads = rows_ref[kind, :, :, at].reshape(heads * HEAD_DIM, half)
            total = total + dot(grads, w_ref[kind], ((0,), (0,)))
        part[pl.ds(2 * pairs[index], 2)] = total.astype(low).reshape(2, own, total.shape[1])

    first = lambda d: (ten < n // 2) if d == 0 else (ten >= n // 2)
    second = lambda d: (ten >= n // 2) if d == 0 else (ten < n // 2)
    feed_line.step(0, first)
    partials(0)
    for line in lines:
        line.begin((0, 1))
    partials(1)
    for line in lines:
        line.begin((2,))
    feed_line.begin((1, 2))
    for item in feeds:
        item.spread2()
    for line in lines:
        line.step(0, first)
    for kind in range(3):
        grads = rows_ref[kind].reshape(heads * HEAD_DIM, n * own)
        u_ref[kind] = dot(grads, h_ref[...], ((1,), (0,))).astype(low)
    project.begin()
    for line in lines:
        line.step(1, first)
    feed_line.step(0, second)
    ends = jnp.concatenate(
        [rows_ref[kind].reshape(heads * HEAD_DIM, n * own) for kind in (0, 2)], axis=0
    )
    bias = dot(jnp.ones((8, n * own), low), ends, ((1,), (1,)))
    now[0, 7:8, 0 : bias.shape[1]] = bias[0:1]
    project.first()
    for item in feeds:
        item.spread3()
    project.second()
    for k in range(n - 1):
        for line in lines:
            line.step(k, second)
    project.third()
    project.spread1()
    for line in lines:
        line.end()
    grad = sum_ref[...]
    now[0, 0:1] = jnp.sum(grad * normed, axis=0, keepdims=True)
    now[0, 1:2] = jnp.sum(grad, axis=0, keepdims=True)
    alone = now[0]

    def where(stage):
        return ten if stage == 0 else place

    def stage_copy(stage, shift):
        other = lax.rem(where(stage) + shift, sizes[stage])
        peer = {"tensor": other} if stage == 0 else {"context": lax.div(other, 2), "dp": lax.rem(other, 2)}
        return pltpu.make_async_remote_copy(
            src_ref=now.at[stage],
            dst_ref=bufs[stage].at[where(stage)],
            send_sem=sems[2 * stage].at[shift],
            recv_sem=sems[2 * stage + 1].at[shift],
            device_id=peer,
            device_id_type=MESH,
        )

    def stage_start(stage):
        for shift in range(1, sizes[stage]):
            stage_copy(stage, shift).start()
        bufs[stage][where(stage)] = now[stage]

    def stage_end(stage):
        buf, size = bufs[stage], sizes[stage]
        for shift in range(1, size):
            source = lax.rem(where(stage) + size - shift, size)
            pltpu.make_async_copy(buf.at[source], buf.at[source], sems[2 * stage + 1].at[shift]).wait()
        total = buf[0]
        for at in range(1, size):
            total = total + buf[at]
        if stage == 0:
            line_ = lax.broadcasted_iota(jnp.int32, total.shape, 0)
            now[1] = jnp.where(line_ < shared, total, alone)
        else:
            v_ref[...] = total

    stage_start(0)
    back = norm_backward(grad, normed, scale, row(gain_ref))
    g_ref[...] = (middle_ref[...] + back).astype(g_ref.dtype)
    project.spread2()
    feed_line.step(1, first)
    stage_end(0)
    stage_start(1)
    project.spread3()
    feed_line.end()
    out_ref[...] = (mid_ref[...] + fsum_ref[...] + row(bias_ref)).astype(low)
    kept.wait()
    for shift in range(1, 8):
        source = there(lax.rem(place + 8 - shift, 8))
        pltpu.make_async_copy(source, source, arecv.at[shift]).wait()
    for item in feeds:
        item.everywhere()
    stage_end(1)
    project.everywhere()
    project.reduced()

    @pl.when(ctx < heads)
    def _():
        for index in range(2):
            for shift in range(1, nc):
                ship(index, shift).wait_send()

    for shift in range(1, n):
        across(shift).wait_send()
    for shift in range(1, 8):
        push(shift).wait_send()
    for stage in range(2):
        for shift in range(1, sizes[stage]):
            stage_copy(stage, shift).wait_send()


def last_part(x, weight, hidden, attend_pieces, feed, middle, bias, pieces, tokens, gain, grad_middle, vectors, shared, n, heads, collective_id):
    nc = x.shape[0]
    own, cols = tokens.shape
    count = len(pieces)
    f32, low = jnp.float32, jnp.bfloat16
    whole = lambda item: jax.ShapeDtypeStruct((16,) + item.shape[1:], item.dtype)
    wide, deep = attend_pieces.shape[2:]
    unit = (3, heads * HEAD_DIM, cols)
    result = pl.pallas_call(
        functools.partial(last_kernel, n, nc, heads, shared, count),
        out_shape=(
            jax.ShapeDtypeStruct((own, cols), low),
            jax.ShapeDtypeStruct((own, cols), low),
            jax.ShapeDtypeStruct(vectors.shape, f32),
            jax.ShapeDtypeStruct(unit, low),
            jax.ShapeDtypeStruct((4 * wide, 2 * deep), low),
        )
        + tuple(whole(item) for item in pieces),
        in_specs=[VM] + [HB] * (10 + count),
        out_specs=(VM,) * (5 + count),
        scratch_shapes=[
            pltpu.VMEM((3, heads, HEAD_DIM, n * own), low),
            pltpu.VMEM(weight.shape, low),
            pltpu.VMEM(hidden.shape, low),
            pltpu.VMEM(tokens.shape, low),
            pltpu.VMEM((own, cols), f32),
            pltpu.VMEM((n, own, cols), low),
            pltpu.VMEM((own, cols), f32),
            pltpu.VMEM(unit, low),
            pltpu.VMEM((2, 2, unit[1] // 4, cols // 2), low),
            DMA((2, nc)),
            DMA((2, nc)),
            DMA,
            DMA((9,)),
            pltpu.VMEM((n, own, cols), low),
            pltpu.VMEM((own, cols), f32),
            pltpu.VMEM((own, cols), f32),
            pltpu.VMEM((cols,), f32),
            pltpu.VMEM((cols,), f32),
            pltpu.VMEM(vectors.shape, f32),
        ]
        + LineScatter.scratch(n, own, cols, low)
        + LineScatter.scratch(n, own // 2, cols, low) * 2
        + StripSum.reduce_scratch(unit, low)
        + PlaneSum.spread_scratch()
        + [item for _ in pieces for item in PlaneSum.spread_scratch()]
        + [pltpu.VMEM((n, wide, deep), low), DMA((n,)), DMA((n,)), DMA, pltpu.VMEM((wide, deep), low)]
        + [DMA((8,)), DMA((8,)), DMA, pltpu.VMEM((2,) + vectors.shape, f32)]
        + [pltpu.VMEM((size,) + vectors.shape, f32) for size in (n, 2 * nc)]
        + [DMA((size,)) for size in (n, 2 * nc) for _ in range(2)],
        compiler_params=remote_params(collective_id, 32),
    )(
        x, weight, hidden, attend_pieces, feed.reshape(n, own, cols), middle, bias,
        *pieces, tokens, gain, grad_middle, vectors,
    )
    return result[:5] + (result[5:],)


class LineGather:
    def __init__(self, n, x, o, send, recv):
        self.n, self.x, self.o, self.send, self.recv = n, x, o, send, recv
        self.me = lax.axis_index("tensor")

    def copy(self, d, s):
        me, n = self.me, self.n
        shard = jnp.clip(me - s if d == 0 else me + s, 0, n - 1)
        return pltpu.make_async_remote_copy(
            src_ref=self.x if s == 0 else self.o.at[shard],
            dst_ref=self.o.at[shard],
            send_sem=self.send.at[d, s],
            recv_sem=self.recv.at[d, s],
            device_id={"tensor": jnp.clip(me + 1 if d == 0 else me - 1, 0, n - 1)},
            device_id_type=MESH,
        )

    def sends(self, d, s):
        me, n = self.me, self.n
        return (me - s >= 0) & (me < n - 1) if d == 0 else (me + s < n) & (me > 0)

    def wait(self, d, s):
        me, n = self.me, self.n

        @pl.when(me - 1 - s >= 0 if d == 0 else me + 1 + s < n)
        def _():
            shard = jnp.clip(me - 1 - s if d == 0 else me + 1 + s, 0, n - 1)
            pltpu.make_async_copy(self.o.at[shard], self.o.at[shard], self.recv.at[d, s]).wait()

    def step(self, s):
        for d in range(2):
            if s > 0:
                self.wait(d, s - 1)

            @pl.when(self.sends(d, s))
            def _():
                self.copy(d, s).start()

    def pass_on(self, d, s, now):
        @pl.when(self.sends(d, s) & now)
        def _():
            self.copy(d, s).start()

    def last(self):
        for d in range(2):
            self.wait(d, self.n - 2)

    def finish(self, steps=None):
        for d in range(2):
            for s in range(steps or self.n - 1):

                @pl.when(self.sends(d, s))
                def _():
                    self.copy(d, s).wait_send()


def start_kernel(n, nc, heads, t_hbm, gain_hbm, shift_hbm, full_ref, w_hbm, b_hbm, c_ref, o_hbm, f_ref, q_ref, g_ref, *rest):
    (x_ref, held, proj, w_ref, o_ref, t_ref, gain_ref, shift_ref, b_ref, win), rest = rest[:10], rest[10:]
    arrive = copies(((t_hbm, t_ref), (gain_hbm, gain_ref), (shift_hbm, shift_ref), (b_hbm, b_ref)), win)
    for item in arrive:
        item.start()
    s1, r1, s2, r2, s5, r5, s3, r3, s4, r4, loc = rest
    me, ctx, x = lax.axis_index("tensor"), lax.axis_index("context"), lax.axis_index("dp")
    core, y = lax.rem(ctx, 2), lax.div(ctx, 2)
    rows, width = t_ref.shape
    half = 2 * rows
    bar = pltpu.get_barrier_semaphore()
    met = line_greet(bar, me, n)
    for shift in range(1, nc):
        pl.semaphore_signal(bar, inc=1, device_id={"context": lax.rem(ctx + shift, nc)}, device_id_type=MESH)
    pl.semaphore_signal(bar, inc=1, device_id={"dp": 1 - x}, device_id_type=MESH)
    weight_in = pltpu.make_async_copy(w_hbm, w_ref, loc.at[4])
    weight_in.start()
    for item in arrive:
        item.wait()
    normed, _ = norm_parts(t_ref[...].astype(jnp.float32))
    x_ref[...] = (normed * row(gain_ref) + row(shift_ref)).astype(x_ref.dtype)
    pl.semaphore_wait(bar, met + nc)

    tall, deep = held.shape[1:]
    strip = pl.ds(pl.multiple_of(core * deep, 128), deep)
    piece = full_ref.at[pl.ds(pl.multiple_of((2 * y + x) * tall, 16), tall), strip]
    small = LineGather(n, piece, held, s1, r1)
    large = LineGather(n, x_ref, o_ref, s2, r2)
    grads = LineGather(n, c_ref, g_ref, s5, r5)
    def move(s):
        large.step(s)
        for d in range(2):
            grads.pass_on(d, 0, me == (s if d == 0 else n - 1 - s))

    small.step(0)
    move(0)
    own = pltpu.make_async_copy(x_ref, o_ref.at[me], loc.at[0])
    own.start()
    mine = pltpu.make_async_copy(piece, held.at[me], loc.at[1])
    mine.start()
    mine.wait()
    own.wait()
    for s in range(1, n - 1):
        small.step(s)
    small.last()

    def there(y_, x_):
        return f_ref.at[:, pl.ds(pl.multiple_of((2 * y_ + x_) * tall, 16), tall), strip]

    x_peer, y_peer = {"dp": 1 - x}, {"context": lax.rem(ctx + 2, 4)}

    def hop(at):
        src, dst, peer = [
            (held, there(y, x), x_peer),
            (held, there(y, x), y_peer),
            (there(y, 1 - x), there(y, 1 - x), y_peer),
            (f_ref.at[:, :, strip], f_ref.at[:, :, strip], {"context": ctx + 1 - 2 * core}),
        ][at]
        return pltpu.make_async_remote_copy(
            src_ref=src,
            dst_ref=dst,
            send_sem=s3.at[at],
            recv_sem=r3.at[at],
            device_id=peer,
            device_id_type=MESH,
        )

    def got(at):
        other = pl.ds(pl.multiple_of((1 - core) * deep, 128), deep)
        ref = [there(y, 1 - x), there(1 - y, x), there(1 - y, 1 - x), f_ref.at[:, :, other]][at]
        pltpu.make_async_copy(ref, ref, r3.at[at]).wait()

    hop(0).start()
    kept = pltpu.make_async_copy(held, there(y, x), loc.at[2])
    kept.start()

    def columns(pair):
        return pl.ds(pl.multiple_of(pair * half, 128), half)

    def project(pair):
        token = jnp.concatenate([o_ref[2 * pair], o_ref[2 * pair + 1]], axis=0)
        for kind in range(3):
            value = dot(w_ref[kind], token, ((1,), (1,))) + b_ref[kind]
            proj[kind, :, :, columns(pair)] = value.astype(proj.dtype).reshape(heads, HEAD_DIM, half)

    def ship(index, pair, shift):
        other = lax.rem(ctx + shift, nc)
        return other, pltpu.make_async_remote_copy(
            src_ref=proj.at[:, jnp.minimum(other, heads - 1), :, columns(pair)],
            dst_ref=q_ref.at[ctx, :, :, columns(pair)],
            send_sem=s4.at[index, shift],
            recv_sem=r4.at[index, shift],
            device_id={"context": other},
            device_id_type=MESH,
        )

    def ship_all(index, pair):
        for shift in range(1, nc):
            other, item = ship(index, pair, shift)

            @pl.when(other < heads)
            def _():
                item.start()

    near = lax.div(me, 2)
    move(1)
    weight_in.wait()
    project(near)
    ship_all(0, near)
    hop(1).start()
    for s in range(2, n - 1):
        move(s)
    got(0)
    hop(2).start()
    large.last()
    project(1 - near)
    ship_all(1, 1 - near)
    result = pltpu.make_async_copy(o_ref, o_hbm, loc.at[5])
    result.start()
    stay = pltpu.make_async_copy(proj.at[:, jnp.minimum(ctx, heads - 1)], q_ref.at[ctx], loc.at[3])
    stay.start()
    kept.wait()
    got(1)
    got(2)
    hop(3).start()
    stay.wait()

    @pl.when(ctx < heads)
    def _():
        for index in range(2):
            for shift in range(1, nc):
                source = lax.rem(ctx + nc - shift, nc)
                pair = near if index == 0 else 1 - near
                ref = q_ref.at[source, :, :, columns(pair)]
                pltpu.make_async_copy(ref, ref, r4.at[index, shift]).wait()

    got(3)
    for d in range(2):
        grads.wait(d, 0)
    result.wait()
    small.finish()
    large.finish()
    grads.finish(1)
    for at in range(4):
        hop(at).wait_send()
    for index in range(2):
        for shift in range(1, nc):
            other, item = ship(index, near if index == 0 else 1 - near, shift)

            @pl.when(other < heads)
            def _():
                item.wait_send()


def start_part(tokens, gain, shift, w, project_weight, bias, cotangent, n, nc, heads, collective_id):
    rows, cols = tokens.shape
    wide, deep = w.shape
    low = jnp.bfloat16
    full, weight, qkv, grads = pl.pallas_call(
        functools.partial(start_kernel, n, nc, heads),
        out_shape=(
            jax.ShapeDtypeStruct((n, rows, cols), low),
            jax.ShapeDtypeStruct((n, wide, deep), w.dtype),
            jax.ShapeDtypeStruct((nc, 3, HEAD_DIM, n * rows), low),
            jax.ShapeDtypeStruct((n, rows, cols), low),
        ),
        in_specs=[HB] * 7,
        out_specs=(HB, VM, VM, VM),
        scratch_shapes=[
            pltpu.VMEM((rows, cols), low),
            pltpu.VMEM((n, wide // 4, deep // 2), w.dtype),
            pltpu.VMEM((3, heads, HEAD_DIM, n * rows), low),
            pltpu.VMEM(project_weight.shape, low),
            pltpu.VMEM((n, rows, cols), low),
            pltpu.VMEM((rows, cols), tokens.dtype),
            pltpu.VMEM(gain.shape, jnp.float32),
            pltpu.VMEM(shift.shape, jnp.float32),
            pltpu.VMEM(bias.shape, jnp.float32),
            DMA((4,)),
        ]
        + [DMA((2, n - 1)) for _ in range(6)]
        + [DMA((4,)), DMA((4,)), DMA((2, nc)), DMA((2, nc)), DMA((6,))],
        compiler_params=remote_params(collective_id, 56),
    )(tokens, gain, shift, w, project_weight, bias, cotangent)
    return full.reshape(n * rows, cols), weight.reshape(n * wide, deep), qkv, grads


def dot(left, right, dims):
    return lax.dot_general(left, right, ((dims[0], dims[1]), ((), ())), preferred_element_type=jnp.float32)


def key_positions(first, keys, queries):
    return first + lax.broadcasted_iota(jnp.int32, (keys, queries), 0)


def load_rows(qkv_ref, nb, half, qs, kt, ks, vs):
    for block in range(nb):
        part = slice(block % 2 * half, block % 2 * half + half)
        at = block // 2
        qs[block] = qkv_ref[at, 0, :, part] * jnp.asarray(HEAD_DIM**-0.5, qs.dtype)
        item = qkv_ref[at, 1, :, part]
        if kt is not None:
            kt[block] = item
        ks[block] = item.T
        if vs is not None:
            vs[block] = qkv_ref[at, 2, :, part].T


def fill_tables(nb, half, seg_ref, order_ref, slot_ref, low_ref, high_ref):
    for block in range(nb):
        slot_ref[order_ref[block]] = jnp.int32(block)
    first = [seg_ref[0, block * half] for block in range(nb)]
    last = [seg_ref[0, block * half + half - 1] for block in range(nb)]
    for block in range(nb):
        if low_ref is not None:
            low_ref[block] = sum(jnp.where(item < first[block], 1, 0) for item in last)
        if high_ref is not None:
            high_ref[block] = sum(jnp.where(item <= last[block], 1, 0) for item in first)


def forward_kernel(half, heads, seg_s, order_ref, seg_ref, qkv_ref, o_ref, full_ref, lse_ref, start_ref, qs, ks, slot_ref, low_ref):
    nb = full_ref.shape[0]

    @pl.when(lax.axis_index("context") < heads)
    def _():
        load_rows(qkv_ref, nb, half, qs, None, ks, None)
        fill_tables(nb, half, seg_s, order_ref, slot_ref, low_ref, None)
        seg = seg_ref[...]
        start = jnp.zeros(seg.shape, jnp.float32)
        for doc in range(1, DOC_LIMIT):
            before = jnp.sum(jnp.where(seg < doc, 1.0, 0.0), axis=1, keepdims=True)
            start = jnp.where(seg == doc, before, start)
        start_ref[...] = start.astype(jnp.int32)

        @pl.loop(0, nb)
        def _(nq):
            slot = slot_ref[nq]
            query = qs[slot]
            begin = start_ref[:, pl.ds(pl.multiple_of(nq * half, 128), half)]
            here = nq * half + lax.broadcasted_iota(jnp.int32, (1, half), 1)

            def step(nk, state):
                top, total, acc = state
                at = slot_ref[nk]
                score = dot(ks[at], query, ((1,), (0,)))
                place = key_positions(nk * half, half, half)
                score = jnp.where((place >= begin) & (place <= here), score, NEG_FILL)
                new_top = jnp.maximum(top, jnp.max(score, axis=0, keepdims=True))
                factor = jnp.exp(top - new_top)
                weight = jnp.exp(score - new_top)
                total = total * factor + jnp.sum(weight, axis=0, keepdims=True)
                value = qkv_ref[at // 2, 2, :, pl.ds(pl.multiple_of(at % 2 * half, 128), half)]
                acc = acc * factor + dot(value, weight.astype(jnp.bfloat16), ((1,), (0,)))
                return new_top, total, acc

            top, total, acc = lax.fori_loop(
                low_ref[nq],
                nq + 1,
                step,
                (
                    jnp.full((1, half), NEG_FILL, jnp.float32),
                    jnp.zeros((1, half), jnp.float32),
                    jnp.zeros((HEAD_DIM, half), jnp.float32),
                ),
            )
            result = acc / total
            full_ref[slot] = result
            lse_ref[slot] = top + jnp.log(total)
            low = result.astype(jnp.bfloat16)
            o_ref[2 * slot] = low[:, : half // 2]
            o_ref[2 * slot + 1] = low[:, half // 2 :]


def attend_forward(qkv, segments, order, half, heads):
    nc = qkv.shape[0]
    nb = 2 * nc
    return pl.pallas_call(
        functools.partial(forward_kernel, half, heads),
        out_shape=(
            jax.ShapeDtypeStruct((2 * nb, HEAD_DIM, half // 2), jnp.bfloat16),
            jax.ShapeDtypeStruct((nb, HEAD_DIM, half), jnp.float32),
            jax.ShapeDtypeStruct((nb, 1, half), jnp.float32),
            jax.ShapeDtypeStruct(segments.shape, jnp.int32),
        ),
        in_specs=[SM, SM, VM, VM],
        out_specs=(VM, VM, VM, VM),
        scratch_shapes=[
            pltpu.VMEM((nb, HEAD_DIM, half), jnp.bfloat16),
            pltpu.VMEM((nb, half, HEAD_DIM), jnp.bfloat16),
            pltpu.SMEM((nb,), jnp.int32),
            pltpu.SMEM((nb,), jnp.int32),
        ],
        compiler_params=pltpu.CompilerParams(vmem_limit_bytes=24 << 20),
    )(segments, order, segments, qkv)


def backward_kernel(
    half, heads, seg_s, order_ref, start_ref, qkv_ref, full_ref, lse_ref, grad_ref, o_ref,
    qs, kt, ks, vs, gs, ds, dq, slot_ref, high_ref,
):
    nb = full_ref.shape[0]

    @pl.when(lax.axis_index("context") < heads)
    def _():
        load_rows(qkv_ref, nb, half, qs, kt, ks, vs)
        fill_tables(nb, half, seg_s, order_ref, slot_ref, None, high_ref)
        for block in range(nb):
            both = jnp.concatenate([grad_ref[2 * block], grad_ref[2 * block + 1]], axis=1)
            gs[block] = both
            ds[block] = jnp.sum(both.astype(jnp.float32) * full_ref[block], axis=0, keepdims=True)
            dq[block] = jnp.zeros((HEAD_DIM, half), jnp.float32)

        @pl.loop(0, nb)
        def _(nk):
            at = slot_ref[nk]
            place = key_positions(nk * half, half, half)

            def step(nq, state):
                grad_key, grad_value = state
                slot = slot_ref[nq]
                query, grad = qs[slot], gs[slot]
                begin = start_ref[:, pl.ds(pl.multiple_of(nq * half, 128), half)]
                here = nq * half + lax.broadcasted_iota(jnp.int32, (1, half), 1)
                score = dot(ks[at], query, ((1,), (0,)))
                score = jnp.where((place >= begin) & (place <= here), score, NEG_FILL)
                weight = jnp.exp(score - lse_ref[slot])
                grad_weight = dot(vs[at], grad, ((1,), (0,)))
                grad_score = (weight * (grad_weight - ds[slot])).astype(jnp.bfloat16)
                grad_value = grad_value + dot(grad, weight.astype(jnp.bfloat16), ((1,), (1,)))
                grad_key = grad_key + dot(query, grad_score, ((1,), (1,)))
                dq[slot] += dot(kt[at], grad_score, ((1,), (0,)))
                return grad_key, grad_value

            zero = jnp.zeros((HEAD_DIM, half), jnp.float32)
            grad_key, grad_value = lax.fori_loop(nk, high_ref[nk], step, (zero, zero))
            columns = pl.ds(pl.multiple_of(at % 2 * half, 128), half)
            o_ref[at // 2, 1, :, columns] = grad_key.astype(jnp.bfloat16)
            o_ref[at // 2, 2, :, columns] = grad_value.astype(jnp.bfloat16)

        for block in range(nb):
            part = slice(block % 2 * half, block % 2 * half + half)
            o_ref[block // 2, 0, :, part] = (dq[block] * HEAD_DIM**-0.5).astype(jnp.bfloat16)


def attend_backward(qkv, segments, order, start, full, lse, grad, half, heads):
    nc = qkv.shape[0]
    nb = 2 * nc
    low = jnp.bfloat16
    return pl.pallas_call(
        functools.partial(backward_kernel, half, heads),
        out_shape=jax.ShapeDtypeStruct(qkv.shape, low),
        in_specs=[SM, SM, VM, VM, VM, VM, VM],
        out_specs=VM,
        scratch_shapes=[
            pltpu.VMEM((nb, HEAD_DIM, half), low),
            pltpu.VMEM((nb, HEAD_DIM, half), low),
            pltpu.VMEM((nb, half, HEAD_DIM), low),
            pltpu.VMEM((nb, half, HEAD_DIM), low),
            pltpu.VMEM((nb, HEAD_DIM, half), low),
            pltpu.VMEM((nb, 1, half), jnp.float32),
            pltpu.VMEM((nb, HEAD_DIM, half), jnp.float32),
            pltpu.SMEM((nb,), jnp.int32),
            pltpu.SMEM((nb,), jnp.int32),
        ],
        compiler_params=pltpu.CompilerParams(vmem_limit_bytes=24 << 20),
    )(segments, order, start, qkv, full, lse, grad)


def norm_parts(values):
    centre = jnp.mean(values, axis=-1, keepdims=True)
    shifted = values - centre
    spread_ = jnp.mean(shifted * shifted, axis=-1, keepdims=True)
    scale = lax.rsqrt(spread_ + NORM_EPS)
    return shifted * scale, scale


def norm_backward(grad, normed, scale, gain):
    e = grad * gain
    mean_e = jnp.mean(e, axis=-1, keepdims=True)
    mean_en = jnp.mean(e * normed, axis=-1, keepdims=True)
    return (e - mean_e - normed * mean_en) * scale


def gelu_tanh(values):
    return jax.nn.gelu(values, approximate=True)


def cross_rows(left, right):
    return lax.dot_general(
        left, right, (((0,), (0,)), ((), ())), preferred_element_type=jnp.float32
    )


def after(value, done):
    return lax.optimization_barrier((value, done))[0]


def per_device(
    mesh_sizes,
    inputs,
    first_gain,
    first_shift,
    project_weight,
    project_bias,
    attend_weight,
    attend_bias,
    second_gain,
    second_shift,
    expand_weight,
    expand_bias,
    shrink_weight,
    shrink_bias,
    segments,
    block_order,
    cotangent,
):
    nt, nc = mesh_sizes["tensor"], mesh_sizes["context"]
    own_rows, width = inputs.shape[1], inputs.shape[2]
    local_width = project_weight.shape[2]
    heads = local_width // HEAD_DIM
    block_rows = own_rows * nt
    half = block_rows // 2
    low = jnp.bfloat16
    f32 = lambda value: value.astype(jnp.float32)
    square = nt == 4 and nc == 4 and mesh_sizes["dp"] == 2
    plane = ("context", "dp")

    tokens_own = f32(inputs[0])
    grad_out = cotangent[0]
    bias = jnp.stack([project_bias[0], jnp.zeros_like(project_bias[0]), project_bias[1]])[:, :, None]
    weight_rows = project_weight.transpose(0, 2, 1)
    if square:
        hidden1_full, attend_full, qkv, grads_near = start_part(
            inputs[0], first_gain, first_shift, attend_weight, weight_rows, bias, grad_out, nt, nc, heads, 0
        )
        pieces, attended_full, lse, start = attend_forward(qkv, segments, block_order, half, heads)
        feed, *feed_pieces, middle, grad_middle, vectors, attend_pieces, grad_heads = feed_part(
            pieces,
            inputs[0],
            attend_full,
            (attend_bias, second_gain, second_shift),
            expand_weight,
            shrink_weight,
            expand_bias,
            grads_near,
            grad_out,
            nt,
            nc,
            heads,
            3,
        )
        grad_qkv = attend_backward(
            qkv, segments, block_order, start, attended_full, lse, grad_heads, half, heads
        )
        outputs, grad_inputs, summed, grad_project, grad_attend, feeds = last_part(
            grad_qkv,
            weight_rows,
            hidden1_full,
            attend_pieces,
            feed,
            middle,
            shrink_bias,
            feed_pieces,
            inputs[0],
            first_gain,
            grad_middle,
            vectors,
            6,
            nt,
            heads,
            7,
        )
        grad_project = grad_project.transpose(0, 2, 1)
        grad_shrink, grad_expand = feeds[0].reshape(-1, width), feeds[1].reshape(width, -1)
        wide = expand_bias.shape[0]
    else:
        hidden1 = norm_parts(tokens_own)[0] * first_gain + first_shift
        hidden1_full = gather_rows(hidden1.astype(low), nt, 0)
        attend_full = lax.all_gather(attend_weight, "tensor", axis=0, tiled=True)
        projected = jnp.einsum(
            "ked,rd->ker", weight_rows, hidden1_full, preferred_element_type=jnp.float32
        )
        projected = (projected + bias).astype(low).reshape(3, heads, HEAD_DIM, block_rows)
        qkv = to_heads(projected, nc, 1)
        pieces, attended_full, lse, start = attend_forward(qkv, segments, block_order, half, heads)
        grad_full = lax.all_gather(grad_out, "tensor", axis=0, tiled=True)
        attended = to_rows(pieces, nc, nt, heads, 2).reshape(width, own_rows)
        middle = tokens_own + cross_rows(attended, attend_full) + attend_bias
        normed2, scale2 = norm_parts(middle)
        hidden2 = (normed2 * second_gain + second_shift).astype(low)
        hidden2_full = gather_rows(hidden2, nt, 3)
        pre_act = jnp.dot(hidden2_full, expand_weight, preferred_element_type=jnp.float32) + expand_bias
        activ = gelu_tanh(pre_act).astype(low)
        grad_act = dot(grad_full, shrink_weight, ((1,), (1,)))
        grad_pre = jax.vjp(gelu_tanh, pre_act)[1](grad_act)[0].astype(low)
        grad_shrink = cross_rows(activ, grad_full).astype(low)
        grad_expand = cross_rows(hidden2_full, grad_pre).astype(low)
        grad_hidden2 = scatter_rows(dot(grad_pre, expand_weight, ((1,), (1,))).astype(low), nt, 4)
        grad_expand_bias = jnp.sum(f32(grad_pre), axis=0)
        feed = jnp.dot(activ, shrink_weight, preferred_element_type=jnp.float32).astype(low)

        grad_shrink_bias = jnp.sum(f32(grad_out), axis=0)
        grad_second_gain = jnp.sum(grad_hidden2 * normed2, axis=0)
        grad_second_shift = jnp.sum(grad_hidden2, axis=0)
        grad_middle = f32(grad_out) + norm_backward(grad_hidden2, normed2, scale2, second_gain)
        grad_middle_low = grad_middle.astype(low)
        grad_attend_bias = jnp.sum(f32(grad_middle_low), axis=0)
        grad_attended = dot(attend_full, grad_middle_low, ((1,), (1,))).astype(low)
        grad_attended = grad_attended.reshape(nt * heads, HEAD_DIM, own_rows)
        grad_attend = jnp.dot(attended, grad_middle_low, preferred_element_type=jnp.float32).astype(low)
        grad_heads = rows_back(grad_attended, nc, nt, heads, 5)
        feed_sum = lax.psum_scatter(after(feed, grad_heads), "tensor", scatter_dimension=0, tiled=True)

        grad_qkv = attend_backward(
            qkv, segments, block_order, start, attended_full, lse, grad_heads, half, heads
        )
        grad_rows = from_heads(grad_qkv, nc, heads, 6).reshape(3 * local_width, block_rows)
        grad_project = dot(hidden1_full, grad_rows, ((0,), (1,))).astype(low)
        grad_hidden1 = cross_rows(grad_rows, weight_rows.reshape(3 * local_width, width)).astype(low)
        row_sums = jnp.sum(f32(grad_rows), axis=1)
        grad_project_bias = jnp.concatenate([row_sums[:local_width], row_sums[2 * local_width :]])
        grad_hidden1 = scatter_rows(grad_hidden1, nt, 7)
        normed1, scale1 = norm_parts(tokens_own)
        back = norm_backward(grad_hidden1, normed1, scale1, first_gain)
        grad_inputs = (grad_middle + back).astype(low)
        wide = grad_expand_bias.shape[0]
        vectors = jnp.concatenate(
            [
                jnp.sum(grad_hidden1 * normed1, axis=0),
                jnp.sum(grad_hidden1, axis=0),
                grad_attend_bias,
                grad_second_gain,
                grad_second_shift,
                grad_shrink_bias,
                grad_expand_bias,
                jnp.pad(grad_project_bias, (0, -(wide + 2 * local_width) % width)),
            ]
        ).reshape(-1, width)
        summed = sum_vectors(vectors, 6, mesh_sizes, 8)
        grad_attend = lax.psum_scatter(grad_attend, "tensor", scatter_dimension=0, tiled=True)
        grad_project, grad_attend, grad_shrink, grad_expand = lax.psum(
            (grad_project, grad_attend, grad_shrink, grad_expand), plane
        )
        grad_project = jnp.stack(
            [grad_project[:, at * local_width : (at + 1) * local_width] for at in range(3)]
        )
        outputs = (middle + f32(feed_sum) + shrink_bias).astype(low)
    tail = summed[6:].reshape(-1)
    return (
        outputs[None],
        grad_inputs[None],
        summed[0],
        summed[1],
        f32(grad_project),
        tail[wide : wide + 2 * local_width].reshape(2, local_width),
        f32(grad_attend),
        summed[2],
        summed[3],
        summed[4],
        f32(grad_expand),
        tail[:wide],
        f32(grad_shrink),
        summed[5],
    )


def solution(mesh):
    rows = P("dp", ("context", "tensor"), None)
    in_specs = (
        rows,
        P(),
        P(),
        P(None, None, "tensor"),
        P(None, "tensor"),
        P("tensor", None),
        P(),
        P(),
        P(),
        P(None, "tensor"),
        P("tensor"),
        P("tensor", None),
        P(),
        P("dp", None),
        P(),
        rows,
    )
    out_specs = (
        rows,
        rows,
        P(),
        P(),
        P(None, None, "tensor"),
        P(None, "tensor"),
        P("tensor", None),
        P(),
        P(),
        P(),
        P(None, "tensor"),
        P("tensor"),
        P("tensor", None),
        P(),
    )
    return jax.shard_map(
        functools.partial(per_device, dict(mesh.shape)),
        mesh=mesh,
        in_specs=in_specs,
        out_specs=out_specs,
        check_vma=False,
    )
```

```python
import functools

import jax
import jax.numpy as jnp
from jax import lax
from jax.experimental import pallas as pl
from jax.experimental.pallas import tpu as pltpu
from jax.sharding import PartitionSpec as P

HEAD_DIM = 64
NEG_FILL = -1e30
NORM_EPS = 1e-05
DOC_LIMIT = 16
MESH = pl.DeviceIdType.MESH
VM = pl.BlockSpec(memory_space=pltpu.VMEM)
SM = pl.BlockSpec(memory_space=pltpu.SMEM)
DMA = pltpu.SemaphoreType.DMA


def remote_params(collective_id, mib=16):
    return pltpu.CompilerParams(
        collective_id=collective_id, has_side_effects=True, vmem_limit_bytes=mib << 20
    )


HB = pl.BlockSpec(memory_space=pltpu.HBM)


def copies(pairs, sems):
    return [pltpu.make_async_copy(src, dst, sems.at[at]) for at, (src, dst) in enumerate(pairs)]


def row(ref):
    return ref[...].reshape(1, -1)


def line_barrier(me, n):
    bar = pltpu.get_barrier_semaphore()

    @pl.when(me > 0)
    def _():
        pl.semaphore_signal(bar, inc=1, device_id={"tensor": me - 1}, device_id_type=MESH)

    @pl.when(me < n - 1)
    def _():
        pl.semaphore_signal(bar, inc=1, device_id={"tensor": me + 1}, device_id_type=MESH)

    pl.semaphore_wait(bar, jnp.where(me > 0, 1, 0) + jnp.where(me < n - 1, 1, 0))


def gather_kernel(n, x_ref, o_ref, send, recv, loc):
    me = lax.axis_index("tensor")
    line_barrier(me, n)
    own = pltpu.make_async_copy(x_ref, o_ref.at[me], loc)
    own.start()

    def copy(d, s):
        shard = jnp.clip(me - s if d == 0 else me + s, 0, n - 1)
        return pltpu.make_async_remote_copy(
            src_ref=x_ref if s == 0 else o_ref.at[shard],
            dst_ref=o_ref.at[shard],
            send_sem=send.at[d, s],
            recv_sem=recv.at[d, s],
            device_id={"tensor": jnp.clip(me + 1 if d == 0 else me - 1, 0, n - 1)},
            device_id_type=MESH,
        )

    def sends(d, s):
        return (me - s >= 0) & (me < n - 1) if d == 0 else (me + s < n) & (me > 0)

    def gets(d, s):
        return me - 1 - s >= 0 if d == 0 else me + 1 + s < n

    def landed(d, s):
        shard = jnp.clip(me - 1 - s if d == 0 else me + 1 + s, 0, n - 1)
        return pltpu.make_async_copy(o_ref.at[shard], o_ref.at[shard], recv.at[d, s])

    for s in range(n - 1):
        for d in range(2):
            if s > 0:

                @pl.when(gets(d, s - 1))
                def _():
                    landed(d, s - 1).wait()

            @pl.when(sends(d, s))
            def _():
                copy(d, s).start()

    for d in range(2):

        @pl.when(gets(d, n - 2))
        def _():
            landed(d, n - 2).wait()

        for s in range(n - 1):

            @pl.when(sends(d, s))
            def _():
                copy(d, s).wait_send()

    own.wait()


def gather_rows(x, n, collective_id):
    rows, cols = x.shape
    return pl.pallas_call(
        functools.partial(gather_kernel, n),
        out_shape=jax.ShapeDtypeStruct((n, rows, cols), x.dtype),
        in_specs=[VM],
        out_specs=VM,
        scratch_shapes=[DMA((2, n - 1)), DMA((2, n - 1)), DMA],
        compiler_params=remote_params(collective_id),
    )(x).reshape(n * rows, cols)


def scatter_kernel(n, x_ref, o_ref, buf, tmp, send, recv):
    me = lax.axis_index("tensor")
    line_barrier(me, n)

    def term(d, k):
        return n - 1 - k if d == 0 else k

    def sends(d, k):
        return me < n - 1 - k if d == 0 else me > k

    def behind(d):
        return me > 0 if d == 0 else me < n - 1

    def copy(d, k, first):
        return pltpu.make_async_remote_copy(
            src_ref=x_ref.at[term(d, k)] if first else tmp.at[d, k],
            dst_ref=buf.at[d, k],
            send_sem=send.at[d, k],
            recv_sem=recv.at[d, k],
            device_id={"tensor": jnp.clip(me + 1 if d == 0 else me - 1, 0, n - 1)},
            device_id_type=MESH,
        )

    def landed(d, k):
        return pltpu.make_async_copy(buf.at[d, k], buf.at[d, k], recv.at[d, k])

    for d in range(2):

        @pl.when(jnp.logical_not(behind(d)))
        def _():
            for k in range(n - 1):
                copy(d, k, True).start()

    for k in range(n - 1):
        for d in range(2):

            @pl.when(behind(d) & sends(d, k))
            def _():
                landed(d, k).wait()
                both = buf[d, k].astype(jnp.float32) + x_ref[term(d, k)].astype(jnp.float32)
                tmp[d, k] = both.astype(tmp.dtype)
                copy(d, k, False).start()

    o_ref[...] = x_ref[me].astype(jnp.float32)
    for d in range(2):
        for k in range(n - 1):

            @pl.when(behind(d) & (me == term(d, k)))
            def _():
                landed(d, k).wait()
                o_ref[...] += buf[d, k].astype(jnp.float32)

    for d in range(2):
        for k in range(n - 1):

            @pl.when(sends(d, k))
            def _():
                copy(d, k, False).wait_send()


def scatter_rows(x, n, collective_id):
    rows, cols = x.shape
    own = rows // n
    return pl.pallas_call(
        functools.partial(scatter_kernel, n),
        out_shape=jax.ShapeDtypeStruct((own, cols), jnp.float32),
        in_specs=[VM],
        out_specs=VM,
        scratch_shapes=[
            pltpu.VMEM((2, n - 1, own, cols), x.dtype),
            pltpu.VMEM((2, n - 1, own, cols), x.dtype),
            DMA((2, n - 1)),
            DMA((2, n - 1)),
        ],
        compiler_params=remote_params(collective_id),
    )(x.reshape(n, own, cols))


def group_barrier(axes, sizes):
    mine = [lax.axis_index(name) for name in axes]
    place = sum_index(mine, sizes)
    total = 1
    for size in sizes:
        total *= size
    bar = pltpu.get_barrier_semaphore()
    for shift in range(1, total):
        other = lax.rem(place + shift, total)
        pl.semaphore_signal(bar, inc=1, device_id=spread(other, axes, sizes), device_id_type=MESH)
    pl.semaphore_wait(bar, total - 1)
    return place, total


def sum_index(mine, sizes):
    place = 0
    for at, size in zip(mine, sizes):
        place = place * size + at
    return place


def spread(place, axes, sizes):
    found = {}
    for name, size in reversed(tuple(zip(axes, sizes))):
        found[name] = lax.rem(place, size)
        place = lax.div(place, size)
    return found


def to_heads_kernel(nc, heads, x_ref, o_ref, send, recv, loc):
    me, _ = group_barrier(("context",), (nc,))

    def copy(shift):
        other = lax.rem(me + shift, nc)
        return other, pltpu.make_async_remote_copy(
            src_ref=x_ref.at[:, jnp.minimum(other, heads - 1)],
            dst_ref=o_ref.at[me],
            send_sem=send.at[shift],
            recv_sem=recv.at[shift],
            device_id={"context": other},
            device_id_type=MESH,
        )

    for shift in range(1, nc):
        other, item = copy(shift)

        @pl.when(other < heads)
        def _():
            item.start()

    own = pltpu.make_async_copy(x_ref.at[:, jnp.minimum(me, heads - 1)], o_ref.at[me], loc)
    own.start()
    own.wait()

    @pl.when(me < heads)
    def _():
        for shift in range(1, nc):
            source = lax.rem(me + nc - shift, nc)
            pltpu.make_async_copy(o_ref.at[source], o_ref.at[source], recv.at[shift]).wait()

    for shift in range(1, nc):
        other, item = copy(shift)

        @pl.when(other < heads)
        def _():
            item.wait_send()


def to_heads(x, nc, collective_id):
    heads = x.shape[1]
    return pl.pallas_call(
        functools.partial(to_heads_kernel, nc, heads),
        out_shape=jax.ShapeDtypeStruct((nc, x.shape[0]) + x.shape[2:], x.dtype),
        in_specs=[VM],
        out_specs=VM,
        scratch_shapes=[DMA((nc,)), DMA((nc,)), DMA],
        compiler_params=remote_params(collective_id),
    )(x)


def from_heads_kernel(nc, heads, x_ref, o_ref, send, recv, loc):
    me, _ = group_barrier(("context",), (nc,))

    def copy(shift):
        other = lax.rem(me + shift, nc)
        return pltpu.make_async_remote_copy(
            src_ref=x_ref.at[other],
            dst_ref=o_ref.at[:, jnp.minimum(me, heads - 1)],
            send_sem=send.at[shift],
            recv_sem=recv.at[shift],
            device_id={"context": other},
            device_id_type=MESH,
        )

    @pl.when(me < heads)
    def _():
        for shift in range(1, nc):
            copy(shift).start()
        own = pltpu.make_async_copy(x_ref.at[me], o_ref.at[:, me], loc)
        own.start()
        own.wait()

    for shift in range(1, nc):
        source = lax.rem(me + nc - shift, nc)

        @pl.when(source < heads)
        def _():
            at = jnp.minimum(source, heads - 1)
            pltpu.make_async_copy(o_ref.at[:, at], o_ref.at[:, at], recv.at[shift]).wait()

    @pl.when(me < heads)
    def _():
        for shift in range(1, nc):
            copy(shift).wait_send()


def from_heads(x, nc, heads, collective_id):
    return pl.pallas_call(
        functools.partial(from_heads_kernel, nc, heads),
        out_shape=jax.ShapeDtypeStruct((x.shape[1], heads) + x.shape[2:], x.dtype),
        in_specs=[VM],
        out_specs=VM,
        scratch_shapes=[DMA((nc,)), DMA((nc,)), DMA],
        compiler_params=remote_params(collective_id),
    )(x)


AXES = ("context", "tensor")


def rows_kernel(nc, nt, heads, x_ref, o_ref, send, recv, loc):
    me, total = group_barrier(AXES, (nc, nt))
    my_ctx, my_ten = lax.axis_index("context"), lax.axis_index("tensor")
    my_head = my_ten * heads + jnp.minimum(my_ctx, heads - 1)

    def copy(shift):
        other = lax.rem(me + shift, total)
        return pltpu.make_async_remote_copy(
            src_ref=x_ref.at[other],
            dst_ref=o_ref.at[my_head],
            send_sem=send.at[shift],
            recv_sem=recv.at[shift],
            device_id=spread(other, AXES, (nc, nt)),
            device_id_type=MESH,
        )

    @pl.when(my_ctx < heads)
    def _():
        for shift in range(1, total):
            copy(shift).start()
        own = pltpu.make_async_copy(x_ref.at[me], o_ref.at[my_head], loc)
        own.start()
        own.wait()

    for shift in range(1, total):
        source = lax.rem(me + total - shift, total)
        ctx, ten = lax.div(source, nt), lax.rem(source, nt)

        @pl.when(ctx < heads)
        def _():
            at = ten * heads + jnp.minimum(ctx, heads - 1)
            pltpu.make_async_copy(o_ref.at[at], o_ref.at[at], recv.at[shift]).wait()

    @pl.when(my_ctx < heads)
    def _():
        for shift in range(1, total):
            copy(shift).wait_send()


def to_rows(x, nc, nt, heads, collective_id):
    total = nc * nt
    return pl.pallas_call(
        functools.partial(rows_kernel, nc, nt, heads),
        out_shape=jax.ShapeDtypeStruct((nt * heads,) + x.shape[1:], x.dtype),
        in_specs=[VM],
        out_specs=VM,
        scratch_shapes=[DMA((total,)), DMA((total,)), DMA],
        compiler_params=remote_params(collective_id),
    )(x)


def rows_back_kernel(nc, nt, heads, x_ref, o_ref, send, recv, loc):
    me, total = group_barrier(AXES, (nc, nt))
    my_ctx, my_ten = lax.axis_index("context"), lax.axis_index("tensor")

    def copy(shift):
        other = lax.rem(me + shift, total)
        ctx, ten = lax.div(other, nt), lax.rem(other, nt)
        return ctx < heads, pltpu.make_async_remote_copy(
            src_ref=x_ref.at[ten * heads + jnp.minimum(ctx, heads - 1)],
            dst_ref=o_ref.at[me],
            send_sem=send.at[shift],
            recv_sem=recv.at[shift],
            device_id={"context": ctx, "tensor": ten},
            device_id_type=MESH,
        )

    for shift in range(1, total):
        goes, item = copy(shift)

        @pl.when(goes)
        def _():
            item.start()

    own = pltpu.make_async_copy(
        x_ref.at[my_ten * heads + jnp.minimum(my_ctx, heads - 1)], o_ref.at[me], loc
    )
    own.start()
    own.wait()

    @pl.when(my_ctx < heads)
    def _():
        for shift in range(1, total):
            source = lax.rem(me + total - shift, total)
            pltpu.make_async_copy(o_ref.at[source], o_ref.at[source], recv.at[shift]).wait()

    for shift in range(1, total):
        goes, item = copy(shift)

        @pl.when(goes)
        def _():
            item.wait_send()


def rows_back(x, nc, nt, heads, collective_id):
    total = nc * nt
    return pl.pallas_call(
        functools.partial(rows_back_kernel, nc, nt, heads),
        out_shape=jax.ShapeDtypeStruct((total,) + x.shape[1:], x.dtype),
        in_specs=[VM],
        out_specs=VM,
        scratch_shapes=[DMA((total,)), DMA((total,)), DMA],
        compiler_params=remote_params(collective_id),
    )(x)


def vectors_kernel(names, sizes, shared, x_ref, o_ref, now, *rest):
    bufs, sems = rest[: len(names)], rest[len(names) :]
    bar = pltpu.get_barrier_semaphore()
    for name, size in zip(names, sizes):
        me = lax.axis_index(name)
        for shift in range(1, size):
            pl.semaphore_signal(
                bar, inc=1, device_id={name: lax.rem(me + shift, size)}, device_id_type=MESH
            )
    pl.semaphore_wait(bar, sum(sizes) - len(sizes))
    for stage, (name, size) in enumerate(zip(names, sizes)):
        buf, send, recv = bufs[stage], sems[2 * stage], sems[2 * stage + 1]
        me = lax.axis_index(name)

        def copy(shift):
            return pltpu.make_async_remote_copy(
                src_ref=now.at[stage] if stage else x_ref.at[0],
                dst_ref=buf.at[me],
                send_sem=send.at[shift],
                recv_sem=recv.at[shift],
                device_id={name: lax.rem(me + shift, size)},
                device_id_type=MESH,
            )

        for shift in range(1, size):
            copy(shift).start()
        buf[me] = now[stage] if stage else x_ref[0]
        for shift in range(1, size):
            source = lax.rem(me + size - shift, size)
            pltpu.make_async_copy(buf.at[source], buf.at[source], recv.at[shift]).wait()
        total = buf[0]
        for at in range(1, size):
            total = total + buf[at]
        if stage == 0:
            row = lax.broadcasted_iota(jnp.int32, total.shape, 0)
            total = jnp.where(row < shared, total, x_ref[0])
        if stage + 1 < len(names):
            now[stage + 1] = total
        else:
            o_ref[...] = total
        for shift in range(1, size):
            copy(shift).wait_send()


def sum_vectors(rows, shared, mesh_sizes, collective_id):
    names = ("tensor", "context", "dp")
    sizes = tuple(mesh_sizes[name] for name in names)
    shape = rows.shape
    return pl.pallas_call(
        functools.partial(vectors_kernel, names, sizes, shared),
        out_shape=jax.ShapeDtypeStruct(shape, jnp.float32),
        in_specs=[VM],
        out_specs=VM,
        scratch_shapes=[pltpu.VMEM((len(names),) + shape, jnp.float32)]
        + [pltpu.VMEM((size,) + shape, jnp.float32) for size in sizes]
        + [DMA((size,)) for size in sizes for _ in range(2)],
        compiler_params=remote_params(collective_id),
    )(rows[None])


class PlaneSum:
    def __init__(self, u, p, o, bufs=None, spread=None):
        self.u, self.p, self.o = u, p, o
        if bufs is not None:
            self.rc, self.s1, self.ra, self.rb, self.sa, self.sb, self.ta, self.tb = bufs[:8]
            self.send1, self.recv1 = bufs[8:]
        if spread is not None:
            self.send2, self.recv2, self.loc = spread
        ctx, self.x = lax.axis_index("context"), lax.axis_index("dp")
        self.core, self.y = lax.rem(ctx, 2), lax.div(ctx, 2)
        self.chip_peer = {"context": ctx + 1 - 2 * self.core}
        self.y_peer = {"context": lax.rem(ctx + 2, 4)}
        self.x_peer = {"dp": 1 - self.x}

    @staticmethod
    def reduce_scratch(shape, dtype):
        tail = tuple(shape[1:])
        bufs = [pltpu.VMEM((count,) + tail, dtype) for count in (8, 8, 2, 2, 2, 2, 1, 1)]
        return bufs + [DMA((5,)), DMA((5,))]

    @staticmethod
    def spread_scratch():
        return [DMA((5,)), DMA((5,)), DMA((2,))]

    @staticmethod
    def greet(bar):
        ctx, x = lax.axis_index("context"), lax.axis_index("dp")
        for peer in (
            {"context": ctx + 1 - 2 * lax.rem(ctx, 2)},
            {"context": lax.rem(ctx + 2, 4)},
            {"dp": 1 - x},
        ):
            pl.semaphore_signal(bar, inc=1, device_id=peer, device_id_type=MESH)
        return 3

    def copy(self, at, src, dst, peer):
        send, recv = (self.send1, self.recv1) if at < 5 else (self.send2, self.recv2)
        return pltpu.make_async_remote_copy(
            src_ref=src,
            dst_ref=dst,
            send_sem=send.at[at % 5],
            recv_sem=recv.at[at % 5],
            device_id=peer,
            device_id_type=MESH,
        )

    def got(self, at, ref):
        recv = self.recv1 if at < 5 else self.recv2
        pltpu.make_async_copy(ref, ref, recv.at[at % 5]).wait()

    def add(self, out, left, right):
        f32 = jnp.float32
        out[...] = (left[...].astype(f32) + right[...].astype(f32)).astype(out.dtype)

    def mine(self, half):
        if half == 0:
            return pl.ds(self.core * 8 + 2 * self.x + self.y, 1)
        return pl.ds(self.core * 8 + 4 + 2 * self.y + self.x, 1)

    def hop(self, at):
        x, y, core = self.x, self.y, self.core
        o, p = self.o, self.p
        pair_a, pair_b = pl.ds(core * 8 + 2 * x, 2), pl.ds(core * 8 + 4 + 2 * y, 2)
        one = lambda at: pl.ds(at, 1)
        return [
            lambda: self.copy(0, self.by_core(1 - core), self.rc, self.chip_peer),
            lambda: self.copy(1, self.quarter(0, 1 - x), self.ra, self.x_peer),
            lambda: self.copy(2, self.quarter(1, 1 - y), self.rb, self.y_peer),
            lambda: self.copy(3, self.eighth(0, 1 - y), self.ta, self.y_peer),
            lambda: self.copy(4, self.eighth(1, 1 - x), self.tb, self.x_peer),
            lambda: self.copy(5, p.at[one(0)], o.at[self.mine(0)], self.y_peer),
            lambda: self.copy(6, p.at[one(1)], o.at[self.mine(1)], self.x_peer),
            lambda: self.copy(7, o.at[pair_a], o.at[pair_a], self.x_peer),
            lambda: self.copy(8, o.at[pair_b], o.at[pair_b], self.y_peer),
            lambda: self.copy(9, o.at[pl.ds(core * 8, 8)], o.at[pl.ds(core * 8, 8)], self.chip_peer),
        ][at]()

    def begin(self):
        self.hop(0).start()

    def by_core(self, core):
        return self.u.at[pl.ds(core * 8, 8)]

    def quarter(self, half, at):
        return self.s1.at[pl.ds(4 * half + 2 * at, 2)]

    def eighth(self, half, at):
        return (self.sa, self.sb)[half].at[pl.ds(at, 1)]

    def result(self, half):
        return self.p.at[pl.ds(half, 1)]

    def first(self):
        self.got(0, self.rc)
        self.add(self.s1, self.by_core(self.core), self.rc)
        self.hop(1).start()
        self.hop(2).start()

    def second(self):
        self.got(1, self.ra)
        self.add(self.sa, self.quarter(0, self.x), self.ra)
        self.hop(3).start()
        self.got(2, self.rb)
        self.add(self.sb, self.quarter(1, self.y), self.rb)
        self.hop(4).start()

    def third(self):
        self.got(3, self.ta)
        self.add(self.result(0), self.eighth(0, self.y), self.ta)
        self.got(4, self.tb)
        self.add(self.result(1), self.eighth(1, self.x), self.tb)

    def reduced(self):
        for at in range(5):
            self.hop(at).wait_send()

    def kept(self, half):
        return pltpu.make_async_copy(self.p.at[pl.ds(half, 1)], self.o.at[self.mine(half)], self.loc.at[half])

    def spread1(self):
        self.hop(5).start()
        self.hop(6).start()
        self.kept(0).start()
        self.kept(1).start()

    def spread2(self):
        x, y, core = self.x, self.y, self.core
        self.kept(0).wait()
        self.got(5, self.o.at[pl.ds(core * 8 + 2 * x + 1 - y, 1)])
        self.hop(7).start()
        self.kept(1).wait()
        self.got(6, self.o.at[pl.ds(core * 8 + 4 + 2 * y + 1 - x, 1)])
        self.hop(8).start()

    def spread3(self):
        x, y, core = self.x, self.y, self.core
        self.got(7, self.o.at[pl.ds(core * 8 + 2 - 2 * x, 2)])
        self.got(8, self.o.at[pl.ds(core * 8 + 6 - 2 * y, 2)])
        self.hop(9).start()

    def everywhere(self):
        self.got(9, self.o.at[pl.ds(8 - self.core * 8, 8)])
        for at in range(5, 10):
            self.hop(at).wait_send()


class StripSum(PlaneSum):
    @staticmethod
    def reduce_scratch(shape, dtype):
        lead, rows, cols = shape
        rest = lead - 2
        shapes = [(lead, rows)] * 2
        shapes += [(count, rows // 2) for count in (2, rest, 2, rest)] + [(count, rows // 4) for count in (2, rest)]
        return [pltpu.VMEM(item + (cols // 2,), dtype) for item in shapes] + [DMA((5,)), DMA((5,))]

    def lead(self, half):
        whole = (self.u if self.u is not None else self.o).shape[0]
        return pl.ds(0, 2) if half == 0 else pl.ds(2, whole - 2)

    def strip(self, core):
        size = (self.u if self.u is not None else self.o).shape[2] // 2
        return pl.ds(pl.multiple_of(core * size, 128), size)

    def rows(self, at, parts):
        size = (self.u if self.u is not None else self.o).shape[1] // parts
        return pl.ds(pl.multiple_of(at * size, 16), size)

    def by_core(self, core):
        return self.u.at[:, :, self.strip(core)]

    def quarter(self, half, at):
        return self.s1.at[self.lead(half), self.rows(at, 2)]

    def eighth(self, half, at):
        return (self.sa, self.sb)[half].at[:, self.rows(at, 4)]

    def result(self, half):
        return self.p.at[half, pl.ds(0, 2 if half == 0 else self.u.shape[0] - 2)]

    def hop(self, at):
        if at < 5:
            return super().hop(at)
        o, x, y = self.o, self.x, self.y
        mine = lambda half: o.at[
            self.lead(half), self.rows(2 * x + y if half == 0 else 2 * y + x, 4), self.strip(self.core)
        ]
        pair = lambda half: o.at[self.lead(half), self.rows(x if half == 0 else y, 2), self.strip(self.core)]
        both = o.at[:, :, self.strip(self.core)]
        return [
            lambda: self.copy(5, self.result(0), mine(0), self.y_peer),
            lambda: self.copy(6, self.result(1), mine(1), self.x_peer),
            lambda: self.copy(7, pair(0), pair(0), self.x_peer),
            lambda: self.copy(8, pair(1), pair(1), self.y_peer),
            lambda: self.copy(9, both, both, self.chip_peer),
        ][at - 5]()

    def kept(self, half):
        x, y = self.x, self.y
        mine = self.o.at[
            self.lead(half), self.rows(2 * x + y if half == 0 else 2 * y + x, 4), self.strip(self.core)
        ]
        return pltpu.make_async_copy(self.result(half), mine, self.loc.at[half])

    def spread2(self):
        x, y, mine = self.x, self.y, self.strip(self.core)
        self.kept(0).wait()
        self.got(5, self.o.at[self.lead(0), self.rows(2 * x + 1 - y, 4), mine])
        self.hop(7).start()
        self.kept(1).wait()
        self.got(6, self.o.at[self.lead(1), self.rows(2 * y + 1 - x, 4), mine])
        self.hop(8).start()

    def spread3(self):
        mine = self.strip(self.core)
        self.got(7, self.o.at[self.lead(0), self.rows(1 - self.x, 2), mine])
        self.got(8, self.o.at[self.lead(1), self.rows(1 - self.y, 2), mine])
        self.hop(9).start()

    def everywhere(self):
        self.got(9, self.o.at[:, :, self.strip(1 - self.core)])
        for at in range(5, 10):
            self.hop(at).wait_send()


def unit_pieces(unit):
    return jax.ShapeDtypeStruct((2,) + unit.shape[1:], unit.dtype)


def line_greet(bar, me, n):
    @pl.when(me > 0)
    def _():
        pl.semaphore_signal(bar, inc=1, device_id={"tensor": me - 1}, device_id_type=MESH)

    @pl.when(me < n - 1)
    def _():
        pl.semaphore_signal(bar, inc=1, device_id={"tensor": me + 1}, device_id_type=MESH)

    return jnp.where(me > 0, 1, 0) + jnp.where(me < n - 1, 1, 0)


class LineScatter:
    def __init__(self, n, x, o, buf, tmp, send, recv):
        self.n, self.x, self.o, self.buf, self.tmp, self.send, self.recv = n, x, o, buf, tmp, send, recv
        self.me = lax.axis_index("tensor")

    @staticmethod
    def scratch(n, own, cols, dtype):
        return [
            pltpu.VMEM((2, n - 1, own, cols), dtype),
            pltpu.VMEM((2, n - 1, own, cols), dtype),
            DMA((2, n - 1)),
            DMA((2, n - 1)),
        ]

    def term(self, d, k):
        return self.n - 1 - k if d == 0 else k

    def sends(self, d, k):
        return self.me < self.n - 1 - k if d == 0 else self.me > k

    def behind(self, d):
        return self.me > 0 if d == 0 else self.me < self.n - 1

    def copy(self, d, k, first):
        return pltpu.make_async_remote_copy(
            src_ref=self.x.at[self.term(d, k)] if first else self.tmp.at[d, k],
            dst_ref=self.buf.at[d, k],
            send_sem=self.send.at[d, k],
            recv_sem=self.recv.at[d, k],
            device_id={"tensor": jnp.clip(self.me + 1 if d == 0 else self.me - 1, 0, self.n - 1)},
            device_id_type=MESH,
        )

    def landed(self, d, k):
        return pltpu.make_async_copy(self.buf.at[d, k], self.buf.at[d, k], self.recv.at[d, k])

    def begin(self, ks):
        for d in range(2):

            @pl.when(jnp.logical_not(self.behind(d)))
            def _():
                for k in ks:
                    self.copy(d, k, True).start()

    def step(self, k, which=None):
        for d in range(2):
            now = self.behind(d) & self.sends(d, k)

            @pl.when(now if which is None else now & which(d))
            def _():
                self.landed(d, k).wait()
                at = self.term(d, k)
                both = self.buf[d, k].astype(jnp.float32) + self.x[at].astype(jnp.float32)
                self.tmp[d, k] = both.astype(self.tmp.dtype)
                self.copy(d, k, False).start()

    def end(self):
        self.o[...] = self.x[self.me].astype(jnp.float32)
        for d in range(2):
            for k in range(self.n - 1):

                @pl.when(self.behind(d) & (self.me == self.term(d, k)))
                def _():
                    self.landed(d, k).wait()
                    self.o[...] += self.buf[d, k].astype(jnp.float32)

        for d in range(2):
            for k in range(self.n - 1):

                @pl.when(self.sends(d, k))
                def _():
                    self.copy(d, k, False).wait_send()


GELU_SCALE = 0.7978845608028654
GELU_CUBE = 0.044715


def feed_kernel(n, nc, heads, chunks, piece_ref, *rest):
    (token_hbm, out_ref, abias_hbm, gain_hbm, shift_hbm, up_hbm, down_hbm, bias_hbm, near_ref, cot_ref), rest = rest[:10], rest[10:]
    outs, heads_ref, rest = rest[:7], rest[7], rest[8:]
    kept_refs, rest = rest[:7], rest[7:]
    feed_ref, p1_ref, p2_ref, middle_ref, gm_ref, vec_ref, u3 = kept_refs
    (token_ref, abias_ref, gain_ref, shift_ref, bias_ref, osem), rest = rest[:6], rest[6:]
    leave = copies(tuple(zip(kept_refs, outs)), osem)
    (o_ref, sum_ref, att_ref, gpiece, bsend, brecv, bloc), rest = rest[:7], rest[7:]
    (x_ref, up_ref, down_ref, grad_ref, wsem, asend, arecv, aloc, csend, crecv, cloc), rest = rest[:11], rest[11:]
    (held, act, gp, part, acc, buf, tmp, u1, u2), rest = rest[:9], rest[9:]
    (gsend, grecv, loc, ssend, srecv), rest = rest[:5], rest[5:]
    plane = [PlaneSum(u1, p1_ref, None, rest[:10]), PlaneSum(u2, p2_ref, None, rest[10:20])]
    me = lax.axis_index("tensor")
    rows, width = token_ref.shape
    wide = up_ref.shape[1]
    few = rows // chunks
    f32, low = jnp.float32, jnp.bfloat16
    ctx, dp = lax.axis_index("context"), lax.axis_index("dp")
    place, total = ctx * n + me, nc * n
    my_head = me * heads + jnp.minimum(ctx, heads - 1)
    bar = pltpu.get_barrier_semaphore()
    for shift in range(1, total):
        other = lax.rem(place + shift, total)
        pl.semaphore_signal(bar, inc=1, device_id=spread(other, AXES, (nc, n)), device_id_type=MESH)
    pl.semaphore_signal(bar, inc=1, device_id={"dp": 1 - dp}, device_id_type=MESH)
    weights_in = copies(
        (
            (token_hbm, token_ref),
            (abias_hbm, abias_ref),
            (gain_hbm, gain_ref),
            (shift_hbm, shift_ref),
            (bias_hbm, bias_ref),
            (up_hbm, up_ref),
            (down_hbm, down_ref),
        ),
        wsem,
    )
    for item in weights_in:
        item.start()

    def grad_rows(block):
        return grad_ref.at[pl.ds(pl.multiple_of(block * rows, rows), rows)]

    def grad_on(d, s):
        block = jnp.clip(me - s if d == 0 else me + s, 0, n - 1)
        return pltpu.make_async_remote_copy(
            src_ref=near_ref.at[block] if s == 1 else grad_rows(block),
            dst_ref=grad_rows(block),
            send_sem=csend.at[d, s],
            recv_sem=crecv.at[d, s],
            device_id={"tensor": jnp.clip(me + 1 if d == 0 else me - 1, 0, n - 1)},
            device_id_type=MESH,
        )

    def grad_sends(d, s):
        return (me - s >= 0) & (me < n - 1) if d == 0 else (me + s < n) & (me > 0)

    def grad_near(d):
        block = jnp.clip(me - 1 if d == 0 else me + 1, 0, n - 1)
        return pltpu.make_async_copy(near_ref.at[block], grad_rows(block), cloc.at[d])

    def grad_own():
        return pltpu.make_async_copy(cot_ref, grad_rows(me), cloc.at[2])

    def beside(d):
        return me > 0 if d == 0 else me < n - 1

    grad_own().start()
    for d in range(2):

        @pl.when(beside(d))
        def _():
            grad_near(d).start()

    pl.semaphore_wait(bar, total)

    def to_place(shift):
        other = lax.rem(place + shift, total)
        return pltpu.make_async_remote_copy(
            src_ref=piece_ref.at[other],
            dst_ref=att_ref.at[my_head],
            send_sem=asend.at[shift],
            recv_sem=arecv.at[shift],
            device_id=spread(other, AXES, (nc, n)),
            device_id_type=MESH,
        )

    @pl.when(ctx < heads)
    def _():
        for shift in range(1, total):
            to_place(shift).start()
        stay = pltpu.make_async_copy(piece_ref.at[place], att_ref.at[my_head], aloc)
        stay.start()
        stay.wait()

    for d in range(2):

        @pl.when(grad_sends(d, 1))
        def _():
            grad_on(d, 1).start()

    for shift in range(1, total):
        source = lax.rem(place + total - shift, total)
        at_ctx, at_ten = lax.div(source, n), lax.rem(source, n)

        @pl.when(at_ctx < heads)
        def _():
            landed = att_ref.at[at_ten * heads + jnp.minimum(at_ctx, heads - 1)]
            pltpu.make_async_copy(landed, landed, arecv.at[shift]).wait()

    for item in weights_in[:4]:
        item.wait()
    attended = att_ref[...].reshape(width, rows)
    middle = token_ref[...].astype(f32) + dot(attended, out_ref[...], ((0,), (0,))) + row(abias_ref)
    middle_ref[...] = middle
    leave[3].start()
    x_ref[...] = (norm_parts(middle)[0] * row(gain_ref) + row(shift_ref)).astype(low)

    @pl.when(ctx < heads)
    def _():
        for shift in range(1, total):
            to_place(shift).wait_send()

    def rows_of(block):
        return pl.ds(pl.multiple_of(block * rows, rows), rows)

    def neighbour(d):
        return {"tensor": jnp.clip(jnp.where(d == 0, me + 1, me - 1), 0, n - 1)}

    def onward(d):
        return jnp.where(d == 0, me, n - 1 - me) < n - 1

    def hand_on(d, s, block, first):
        return pltpu.make_async_remote_copy(
            src_ref=x_ref if first else held.at[rows_of(block)],
            dst_ref=held.at[rows_of(block)],
            send_sem=gsend.at[d, s],
            recv_sem=grecv.at[d, s],
            device_id=neighbour(d),
            device_id_type=MESH,
        )

    def chunk(block, c):
        return pl.ds(pl.multiple_of(block * rows + c * few, few), few)

    def back(d, block, c, first):
        at = chunk(block, c)
        return pltpu.make_async_remote_copy(
            src_ref=part.at[at] if first else tmp.at[at],
            dst_ref=buf.at[d, at],
            send_sem=ssend.at[block, c],
            recv_sem=srecv.at[d, block, c],
            device_id=neighbour(d),
            device_id_type=MESH,
        )

    for d in range(2):

        @pl.when(onward(d))
        def _():
            hand_on(d, 0, me, True).start()

    own = pltpu.make_async_copy(x_ref, held.at[rows_of(me)], loc)
    own.start()
    sum_ref[...] = jnp.zeros_like(sum_ref)
    own.wait()
    for item in weights_in[4:]:
        item.wait()
    grad_own().wait()
    for d in range(2):

        @pl.when(beside(d))
        def _():
            grad_near(d).wait()

    for s in range(1, n - 1):
        for d in range(2):
            block = me - 1 - s if d == 0 else me + 1 + s

            @pl.when((block >= 0) & (block < n))
            def _():
                landed = grad_rows(jnp.clip(block, 0, n - 1))
                pltpu.make_async_copy(landed, landed, crecv.at[d, s]).wait()

            if s + 1 < n - 1:

                @pl.when(grad_sends(d, s + 1))
                def _():
                    grad_on(d, s + 1).start()

        if s == n - 3:
            break
    columns = 256

    def work(block):
        here = rows_of(block)
        acc[...] = jnp.zeros_like(acc)

        @pl.loop(0, wide // columns)
        def _(j):
            at = pl.ds(pl.multiple_of(j * columns, columns), columns)
            pre = dot(held[here, :], up_ref[:, at], ((1,), (0,))) + bias_ref[at].reshape(1, -1)
            square = pre * pre
            tanh = jnp.tanh(GELU_SCALE * pre * (1.0 + GELU_CUBE * square))
            act[here, at] = (0.5 * pre * (1.0 + tanh)).astype(low)
            slope = 0.5 * (1.0 + tanh) + 0.5 * pre * (1.0 - tanh * tanh) * (
                GELU_SCALE * (1.0 + 3.0 * GELU_CUBE * square)
            )
            grad = (dot(grad_ref[here, :], down_ref[at, :], ((1,), (1,))) * slope).astype(low)
            gp[here, at] = grad
            acc[...] += dot(grad, up_ref[:, at], ((1,), (1,)))

        part[here, :] = acc[...].astype(low)
        sum_ref[...] += jnp.sum(gp[here, :].astype(f32), axis=0, keepdims=True)

    near = jnp.minimum(me, n - 1 - me)
    toward = jnp.where(2 * me < n - 1, -1, 1)

    @pl.loop(0, n)
    def _(slot):
        paired = slot <= 2 * near
        distance = jnp.where(paired, lax.div(slot + 1, 2), slot - near)
        side = jnp.where(paired & (lax.rem(slot, 2) == 1), toward, -toward)
        block = me + side * distance
        d = jnp.where(block < me, 0, 1)
        s = jnp.maximum(distance - 1, 0)

        @pl.when(slot > 0)
        def _():
            landed = held.at[rows_of(block)]
            pltpu.make_async_copy(landed, landed, grecv.at[d, s]).wait()

            @pl.when(onward(d))
            def _():
                hand_on(d, jnp.minimum(s + 1, n - 2), block, False).start()

        @pl.when(distance == n - 1)
        def _():
            landed = grad_rows(block)
            pltpu.make_async_copy(landed, landed, crecv.at[d, n - 2]).wait()

        work(block)

        @pl.when((slot > 0) & ((me == 0) | (me == n - 1)))
        def _():
            for c in range(chunks):
                back(1 - d, block, c, True).start()

    def weights(left, right, unit):
        half = wide // 2

        @pl.loop(0, 2)
        def _(j):
            at = pl.ds(pl.multiple_of(j * half, 128), half)
            total = dot(left[:, at], right[...], ((0,), (0,)))
            unit[pl.ds(8 * j, 8)] = total.astype(low).reshape((8,) + unit.shape[1:])

    weights(act, grad_ref, u1)
    plane[0].begin()
    weights(held, gp, u2)
    plane[1].begin()

    def relay(way, block):
        d = jnp.where(way > 0, 0, 1)

        @pl.when((me > 0) & (me < n - 1) & (block >= 0) & (block < n))
        def _():
            for c in range(chunks):
                at = chunk(block, c)
                landed = buf.at[d, at]
                pltpu.make_async_copy(landed, landed, srecv.at[d, block, c]).wait()
                tmp[at, :] = (buf[d, at, :].astype(f32) + part[at, :].astype(f32)).astype(low)
                back(d, block, c, False).start()

    plane[0].first()
    for j in range(1, n):
        relay(-toward, me - toward * j)
        if j == 1:
            plane[1].first()

    @pl.loop(0, n)
    def _(block):
        here = rows_of(block)
        feed_ref[here, :] = dot(act[here, :], down_ref[...], ((1,), (0,))).astype(low)

    leave[0].start()

    plane[0].second()
    plane[1].second()
    for j in range(1, n):
        relay(toward, me + toward * j)
    for item in plane:
        item.third()
    for c in range(chunks):
        at = chunk(me, c)
        mine = pl.ds(c * few, few)
        o_ref[mine, :] = part[at, :].astype(f32)
        for d in range(2):

            @pl.when(me > 0 if d == 0 else me < n - 1)
            def _():
                landed = buf.at[d, at]
                pltpu.make_async_copy(landed, landed, srecv.at[d, me, c]).wait()
                o_ref[mine, :] += buf[d, at, :].astype(f32)

    grad = o_ref[...]
    normed, scale = norm_parts(middle_ref[...])
    above = grad_ref[rows_of(me), :].astype(f32)
    grad_middle = above + norm_backward(grad, normed, scale, row(gain_ref))
    gm_ref[...] = grad_middle
    for at in (1, 2, 4):
        leave[at].start()
    gm_low = grad_middle.astype(low)
    back_out = dot(out_ref[...], gm_low, ((1,), (1,))).astype(low)
    gpiece[...] = back_out.reshape(gpiece.shape)
    vec_ref[...] = jnp.zeros_like(vec_ref)
    vec_ref[2:3, :] = jnp.sum(gm_low.astype(f32), axis=0, keepdims=True)

    def to_head(shift):
        other = lax.rem(place + shift, total)
        at_ctx, at_ten = lax.div(other, n), lax.rem(other, n)
        return at_ctx < heads, pltpu.make_async_remote_copy(
            src_ref=gpiece.at[at_ten * heads + jnp.minimum(at_ctx, heads - 1)],
            dst_ref=heads_ref.at[place],
            send_sem=bsend.at[shift],
            recv_sem=brecv.at[shift],
            device_id={"context": at_ctx, "tensor": at_ten},
            device_id_type=MESH,
        )

    for shift in range(1, total):
        goes, item = to_head(shift)

        @pl.when(goes)
        def _():
            item.start()

    stay = pltpu.make_async_copy(gpiece.at[my_head], heads_ref.at[place], bloc)
    stay.start()
    u3[...] = dot(att_ref[...].reshape(width, rows), gm_low, ((1,), (0,))).astype(low).reshape(u3.shape)
    leave[6].start()
    vec_ref[3:4, :] = jnp.sum(grad * normed, axis=0, keepdims=True)
    vec_ref[4:5, :] = jnp.sum(grad, axis=0, keepdims=True)
    vec_ref[5:6, :] = jnp.sum(above, axis=0, keepdims=True)
    vec_ref[6:7, :] = sum_ref[...]
    leave[5].start()
    stay.wait()

    @pl.when(ctx < heads)
    def _():
        for shift in range(1, total):
            source = lax.rem(place + total - shift, total)
            landed = heads_ref.at[source]
            pltpu.make_async_copy(landed, landed, brecv.at[shift]).wait()

    for shift in range(1, total):
        goes, item = to_head(shift)

        @pl.when(goes)
        def _():
            item.wait_send()

    for item in leave:
        item.wait()
    for d in range(2):
        for s in range(n - 1):
            block = me - s if d == 0 else me + s

            @pl.when(onward(d) & (block >= 0) & (block < n))
            def _():
                hand_on(d, s, me, True).wait_send()

    for block in range(n):

        @pl.when(me != block)
        def _():
            for c in range(chunks):
                back(jnp.where(me < block, 0, 1), block, c, True).wait_send()

    for d in range(2):
        for s in range(1, n - 1):

            @pl.when(grad_sends(d, s))
            def _():
                grad_on(d, s).wait_send()

    for item in plane:
        item.reduced()


def feed_part(pieces, tokens, out_weight, vectors, up, down, bias, near, cotangent, n, nc, heads, collective_id):
    rows, width = tokens.shape
    wide = up.shape[1]
    chunks = 4
    total = n * rows
    low, f32 = jnp.bfloat16, jnp.float32
    unit = (16, wide // 16, width)
    piece = jax.ShapeDtypeStruct((2,) + unit[1:], low)
    return pl.pallas_call(
        functools.partial(feed_kernel, n, nc, heads, chunks),
        out_shape=(
            jax.ShapeDtypeStruct((total, width), low),
            piece,
            piece,
            jax.ShapeDtypeStruct((rows, width), f32),
            jax.ShapeDtypeStruct((rows, width), f32),
            jax.ShapeDtypeStruct((8, width), f32),
            jax.ShapeDtypeStruct((n, width // n, width), low),
            jax.ShapeDtypeStruct(pieces.shape, low),
        ),
        in_specs=[VM, HB, VM, HB, HB, HB, HB, HB, HB, VM, HB],
        out_specs=(HB,) * 7 + (VM,),
        scratch_shapes=[
            pltpu.VMEM((total, width), low),
            pltpu.VMEM(piece.shape, low),
            pltpu.VMEM(piece.shape, low),
            pltpu.VMEM((rows, width), f32),
            pltpu.VMEM((rows, width), f32),
            pltpu.VMEM((8, width), f32),
            pltpu.VMEM((n, width // n, width), low),
            pltpu.VMEM(tokens.shape, tokens.dtype),
            pltpu.VMEM((width,), f32),
            pltpu.VMEM((width,), f32),
            pltpu.VMEM((width,), f32),
            pltpu.VMEM((wide,), f32),
            DMA((7,)),
            pltpu.VMEM((rows, width), f32),
            pltpu.VMEM((1, wide), f32),
            pltpu.VMEM((n * heads,) + pieces.shape[1:], low),
            pltpu.VMEM((n * heads,) + pieces.shape[1:], low),
            DMA((nc * n,)),
            DMA((nc * n,)),
            DMA,
            pltpu.VMEM((rows, width), low),
            pltpu.VMEM(up.shape, low),
            pltpu.VMEM(down.shape, low),
            pltpu.VMEM((total, width), low),
            DMA((7,)),
            DMA((nc * n,)),
            DMA((nc * n,)),
            DMA,
            DMA((2, n - 1)),
            DMA((2, n - 1)),
            DMA((3,)),
            pltpu.VMEM((total, width), low),
            pltpu.VMEM((total, wide), low),
            pltpu.VMEM((total, wide), low),
            pltpu.VMEM((total, width), low),
            pltpu.VMEM((rows, width), f32),
            pltpu.VMEM((2, total, width), low),
            pltpu.VMEM((total, width), low),
            pltpu.VMEM(unit, low),
            pltpu.VMEM(unit, low),
            DMA((2, n - 1)),
            DMA((2, n - 1)),
            DMA,
            DMA((n, chunks)),
            DMA((2, n, chunks)),
        ]
        + PlaneSum.reduce_scratch(unit, low) * 2,

        compiler_params=remote_params(collective_id, 40),
    )(pieces, tokens, out_weight, *vectors, up, down, bias, near, cotangent)


def last_kernel(n, nc, heads, shared, count, x_ref, w_hbm, h_hbm, a_hbm, feed_hbm, mid_hbm, bias_hbm, *rest):
    ps, rest = rest[:count], rest[count:]
    (token_hbm, gain_hbm, middle_hbm, vec_hbm), rest = rest[:4], rest[4:]
    (out_ref, g_ref, v_ref, po_ref, ao_ref), rest = rest[:5], rest[5:]
    outs, rest = rest[:count], rest[count:]
    (rows_ref, w_ref, h_ref, token_ref, middle_ref, part, sum_ref, u_ref, piece), rest = rest[:9], rest[9:]
    (hsend, hrecv, hloc, win), rest = rest[:4], rest[4:]
    (feed_ref, fsum_ref, mid_ref, bias_ref, gain_ref, vec_ref), rest = rest[:6], rest[6:]
    feed_line = LineScatter(n, feed_ref, fsum_ref, *rest[:4])
    rest = rest[4:]
    chunks = 4
    own = token_ref.shape[0]
    few = own // chunks
    lines = [
        LineScatter(n, part.at[:, pl.ds(c * few, few)], sum_ref.at[pl.ds(c * few, few)], *rest[4 * c : 4 * c + 4])
        for c in range(chunks)
    ]
    rest = rest[4 * chunks :]
    project = StripSum(u_ref, piece, po_ref, rest[:10], rest[10:13])
    rest = rest[13:]
    feeds = [PlaneSum(None, ps[i], outs[i], None, rest[3 * i : 3 * i + 3]) for i in range(count)]
    rest = rest[3 * count :]
    (land, zsend, zrecv, zloc, a_ref, strip_ref, strip_piece), rest = rest[:7], rest[7:]
    attend = StripSum(strip_ref, strip_piece, None, rest[:10])
    rest = rest[10:]
    (asend, arecv, aloc, now), rest = rest[:4], rest[4:]
    sizes = (n, 2 * nc)
    bufs, sems = rest[:2], rest[2:]
    f32, low = jnp.float32, jnp.bfloat16

    ten, ctx, x = (lax.axis_index(name) for name in ("tensor", "context", "dp"))
    place = ctx * 2 + x
    bar = pltpu.get_barrier_semaphore()
    for shift in range(1, n):
        pl.semaphore_signal(bar, inc=1, device_id={"tensor": lax.rem(ten + shift, n)}, device_id_type=MESH)
    for shift in range(1, 8):
        other = lax.rem(place + shift, 8)
        pl.semaphore_signal(
            bar, inc=1, device_id={"context": lax.div(other, 2), "dp": lax.rem(other, 2)}, device_id_type=MESH
        )
    copies_in = copies(
        (
            (feed_hbm, feed_ref),
            (a_hbm, strip_ref),
            (token_hbm, token_ref),
            (w_hbm, w_ref),
            (h_hbm, h_ref),
            (middle_hbm, middle_ref),
            (mid_hbm, mid_ref),
            (bias_hbm, bias_ref),
            (gain_hbm, gain_ref),
            (vec_hbm, vec_ref),
        ),
        win,
    )
    for item in copies_in:
        item.start()
    pl.semaphore_wait(bar, n + 6)

    half = 2 * own
    far = 1 - lax.div(ten, 2)
    pairs = (far, 1 - far)

    def columns(pair):
        return pl.ds(pl.multiple_of(pair * half, 128), half)

    def ship(index, shift):
        other = lax.rem(ctx + shift, nc)
        return pltpu.make_async_remote_copy(
            src_ref=x_ref.at[other, :, :, columns(pairs[index])],
            dst_ref=rows_ref.at[:, jnp.minimum(ctx, heads - 1), :, columns(pairs[index])],
            send_sem=hsend.at[index, shift],
            recv_sem=hrecv.at[index, shift],
            device_id={"context": other},
            device_id_type=MESH,
        )

    @pl.when(ctx < heads)
    def _():
        for index in range(2):
            for shift in range(1, nc):
                ship(index, shift).start()
        stay = pltpu.make_async_copy(x_ref.at[ctx], rows_ref.at[:, ctx], hloc)
        stay.start()
        stay.wait()

    def across(shift):
        other = lax.rem(ten + shift, n)
        return pltpu.make_async_remote_copy(
            src_ref=strip_piece.at[lax.div(other, 2), lax.rem(other, 2)],
            dst_ref=land.at[ten],
            send_sem=zsend.at[shift],
            recv_sem=zrecv.at[shift],
            device_id={"tensor": other},
            device_id_type=MESH,
        )

    copies_in[0].wait()
    feed_line.begin((0,))
    mine = pltpu.make_async_copy(strip_piece.at[lax.div(ten, 2), lax.rem(ten, 2)], land.at[ten], zloc)
    copies_in[1].wait()
    attend.begin()
    for item in feeds:
        item.spread1()

    def there(at):
        ctx_, x_ = lax.div(at, 2), lax.rem(at, 2)
        y_ = lax.div(ctx_, 2)
        row_ = jnp.where(ten < n // 2, 2 * x_ + y_, 2 * y_ + x_)
        rows = pl.ds(pl.multiple_of(row_ * a_ref.shape[0], 16), a_ref.shape[0])
        cols = pl.ds(pl.multiple_of(lax.rem(ctx_, 2) * a_ref.shape[1], 128), a_ref.shape[1])
        return ao_ref.at[rows, cols]

    def push(shift):
        other = lax.rem(place + shift, 8)
        return pltpu.make_async_remote_copy(
            src_ref=a_ref,
            dst_ref=there(place),
            send_sem=asend.at[shift],
            recv_sem=arecv.at[shift],
            device_id={"context": lax.div(other, 2), "dp": lax.rem(other, 2)},
            device_id_type=MESH,
        )

    kept = pltpu.make_async_copy(a_ref, there(place), aloc)

    def exchange():
        for shift in range(1, n):
            across(shift).start()
        mine.start()

    def gathered():
        mine.wait()
        for shift in range(1, n):
            source = lax.rem(ten + n - shift, n)
            pltpu.make_async_copy(land.at[source], land.at[source], zrecv.at[shift]).wait()
        value = land[0].astype(f32)
        for at in range(1, n):
            value = value + land[at].astype(f32)
        a_ref[...] = value.astype(low)
        for shift in range(1, 8):
            push(shift).start()
        kept.start()

    for item in copies_in[2:]:
        item.wait()
    normed, scale = norm_parts(token_ref[...].astype(f32))
    now[0] = vec_ref[...]
    attend.first()

    def partials(index):
        at = columns(pairs[index])
        for shift in range(1, nc):
            source = lax.rem(ctx + nc - shift, nc)

            @pl.when(source < heads)
            def _():
                ref = rows_ref.at[:, jnp.minimum(source, heads - 1), :, at]
                pltpu.make_async_copy(ref, ref, hrecv.at[index, shift]).wait()

        total = 0.0
        for kind in range(3):
            grads = rows_ref[kind, :, :, at].reshape(heads * HEAD_DIM, half)
            total = total + dot(grads, w_ref[kind], ((0,), (0,)))
        part[pl.ds(2 * pairs[index], 2)] = total.astype(low).reshape(2, own, total.shape[1])

    first = lambda d: (ten < n // 2) if d == 0 else (ten >= n // 2)
    second = lambda d: (ten >= n // 2) if d == 0 else (ten < n // 2)
    feed_line.step(0, first)
    partials(0)
    for line in lines:
        line.begin((0, 1))
    partials(1)
    for line in lines:
        line.begin((2,))
    for item in feeds:
        item.spread2()
    attend.second()
    for line in lines:
        line.step(0, first)
    attend.third()
    exchange()
    feed_line.begin((1, 2))
    for kind in range(3):
        grads = rows_ref[kind].reshape(heads * HEAD_DIM, n * own)
        u_ref[kind] = dot(grads, h_ref[...], ((1,), (0,))).astype(low)
    project.begin()
    for line in lines:
        line.step(1, first)
    feed_line.step(0, second)
    ends = jnp.concatenate(
        [rows_ref[kind].reshape(heads * HEAD_DIM, n * own) for kind in (0, 2)], axis=0
    )
    bias = dot(jnp.ones((8, n * own), low), ends, ((1,), (1,)))
    now[0, 7:8, 0 : bias.shape[1]] = bias[0:1]
    gathered()
    project.first()
    for item in feeds:
        item.spread3()
    project.second()
    for k in range(n - 1):
        for line in lines:
            line.step(k, second)
    project.third()
    project.spread1()
    for line in lines:
        line.end()
    grad = sum_ref[...]
    now[0, 0:1] = jnp.sum(grad * normed, axis=0, keepdims=True)
    now[0, 1:2] = jnp.sum(grad, axis=0, keepdims=True)
    alone = now[0]

    def where(stage):
        return ten if stage == 0 else place

    def stage_copy(stage, shift):
        other = lax.rem(where(stage) + shift, sizes[stage])
        peer = {"tensor": other} if stage == 0 else {"context": lax.div(other, 2), "dp": lax.rem(other, 2)}
        return pltpu.make_async_remote_copy(
            src_ref=now.at[stage],
            dst_ref=bufs[stage].at[where(stage)],
            send_sem=sems[2 * stage].at[shift],
            recv_sem=sems[2 * stage + 1].at[shift],
            device_id=peer,
            device_id_type=MESH,
        )

    def stage_start(stage):
        for shift in range(1, sizes[stage]):
            stage_copy(stage, shift).start()
        bufs[stage][where(stage)] = now[stage]

    def stage_end(stage):
        buf, size = bufs[stage], sizes[stage]
        for shift in range(1, size):
            source = lax.rem(where(stage) + size - shift, size)
            pltpu.make_async_copy(buf.at[source], buf.at[source], sems[2 * stage + 1].at[shift]).wait()
        total = buf[0]
        for at in range(1, size):
            total = total + buf[at]
        if stage == 0:
            line_ = lax.broadcasted_iota(jnp.int32, total.shape, 0)
            now[1] = jnp.where(line_ < shared, total, alone)
        else:
            v_ref[...] = total

    stage_start(0)
    back = norm_backward(grad, normed, scale, row(gain_ref))
    g_ref[...] = (middle_ref[...] + back).astype(g_ref.dtype)
    project.spread2()
    feed_line.step(1, first)
    stage_end(0)
    stage_start(1)
    project.spread3()
    feed_line.end()
    out_ref[...] = (mid_ref[...] + fsum_ref[...] + row(bias_ref)).astype(low)
    kept.wait()
    for shift in range(1, 8):
        source = there(lax.rem(place + 8 - shift, 8))
        pltpu.make_async_copy(source, source, arecv.at[shift]).wait()
    for item in feeds:
        item.everywhere()
    stage_end(1)
    project.everywhere()
    project.reduced()
    attend.reduced()

    @pl.when(ctx < heads)
    def _():
        for index in range(2):
            for shift in range(1, nc):
                ship(index, shift).wait_send()

    for shift in range(1, n):
        across(shift).wait_send()
    for shift in range(1, 8):
        push(shift).wait_send()
    for stage in range(2):
        for shift in range(1, sizes[stage]):
            stage_copy(stage, shift).wait_send()


def last_part(x, weight, hidden, attend_pieces, feed, middle, bias, pieces, tokens, gain, grad_middle, vectors, shared, n, heads, collective_id):
    nc = x.shape[0]
    own, cols = tokens.shape
    count = len(pieces)
    f32, low = jnp.float32, jnp.bfloat16
    whole = lambda item: jax.ShapeDtypeStruct((16,) + item.shape[1:], item.dtype)
    wide, deep = attend_pieces.shape[1] // 4, attend_pieces.shape[2] // 2
    unit = (3, heads * HEAD_DIM, cols)
    result = pl.pallas_call(
        functools.partial(last_kernel, n, nc, heads, shared, count),
        out_shape=(
            jax.ShapeDtypeStruct((own, cols), low),
            jax.ShapeDtypeStruct((own, cols), low),
            jax.ShapeDtypeStruct(vectors.shape, f32),
            jax.ShapeDtypeStruct(unit, low),
            jax.ShapeDtypeStruct((4 * wide, 2 * deep), low),
        )
        + tuple(whole(item) for item in pieces),
        in_specs=[VM] + [HB] * (10 + count),
        out_specs=(VM,) * (5 + count),
        scratch_shapes=[
            pltpu.VMEM((3, heads, HEAD_DIM, n * own), low),
            pltpu.VMEM(weight.shape, low),
            pltpu.VMEM(hidden.shape, low),
            pltpu.VMEM(tokens.shape, low),
            pltpu.VMEM((own, cols), f32),
            pltpu.VMEM((n, own, cols), low),
            pltpu.VMEM((own, cols), f32),
            pltpu.VMEM(unit, low),
            pltpu.VMEM((2, 2, unit[1] // 4, cols // 2), low),
            DMA((2, nc)),
            DMA((2, nc)),
            DMA,
            DMA((10,)),
            pltpu.VMEM((n, own, cols), low),
            pltpu.VMEM((own, cols), f32),
            pltpu.VMEM((own, cols), f32),
            pltpu.VMEM((cols,), f32),
            pltpu.VMEM((cols,), f32),
            pltpu.VMEM(vectors.shape, f32),
        ]
        + LineScatter.scratch(n, own, cols, low)
        + LineScatter.scratch(n, own // 4, cols, low) * 4
        + StripSum.reduce_scratch(unit, low)
        + PlaneSum.spread_scratch()
        + [item for _ in pieces for item in PlaneSum.spread_scratch()]
        + [pltpu.VMEM((n, wide, deep), low), DMA((n,)), DMA((n,)), DMA, pltpu.VMEM((wide, deep), low)]
        + [pltpu.VMEM(attend_pieces.shape, low), pltpu.VMEM((2, 2, wide, deep), low)]
        + StripSum.reduce_scratch(attend_pieces.shape, low)
        + [DMA((8,)), DMA((8,)), DMA, pltpu.VMEM((2,) + vectors.shape, f32)]
        + [pltpu.VMEM((size,) + vectors.shape, f32) for size in (n, 2 * nc)]
        + [DMA((size,)) for size in (n, 2 * nc) for _ in range(2)],
        compiler_params=remote_params(collective_id, 32),
    )(
        x, weight, hidden, attend_pieces, feed.reshape(n, own, cols), middle, bias,
        *pieces, tokens, gain, grad_middle, vectors,
    )
    return result[:5] + (result[5:],)


class LineGather:
    def __init__(self, n, x, o, send, recv):
        self.n, self.x, self.o, self.send, self.recv = n, x, o, send, recv
        self.me = lax.axis_index("tensor")

    def copy(self, d, s):
        me, n = self.me, self.n
        shard = jnp.clip(me - s if d == 0 else me + s, 0, n - 1)
        return pltpu.make_async_remote_copy(
            src_ref=self.x if s == 0 else self.o.at[shard],
            dst_ref=self.o.at[shard],
            send_sem=self.send.at[d, s],
            recv_sem=self.recv.at[d, s],
            device_id={"tensor": jnp.clip(me + 1 if d == 0 else me - 1, 0, n - 1)},
            device_id_type=MESH,
        )

    def sends(self, d, s):
        me, n = self.me, self.n
        return (me - s >= 0) & (me < n - 1) if d == 0 else (me + s < n) & (me > 0)

    def wait(self, d, s):
        me, n = self.me, self.n

        @pl.when(me - 1 - s >= 0 if d == 0 else me + 1 + s < n)
        def _():
            shard = jnp.clip(me - 1 - s if d == 0 else me + 1 + s, 0, n - 1)
            pltpu.make_async_copy(self.o.at[shard], self.o.at[shard], self.recv.at[d, s]).wait()

    def step(self, s):
        for d in range(2):
            if s > 0:
                self.wait(d, s - 1)

            @pl.when(self.sends(d, s))
            def _():
                self.copy(d, s).start()

    def pass_on(self, d, s, now):
        @pl.when(self.sends(d, s) & now)
        def _():
            self.copy(d, s).start()

    def last(self):
        for d in range(2):
            self.wait(d, self.n - 2)

    def finish(self, steps=None):
        for d in range(2):
            for s in range(steps or self.n - 1):

                @pl.when(self.sends(d, s))
                def _():
                    self.copy(d, s).wait_send()


def start_kernel(n, nc, heads, t_hbm, gain_hbm, shift_hbm, full_ref, w_hbm, b_hbm, c_ref, o_hbm, f_ref, q_ref, g_ref, *rest):
    (x_ref, held, proj, w_ref, o_ref, t_ref, gain_ref, shift_ref, b_ref, win), rest = rest[:10], rest[10:]
    arrive = copies(((t_hbm, t_ref), (gain_hbm, gain_ref), (shift_hbm, shift_ref), (b_hbm, b_ref)), win)
    for item in arrive:
        item.start()
    s1, r1, s2, r2, s5, r5, s3, r3, s4, r4, loc = rest
    me, ctx, x = lax.axis_index("tensor"), lax.axis_index("context"), lax.axis_index("dp")
    core, y = lax.rem(ctx, 2), lax.div(ctx, 2)
    rows, width = t_ref.shape
    half = 2 * rows
    bar = pltpu.get_barrier_semaphore()
    met = line_greet(bar, me, n)
    for shift in range(1, nc):
        pl.semaphore_signal(bar, inc=1, device_id={"context": lax.rem(ctx + shift, nc)}, device_id_type=MESH)
    pl.semaphore_signal(bar, inc=1, device_id={"dp": 1 - x}, device_id_type=MESH)
    weight_in = pltpu.make_async_copy(w_hbm, w_ref, loc.at[4])
    weight_in.start()
    for item in arrive:
        item.wait()
    normed, _ = norm_parts(t_ref[...].astype(jnp.float32))
    x_ref[...] = (normed * row(gain_ref) + row(shift_ref)).astype(x_ref.dtype)
    pl.semaphore_wait(bar, met + nc)

    tall, deep = held.shape[1:]
    strip = pl.ds(pl.multiple_of(core * deep, 128), deep)
    piece = full_ref.at[pl.ds(pl.multiple_of((2 * y + x) * tall, 16), tall), strip]
    small = LineGather(n, piece, held, s1, r1)
    large = LineGather(n, x_ref, o_ref, s2, r2)
    grads = LineGather(n, c_ref, g_ref, s5, r5)
    def move(s):
        large.step(s)
        for d in range(2):
            grads.pass_on(d, 0, me == (s if d == 0 else n - 1 - s))

    small.step(0)
    move(0)
    own = pltpu.make_async_copy(x_ref, o_ref.at[me], loc.at[0])
    own.start()
    mine = pltpu.make_async_copy(piece, held.at[me], loc.at[1])
    mine.start()
    mine.wait()
    own.wait()
    for s in range(1, n - 1):
        small.step(s)
    small.last()

    def there(y_, x_):
        return f_ref.at[:, pl.ds(pl.multiple_of((2 * y_ + x_) * tall, 16), tall), strip]

    x_peer, y_peer = {"dp": 1 - x}, {"context": lax.rem(ctx + 2, 4)}

    def hop(at):
        src, dst, peer = [
            (held, there(y, x), x_peer),
            (held, there(y, x), y_peer),
            (there(y, 1 - x), there(y, 1 - x), y_peer),
            (f_ref.at[:, :, strip], f_ref.at[:, :, strip], {"context": ctx + 1 - 2 * core}),
        ][at]
        return pltpu.make_async_remote_copy(
            src_ref=src,
            dst_ref=dst,
            send_sem=s3.at[at],
            recv_sem=r3.at[at],
            device_id=peer,
            device_id_type=MESH,
        )

    def got(at):
        other = pl.ds(pl.multiple_of((1 - core) * deep, 128), deep)
        ref = [there(y, 1 - x), there(1 - y, x), there(1 - y, 1 - x), f_ref.at[:, :, other]][at]
        pltpu.make_async_copy(ref, ref, r3.at[at]).wait()

    hop(0).start()
    kept = pltpu.make_async_copy(held, there(y, x), loc.at[2])
    kept.start()

    def columns(pair):
        return pl.ds(pl.multiple_of(pair * half, 128), half)

    def project(pair):
        token = jnp.concatenate([o_ref[2 * pair], o_ref[2 * pair + 1]], axis=0)
        for kind in range(3):
            value = dot(w_ref[kind], token, ((1,), (1,))) + b_ref[kind]
            proj[kind, :, :, columns(pair)] = value.astype(proj.dtype).reshape(heads, HEAD_DIM, half)

    def ship(index, pair, shift):
        other = lax.rem(ctx + shift, nc)
        return other, pltpu.make_async_remote_copy(
            src_ref=proj.at[:, jnp.minimum(other, heads - 1), :, columns(pair)],
            dst_ref=q_ref.at[ctx, :, :, columns(pair)],
            send_sem=s4.at[index, shift],
            recv_sem=r4.at[index, shift],
            device_id={"context": other},
            device_id_type=MESH,
        )

    def ship_all(index, pair):
        for shift in range(1, nc):
            other, item = ship(index, pair, shift)

            @pl.when(other < heads)
            def _():
                item.start()

    near = lax.div(me, 2)
    move(1)
    weight_in.wait()
    project(near)
    ship_all(0, near)
    hop(1).start()
    for s in range(2, n - 1):
        move(s)
    got(0)
    hop(2).start()
    large.last()
    project(1 - near)
    ship_all(1, 1 - near)
    result = pltpu.make_async_copy(o_ref, o_hbm, loc.at[5])
    result.start()
    stay = pltpu.make_async_copy(proj.at[:, jnp.minimum(ctx, heads - 1)], q_ref.at[ctx], loc.at[3])
    stay.start()
    kept.wait()
    got(1)
    got(2)
    hop(3).start()
    stay.wait()

    @pl.when(ctx < heads)
    def _():
        for index in range(2):
            for shift in range(1, nc):
                source = lax.rem(ctx + nc - shift, nc)
                pair = near if index == 0 else 1 - near
                ref = q_ref.at[source, :, :, columns(pair)]
                pltpu.make_async_copy(ref, ref, r4.at[index, shift]).wait()

    got(3)
    for d in range(2):
        grads.wait(d, 0)
    result.wait()
    small.finish()
    large.finish()
    grads.finish(1)
    for at in range(4):
        hop(at).wait_send()
    for index in range(2):
        for shift in range(1, nc):
            other, item = ship(index, near if index == 0 else 1 - near, shift)

            @pl.when(other < heads)
            def _():
                item.wait_send()


def start_part(tokens, gain, shift, w, project_weight, bias, cotangent, n, nc, heads, collective_id):
    rows, cols = tokens.shape
    wide, deep = w.shape
    low = jnp.bfloat16
    full, weight, qkv, grads = pl.pallas_call(
        functools.partial(start_kernel, n, nc, heads),
        out_shape=(
            jax.ShapeDtypeStruct((n, rows, cols), low),
            jax.ShapeDtypeStruct((n, wide, deep), w.dtype),
            jax.ShapeDtypeStruct((nc, 3, HEAD_DIM, n * rows), low),
            jax.ShapeDtypeStruct((n, rows, cols), low),
        ),
        in_specs=[HB] * 7,
        out_specs=(HB, VM, VM, VM),
        scratch_shapes=[
            pltpu.VMEM((rows, cols), low),
            pltpu.VMEM((n, wide // 4, deep // 2), w.dtype),
            pltpu.VMEM((3, heads, HEAD_DIM, n * rows), low),
            pltpu.VMEM(project_weight.shape, low),
            pltpu.VMEM((n, rows, cols), low),
            pltpu.VMEM((rows, cols), tokens.dtype),
            pltpu.VMEM(gain.shape, jnp.float32),
            pltpu.VMEM(shift.shape, jnp.float32),
            pltpu.VMEM(bias.shape, jnp.float32),
            DMA((4,)),
        ]
        + [DMA((2, n - 1)) for _ in range(6)]
        + [DMA((4,)), DMA((4,)), DMA((2, nc)), DMA((2, nc)), DMA((6,))],
        compiler_params=remote_params(collective_id, 56),
    )(tokens, gain, shift, w, project_weight, bias, cotangent)
    return full.reshape(n * rows, cols), weight.reshape(n * wide, deep), qkv, grads


def dot(left, right, dims):
    return lax.dot_general(left, right, ((dims[0], dims[1]), ((), ())), preferred_element_type=jnp.float32)


def key_positions(first, keys, queries):
    return first + lax.broadcasted_iota(jnp.int32, (keys, queries), 0)


def load_rows(qkv_ref, nb, half, qs, kt, ks, vs):
    for block in range(nb):
        part = slice(block % 2 * half, block % 2 * half + half)
        at = block // 2
        qs[block] = qkv_ref[at, 0, :, part] * jnp.asarray(HEAD_DIM**-0.5, qs.dtype)
        item = qkv_ref[at, 1, :, part]
        if kt is not None:
            kt[block] = item
        ks[block] = item.T
        if vs is not None:
            vs[block] = qkv_ref[at, 2, :, part].T


def fill_tables(nb, half, seg_ref, order_ref, slot_ref, low_ref, high_ref):
    for block in range(nb):
        slot_ref[order_ref[block]] = jnp.int32(block)
    first = [seg_ref[0, block * half] for block in range(nb)]
    last = [seg_ref[0, block * half + half - 1] for block in range(nb)]
    for block in range(nb):
        if low_ref is not None:
            low_ref[block] = sum(jnp.where(item < first[block], 1, 0) for item in last)
        if high_ref is not None:
            high_ref[block] = sum(jnp.where(item <= last[block], 1, 0) for item in first)


def forward_kernel(half, heads, seg_s, order_ref, seg_ref, qkv_ref, o_ref, full_ref, lse_ref, start_ref, qs, ks, slot_ref, low_ref):
    nb = full_ref.shape[0]

    @pl.when(lax.axis_index("context") < heads)
    def _():
        load_rows(qkv_ref, nb, half, qs, None, ks, None)
        fill_tables(nb, half, seg_s, order_ref, slot_ref, low_ref, None)
        seg = seg_ref[...]
        start = jnp.zeros(seg.shape, jnp.float32)
        for doc in range(1, DOC_LIMIT):
            before = jnp.sum(jnp.where(seg < doc, 1.0, 0.0), axis=1, keepdims=True)
            start = jnp.where(seg == doc, before, start)
        start_ref[...] = start.astype(jnp.int32)

        @pl.loop(0, nb)
        def _(nq):
            slot = slot_ref[nq]
            query = qs[slot]
            begin = start_ref[:, pl.ds(pl.multiple_of(nq * half, 128), half)]
            here = nq * half + lax.broadcasted_iota(jnp.int32, (1, half), 1)

            def step(nk, state):
                top, total, acc = state
                at = slot_ref[nk]
                score = dot(ks[at], query, ((1,), (0,)))
                place = key_positions(nk * half, half, half)
                score = jnp.where((place >= begin) & (place <= here), score, NEG_FILL)
                new_top = jnp.maximum(top, jnp.max(score, axis=0, keepdims=True))
                factor = jnp.exp(top - new_top)
                weight = jnp.exp(score - new_top)
                total = total * factor + jnp.sum(weight, axis=0, keepdims=True)
                value = qkv_ref[at // 2, 2, :, pl.ds(pl.multiple_of(at % 2 * half, 128), half)]
                acc = acc * factor + dot(value, weight.astype(jnp.bfloat16), ((1,), (0,)))
                return new_top, total, acc

            top, total, acc = lax.fori_loop(
                low_ref[nq],
                nq + 1,
                step,
                (
                    jnp.full((1, half), NEG_FILL, jnp.float32),
                    jnp.zeros((1, half), jnp.float32),
                    jnp.zeros((HEAD_DIM, half), jnp.float32),
                ),
            )
            result = acc / total
            full_ref[slot] = result
            lse_ref[slot] = top + jnp.log(total)
            low = result.astype(jnp.bfloat16)
            o_ref[2 * slot] = low[:, : half // 2]
            o_ref[2 * slot + 1] = low[:, half // 2 :]


def attend_forward(qkv, segments, order, half, heads):
    nc = qkv.shape[0]
    nb = 2 * nc
    return pl.pallas_call(
        functools.partial(forward_kernel, half, heads),
        out_shape=(
            jax.ShapeDtypeStruct((2 * nb, HEAD_DIM, half // 2), jnp.bfloat16),
            jax.ShapeDtypeStruct((nb, HEAD_DIM, half), jnp.float32),
            jax.ShapeDtypeStruct((nb, 1, half), jnp.float32),
            jax.ShapeDtypeStruct(segments.shape, jnp.int32),
        ),
        in_specs=[SM, SM, VM, VM],
        out_specs=(VM, VM, VM, VM),
        scratch_shapes=[
            pltpu.VMEM((nb, HEAD_DIM, half), jnp.bfloat16),
            pltpu.VMEM((nb, half, HEAD_DIM), jnp.bfloat16),
            pltpu.SMEM((nb,), jnp.int32),
            pltpu.SMEM((nb,), jnp.int32),
        ],
        compiler_params=pltpu.CompilerParams(vmem_limit_bytes=24 << 20),
    )(segments, order, segments, qkv)


def backward_kernel(
    half, heads, seg_s, order_ref, start_ref, qkv_ref, full_ref, lse_ref, grad_ref, o_ref,
    qs, kt, ks, vs, gs, ds, dq, slot_ref, high_ref,
):
    nb = full_ref.shape[0]

    @pl.when(lax.axis_index("context") < heads)
    def _():
        load_rows(qkv_ref, nb, half, qs, kt, ks, vs)
        fill_tables(nb, half, seg_s, order_ref, slot_ref, None, high_ref)
        for block in range(nb):
            both = jnp.concatenate([grad_ref[2 * block], grad_ref[2 * block + 1]], axis=1)
            gs[block] = both
            ds[block] = jnp.sum(both.astype(jnp.float32) * full_ref[block], axis=0, keepdims=True)
            dq[block] = jnp.zeros((HEAD_DIM, half), jnp.float32)

        @pl.loop(0, nb)
        def _(nk):
            at = slot_ref[nk]
            place = key_positions(nk * half, half, half)

            def step(nq, state):
                grad_key, grad_value = state
                slot = slot_ref[nq]
                query, grad = qs[slot], gs[slot]
                begin = start_ref[:, pl.ds(pl.multiple_of(nq * half, 128), half)]
                here = nq * half + lax.broadcasted_iota(jnp.int32, (1, half), 1)
                score = dot(ks[at], query, ((1,), (0,)))
                score = jnp.where((place >= begin) & (place <= here), score, NEG_FILL)
                weight = jnp.exp(score - lse_ref[slot])
                grad_weight = dot(vs[at], grad, ((1,), (0,)))
                grad_score = (weight * (grad_weight - ds[slot])).astype(jnp.bfloat16)
                grad_value = grad_value + dot(grad, weight.astype(jnp.bfloat16), ((1,), (1,)))
                grad_key = grad_key + dot(query, grad_score, ((1,), (1,)))
                dq[slot] += dot(kt[at], grad_score, ((1,), (0,)))
                return grad_key, grad_value

            zero = jnp.zeros((HEAD_DIM, half), jnp.float32)
            grad_key, grad_value = lax.fori_loop(nk, high_ref[nk], step, (zero, zero))
            columns = pl.ds(pl.multiple_of(at % 2 * half, 128), half)
            o_ref[at // 2, 1, :, columns] = grad_key.astype(jnp.bfloat16)
            o_ref[at // 2, 2, :, columns] = grad_value.astype(jnp.bfloat16)

        for block in range(nb):
            part = slice(block % 2 * half, block % 2 * half + half)
            o_ref[block // 2, 0, :, part] = (dq[block] * HEAD_DIM**-0.5).astype(jnp.bfloat16)


def attend_backward(qkv, segments, order, start, full, lse, grad, half, heads):
    nc = qkv.shape[0]
    nb = 2 * nc
    low = jnp.bfloat16
    return pl.pallas_call(
        functools.partial(backward_kernel, half, heads),
        out_shape=jax.ShapeDtypeStruct(qkv.shape, low),
        in_specs=[SM, SM, VM, VM, VM, VM, VM],
        out_specs=VM,
        scratch_shapes=[
            pltpu.VMEM((nb, HEAD_DIM, half), low),
            pltpu.VMEM((nb, HEAD_DIM, half), low),
            pltpu.VMEM((nb, half, HEAD_DIM), low),
            pltpu.VMEM((nb, half, HEAD_DIM), low),
            pltpu.VMEM((nb, HEAD_DIM, half), low),
            pltpu.VMEM((nb, 1, half), jnp.float32),
            pltpu.VMEM((nb, HEAD_DIM, half), jnp.float32),
            pltpu.SMEM((nb,), jnp.int32),
            pltpu.SMEM((nb,), jnp.int32),
        ],
        compiler_params=pltpu.CompilerParams(vmem_limit_bytes=24 << 20),
    )(segments, order, start, qkv, full, lse, grad)


def norm_parts(values):
    centre = jnp.mean(values, axis=-1, keepdims=True)
    shifted = values - centre
    spread_ = jnp.mean(shifted * shifted, axis=-1, keepdims=True)
    scale = lax.rsqrt(spread_ + NORM_EPS)
    return shifted * scale, scale


def norm_backward(grad, normed, scale, gain):
    e = grad * gain
    mean_e = jnp.mean(e, axis=-1, keepdims=True)
    mean_en = jnp.mean(e * normed, axis=-1, keepdims=True)
    return (e - mean_e - normed * mean_en) * scale


def gelu_tanh(values):
    return jax.nn.gelu(values, approximate=True)


def cross_rows(left, right):
    return lax.dot_general(
        left, right, (((0,), (0,)), ((), ())), preferred_element_type=jnp.float32
    )


def after(value, done):
    return lax.optimization_barrier((value, done))[0]


def per_device(
    mesh_sizes,
    inputs,
    first_gain,
    first_shift,
    project_weight,
    project_bias,
    attend_weight,
    attend_bias,
    second_gain,
    second_shift,
    expand_weight,
    expand_bias,
    shrink_weight,
    shrink_bias,
    segments,
    block_order,
    cotangent,
):
    nt, nc = mesh_sizes["tensor"], mesh_sizes["context"]
    own_rows, width = inputs.shape[1], inputs.shape[2]
    local_width = project_weight.shape[2]
    heads = local_width // HEAD_DIM
    block_rows = own_rows * nt
    half = block_rows // 2
    low = jnp.bfloat16
    f32 = lambda value: value.astype(jnp.float32)
    square = nt == 4 and nc == 4 and mesh_sizes["dp"] == 2
    plane = ("context", "dp")

    tokens_own = f32(inputs[0])
    grad_out = cotangent[0]
    bias = jnp.stack([project_bias[0], jnp.zeros_like(project_bias[0]), project_bias[1]])[:, :, None]
    weight_rows = project_weight.transpose(0, 2, 1)
    if square:
        hidden1_full, attend_full, qkv, grads_near = start_part(
            inputs[0], first_gain, first_shift, attend_weight, weight_rows, bias, grad_out, nt, nc, heads, 0
        )
        pieces, attended_full, lse, start = attend_forward(qkv, segments, block_order, half, heads)
        feed, *feed_pieces, middle, grad_middle, vectors, attend_pieces, grad_heads = feed_part(
            pieces,
            inputs[0],
            attend_full,
            (attend_bias, second_gain, second_shift),
            expand_weight,
            shrink_weight,
            expand_bias,
            grads_near,
            grad_out,
            nt,
            nc,
            heads,
            3,
        )
        grad_qkv = attend_backward(
            qkv, segments, block_order, start, attended_full, lse, grad_heads, half, heads
        )
        outputs, grad_inputs, summed, grad_project, grad_attend, feeds = last_part(
            grad_qkv,
            weight_rows,
            hidden1_full,
            attend_pieces,
            feed,
            middle,
            shrink_bias,
            feed_pieces,
            inputs[0],
            first_gain,
            grad_middle,
            vectors,
            6,
            nt,
            heads,
            7,
        )
        grad_project = grad_project.transpose(0, 2, 1)
        grad_shrink, grad_expand = feeds[0].reshape(-1, width), feeds[1].reshape(width, -1)
        wide = expand_bias.shape[0]
    else:
        hidden1 = norm_parts(tokens_own)[0] * first_gain + first_shift
        hidden1_full = gather_rows(hidden1.astype(low), nt, 0)
        attend_full = lax.all_gather(attend_weight, "tensor", axis=0, tiled=True)
        projected = jnp.einsum(
            "ked,rd->ker", weight_rows, hidden1_full, preferred_element_type=jnp.float32
        )
        projected = (projected + bias).astype(low).reshape(3, heads, HEAD_DIM, block_rows)
        qkv = to_heads(projected, nc, 1)
        pieces, attended_full, lse, start = attend_forward(qkv, segments, block_order, half, heads)
        grad_full = lax.all_gather(grad_out, "tensor", axis=0, tiled=True)
        attended = to_rows(pieces, nc, nt, heads, 2).reshape(width, own_rows)
        middle = tokens_own + cross_rows(attended, attend_full) + attend_bias
        normed2, scale2 = norm_parts(middle)
        hidden2 = (normed2 * second_gain + second_shift).astype(low)
        hidden2_full = gather_rows(hidden2, nt, 3)
        pre_act = jnp.dot(hidden2_full, expand_weight, preferred_element_type=jnp.float32) + expand_bias
        activ = gelu_tanh(pre_act).astype(low)
        grad_act = dot(grad_full, shrink_weight, ((1,), (1,)))
        grad_pre = jax.vjp(gelu_tanh, pre_act)[1](grad_act)[0].astype(low)
        grad_shrink = cross_rows(activ, grad_full).astype(low)
        grad_expand = cross_rows(hidden2_full, grad_pre).astype(low)
        grad_hidden2 = scatter_rows(dot(grad_pre, expand_weight, ((1,), (1,))).astype(low), nt, 4)
        grad_expand_bias = jnp.sum(f32(grad_pre), axis=0)
        feed = jnp.dot(activ, shrink_weight, preferred_element_type=jnp.float32).astype(low)

        grad_shrink_bias = jnp.sum(f32(grad_out), axis=0)
        grad_second_gain = jnp.sum(grad_hidden2 * normed2, axis=0)
        grad_second_shift = jnp.sum(grad_hidden2, axis=0)
        grad_middle = f32(grad_out) + norm_backward(grad_hidden2, normed2, scale2, second_gain)
        grad_middle_low = grad_middle.astype(low)
        grad_attend_bias = jnp.sum(f32(grad_middle_low), axis=0)
        grad_attended = dot(attend_full, grad_middle_low, ((1,), (1,))).astype(low)
        grad_attended = grad_attended.reshape(nt * heads, HEAD_DIM, own_rows)
        grad_attend = jnp.dot(attended, grad_middle_low, preferred_element_type=jnp.float32).astype(low)
        grad_heads = rows_back(grad_attended, nc, nt, heads, 5)
        feed_sum = lax.psum_scatter(after(feed, grad_heads), "tensor", scatter_dimension=0, tiled=True)

        grad_qkv = attend_backward(
            qkv, segments, block_order, start, attended_full, lse, grad_heads, half, heads
        )
        grad_rows = from_heads(grad_qkv, nc, heads, 6).reshape(3 * local_width, block_rows)
        grad_project = dot(hidden1_full, grad_rows, ((0,), (1,))).astype(low)
        grad_hidden1 = cross_rows(grad_rows, weight_rows.reshape(3 * local_width, width)).astype(low)
        row_sums = jnp.sum(f32(grad_rows), axis=1)
        grad_project_bias = jnp.concatenate([row_sums[:local_width], row_sums[2 * local_width :]])
        grad_hidden1 = scatter_rows(grad_hidden1, nt, 7)
        normed1, scale1 = norm_parts(tokens_own)
        back = norm_backward(grad_hidden1, normed1, scale1, first_gain)
        grad_inputs = (grad_middle + back).astype(low)
        wide = grad_expand_bias.shape[0]
        vectors = jnp.concatenate(
            [
                jnp.sum(grad_hidden1 * normed1, axis=0),
                jnp.sum(grad_hidden1, axis=0),
                grad_attend_bias,
                grad_second_gain,
                grad_second_shift,
                grad_shrink_bias,
                grad_expand_bias,
                jnp.pad(grad_project_bias, (0, -(wide + 2 * local_width) % width)),
            ]
        ).reshape(-1, width)
        summed = sum_vectors(vectors, 6, mesh_sizes, 8)
        grad_attend = lax.psum_scatter(grad_attend, "tensor", scatter_dimension=0, tiled=True)
        grad_project, grad_attend, grad_shrink, grad_expand = lax.psum(
            (grad_project, grad_attend, grad_shrink, grad_expand), plane
        )
        grad_project = jnp.stack(
            [grad_project[:, at * local_width : (at + 1) * local_width] for at in range(3)]
        )
        outputs = (middle + f32(feed_sum) + shrink_bias).astype(low)
    tail = summed[6:].reshape(-1)
    return (
        outputs[None],
        grad_inputs[None],
        summed[0],
        summed[1],
        f32(grad_project),
        tail[wide : wide + 2 * local_width].reshape(2, local_width),
        f32(grad_attend),
        summed[2],
        summed[3],
        summed[4],
        f32(grad_expand),
        tail[:wide],
        f32(grad_shrink),
        summed[5],
    )


def solution(mesh):
    rows = P("dp", ("context", "tensor"), None)
    in_specs = (
        rows,
        P(),
        P(),
        P(None, None, "tensor"),
        P(None, "tensor"),
        P("tensor", None),
        P(),
        P(),
        P(),
        P(None, "tensor"),
        P("tensor"),
        P("tensor", None),
        P(),
        P("dp", None),
        P(),
        rows,
    )
    out_specs = (
        rows,
        rows,
        P(),
        P(),
        P(None, None, "tensor"),
        P(None, "tensor"),
        P("tensor", None),
        P(),
        P(),
        P(),
        P(None, "tensor"),
        P("tensor"),
        P("tensor", None),
        P(),
    )
    return jax.shard_map(
        functools.partial(per_device, dict(mesh.shape)),
        mesh=mesh,
        in_specs=in_specs,
        out_specs=out_specs,
        check_vma=False,
    )
```

```python
import functools

import jax
import jax.numpy as jnp
from jax import lax
from jax.experimental import pallas as pl
from jax.experimental.pallas import tpu as pltpu
from jax.sharding import PartitionSpec as P

HEAD_DIM = 64
NEG_FILL = -1e30
NORM_EPS = 1e-05
DOC_LIMIT = 16
MESH = pl.DeviceIdType.MESH
VM = pl.BlockSpec(memory_space=pltpu.VMEM)
SM = pl.BlockSpec(memory_space=pltpu.SMEM)
DMA = pltpu.SemaphoreType.DMA


def remote_params(collective_id, mib=16):
    return pltpu.CompilerParams(
        collective_id=collective_id, has_side_effects=True, vmem_limit_bytes=mib << 20
    )


HB = pl.BlockSpec(memory_space=pltpu.HBM)


def copies(pairs, sems):
    return [pltpu.make_async_copy(src, dst, sems.at[at]) for at, (src, dst) in enumerate(pairs)]


def row(ref):
    return ref[...].reshape(1, -1)


def line_barrier(me, n):
    bar = pltpu.get_barrier_semaphore()

    @pl.when(me > 0)
    def _():
        pl.semaphore_signal(bar, inc=1, device_id={"tensor": me - 1}, device_id_type=MESH)

    @pl.when(me < n - 1)
    def _():
        pl.semaphore_signal(bar, inc=1, device_id={"tensor": me + 1}, device_id_type=MESH)

    pl.semaphore_wait(bar, jnp.where(me > 0, 1, 0) + jnp.where(me < n - 1, 1, 0))


def gather_kernel(n, x_ref, o_ref, send, recv, loc):
    me = lax.axis_index("tensor")
    line_barrier(me, n)
    own = pltpu.make_async_copy(x_ref, o_ref.at[me], loc)
    own.start()

    def copy(d, s):
        shard = jnp.clip(me - s if d == 0 else me + s, 0, n - 1)
        return pltpu.make_async_remote_copy(
            src_ref=x_ref if s == 0 else o_ref.at[shard],
            dst_ref=o_ref.at[shard],
            send_sem=send.at[d, s],
            recv_sem=recv.at[d, s],
            device_id={"tensor": jnp.clip(me + 1 if d == 0 else me - 1, 0, n - 1)},
            device_id_type=MESH,
        )

    def sends(d, s):
        return (me - s >= 0) & (me < n - 1) if d == 0 else (me + s < n) & (me > 0)

    def gets(d, s):
        return me - 1 - s >= 0 if d == 0 else me + 1 + s < n

    def landed(d, s):
        shard = jnp.clip(me - 1 - s if d == 0 else me + 1 + s, 0, n - 1)
        return pltpu.make_async_copy(o_ref.at[shard], o_ref.at[shard], recv.at[d, s])

    for s in range(n - 1):
        for d in range(2):
            if s > 0:

                @pl.when(gets(d, s - 1))
                def _():
                    landed(d, s - 1).wait()

            @pl.when(sends(d, s))
            def _():
                copy(d, s).start()

    for d in range(2):

        @pl.when(gets(d, n - 2))
        def _():
            landed(d, n - 2).wait()

        for s in range(n - 1):

            @pl.when(sends(d, s))
            def _():
                copy(d, s).wait_send()

    own.wait()


def gather_rows(x, n, collective_id):
    rows, cols = x.shape
    return pl.pallas_call(
        functools.partial(gather_kernel, n),
        out_shape=jax.ShapeDtypeStruct((n, rows, cols), x.dtype),
        in_specs=[VM],
        out_specs=VM,
        scratch_shapes=[DMA((2, n - 1)), DMA((2, n - 1)), DMA],
        compiler_params=remote_params(collective_id),
    )(x).reshape(n * rows, cols)


def scatter_kernel(n, x_ref, o_ref, buf, tmp, send, recv):
    me = lax.axis_index("tensor")
    line_barrier(me, n)

    def term(d, k):
        return n - 1 - k if d == 0 else k

    def sends(d, k):
        return me < n - 1 - k if d == 0 else me > k

    def behind(d):
        return me > 0 if d == 0 else me < n - 1

    def copy(d, k, first):
        return pltpu.make_async_remote_copy(
            src_ref=x_ref.at[term(d, k)] if first else tmp.at[d, k],
            dst_ref=buf.at[d, k],
            send_sem=send.at[d, k],
            recv_sem=recv.at[d, k],
            device_id={"tensor": jnp.clip(me + 1 if d == 0 else me - 1, 0, n - 1)},
            device_id_type=MESH,
        )

    def landed(d, k):
        return pltpu.make_async_copy(buf.at[d, k], buf.at[d, k], recv.at[d, k])

    for d in range(2):

        @pl.when(jnp.logical_not(behind(d)))
        def _():
            for k in range(n - 1):
                copy(d, k, True).start()

    for k in range(n - 1):
        for d in range(2):

            @pl.when(behind(d) & sends(d, k))
            def _():
                landed(d, k).wait()
                both = buf[d, k].astype(jnp.float32) + x_ref[term(d, k)].astype(jnp.float32)
                tmp[d, k] = both.astype(tmp.dtype)
                copy(d, k, False).start()

    o_ref[...] = x_ref[me].astype(jnp.float32)
    for d in range(2):
        for k in range(n - 1):

            @pl.when(behind(d) & (me == term(d, k)))
            def _():
                landed(d, k).wait()
                o_ref[...] += buf[d, k].astype(jnp.float32)

    for d in range(2):
        for k in range(n - 1):

            @pl.when(sends(d, k))
            def _():
                copy(d, k, False).wait_send()


def scatter_rows(x, n, collective_id):
    rows, cols = x.shape
    own = rows // n
    return pl.pallas_call(
        functools.partial(scatter_kernel, n),
        out_shape=jax.ShapeDtypeStruct((own, cols), jnp.float32),
        in_specs=[VM],
        out_specs=VM,
        scratch_shapes=[
            pltpu.VMEM((2, n - 1, own, cols), x.dtype),
            pltpu.VMEM((2, n - 1, own, cols), x.dtype),
            DMA((2, n - 1)),
            DMA((2, n - 1)),
        ],
        compiler_params=remote_params(collective_id),
    )(x.reshape(n, own, cols))


def group_barrier(axes, sizes):
    mine = [lax.axis_index(name) for name in axes]
    place = sum_index(mine, sizes)
    total = 1
    for size in sizes:
        total *= size
    bar = pltpu.get_barrier_semaphore()
    for shift in range(1, total):
        other = lax.rem(place + shift, total)
        pl.semaphore_signal(bar, inc=1, device_id=spread(other, axes, sizes), device_id_type=MESH)
    pl.semaphore_wait(bar, total - 1)
    return place, total


def sum_index(mine, sizes):
    place = 0
    for at, size in zip(mine, sizes):
        place = place * size + at
    return place


def spread(place, axes, sizes):
    found = {}
    for name, size in reversed(tuple(zip(axes, sizes))):
        found[name] = lax.rem(place, size)
        place = lax.div(place, size)
    return found


def to_heads_kernel(nc, heads, x_ref, o_ref, send, recv, loc):
    me, _ = group_barrier(("context",), (nc,))

    def copy(shift):
        other = lax.rem(me + shift, nc)
        return other, pltpu.make_async_remote_copy(
            src_ref=x_ref.at[:, jnp.minimum(other, heads - 1)],
            dst_ref=o_ref.at[me],
            send_sem=send.at[shift],
            recv_sem=recv.at[shift],
            device_id={"context": other},
            device_id_type=MESH,
        )

    for shift in range(1, nc):
        other, item = copy(shift)

        @pl.when(other < heads)
        def _():
            item.start()

    own = pltpu.make_async_copy(x_ref.at[:, jnp.minimum(me, heads - 1)], o_ref.at[me], loc)
    own.start()
    own.wait()

    @pl.when(me < heads)
    def _():
        for shift in range(1, nc):
            source = lax.rem(me + nc - shift, nc)
            pltpu.make_async_copy(o_ref.at[source], o_ref.at[source], recv.at[shift]).wait()

    for shift in range(1, nc):
        other, item = copy(shift)

        @pl.when(other < heads)
        def _():
            item.wait_send()


def to_heads(x, nc, collective_id):
    heads = x.shape[1]
    return pl.pallas_call(
        functools.partial(to_heads_kernel, nc, heads),
        out_shape=jax.ShapeDtypeStruct((nc, x.shape[0]) + x.shape[2:], x.dtype),
        in_specs=[VM],
        out_specs=VM,
        scratch_shapes=[DMA((nc,)), DMA((nc,)), DMA],
        compiler_params=remote_params(collective_id),
    )(x)


def from_heads_kernel(nc, heads, x_ref, o_ref, send, recv, loc):
    me, _ = group_barrier(("context",), (nc,))

    def copy(shift):
        other = lax.rem(me + shift, nc)
        return pltpu.make_async_remote_copy(
            src_ref=x_ref.at[other],
            dst_ref=o_ref.at[:, jnp.minimum(me, heads - 1)],
            send_sem=send.at[shift],
            recv_sem=recv.at[shift],
            device_id={"context": other},
            device_id_type=MESH,
        )

    @pl.when(me < heads)
    def _():
        for shift in range(1, nc):
            copy(shift).start()
        own = pltpu.make_async_copy(x_ref.at[me], o_ref.at[:, me], loc)
        own.start()
        own.wait()

    for shift in range(1, nc):
        source = lax.rem(me + nc - shift, nc)

        @pl.when(source < heads)
        def _():
            at = jnp.minimum(source, heads - 1)
            pltpu.make_async_copy(o_ref.at[:, at], o_ref.at[:, at], recv.at[shift]).wait()

    @pl.when(me < heads)
    def _():
        for shift in range(1, nc):
            copy(shift).wait_send()


def from_heads(x, nc, heads, collective_id):
    return pl.pallas_call(
        functools.partial(from_heads_kernel, nc, heads),
        out_shape=jax.ShapeDtypeStruct((x.shape[1], heads) + x.shape[2:], x.dtype),
        in_specs=[VM],
        out_specs=VM,
        scratch_shapes=[DMA((nc,)), DMA((nc,)), DMA],
        compiler_params=remote_params(collective_id),
    )(x)


AXES = ("context", "tensor")


def rows_kernel(nc, nt, heads, x_ref, o_ref, send, recv, loc):
    me, total = group_barrier(AXES, (nc, nt))
    my_ctx, my_ten = lax.axis_index("context"), lax.axis_index("tensor")
    my_head = my_ten * heads + jnp.minimum(my_ctx, heads - 1)

    def copy(shift):
        other = lax.rem(me + shift, total)
        return pltpu.make_async_remote_copy(
            src_ref=x_ref.at[other],
            dst_ref=o_ref.at[my_head],
            send_sem=send.at[shift],
            recv_sem=recv.at[shift],
            device_id=spread(other, AXES, (nc, nt)),
            device_id_type=MESH,
        )

    @pl.when(my_ctx < heads)
    def _():
        for shift in range(1, total):
            copy(shift).start()
        own = pltpu.make_async_copy(x_ref.at[me], o_ref.at[my_head], loc)
        own.start()
        own.wait()

    for shift in range(1, total):
        source = lax.rem(me + total - shift, total)
        ctx, ten = lax.div(source, nt), lax.rem(source, nt)

        @pl.when(ctx < heads)
        def _():
            at = ten * heads + jnp.minimum(ctx, heads - 1)
            pltpu.make_async_copy(o_ref.at[at], o_ref.at[at], recv.at[shift]).wait()

    @pl.when(my_ctx < heads)
    def _():
        for shift in range(1, total):
            copy(shift).wait_send()


def to_rows(x, nc, nt, heads, collective_id):
    total = nc * nt
    return pl.pallas_call(
        functools.partial(rows_kernel, nc, nt, heads),
        out_shape=jax.ShapeDtypeStruct((nt * heads,) + x.shape[1:], x.dtype),
        in_specs=[VM],
        out_specs=VM,
        scratch_shapes=[DMA((total,)), DMA((total,)), DMA],
        compiler_params=remote_params(collective_id),
    )(x)


def rows_back_kernel(nc, nt, heads, x_ref, o_ref, send, recv, loc):
    me, total = group_barrier(AXES, (nc, nt))
    my_ctx, my_ten = lax.axis_index("context"), lax.axis_index("tensor")

    def copy(shift):
        other = lax.rem(me + shift, total)
        ctx, ten = lax.div(other, nt), lax.rem(other, nt)
        return ctx < heads, pltpu.make_async_remote_copy(
            src_ref=x_ref.at[ten * heads + jnp.minimum(ctx, heads - 1)],
            dst_ref=o_ref.at[me],
            send_sem=send.at[shift],
            recv_sem=recv.at[shift],
            device_id={"context": ctx, "tensor": ten},
            device_id_type=MESH,
        )

    for shift in range(1, total):
        goes, item = copy(shift)

        @pl.when(goes)
        def _():
            item.start()

    own = pltpu.make_async_copy(
        x_ref.at[my_ten * heads + jnp.minimum(my_ctx, heads - 1)], o_ref.at[me], loc
    )
    own.start()
    own.wait()

    @pl.when(my_ctx < heads)
    def _():
        for shift in range(1, total):
            source = lax.rem(me + total - shift, total)
            pltpu.make_async_copy(o_ref.at[source], o_ref.at[source], recv.at[shift]).wait()

    for shift in range(1, total):
        goes, item = copy(shift)

        @pl.when(goes)
        def _():
            item.wait_send()


def rows_back(x, nc, nt, heads, collective_id):
    total = nc * nt
    return pl.pallas_call(
        functools.partial(rows_back_kernel, nc, nt, heads),
        out_shape=jax.ShapeDtypeStruct((total,) + x.shape[1:], x.dtype),
        in_specs=[VM],
        out_specs=VM,
        scratch_shapes=[DMA((total,)), DMA((total,)), DMA],
        compiler_params=remote_params(collective_id),
    )(x)


def vectors_kernel(names, sizes, shared, x_ref, o_ref, now, *rest):
    bufs, sems = rest[: len(names)], rest[len(names) :]
    bar = pltpu.get_barrier_semaphore()
    for name, size in zip(names, sizes):
        me = lax.axis_index(name)
        for shift in range(1, size):
            pl.semaphore_signal(
                bar, inc=1, device_id={name: lax.rem(me + shift, size)}, device_id_type=MESH
            )
    pl.semaphore_wait(bar, sum(sizes) - len(sizes))
    for stage, (name, size) in enumerate(zip(names, sizes)):
        buf, send, recv = bufs[stage], sems[2 * stage], sems[2 * stage + 1]
        me = lax.axis_index(name)

        def copy(shift):
            return pltpu.make_async_remote_copy(
                src_ref=now.at[stage] if stage else x_ref.at[0],
                dst_ref=buf.at[me],
                send_sem=send.at[shift],
                recv_sem=recv.at[shift],
                device_id={name: lax.rem(me + shift, size)},
                device_id_type=MESH,
            )

        for shift in range(1, size):
            copy(shift).start()
        buf[me] = now[stage] if stage else x_ref[0]
        for shift in range(1, size):
            source = lax.rem(me + size - shift, size)
            pltpu.make_async_copy(buf.at[source], buf.at[source], recv.at[shift]).wait()
        total = buf[0]
        for at in range(1, size):
            total = total + buf[at]
        if stage == 0:
            row = lax.broadcasted_iota(jnp.int32, total.shape, 0)
            total = jnp.where(row < shared, total, x_ref[0])
        if stage + 1 < len(names):
            now[stage + 1] = total
        else:
            o_ref[...] = total
        for shift in range(1, size):
            copy(shift).wait_send()


def sum_vectors(rows, shared, mesh_sizes, collective_id):
    names = ("tensor", "context", "dp")
    sizes = tuple(mesh_sizes[name] for name in names)
    shape = rows.shape
    return pl.pallas_call(
        functools.partial(vectors_kernel, names, sizes, shared),
        out_shape=jax.ShapeDtypeStruct(shape, jnp.float32),
        in_specs=[VM],
        out_specs=VM,
        scratch_shapes=[pltpu.VMEM((len(names),) + shape, jnp.float32)]
        + [pltpu.VMEM((size,) + shape, jnp.float32) for size in sizes]
        + [DMA((size,)) for size in sizes for _ in range(2)],
        compiler_params=remote_params(collective_id),
    )(rows[None])


class PlaneSum:
    def __init__(self, u, p, o, bufs=None, spread=None):
        self.u, self.p, self.o = u, p, o
        if bufs is not None:
            self.rc, self.s1, self.ra, self.rb, self.sa, self.sb, self.ta, self.tb = bufs[:8]
            self.send1, self.recv1 = bufs[8:]
        if spread is not None:
            self.send2, self.recv2, self.loc = spread
        ctx, self.x = lax.axis_index("context"), lax.axis_index("dp")
        self.core, self.y = lax.rem(ctx, 2), lax.div(ctx, 2)
        self.chip_peer = {"context": ctx + 1 - 2 * self.core}
        self.y_peer = {"context": lax.rem(ctx + 2, 4)}
        self.x_peer = {"dp": 1 - self.x}

    @staticmethod
    def reduce_scratch(shape, dtype):
        tail = tuple(shape[1:])
        bufs = [pltpu.VMEM((count,) + tail, dtype) for count in (8, 8, 2, 2, 2, 2, 1, 1)]
        return bufs + [DMA((5,)), DMA((5,))]

    @staticmethod
    def spread_scratch():
        return [DMA((5,)), DMA((5,)), DMA((2,))]

    @staticmethod
    def greet(bar):
        ctx, x = lax.axis_index("context"), lax.axis_index("dp")
        for peer in (
            {"context": ctx + 1 - 2 * lax.rem(ctx, 2)},
            {"context": lax.rem(ctx + 2, 4)},
            {"dp": 1 - x},
        ):
            pl.semaphore_signal(bar, inc=1, device_id=peer, device_id_type=MESH)
        return 3

    def copy(self, at, src, dst, peer):
        send, recv = (self.send1, self.recv1) if at < 5 else (self.send2, self.recv2)
        return pltpu.make_async_remote_copy(
            src_ref=src,
            dst_ref=dst,
            send_sem=send.at[at % 5],
            recv_sem=recv.at[at % 5],
            device_id=peer,
            device_id_type=MESH,
        )

    def got(self, at, ref):
        recv = self.recv1 if at < 5 else self.recv2
        pltpu.make_async_copy(ref, ref, recv.at[at % 5]).wait()

    def add(self, out, left, right):
        f32 = jnp.float32
        out[...] = (left[...].astype(f32) + right[...].astype(f32)).astype(out.dtype)

    def mine(self, half):
        if half == 0:
            return pl.ds(self.core * 8 + 2 * self.x + self.y, 1)
        return pl.ds(self.core * 8 + 4 + 2 * self.y + self.x, 1)

    def hop(self, at):
        x, y, core = self.x, self.y, self.core
        o, p = self.o, self.p
        pair_a, pair_b = pl.ds(core * 8 + 2 * x, 2), pl.ds(core * 8 + 4 + 2 * y, 2)
        one = lambda at: pl.ds(at, 1)
        return [
            lambda: self.copy(0, self.by_core(1 - core), self.rc, self.chip_peer),
            lambda: self.copy(1, self.quarter(0, 1 - x), self.ra, self.x_peer),
            lambda: self.copy(2, self.quarter(1, 1 - y), self.rb, self.y_peer),
            lambda: self.copy(3, self.eighth(0, 1 - y), self.ta, self.y_peer),
            lambda: self.copy(4, self.eighth(1, 1 - x), self.tb, self.x_peer),
            lambda: self.copy(5, p.at[one(0)], o.at[self.mine(0)], self.y_peer),
            lambda: self.copy(6, p.at[one(1)], o.at[self.mine(1)], self.x_peer),
            lambda: self.copy(7, o.at[pair_a], o.at[pair_a], self.x_peer),
            lambda: self.copy(8, o.at[pair_b], o.at[pair_b], self.y_peer),
            lambda: self.copy(9, o.at[pl.ds(core * 8, 8)], o.at[pl.ds(core * 8, 8)], self.chip_peer),
        ][at]()

    def begin(self):
        self.hop(0).start()

    def by_core(self, core):
        return self.u.at[pl.ds(core * 8, 8)]

    def quarter(self, half, at):
        return self.s1.at[pl.ds(4 * half + 2 * at, 2)]

    def eighth(self, half, at):
        return (self.sa, self.sb)[half].at[pl.ds(at, 1)]

    def result(self, half):
        return self.p.at[pl.ds(half, 1)]

    def first(self):
        self.got(0, self.rc)
        self.add(self.s1, self.by_core(self.core), self.rc)
        self.hop(1).start()
        self.hop(2).start()

    def second(self):
        self.got(1, self.ra)
        self.add(self.sa, self.quarter(0, self.x), self.ra)
        self.hop(3).start()
        self.got(2, self.rb)
        self.add(self.sb, self.quarter(1, self.y), self.rb)
        self.hop(4).start()

    def third(self):
        self.got(3, self.ta)
        self.add(self.result(0), self.eighth(0, self.y), self.ta)
        self.got(4, self.tb)
        self.add(self.result(1), self.eighth(1, self.x), self.tb)

    def reduced(self):
        for at in range(5):
            self.hop(at).wait_send()

    def kept(self, half):
        return pltpu.make_async_copy(self.p.at[pl.ds(half, 1)], self.o.at[self.mine(half)], self.loc.at[half])

    def spread1(self):
        self.hop(5).start()
        self.hop(6).start()
        self.kept(0).start()
        self.kept(1).start()

    def spread2(self):
        x, y, core = self.x, self.y, self.core
        self.kept(0).wait()
        self.got(5, self.o.at[pl.ds(core * 8 + 2 * x + 1 - y, 1)])
        self.hop(7).start()
        self.kept(1).wait()
        self.got(6, self.o.at[pl.ds(core * 8 + 4 + 2 * y + 1 - x, 1)])
        self.hop(8).start()

    def spread3(self):
        x, y, core = self.x, self.y, self.core
        self.got(7, self.o.at[pl.ds(core * 8 + 2 - 2 * x, 2)])
        self.got(8, self.o.at[pl.ds(core * 8 + 6 - 2 * y, 2)])
        self.hop(9).start()

    def everywhere(self):
        self.got(9, self.o.at[pl.ds(8 - self.core * 8, 8)])
        for at in range(5, 10):
            self.hop(at).wait_send()


class StripSum(PlaneSum):
    @staticmethod
    def reduce_scratch(shape, dtype):
        lead, rows, cols = shape
        rest = lead - 2
        shapes = [(lead, rows)] * 2
        shapes += [(count, rows // 2) for count in (2, rest, 2, rest)] + [(count, rows // 4) for count in (2, rest)]
        return [pltpu.VMEM(item + (cols // 2,), dtype) for item in shapes] + [DMA((5,)), DMA((5,))]

    def lead(self, half):
        whole = (self.u if self.u is not None else self.o).shape[0]
        return pl.ds(0, 2) if half == 0 else pl.ds(2, whole - 2)

    def strip(self, core):
        size = (self.u if self.u is not None else self.o).shape[2] // 2
        return pl.ds(pl.multiple_of(core * size, 128), size)

    def rows(self, at, parts):
        size = (self.u if self.u is not None else self.o).shape[1] // parts
        return pl.ds(pl.multiple_of(at * size, 16), size)

    def by_core(self, core):
        return self.u.at[:, :, self.strip(core)]

    def quarter(self, half, at):
        return self.s1.at[self.lead(half), self.rows(at, 2)]

    def eighth(self, half, at):
        return (self.sa, self.sb)[half].at[:, self.rows(at, 4)]

    def result(self, half):
        return self.p.at[half, pl.ds(0, 2 if half == 0 else self.u.shape[0] - 2)]

    def hop(self, at):
        if at < 5:
            return super().hop(at)
        o, x, y = self.o, self.x, self.y
        mine = lambda half: o.at[
            self.lead(half), self.rows(2 * x + y if half == 0 else 2 * y + x, 4), self.strip(self.core)
        ]
        pair = lambda half: o.at[self.lead(half), self.rows(x if half == 0 else y, 2), self.strip(self.core)]
        both = o.at[:, :, self.strip(self.core)]
        return [
            lambda: self.copy(5, self.result(0), mine(0), self.y_peer),
            lambda: self.copy(6, self.result(1), mine(1), self.x_peer),
            lambda: self.copy(7, pair(0), pair(0), self.x_peer),
            lambda: self.copy(8, pair(1), pair(1), self.y_peer),
            lambda: self.copy(9, both, both, self.chip_peer),
        ][at - 5]()

    def kept(self, half):
        x, y = self.x, self.y
        mine = self.o.at[
            self.lead(half), self.rows(2 * x + y if half == 0 else 2 * y + x, 4), self.strip(self.core)
        ]
        return pltpu.make_async_copy(self.result(half), mine, self.loc.at[half])

    def spread2(self):
        x, y, mine = self.x, self.y, self.strip(self.core)
        self.kept(0).wait()
        self.got(5, self.o.at[self.lead(0), self.rows(2 * x + 1 - y, 4), mine])
        self.hop(7).start()
        self.kept(1).wait()
        self.got(6, self.o.at[self.lead(1), self.rows(2 * y + 1 - x, 4), mine])
        self.hop(8).start()

    def spread3(self):
        mine = self.strip(self.core)
        self.got(7, self.o.at[self.lead(0), self.rows(1 - self.x, 2), mine])
        self.got(8, self.o.at[self.lead(1), self.rows(1 - self.y, 2), mine])
        self.hop(9).start()

    def everywhere(self):
        self.got(9, self.o.at[:, :, self.strip(1 - self.core)])
        for at in range(5, 10):
            self.hop(at).wait_send()


def unit_pieces(unit):
    return jax.ShapeDtypeStruct((2,) + unit.shape[1:], unit.dtype)


def line_greet(bar, me, n):
    @pl.when(me > 0)
    def _():
        pl.semaphore_signal(bar, inc=1, device_id={"tensor": me - 1}, device_id_type=MESH)

    @pl.when(me < n - 1)
    def _():
        pl.semaphore_signal(bar, inc=1, device_id={"tensor": me + 1}, device_id_type=MESH)

    return jnp.where(me > 0, 1, 0) + jnp.where(me < n - 1, 1, 0)


class LineScatter:
    def __init__(self, n, x, o, buf, tmp, send, recv):
        self.n, self.x, self.o, self.buf, self.tmp, self.send, self.recv = n, x, o, buf, tmp, send, recv
        self.me = lax.axis_index("tensor")

    @staticmethod
    def scratch(n, own, cols, dtype):
        return [
            pltpu.VMEM((2, n - 1, own, cols), dtype),
            pltpu.VMEM((2, n - 1, own, cols), dtype),
            DMA((2, n - 1)),
            DMA((2, n - 1)),
        ]

    def term(self, d, k):
        return self.n - 1 - k if d == 0 else k

    def sends(self, d, k):
        return self.me < self.n - 1 - k if d == 0 else self.me > k

    def behind(self, d):
        return self.me > 0 if d == 0 else self.me < self.n - 1

    def copy(self, d, k, first):
        return pltpu.make_async_remote_copy(
            src_ref=self.x.at[self.term(d, k)] if first else self.tmp.at[d, k],
            dst_ref=self.buf.at[d, k],
            send_sem=self.send.at[d, k],
            recv_sem=self.recv.at[d, k],
            device_id={"tensor": jnp.clip(self.me + 1 if d == 0 else self.me - 1, 0, self.n - 1)},
            device_id_type=MESH,
        )

    def landed(self, d, k):
        return pltpu.make_async_copy(self.buf.at[d, k], self.buf.at[d, k], self.recv.at[d, k])

    def begin(self, ks):
        for d in range(2):

            @pl.when(jnp.logical_not(self.behind(d)))
            def _():
                for k in ks:
                    self.copy(d, k, True).start()

    def step(self, k, which=None):
        for d in range(2):
            now = self.behind(d) & self.sends(d, k)

            @pl.when(now if which is None else now & which(d))
            def _():
                self.landed(d, k).wait()
                at = self.term(d, k)
                both = self.buf[d, k].astype(jnp.float32) + self.x[at].astype(jnp.float32)
                self.tmp[d, k] = both.astype(self.tmp.dtype)
                self.copy(d, k, False).start()

    def end(self):
        self.o[...] = self.x[self.me].astype(jnp.float32)
        for d in range(2):
            for k in range(self.n - 1):

                @pl.when(self.behind(d) & (self.me == self.term(d, k)))
                def _():
                    self.landed(d, k).wait()
                    self.o[...] += self.buf[d, k].astype(jnp.float32)

        for d in range(2):
            for k in range(self.n - 1):

                @pl.when(self.sends(d, k))
                def _():
                    self.copy(d, k, False).wait_send()


GELU_SCALE = 0.7978845608028654
GELU_CUBE = 0.044715


def feed_kernel(n, nc, heads, chunks, piece_ref, *rest):
    (token_hbm, out_ref, abias_hbm, gain_hbm, shift_hbm, up_hbm, down_hbm, bias_hbm, near_ref, cot_ref), rest = rest[:10], rest[10:]
    outs, heads_ref, rest = rest[:7], rest[7], rest[8:]
    kept_refs, rest = rest[:7], rest[7:]
    feed_ref, p1_ref, p2_ref, middle_ref, gm_ref, vec_ref, p3_ref = kept_refs
    (token_ref, abias_ref, gain_ref, shift_ref, bias_ref, osem), rest = rest[:6], rest[6:]
    leave = copies(tuple(zip(kept_refs, outs)), osem)
    (o_ref, sum_ref, att_ref, gpiece, u3, bsend, brecv, bloc), rest = rest[:8], rest[8:]
    (x_ref, up_ref, down_ref, grad_ref, wsem, asend, arecv, aloc, csend, crecv, cloc), rest = rest[:11], rest[11:]
    (held, act, gp, part, acc, buf, tmp, u1, u2), rest = rest[:9], rest[9:]
    (gsend, grecv, loc, ssend, srecv), rest = rest[:5], rest[5:]
    plane = [PlaneSum(u1, p1_ref, None, rest[:10]), PlaneSum(u2, p2_ref, None, rest[10:20])]
    out_sum = StripSum(u3, p3_ref, None, rest[20:30])
    me = lax.axis_index("tensor")
    rows, width = token_ref.shape
    wide = up_ref.shape[1]
    few = rows // chunks
    f32, low = jnp.float32, jnp.bfloat16
    ctx, dp = lax.axis_index("context"), lax.axis_index("dp")
    place, total = ctx * n + me, nc * n
    my_head = me * heads + jnp.minimum(ctx, heads - 1)
    bar = pltpu.get_barrier_semaphore()
    for shift in range(1, total):
        other = lax.rem(place + shift, total)
        pl.semaphore_signal(bar, inc=1, device_id=spread(other, AXES, (nc, n)), device_id_type=MESH)
    pl.semaphore_signal(bar, inc=1, device_id={"dp": 1 - dp}, device_id_type=MESH)
    weights_in = copies(
        (
            (token_hbm, token_ref),
            (abias_hbm, abias_ref),
            (gain_hbm, gain_ref),
            (shift_hbm, shift_ref),
            (bias_hbm, bias_ref),
            (up_hbm, up_ref),
            (down_hbm, down_ref),
        ),
        wsem,
    )
    for item in weights_in:
        item.start()

    def grad_rows(block):
        return grad_ref.at[pl.ds(pl.multiple_of(block * rows, rows), rows)]

    def grad_on(d, s):
        block = jnp.clip(me - s if d == 0 else me + s, 0, n - 1)
        return pltpu.make_async_remote_copy(
            src_ref=near_ref.at[block] if s == 1 else grad_rows(block),
            dst_ref=grad_rows(block),
            send_sem=csend.at[d, s],
            recv_sem=crecv.at[d, s],
            device_id={"tensor": jnp.clip(me + 1 if d == 0 else me - 1, 0, n - 1)},
            device_id_type=MESH,
        )

    def grad_sends(d, s):
        return (me - s >= 0) & (me < n - 1) if d == 0 else (me + s < n) & (me > 0)

    def grad_near(d):
        block = jnp.clip(me - 1 if d == 0 else me + 1, 0, n - 1)
        return pltpu.make_async_copy(near_ref.at[block], grad_rows(block), cloc.at[d])

    def grad_own():
        return pltpu.make_async_copy(cot_ref, grad_rows(me), cloc.at[2])

    def beside(d):
        return me > 0 if d == 0 else me < n - 1

    grad_own().start()
    for d in range(2):

        @pl.when(beside(d))
        def _():
            grad_near(d).start()

    pl.semaphore_wait(bar, total)

    def to_place(shift):
        other = lax.rem(place + shift, total)
        return pltpu.make_async_remote_copy(
            src_ref=piece_ref.at[other],
            dst_ref=att_ref.at[my_head],
            send_sem=asend.at[shift],
            recv_sem=arecv.at[shift],
            device_id=spread(other, AXES, (nc, n)),
            device_id_type=MESH,
        )

    @pl.when(ctx < heads)
    def _():
        for shift in range(1, total):
            to_place(shift).start()
        stay = pltpu.make_async_copy(piece_ref.at[place], att_ref.at[my_head], aloc)
        stay.start()
        stay.wait()

    for d in range(2):

        @pl.when(grad_sends(d, 1))
        def _():
            grad_on(d, 1).start()

    for shift in range(1, total):
        source = lax.rem(place + total - shift, total)
        at_ctx, at_ten = lax.div(source, n), lax.rem(source, n)

        @pl.when(at_ctx < heads)
        def _():
            landed = att_ref.at[at_ten * heads + jnp.minimum(at_ctx, heads - 1)]
            pltpu.make_async_copy(landed, landed, arecv.at[shift]).wait()

    for item in weights_in[:4]:
        item.wait()
    attended = att_ref[...].reshape(width, rows)
    middle = token_ref[...].astype(f32) + dot(attended, out_ref[...], ((0,), (0,))) + row(abias_ref)
    middle_ref[...] = middle
    leave[3].start()
    x_ref[...] = (norm_parts(middle)[0] * row(gain_ref) + row(shift_ref)).astype(low)

    @pl.when(ctx < heads)
    def _():
        for shift in range(1, total):
            to_place(shift).wait_send()

    def rows_of(block):
        return pl.ds(pl.multiple_of(block * rows, rows), rows)

    def neighbour(d):
        return {"tensor": jnp.clip(jnp.where(d == 0, me + 1, me - 1), 0, n - 1)}

    def onward(d):
        return jnp.where(d == 0, me, n - 1 - me) < n - 1

    def hand_on(d, s, block, first):
        return pltpu.make_async_remote_copy(
            src_ref=x_ref if first else held.at[rows_of(block)],
            dst_ref=held.at[rows_of(block)],
            send_sem=gsend.at[d, s],
            recv_sem=grecv.at[d, s],
            device_id=neighbour(d),
            device_id_type=MESH,
        )

    def chunk(block, c):
        return pl.ds(pl.multiple_of(block * rows + c * few, few), few)

    def back(d, block, c, first):
        at = chunk(block, c)
        return pltpu.make_async_remote_copy(
            src_ref=part.at[at] if first else tmp.at[at],
            dst_ref=buf.at[d, at],
            send_sem=ssend.at[block, c],
            recv_sem=srecv.at[d, block, c],
            device_id=neighbour(d),
            device_id_type=MESH,
        )

    for d in range(2):

        @pl.when(onward(d))
        def _():
            hand_on(d, 0, me, True).start()

    own = pltpu.make_async_copy(x_ref, held.at[rows_of(me)], loc)
    own.start()
    sum_ref[...] = jnp.zeros_like(sum_ref)
    own.wait()
    for item in weights_in[4:]:
        item.wait()
    grad_own().wait()
    for d in range(2):

        @pl.when(beside(d))
        def _():
            grad_near(d).wait()

    for s in range(1, n - 1):
        for d in range(2):
            block = me - 1 - s if d == 0 else me + 1 + s

            @pl.when((block >= 0) & (block < n))
            def _():
                landed = grad_rows(jnp.clip(block, 0, n - 1))
                pltpu.make_async_copy(landed, landed, crecv.at[d, s]).wait()

            if s + 1 < n - 1:

                @pl.when(grad_sends(d, s + 1))
                def _():
                    grad_on(d, s + 1).start()

        if s == n - 3:
            break
    columns = wide

    def work(block):
        here = rows_of(block)
        acc[...] = jnp.zeros_like(acc)

        @pl.loop(0, wide // columns)
        def _(j):
            at = pl.ds(pl.multiple_of(j * columns, columns), columns)
            pre = dot(held[here, :], up_ref[:, at], ((1,), (0,))) + bias_ref[at].reshape(1, -1)
            square = pre * pre
            tanh = jnp.tanh(GELU_SCALE * pre * (1.0 + GELU_CUBE * square))
            act[here, at] = (0.5 * pre * (1.0 + tanh)).astype(low)
            slope = 0.5 * (1.0 + tanh) + 0.5 * pre * (1.0 - tanh * tanh) * (
                GELU_SCALE * (1.0 + 3.0 * GELU_CUBE * square)
            )
            grad = (dot(grad_ref[here, :], down_ref[at, :], ((1,), (1,))) * slope).astype(low)
            gp[here, at] = grad
            acc[...] += dot(grad, up_ref[:, at], ((1,), (1,)))

        part[here, :] = acc[...].astype(low)
        sum_ref[...] += jnp.sum(gp[here, :].astype(f32), axis=0, keepdims=True)

    near = jnp.minimum(me, n - 1 - me)
    toward = jnp.where(2 * me < n - 1, -1, 1)

    @pl.loop(0, n)
    def _(slot):
        paired = slot <= 2 * near
        distance = jnp.where(paired, lax.div(slot + 1, 2), slot - near)
        side = jnp.where(paired & (lax.rem(slot, 2) == 1), toward, -toward)
        block = me + side * distance
        d = jnp.where(block < me, 0, 1)
        s = jnp.maximum(distance - 1, 0)

        @pl.when(slot > 0)
        def _():
            landed = held.at[rows_of(block)]
            pltpu.make_async_copy(landed, landed, grecv.at[d, s]).wait()

            @pl.when(onward(d))
            def _():
                hand_on(d, jnp.minimum(s + 1, n - 2), block, False).start()

        @pl.when(distance == n - 1)
        def _():
            landed = grad_rows(block)
            pltpu.make_async_copy(landed, landed, crecv.at[d, n - 2]).wait()

        work(block)

        @pl.when((slot > 0) & ((me == 0) | (me == n - 1)))
        def _():
            for c in range(chunks):
                back(1 - d, block, c, True).start()

    def weights(left, right, unit):
        half = wide // 2

        @pl.loop(0, 2)
        def _(j):
            at = pl.ds(pl.multiple_of(j * half, 128), half)
            total = dot(left[:, at], right[...], ((0,), (0,)))
            unit[pl.ds(8 * j, 8)] = total.astype(low).reshape((8,) + unit.shape[1:])

    weights(act, grad_ref, u1)
    plane[0].begin()
    weights(held, gp, u2)
    plane[1].begin()

    def relay(way, block):
        d = jnp.where(way > 0, 0, 1)

        @pl.when((me > 0) & (me < n - 1) & (block >= 0) & (block < n))
        def _():
            for c in range(chunks):
                at = chunk(block, c)
                landed = buf.at[d, at]
                pltpu.make_async_copy(landed, landed, srecv.at[d, block, c]).wait()
                tmp[at, :] = (buf[d, at, :].astype(f32) + part[at, :].astype(f32)).astype(low)
                back(d, block, c, False).start()

    plane[0].first()
    for j in range(1, n):
        relay(-toward, me - toward * j)
        if j == 1:
            plane[1].first()

    @pl.loop(0, n)
    def _(block):
        here = rows_of(block)
        feed_ref[here, :] = dot(act[here, :], down_ref[...], ((1,), (0,))).astype(low)

    leave[0].start()

    plane[0].second()
    plane[1].second()
    for j in range(1, n):
        relay(toward, me + toward * j)
    for item in plane:
        item.third()
    for c in range(chunks):
        at = chunk(me, c)
        mine = pl.ds(c * few, few)
        o_ref[mine, :] = part[at, :].astype(f32)
        for d in range(2):

            @pl.when(me > 0 if d == 0 else me < n - 1)
            def _():
                landed = buf.at[d, at]
                pltpu.make_async_copy(landed, landed, srecv.at[d, me, c]).wait()
                o_ref[mine, :] += buf[d, at, :].astype(f32)

    grad = o_ref[...]
    normed, scale = norm_parts(middle_ref[...])
    above = grad_ref[rows_of(me), :].astype(f32)
    grad_middle = above + norm_backward(grad, normed, scale, row(gain_ref))
    gm_ref[...] = grad_middle
    for at in (1, 2, 4):
        leave[at].start()
    gm_low = grad_middle.astype(low)
    back_out = dot(out_ref[...], gm_low, ((1,), (1,))).astype(low)
    gpiece[...] = back_out.reshape(gpiece.shape)
    vec_ref[...] = jnp.zeros_like(vec_ref)
    vec_ref[2:3, :] = jnp.sum(gm_low.astype(f32), axis=0, keepdims=True)

    def to_head(shift):
        other = lax.rem(place + shift, total)
        at_ctx, at_ten = lax.div(other, n), lax.rem(other, n)
        return at_ctx < heads, pltpu.make_async_remote_copy(
            src_ref=gpiece.at[at_ten * heads + jnp.minimum(at_ctx, heads - 1)],
            dst_ref=heads_ref.at[place],
            send_sem=bsend.at[shift],
            recv_sem=brecv.at[shift],
            device_id={"context": at_ctx, "tensor": at_ten},
            device_id_type=MESH,
        )

    for shift in range(1, total):
        goes, item = to_head(shift)

        @pl.when(goes)
        def _():
            item.start()

    stay = pltpu.make_async_copy(gpiece.at[my_head], heads_ref.at[place], bloc)
    stay.start()
    u3[...] = dot(att_ref[...].reshape(width, rows), gm_low, ((1,), (0,))).astype(low).reshape(u3.shape)
    out_sum.begin()
    vec_ref[3:4, :] = jnp.sum(grad * normed, axis=0, keepdims=True)
    vec_ref[4:5, :] = jnp.sum(grad, axis=0, keepdims=True)
    vec_ref[5:6, :] = jnp.sum(above, axis=0, keepdims=True)
    vec_ref[6:7, :] = sum_ref[...]
    out_sum.first()
    out_sum.second()
    out_sum.third()
    leave[5].start()
    leave[6].start()
    stay.wait()

    @pl.when(ctx < heads)
    def _():
        for shift in range(1, total):
            source = lax.rem(place + total - shift, total)
            landed = heads_ref.at[source]
            pltpu.make_async_copy(landed, landed, brecv.at[shift]).wait()

    for shift in range(1, total):
        goes, item = to_head(shift)

        @pl.when(goes)
        def _():
            item.wait_send()

    out_sum.reduced()
    for item in leave:
        item.wait()
    for d in range(2):
        for s in range(n - 1):
            block = me - s if d == 0 else me + s

            @pl.when(onward(d) & (block >= 0) & (block < n))
            def _():
                hand_on(d, s, me, True).wait_send()

    for block in range(n):

        @pl.when(me != block)
        def _():
            for c in range(chunks):
                back(jnp.where(me < block, 0, 1), block, c, True).wait_send()

    for d in range(2):
        for s in range(1, n - 1):

            @pl.when(grad_sends(d, s))
            def _():
                grad_on(d, s).wait_send()

    for item in plane:
        item.reduced()


def feed_part(pieces, tokens, out_weight, vectors, up, down, bias, near, cotangent, n, nc, heads, collective_id):
    rows, width = tokens.shape
    wide = up.shape[1]
    chunks = 4
    total = n * rows
    low, f32 = jnp.bfloat16, jnp.float32
    unit = (16, wide // 16, width)
    piece = jax.ShapeDtypeStruct((2,) + unit[1:], low)
    return pl.pallas_call(
        functools.partial(feed_kernel, n, nc, heads, chunks),
        out_shape=(
            jax.ShapeDtypeStruct((total, width), low),
            piece,
            piece,
            jax.ShapeDtypeStruct((rows, width), f32),
            jax.ShapeDtypeStruct((rows, width), f32),
            jax.ShapeDtypeStruct((8, width), f32),
            jax.ShapeDtypeStruct((2, 2, rows // 4, width // 2), low),
            jax.ShapeDtypeStruct(pieces.shape, low),
        ),
        in_specs=[VM, HB, VM, HB, HB, HB, HB, HB, HB, VM, HB],
        out_specs=(HB,) * 7 + (VM,),
        scratch_shapes=[
            pltpu.VMEM((total, width), low),
            pltpu.VMEM(piece.shape, low),
            pltpu.VMEM(piece.shape, low),
            pltpu.VMEM((rows, width), f32),
            pltpu.VMEM((rows, width), f32),
            pltpu.VMEM((8, width), f32),
            pltpu.VMEM((2, 2, rows // 4, width // 2), low),
            pltpu.VMEM(tokens.shape, tokens.dtype),
            pltpu.VMEM((width,), f32),
            pltpu.VMEM((width,), f32),
            pltpu.VMEM((width,), f32),
            pltpu.VMEM((wide,), f32),
            DMA((7,)),
            pltpu.VMEM((rows, width), f32),
            pltpu.VMEM((1, wide), f32),
            pltpu.VMEM((n * heads,) + pieces.shape[1:], low),
            pltpu.VMEM((n * heads,) + pieces.shape[1:], low),
            pltpu.VMEM((n, width // n, width), low),
            DMA((nc * n,)),
            DMA((nc * n,)),
            DMA,
            pltpu.VMEM((rows, width), low),
            pltpu.VMEM(up.shape, low),
            pltpu.VMEM(down.shape, low),
            pltpu.VMEM((total, width), low),
            DMA((7,)),
            DMA((nc * n,)),
            DMA((nc * n,)),
            DMA,
            DMA((2, n - 1)),
            DMA((2, n - 1)),
            DMA((3,)),
            pltpu.VMEM((total, width), low),
            pltpu.VMEM((total, wide), low),
            pltpu.VMEM((total, wide), low),
            pltpu.VMEM((total, width), low),
            pltpu.VMEM((rows, width), f32),
            pltpu.VMEM((2, total, width), low),
            pltpu.VMEM((total, width), low),
            pltpu.VMEM(unit, low),
            pltpu.VMEM(unit, low),
            DMA((2, n - 1)),
            DMA((2, n - 1)),
            DMA,
            DMA((n, chunks)),
            DMA((2, n, chunks)),
        ]
        + PlaneSum.reduce_scratch(unit, low) * 2
        + StripSum.reduce_scratch((n, width // n, width), low),
        compiler_params=remote_params(collective_id, 40),
    )(pieces, tokens, out_weight, *vectors, up, down, bias, near, cotangent)


def last_kernel(n, nc, heads, shared, count, x_ref, w_hbm, h_hbm, a_hbm, feed_hbm, mid_hbm, bias_hbm, *rest):
    ps, rest = rest[:count], rest[count:]
    (token_hbm, gain_hbm, middle_hbm, vec_hbm), rest = rest[:4], rest[4:]
    (out_ref, g_ref, v_ref, po_ref, ao_ref), rest = rest[:5], rest[5:]
    outs, rest = rest[:count], rest[count:]
    (rows_ref, w_ref, h_ref, token_ref, middle_ref, part, sum_ref, u_ref, piece), rest = rest[:9], rest[9:]
    (hsend, hrecv, hloc, win), rest = rest[:4], rest[4:]
    (feed_ref, fsum_ref, mid_ref, bias_ref, gain_ref, vec_ref), rest = rest[:6], rest[6:]
    feed_line = LineScatter(n, feed_ref, fsum_ref, *rest[:4])
    rest = rest[4:]
    chunks = 2
    own = token_ref.shape[0]
    few = own // chunks
    lines = [
        LineScatter(n, part.at[:, pl.ds(c * few, few)], sum_ref.at[pl.ds(c * few, few)], *rest[4 * c : 4 * c + 4])
        for c in range(chunks)
    ]
    rest = rest[4 * chunks :]
    project = StripSum(u_ref, piece, po_ref, rest[:10], rest[10:13])
    rest = rest[13:]
    feeds = [PlaneSum(None, ps[i], outs[i], None, rest[3 * i : 3 * i + 3]) for i in range(count)]
    rest = rest[3 * count :]
    (land, zsend, zrecv, zloc, a_ref), rest = rest[:5], rest[5:]
    (asend, arecv, aloc, now), rest = rest[:4], rest[4:]
    sizes = (n, 2 * nc)
    bufs, sems = rest[:2], rest[2:]
    f32, low = jnp.float32, jnp.bfloat16

    ten, ctx, x = (lax.axis_index(name) for name in ("tensor", "context", "dp"))
    place = ctx * 2 + x
    bar = pltpu.get_barrier_semaphore()
    for shift in range(1, n):
        pl.semaphore_signal(bar, inc=1, device_id={"tensor": lax.rem(ten + shift, n)}, device_id_type=MESH)
    for shift in range(1, 8):
        other = lax.rem(place + shift, 8)
        pl.semaphore_signal(
            bar, inc=1, device_id={"context": lax.div(other, 2), "dp": lax.rem(other, 2)}, device_id_type=MESH
        )
    copies_in = copies(
        (
            (feed_hbm, feed_ref),
            (token_hbm, token_ref),
            (w_hbm, w_ref),
            (h_hbm, h_ref),
            (middle_hbm, middle_ref),
            (mid_hbm, mid_ref),
            (bias_hbm, bias_ref),
            (gain_hbm, gain_ref),
            (vec_hbm, vec_ref),
        ),
        win,
    )
    for item in copies_in:
        item.start()
    pl.semaphore_wait(bar, n + 6)

    half = 2 * own
    far = 1 - lax.div(ten, 2)
    pairs = (far, 1 - far)

    def columns(pair):
        return pl.ds(pl.multiple_of(pair * half, 128), half)

    def ship(index, shift):
        other = lax.rem(ctx + shift, nc)
        return pltpu.make_async_remote_copy(
            src_ref=x_ref.at[other, :, :, columns(pairs[index])],
            dst_ref=rows_ref.at[:, jnp.minimum(ctx, heads - 1), :, columns(pairs[index])],
            send_sem=hsend.at[index, shift],
            recv_sem=hrecv.at[index, shift],
            device_id={"context": other},
            device_id_type=MESH,
        )

    @pl.when(ctx < heads)
    def _():
        for index in range(2):
            for shift in range(1, nc):
                ship(index, shift).start()
        stay = pltpu.make_async_copy(x_ref.at[ctx], rows_ref.at[:, ctx], hloc)
        stay.start()
        stay.wait()

    def across(shift):
        other = lax.rem(ten + shift, n)
        return pltpu.make_async_remote_copy(
            src_ref=a_hbm.at[lax.div(other, 2), lax.rem(other, 2)],
            dst_ref=land.at[ten],
            send_sem=zsend.at[shift],
            recv_sem=zrecv.at[shift],
            device_id={"tensor": other},
            device_id_type=MESH,
        )

    copies_in[0].wait()
    feed_line.begin((0,))
    for shift in range(1, n):
        across(shift).start()
    mine = pltpu.make_async_copy(a_hbm.at[lax.div(ten, 2), lax.rem(ten, 2)], land.at[ten], zloc)
    mine.start()
    for item in feeds:
        item.spread1()

    def there(at):
        ctx_, x_ = lax.div(at, 2), lax.rem(at, 2)
        y_ = lax.div(ctx_, 2)
        row_ = jnp.where(ten < n // 2, 2 * x_ + y_, 2 * y_ + x_)
        rows = pl.ds(pl.multiple_of(row_ * a_ref.shape[0], 16), a_ref.shape[0])
        cols = pl.ds(pl.multiple_of(lax.rem(ctx_, 2) * a_ref.shape[1], 128), a_ref.shape[1])
        return ao_ref.at[rows, cols]

    def push(shift):
        other = lax.rem(place + shift, 8)
        return pltpu.make_async_remote_copy(
            src_ref=a_ref,
            dst_ref=there(place),
            send_sem=asend.at[shift],
            recv_sem=arecv.at[shift],
            device_id={"context": lax.div(other, 2), "dp": lax.rem(other, 2)},
            device_id_type=MESH,
        )

    copies_in[1].wait()
    normed, scale = norm_parts(token_ref[...].astype(f32))
    mine.wait()
    for shift in range(1, n):
        source = lax.rem(ten + n - shift, n)
        pltpu.make_async_copy(land.at[source], land.at[source], zrecv.at[shift]).wait()
    value = land[0].astype(f32)
    for at in range(1, n):
        value = value + land[at].astype(f32)
    a_ref[...] = value.astype(low)
    for item in copies_in[2:]:
        item.wait()
    now[0] = vec_ref[...]
    for shift in range(1, 8):
        push(shift).start()
    kept = pltpu.make_async_copy(a_ref, there(place), aloc)
    kept.start()

    def partials(index):
        at = columns(pairs[index])
        for shift in range(1, nc):
            source = lax.rem(ctx + nc - shift, nc)

            @pl.when(source < heads)
            def _():
                ref = rows_ref.at[:, jnp.minimum(source, heads - 1), :, at]
                pltpu.make_async_copy(ref, ref, hrecv.at[index, shift]).wait()

        total = 0.0
        for kind in range(3):
            grads = rows_ref[kind, :, :, at].reshape(heads * HEAD_DIM, half)
            total = total + dot(grads, w_ref[kind], ((0,), (0,)))
        part[pl.ds(2 * pairs[index], 2)] = total.astype(low).reshape(2, own, total.shape[1])

    first = lambda d: (ten < n // 2) if d == 0 else (ten >= n // 2)
    second = lambda d: (ten >= n // 2) if d == 0 else (ten < n // 2)
    feed_line.step(0, first)
    partials(0)
    for line in lines:
        line.begin((0, 1))
    partials(1)
    for line in lines:
        line.begin((2,))
    feed_line.begin((1, 2))
    for item in feeds:
        item.spread2()
    for line in lines:
        line.step(0, first)
    for kind in range(3):
        grads = rows_ref[kind].reshape(heads * HEAD_DIM, n * own)
        u_ref[kind] = dot(grads, h_ref[...], ((1,), (0,))).astype(low)
    project.begin()
    for line in lines:
        line.step(1, first)
    feed_line.step(0, second)
    ends = jnp.concatenate(
        [rows_ref[kind].reshape(heads * HEAD_DIM, n * own) for kind in (0, 2)], axis=0
    )
    bias = dot(jnp.ones((8, n * own), low), ends, ((1,), (1,)))
    now[0, 7:8, 0 : bias.shape[1]] = bias[0:1]
    project.first()
    for item in feeds:
        item.spread3()
    project.second()
    for k in range(n - 1):
        for line in lines:
            line.step(k, second)
    project.third()
    project.spread1()
    for line in lines:
        line.end()
    grad = sum_ref[...]
    now[0, 0:1] = jnp.sum(grad * normed, axis=0, keepdims=True)
    now[0, 1:2] = jnp.sum(grad, axis=0, keepdims=True)
    alone = now[0]

    def where(stage):
        return ten if stage == 0 else place

    def stage_copy(stage, shift):
        other = lax.rem(where(stage) + shift, sizes[stage])
        peer = {"tensor": other} if stage == 0 else {"context": lax.div(other, 2), "dp": lax.rem(other, 2)}
        return pltpu.make_async_remote_copy(
            src_ref=now.at[stage],
            dst_ref=bufs[stage].at[where(stage)],
            send_sem=sems[2 * stage].at[shift],
            recv_sem=sems[2 * stage + 1].at[shift],
            device_id=peer,
            device_id_type=MESH,
        )

    def stage_start(stage):
        for shift in range(1, sizes[stage]):
            stage_copy(stage, shift).start()
        bufs[stage][where(stage)] = now[stage]

    def stage_end(stage):
        buf, size = bufs[stage], sizes[stage]
        for shift in range(1, size):
            source = lax.rem(where(stage) + size - shift, size)
            pltpu.make_async_copy(buf.at[source], buf.at[source], sems[2 * stage + 1].at[shift]).wait()
        total = buf[0]
        for at in range(1, size):
            total = total + buf[at]
        if stage == 0:
            line_ = lax.broadcasted_iota(jnp.int32, total.shape, 0)
            now[1] = jnp.where(line_ < shared, total, alone)
        else:
            v_ref[...] = total

    stage_start(0)
    back = norm_backward(grad, normed, scale, row(gain_ref))
    g_ref[...] = (middle_ref[...] + back).astype(g_ref.dtype)
    project.spread2()
    feed_line.step(1, first)
    stage_end(0)
    stage_start(1)
    project.spread3()
    feed_line.end()
    out_ref[...] = (mid_ref[...] + fsum_ref[...] + row(bias_ref)).astype(low)
    kept.wait()
    for shift in range(1, 8):
        source = there(lax.rem(place + 8 - shift, 8))
        pltpu.make_async_copy(source, source, arecv.at[shift]).wait()
    for item in feeds:
        item.everywhere()
    stage_end(1)
    project.everywhere()
    project.reduced()

    @pl.when(ctx < heads)
    def _():
        for index in range(2):
            for shift in range(1, nc):
                ship(index, shift).wait_send()

    for shift in range(1, n):
        across(shift).wait_send()
    for shift in range(1, 8):
        push(shift).wait_send()
    for stage in range(2):
        for shift in range(1, sizes[stage]):
            stage_copy(stage, shift).wait_send()


def last_part(x, weight, hidden, attend_pieces, feed, middle, bias, pieces, tokens, gain, grad_middle, vectors, shared, n, heads, collective_id):
    nc = x.shape[0]
    own, cols = tokens.shape
    count = len(pieces)
    f32, low = jnp.float32, jnp.bfloat16
    whole = lambda item: jax.ShapeDtypeStruct((16,) + item.shape[1:], item.dtype)
    wide, deep = attend_pieces.shape[2:]
    unit = (3, heads * HEAD_DIM, cols)
    result = pl.pallas_call(
        functools.partial(last_kernel, n, nc, heads, shared, count),
        out_shape=(
            jax.ShapeDtypeStruct((own, cols), low),
            jax.ShapeDtypeStruct((own, cols), low),
            jax.ShapeDtypeStruct(vectors.shape, f32),
            jax.ShapeDtypeStruct(unit, low),
            jax.ShapeDtypeStruct((4 * wide, 2 * deep), low),
        )
        + tuple(whole(item) for item in pieces),
        in_specs=[VM] + [HB] * (10 + count),
        out_specs=(VM,) * (5 + count),
        scratch_shapes=[
            pltpu.VMEM((3, heads, HEAD_DIM, n * own), low),
            pltpu.VMEM(weight.shape, low),
            pltpu.VMEM(hidden.shape, low),
            pltpu.VMEM(tokens.shape, low),
            pltpu.VMEM((own, cols), f32),
            pltpu.VMEM((n, own, cols), low),
            pltpu.VMEM((own, cols), f32),
            pltpu.VMEM(unit, low),
            pltpu.VMEM((2, 2, unit[1] // 4, cols // 2), low),
            DMA((2, nc)),
            DMA((2, nc)),
            DMA,
            DMA((9,)),
            pltpu.VMEM((n, own, cols), low),
            pltpu.VMEM((own, cols), f32),
            pltpu.VMEM((own, cols), f32),
            pltpu.VMEM((cols,), f32),
            pltpu.VMEM((cols,), f32),
            pltpu.VMEM(vectors.shape, f32),
        ]
        + LineScatter.scratch(n, own, cols, low)
        + LineScatter.scratch(n, own // 2, cols, low) * 2
        + StripSum.reduce_scratch(unit, low)
        + PlaneSum.spread_scratch()
        + [item for _ in pieces for item in PlaneSum.spread_scratch()]
        + [pltpu.VMEM((n, wide, deep), low), DMA((n,)), DMA((n,)), DMA, pltpu.VMEM((wide, deep), low)]
        + [DMA((8,)), DMA((8,)), DMA, pltpu.VMEM((2,) + vectors.shape, f32)]
        + [pltpu.VMEM((size,) + vectors.shape, f32) for size in (n, 2 * nc)]
        + [DMA((size,)) for size in (n, 2 * nc) for _ in range(2)],
        compiler_params=remote_params(collective_id, 32),
    )(
        x, weight, hidden, attend_pieces, feed.reshape(n, own, cols), middle, bias,
        *pieces, tokens, gain, grad_middle, vectors,
    )
    return result[:5] + (result[5:],)


class LineGather:
    def __init__(self, n, x, o, send, recv):
        self.n, self.x, self.o, self.send, self.recv = n, x, o, send, recv
        self.me = lax.axis_index("tensor")

    def copy(self, d, s):
        me, n = self.me, self.n
        shard = jnp.clip(me - s if d == 0 else me + s, 0, n - 1)
        return pltpu.make_async_remote_copy(
            src_ref=self.x if s == 0 else self.o.at[shard],
            dst_ref=self.o.at[shard],
            send_sem=self.send.at[d, s],
            recv_sem=self.recv.at[d, s],
            device_id={"tensor": jnp.clip(me + 1 if d == 0 else me - 1, 0, n - 1)},
            device_id_type=MESH,
        )

    def sends(self, d, s):
        me, n = self.me, self.n
        return (me - s >= 0) & (me < n - 1) if d == 0 else (me + s < n) & (me > 0)

    def wait(self, d, s):
        me, n = self.me, self.n

        @pl.when(me - 1 - s >= 0 if d == 0 else me + 1 + s < n)
        def _():
            shard = jnp.clip(me - 1 - s if d == 0 else me + 1 + s, 0, n - 1)
            pltpu.make_async_copy(self.o.at[shard], self.o.at[shard], self.recv.at[d, s]).wait()

    def step(self, s):
        for d in range(2):
            if s > 0:
                self.wait(d, s - 1)

            @pl.when(self.sends(d, s))
            def _():
                self.copy(d, s).start()

    def pass_on(self, d, s, now):
        @pl.when(self.sends(d, s) & now)
        def _():
            self.copy(d, s).start()

    def last(self):
        for d in range(2):
            self.wait(d, self.n - 2)

    def finish(self, steps=None):
        for d in range(2):
            for s in range(steps or self.n - 1):

                @pl.when(self.sends(d, s))
                def _():
                    self.copy(d, s).wait_send()


def start_kernel(n, nc, heads, t_hbm, gain_hbm, shift_hbm, full_ref, w_hbm, b_hbm, c_ref, o_hbm, f_ref, q_ref, g_ref, *rest):
    (x_ref, held, proj, w_ref, o_ref, t_ref, gain_ref, shift_ref, b_ref, win), rest = rest[:10], rest[10:]
    arrive = copies(((t_hbm, t_ref), (gain_hbm, gain_ref), (shift_hbm, shift_ref), (b_hbm, b_ref)), win)
    for item in arrive:
        item.start()
    s1, r1, s2, r2, s5, r5, s3, r3, s4, r4, loc = rest
    me, ctx, x = lax.axis_index("tensor"), lax.axis_index("context"), lax.axis_index("dp")
    core, y = lax.rem(ctx, 2), lax.div(ctx, 2)
    rows, width = t_ref.shape
    half = 2 * rows
    bar = pltpu.get_barrier_semaphore()
    met = line_greet(bar, me, n)
    for shift in range(1, nc):
        pl.semaphore_signal(bar, inc=1, device_id={"context": lax.rem(ctx + shift, nc)}, device_id_type=MESH)
    pl.semaphore_signal(bar, inc=1, device_id={"dp": 1 - x}, device_id_type=MESH)
    weight_in = pltpu.make_async_copy(w_hbm, w_ref, loc.at[4])
    weight_in.start()
    for item in arrive:
        item.wait()
    normed, _ = norm_parts(t_ref[...].astype(jnp.float32))
    x_ref[...] = (normed * row(gain_ref) + row(shift_ref)).astype(x_ref.dtype)
    pl.semaphore_wait(bar, met + nc)

    tall, deep = held.shape[1:]
    strip = pl.ds(pl.multiple_of(core * deep, 128), deep)
    piece = full_ref.at[pl.ds(pl.multiple_of((2 * y + x) * tall, 16), tall), strip]
    small = LineGather(n, piece, held, s1, r1)
    large = LineGather(n, x_ref, o_ref, s2, r2)
    grads = LineGather(n, c_ref, g_ref, s5, r5)
    def move(s):
        large.step(s)
        for d in range(2):
            grads.pass_on(d, 0, me == (s if d == 0 else n - 1 - s))

    small.step(0)
    move(0)
    own = pltpu.make_async_copy(x_ref, o_ref.at[me], loc.at[0])
    own.start()
    mine = pltpu.make_async_copy(piece, held.at[me], loc.at[1])
    mine.start()
    mine.wait()
    own.wait()
    for s in range(1, n - 1):
        small.step(s)
    small.last()

    def there(y_, x_):
        return f_ref.at[:, pl.ds(pl.multiple_of((2 * y_ + x_) * tall, 16), tall), strip]

    x_peer, y_peer = {"dp": 1 - x}, {"context": lax.rem(ctx + 2, 4)}

    def hop(at):
        src, dst, peer = [
            (held, there(y, x), x_peer),
            (held, there(y, x), y_peer),
            (there(y, 1 - x), there(y, 1 - x), y_peer),
            (f_ref.at[:, :, strip], f_ref.at[:, :, strip], {"context": ctx + 1 - 2 * core}),
        ][at]
        return pltpu.make_async_remote_copy(
            src_ref=src,
            dst_ref=dst,
            send_sem=s3.at[at],
            recv_sem=r3.at[at],
            device_id=peer,
            device_id_type=MESH,
        )

    def got(at):
        other = pl.ds(pl.multiple_of((1 - core) * deep, 128), deep)
        ref = [there(y, 1 - x), there(1 - y, x), there(1 - y, 1 - x), f_ref.at[:, :, other]][at]
        pltpu.make_async_copy(ref, ref, r3.at[at]).wait()

    hop(0).start()
    kept = pltpu.make_async_copy(held, there(y, x), loc.at[2])
    kept.start()

    def columns(pair):
        return pl.ds(pl.multiple_of(pair * half, 128), half)

    def project(pair):
        token = jnp.concatenate([o_ref[2 * pair], o_ref[2 * pair + 1]], axis=0)
        for kind in range(3):
            value = dot(w_ref[kind], token, ((1,), (1,))) + b_ref[kind]
            proj[kind, :, :, columns(pair)] = value.astype(proj.dtype).reshape(heads, HEAD_DIM, half)

    def ship(index, pair, shift):
        other = lax.rem(ctx + shift, nc)
        return other, pltpu.make_async_remote_copy(
            src_ref=proj.at[:, jnp.minimum(other, heads - 1), :, columns(pair)],
            dst_ref=q_ref.at[ctx, :, :, columns(pair)],
            send_sem=s4.at[index, shift],
            recv_sem=r4.at[index, shift],
            device_id={"context": other},
            device_id_type=MESH,
        )

    def ship_all(index, pair):
        for shift in range(1, nc):
            other, item = ship(index, pair, shift)

            @pl.when(other < heads)
            def _():
                item.start()

    near = lax.div(me, 2)
    move(1)
    weight_in.wait()
    project(near)
    ship_all(0, near)
    hop(1).start()
    for s in range(2, n - 1):
        move(s)
    got(0)
    hop(2).start()
    large.last()
    project(1 - near)
    ship_all(1, 1 - near)
    result = pltpu.make_async_copy(o_ref, o_hbm, loc.at[5])
    result.start()
    stay = pltpu.make_async_copy(proj.at[:, jnp.minimum(ctx, heads - 1)], q_ref.at[ctx], loc.at[3])
    stay.start()
    kept.wait()
    got(1)
    got(2)
    hop(3).start()
    stay.wait()

    @pl.when(ctx < heads)
    def _():
        for index in range(2):
            for shift in range(1, nc):
                source = lax.rem(ctx + nc - shift, nc)
                pair = near if index == 0 else 1 - near
                ref = q_ref.at[source, :, :, columns(pair)]
                pltpu.make_async_copy(ref, ref, r4.at[index, shift]).wait()

    got(3)
    for d in range(2):
        grads.wait(d, 0)
    result.wait()
    small.finish()
    large.finish()
    grads.finish(1)
    for at in range(4):
        hop(at).wait_send()
    for index in range(2):
        for shift in range(1, nc):
            other, item = ship(index, near if index == 0 else 1 - near, shift)

            @pl.when(other < heads)
            def _():
                item.wait_send()


def start_part(tokens, gain, shift, w, project_weight, bias, cotangent, n, nc, heads, collective_id):
    rows, cols = tokens.shape
    wide, deep = w.shape
    low = jnp.bfloat16
    full, weight, qkv, grads = pl.pallas_call(
        functools.partial(start_kernel, n, nc, heads),
        out_shape=(
            jax.ShapeDtypeStruct((n, rows, cols), low),
            jax.ShapeDtypeStruct((n, wide, deep), w.dtype),
            jax.ShapeDtypeStruct((nc, 3, HEAD_DIM, n * rows), low),
            jax.ShapeDtypeStruct((n, rows, cols), low),
        ),
        in_specs=[HB] * 7,
        out_specs=(HB, VM, VM, VM),
        scratch_shapes=[
            pltpu.VMEM((rows, cols), low),
            pltpu.VMEM((n, wide // 4, deep // 2), w.dtype),
            pltpu.VMEM((3, heads, HEAD_DIM, n * rows), low),
            pltpu.VMEM(project_weight.shape, low),
            pltpu.VMEM((n, rows, cols), low),
            pltpu.VMEM((rows, cols), tokens.dtype),
            pltpu.VMEM(gain.shape, jnp.float32),
            pltpu.VMEM(shift.shape, jnp.float32),
            pltpu.VMEM(bias.shape, jnp.float32),
            DMA((4,)),
        ]
        + [DMA((2, n - 1)) for _ in range(6)]
        + [DMA((4,)), DMA((4,)), DMA((2, nc)), DMA((2, nc)), DMA((6,))],
        compiler_params=remote_params(collective_id, 44),
    )(tokens, gain, shift, w, project_weight, bias, cotangent)
    return full.reshape(n * rows, cols), weight.reshape(n * wide, deep), qkv, grads


def dot(left, right, dims):
    return lax.dot_general(left, right, ((dims[0], dims[1]), ((), ())), preferred_element_type=jnp.float32)


def key_positions(first, keys, queries):
    return first + lax.broadcasted_iota(jnp.int32, (keys, queries), 0)


def load_rows(qkv_ref, nb, half, qs, kt, ks, vs):
    for block in range(nb):
        part = slice(block % 2 * half, block % 2 * half + half)
        at = block // 2
        qs[block] = qkv_ref[at, 0, :, part] * jnp.asarray(HEAD_DIM**-0.5, qs.dtype)
        item = qkv_ref[at, 1, :, part]
        if kt is not None:
            kt[block] = item
        ks[block] = item.T
        if vs is not None:
            vs[block] = qkv_ref[at, 2, :, part].T


def fill_tables(nb, half, seg_ref, order_ref, slot_ref, low_ref, high_ref):
    for block in range(nb):
        slot_ref[order_ref[block]] = jnp.int32(block)
    first = [seg_ref[0, block * half] for block in range(nb)]
    last = [seg_ref[0, block * half + half - 1] for block in range(nb)]
    for block in range(nb):
        if low_ref is not None:
            low_ref[block] = sum(jnp.where(item < first[block], 1, 0) for item in last)
        if high_ref is not None:
            high_ref[block] = sum(jnp.where(item <= last[block], 1, 0) for item in first)


def forward_kernel(half, heads, seg_s, order_ref, seg_ref, qkv_ref, o_ref, full_ref, lse_ref, start_ref, qs, ks, slot_ref, low_ref):
    nb = full_ref.shape[0]

    @pl.when(lax.axis_index("context") < heads)
    def _():
        load_rows(qkv_ref, nb, half, qs, None, ks, None)
        fill_tables(nb, half, seg_s, order_ref, slot_ref, low_ref, None)
        seg = seg_ref[...]
        start = jnp.zeros(seg.shape, jnp.float32)
        for doc in range(1, DOC_LIMIT):
            before = jnp.sum(jnp.where(seg < doc, 1.0, 0.0), axis=1, keepdims=True)
            start = jnp.where(seg == doc, before, start)
        start_ref[...] = start.astype(jnp.int32)

        @pl.loop(0, nb)
        def _(nq):
            slot = slot_ref[nq]
            query = qs[slot]
            begin = start_ref[:, pl.ds(pl.multiple_of(nq * half, 128), half)]
            here = nq * half + lax.broadcasted_iota(jnp.int32, (1, half), 1)

            def step(nk, state):
                top, total, acc = state
                at = slot_ref[nk]
                score = dot(ks[at], query, ((1,), (0,)))
                place = key_positions(nk * half, half, half)
                score = jnp.where((place >= begin) & (place <= here), score, NEG_FILL)
                new_top = jnp.maximum(top, jnp.max(score, axis=0, keepdims=True))
                factor = jnp.exp(top - new_top)
                weight = jnp.exp(score - new_top)
                total = total * factor + jnp.sum(weight, axis=0, keepdims=True)
                value = qkv_ref[at // 2, 2, :, pl.ds(pl.multiple_of(at % 2 * half, 128), half)]
                acc = acc * factor + dot(value, weight.astype(jnp.bfloat16), ((1,), (0,)))
                return new_top, total, acc

            top, total, acc = lax.fori_loop(
                low_ref[nq],
                nq + 1,
                step,
                (
                    jnp.full((1, half), NEG_FILL, jnp.float32),
                    jnp.zeros((1, half), jnp.float32),
                    jnp.zeros((HEAD_DIM, half), jnp.float32),
                ),
            )
            result = acc / total
            full_ref[slot] = result
            lse_ref[slot] = top + jnp.log(total)
            low = result.astype(jnp.bfloat16)
            o_ref[2 * slot] = low[:, : half // 2]
            o_ref[2 * slot + 1] = low[:, half // 2 :]


def attend_forward(qkv, segments, order, half, heads):
    nc = qkv.shape[0]
    nb = 2 * nc
    return pl.pallas_call(
        functools.partial(forward_kernel, half, heads),
        out_shape=(
            jax.ShapeDtypeStruct((2 * nb, HEAD_DIM, half // 2), jnp.bfloat16),
            jax.ShapeDtypeStruct((nb, HEAD_DIM, half), jnp.float32),
            jax.ShapeDtypeStruct((nb, 1, half), jnp.float32),
            jax.ShapeDtypeStruct(segments.shape, jnp.int32),
        ),
        in_specs=[SM, SM, VM, VM],
        out_specs=(VM, VM, VM, VM),
        scratch_shapes=[
            pltpu.VMEM((nb, HEAD_DIM, half), jnp.bfloat16),
            pltpu.VMEM((nb, half, HEAD_DIM), jnp.bfloat16),
            pltpu.SMEM((nb,), jnp.int32),
            pltpu.SMEM((nb,), jnp.int32),
        ],
        compiler_params=pltpu.CompilerParams(vmem_limit_bytes=24 << 20),
    )(segments, order, segments, qkv)


def backward_kernel(
    half, heads, seg_s, order_ref, start_ref, qkv_ref, full_ref, lse_ref, grad_ref, o_ref,
    qs, kt, ks, vs, gs, ds, dq, slot_ref, high_ref,
):
    nb = full_ref.shape[0]

    @pl.when(lax.axis_index("context") < heads)
    def _():
        load_rows(qkv_ref, nb, half, qs, kt, ks, vs)
        fill_tables(nb, half, seg_s, order_ref, slot_ref, None, high_ref)
        for block in range(nb):
            both = jnp.concatenate([grad_ref[2 * block], grad_ref[2 * block + 1]], axis=1)
            gs[block] = both
            ds[block] = jnp.sum(both.astype(jnp.float32) * full_ref[block], axis=0, keepdims=True)
            dq[block] = jnp.zeros((HEAD_DIM, half), jnp.float32)

        @pl.loop(0, nb)
        def _(nk):
            at = slot_ref[nk]
            place = key_positions(nk * half, half, half)

            def step(nq, state):
                grad_key, grad_value = state
                slot = slot_ref[nq]
                query, grad = qs[slot], gs[slot]
                begin = start_ref[:, pl.ds(pl.multiple_of(nq * half, 128), half)]
                here = nq * half + lax.broadcasted_iota(jnp.int32, (1, half), 1)
                score = dot(ks[at], query, ((1,), (0,)))
                score = jnp.where((place >= begin) & (place <= here), score, NEG_FILL)
                weight = jnp.exp(score - lse_ref[slot])
                grad_weight = dot(vs[at], grad, ((1,), (0,)))
                grad_score = (weight * (grad_weight - ds[slot])).astype(jnp.bfloat16)
                grad_value = grad_value + dot(grad, weight.astype(jnp.bfloat16), ((1,), (1,)))
                grad_key = grad_key + dot(query, grad_score, ((1,), (1,)))
                dq[slot] += dot(kt[at], grad_score, ((1,), (0,)))
                return grad_key, grad_value

            zero = jnp.zeros((HEAD_DIM, half), jnp.float32)
            grad_key, grad_value = lax.fori_loop(nk, high_ref[nk], step, (zero, zero))
            columns = pl.ds(pl.multiple_of(at % 2 * half, 128), half)
            o_ref[at // 2, 1, :, columns] = grad_key.astype(jnp.bfloat16)
            o_ref[at // 2, 2, :, columns] = grad_value.astype(jnp.bfloat16)

        for block in range(nb):
            part = slice(block % 2 * half, block % 2 * half + half)
            o_ref[block // 2, 0, :, part] = (dq[block] * HEAD_DIM**-0.5).astype(jnp.bfloat16)


def attend_backward(qkv, segments, order, start, full, lse, grad, half, heads):
    nc = qkv.shape[0]
    nb = 2 * nc
    low = jnp.bfloat16
    return pl.pallas_call(
        functools.partial(backward_kernel, half, heads),
        out_shape=jax.ShapeDtypeStruct(qkv.shape, low),
        in_specs=[SM, SM, VM, VM, VM, VM, VM],
        out_specs=VM,
        scratch_shapes=[
            pltpu.VMEM((nb, HEAD_DIM, half), low),
            pltpu.VMEM((nb, HEAD_DIM, half), low),
            pltpu.VMEM((nb, half, HEAD_DIM), low),
            pltpu.VMEM((nb, half, HEAD_DIM), low),
            pltpu.VMEM((nb, HEAD_DIM, half), low),
            pltpu.VMEM((nb, 1, half), jnp.float32),
            pltpu.VMEM((nb, HEAD_DIM, half), jnp.float32),
            pltpu.SMEM((nb,), jnp.int32),
            pltpu.SMEM((nb,), jnp.int32),
        ],
        compiler_params=pltpu.CompilerParams(vmem_limit_bytes=24 << 20),
    )(segments, order, start, qkv, full, lse, grad)


def norm_parts(values):
    centre = jnp.mean(values, axis=-1, keepdims=True)
    shifted = values - centre
    spread_ = jnp.mean(shifted * shifted, axis=-1, keepdims=True)
    scale = lax.rsqrt(spread_ + NORM_EPS)
    return shifted * scale, scale


def norm_backward(grad, normed, scale, gain):
    e = grad * gain
    mean_e = jnp.mean(e, axis=-1, keepdims=True)
    mean_en = jnp.mean(e * normed, axis=-1, keepdims=True)
    return (e - mean_e - normed * mean_en) * scale


def gelu_tanh(values):
    return jax.nn.gelu(values, approximate=True)


def cross_rows(left, right):
    return lax.dot_general(
        left, right, (((0,), (0,)), ((), ())), preferred_element_type=jnp.float32
    )


def after(value, done):
    return lax.optimization_barrier((value, done))[0]


def per_device(
    mesh_sizes,
    inputs,
    first_gain,
    first_shift,
    project_weight,
    project_bias,
    attend_weight,
    attend_bias,
    second_gain,
    second_shift,
    expand_weight,
    expand_bias,
    shrink_weight,
    shrink_bias,
    segments,
    block_order,
    cotangent,
):
    nt, nc = mesh_sizes["tensor"], mesh_sizes["context"]
    own_rows, width = inputs.shape[1], inputs.shape[2]
    local_width = project_weight.shape[2]
    heads = local_width // HEAD_DIM
    block_rows = own_rows * nt
    half = block_rows // 2
    low = jnp.bfloat16
    f32 = lambda value: value.astype(jnp.float32)
    square = nt == 4 and nc == 4 and mesh_sizes["dp"] == 2
    plane = ("context", "dp")

    tokens_own = f32(inputs[0])
    grad_out = cotangent[0]
    bias = jnp.stack([project_bias[0], jnp.zeros_like(project_bias[0]), project_bias[1]])[:, :, None]
    weight_rows = project_weight.transpose(0, 2, 1)
    if square:
        hidden1_full, attend_full, qkv, grads_near = start_part(
            inputs[0], first_gain, first_shift, attend_weight, weight_rows, bias, grad_out, nt, nc, heads, 0
        )
        pieces, attended_full, lse, start = attend_forward(qkv, segments, block_order, half, heads)
        feed, *feed_pieces, middle, grad_middle, vectors, attend_pieces, grad_heads = feed_part(
            pieces,
            inputs[0],
            attend_full,
            (attend_bias, second_gain, second_shift),
            expand_weight,
            shrink_weight,
            expand_bias,
            grads_near,
            grad_out,
            nt,
            nc,
            heads,
            3,
        )
        grad_qkv = attend_backward(
            qkv, segments, block_order, start, attended_full, lse, grad_heads, half, heads
        )
        outputs, grad_inputs, summed, grad_project, grad_attend, feeds = last_part(
            grad_qkv,
            weight_rows,
            hidden1_full,
            attend_pieces,
            feed,
            middle,
            shrink_bias,
            feed_pieces,
            inputs[0],
            first_gain,
            grad_middle,
            vectors,
            6,
            nt,
            heads,
            7,
        )
        grad_project = grad_project.transpose(0, 2, 1)
        grad_shrink, grad_expand = feeds[0].reshape(-1, width), feeds[1].reshape(width, -1)
        wide = expand_bias.shape[0]
    else:
        hidden1 = norm_parts(tokens_own)[0] * first_gain + first_shift
        hidden1_full = gather_rows(hidden1.astype(low), nt, 0)
        attend_full = lax.all_gather(attend_weight, "tensor", axis=0, tiled=True)
        projected = jnp.einsum(
            "ked,rd->ker", weight_rows, hidden1_full, preferred_element_type=jnp.float32
        )
        projected = (projected + bias).astype(low).reshape(3, heads, HEAD_DIM, block_rows)
        qkv = to_heads(projected, nc, 1)
        pieces, attended_full, lse, start = attend_forward(qkv, segments, block_order, half, heads)
        grad_full = lax.all_gather(grad_out, "tensor", axis=0, tiled=True)
        attended = to_rows(pieces, nc, nt, heads, 2).reshape(width, own_rows)
        middle = tokens_own + cross_rows(attended, attend_full) + attend_bias
        normed2, scale2 = norm_parts(middle)
        hidden2 = (normed2 * second_gain + second_shift).astype(low)
        hidden2_full = gather_rows(hidden2, nt, 3)
        pre_act = jnp.dot(hidden2_full, expand_weight, preferred_element_type=jnp.float32) + expand_bias
        activ = gelu_tanh(pre_act).astype(low)
        grad_act = dot(grad_full, shrink_weight, ((1,), (1,)))
        grad_pre = jax.vjp(gelu_tanh, pre_act)[1](grad_act)[0].astype(low)
        grad_shrink = cross_rows(activ, grad_full).astype(low)
        grad_expand = cross_rows(hidden2_full, grad_pre).astype(low)
        grad_hidden2 = scatter_rows(dot(grad_pre, expand_weight, ((1,), (1,))).astype(low), nt, 4)
        grad_expand_bias = jnp.sum(f32(grad_pre), axis=0)
        feed = jnp.dot(activ, shrink_weight, preferred_element_type=jnp.float32).astype(low)

        grad_shrink_bias = jnp.sum(f32(grad_out), axis=0)
        grad_second_gain = jnp.sum(grad_hidden2 * normed2, axis=0)
        grad_second_shift = jnp.sum(grad_hidden2, axis=0)
        grad_middle = f32(grad_out) + norm_backward(grad_hidden2, normed2, scale2, second_gain)
        grad_middle_low = grad_middle.astype(low)
        grad_attend_bias = jnp.sum(f32(grad_middle_low), axis=0)
        grad_attended = dot(attend_full, grad_middle_low, ((1,), (1,))).astype(low)
        grad_attended = grad_attended.reshape(nt * heads, HEAD_DIM, own_rows)
        grad_attend = jnp.dot(attended, grad_middle_low, preferred_element_type=jnp.float32).astype(low)
        grad_heads = rows_back(grad_attended, nc, nt, heads, 5)
        feed_sum = lax.psum_scatter(after(feed, grad_heads), "tensor", scatter_dimension=0, tiled=True)

        grad_qkv = attend_backward(
            qkv, segments, block_order, start, attended_full, lse, grad_heads, half, heads
        )
        grad_rows = from_heads(grad_qkv, nc, heads, 6).reshape(3 * local_width, block_rows)
        grad_project = dot(hidden1_full, grad_rows, ((0,), (1,))).astype(low)
        grad_hidden1 = cross_rows(grad_rows, weight_rows.reshape(3 * local_width, width)).astype(low)
        row_sums = jnp.sum(f32(grad_rows), axis=1)
        grad_project_bias = jnp.concatenate([row_sums[:local_width], row_sums[2 * local_width :]])
        grad_hidden1 = scatter_rows(grad_hidden1, nt, 7)
        normed1, scale1 = norm_parts(tokens_own)
        back = norm_backward(grad_hidden1, normed1, scale1, first_gain)
        grad_inputs = (grad_middle + back).astype(low)
        wide = grad_expand_bias.shape[0]
        vectors = jnp.concatenate(
            [
                jnp.sum(grad_hidden1 * normed1, axis=0),
                jnp.sum(grad_hidden1, axis=0),
                grad_attend_bias,
                grad_second_gain,
                grad_second_shift,
                grad_shrink_bias,
                grad_expand_bias,
                jnp.pad(grad_project_bias, (0, -(wide + 2 * local_width) % width)),
            ]
        ).reshape(-1, width)
        summed = sum_vectors(vectors, 6, mesh_sizes, 8)
        grad_attend = lax.psum_scatter(grad_attend, "tensor", scatter_dimension=0, tiled=True)
        grad_project, grad_attend, grad_shrink, grad_expand = lax.psum(
            (grad_project, grad_attend, grad_shrink, grad_expand), plane
        )
        grad_project = jnp.stack(
            [grad_project[:, at * local_width : (at + 1) * local_width] for at in range(3)]
        )
        outputs = (middle + f32(feed_sum) + shrink_bias).astype(low)
    tail = summed[6:].reshape(-1)
    return (
        outputs[None],
        grad_inputs[None],
        summed[0],
        summed[1],
        f32(grad_project),
        tail[wide : wide + 2 * local_width].reshape(2, local_width),
        f32(grad_attend),
        summed[2],
        summed[3],
        summed[4],
        f32(grad_expand),
        tail[:wide],
        f32(grad_shrink),
        summed[5],
    )


def solution(mesh):
    rows = P("dp", ("context", "tensor"), None)
    in_specs = (
        rows,
        P(),
        P(),
        P(None, None, "tensor"),
        P(None, "tensor"),
        P("tensor", None),
        P(),
        P(),
        P(),
        P(None, "tensor"),
        P("tensor"),
        P("tensor", None),
        P(),
        P("dp", None),
        P(),
        rows,
    )
    out_specs = (
        rows,
        rows,
        P(),
        P(),
        P(None, None, "tensor"),
        P(None, "tensor"),
        P("tensor", None),
        P(),
        P(),
        P(),
        P(None, "tensor"),
        P("tensor"),
        P("tensor", None),
        P(),
    )
    return jax.shard_map(
        functools.partial(per_device, dict(mesh.shape)),
        mesh=mesh,
        in_specs=in_specs,
        out_specs=out_specs,
        check_vma=False,
    )
```
